32 devices in a mesh: fsdp: 4 (over z), ctx: 4 (over x, core), tp: 2 (over y).
Axes of the slice: x: 2, y: 2, z: 4, core: 2. Of those that a mesh axis runs over, the one named last changes fastest.
Arguments:
- tokens: bfloat16 [4, 8192, 768], P('fsdp', 'ctx'), may hold values from -6 to 6
- lengths: int32 [4], P('fsdp'), may hold values from 4096 to 8192
- qk_weight: bfloat16 [2, 768, 768], P(None, 'fsdp', 'tp'), may hold values from -0.3125 to 0.3125
- value_weight: bfloat16 [768, 768], P('fsdp', 'tp'), may hold values from -0.21875 to 0.21875
- out_weight: bfloat16 [768, 768], P('tp', 'fsdp'), may hold values from -0.4375 to 0.4375
- in_weight: bfloat16 [768, 3072], P('fsdp', 'tp'), may hold values from -0.21875 to 0.21875
- down_weight: bfloat16 [3072, 768], P('tp', 'fsdp'), may hold values from -0.109375 to 0.109375
- norm_gains: bfloat16 [2, 768], P(None, 'fsdp'), may hold values from 0.099609375 to 1.8984375
- norm_shifts: bfloat16 [2, 768], P(None, 'fsdp'), may hold values from -3 to 3
- conv_weight: bfloat16 [12, 33], P('tp'), may hold values from -0.3984375 to 0.3984375
- cotangent: bfloat16 [4, 8192, 768], P('fsdp', 'ctx'), may hold values from -6 to 6
Outputs:
- output: bfloat16 [4, 8192, 768], P('fsdp', 'ctx')
- grad_tokens: float32 [4, 8192, 768], P('fsdp', 'ctx')
- grad_qk: float32 [2, 768, 768], P(None, 'fsdp', 'tp')
- grad_value: float32 [768, 768], P('fsdp', 'tp')
- grad_out: float32 [768, 768], P('tp', 'fsdp')
- grad_in: float32 [768, 3072], P('fsdp', 'tp')
- grad_down: float32 [3072, 768], P('tp', 'fsdp')
- grad_gains: float32 [2, 768], P(None, 'fsdp')
- grad_shifts: float32 [2, 768], P(None, 'fsdp')
- grad_conv: float32 [12, 33], P('tp')
The draws below stay inside these ranges and needn't reach their ends.
All inputs are finite; a program needn't handle non-finite values.
Results may differ from the reference program's by a relative error of at most 0.014.
The reference program's roundings to bfloat16 on the way count: a program that leaves them out, or rounds other values in their place, can miss the bound.
Values may be sent and summed in bfloat16 or wider, within the bound.
No kernel may reach another device: no remote copies, remote signals or barrier semaphores. Data moves between devices by JAX's collectives and lax.ppermute only.
A program may use at most 192 MiB of HBM per device.

```python
import jax
import jax.numpy as jnp
from jax import lax

D = 768
HEADS = 12
DH = 64
FF = 3072
LANDMARKS = 64
KW = 33
NEWTON = 6
PAD = 8192
SEQS = 4


def draw_lengths(key, part):
    drawn = jax.random.randint(jax.random.fold_in(key, 11), (SEQS,), PAD // 2, PAD + 1)
    order = jax.random.permutation(jax.random.fold_in(key, 12), SEQS)
    drawn = drawn.at[order[0]].set(PAD)
    drawn = drawn.at[order[1]].set(PAD // 2)
    return drawn.astype(jnp.int32)


def draw_tokens(key, part):
    rough = 0.7 * jax.random.normal(jax.random.fold_in(key, 21), (SEQS, PAD, D), jnp.float32)
    place = jnp.arange(PAD, dtype=jnp.float32) / PAD
    smooth = jnp.zeros((SEQS, PAD, D), jnp.float32)
    for term in range(4):
        cycles = jax.random.randint(jax.random.fold_in(key, 30 + term), (D,), 1, 16).astype(jnp.float32)
        phase = jax.random.uniform(jax.random.fold_in(key, 40 + term), (D,), jnp.float32, -3.14159, 3.14159)
        amplitude = 0.5 * jax.random.normal(jax.random.fold_in(key, 50 + term), (SEQS, 1, D), jnp.float32)
        wave = jnp.sin(6.2831853 * cycles[None, :] * place[:, None] + phase[None, :])
        smooth = smooth + amplitude * wave[None]
    return jnp.clip(rough + smooth, -6.0, 6.0).astype(jnp.bfloat16)


def strengthened(entries, rng, source, target, shards_of, factor):
    owner, partner = [(jnp.arange(entries.shape[axis_at]) // (entries.shape[axis_at] // shards_of)).reshape([-1 if axis == axis_at else 1 for axis in range(entries.ndim)]) for axis_at in (source, target)]
    chosen = jax.random.permutation(rng, shards_of)[partner]
    strong = (owner == chosen) | (owner == (partner + shards_of // 2) % shards_of)
    return jnp.where(strong, factor * entries, entries)


def shard_levels(stream_key, shape, cuts, low, largest):
    def one(axis_at, parts):
        heights = jax.random.uniform(jax.random.fold_in(jax.random.fold_in(stream_key, 6), axis_at), (parts,), jnp.float32, low / len(cuts), largest / len(cuts))
        return jnp.repeat(jnp.exp(heights), shape[axis_at] // parts).reshape((-1,) + (1,) * (len(shape) - axis_at - 1))

    loudness = one(*cuts[0])
    for cut in cuts[1:]:
        loudness = loudness * one(*cut)
    return loudness


def bell_draw(own_key, dims, width, most, shards=(), kind=jnp.bfloat16):
    values = width * jax.random.normal(own_key, dims, jnp.float32)
    if shards:
        values = values * shard_levels(own_key, dims, shards, -0.22, 0.18)
    return jnp.clip(values, -most, most).astype(kind)


def gaussian_with(key, dims, deviation, bound, pieces, heavy, kind=jnp.bfloat16):
    array = deviation * jax.random.normal(key, dims, jnp.float32)
    if pieces:
        array = array * shard_levels(key, dims, pieces, -0.22, 0.18)
    return jnp.clip(strengthened(array, jax.random.fold_in(key, 3), *heavy), -bound, bound).astype(kind)


def setup_inputs(seed: int = 0) -> dict:
    key_list = jax.random.split(jax.random.key(seed), 12)
    return {
        "tokens": draw_tokens(jax.random.fold_in(key_list[11], 71), 0),
        "lengths": draw_lengths(jax.random.fold_in(key_list[11], 71), 0),
        "qk_weight": bell_draw(key_list[2], (2, D, D), (D // 2) ** -0.5, 0.3125, ((1, 4), (2, 2))),
        "value_weight": bell_draw(key_list[3], (D, D), D ** -0.5, 0.21875, ((0, 4), (1, 2))),
        "out_weight": bell_draw(key_list[4], (D, D), (D // 4) ** -0.5, 0.4375, ((0, 2), (1, 4))),
        "in_weight": bell_draw(key_list[5], (D, FF), D ** -0.5, 0.21875, ((0, 4), (1, 2))),
        "down_weight": bell_draw(key_list[6], (FF, D), FF ** -0.5, 0.109375, ((0, 2), (1, 4))),
        "norm_gains": jnp.clip(1.0 + 0.18 * jax.random.normal(key_list[7], (2, D), jnp.float32), 0.099609375, 1.8984375).astype(jnp.bfloat16),
        "norm_shifts": bell_draw(key_list[8], (2, D), 0.5, 3.0, ((1, 4),)),
        "conv_weight": bell_draw(key_list[9], (HEADS, KW), 0.06, 0.3984375, ((0, 2),)),
        "cotangent": gaussian_with(key_list[10], (SEQS, PAD, D), 1.0, 6.0, ((0, 4), (1, 4)), (0, 2, 4, 2.0)),
    }


@jax.custom_vjp
def low(v):
    return lax.optimization_barrier(v.astype(jnp.bfloat16)).astype(jnp.float32)

@jax.custom_vjp
def low_back(v):
    return v

def low_keep(v):
    return (low(v), None)

def low_pass(kept, grad):
    return (grad,)

def back_keep(v):
    return (v, None)

def back_low(kept, grad):
    return (low(grad),)
low.defvjp(low_keep, low_pass)
low_back.defvjp(back_keep, back_low)
highest_precision = lax.Precision.HIGHEST

def layer_norm(inputs, gain_row, shift_row):
    centred = inputs - lax.optimization_barrier(jnp.mean(inputs, axis=-1, keepdims=True))
    spread = lax.optimization_barrier(jnp.mean(centred * centred, axis=-1, keepdims=True))
    return centred * lax.rsqrt(spread + 1e-05) * gain_row + shift_row

def rowwise_softmax(scores):
    summit = lax.optimization_barrier(jnp.max(scores, axis=-1, keepdims=True))
    raised = jnp.exp(scores - summit)
    return raised / lax.optimization_barrier(jnp.sum(raised, axis=-1, keepdims=True))

def gelu_exact(inputs):
    return 0.5 * inputs * (1.0 + lax.erf(inputs * 0.7071067811865476))

def iterative_pseudo_inverse(matrix):
    identity = jnp.eye(matrix.shape[-1], dtype=jnp.float32)
    approx = jnp.swapaxes(matrix, -1, -2) / lax.optimization_barrier(jnp.sum(matrix * matrix, axis=(-2, -1), keepdims=True))
    for turn_index in range(NEWTON):
        product = jnp.einsum('...ij,...jk->...ik', matrix, approx, precision=highest_precision)
        bracket = 7.0 * identity - product
        bracket = 15.0 * identity - jnp.einsum('...ij,...jk->...ik', product, bracket, precision=highest_precision)
        bracket = 13.0 * identity - jnp.einsum('...ij,...jk->...ik', product, bracket, precision=highest_precision)
        approx = 0.25 * jnp.einsum('...ij,...jk->...ik', approx, bracket, precision=highest_precision)
    return approx

def forward(inputs, qk_mat, value_mat, out_mat, in_mat, down_mat, gain_rows, shift_rows, conv_taps, seq_length):
    position = jnp.arange(PAD, dtype=jnp.int32)
    is_live = position < seq_length
    live_mask = is_live.astype(jnp.float32)[:, None]
    query_scale = DH ** (-0.25)
    query_rows = low(live_mask * query_scale * low_back(jnp.dot(inputs, qk_mat[0], precision=highest_precision)))
    key_rows = low(live_mask * query_scale * low_back(jnp.dot(inputs, qk_mat[1], precision=highest_precision)))
    value_rows = low(live_mask * low_back(jnp.dot(inputs, value_mat, precision=highest_precision)))
    segment = position * LANDMARKS // seq_length
    landmark_ids = jnp.arange(LANDMARKS, dtype=jnp.int32)
    segment_table = ((segment[None, :] == landmark_ids[:, None]) & is_live[None, :]).astype(jnp.float32)
    counts = lax.optimization_barrier(jnp.sum(segment_table, axis=1, keepdims=True))
    land_query = low(jnp.dot(segment_table, query_rows, precision=highest_precision) / counts)
    land_key = low(jnp.dot(segment_table, key_rows, precision=highest_precision) / counts)
    query_head_split = query_rows.reshape(PAD, HEADS, DH)
    key_head_split = key_rows.reshape(PAD, HEADS, DH)
    value_head_split = value_rows.reshape(PAD, HEADS, DH)
    landmark_query_split = land_query.reshape(LANDMARKS, HEADS, DH)
    landmark_key_split = land_key.reshape(LANDMARKS, HEADS, DH)
    first_similarity_kernel = rowwise_softmax(low_back(jnp.einsum('put,sut->ups', query_head_split, landmark_key_split, precision=highest_precision)))
    middle_kernel = rowwise_softmax(jnp.einsum('gfw,efw->fge', landmark_query_split, landmark_key_split, precision=highest_precision))
    third_kernel_scores = jnp.einsum('tua,pua->utp', landmark_query_split, key_head_split, precision=highest_precision)
    third_similarity_kernel = rowwise_softmax(jnp.where(is_live[None, None, :], third_kernel_scores, -1e+30))
    attention_mixture = jnp.einsum('xlg,gxf->xlf', third_similarity_kernel, value_head_split, precision=highest_precision)
    landmark_output_rows = low(jnp.einsum('voi,viz->voz', iterative_pseudo_inverse(middle_kernel), attention_mixture, precision=highest_precision))
    landmark_attention = jnp.einsum('xeq,xqa->exa', low(first_similarity_kernel), landmark_output_rows, precision=highest_precision)
    radius = KW // 2
    padded = jnp.pad(value_head_split, ((radius, radius), (0, 0), (0, 0)))
    convolved = jnp.zeros((PAD, HEADS, DH), jnp.float32)
    for tap_index in range(KW):
        convolved = convolved + conv_taps[:, tap_index][None, :, None] * padded[tap_index:tap_index + PAD]
    context = low_back(low((landmark_attention + convolved).reshape(PAD, D)))
    attended = low_back(jnp.dot(context, out_mat, precision=highest_precision))
    normed = layer_norm(inputs + attended, gain_rows[0], shift_rows[0])
    hidden = low_back(jnp.dot(low(normed), in_mat, precision=highest_precision))
    activated = low(gelu_exact(hidden))
    feed_result = low_back(jnp.dot(activated, down_mat, precision=highest_precision))
    return live_mask * layer_norm(normed + feed_result, gain_rows[1], shift_rows[1])

def reference(tokens, lengths, qk_weight, value_weight, out_weight, in_weight, down_weight, norm_gains, norm_shifts, conv_weight, cotangent):
    weight_set = (qk_weight.astype(jnp.float32), value_weight.astype(jnp.float32), out_weight.astype(jnp.float32), in_weight.astype(jnp.float32), down_weight.astype(jnp.float32), norm_gains.astype(jnp.float32), norm_shifts.astype(jnp.float32), conv_weight.astype(jnp.float32))

    def one_sequence(running, seq_item):
        seq_tokens, seq_length, seq_cotangent = seq_item

        def one_layer(inputs, qk_mat, value_mat, out_mat, in_mat, down_mat, gain_rows, shift_rows, conv_taps):
            return forward(inputs, qk_mat, value_mat, out_mat, in_mat, down_mat, gain_rows, shift_rows, conv_taps, seq_length)
        result, pull_back = jax.vjp(one_layer, seq_tokens.astype(jnp.float32), weight_set[0], weight_set[1], weight_set[2], weight_set[3], weight_set[4], weight_set[5], weight_set[6], weight_set[7])
        gradients = pull_back(seq_cotangent.astype(jnp.float32))
        updated = tuple((total + piece for total, piece in zip(running, gradients[1:])))
        return (updated, (result.astype(jnp.bfloat16), gradients[0]))
    zero_set = tuple((jnp.zeros_like(weight) for weight in weight_set))
    totals, (outputs, grad_inputs) = lax.scan(one_sequence, zero_set, (tokens, lengths, cotangent))
    return (outputs, grad_inputs, totals[0], totals[1], totals[2], totals[3], totals[4], totals[5], totals[6], totals[7])
```

```python
import jax
import jax.numpy as jnp
from jax import lax
from jax.sharding import PartitionSpec as P

LANDMARKS = 64
NEWTON = 6

HIGH = lax.Precision.HIGHEST
F32 = jnp.float32
BF16 = jnp.bfloat16


def flipped(values, axis, bit):
    count = lax.axis_size(axis)
    return lax.ppermute(values, axis, [(i, i ^ bit) for i in range(count)])


def in_order(axis, bit, mine, other, dim):
    low = (lax.axis_index(axis) & bit) == 0
    return jnp.where(
        low, jnp.concatenate([mine, other], axis=dim), jnp.concatenate([other, mine], axis=dim)
    )


def sequence_sum(values):
    width = values.shape[-1] // 2
    low = (lax.axis_index("ctx") & 1) == 0
    head, tail = values[..., :width], values[..., width:]
    kept = jnp.where(low, head, tail) + flipped(jnp.where(low, tail, head), "ctx", 1)
    kept = kept + flipped(kept, "tp", 1)
    bit = 2
    while bit < lax.axis_size("ctx"):
        kept = kept + flipped(kept, "ctx", bit)
        bit *= 2
    return in_order("ctx", 1, kept, flipped(kept, "ctx", 1), values.ndim - 1)


def sequence_merge(state, combine):
    state = combine(state, jax.tree.map(lambda a: flipped(a, "tp", 1), state))
    bit = 1
    while bit < lax.axis_size("ctx"):
        state = combine(state, jax.tree.map(lambda a: flipped(a, "ctx", bit), state))
        bit *= 2
    return state


def with_edges(cells, width):
    count = lax.axis_size("ctx") * lax.axis_size("tp")
    before = lax.ppermute(cells[-width:], ("ctx", "tp"), [(i, i + 1) for i in range(count - 1)])
    after = lax.ppermute(cells[:width], ("ctx", "tp"), [(i + 1, i) for i in range(count - 1)])
    return jnp.concatenate([before, cells, after], axis=0)


def layer_norm(inputs, gain_row, shift_row):
    centred = inputs - jnp.mean(inputs, axis=-1, keepdims=True)
    spread = jnp.mean(centred * centred, axis=-1, keepdims=True)
    return centred * lax.rsqrt(spread + 1e-05) * gain_row + shift_row


def rowwise_softmax(scores):
    summit = jnp.max(scores, axis=-1, keepdims=True)
    raised = jnp.exp(scores - summit)
    return raised / jnp.sum(raised, axis=-1, keepdims=True)


def gelu_exact(inputs):
    return 0.5 * inputs * (1.0 + lax.erf(inputs * 0.7071067811865476))


def iterative_pseudo_inverse(matrix):
    identity = jnp.eye(matrix.shape[-1], dtype=F32)
    approx = jnp.swapaxes(matrix, -1, -2) / jnp.sum(matrix * matrix, axis=(-2, -1), keepdims=True)
    for _ in range(NEWTON):
        product = jnp.einsum("...ij,...jk->...ik", matrix, approx, precision=HIGH)
        bracket = 7.0 * identity - product
        bracket = 15.0 * identity - jnp.einsum(
            "...ij,...jk->...ik", product, bracket, precision=HIGH
        )
        bracket = 13.0 * identity - jnp.einsum(
            "...ij,...jk->...ik", product, bracket, precision=HIGH
        )
        approx = 0.25 * jnp.einsum("...ij,...jk->...ik", approx, bracket, precision=HIGH)
    return approx


def landmark_map(queries, keyset, attention_mixture):
    middle_kernel = rowwise_softmax(jnp.einsum("mhd,lhd->hml", queries, keyset, precision=HIGH))
    return jnp.einsum(
        "hml,hld->hmd", iterative_pseudo_inverse(middle_kernel), attention_mixture, precision=HIGH
    )


def merge_keys(earlier, later):
    first_top, first_total, first_mixed = earlier
    second_top, second_total, second_mixed = later
    summit = jnp.maximum(first_top, second_top)
    first_factor = jnp.exp(first_top - summit)
    second_factor = jnp.exp(second_top - summit)
    return (
        summit,
        first_total * first_factor + second_total * second_factor,
        first_mixed * first_factor[..., None] + second_mixed * second_factor[..., None],
    )


def dotf(spec, *operands):
    return jnp.einsum(spec, *operands, preferred_element_type=F32)


def own_quarter(shard):
    rows = shard.shape[0] // lax.axis_size("ctx")
    return lax.dynamic_slice_in_dim(shard, lax.axis_index("ctx") * rows, rows, axis=0)


def gathered(shard):
    full = lax.all_gather(own_quarter(shard), ("tp", "fsdp", "ctx"), tiled=True)
    return full.reshape(lax.axis_size("tp"), -1, shard.shape[1])


def scattered(grads):
    flat = grads.astype(BF16).reshape(-1, grads.shape[-1])
    part = lax.psum_scatter(flat, ("tp", "fsdp", "ctx"), scatter_dimension=0, tiled=True)
    return lax.all_gather(part, "ctx", tiled=True).astype(F32)


def on_device(
    tokens,
    lengths,
    qk_weight,
    value_weight,
    out_weight,
    in_weight,
    down_weight,
    norm_gains,
    norm_shifts,
    conv_weight,
    cotangent,
):
    tp_count = lax.axis_size("tp")
    tp_index = lax.axis_index("tp")
    _, slot_len, model_width = tokens.shape
    rows = slot_len // tp_count
    local_heads, tap_count = conv_weight.shape
    local_width = value_weight.shape[1]
    head_size = local_width // local_heads
    heads = local_heads * tp_count
    width = local_width * tp_count
    radius = tap_count // 2
    length = lengths[0]

    qkv_full = gathered(jnp.concatenate([qk_weight[0], qk_weight[1], value_weight], axis=1))
    ffn_local = jnp.concatenate([out_weight.T, in_weight, down_weight.T], axis=1)
    ffn_local, qkv_full = lax.optimization_barrier((ffn_local, qkv_full))
    ffn_full = gathered(ffn_local)
    out_t = ffn_full[:, :, :local_width]
    ff_width = in_weight.shape[1]
    in_full = ffn_full[:, :, local_width : local_width + ff_width]
    down_t = ffn_full[:, :, local_width + ff_width :]
    full_gains = lax.all_gather(norm_gains, "fsdp", axis=1, tiled=True).astype(F32)
    full_shifts = lax.all_gather(norm_shifts, "fsdp", axis=1, tiled=True).astype(F32)
    tap_weights = lax.all_gather(conv_weight, "tp", axis=0, tiled=True).astype(F32)

    own = lax.dynamic_slice_in_dim(tokens[0], tp_index * rows, rows, axis=0)
    own_cotangent = lax.dynamic_slice_in_dim(cotangent[0], tp_index * rows, rows, axis=0)
    first_row = (lax.axis_index("ctx") * tp_count + tp_index) * rows
    position = first_row + jnp.arange(rows, dtype=jnp.int32)
    is_live = position < length
    live_rows = is_live.astype(F32)[:, None]
    scaled_live = live_rows * head_size ** (-0.25)

    def projected(part, scale):
        cells = dotf("tk,pkn->tpn", own, qkv_full[:, :, part * local_width : (part + 1) * local_width])
        return (scale * cells.reshape(rows, width)).astype(BF16)

    query_rows = projected(0, scaled_live)
    key_rows = projected(1, scaled_live)
    value_rows = projected(2, live_rows)
    segment = position * LANDMARKS // length
    landmark_ids = jnp.arange(LANDMARKS, dtype=jnp.int32)
    in_segment = (segment[None, :] == landmark_ids[:, None]) & is_live[None, :]
    segment_bits = in_segment.astype(BF16)
    starts = (landmark_ids * length + LANDMARKS - 1) // LANDMARKS
    ends = ((landmark_ids + 1) * length + LANDMARKS - 1) // LANDMARKS
    counts = (ends - starts).astype(F32)[:, None]
    sums = sequence_sum(
        jnp.concatenate(
            [dotf("mn,nc->mc", segment_bits, query_rows), dotf("mn,nc->mc", segment_bits, key_rows)],
            axis=1,
        )
    )
    lands = (sums / counts).astype(BF16)
    land_query = lands[:, :width].reshape(LANDMARKS, heads, head_size)
    land_key = lands[:, width:].reshape(LANDMARKS, heads, head_size)
    query_heads = query_rows.reshape(rows, heads, head_size)
    key_heads = key_rows.reshape(rows, heads, head_size)
    value_heads = value_rows.reshape(rows, heads, head_size)
    first_kernel = rowwise_softmax(dotf("nhd,mhd->hnm", query_heads, land_key))
    first_low = first_kernel.astype(BF16)
    land_query_wide = land_query.astype(F32)
    land_key_wide = land_key.astype(F32)
    key_wide = key_heads.astype(F32)
    value_wide = value_heads.astype(F32)
    key_live = is_live[None, None, :]
    third_scores = jnp.where(key_live, dotf("mhd,nhd->hmn", land_query, key_heads), -1e30)
    local_top = jnp.max(third_scores, axis=-1)
    local_weights = jnp.where(key_live, jnp.exp(third_scores - local_top[..., None]), 0.0)
    local_total = jnp.sum(local_weights, axis=-1)
    local_mixed = jnp.einsum("hmn,nhd->hmd", local_weights, value_wide, precision=HIGH)
    global_top, global_total, global_mixed = sequence_merge(
        (local_top, local_total, local_mixed), merge_keys
    )
    mixed_values = global_mixed / global_total[..., None]
    landmark_rows, pull_land = jax.vjp(landmark_map, land_query_wide, land_key_wide, mixed_values)
    land_low = landmark_rows.astype(BF16)
    landmark_attention = dotf("hnm,hmd->nhd", first_low, land_low)
    padded_values = with_edges(value_heads, radius)
    convolved = jnp.zeros((rows, heads, head_size), F32)
    for tap in range(tap_count):
        window = padded_values[tap : tap + rows].astype(F32)
        convolved = convolved + tap_weights[:, tap][None, :, None] * window
    context = (landmark_attention + convolved).reshape(rows, width).astype(BF16)
    context_parts = context.reshape(rows, tp_count, local_width)

    attended = dotf("tpc,pdc->td", context_parts, out_t)
    normed, pull_first_norm = jax.vjp(
        layer_norm, own.astype(F32) + attended, full_gains[0], full_shifts[0]
    )
    normed_low = normed.astype(BF16)
    hidden = dotf("td,pdf->ptf", normed_low, in_full)
    activated, pull_gelu = jax.vjp(gelu_exact, hidden)
    activated_low = activated.astype(BF16)
    fed = dotf("ptf,pdf->td", activated_low, down_t)
    final, pull_last_norm = jax.vjp(layer_norm, normed + fed, full_gains[1], full_shifts[1])
    own_output = (live_rows * final).astype(BF16)
    output = in_order("tp", 1, own_output, flipped(own_output, "tp", 1), 0)[None]

    grad_final = live_rows * own_cotangent.astype(F32)
    grad_second, gain_last, shift_last = pull_last_norm(grad_final)
    grad_fed_low = grad_second.astype(BF16)
    grad_down_t = dotf("td,ptf->pdf", grad_fed_low, activated_low)
    grad_act = dotf("td,pdf->ptf", grad_fed_low, down_t)
    (grad_hidden,) = pull_gelu(grad_act)
    grad_hidden_low = grad_hidden.astype(BF16)
    grad_in = dotf("td,ptf->pdf", normed_low, grad_hidden_low)
    grad_normed = grad_second + dotf("ptf,pdf->td", grad_hidden_low, in_full)
    grad_first_res, gain_first, shift_first = pull_first_norm(grad_normed)
    grad_att_low = grad_first_res.astype(BF16)
    grad_out_t = dotf("td,tpc->pdc", grad_att_low, context_parts)
    grad_context = dotf("td,pdc->tpc", grad_att_low, out_t).astype(BF16)
    ffn_grads = scattered(
        jnp.concatenate(
            [grad_out_t.astype(BF16), grad_in.astype(BF16), grad_down_t.astype(BF16)], axis=2
        )
    )

    grad_context = grad_context.reshape(rows, heads, head_size)
    padded_grads = with_edges(grad_context, radius)
    grad_values = jnp.zeros((rows, heads, head_size), F32)
    tap_grads = []
    for tap in range(tap_count):
        window = padded_values[tap : tap + rows]
        tap_grads.append(dotf("nhd,nhd->h", grad_context, window))
        start = tap_count - 1 - tap
        mirror = padded_grads[start : start + rows].astype(F32)
        grad_values = grad_values + tap_weights[:, tap][None, :, None] * mirror
    grad_conv = jnp.stack(tap_grads, axis=1)
    grad_first = dotf("nhd,hmd->hnm", grad_context, land_low)
    row_sums = jnp.sum(grad_first * first_kernel, axis=-1, keepdims=True)
    grad_first_scores = (first_kernel * (grad_first - row_sums)).astype(BF16)
    grad_land_part = dotf("hnm,nhd->mhd", first_low, grad_context).reshape(LANDMARKS, width)
    grad_query_first = dotf("hnm,mhd->nhd", grad_first_scores, land_key)
    grad_lk_part = dotf("hnm,nhd->mhd", grad_first_scores, query_heads).reshape(LANDMARKS, width)
    land_sums = sequence_sum(jnp.concatenate([grad_land_part, grad_lk_part], axis=1))
    grad_land = land_sums[:, :width].reshape(LANDMARKS, heads, head_size).transpose(1, 0, 2)
    grad_lk_first = land_sums[:, width:].reshape(LANDMARKS, heads, head_size)
    grad_lq_mid, grad_lk_mid, grad_mixed = pull_land(grad_land)
    third_kernel = (
        jnp.where(key_live, jnp.exp(third_scores - global_top[..., None]), 0.0)
        / global_total[..., None]
    )
    grad_third = jnp.einsum("hmd,nhd->hmn", grad_mixed, value_wide, precision=HIGH)
    row_dots = jnp.sum(grad_mixed * mixed_values, axis=-1)
    grad_third_scores = third_kernel * (grad_third - row_dots[..., None])
    grad_lq_part = jnp.einsum("hmn,nhd->mhd", grad_third_scores, key_wide, precision=HIGH)
    grad_keys_third = jnp.einsum(
        "hmn,mhd->nhd", grad_third_scores, land_query_wide, precision=HIGH
    )
    grad_values_third = jnp.einsum("hmn,hmd->nhd", third_kernel, grad_mixed, precision=HIGH)
    grad_lq_third = sequence_sum(grad_lq_part.reshape(LANDMARKS, width))
    grad_lq = (grad_lq_mid.reshape(LANDMARKS, width) + grad_lq_third) / counts
    grad_lk = (grad_lk_first + grad_lk_mid).reshape(LANDMARKS, width) / counts
    segment_float = in_segment.astype(F32)
    grad_query = grad_query_first.reshape(rows, width) + jnp.einsum(
        "mn,mc->nc", segment_float, grad_lq, precision=HIGH
    )
    grad_keys = grad_keys_third.reshape(rows, width) + jnp.einsum(
        "mn,mc->nc", segment_float, grad_lk, precision=HIGH
    )
    grad_values_all = (grad_values + grad_values_third).reshape(rows, width)
    grad_q_low = (scaled_live * grad_query).astype(BF16).reshape(rows, tp_count, local_width)
    grad_k_low = (scaled_live * grad_keys).astype(BF16).reshape(rows, tp_count, local_width)
    grad_v_low = (live_rows * grad_values_all).astype(BF16).reshape(rows, tp_count, local_width)
    grad_qkv_low = jnp.concatenate([grad_q_low, grad_k_low, grad_v_low], axis=2)
    back_terms = dotf("tpk,pck->tc", grad_qkv_low, qkv_full)
    own_grad = (grad_first_res + back_terms).astype(BF16)
    grad_tokens = in_order("tp", 1, own_grad, flipped(own_grad, "tp", 1), 0).astype(F32)[None]
    grad_qkv = scattered(dotf("tc,tpk->pck", own, grad_qkv_low).astype(BF16))

    small = jnp.concatenate(
        [
            jnp.stack([gain_first, gain_last, shift_first, shift_last]).reshape(-1),
            grad_conv.reshape(-1),
        ]
    )
    small = lax.psum(small, ("fsdp", "ctx", "tp"))
    rows_sum = small[: 4 * model_width].reshape(4, model_width)
    own_cols = norm_gains.shape[1]
    rows_sum = lax.dynamic_slice_in_dim(
        rows_sum, lax.axis_index("fsdp") * own_cols, own_cols, axis=1
    )
    taps_sum = small[4 * model_width :].reshape(heads, tap_count)
    taps_sum = lax.dynamic_slice_in_dim(taps_sum, tp_index * local_heads, local_heads, axis=0)
    return (
        output,
        grad_tokens,
        jnp.stack([grad_qkv[:, :local_width], grad_qkv[:, local_width : 2 * local_width]]),
        grad_qkv[:, 2 * local_width :],
        ffn_grads[:, :local_width].T,
        ffn_grads[:, local_width : local_width + ff_width],
        ffn_grads[:, local_width + ff_width :].T,
        rows_sum[:2],
        rows_sum[2:],
        taps_sum,
    )


def solution(mesh):
    in_specs = (
        P("fsdp", "ctx", None),
        P("fsdp"),
        P(None, "fsdp", "tp"),
        P("fsdp", "tp"),
        P("tp", "fsdp"),
        P("fsdp", "tp"),
        P("tp", "fsdp"),
        P(None, "fsdp"),
        P(None, "fsdp"),
        P("tp", None),
        P("fsdp", "ctx", None),
    )
    out_specs = (
        P("fsdp", "ctx", None),
        P("fsdp", "ctx", None),
        P(None, "fsdp", "tp"),
        P("fsdp", "tp"),
        P("tp", "fsdp"),
        P("fsdp", "tp"),
        P("tp", "fsdp"),
        P(None, "fsdp"),
        P(None, "fsdp"),
        P("tp", None),
    )
    return jax.shard_map(
        on_device, mesh=mesh, in_specs=in_specs, out_specs=out_specs, check_vma=False
    )
```

```python
import jax
import jax.numpy as jnp
from jax import lax
from jax.experimental import pallas as pl
from jax.experimental.pallas import tpu as pltpu
from jax.sharding import PartitionSpec as P

LANDMARKS = 64
NEWTON = 6
LANES = 128
VMEM_BYTES = 56 * 2**20

HIGH = lax.Precision.HIGHEST
F32 = jnp.float32
BF16 = jnp.bfloat16


def nn(left, right):
    return jnp.dot(left, right, preferred_element_type=F32)


def nt(left, right):
    return lax.dot_general(left, right, (((1,), (1,)), ((), ())), preferred_element_type=F32)


def split(wide):
    high = wide.astype(BF16)
    return high, (wide - high.astype(F32)).astype(BF16)


def whole(count):
    return [pl.BlockSpec(memory_space=pltpu.VMEM)] * count


SCALARS = pl.BlockSpec(memory_space=pltpu.SMEM)
PARAMS = pltpu.CompilerParams(vmem_limit_bytes=VMEM_BYTES)


def landmark_onehot(place, rows, landmark_axis):
    shape = (LANDMARKS, rows) if landmark_axis == 0 else (rows, LANDMARKS)
    landmark = lax.broadcasted_iota(jnp.int32, shape, landmark_axis)
    position = place[0] + lax.broadcasted_iota(jnp.int32, shape, 1 - landmark_axis)
    start = lax.shift_right_logical(landmark * place[1] + (LANDMARKS - 1), 6)
    end = lax.shift_right_logical((landmark + 1) * place[1] + (LANDMARKS - 1), 6)
    return jnp.where((position >= start) & (position < end), 1.0, 0.0).astype(BF16)


def live_lanes(place, rows):
    position = place[0] + lax.broadcasted_iota(jnp.int32, (1, rows), 1)
    return position < place[1]


def band(base_row):
    ring = pltpu.roll(jnp.broadcast_to(base_row, (LANES, LANES)), 0, 1, stride=1, stride_axis=0)
    gap = lax.broadcasted_iota(jnp.int32, (LANES, LANES), 0) - lax.broadcasted_iota(
        jnp.int32, (LANES, LANES), 1
    )
    zero = jnp.zeros_like(ring)
    before = jnp.where(gap >= LANES - 16, ring, zero).astype(BF16)
    here = jnp.where(jnp.abs(gap) <= 16, ring, zero).astype(BF16)
    after = jnp.where(gap <= 16 - LANES, ring, zero).astype(BF16)
    return before, here, after


def convolved(blocks, bands):
    before, here, after = bands
    return jnp.concatenate(
        [
            nn(blocks[i], before) + nn(blocks[i + 1], here) + nn(blocks[i + 2], after)
            for i in range(len(blocks) - 2)
        ],
        axis=1,
    )


def projection_kernel(place, tokens, weights, q_out, k_out, v_out, v_plain, sums):
    rows = tokens.shape[0]
    halves, _, packed = weights.shape
    width = packed // 3
    position = place[0] + lax.broadcasted_iota(jnp.int32, (rows, 1), 0)
    live = jnp.where(position < place[1], 1.0, 0.0)
    scaled = live * 64**-0.25
    onehot = landmark_onehot(place, rows, 0)
    cells = tokens[...]
    for half in range(halves):
        for part, out in enumerate((q_out, k_out, v_out)):
            product = nn(cells, weights[half, :, part * width : (part + 1) * width])
            low = ((live if part == 2 else scaled) * product).astype(BF16)
            out[half * width : (half + 1) * width, :] = low.T
            if part == 2:
                v_plain[:, half * width : (half + 1) * width] = low
            else:
                at = part * halves * width + half * width
                sums[:, at : at + width] = nn(onehot, low)


def projections(place, tokens, weights):
    rows = tokens.shape[0]
    width = weights.shape[0] * weights.shape[2] // 3
    turned = jax.ShapeDtypeStruct((width, rows), BF16)
    return pl.pallas_call(
        projection_kernel,
        out_shape=(
            turned,
            turned,
            turned,
            jax.ShapeDtypeStruct((rows, width), BF16),
            jax.ShapeDtypeStruct((LANDMARKS, 2 * width), F32),
        ),
        in_specs=[SCALARS] + whole(2),
        out_specs=tuple(whole(5)),
        compiler_params=PARAMS,
        name="projections",
    )(place, tokens, weights)


def third_kernel(place, keys, values, land_q, packed):
    heads = land_q.shape[0]
    size = land_q.shape[2]
    rows = keys.shape[1]
    live = live_lanes(place, rows)

    def head(h):
        at = pl.ds(pl.multiple_of(h * size, size), size)
        scores = jnp.where(live, nn(land_q[h], keys[at, :]), -1e30)
        top = jnp.max(scores, axis=1, keepdims=True)
        raised = jnp.where(live, jnp.exp(scores - top), 0.0)
        total = jnp.sum(raised, axis=1, keepdims=True)
        high, low = split(raised)
        value = values[at, :]
        mixed = nt(high, value) + nt(low, value)
        lane = lax.broadcasted_iota(jnp.int32, (LANDMARKS, LANES - size), 1)
        stats = jnp.where(lane == 0, top, jnp.where(lane == 1, total, 0.0))
        packed[h] = jnp.concatenate([mixed, stats], axis=1)

    def pair(i, _):
        head(2 * i)
        head(2 * i + 1)
        return 0

    lax.fori_loop(0, heads // 2, pair, 0)


def third_parts(place, keys, values, land_q):
    heads = land_q.shape[0]
    return pl.pallas_call(
        third_kernel,
        out_shape=jax.ShapeDtypeStruct((heads, LANDMARKS, LANES), F32),
        in_specs=[SCALARS] + whole(3),
        out_specs=whole(1)[0],
        compiler_params=PARAMS,
        name="third_parts",
    )(place, keys, values, land_q)


def dot_high(left, right):
    return jnp.dot(left, right, preferred_element_type=F32, precision=HIGH)


def dot_high_nt(left, right):
    return lax.dot_general(
        left, right, (((1,), (1,)), ((), ())), preferred_element_type=F32, precision=HIGH
    )


def eye():
    row = lax.broadcasted_iota(jnp.int32, (LANDMARKS, LANDMARKS), 0)
    column = lax.broadcasted_iota(jnp.int32, (LANDMARKS, LANDMARKS), 1)
    return jnp.where(row == column, 1.0, 0.0)


def middle_map(land_q, land_k):
    scores = nt(land_q, land_k)
    raised = jnp.exp(scores - jnp.max(scores, axis=1, keepdims=True))
    return raised / jnp.sum(raised, axis=1, keepdims=True)


def inverse_kernel(land_q, land_k, merged, land_out, kept_v, kept_p):
    heads = range(land_q.shape[0])
    size = land_q.shape[2]
    one = eye()
    middle = [middle_map(land_q[h], land_k[h]) for h in heads]
    approx = [m.T / jnp.sum(m * m, keepdims=True) for m in middle]
    for turn in range(NEWTON):
        product = [dot_high(middle[h], approx[h]) for h in heads]
        for h in heads:
            kept_v[turn, h] = approx[h]
            kept_p[turn, h] = product[h]
        bracket = [7.0 * one - p for p in product]
        bracket = [15.0 * one - dot_high(product[h], bracket[h]) for h in heads]
        bracket = [13.0 * one - dot_high(product[h], bracket[h]) for h in heads]
        approx = [0.25 * dot_high(approx[h], bracket[h]) for h in heads]
    for h in heads:
        kept_v[NEWTON, h] = approx[h]
        mixed = merged[h][:, :size] / merged[h][:, size + 1 : size + 2]
        land_out[h] = dot_high(approx[h], mixed).astype(BF16)


def inverse_forward(land_q, land_k, merged):
    heads = land_q.shape[0]
    square = (heads, LANDMARKS, LANDMARKS)
    return pl.pallas_call(
        inverse_kernel,
        out_shape=(
            jax.ShapeDtypeStruct(land_q.shape, BF16),
            jax.ShapeDtypeStruct((NEWTON + 1,) + square, F32),
            jax.ShapeDtypeStruct((NEWTON,) + square, F32),
        ),
        in_specs=whole(3),
        out_specs=tuple(whole(3)),
        compiler_params=PARAMS,
        name="inverse_forward",
    )(land_q, land_k, merged)


def inverse_back_kernel(land_q, land_k, merged, grads, kept_v, kept_p, spread, land_grads):
    heads = range(land_q.shape[0])
    size = land_q.shape[2]
    one = eye()
    middle = [middle_map(land_q[h], land_k[h]) for h in heads]
    turned = [m.T for m in middle]
    g_approx = []
    for h in heads:
        mixed = merged[h][:, :size] / merged[h][:, size + 1 : size + 2]
        g_land = grads[h][:, :size]
        g_approx.append(dot_high_nt(g_land, mixed))
        g_mixed = dot_high(kept_v[NEWTON, h].T, g_land)
        row_dot = jnp.sum(g_mixed * mixed, axis=1, keepdims=True)
        lane = lax.broadcasted_iota(jnp.int32, (LANDMARKS, LANES - size), 1)
        top = merged[h][:, size : size + 1]
        total = merged[h][:, size + 1 : size + 2]
        stats = jnp.where(
            lane == 0, row_dot, jnp.where(lane == 1, top, jnp.where(lane == 2, total, 0.0))
        )
        spread[h] = jnp.concatenate([g_mixed, stats], axis=1)
    g_middle = [jnp.zeros((LANDMARKS, LANDMARKS), F32) for _ in heads]
    for turn in reversed(range(NEWTON)):
        approx = [kept_v[turn, h] for h in heads]
        product = [kept_p[turn, h] for h in heads]
        first = [7.0 * one - p for p in product]
        second = [15.0 * one - dot_high(product[h], first[h]) for h in heads]
        third = [13.0 * one - dot_high(product[h], second[h]) for h in heads]
        g_third = [0.25 * dot_high(approx[h].T, g_approx[h]) for h in heads]
        g_back = [0.25 * dot_high_nt(g_approx[h], third[h]) for h in heads]
        g_product = [-dot_high_nt(g_third[h], second[h]) for h in heads]
        pt = [p.T for p in product]
        g_second = [-dot_high(pt[h], g_third[h]) for h in heads]
        g_product = [g_product[h] - dot_high_nt(g_second[h], first[h]) for h in heads]
        g_product = [g_product[h] + dot_high(pt[h], g_second[h]) for h in heads]
        g_middle = [g_middle[h] + dot_high_nt(g_product[h], approx[h]) for h in heads]
        g_approx = [g_back[h] + dot_high(turned[h], g_product[h]) for h in heads]
    for h in heads:
        m = middle[h]
        size_sum = jnp.sum(m * m, keepdims=True)
        g_size = -jnp.sum(g_approx[h] * turned[h], keepdims=True) / (size_sum * size_sum)
        g_m = g_middle[h] + g_approx[h].T / size_sum + 2.0 * g_size * m
        g_scores = m * (g_m - jnp.sum(g_m * m, axis=1, keepdims=True))
        g_q = dot_high(g_scores, land_k[h].astype(F32))
        g_k = dot_high(g_scores.T, land_q[h].astype(F32)) + grads[h][:, size:]
        land_grads[h] = jnp.concatenate([g_k, g_q], axis=1)


def inverse_backward(land_q, land_k, merged, grads, kept_v, kept_p):
    heads = land_q.shape[0]
    wide = jax.ShapeDtypeStruct((heads, LANDMARKS, LANES), F32)
    return pl.pallas_call(
        inverse_back_kernel,
        out_shape=(wide, wide),
        in_specs=whole(6),
        out_specs=tuple(whole(2)),
        compiler_params=PARAMS,
        name="inverse_backward",
    )(land_q, land_k, merged, grads, kept_v, kept_p)


def first_map(land_k, queries):
    scores = nn(land_k, queries)
    raised = jnp.exp(scores - jnp.max(scores, axis=0, keepdims=True))
    return raised * (1.0 / jnp.sum(raised, axis=0, keepdims=True))


def head_blocks(cells, ends, at):
    rows = cells.shape[1]
    left, right = ends
    return (
        [left[at, :]]
        + [cells[at, i * LANES : (i + 1) * LANES] for i in range(rows // LANES)]
        + [right[at, :]]
    )


def context_kernel(queries, values, left, right, land_k, land_out, base, context, ends):
    heads, _, size = land_k.shape
    ends[0] = left[...].T
    ends[1] = right[...].T

    def head(h):
        at = pl.ds(pl.multiple_of(h * size, size), size)
        first = first_map(land_k[h], queries[at, :]).astype(BF16)
        attended = nn(land_out[h].T, first)
        blocks = head_blocks(values, (ends.at[0], ends.at[1]), at)
        return (attended + convolved(blocks, band(base[pl.ds(h, 1), :]))).astype(BF16)

    def pair(i, _):
        both = jnp.concatenate([head(2 * i), head(2 * i + 1)], axis=0)
        context[:, pl.ds(pl.multiple_of(i * LANES, LANES), LANES)] = both.T
        return 0

    lax.fori_loop(0, heads // 2, pair, 0)


def contexts(queries, values, left, right, land_k, land_out, base):
    width, rows = queries.shape
    return pl.pallas_call(
        context_kernel,
        out_shape=jax.ShapeDtypeStruct((rows, width), BF16),
        in_specs=whole(7),
        out_specs=whole(1)[0],
        scratch_shapes=[pltpu.VMEM((2, width, LANES), BF16)],
        compiler_params=PARAMS,
        name="contexts",
    )(queries, values, left, right, land_k, land_out, base)


def context_back_kernel(
    queries, v_plain, v_left, v_right, grads, g_left, g_right, land_k, land_out, base_back,
    land_grads, g_query, g_value, g_taps, ends,
):
    heads, _, size = land_k.shape
    rows = queries.shape[1]
    blocks_in = rows // LANES
    row = lax.broadcasted_iota(jnp.int32, (LANES, LANES), 0)
    column = lax.broadcasted_iota(jnp.int32, (LANES, LANES), 1)
    reverse = jnp.where(row + column == LANES - 1, 1.0, 0.0)
    gap = row - column
    ends[0] = g_left[...].T
    ends[1] = g_right[...].T

    def pair(i, _):
        lanes = pl.ds(pl.multiple_of(i * LANES, LANES), LANES)
        turned = grads[:, lanes].T
        plain = [v_left[LANES - 16 :, lanes]]
        plain += [v_plain[b * LANES : (b + 1) * LANES, lanes] for b in range(blocks_in)]
        plain += [v_right[:16, lanes]]
        g_queries = []
        for side in range(2):
            h = 2 * i + side
            at = pl.ds(pl.multiple_of(h * size, size), size)
            query = queries[at, :]
            g_context = turned[side * size : (side + 1) * size]
            first = first_map(land_k[h], query)
            low = first.astype(BF16)
            g_first = nn(land_out[h], g_context)
            inner = jnp.sum(g_first * first, axis=0, keepdims=True)
            g_scores = (first * (g_first - inner)).astype(BF16)
            land_grads[h] = jnp.concatenate([nt(low, g_context), nt(g_scores, query)], axis=1)
            g_queries.append(nn(land_k[h].T, g_scores))
            blocks = [ends[0, at, :]]
            blocks += [g_context[:, b * LANES : (b + 1) * LANES] for b in range(blocks_in)]
            blocks += [ends[1, at, :]]
            g_value[at, :] = convolved(blocks, band(base_back[pl.ds(h, 1), :]))
            own = (row >= size) == (side == 1)
            here = jnp.zeros((LANES, LANES), F32)
            before = jnp.zeros((16, LANES), F32)
            after = jnp.zeros((16, LANES), F32)
            for b in range(blocks_in):
                piece = turned[:, b * LANES : (b + 1) * LANES]
                masked = jnp.where(own, piece, jnp.zeros_like(piece))
                prior = plain[0] if b == 0 else plain[b][LANES - 16 :]
                later = plain[b + 2][:16]
                here = here + nn(plain[b + 1], masked)
                before = before + nn(prior, masked)
                after = after + nn(later, masked)
            empty = jnp.zeros((LANES - 16, LANES), F32)
            ring = jnp.where(jnp.abs(gap) <= 16, here, 0.0)
            ring = ring + jnp.where(
                gap >= LANES - 16, jnp.concatenate([empty, before], axis=0), 0.0
            )
            ring = ring + jnp.where(
                gap <= 16 - LANES, jnp.concatenate([after, empty], axis=0), 0.0
            )
            straight = pltpu.roll(dot_high(reverse, ring), 0, 1, stride=1, stride_axis=0)
            g_taps[pl.ds(h, 1), :] = jnp.sum(straight, axis=0, keepdims=True)
        g_query[:, lanes] = jnp.concatenate(g_queries, axis=0).T
        return 0

    lax.fori_loop(0, heads // 2, pair, 0)


def contexts_back(queries, v_plain, v_ends, grads, g_ends, land_k, land_out, base_back):
    width, rows = queries.shape
    heads = land_k.shape[0]
    return pl.pallas_call(
        context_back_kernel,
        out_shape=(
            jax.ShapeDtypeStruct((heads, LANDMARKS, LANES), F32),
            jax.ShapeDtypeStruct((rows, width), F32),
            jax.ShapeDtypeStruct((width, rows), F32),
            jax.ShapeDtypeStruct((heads, LANES), F32),
        ),
        in_specs=whole(10),
        out_specs=tuple(whole(4)),
        scratch_shapes=[pltpu.VMEM((2, width, LANES), BF16)],
        compiler_params=PARAMS,
        name="contexts_back",
    )(queries, v_plain, *v_ends, grads, *g_ends, land_k, land_out, base_back)


def third_back_kernel(place, keys, values, land_q, spread, g_land_k, g_conv, g_k, g_v, g_lq):
    heads, _, size = land_q.shape
    rows = keys.shape[1]
    live = live_lanes(place, rows)
    live_row = jnp.where(live, 1.0, 0.0)
    scaled_row = live_row * 64**-0.25
    onehot = landmark_onehot(place, rows, 0)

    def pair(i, _):
        lanes = pl.ds(pl.multiple_of(i * LANES, LANES), LANES)
        g_keys, g_values, g_lqs = [], [], []
        for side in range(2):
            h = 2 * i + side
            at = pl.ds(pl.multiple_of(h * size, size), size)
            key, value = keys[at, :], values[at, :]
            pack = spread[h]
            g_mixed = pack[:, :size]
            row_dot = pack[:, size : size + 1]
            top = pack[:, size + 1 : size + 2]
            total = pack[:, size + 2 : size + 3]
            scores = nn(land_q[h], key)
            third = jnp.where(live, jnp.exp(scores - top), 0.0) * (1.0 / total)
            gm_high, gm_low = split(g_mixed)
            g_third = nn(gm_high, value) + nn(gm_low, value)
            g_high, g_low = split(third * (g_third - row_dot))
            g_lqs.append(nt(g_high, key) + nt(g_low, key))
            turned = land_q[h].T
            glk_high, glk_low = split(g_land_k[h].T)
            g_key = nn(turned, g_high) + nn(turned, g_low)
            g_key = g_key + nn(glk_high, onehot) + nn(glk_low, onehot)
            g_keys.append((scaled_row * g_key).astype(BF16))
            t_high, t_low = split(third)
            gmt_high, gmt_low = split(g_mixed.T)
            g_value = nn(gmt_high, t_high) + nn(gmt_high, t_low) + nn(gmt_low, t_high)
            g_values.append((live_row * (g_value + g_conv[at, :])).astype(BF16))
        g_k[:, lanes] = jnp.concatenate(g_keys, axis=0).T
        g_v[:, lanes] = jnp.concatenate(g_values, axis=0).T
        g_lq[:, lanes] = jnp.concatenate(g_lqs, axis=1)
        return 0

    lax.fori_loop(0, heads // 2, pair, 0)


def third_back(place, keys, values, land_q, spread, g_land_k, g_conv):
    width, rows = keys.shape
    plain = jax.ShapeDtypeStruct((rows, width), BF16)
    return pl.pallas_call(
        third_back_kernel,
        out_shape=(plain, plain, jax.ShapeDtypeStruct((LANDMARKS, width), F32)),
        in_specs=[SCALARS] + whole(6),
        out_specs=tuple(whole(3)),
        compiler_params=PARAMS,
        name="third_back",
    )(place, keys, values, land_q, spread, g_land_k, g_conv)


def query_back_kernel(place, g_first, g_land_q, g_q):
    rows = g_first.shape[0]
    onehot = landmark_onehot(place, rows, 1)
    high, low = split(g_land_q[...])
    position = place[0] + lax.broadcasted_iota(jnp.int32, (rows, 1), 0)
    scaled = jnp.where(position < place[1], 64**-0.25, 0.0)
    g_q[...] = (scaled * (g_first[...] + nn(onehot, high) + nn(onehot, low))).astype(BF16)


def query_back(place, g_first, g_land_q):
    return pl.pallas_call(
        query_back_kernel,
        out_shape=jax.ShapeDtypeStruct(g_first.shape, BF16),
        in_specs=[SCALARS] + whole(2),
        out_specs=whole(1)[0],
        compiler_params=PARAMS,
        name="query_back",
    )(place, g_first, g_land_q)


def flipped(values, axis, bit):
    count = lax.axis_size(axis)
    return lax.ppermute(values, axis, [(i, i ^ bit) for i in range(count)])


def side_of(axis, bit):
    return (lax.axis_index(axis) // bit) % 2


def paired(mine, axis, bit, dim):
    other = flipped(mine, axis, bit)
    both = jnp.zeros(mine.shape[:dim] + (2,) + mine.shape[dim:], mine.dtype)
    side = side_of(axis, bit)
    both = lax.dynamic_update_slice_in_dim(both, jnp.expand_dims(mine, dim), side, dim)
    return lax.dynamic_update_slice_in_dim(both, jnp.expand_dims(other, dim), 1 - side, dim)


def ctx_bits():
    bits, bit = [], 1
    while bit < lax.axis_size("ctx"):
        bits.append(bit)
        bit *= 2
    return bits


def sequence_sum(values):
    width = values.shape[1] // 2
    side = side_of("ctx", 1)
    kept = lax.dynamic_slice_in_dim(values, side * width, width, axis=1)
    sent = lax.dynamic_slice_in_dim(values, (1 - side) * width, width, axis=1)
    kept = kept + flipped(sent, "ctx", 1)
    kept = kept + flipped(kept, "tp", 1)
    for bit in ctx_bits()[1:]:
        kept = kept + flipped(kept, "ctx", bit)
    other = flipped(kept, "ctx", 1)
    return jnp.where(
        side == 0,
        jnp.concatenate([kept, other], axis=1),
        jnp.concatenate([other, kept], axis=1),
    )


def to_owner(packed, combine):
    kept = packed.reshape((lax.axis_size("ctx"), -1) + packed.shape[1:])
    for bit in ctx_bits():
        view = kept.reshape((kept.shape[0] // 2, 2) + kept.shape[1:])
        side = side_of("ctx", bit)
        sent = lax.dynamic_index_in_dim(view, 1 - side, 1, False)
        kept = lax.dynamic_index_in_dim(view, side, 1, False)
        kept = combine(kept, flipped(sent, "ctx", bit))
    kept = kept[0]
    return combine(kept, flipped(kept, "tp", 1))


def from_owners(part):
    whole_part = part[None]
    for bit in reversed(ctx_bits()):
        both = paired(whole_part, "ctx", bit, 1)
        whole_part = both.reshape((-1,) + part.shape)
    return whole_part.reshape((-1,) + part.shape[1:])


def merge_keys(one, two):
    size = LANES // 2
    one_top, two_top = one[..., size : size + 1], two[..., size : size + 1]
    top = jnp.maximum(one_top, two_top)
    one_factor, two_factor = jnp.exp(one_top - top), jnp.exp(two_top - top)
    summed = one * one_factor + two * two_factor
    lane = lax.broadcasted_iota(jnp.int32, summed.shape, summed.ndim - 1)
    return jnp.where(lane == size, top, summed)


def neighbour_rows(cells, count):
    pieces = lax.axis_size("ctx") * lax.axis_size("tp")
    up = [(i, i + 1) for i in range(pieces - 1)]
    before = lax.ppermute(cells[-count:], ("ctx", "tp"), up)
    after = lax.ppermute(cells[:count], ("ctx", "tp"), [(j, i) for i, j in up])
    return (
        jnp.pad(before, ((LANES - count, 0), (0, 0))),
        jnp.pad(after, ((0, LANES - count), (0, 0))),
    )


def own_quarter(shard):
    rows = shard.shape[0] // lax.axis_size("ctx")
    return lax.dynamic_slice_in_dim(shard, lax.axis_index("ctx") * rows, rows, axis=0)


def gathered(shard):
    full = lax.all_gather(own_quarter(shard), ("tp", "fsdp", "ctx"), tiled=True)
    return full.reshape(lax.axis_size("tp"), -1, shard.shape[1])


def gathered_early(shard):
    count = lax.axis_size("fsdp")
    piece = own_quarter(shard)
    if count > 4:
        held = lax.all_gather(piece, "fsdp")
    else:
        here = lax.axis_index("fsdp")
        held = jnp.zeros((count,) + piece.shape, piece.dtype)
        held = lax.dynamic_update_slice_in_dim(held, piece[None], here, 0)
        for step in range(1, count):
            moved = lax.ppermute(piece, "fsdp", [(i, (i + step) % count) for i in range(count)])
            held = lax.dynamic_update_slice_in_dim(held, moved[None], (here - step) % count, 0)
    bits = ctx_bits()
    halves = []
    for number, half in enumerate((held[: count // 2], held[count // 2 :])):
        half = half[None]
        if number == 0:
            half = paired(half[0], "tp", 1, 0)
        for place, bit in enumerate(reversed(bits[1:])):
            half = paired(half, "ctx", bit, 2 + place)
        if number == 1:
            half = paired(half[0], "tp", 1, 0)
        halves.append(paired(half, "ctx", bits[0], 1 + len(bits)))
    full = jnp.concatenate(halves, axis=1)
    return full.reshape(lax.axis_size("tp"), -1, shard.shape[1])


def scattered(grads):
    flat = grads.astype(BF16).reshape(-1, grads.shape[-1])
    part = lax.psum_scatter(flat, ("tp", "fsdp", "ctx"), scatter_dimension=0, tiled=True)
    return from_owners(part).astype(F32)


def layer_norm(inputs, gain_row, shift_row):
    centred = inputs - jnp.mean(inputs, axis=-1, keepdims=True)
    spread = jnp.mean(centred * centred, axis=-1, keepdims=True)
    return centred * lax.rsqrt(spread + 1e-05) * gain_row + shift_row


def gelu_exact(inputs):
    return 0.5 * inputs * (1.0 + lax.erf(inputs * 0.7071067811865476))


def dotf(spec, *operands):
    return jnp.einsum(spec, *operands, preferred_element_type=F32)


def taps_round(taps):
    middle = taps.shape[1] // 2
    gap = jnp.zeros((taps.shape[0], LANES - taps.shape[1]), F32)
    return jnp.concatenate([taps[:, middle::-1], gap, taps[:, :middle:-1]], axis=1)


def on_device(
    tokens,
    lengths,
    qk_weight,
    value_weight,
    out_weight,
    in_weight,
    down_weight,
    norm_gains,
    norm_shifts,
    conv_weight,
    cotangent,
):
    tp_count = lax.axis_size("tp")
    tp_index = lax.axis_index("tp")
    ctx_index = lax.axis_index("ctx")
    _, slot_len, model_width = tokens.shape
    rows = slot_len // tp_count
    local_heads, tap_count = conv_weight.shape
    local_width = value_weight.shape[1]
    ff_width = in_weight.shape[1]
    head_size = local_width // local_heads
    heads = local_heads * tp_count
    own_heads = heads // lax.axis_size("ctx")
    width = local_width * tp_count
    radius = tap_count // 2
    length = lengths[0]

    qkv_full = gathered_early(jnp.concatenate([qk_weight[0], qk_weight[1], value_weight], axis=1))
    norm_columns = jnp.concatenate([norm_gains, norm_shifts], axis=0).T
    norm_columns = jnp.pad(norm_columns, ((0, 0), (0, LANES - norm_columns.shape[1])))
    ffn_local = jnp.concatenate([in_weight, down_weight.T, out_weight.T, norm_columns], axis=1)
    ffn_local, qkv_full = lax.optimization_barrier((ffn_local, qkv_full))
    ffn_full = gathered(ffn_local)
    in_full = ffn_full[:, :, :ff_width]
    down_t = ffn_full[:, :, ff_width : 2 * ff_width]
    out_t = ffn_full[:, :, 2 * ff_width : 2 * ff_width + local_width]
    norm_rows = ffn_full[0, :, 2 * ff_width + local_width :][:, :4].T.astype(F32)
    full_gains, full_shifts = norm_rows[:2], norm_rows[2:]
    tap_weights = paired(conv_weight, "tp", 1, 0).reshape(heads, tap_count).astype(F32)
    base, base_back = taps_round(tap_weights), taps_round(tap_weights[:, ::-1])

    own = lax.dynamic_slice_in_dim(tokens[0], tp_index * rows, rows, axis=0)
    own_cotangent = lax.dynamic_slice_in_dim(cotangent[0], tp_index * rows, rows, axis=0)
    first_row = (ctx_index * tp_count + tp_index) * rows
    place = jnp.stack([first_row, length]).astype(jnp.int32)
    live_rows = (first_row + jnp.arange(rows, dtype=jnp.int32) < length).astype(F32)[:, None]

    queries, keys, values, v_plain, sums = projections(place, own, qkv_full)
    v_ends = neighbour_rows(v_plain, radius)
    landmark_ids = jnp.arange(LANDMARKS, dtype=jnp.int32)
    starts = (landmark_ids * length + LANDMARKS - 1) // LANDMARKS
    ends = ((landmark_ids + 1) * length + LANDMARKS - 1) // LANDMARKS
    counts = (ends - starts).astype(F32)[:, None]
    lands = (sequence_sum(sums) / counts).astype(BF16)
    lands = lands.reshape(LANDMARKS, 2, heads, head_size).transpose(1, 2, 0, 3)
    land_q, land_k = lands[0], lands[1]
    own_lands = lax.dynamic_slice_in_dim(lands, ctx_index * own_heads, own_heads, axis=1)
    own_q, own_k = own_lands[0], own_lands[1]

    merged = to_owner(third_parts(place, keys, values, land_q), merge_keys)
    own_out, kept_v, kept_p = inverse_forward(own_q, own_k, merged)
    land_out = from_owners(own_out)
    context = contexts(queries, values, *v_ends, land_k, land_out, base)
    context_parts = context.reshape(rows, tp_count, local_width)

    attended = dotf("tpc,pdc->td", context_parts, out_t)
    normed, pull_first_norm = jax.vjp(
        layer_norm, own.astype(F32) + attended, full_gains[0], full_shifts[0]
    )
    normed_low = normed.astype(BF16)
    hidden = dotf("td,pdf->ptf", normed_low, in_full)
    activated, pull_gelu = jax.vjp(gelu_exact, hidden)
    activated_low = activated.astype(BF16)
    fed = dotf("ptf,pdf->td", activated_low, down_t)
    final, pull_last_norm = jax.vjp(layer_norm, normed + fed, full_gains[1], full_shifts[1])
    own_output = (live_rows * final).astype(BF16)
    output = paired(own_output, "tp", 1, 0).reshape(1, slot_len, model_width)

    grad_final = live_rows * own_cotangent.astype(F32)
    grad_second, gain_last, shift_last = pull_last_norm(grad_final)
    grad_fed_low = grad_second.astype(BF16)
    grad_down = scattered(dotf("td,ptf->pdf", grad_fed_low, activated_low)).T
    grad_act = dotf("td,pdf->ptf", grad_fed_low, down_t)
    (grad_hidden,) = pull_gelu(grad_act)
    grad_hidden_low = grad_hidden.astype(BF16)
    grad_in = scattered(dotf("td,ptf->pdf", normed_low, grad_hidden_low))
    grad_normed = grad_second + dotf("ptf,pdf->td", grad_hidden_low, in_full)
    grad_first_res, gain_first, shift_first = pull_first_norm(grad_normed)
    grad_att_low = grad_first_res.astype(BF16)
    grad_out_t = dotf("td,tpc->pdc", grad_att_low, context_parts)
    grad_context = dotf("td,pdc->tpc", grad_att_low, out_t).astype(BF16).reshape(rows, width)

    g_ends = neighbour_rows(grad_context, radius)
    land_parts, g_query_first, g_value_conv, g_taps = contexts_back(
        queries, v_plain, v_ends, grad_context, g_ends, land_k, land_out, base_back
    )
    own_grads = to_owner(land_parts, jnp.add)
    spread, land_grads = inverse_backward(own_q, own_k, merged, own_grads, kept_v, kept_p)
    own_lk = jnp.concatenate(
        [land_grads[:, :, :head_size] / counts, jnp.zeros_like(spread[:, :, head_size:])], axis=2
    )
    shared = from_owners(jnp.stack([spread, own_lk], axis=1))
    g_k, g_v, g_lq = third_back(
        place, keys, values, land_q, shared[:, 0], shared[:, 1, :, :head_size], g_value_conv
    )
    own_lq = land_grads[:, :, head_size:].transpose(1, 0, 2).reshape(LANDMARKS, -1)
    own_lq = jnp.where(tp_index == 0, own_lq, 0.0)
    own_lq = lax.dynamic_update_slice_in_dim(
        jnp.zeros_like(g_lq), own_lq, ctx_index * own_heads * head_size, axis=1
    )
    g_q = query_back(place, g_query_first, sequence_sum(g_lq + own_lq) / counts)

    owners = lax.axis_size("fsdp")
    owner_rows = model_width // owners
    taps_grad = jnp.take(
        g_taps, jnp.array([(LANES + radius - 1 - i) % LANES for i in range(tap_count)]), axis=1
    ).reshape(tp_count, -1)
    tap_columns = -(-taps_grad.shape[1] // owner_rows)
    taps_grad = jnp.pad(taps_grad, ((0, 0), (0, tap_columns * owner_rows - taps_grad.shape[1])))
    taps_grad = jnp.tile(taps_grad.reshape(tp_count, owner_rows, tap_columns), (1, owners, 1))
    norm_grads = jnp.stack([gain_first, gain_last, shift_first, shift_last], axis=1)
    small = jnp.concatenate(
        [jnp.broadcast_to(norm_grads[None], (tp_count,) + norm_grads.shape), taps_grad], axis=2
    )
    small = jnp.pad(small, ((0, 0), (0, 0), (0, LANES - small.shape[2])))
    mixed_grads = scattered(jnp.concatenate([grad_out_t, small], axis=2))
    own_small = mixed_grads[:, local_width:]
    grad_taps = own_small[:, 4 : 4 + tap_columns].reshape(-1)[: local_heads * tap_count]

    g_qkv = jnp.concatenate(
        [cells.reshape(rows, tp_count, local_width) for cells in (g_q, g_k, g_v)], axis=2
    )
    back_terms = dotf("tpk,pck->tc", g_qkv, qkv_full)
    own_grad = (grad_first_res + back_terms).astype(BF16)
    grad_tokens = paired(own_grad, "tp", 1, 0).reshape(1, slot_len, model_width).astype(F32)
    grad_qkv = scattered(dotf("tc,tpk->pck", own, g_qkv))
    return (
        output,
        grad_tokens,
        jnp.stack([grad_qkv[:, :local_width], grad_qkv[:, local_width : 2 * local_width]]),
        grad_qkv[:, 2 * local_width :],
        mixed_grads[:, :local_width].T,
        grad_in,
        grad_down,
        own_small[:, :2].T,
        own_small[:, 2:4].T,
        grad_taps.reshape(local_heads, tap_count),
    )


def solution(mesh):
    in_specs = (
        P("fsdp", "ctx", None),
        P("fsdp"),
        P(None, "fsdp", "tp"),
        P("fsdp", "tp"),
        P("tp", "fsdp"),
        P("fsdp", "tp"),
        P("tp", "fsdp"),
        P(None, "fsdp"),
        P(None, "fsdp"),
        P("tp", None),
        P("fsdp", "ctx", None),
    )
    out_specs = (
        P("fsdp", "ctx", None),
        P("fsdp", "ctx", None),
        P(None, "fsdp", "tp"),
        P("fsdp", "tp"),
        P("tp", "fsdp"),
        P("fsdp", "tp"),
        P("tp", "fsdp"),
        P(None, "fsdp"),
        P(None, "fsdp"),
        P("tp", None),
    )
    return jax.shard_map(
        on_device, mesh=mesh, in_specs=in_specs, out_specs=out_specs, check_vma=False
    )
```

```python
import jax
import jax.numpy as jnp
from jax import lax
from jax.experimental import pallas as pl
from jax.experimental.pallas import tpu as pltpu
from jax.sharding import PartitionSpec as P

LANDMARKS = 64
NEWTON = 6
LANES = 128
VMEM_BYTES = 56 * 2**20

HIGH = lax.Precision.HIGHEST
F32 = jnp.float32
BF16 = jnp.bfloat16


def nn(left, right):
    return jnp.dot(left, right, preferred_element_type=F32)


def nt(left, right):
    return lax.dot_general(left, right, (((1,), (1,)), ((), ())), preferred_element_type=F32)


def split(wide):
    high = wide.astype(BF16)
    return high, (wide - high.astype(F32)).astype(BF16)


def whole(count):
    return [pl.BlockSpec(memory_space=pltpu.VMEM)] * count


SCALARS = pl.BlockSpec(memory_space=pltpu.SMEM)
PARAMS = pltpu.CompilerParams(vmem_limit_bytes=VMEM_BYTES)


def landmark_onehot(place, rows, landmark_axis):
    shape = (LANDMARKS, rows) if landmark_axis == 0 else (rows, LANDMARKS)
    landmark = lax.broadcasted_iota(jnp.int32, shape, landmark_axis)
    position = place[0] + lax.broadcasted_iota(jnp.int32, shape, 1 - landmark_axis)
    start = lax.shift_right_logical(landmark * place[1] + (LANDMARKS - 1), 6)
    end = lax.shift_right_logical((landmark + 1) * place[1] + (LANDMARKS - 1), 6)
    return jnp.where((position >= start) & (position < end), 1.0, 0.0).astype(BF16)


def live_lanes(place, rows):
    position = place[0] + lax.broadcasted_iota(jnp.int32, (1, rows), 1)
    return position < place[1]


def band(base_row):
    ring = pltpu.roll(jnp.broadcast_to(base_row, (LANES, LANES)), 0, 1, stride=1, stride_axis=0)
    gap = lax.broadcasted_iota(jnp.int32, (LANES, LANES), 0) - lax.broadcasted_iota(
        jnp.int32, (LANES, LANES), 1
    )
    zero = jnp.zeros_like(ring)
    before = jnp.where(gap >= LANES - 16, ring, zero).astype(BF16)
    here = jnp.where(jnp.abs(gap) <= 16, ring, zero).astype(BF16)
    after = jnp.where(gap <= 16 - LANES, ring, zero).astype(BF16)
    return before, here, after


def convolved(blocks, bands):
    before, here, after = bands
    return jnp.concatenate(
        [
            nn(blocks[i], before) + nn(blocks[i + 1], here) + nn(blocks[i + 2], after)
            for i in range(len(blocks) - 2)
        ],
        axis=1,
    )


def projection_kernel(place, tokens, weights, q_out, k_out, v_out, v_plain, sums):
    rows = tokens.shape[0]
    halves, _, packed = weights.shape
    width = packed // 3
    position = place[0] + lax.broadcasted_iota(jnp.int32, (rows, 1), 0)
    live = jnp.where(position < place[1], 1.0, 0.0)
    scaled = live * 64**-0.25
    onehot = landmark_onehot(place, rows, 0)
    cells = tokens[...]
    for half in range(halves):
        for part, out in enumerate((q_out, k_out, v_out)):
            product = nn(cells, weights[half, :, part * width : (part + 1) * width])
            low = ((live if part == 2 else scaled) * product).astype(BF16)
            out[half * width : (half + 1) * width, :] = low.T
            if part == 2:
                v_plain[:, half * width : (half + 1) * width] = low
            else:
                at = part * halves * width + half * width
                sums[:, at : at + width] = nn(onehot, low)


def projections(place, tokens, weights):
    rows = tokens.shape[0]
    width = weights.shape[0] * weights.shape[2] // 3
    turned = jax.ShapeDtypeStruct((width, rows), BF16)
    return pl.pallas_call(
        projection_kernel,
        out_shape=(
            turned,
            turned,
            turned,
            jax.ShapeDtypeStruct((rows, width), BF16),
            jax.ShapeDtypeStruct((LANDMARKS, 2 * width), F32),
        ),
        in_specs=[SCALARS] + whole(2),
        out_specs=tuple(whole(5)),
        compiler_params=PARAMS,
        name="projections",
    )(place, tokens, weights)


def third_kernel(place, keys, values, land_q, packed):
    heads = land_q.shape[0]
    size = land_q.shape[2]
    rows = keys.shape[1]
    live = live_lanes(place, rows)

    def head(h):
        at = pl.ds(pl.multiple_of(h * size, size), size)
        scores = jnp.where(live, nn(land_q[h], keys[at, :]), -1e30)
        top = jnp.max(scores, axis=1, keepdims=True)
        raised = jnp.where(live, jnp.exp(scores - top), 0.0)
        total = jnp.sum(raised, axis=1, keepdims=True)
        high, low = split(raised)
        value = values[at, :]
        mixed = nt(high, value) + nt(low, value)
        lane = lax.broadcasted_iota(jnp.int32, (LANDMARKS, LANES - size), 1)
        stats = jnp.where(lane == 0, top, jnp.where(lane == 1, total, 0.0))
        packed[h] = jnp.concatenate([mixed, stats], axis=1)

    def pair(i, _):
        head(2 * i)
        head(2 * i + 1)
        return 0

    lax.fori_loop(0, heads // 2, pair, 0)


def third_parts(place, keys, values, land_q):
    heads = land_q.shape[0]
    return pl.pallas_call(
        third_kernel,
        out_shape=jax.ShapeDtypeStruct((heads, LANDMARKS, LANES), F32),
        in_specs=[SCALARS] + whole(3),
        out_specs=whole(1)[0],
        compiler_params=PARAMS,
        name="third_parts",
    )(place, keys, values, land_q)


def dot_high(left, right):
    return jnp.dot(left, right, preferred_element_type=F32, precision=HIGH)


def dot_high_nt(left, right):
    return lax.dot_general(
        left, right, (((1,), (1,)), ((), ())), preferred_element_type=F32, precision=HIGH
    )


def eye():
    row = lax.broadcasted_iota(jnp.int32, (LANDMARKS, LANDMARKS), 0)
    column = lax.broadcasted_iota(jnp.int32, (LANDMARKS, LANDMARKS), 1)
    return jnp.where(row == column, 1.0, 0.0)


def middle_map(land_q, land_k):
    scores = nt(land_q, land_k)
    raised = jnp.exp(scores - jnp.max(scores, axis=1, keepdims=True))
    return raised / jnp.sum(raised, axis=1, keepdims=True)


def inverse_kernel(land_q, land_k, merged, land_out, kept_v, kept_p):
    heads = range(land_q.shape[0])
    size = land_q.shape[2]
    one = eye()
    middle = [middle_map(land_q[h], land_k[h]) for h in heads]
    approx = [m.T / jnp.sum(m * m, keepdims=True) for m in middle]
    for turn in range(NEWTON):
        product = [dot_high(middle[h], approx[h]) for h in heads]
        for h in heads:
            kept_v[turn, h] = approx[h]
            kept_p[turn, h] = product[h]
        bracket = [7.0 * one - p for p in product]
        bracket = [15.0 * one - dot_high(product[h], bracket[h]) for h in heads]
        bracket = [13.0 * one - dot_high(product[h], bracket[h]) for h in heads]
        approx = [0.25 * dot_high(approx[h], bracket[h]) for h in heads]
    for h in heads:
        kept_v[NEWTON, h] = approx[h]
        mixed = merged[h][:, :size] / merged[h][:, size + 1 : size + 2]
        land_out[h] = dot_high(approx[h], mixed).astype(BF16)


def inverse_forward(land_q, land_k, merged):
    heads = land_q.shape[0]
    square = (heads, LANDMARKS, LANDMARKS)
    return pl.pallas_call(
        inverse_kernel,
        out_shape=(
            jax.ShapeDtypeStruct(land_q.shape, BF16),
            jax.ShapeDtypeStruct((NEWTON + 1,) + square, F32),
            jax.ShapeDtypeStruct((NEWTON,) + square, F32),
        ),
        in_specs=whole(3),
        out_specs=tuple(whole(3)),
        compiler_params=PARAMS,
        name="inverse_forward",
    )(land_q, land_k, merged)


def inverse_back_kernel(land_q, land_k, merged, grads, kept_v, kept_p, spread, land_grads):
    heads = range(land_q.shape[0])
    size = land_q.shape[2]
    one = eye()
    middle = [middle_map(land_q[h], land_k[h]) for h in heads]
    turned = [m.T for m in middle]
    g_approx = []
    for h in heads:
        mixed = merged[h][:, :size] / merged[h][:, size + 1 : size + 2]
        g_land = grads[h][:, :size]
        g_approx.append(dot_high_nt(g_land, mixed))
        g_mixed = dot_high(kept_v[NEWTON, h].T, g_land)
        row_dot = jnp.sum(g_mixed * mixed, axis=1, keepdims=True)
        lane = lax.broadcasted_iota(jnp.int32, (LANDMARKS, LANES - size), 1)
        top = merged[h][:, size : size + 1]
        total = merged[h][:, size + 1 : size + 2]
        stats = jnp.where(
            lane == 0, row_dot, jnp.where(lane == 1, top, jnp.where(lane == 2, total, 0.0))
        )
        spread[h] = jnp.concatenate([g_mixed, stats], axis=1)
    g_middle = [jnp.zeros((LANDMARKS, LANDMARKS), F32) for _ in heads]
    for turn in reversed(range(NEWTON)):
        approx = [kept_v[turn, h] for h in heads]
        product = [kept_p[turn, h] for h in heads]
        first = [7.0 * one - p for p in product]
        second = [15.0 * one - dot_high(product[h], first[h]) for h in heads]
        third = [13.0 * one - dot_high(product[h], second[h]) for h in heads]
        g_third = [0.25 * dot_high(approx[h].T, g_approx[h]) for h in heads]
        g_back = [0.25 * dot_high_nt(g_approx[h], third[h]) for h in heads]
        g_product = [-dot_high_nt(g_third[h], second[h]) for h in heads]
        pt = [p.T for p in product]
        g_second = [-dot_high(pt[h], g_third[h]) for h in heads]
        g_product = [g_product[h] - dot_high_nt(g_second[h], first[h]) for h in heads]
        g_product = [g_product[h] + dot_high(pt[h], g_second[h]) for h in heads]
        g_middle = [g_middle[h] + dot_high_nt(g_product[h], approx[h]) for h in heads]
        g_approx = [g_back[h] + dot_high(turned[h], g_product[h]) for h in heads]
    for h in heads:
        m = middle[h]
        size_sum = jnp.sum(m * m, keepdims=True)
        g_size = -jnp.sum(g_approx[h] * turned[h], keepdims=True) / (size_sum * size_sum)
        g_m = g_middle[h] + g_approx[h].T / size_sum + 2.0 * g_size * m
        g_scores = m * (g_m - jnp.sum(g_m * m, axis=1, keepdims=True))
        g_q = dot_high(g_scores, land_k[h].astype(F32))
        g_k = dot_high(g_scores.T, land_q[h].astype(F32)) + grads[h][:, size:]
        land_grads[h] = jnp.concatenate([g_k, g_q], axis=1)


def inverse_backward(land_q, land_k, merged, grads, kept_v, kept_p):
    heads = land_q.shape[0]
    wide = jax.ShapeDtypeStruct((heads, LANDMARKS, LANES), F32)
    return pl.pallas_call(
        inverse_back_kernel,
        out_shape=(wide, wide),
        in_specs=whole(6),
        out_specs=tuple(whole(2)),
        compiler_params=PARAMS,
        name="inverse_backward",
    )(land_q, land_k, merged, grads, kept_v, kept_p)


def first_map(land_k, queries):
    scores = nn(land_k, queries)
    raised = jnp.exp(scores - jnp.max(scores, axis=0, keepdims=True))
    return raised * (1.0 / jnp.sum(raised, axis=0, keepdims=True))


def head_blocks(cells, ends, at):
    rows = cells.shape[1]
    left, right = ends
    return (
        [left[at, :]]
        + [cells[at, i * LANES : (i + 1) * LANES] for i in range(rows // LANES)]
        + [right[at, :]]
    )


def context_kernel(queries, values, left, right, land_k, land_out, base, context, ends):
    heads, _, size = land_k.shape
    ends[0] = left[...].T
    ends[1] = right[...].T

    def head(h):
        at = pl.ds(pl.multiple_of(h * size, size), size)
        first = first_map(land_k[h], queries[at, :]).astype(BF16)
        attended = nn(land_out[h].T, first)
        blocks = head_blocks(values, (ends.at[0], ends.at[1]), at)
        return (attended + convolved(blocks, band(base[pl.ds(h, 1), :]))).astype(BF16)

    def pair(i, _):
        both = jnp.concatenate([head(2 * i), head(2 * i + 1)], axis=0)
        context[:, pl.ds(pl.multiple_of(i * LANES, LANES), LANES)] = both.T
        return 0

    lax.fori_loop(0, heads // 2, pair, 0)


def contexts(queries, values, left, right, land_k, land_out, base):
    width, rows = queries.shape
    return pl.pallas_call(
        context_kernel,
        out_shape=jax.ShapeDtypeStruct((rows, width), BF16),
        in_specs=whole(7),
        out_specs=whole(1)[0],
        scratch_shapes=[pltpu.VMEM((2, width, LANES), BF16)],
        compiler_params=PARAMS,
        name="contexts",
    )(queries, values, left, right, land_k, land_out, base)


def context_back_kernel(
    queries, v_plain, v_left, v_right, grads, g_left, g_right, land_k, land_out, base_back,
    land_grads, g_query, g_value, g_taps, ends,
):
    heads, _, size = land_k.shape
    rows = queries.shape[1]
    blocks_in = rows // LANES
    row = lax.broadcasted_iota(jnp.int32, (LANES, LANES), 0)
    column = lax.broadcasted_iota(jnp.int32, (LANES, LANES), 1)
    reverse = jnp.where(row + column == LANES - 1, 1.0, 0.0)
    gap = row - column
    ends[0] = g_left[...].T
    ends[1] = g_right[...].T

    def pair(i, _):
        lanes = pl.ds(pl.multiple_of(i * LANES, LANES), LANES)
        turned = grads[:, lanes].T
        plain = [v_left[LANES - 16 :, lanes]]
        plain += [v_plain[b * LANES : (b + 1) * LANES, lanes] for b in range(blocks_in)]
        plain += [v_right[:16, lanes]]
        g_queries = []
        for side in range(2):
            h = 2 * i + side
            at = pl.ds(pl.multiple_of(h * size, size), size)
            query = queries[at, :]
            g_context = turned[side * size : (side + 1) * size]
            first = first_map(land_k[h], query)
            low = first.astype(BF16)
            g_first = nn(land_out[h], g_context)
            inner = jnp.sum(g_first * first, axis=0, keepdims=True)
            g_scores = (first * (g_first - inner)).astype(BF16)
            land_grads[h] = jnp.concatenate([nt(low, g_context), nt(g_scores, query)], axis=1)
            g_queries.append(nn(land_k[h].T, g_scores))
            blocks = [ends[0, at, :]]
            blocks += [g_context[:, b * LANES : (b + 1) * LANES] for b in range(blocks_in)]
            blocks += [ends[1, at, :]]
            g_value[at, :] = convolved(blocks, band(base_back[pl.ds(h, 1), :]))
            own = (row >= size) == (side == 1)
            here = jnp.zeros((LANES, LANES), F32)
            before = jnp.zeros((16, LANES), F32)
            after = jnp.zeros((16, LANES), F32)
            for b in range(blocks_in):
                piece = turned[:, b * LANES : (b + 1) * LANES]
                masked = jnp.where(own, piece, jnp.zeros_like(piece))
                prior = plain[0] if b == 0 else plain[b][LANES - 16 :]
                later = plain[b + 2][:16]
                here = here + nn(plain[b + 1], masked)
                before = before + nn(prior, masked)
                after = after + nn(later, masked)
            empty = jnp.zeros((LANES - 16, LANES), F32)
            ring = jnp.where(jnp.abs(gap) <= 16, here, 0.0)
            ring = ring + jnp.where(
                gap >= LANES - 16, jnp.concatenate([empty, before], axis=0), 0.0
            )
            ring = ring + jnp.where(
                gap <= 16 - LANES, jnp.concatenate([after, empty], axis=0), 0.0
            )
            straight = pltpu.roll(dot_high(reverse, ring), 0, 1, stride=1, stride_axis=0)
            g_taps[pl.ds(h, 1), :] = jnp.sum(straight, axis=0, keepdims=True)
        g_query[:, lanes] = jnp.concatenate(g_queries, axis=0).T
        return 0

    lax.fori_loop(0, heads // 2, pair, 0)


def contexts_back(queries, v_plain, v_ends, grads, g_ends, land_k, land_out, base_back):
    width, rows = queries.shape
    heads = land_k.shape[0]
    return pl.pallas_call(
        context_back_kernel,
        out_shape=(
            jax.ShapeDtypeStruct((heads, LANDMARKS, LANES), F32),
            jax.ShapeDtypeStruct((rows, width), F32),
            jax.ShapeDtypeStruct((width, rows), F32),
            jax.ShapeDtypeStruct((heads, LANES), F32),
        ),
        in_specs=whole(10),
        out_specs=tuple(whole(4)),
        scratch_shapes=[pltpu.VMEM((2, width, LANES), BF16)],
        compiler_params=PARAMS,
        name="contexts_back",
    )(queries, v_plain, *v_ends, grads, *g_ends, land_k, land_out, base_back)


def third_back_kernel(place, keys, values, land_q, spread, g_land_k, g_conv, g_k, g_v, g_lq):
    heads, _, size = land_q.shape
    rows = keys.shape[1]
    live = live_lanes(place, rows)
    live_row = jnp.where(live, 1.0, 0.0)
    scaled_row = live_row * 64**-0.25
    onehot = landmark_onehot(place, rows, 0)

    def pair(i, _):
        lanes = pl.ds(pl.multiple_of(i * LANES, LANES), LANES)
        g_keys, g_values, g_lqs = [], [], []
        for side in range(2):
            h = 2 * i + side
            at = pl.ds(pl.multiple_of(h * size, size), size)
            key, value = keys[at, :], values[at, :]
            pack = spread[h]
            g_mixed = pack[:, :size]
            row_dot = pack[:, size : size + 1]
            top = pack[:, size + 1 : size + 2]
            total = pack[:, size + 2 : size + 3]
            scores = nn(land_q[h], key)
            third = jnp.where(live, jnp.exp(scores - top), 0.0) * (1.0 / total)
            gm_high, gm_low = split(g_mixed)
            g_third = nn(gm_high, value) + nn(gm_low, value)
            g_high, g_low = split(third * (g_third - row_dot))
            g_lqs.append(nt(g_high, key) + nt(g_low, key))
            turned = land_q[h].T
            glk_high, glk_low = split(g_land_k[h].T)
            g_key = nn(turned, g_high) + nn(turned, g_low)
            g_key = g_key + nn(glk_high, onehot) + nn(glk_low, onehot)
            g_keys.append((scaled_row * g_key).astype(BF16))
            t_high, t_low = split(third)
            gmt_high, gmt_low = split(g_mixed.T)
            g_value = nn(gmt_high, t_high) + nn(gmt_high, t_low) + nn(gmt_low, t_high)
            g_values.append((live_row * (g_value + g_conv[at, :])).astype(BF16))
        g_k[:, lanes] = jnp.concatenate(g_keys, axis=0).T
        g_v[:, lanes] = jnp.concatenate(g_values, axis=0).T
        g_lq[:, lanes] = jnp.concatenate(g_lqs, axis=1)
        return 0

    lax.fori_loop(0, heads // 2, pair, 0)


def third_back(place, keys, values, land_q, spread, g_land_k, g_conv):
    width, rows = keys.shape
    plain = jax.ShapeDtypeStruct((rows, width), BF16)
    return pl.pallas_call(
        third_back_kernel,
        out_shape=(plain, plain, jax.ShapeDtypeStruct((LANDMARKS, width), F32)),
        in_specs=[SCALARS] + whole(6),
        out_specs=tuple(whole(3)),
        compiler_params=PARAMS,
        name="third_back",
    )(place, keys, values, land_q, spread, g_land_k, g_conv)


def query_back_kernel(place, g_first, g_land_q, g_q):
    rows = g_first.shape[0]
    onehot = landmark_onehot(place, rows, 1)
    high, low = split(g_land_q[...])
    position = place[0] + lax.broadcasted_iota(jnp.int32, (rows, 1), 0)
    scaled = jnp.where(position < place[1], 64**-0.25, 0.0)
    g_q[...] = (scaled * (g_first[...] + nn(onehot, high) + nn(onehot, low))).astype(BF16)


def query_back(place, g_first, g_land_q):
    return pl.pallas_call(
        query_back_kernel,
        out_shape=jax.ShapeDtypeStruct(g_first.shape, BF16),
        in_specs=[SCALARS] + whole(2),
        out_specs=whole(1)[0],
        compiler_params=PARAMS,
        name="query_back",
    )(place, g_first, g_land_q)


def centred_rows(rows):
    centred = rows - jnp.mean(rows, axis=1, keepdims=True)
    scale = lax.rsqrt(jnp.mean(centred * centred, axis=1, keepdims=True) + 1e-05)
    return centred * scale, scale


def norm_back(grads, gain, unit, scale):
    scaled = grads * gain
    inner = jnp.mean(scaled * unit, axis=1, keepdims=True)
    return scale * (scaled - jnp.mean(scaled, axis=1, keepdims=True) - unit * inner)


def gelu_pair(hidden):
    share = 0.5 * (1.0 + lax.erf(hidden * 0.7071067811865476))
    density = jnp.exp(-0.5 * hidden * hidden) * 0.3989422804014327
    return hidden * share, share + hidden * density


class Copies:
    def __init__(self, sems):
        self.sems, self.used, self.open = sems, 0, []

    def start(self, source, target):
        copy = pltpu.make_async_copy(source, target, self.sems.at[self.used])
        self.used += 1
        copy.start()
        return copy

    def out(self, source, target):
        self.open.append(self.start(source, target))

    def finish(self):
        for copy in self.open:
            copy.wait()


def each_tile(count, tile, body):
    def step(i, _):
        body(i, pl.ds(pl.multiple_of(i * tile, tile), tile))
        return 0

    lax.fori_loop(0, count // tile, step, 0)


def weight_grad(turned, cells, halves, which, out):
    ff = cells.shape[1] // halves
    columns = ff // 2
    for half in range(halves):
        from_column = pl.ds(pl.multiple_of(half * ff + which * columns, columns), columns)

        def rows_of(i, at, half=half, from_column=from_column):
            out[half, at, :] = nn(turned[at, :], cells[:, from_column]).astype(BF16)

        each_tile(turned.shape[0], 384, rows_of)


def feed_kernel(
    place, context_in, tokens_in, cotangent_in, weights,
    output_to, slope_to, g_fed_to, g_second_to, unit_to, scale_to, turned_to, kept_to, sent_to, norm_grads,
    in_w, down_w, out_w, norms, context, tokens, cotangent,
    low, unit, scales, fed, active, slopes, g_fed, g_fed_turned, normed_turned, output, kept, sent,
    sems,
):
    rows, width = tokens.shape
    halves, _, ff = in_w.shape
    part = out_w.shape[2]
    tile = 256
    copies = Copies(sems)
    early = [
        copies.start(weights.at[:, :, pl.ds(2 * ff, part)], out_w),
        copies.start(context_in, context),
        copies.start(tokens_in, tokens),
        copies.start(weights.at[:, :, pl.ds(2 * ff + part, LANES)], norms),
    ]
    in_copy = copies.start(weights.at[:, :, pl.ds(0, ff)], in_w)
    down_copy = copies.start(weights.at[:, :, pl.ds(ff, ff)], down_w)
    cotangent_copy = copies.start(cotangent_in, cotangent)
    for copy in early:
        copy.wait()
    columns = norms[0].astype(F32).T
    gain0, gain1 = columns[0:1], columns[1:2]
    shift0, shift1 = columns[2:3], columns[3:4]
    norm_grads[...] = jnp.zeros_like(norm_grads)

    def project(i, at):
        attended = nt(context[at, :part], out_w[0])
        for half in range(1, halves):
            attended = attended + nt(context[at, half * part : (half + 1) * part], out_w[half])
        rows_unit, scale = centred_rows(tokens[at, :].astype(F32) + attended)
        unit[at, :] = rows_unit
        scales[at, :] = jnp.broadcast_to(scale, (tile, LANES))
        normed = (rows_unit * gain0 + shift0).astype(BF16)
        low[at, :] = normed
        normed_turned[:, at] = normed.T

    each_tile(rows, tile, project)
    copies.out(unit, unit_to)
    copies.out(scales, scale_to)
    copies.out(normed_turned, turned_to)
    in_copy.wait()
    big = 512

    def hidden_rows(i, at):
        for half in range(halves):
            value, slope = gelu_pair(nn(low[at, :], in_w[half]))
            active[at, half * ff : (half + 1) * ff] = value.astype(BF16)
            slopes[at, half * ff : (half + 1) * ff] = slope.astype(BF16)

    each_tile(rows, tile, hidden_rows)
    copies.out(slopes, slope_to)
    down_copy.wait()

    def fed_rows(i, at):
        total = nt(active[at, :ff], down_w[0])
        for half in range(1, halves):
            total = total + nt(active[at, half * ff : (half + 1) * ff], down_w[half])
        fed[at, :] = total

    each_tile(rows, big, fed_rows)
    cotangent_copy.wait()

    def second_norm(i, at):
        normed = unit[at, :] * gain0 + shift0
        unit1, scale1 = centred_rows(normed + fed[at, :])
        position = place[0] + i * tile + lax.broadcasted_iota(jnp.int32, (tile, 1), 0)
        live = jnp.where(position < place[1], 1.0, 0.0)
        output[at, :] = (live * (unit1 * gain1 + shift1)).astype(BF16)
        grads = live * cotangent[at, :].astype(F32)
        norm_grads[0:1, :] += jnp.sum(grads * unit1, axis=0, keepdims=True)
        norm_grads[1:2, :] += jnp.sum(grads, axis=0, keepdims=True)
        second = norm_back(grads, gain1, unit1, scale1)
        fed[at, :] = second
        g_low = second.astype(BF16)
        g_fed[at, :] = g_low
        g_fed_turned[:, at] = g_low.T

    each_tile(rows, tile, second_norm)
    copies.out(output, output_to)
    copies.out(fed, g_second_to)
    copies.out(g_fed, g_fed_to)

    weight_grad(g_fed_turned, active, halves, 1 - place[2], sent)
    copies.out(sent, sent_to)
    weight_grad(g_fed_turned, active, halves, place[2], kept)
    copies.out(kept, kept_to)
    copies.finish()


ANYWHERE = pl.BlockSpec(memory_space=pl.ANY)


def feed_forward(place, context, tokens, cotangent, weights, ff, part):
    rows, width = tokens.shape
    halves = weights.shape[0]
    grad = (halves, width, ff // 2)
    shapes = [
        ((rows, width), BF16), ((rows, halves * ff), BF16), ((rows, width), BF16),
        ((rows, width), F32), ((rows, width), F32), ((rows, LANES), F32), ((width, rows), BF16),
        (grad, BF16), (grad, BF16), ((8, width), F32),
    ]
    scratch = [
        ((halves, width, ff), BF16), ((halves, width, ff), BF16), ((halves, width, part), BF16),
        ((halves, width, LANES), BF16), ((rows, width), BF16), ((rows, width), BF16),
        ((rows, width), BF16),
        ((rows, width), BF16), ((rows, width), F32), ((rows, LANES), F32), ((rows, width), F32),
        ((rows, halves * ff), BF16), ((rows, halves * ff), BF16), ((rows, width), BF16),
        ((width, rows), BF16), ((width, rows), BF16), ((rows, width), BF16), (grad, BF16),
        (grad, BF16),
    ]
    return pl.pallas_call(
        feed_kernel,
        out_shape=tuple(jax.ShapeDtypeStruct(*shape) for shape in shapes),
        in_specs=[SCALARS] + [ANYWHERE] * 4,
        out_specs=tuple([ANYWHERE] * 9 + whole(1)),
        scratch_shapes=[pltpu.VMEM(*shape) for shape in scratch]
        + [pltpu.SemaphoreType.DMA((16,))],
        compiler_params=PARAMS,
        name="feed_forward",
    )(place, context, tokens, cotangent, weights)


def feed_back_kernel(
    place, slope_in, g_fed_in, g_second_in, unit_in, scale_in, turned_in, context_in, weights,
    g_first_to, g_context_to, kept_to, sent_to, g_out_to, norm_grads,
    in_w, down_w, out_w, norms, g_hidden, g_fed, second, unit, scales, normed_turned, context,
    g_att, g_att_turned, g_context, kept, sent, g_out,
    sems,
):
    rows, width = second.shape
    halves, _, ff = in_w.shape
    part = out_w.shape[2]
    tile = 256
    copies = Copies(sems)
    early = [
        copies.start(g_fed_in, g_fed),
        copies.start(weights.at[:, :, pl.ds(ff, ff)], down_w),
        copies.start(slope_in, g_hidden),
    ]
    later = [
        copies.start(turned_in, normed_turned),
        copies.start(weights.at[:, :, pl.ds(0, ff)], in_w),
        copies.start(g_second_in, second),
        copies.start(unit_in, unit),
        copies.start(scale_in, scales),
        copies.start(weights.at[:, :, pl.ds(2 * ff + part, LANES)], norms),
        copies.start(weights.at[:, :, pl.ds(2 * ff, part)], out_w),
        copies.start(context_in, context),
    ]
    for copy in early:
        copy.wait()
    norm_grads[...] = jnp.zeros_like(norm_grads)
    big = 512

    def back_rows(i, at):
        for half in range(halves):
            g_act = nn(g_fed[at, :], down_w[half])
            to = slice(half * ff, (half + 1) * ff)
            g_hidden[at, to] = (g_act * g_hidden[at, to].astype(F32)).astype(BF16)

    each_tile(rows, big, back_rows)
    later.pop(0).wait()
    weight_grad(normed_turned, g_hidden, halves, 1 - place[2], sent)
    copies.out(sent, sent_to)
    weight_grad(normed_turned, g_hidden, halves, place[2], kept)
    copies.out(kept, kept_to)
    for copy in later:
        copy.wait()
    gain0 = norms[0].astype(F32).T[0:1]

    def normed_rows(i, at):
        total = second[at, :]
        for half in range(halves):
            total = total + nt(g_hidden[at, half * ff : (half + 1) * ff], in_w[half])
        second[at, :] = total

    each_tile(rows, big, normed_rows)

    def first_norm(i, at):
        grads = second[at, :]
        rows_unit, scale = unit[at, :], scales[at, 0:1]
        norm_grads[0:1, :] += jnp.sum(grads * rows_unit, axis=0, keepdims=True)
        norm_grads[1:2, :] += jnp.sum(grads, axis=0, keepdims=True)
        first = norm_back(grads, gain0, rows_unit, scale)
        second[at, :] = first
        low = first.astype(BF16)
        g_att[at, :] = low
        g_att_turned[:, at] = low.T

    each_tile(rows, tile, first_norm)
    copies.out(second, g_first_to)
    for half in range(halves):
        g_context[:, half * part : (half + 1) * part] = nn(g_att[...], out_w[half]).astype(BF16)
    copies.out(g_context, g_context_to)
    for half in range(halves):
        g_out[half] = nn(
            g_att_turned[...], context[:, half * part : (half + 1) * part]
        ).astype(BF16)
    copies.out(g_out, g_out_to)
    copies.finish()


def feed_backward(place, fed, context, weights, ff, part):
    rows, width = context.shape
    halves = weights.shape[0]
    grad = (halves, width, ff // 2)
    shapes = [
        ((rows, width), F32), ((rows, width), BF16), (grad, BF16), (grad, BF16),
        ((halves, width, part), BF16), ((8, width), F32),
    ]
    scratch = [
        ((halves, width, ff), BF16), ((halves, width, ff), BF16), ((halves, width, part), BF16),
        ((halves, width, LANES), BF16), ((rows, halves * ff), BF16), ((rows, width), BF16),
        ((rows, width), F32), ((rows, width), F32),
        ((rows, LANES), F32), ((width, rows), BF16), ((rows, width), BF16),
        ((rows, width), BF16), ((width, rows), BF16), ((rows, width), BF16), (grad, BF16),
        (grad, BF16), ((halves, width, part), BF16),
    ]
    return pl.pallas_call(
        feed_back_kernel,
        out_shape=tuple(jax.ShapeDtypeStruct(*shape) for shape in shapes),
        in_specs=[SCALARS] + [ANYWHERE] * 8,
        out_specs=tuple([ANYWHERE] * 5 + whole(1)),
        scratch_shapes=[pltpu.VMEM(*shape) for shape in scratch]
        + [pltpu.SemaphoreType.DMA((16,))],
        compiler_params=PARAMS,
        name="feed_backward",
    )(place, *fed, context, weights)


def flipped(values, axis, bit):
    count = lax.axis_size(axis)
    return lax.ppermute(values, axis, [(i, i ^ bit) for i in range(count)])


def side_of(axis, bit):
    return (lax.axis_index(axis) // bit) % 2


def paired(mine, axis, bit, dim):
    other = flipped(mine, axis, bit)
    both = jnp.zeros(mine.shape[:dim] + (2,) + mine.shape[dim:], mine.dtype)
    side = side_of(axis, bit)
    both = lax.dynamic_update_slice_in_dim(both, jnp.expand_dims(mine, dim), side, dim)
    return lax.dynamic_update_slice_in_dim(both, jnp.expand_dims(other, dim), 1 - side, dim)


def ctx_bits():
    bits, bit = [], 1
    while bit < lax.axis_size("ctx"):
        bits.append(bit)
        bit *= 2
    return bits


def sequence_sum(values):
    width = values.shape[1] // 2
    side = side_of("ctx", 1)
    kept = lax.dynamic_slice_in_dim(values, side * width, width, axis=1)
    sent = lax.dynamic_slice_in_dim(values, (1 - side) * width, width, axis=1)
    kept = kept + flipped(sent, "ctx", 1)
    kept = kept + flipped(kept, "tp", 1)
    for bit in ctx_bits()[1:]:
        kept = kept + flipped(kept, "ctx", bit)
    other = flipped(kept, "ctx", 1)
    return jnp.where(
        side == 0,
        jnp.concatenate([kept, other], axis=1),
        jnp.concatenate([other, kept], axis=1),
    )


def to_owner(packed, combine):
    kept = packed.reshape((lax.axis_size("ctx"), -1) + packed.shape[1:])
    for bit in ctx_bits():
        view = kept.reshape((kept.shape[0] // 2, 2) + kept.shape[1:])
        side = side_of("ctx", bit)
        sent = lax.dynamic_index_in_dim(view, 1 - side, 1, False)
        kept = lax.dynamic_index_in_dim(view, side, 1, False)
        kept = combine(kept, flipped(sent, "ctx", bit))
    kept = kept[0]
    return combine(kept, flipped(kept, "tp", 1))


def from_owners(part):
    whole_part = part[None]
    for bit in reversed(ctx_bits()):
        both = paired(whole_part, "ctx", bit, 1)
        whole_part = both.reshape((-1,) + part.shape)
    return whole_part.reshape((-1,) + part.shape[1:])


def merge_keys(one, two):
    size = LANES // 2
    one_top, two_top = one[..., size : size + 1], two[..., size : size + 1]
    top = jnp.maximum(one_top, two_top)
    one_factor, two_factor = jnp.exp(one_top - top), jnp.exp(two_top - top)
    summed = one * one_factor + two * two_factor
    lane = lax.broadcasted_iota(jnp.int32, summed.shape, summed.ndim - 1)
    return jnp.where(lane == size, top, summed)


def neighbour_rows(cells, count):
    pieces = lax.axis_size("ctx") * lax.axis_size("tp")
    up = [(i, i + 1) for i in range(pieces - 1)]
    before = lax.ppermute(cells[-count:], ("ctx", "tp"), up)
    after = lax.ppermute(cells[:count], ("ctx", "tp"), [(j, i) for i, j in up])
    return (
        jnp.pad(before, ((LANES - count, 0), (0, 0))),
        jnp.pad(after, ((0, LANES - count), (0, 0))),
    )


def own_quarter(shard):
    rows = shard.shape[0] // lax.axis_size("ctx")
    return lax.dynamic_slice_in_dim(shard, lax.axis_index("ctx") * rows, rows, axis=0)


def gathered(shard):
    full = lax.all_gather(own_quarter(shard), ("tp", "fsdp", "ctx"), tiled=True)
    return full.reshape(lax.axis_size("tp"), -1, shard.shape[1])


def gathered_early(shard):
    count = lax.axis_size("fsdp")
    piece = own_quarter(shard)
    if count > 4:
        held = lax.all_gather(piece, "fsdp")
    else:
        here = lax.axis_index("fsdp")
        held = jnp.zeros((count,) + piece.shape, piece.dtype)
        held = lax.dynamic_update_slice_in_dim(held, piece[None], here, 0)
        for step in range(1, count):
            moved = lax.ppermute(piece, "fsdp", [(i, (i + step) % count) for i in range(count)])
            held = lax.dynamic_update_slice_in_dim(held, moved[None], (here - step) % count, 0)
    bits = ctx_bits()
    halves = []
    for number, half in enumerate((held[: count // 2], held[count // 2 :])):
        half = half[None]
        if number == 0:
            half = paired(half[0], "tp", 1, 0)
        for place, bit in enumerate(reversed(bits[1:])):
            half = paired(half, "ctx", bit, 2 + place)
        if number == 1:
            half = paired(half[0], "tp", 1, 0)
        halves.append(paired(half, "ctx", bits[0], 1 + len(bits)))
    full = jnp.concatenate(halves, axis=1)
    return full.reshape(lax.axis_size("tp"), -1, shard.shape[1])


def bits_of(axis):
    bits, bit = [], lax.axis_size(axis) // 2
    while bit:
        bits.append(bit)
        bit //= 2
    return bits


def scattered(grads, first):
    labels = [(axis, bit) for axis in ("tp", "fsdp", "ctx") for bit in bits_of(axis)]
    order = [("ctx", 1)] + [label for label in labels if label[0] == first]
    order += [label for label in labels if label[0] != "fsdp"] + labels[::-1]
    rows = grads.shape[1] // (lax.axis_size("fsdp") * lax.axis_size("ctx"))
    kept = grads.reshape((2,) * len(labels) + (rows, grads.shape[2]))
    for label in order:
        if label not in labels:
            continue
        dim = labels.index(label)
        labels.pop(dim)
        side = side_of(*label)
        sent = lax.dynamic_index_in_dim(kept, 1 - side, dim, False)
        kept = lax.dynamic_index_in_dim(kept, side, dim, False).astype(F32)
        kept = (kept + flipped(sent, *label).astype(F32)).astype(BF16)
    return from_owners(kept).astype(F32)


def added(one, two):
    return (one.astype(F32) + two.astype(F32)).astype(BF16)


def halved(kept, axis, bit, dim):
    size = kept.shape[dim] // 2
    side = side_of(axis, bit)
    sent = lax.dynamic_slice_in_dim(kept, (1 - side) * size, size, axis=dim)
    kept = lax.dynamic_slice_in_dim(kept, side * size, size, axis=dim)
    return added(kept, flipped(sent, axis, bit))


def over_ctx(kept):
    for bit in ctx_bits()[1:]:
        kept = halved(kept, "ctx", bit, 2)
    return kept


def over_tp(kept):
    return halved(kept, "tp", 1, 0)


def over_fsdp(kept, bits):
    for bit in bits:
        kept = halved(kept, "fsdp", bit, 1)
    return kept


def joined_columns(piece):
    piece = piece[0]
    for bit in ctx_bits()[1:][::-1] + [1]:
        other = flipped(piece, "ctx", bit)
        piece = jnp.where(
            side_of("ctx", bit) == 0,
            jnp.concatenate([piece, other], axis=1),
            jnp.concatenate([other, piece], axis=1),
        )
    return piece.astype(F32)


def gate(*values):
    return lax.optimization_barrier(values)


def dotf(spec, *operands):
    return jnp.einsum(spec, *operands, preferred_element_type=F32)


def taps_round(taps):
    middle = taps.shape[1] // 2
    gap = jnp.zeros((taps.shape[0], LANES - taps.shape[1]), F32)
    return jnp.concatenate([taps[:, middle::-1], gap, taps[:, :middle:-1]], axis=1)


def on_device(
    tokens,
    lengths,
    qk_weight,
    value_weight,
    out_weight,
    in_weight,
    down_weight,
    norm_gains,
    norm_shifts,
    conv_weight,
    cotangent,
):
    tp_count = lax.axis_size("tp")
    tp_index = lax.axis_index("tp")
    ctx_index = lax.axis_index("ctx")
    _, slot_len, model_width = tokens.shape
    rows = slot_len // tp_count
    local_heads, tap_count = conv_weight.shape
    local_width = value_weight.shape[1]
    ff_width = in_weight.shape[1]
    head_size = local_width // local_heads
    heads = local_heads * tp_count
    own_heads = heads // lax.axis_size("ctx")
    width = local_width * tp_count
    radius = tap_count // 2
    length = lengths[0]

    qkv_full = gathered_early(jnp.concatenate([qk_weight[0], qk_weight[1], value_weight], axis=1))
    norm_columns = jnp.concatenate([norm_gains, norm_shifts], axis=0).T
    norm_columns = jnp.pad(norm_columns, ((0, 0), (0, LANES - norm_columns.shape[1])))
    ffn_local = jnp.concatenate([in_weight, down_weight.T, out_weight.T, norm_columns], axis=1)
    ffn_local, qkv_full = lax.optimization_barrier((ffn_local, qkv_full))
    ffn_full = gathered(ffn_local)
    tap_weights = paired(conv_weight, "tp", 1, 0).reshape(heads, tap_count).astype(F32)
    base, base_back = taps_round(tap_weights), taps_round(tap_weights[:, ::-1])

    own = lax.dynamic_slice_in_dim(tokens[0], tp_index * rows, rows, axis=0)
    own_cotangent = lax.dynamic_slice_in_dim(cotangent[0], tp_index * rows, rows, axis=0)
    first_row = (ctx_index * tp_count + tp_index) * rows
    place = jnp.stack([first_row, length, side_of("ctx", 1)]).astype(jnp.int32)

    queries, keys, values, v_plain, sums = projections(place, own, qkv_full)
    v_ends = neighbour_rows(v_plain, radius)
    landmark_ids = jnp.arange(LANDMARKS, dtype=jnp.int32)
    starts = (landmark_ids * length + LANDMARKS - 1) // LANDMARKS
    ends = ((landmark_ids + 1) * length + LANDMARKS - 1) // LANDMARKS
    counts = (ends - starts).astype(F32)[:, None]
    lands = (sequence_sum(sums) / counts).astype(BF16)
    lands = lands.reshape(LANDMARKS, 2, heads, head_size).transpose(1, 2, 0, 3)
    land_q, land_k = lands[0], lands[1]
    own_lands = lax.dynamic_slice_in_dim(lands, ctx_index * own_heads, own_heads, axis=1)
    own_q, own_k = own_lands[0], own_lands[1]

    merged = to_owner(third_parts(place, keys, values, land_q), merge_keys)
    own_out, kept_v, kept_p = inverse_forward(own_q, own_k, merged)
    land_out = from_owners(own_out)
    context = contexts(queries, values, *v_ends, land_k, land_out, base)
    context_parts = context.reshape(rows, tp_count, local_width)

    own_output, *fed, down_kept, down_sent, last_norm = feed_forward(
        place, context, own, own_cotangent, ffn_full, ff_width, local_width
    )
    output = paired(own_output, "tp", 1, 0).reshape(1, slot_len, model_width)
    down = added(down_kept, flipped(down_sent, "ctx", 1))
    grad_first_res, grad_context, in_kept, in_sent, grad_out_t, first_norm = feed_backward(
        place, fed, context, ffn_full, ff_width, local_width
    )
    g_ends = neighbour_rows(grad_context, radius)
    upper = model_width // 2
    in_other = flipped(in_sent, "ctx", 1)
    in_one = added(in_kept[:, :upper], in_other[:, :upper])
    in_two = added(in_kept[:, upper:], in_other[:, upper:])
    grad_context, down, in_one, in_two = gate(grad_context, down, in_one, in_two)
    down, in_one, in_two = over_ctx(down), over_ctx(in_one), over_tp(in_two)

    land_parts, g_query_first, g_value_conv, g_taps = contexts_back(
        queries, v_plain, v_ends, grad_context, g_ends, land_k, land_out, base_back
    )
    own_grads = to_owner(land_parts, jnp.add)
    own_grads, down, in_one, in_two = gate(own_grads, down, in_one, in_two)
    down, in_one, in_two = over_tp(down), over_tp(in_one), over_ctx(in_two)
    spread, land_grads = inverse_backward(own_q, own_k, merged, own_grads, kept_v, kept_p)
    own_lk = jnp.concatenate(
        [land_grads[:, :, :head_size] / counts, jnp.zeros_like(spread[:, :, head_size:])], axis=2
    )
    shared = from_owners(jnp.stack([spread, own_lk], axis=1))
    fsdp_bits = bits_of("fsdp")
    shared, down, in_one, in_two = gate(shared, down, in_one, in_two)
    in_low = side_of("fsdp", fsdp_bits[0]) == 0
    in_both = added(
        jnp.where(in_low, in_one, in_two),
        flipped(jnp.where(in_low, in_two, in_one), "fsdp", fsdp_bits[0]),
    )
    down = over_fsdp(down, fsdp_bits[:1])
    g_k, g_v, g_lq = third_back(
        place, keys, values, land_q, shared[:, 0], shared[:, 1, :, :head_size], g_value_conv
    )
    own_lq = land_grads[:, :, head_size:].transpose(1, 0, 2).reshape(LANDMARKS, -1)
    own_lq = jnp.where(tp_index == 0, own_lq, 0.0)
    own_lq = lax.dynamic_update_slice_in_dim(
        jnp.zeros_like(g_lq), own_lq, ctx_index * own_heads * head_size, axis=1
    )
    g_lq = sequence_sum(g_lq + own_lq) / counts
    g_lq, down, in_both = gate(g_lq, down, in_both)
    grad_down = joined_columns(over_fsdp(down, fsdp_bits[1:])).T
    grad_in = joined_columns(over_fsdp(in_both, fsdp_bits[1:]))
    g_q = query_back(place, g_query_first, g_lq)

    owners = lax.axis_size("fsdp")
    owner_rows = model_width // owners
    taps_grad = jnp.take(
        g_taps, jnp.array([(LANES + radius - 1 - i) % LANES for i in range(tap_count)]), axis=1
    ).reshape(tp_count, -1)
    tap_columns = -(-taps_grad.shape[1] // owner_rows)
    taps_grad = jnp.pad(taps_grad, ((0, 0), (0, tap_columns * owner_rows - taps_grad.shape[1])))
    taps_grad = jnp.tile(taps_grad.reshape(tp_count, owner_rows, tap_columns), (1, owners, 1))
    norm_grads = jnp.stack([first_norm[0], last_norm[0], first_norm[1], last_norm[1]], axis=1)
    small = jnp.concatenate(
        [jnp.broadcast_to(norm_grads[None], (tp_count,) + norm_grads.shape), taps_grad], axis=2
    )
    small = jnp.pad(small, ((0, 0), (0, 0), (0, LANES - small.shape[2])))
    mixed_grads = scattered(jnp.concatenate([grad_out_t, small.astype(BF16)], axis=2), "ctx")
    own_small = mixed_grads[:, local_width:]
    grad_taps = own_small[:, 4 : 4 + tap_columns].reshape(-1)[: local_heads * tap_count]

    g_qkv = jnp.concatenate(
        [cells.reshape(rows, tp_count, local_width) for cells in (g_q, g_k, g_v)], axis=2
    )
    back_terms = dotf("tpk,pck->tc", g_qkv, qkv_full)
    own_grad = (grad_first_res + back_terms).astype(BF16)
    grad_tokens = paired(own_grad, "tp", 1, 0).reshape(1, slot_len, model_width).astype(F32)
    grad_qkv = scattered(dotf("tc,tpk->pck", own, g_qkv).astype(BF16), "ctx")
    return (
        output,
        grad_tokens,
        jnp.stack([grad_qkv[:, :local_width], grad_qkv[:, local_width : 2 * local_width]]),
        grad_qkv[:, 2 * local_width :],
        mixed_grads[:, :local_width].T,
        grad_in,
        grad_down,
        own_small[:, :2].T,
        own_small[:, 2:4].T,
        grad_taps.reshape(local_heads, tap_count),
    )


def solution(mesh):
    in_specs = (
        P("fsdp", "ctx", None),
        P("fsdp"),
        P(None, "fsdp", "tp"),
        P("fsdp", "tp"),
        P("tp", "fsdp"),
        P("fsdp", "tp"),
        P("tp", "fsdp"),
        P(None, "fsdp"),
        P(None, "fsdp"),
        P("tp", None),
        P("fsdp", "ctx", None),
    )
    out_specs = (
        P("fsdp", "ctx", None),
        P("fsdp", "ctx", None),
        P(None, "fsdp", "tp"),
        P("fsdp", "tp"),
        P("tp", "fsdp"),
        P("fsdp", "tp"),
        P("tp", "fsdp"),
        P(None, "fsdp"),
        P(None, "fsdp"),
        P("tp", None),
    )
    return jax.shard_map(
        on_device, mesh=mesh, in_specs=in_specs, out_specs=out_specs, check_vma=False
    )
```

```python
import jax
import jax.numpy as jnp
from jax import lax
from jax.experimental import pallas as pl
from jax.experimental.pallas import tpu as pltpu
from jax.sharding import PartitionSpec as P

LANDMARKS = 64
NEWTON = 6
LANES = 128
VMEM_BYTES = 56 * 2**20

HIGH = lax.Precision.HIGHEST
F32 = jnp.float32
BF16 = jnp.bfloat16


def nn(left, right):
    return jnp.dot(left, right, preferred_element_type=F32)


def nt(left, right):
    return lax.dot_general(left, right, (((1,), (1,)), ((), ())), preferred_element_type=F32)


def split(wide):
    high = wide.astype(BF16)
    return high, (wide - high.astype(F32)).astype(BF16)


def whole(count):
    return [pl.BlockSpec(memory_space=pltpu.VMEM)] * count


SCALARS = pl.BlockSpec(memory_space=pltpu.SMEM)
PARAMS = pltpu.CompilerParams(vmem_limit_bytes=VMEM_BYTES)


def landmark_onehot(place, rows, landmark_axis):
    shape = (LANDMARKS, rows) if landmark_axis == 0 else (rows, LANDMARKS)
    landmark = lax.broadcasted_iota(jnp.int32, shape, landmark_axis)
    position = place[0] + lax.broadcasted_iota(jnp.int32, shape, 1 - landmark_axis)
    start = lax.shift_right_logical(landmark * place[1] + (LANDMARKS - 1), 6)
    end = lax.shift_right_logical((landmark + 1) * place[1] + (LANDMARKS - 1), 6)
    return jnp.where((position >= start) & (position < end), 1.0, 0.0).astype(BF16)


def live_lanes(place, rows):
    position = place[0] + lax.broadcasted_iota(jnp.int32, (1, rows), 1)
    return position < place[1]


def band(base_row):
    ring = pltpu.roll(jnp.broadcast_to(base_row, (LANES, LANES)), 0, 1, stride=1, stride_axis=0)
    gap = lax.broadcasted_iota(jnp.int32, (LANES, LANES), 0) - lax.broadcasted_iota(
        jnp.int32, (LANES, LANES), 1
    )
    zero = jnp.zeros_like(ring)
    before = jnp.where(gap >= LANES - 16, ring, zero).astype(BF16)
    here = jnp.where(jnp.abs(gap) <= 16, ring, zero).astype(BF16)
    after = jnp.where(gap <= 16 - LANES, ring, zero).astype(BF16)
    return before, here, after


def convolved(blocks, bands):
    before, here, after = bands
    return jnp.concatenate(
        [
            nn(blocks[i], before) + nn(blocks[i + 1], here) + nn(blocks[i + 2], after)
            for i in range(len(blocks) - 2)
        ],
        axis=1,
    )


def token_sums_kernel(place, tokens, sums):
    sums[...] = nn(landmark_onehot(place, tokens.shape[0], 0), tokens[...])


def token_sums(place, tokens):
    return pl.pallas_call(
        token_sums_kernel,
        out_shape=jax.ShapeDtypeStruct((LANDMARKS, tokens.shape[1]), F32),
        in_specs=[SCALARS] + whole(1),
        out_specs=whole(1)[0],
        compiler_params=PARAMS,
        name="token_sums",
    )(place, tokens)


def landmark_counts(place):
    landmark = lax.broadcasted_iota(jnp.int32, (LANDMARKS, 1), 0)
    start = lax.shift_right_logical(landmark * place[1] + (LANDMARKS - 1), 6)
    end = lax.shift_right_logical((landmark + 1) * place[1] + (LANDMARKS - 1), 6)
    return (end - start).astype(F32)


def projection_kernel(place, tokens, sums, weights, q_out, k_out, v_out, v_plain, land_q, land_k):
    rows = tokens.shape[0]
    halves, _, packed = weights.shape
    width = packed // 3
    size = land_q.shape[2]
    position = place[0] + lax.broadcasted_iota(jnp.int32, (rows, 1), 0)
    live = jnp.where(position < place[1], 1.0, 0.0)
    scaled = live * 64**-0.25
    means = jnp.concatenate(split(sums[...] / landmark_counts(place)), axis=0)
    cells = tokens[...]
    for half in range(halves):
        for part, out in enumerate((q_out, k_out, v_out)):
            weight = weights[half, :, part * width : (part + 1) * width]
            low = ((live if part == 2 else scaled) * nn(cells, weight)).astype(BF16)
            out[half * width : (half + 1) * width, :] = low.T
            if part == 2:
                v_plain[:, half * width : (half + 1) * width] = low
                continue
            both = nn(means, weight)
            land = (64**-0.25 * (both[:LANDMARKS] + both[LANDMARKS:])).astype(BF16)
            to = land_k if part else land_q
            for head in range(width // size):
                to[half * (width // size) + head] = land[:, head * size : (head + 1) * size]


def projections(place, tokens, sums, weights, size):
    rows = tokens.shape[0]
    width = weights.shape[0] * weights.shape[2] // 3
    turned = jax.ShapeDtypeStruct((width, rows), BF16)
    land = jax.ShapeDtypeStruct((width // size, LANDMARKS, size), BF16)
    return pl.pallas_call(
        projection_kernel,
        out_shape=(turned, turned, turned, jax.ShapeDtypeStruct((rows, width), BF16), land, land),
        in_specs=[SCALARS] + whole(3),
        out_specs=tuple(whole(6)),
        compiler_params=PARAMS,
        name="projections",
    )(place, tokens, sums, weights)


def by_owner(place, h, owners, kept, sent, values):
    per = kept.shape[1]
    for owner in range(owners):
        @pl.when((h >= owner * per) & (h < (owner + 1) * per))
        def _(owner=owner):
            mine = place[2] == owner % 2

            @pl.when(mine)
            def _():
                kept[owner // 2, h - owner * per] = values

            @pl.when(jnp.logical_not(mine))
            def _():
                sent[owner // 2, h - owner * per] = values


def third_kernel(place, keys, values, land_q, kept, sent):
    heads = land_q.shape[0]
    size = land_q.shape[2]
    rows = keys.shape[1]
    owners = 2 * kept.shape[0]
    live = live_lanes(place, rows)

    def head(h):
        at = pl.ds(pl.multiple_of(h * size, size), size)
        scores = jnp.where(live, nn(land_q[h], keys[at, :]), -1e30)
        top = jnp.max(scores, axis=1, keepdims=True)
        raised = jnp.where(live, jnp.exp(scores - top), 0.0)
        total = jnp.sum(raised, axis=1, keepdims=True)
        high, low = split(raised)
        value = values[at, :]
        mixed = nt(high, value) + nt(low, value)
        lane = lax.broadcasted_iota(jnp.int32, (LANDMARKS, LANES - size), 1)
        stats = jnp.where(lane == 0, top, jnp.where(lane == 1, total, 0.0))
        by_owner(place, h, owners, kept, sent, jnp.concatenate([mixed, stats], axis=1))

    def pair(i, _):
        head(2 * i)
        head(2 * i + 1)
        return 0

    lax.fori_loop(0, heads // 2, pair, 0)


def owner_parts(heads, owners):
    part = jax.ShapeDtypeStruct((owners // 2, heads // owners, LANDMARKS, LANES), F32)
    return part, part


def third_parts(place, keys, values, land_q, owners):
    return pl.pallas_call(
        third_kernel,
        out_shape=owner_parts(land_q.shape[0], owners),
        in_specs=[SCALARS] + whole(3),
        out_specs=tuple(whole(2)),
        compiler_params=PARAMS,
        name="third_parts",
    )(place, keys, values, land_q)


def dot_high(left, right):
    return jnp.dot(left, right, preferred_element_type=F32, precision=HIGH)


def dot_high_nt(left, right):
    return lax.dot_general(
        left, right, (((1,), (1,)), ((), ())), preferred_element_type=F32, precision=HIGH
    )


def eye():
    row = lax.broadcasted_iota(jnp.int32, (LANDMARKS, LANDMARKS), 0)
    column = lax.broadcasted_iota(jnp.int32, (LANDMARKS, LANDMARKS), 1)
    return jnp.where(row == column, 1.0, 0.0)


def middle_map(land_q, land_k):
    scores = nt(land_q, land_k)
    raised = jnp.exp(scores - jnp.max(scores, axis=1, keepdims=True))
    return raised / jnp.sum(raised, axis=1, keepdims=True)


def inverse_kernel(place, land_q, land_k, kept_v, kept_p):
    heads = range(kept_v.shape[1])
    one = eye()
    own = [place[3] * len(heads) + h for h in heads]
    middle = [middle_map(land_q[h], land_k[h]) for h in own]
    approx = [m.T / jnp.sum(m * m, keepdims=True) for m in middle]
    for turn in range(NEWTON):
        product = [dot_high(middle[h], approx[h]) for h in heads]
        for h in heads:
            kept_v[turn, h] = approx[h]
            kept_p[turn, h] = product[h]
        bracket = [7.0 * one - p for p in product]
        bracket = [15.0 * one - dot_high(product[h], bracket[h]) for h in heads]
        bracket = [13.0 * one - dot_high(product[h], bracket[h]) for h in heads]
        approx = [0.25 * dot_high(approx[h], bracket[h]) for h in heads]
    for h in heads:
        kept_v[NEWTON, h] = approx[h]


def inverse_forward(place, land_q, land_k, owners):
    heads = land_q.shape[0] // owners
    square = (heads, LANDMARKS, LANDMARKS)
    return pl.pallas_call(
        inverse_kernel,
        out_shape=(
            jax.ShapeDtypeStruct((NEWTON + 1,) + square, F32),
            jax.ShapeDtypeStruct((NEWTON,) + square, F32),
        ),
        in_specs=[SCALARS] + whole(2),
        out_specs=tuple(whole(2)),
        compiler_params=PARAMS,
        name="inverse_forward",
    )(place, land_q, land_k)


def merged_keys(one, two, size):
    one_top, two_top = one[:, size : size + 1], two[:, size : size + 1]
    top = jnp.maximum(one_top, two_top)
    summed = one * jnp.exp(one_top - top) + two * jnp.exp(two_top - top)
    lane = lax.broadcasted_iota(jnp.int32, one.shape, 1)
    return jnp.where(lane == size, top, summed)


def land_out_kernel(one, two, kept_v, merged, land_out):
    size = land_out.shape[2]
    for h in range(one.shape[0]):
        both = merged_keys(one[h], two[h], size)
        merged[h] = both
        mixed = both[:, :size] / both[:, size + 1 : size + 2]
        land_out[h] = dot_high(kept_v[NEWTON, h], mixed).astype(BF16)


def landmark_out(one, two, kept_v):
    heads = one.shape[0]
    return pl.pallas_call(
        land_out_kernel,
        out_shape=(
            jax.ShapeDtypeStruct(one.shape, F32),
            jax.ShapeDtypeStruct((heads, LANDMARKS, LANES // 2), BF16),
        ),
        in_specs=whole(3),
        out_specs=tuple(whole(2)),
        compiler_params=PARAMS,
        name="landmark_out",
    )(one, two, kept_v)


def inverse_back_kernel(
    place, land_q, land_k, merged, grads, kept_v, kept_p, spread, g_lq, g_lk
):
    heads = range(grads.shape[0])
    size = land_q.shape[2]
    one = eye()
    own = [place[3] * len(heads) + h for h in heads]
    middle = [middle_map(land_q[h], land_k[h]) for h in own]
    turned = [m.T for m in middle]
    g_approx = []
    for h in heads:
        mixed = merged[h][:, :size] / merged[h][:, size + 1 : size + 2]
        g_land = grads[h][:, :size]
        g_approx.append(dot_high_nt(g_land, mixed))
        g_mixed = dot_high(kept_v[NEWTON, h].T, g_land)
        row_dot = jnp.sum(g_mixed * mixed, axis=1, keepdims=True)
        lane = lax.broadcasted_iota(jnp.int32, (LANDMARKS, LANES - size), 1)
        top = merged[h][:, size : size + 1]
        total = merged[h][:, size + 1 : size + 2]
        stats = jnp.where(
            lane == 0, row_dot, jnp.where(lane == 1, top, jnp.where(lane == 2, total, 0.0))
        )
        spread[h] = jnp.concatenate([g_mixed, stats], axis=1)
    g_middle = [jnp.zeros((LANDMARKS, LANDMARKS), F32) for _ in heads]
    for turn in reversed(range(NEWTON)):
        approx = [kept_v[turn, h] for h in heads]
        product = [kept_p[turn, h] for h in heads]
        first = [7.0 * one - p for p in product]
        second = [15.0 * one - dot_high(product[h], first[h]) for h in heads]
        third = [13.0 * one - dot_high(product[h], second[h]) for h in heads]
        g_third = [0.25 * dot_high(approx[h].T, g_approx[h]) for h in heads]
        g_back = [0.25 * dot_high_nt(g_approx[h], third[h]) for h in heads]
        g_product = [-dot_high_nt(g_third[h], second[h]) for h in heads]
        pt = [p.T for p in product]
        g_second = [-dot_high(pt[h], g_third[h]) for h in heads]
        g_product = [g_product[h] - dot_high_nt(g_second[h], first[h]) for h in heads]
        g_product = [g_product[h] + dot_high(pt[h], g_second[h]) for h in heads]
        g_middle = [g_middle[h] + dot_high_nt(g_product[h], approx[h]) for h in heads]
        g_approx = [g_back[h] + dot_high(turned[h], g_product[h]) for h in heads]
    for h in heads:
        m = middle[h]
        size_sum = jnp.sum(m * m, keepdims=True)
        g_size = -jnp.sum(g_approx[h] * turned[h], keepdims=True) / (size_sum * size_sum)
        g_m = g_middle[h] + g_approx[h].T / size_sum + 2.0 * g_size * m
        g_scores = m * (g_m - jnp.sum(g_m * m, axis=1, keepdims=True))
        g_lq[h] = dot_high(g_scores, land_k[own[h]].astype(F32))
        g_lk[h] = dot_high(g_scores.T, land_q[own[h]].astype(F32))


def inverse_backward(place, land_q, land_k, merged, grads, kept_v, kept_p):
    heads = grads.shape[0]
    square = jax.ShapeDtypeStruct((heads,) + land_q.shape[1:], F32)
    return pl.pallas_call(
        inverse_back_kernel,
        out_shape=(jax.ShapeDtypeStruct((heads, LANDMARKS, LANES), F32), square, square),
        in_specs=[SCALARS] + whole(6),
        out_specs=tuple(whole(3)),
        compiler_params=PARAMS,
        name="inverse_backward",
    )(place, land_q, land_k, merged, grads, kept_v, kept_p)


def first_map(land_k, queries):
    scores = nn(land_k, queries)
    raised = jnp.exp(scores - jnp.max(scores, axis=0, keepdims=True))
    return raised * (1.0 / jnp.sum(raised, axis=0, keepdims=True))


def head_blocks(cells, ends, at):
    rows = cells.shape[1]
    left, right = ends
    return (
        [left[at, :]]
        + [cells[at, i * LANES : (i + 1) * LANES] for i in range(rows // LANES)]
        + [right[at, :]]
    )


def first_conv_kernel(queries, values, left, right, land_k, base, first, conv, ends):
    heads, _, size = land_k.shape
    ends[0] = left[...].T
    ends[1] = right[...].T

    def head(h):
        at = pl.ds(pl.multiple_of(h * size, size), size)
        first[at, :] = first_map(land_k[h], queries[at, :]).astype(BF16)
        blocks = head_blocks(values, (ends.at[0], ends.at[1]), at)
        conv[at, :] = convolved(blocks, band(base[pl.ds(h, 1), :]))

    def pair(i, _):
        head(2 * i)
        head(2 * i + 1)
        return 0

    lax.fori_loop(0, heads // 2, pair, 0)


def first_and_conv(queries, values, left, right, land_k, base):
    width, rows = queries.shape
    return pl.pallas_call(
        first_conv_kernel,
        out_shape=(
            jax.ShapeDtypeStruct((width, rows), BF16),
            jax.ShapeDtypeStruct((width, rows), F32),
        ),
        in_specs=whole(6),
        out_specs=tuple(whole(2)),
        scratch_shapes=[pltpu.VMEM((2, width, LANES), BF16)],
        compiler_params=PARAMS,
        name="first_and_conv",
    )(queries, values, left, right, land_k, base)


def context_kernel(first, conv, land_out, context):
    heads, _, size = land_out.shape

    def head(h):
        at = pl.ds(pl.multiple_of(h * size, size), size)
        return (nn(land_out[h].T, first[at, :]) + conv[at, :]).astype(BF16)

    def pair(i, _):
        both = jnp.concatenate([head(2 * i), head(2 * i + 1)], axis=0)
        context[:, pl.ds(pl.multiple_of(i * LANES, LANES), LANES)] = both.T
        return 0

    lax.fori_loop(0, heads // 2, pair, 0)


def contexts(first, conv, land_out):
    width, rows = first.shape
    return pl.pallas_call(
        context_kernel,
        out_shape=jax.ShapeDtypeStruct((rows, width), BF16),
        in_specs=whole(3),
        out_specs=whole(1)[0],
        compiler_params=PARAMS,
        name="contexts",
    )(first, conv, land_out)


def attention_back_kernel(
    place, queries, grads, land_k, land_out, kept, sent, g_lk, g_query
):
    heads, _, size = land_k.shape
    rows = queries.shape[1]
    owners = 2 * kept.shape[0]
    scaled = jnp.where(live_lanes(place, rows), 64**-0.25, 0.0)

    def pair(i, _):
        lanes = pl.ds(pl.multiple_of(i * LANES, LANES), LANES)
        turned = grads[:, lanes].T
        g_queries, g_keys = [], []
        for side in range(2):
            h = 2 * i + side
            query = queries[pl.ds(pl.multiple_of(h * size, size), size), :]
            g_context = turned[side * size : (side + 1) * size]
            first = first_map(land_k[h], query)
            g_first = nn(land_out[h], g_context)
            inner = jnp.sum(g_first * first, axis=0, keepdims=True)
            g_scores = (first * (g_first - inner)).astype(BF16)
            g_land = nt(first.astype(BF16), g_context)
            g_key = nt(g_scores, query)
            by_owner(place, h, owners, kept, sent, jnp.concatenate([g_land, g_key], axis=1))
            g_keys.append(g_key)
            g_queries.append((scaled * nn(land_k[h].T, g_scores)).astype(BF16))
        g_query[:, lanes] = jnp.concatenate(g_queries, axis=0).T
        g_lk[:, lanes] = jnp.concatenate(g_keys, axis=1)
        return 0

    lax.fori_loop(0, heads // 2, pair, 0)


def attention_back(place, queries, grads, land_k, land_out, owners):
    width, rows = queries.shape
    heads = land_k.shape[0]
    return pl.pallas_call(
        attention_back_kernel,
        out_shape=owner_parts(heads, owners)
        + (
            jax.ShapeDtypeStruct((LANDMARKS, width), F32),
            jax.ShapeDtypeStruct((rows, width), BF16),
        ),
        in_specs=[SCALARS] + whole(4),
        out_specs=tuple(whole(4)),
        compiler_params=PARAMS,
        name="attention_back",
    )(place, queries, grads, land_k, land_out)


def conv_back_kernel(
    v_plain, v_left, v_right, grads, g_left, g_right, base_back, g_value, g_taps, ends
):
    heads = g_taps.shape[0]
    rows, width = grads.shape
    size = width // heads
    blocks_in = rows // LANES
    row = lax.broadcasted_iota(jnp.int32, (LANES, LANES), 0)
    column = lax.broadcasted_iota(jnp.int32, (LANES, LANES), 1)
    reverse = jnp.where(row + column == LANES - 1, 1.0, 0.0)
    gap = row - column
    ends[0] = g_left[...].T
    ends[1] = g_right[...].T

    def pair(i, _):
        lanes = pl.ds(pl.multiple_of(i * LANES, LANES), LANES)
        turned = grads[:, lanes].T
        plain = [v_left[LANES - 16 :, lanes]]
        plain += [v_plain[b * LANES : (b + 1) * LANES, lanes] for b in range(blocks_in)]
        plain += [v_right[:16, lanes]]
        for side in range(2):
            h = 2 * i + side
            at = pl.ds(pl.multiple_of(h * size, size), size)
            g_context = turned[side * size : (side + 1) * size]
            blocks = [ends[0, at, :]]
            blocks += [g_context[:, b * LANES : (b + 1) * LANES] for b in range(blocks_in)]
            blocks += [ends[1, at, :]]
            g_value[at, :] = convolved(blocks, band(base_back[pl.ds(h, 1), :]))
            own = (row >= size) == (side == 1)
            here = jnp.zeros((LANES, LANES), F32)
            before = jnp.zeros((16, LANES), F32)
            after = jnp.zeros((16, LANES), F32)
            for b in range(blocks_in):
                piece = turned[:, b * LANES : (b + 1) * LANES]
                masked = jnp.where(own, piece, jnp.zeros_like(piece))
                prior = plain[0] if b == 0 else plain[b][LANES - 16 :]
                later = plain[b + 2][:16]
                here = here + nn(plain[b + 1], masked)
                before = before + nn(prior, masked)
                after = after + nn(later, masked)
            empty = jnp.zeros((LANES - 16, LANES), F32)
            ring = jnp.where(jnp.abs(gap) <= 16, here, 0.0)
            ring = ring + jnp.where(
                gap >= LANES - 16, jnp.concatenate([empty, before], axis=0), 0.0
            )
            ring = ring + jnp.where(
                gap <= 16 - LANES, jnp.concatenate([after, empty], axis=0), 0.0
            )
            straight = pltpu.roll(dot_high(reverse, ring), 0, 1, stride=1, stride_axis=0)
            g_taps[pl.ds(h, 1), :] = jnp.sum(straight, axis=0, keepdims=True)
        return 0

    lax.fori_loop(0, heads // 2, pair, 0)


def conv_back(v_plain, v_ends, grads, g_ends, base_back):
    rows, width = grads.shape
    heads = base_back.shape[0]
    return pl.pallas_call(
        conv_back_kernel,
        out_shape=(
            jax.ShapeDtypeStruct((width, rows), F32),
            jax.ShapeDtypeStruct((heads, LANES), F32),
        ),
        in_specs=whole(7),
        out_specs=tuple(whole(2)),
        scratch_shapes=[pltpu.VMEM((2, width, LANES), BF16)],
        compiler_params=PARAMS,
        name="conv_back",
    )(v_plain, *v_ends, grads, *g_ends, base_back)


def third_back_kernel(place, keys, values, land_q, spread, g_conv, g_k, g_v, g_lq):
    heads, _, size = land_q.shape
    rows = keys.shape[1]
    live = live_lanes(place, rows)
    live_row = jnp.where(live, 1.0, 0.0)
    scaled_row = live_row * 64**-0.25

    def pair(i, _):
        lanes = pl.ds(pl.multiple_of(i * LANES, LANES), LANES)
        g_keys, g_values, g_lqs = [], [], []
        for side in range(2):
            h = 2 * i + side
            at = pl.ds(pl.multiple_of(h * size, size), size)
            key, value = keys[at, :], values[at, :]
            pack = spread[h]
            g_mixed = pack[:, :size]
            row_dot = pack[:, size : size + 1]
            top = pack[:, size + 1 : size + 2]
            total = pack[:, size + 2 : size + 3]
            scores = nn(land_q[h], key)
            third = jnp.where(live, jnp.exp(scores - top), 0.0) * (1.0 / total)
            gm_high, gm_low = split(g_mixed)
            g_third = nn(gm_high, value) + nn(gm_low, value)
            g_high, g_low = split(third * (g_third - row_dot))
            g_lqs.append(nt(g_high, key) + nt(g_low, key))
            turned = land_q[h].T
            g_key = nn(turned, g_high) + nn(turned, g_low)
            g_keys.append((scaled_row * g_key).astype(BF16))
            t_high, t_low = split(third)
            gmt_high, gmt_low = split(g_mixed.T)
            g_value = nn(gmt_high, t_high) + nn(gmt_high, t_low) + nn(gmt_low, t_high)
            g_values.append((live_row * (g_value + g_conv[at, :])).astype(BF16))
        g_k[:, lanes] = jnp.concatenate(g_keys, axis=0).T
        g_v[:, lanes] = jnp.concatenate(g_values, axis=0).T
        g_lq[:, lanes] = jnp.concatenate(g_lqs, axis=1)
        return 0

    lax.fori_loop(0, heads // 2, pair, 0)


def third_back(place, keys, values, land_q, spread, g_conv):
    width, rows = keys.shape
    plain = jax.ShapeDtypeStruct((rows, width), BF16)
    return pl.pallas_call(
        third_back_kernel,
        out_shape=(plain, plain, jax.ShapeDtypeStruct((LANDMARKS, width), F32)),
        in_specs=[SCALARS] + whole(5),
        out_specs=tuple(whole(3)),
        compiler_params=PARAMS,
        name="third_back",
    )(place, keys, values, land_q, spread, g_conv)


def centred_rows(rows):
    centred = rows - jnp.mean(rows, axis=1, keepdims=True)
    scale = lax.rsqrt(jnp.mean(centred * centred, axis=1, keepdims=True) + 1e-05)
    return centred * scale, scale


def norm_back(grads, gain, unit, scale):
    scaled = grads * gain
    inner = jnp.mean(scaled * unit, axis=1, keepdims=True)
    return scale * (scaled - jnp.mean(scaled, axis=1, keepdims=True) - unit * inner)


def gelu_pair(hidden):
    share = 0.5 * (1.0 + lax.erf(hidden * 0.7071067811865476))
    density = jnp.exp(-0.5 * hidden * hidden) * 0.3989422804014327
    return hidden * share, share + hidden * density


class Copies:
    def __init__(self, sems):
        self.sems, self.used, self.open = sems, 0, []

    def start(self, source, target):
        copy = pltpu.make_async_copy(source, target, self.sems.at[self.used])
        self.used += 1
        copy.start()
        return copy

    def out(self, source, target):
        self.open.append(self.start(source, target))

    def finish(self):
        for copy in self.open:
            copy.wait()


def each_tile(count, tile, body):
    def step(i, _):
        body(i, pl.ds(pl.multiple_of(i * tile, tile), tile))
        return 0

    lax.fori_loop(0, count // tile, step, 0)


def weight_grad(turned, cells, halves, which, out):
    ff = cells.shape[1] // halves
    columns = ff // 2
    for half in range(halves):
        from_column = pl.ds(pl.multiple_of(half * ff + which * columns, columns), columns)

        def rows_of(i, at, half=half, from_column=from_column):
            out[half, at, :] = nn(turned[at, :], cells[:, from_column]).astype(BF16)

        each_tile(turned.shape[0], 384, rows_of)


def feed_kernel(
    place, context_in, tokens_in, cotangent_in, weights,
    output_to, slope_to, g_fed_to, g_second_to, unit_to, scale_to, turned_to, kept_to, sent_to, norm_grads,
    in_w, down_w, out_w, norms, context, tokens, cotangent,
    low, unit, scales, fed, active, slopes, g_fed, g_fed_turned, normed_turned, output, kept, sent,
    sems,
):
    rows, width = tokens.shape
    halves, _, ff = in_w.shape
    part = out_w.shape[2]
    tile = 256
    copies = Copies(sems)
    early = [
        copies.start(weights.at[:, :, pl.ds(2 * ff, part)], out_w),
        copies.start(context_in, context),
        copies.start(tokens_in, tokens),
        copies.start(weights.at[:, :, pl.ds(2 * ff + part, LANES)], norms),
    ]
    in_copy = copies.start(weights.at[:, :, pl.ds(0, ff)], in_w)
    down_copy = copies.start(weights.at[:, :, pl.ds(ff, ff)], down_w)
    cotangent_copy = copies.start(cotangent_in, cotangent)
    for copy in early:
        copy.wait()
    columns = norms[0].astype(F32).T
    gain0, gain1 = columns[0:1], columns[1:2]
    shift0, shift1 = columns[2:3], columns[3:4]
    norm_grads[...] = jnp.zeros_like(norm_grads)

    def project(i, at):
        attended = nt(context[at, :part], out_w[0])
        for half in range(1, halves):
            attended = attended + nt(context[at, half * part : (half + 1) * part], out_w[half])
        rows_unit, scale = centred_rows(tokens[at, :].astype(F32) + attended)
        unit[at, :] = rows_unit
        scales[at, :] = jnp.broadcast_to(scale, (tile, LANES))
        normed = (rows_unit * gain0 + shift0).astype(BF16)
        low[at, :] = normed
        normed_turned[:, at] = normed.T

    each_tile(rows, tile, project)
    copies.out(unit, unit_to)
    copies.out(scales, scale_to)
    copies.out(normed_turned, turned_to)
    in_copy.wait()
    big = 512

    def hidden_rows(i, at):
        for half in range(halves):
            value, slope = gelu_pair(nn(low[at, :], in_w[half]))
            active[at, half * ff : (half + 1) * ff] = value.astype(BF16)
            slopes[at, half * ff : (half + 1) * ff] = slope.astype(BF16)

    each_tile(rows, tile, hidden_rows)
    copies.out(slopes, slope_to)
    down_copy.wait()

    def fed_rows(i, at):
        total = nt(active[at, :ff], down_w[0])
        for half in range(1, halves):
            total = total + nt(active[at, half * ff : (half + 1) * ff], down_w[half])
        fed[at, :] = total

    each_tile(rows, big, fed_rows)
    cotangent_copy.wait()

    def second_norm(i, at):
        normed = unit[at, :] * gain0 + shift0
        unit1, scale1 = centred_rows(normed + fed[at, :])
        position = place[0] + i * tile + lax.broadcasted_iota(jnp.int32, (tile, 1), 0)
        live = jnp.where(position < place[1], 1.0, 0.0)
        output[at, :] = (live * (unit1 * gain1 + shift1)).astype(BF16)
        grads = live * cotangent[at, :].astype(F32)
        norm_grads[0:1, :] += jnp.sum(grads * unit1, axis=0, keepdims=True)
        norm_grads[1:2, :] += jnp.sum(grads, axis=0, keepdims=True)
        second = norm_back(grads, gain1, unit1, scale1)
        fed[at, :] = second
        g_low = second.astype(BF16)
        g_fed[at, :] = g_low
        g_fed_turned[:, at] = g_low.T

    each_tile(rows, tile, second_norm)
    copies.out(output, output_to)
    copies.out(fed, g_second_to)
    copies.out(g_fed, g_fed_to)

    weight_grad(g_fed_turned, active, halves, 1 - place[2], sent)
    copies.out(sent, sent_to)
    weight_grad(g_fed_turned, active, halves, place[2], kept)
    copies.out(kept, kept_to)
    copies.finish()


ANYWHERE = pl.BlockSpec(memory_space=pl.ANY)


def feed_forward(place, context, tokens, cotangent, weights, ff, part):
    rows, width = tokens.shape
    halves = weights.shape[0]
    grad = (halves, width, ff // 2)
    shapes = [
        ((rows, width), BF16), ((rows, halves * ff), BF16), ((rows, width), BF16),
        ((rows, width), F32), ((rows, width), F32), ((rows, LANES), F32), ((width, rows), BF16),
        (grad, BF16), (grad, BF16), ((8, width), F32),
    ]
    scratch = [
        ((halves, width, ff), BF16), ((halves, width, ff), BF16), ((halves, width, part), BF16),
        ((halves, width, LANES), BF16), ((rows, width), BF16), ((rows, width), BF16),
        ((rows, width), BF16),
        ((rows, width), BF16), ((rows, width), F32), ((rows, LANES), F32), ((rows, width), F32),
        ((rows, halves * ff), BF16), ((rows, halves * ff), BF16), ((rows, width), BF16),
        ((width, rows), BF16), ((width, rows), BF16), ((rows, width), BF16), (grad, BF16),
        (grad, BF16),
    ]
    return pl.pallas_call(
        feed_kernel,
        out_shape=tuple(jax.ShapeDtypeStruct(*shape) for shape in shapes),
        in_specs=[SCALARS] + [ANYWHERE] * 4,
        out_specs=tuple([ANYWHERE] * 9 + whole(1)),
        scratch_shapes=[pltpu.VMEM(*shape) for shape in scratch]
        + [pltpu.SemaphoreType.DMA((16,))],
        compiler_params=PARAMS,
        name="feed_forward",
    )(place, context, tokens, cotangent, weights)


def feed_back_kernel(
    place, slope_in, g_fed_in, g_second_in, unit_in, scale_in, turned_in, context_in, weights,
    g_first_to, g_context_to, kept_to, sent_to, g_out_to, norm_grads,
    in_w, down_w, out_w, norms, g_hidden, g_fed, second, unit, scales, normed_turned, context,
    g_att, g_att_turned, g_context, kept, sent, g_out,
    sems,
):
    rows, width = second.shape
    halves, _, ff = in_w.shape
    part = out_w.shape[2]
    tile = 256
    copies = Copies(sems)
    early = [
        copies.start(g_fed_in, g_fed),
        copies.start(weights.at[:, :, pl.ds(ff, ff)], down_w),
        copies.start(slope_in, g_hidden),
    ]
    later = [
        copies.start(turned_in, normed_turned),
        copies.start(weights.at[:, :, pl.ds(0, ff)], in_w),
        copies.start(g_second_in, second),
        copies.start(unit_in, unit),
        copies.start(scale_in, scales),
        copies.start(weights.at[:, :, pl.ds(2 * ff + part, LANES)], norms),
        copies.start(weights.at[:, :, pl.ds(2 * ff, part)], out_w),
        copies.start(context_in, context),
    ]
    for copy in early:
        copy.wait()
    norm_grads[...] = jnp.zeros_like(norm_grads)
    big = 512

    def back_rows(i, at):
        for half in range(halves):
            g_act = nn(g_fed[at, :], down_w[half])
            to = slice(half * ff, (half + 1) * ff)
            g_hidden[at, to] = (g_act * g_hidden[at, to].astype(F32)).astype(BF16)

    each_tile(rows, big, back_rows)
    later.pop(0).wait()
    weight_grad(normed_turned, g_hidden, halves, 1 - place[2], sent)
    copies.out(sent, sent_to)
    weight_grad(normed_turned, g_hidden, halves, place[2], kept)
    copies.out(kept, kept_to)
    for copy in later:
        copy.wait()
    gain0 = norms[0].astype(F32).T[0:1]

    def normed_rows(i, at):
        total = second[at, :]
        for half in range(halves):
            total = total + nt(g_hidden[at, half * ff : (half + 1) * ff], in_w[half])
        second[at, :] = total

    each_tile(rows, big, normed_rows)

    def first_norm(i, at):
        grads = second[at, :]
        rows_unit, scale = unit[at, :], scales[at, 0:1]
        norm_grads[0:1, :] += jnp.sum(grads * rows_unit, axis=0, keepdims=True)
        norm_grads[1:2, :] += jnp.sum(grads, axis=0, keepdims=True)
        first = norm_back(grads, gain0, rows_unit, scale)
        second[at, :] = first
        low = first.astype(BF16)
        g_att[at, :] = low
        g_att_turned[:, at] = low.T

    each_tile(rows, tile, first_norm)
    copies.out(second, g_first_to)
    for half in range(halves):
        g_context[:, half * part : (half + 1) * part] = nn(g_att[...], out_w[half]).astype(BF16)
    copies.out(g_context, g_context_to)
    for half in range(halves):
        g_out[half] = nn(
            g_att_turned[...], context[:, half * part : (half + 1) * part]
        ).astype(BF16)
    copies.out(g_out, g_out_to)
    copies.finish()


def feed_backward(place, fed, context, weights, ff, part):
    rows, width = context.shape
    halves = weights.shape[0]
    grad = (halves, width, ff // 2)
    shapes = [
        ((rows, width), F32), ((rows, width), BF16), (grad, BF16), (grad, BF16),
        ((halves, width, part), BF16), ((8, width), F32),
    ]
    scratch = [
        ((halves, width, ff), BF16), ((halves, width, ff), BF16), ((halves, width, part), BF16),
        ((halves, width, LANES), BF16), ((rows, halves * ff), BF16), ((rows, width), BF16),
        ((rows, width), F32), ((rows, width), F32),
        ((rows, LANES), F32), ((width, rows), BF16), ((rows, width), BF16),
        ((rows, width), BF16), ((width, rows), BF16), ((rows, width), BF16), (grad, BF16),
        (grad, BF16), ((halves, width, part), BF16),
    ]
    return pl.pallas_call(
        feed_back_kernel,
        out_shape=tuple(jax.ShapeDtypeStruct(*shape) for shape in shapes),
        in_specs=[SCALARS] + [ANYWHERE] * 8,
        out_specs=tuple([ANYWHERE] * 5 + whole(1)),
        scratch_shapes=[pltpu.VMEM(*shape) for shape in scratch]
        + [pltpu.SemaphoreType.DMA((16,))],
        compiler_params=PARAMS,
        name="feed_backward",
    )(place, *fed, context, weights)


def flipped(values, axis, bit):
    count = lax.axis_size(axis)
    return lax.ppermute(values, axis, [(i, i ^ bit) for i in range(count)])


def side_of(axis, bit):
    return (lax.axis_index(axis) // bit) % 2


def paired(mine, axis, bit, dim):
    other = flipped(mine, axis, bit)
    both = jnp.zeros(mine.shape[:dim] + (2,) + mine.shape[dim:], mine.dtype)
    side = side_of(axis, bit)
    both = lax.dynamic_update_slice_in_dim(both, jnp.expand_dims(mine, dim), side, dim)
    return lax.dynamic_update_slice_in_dim(both, jnp.expand_dims(other, dim), 1 - side, dim)


def ctx_bits():
    bits, bit = [], 1
    while bit < lax.axis_size("ctx"):
        bits.append(bit)
        bit *= 2
    return bits


def sequence_sum(values):
    width = values.shape[1] // 2
    side = side_of("ctx", 1)
    kept = lax.dynamic_slice_in_dim(values, side * width, width, axis=1)
    sent = lax.dynamic_slice_in_dim(values, (1 - side) * width, width, axis=1)
    kept = kept + flipped(sent, "ctx", 1)
    kept = kept + flipped(kept, "tp", 1)
    for bit in ctx_bits()[1:]:
        kept = kept + flipped(kept, "ctx", bit)
    other = flipped(kept, "ctx", 1)
    return jnp.where(
        side == 0,
        jnp.concatenate([kept, other], axis=1),
        jnp.concatenate([other, kept], axis=1),
    )


def to_owner(kept, sent, combine):
    kept = combine(kept, flipped(sent, "ctx", 1))
    for bit in ctx_bits()[1:]:
        view = kept.reshape((-1, 2) + kept.shape[1:])
        side = side_of("ctx", bit)
        sent = lax.dynamic_index_in_dim(view, 1 - side, 1, False)
        kept = lax.dynamic_index_in_dim(view, side, 1, False)
        kept = combine(kept, flipped(sent, "ctx", bit))
    return kept[0], flipped(kept[0], "tp", 1)


def from_owners(part):
    whole_part = part[None]
    for bit in reversed(ctx_bits()):
        both = paired(whole_part, "ctx", bit, 1)
        whole_part = both.reshape((-1,) + part.shape)
    return whole_part.reshape((-1,) + part.shape[1:])


def merge_keys(one, two):
    size = LANES // 2
    one_top, two_top = one[..., size : size + 1], two[..., size : size + 1]
    top = jnp.maximum(one_top, two_top)
    one_factor, two_factor = jnp.exp(one_top - top), jnp.exp(two_top - top)
    summed = one * one_factor + two * two_factor
    lane = lax.broadcasted_iota(jnp.int32, summed.shape, summed.ndim - 1)
    return jnp.where(lane == size, top, summed)


def neighbour_rows(cells, count):
    pieces = lax.axis_size("ctx") * lax.axis_size("tp")
    up = [(i, i + 1) for i in range(pieces - 1)]
    before = lax.ppermute(cells[-count:], ("ctx", "tp"), up)
    after = lax.ppermute(cells[:count], ("ctx", "tp"), [(j, i) for i, j in up])
    return (
        jnp.pad(before, ((LANES - count, 0), (0, 0))),
        jnp.pad(after, ((0, LANES - count), (0, 0))),
    )


def own_quarter(shard):
    rows = shard.shape[0] // lax.axis_size("ctx")
    return lax.dynamic_slice_in_dim(shard, lax.axis_index("ctx") * rows, rows, axis=0)


def gathered(shard):
    full = lax.all_gather(own_quarter(shard), ("tp", "fsdp", "ctx"), tiled=True)
    return full.reshape(lax.axis_size("tp"), -1, shard.shape[1])


def gathered_early(shard):
    count = lax.axis_size("fsdp")
    piece = own_quarter(shard)
    if count > 4:
        held = lax.all_gather(piece, "fsdp")
    else:
        here = lax.axis_index("fsdp")
        held = jnp.zeros((count,) + piece.shape, piece.dtype)
        held = lax.dynamic_update_slice_in_dim(held, piece[None], here, 0)
        for step in range(1, count):
            moved = lax.ppermute(piece, "fsdp", [(i, (i + step) % count) for i in range(count)])
            held = lax.dynamic_update_slice_in_dim(held, moved[None], (here - step) % count, 0)
    bits = ctx_bits()
    halves = []
    for number, half in enumerate((held[: count // 2], held[count // 2 :])):
        half = half[None]
        if number == 0:
            half = paired(half[0], "tp", 1, 0)
        for place, bit in enumerate(reversed(bits[1:])):
            half = paired(half, "ctx", bit, 2 + place)
        if number == 1:
            half = paired(half[0], "tp", 1, 0)
        halves.append(paired(half, "ctx", bits[0], 1 + len(bits)))
    full = jnp.concatenate(halves, axis=1)
    return full.reshape(lax.axis_size("tp"), -1, shard.shape[1])


def bits_of(axis):
    bits, bit = [], lax.axis_size(axis) // 2
    while bit:
        bits.append(bit)
        bit //= 2
    return bits


def scattered(grads, first):
    labels = [(axis, bit) for axis in ("tp", "fsdp", "ctx") for bit in bits_of(axis)]
    order = [("ctx", 1)] + [label for label in labels if label[0] == first]
    order += [label for label in labels if label[0] != "fsdp"] + labels[::-1]
    rows = grads.shape[1] // (lax.axis_size("fsdp") * lax.axis_size("ctx"))
    kept = grads.reshape((2,) * len(labels) + (rows, grads.shape[2]))
    for label in order:
        if label not in labels:
            continue
        dim = labels.index(label)
        labels.pop(dim)
        side = side_of(*label)
        sent = lax.dynamic_index_in_dim(kept, 1 - side, dim, False)
        kept = lax.dynamic_index_in_dim(kept, side, dim, False).astype(F32)
        kept = (kept + flipped(sent, *label).astype(F32)).astype(BF16)
    return from_owners(kept).astype(F32)


def added(one, two):
    return (one.astype(F32) + two.astype(F32)).astype(BF16)


def halved(kept, axis, bit, dim):
    size = kept.shape[dim] // 2
    side = side_of(axis, bit)
    sent = lax.dynamic_slice_in_dim(kept, (1 - side) * size, size, axis=dim)
    kept = lax.dynamic_slice_in_dim(kept, side * size, size, axis=dim)
    return added(kept, flipped(sent, axis, bit))


def over_ctx(kept):
    for bit in ctx_bits()[1:]:
        kept = halved(kept, "ctx", bit, 2)
    return kept


def over_tp(kept):
    return halved(kept, "tp", 1, 0)


def over_fsdp(kept, bits):
    for bit in bits:
        kept = halved(kept, "fsdp", bit, 1)
    return kept


def joined_columns(piece):
    piece = piece[0]
    for bit in ctx_bits()[1:][::-1] + [1]:
        other = flipped(piece, "ctx", bit)
        piece = jnp.where(
            side_of("ctx", bit) == 0,
            jnp.concatenate([piece, other], axis=1),
            jnp.concatenate([other, piece], axis=1),
        )
    return piece.astype(F32)


def gate(*values):
    return lax.optimization_barrier(values)


def dotf(spec, *operands):
    return jnp.einsum(spec, *operands, preferred_element_type=F32)


def taps_round(taps):
    middle = taps.shape[1] // 2
    gap = jnp.zeros((taps.shape[0], LANES - taps.shape[1]), F32)
    return jnp.concatenate([taps[:, middle::-1], gap, taps[:, :middle:-1]], axis=1)


def landmark_bounds(length):
    landmark = jnp.arange(LANDMARKS + 1, dtype=jnp.int32)
    return (landmark * length + LANDMARKS - 1) // LANDMARKS


def landmark_counts_of(length):
    bounds = landmark_bounds(length)
    return (bounds[1:] - bounds[:-1]).astype(F32)[:, None]


def landmark_rows(position, length):
    bounds = landmark_bounds(length)
    inside = (position[:, None] >= bounds[None, :-1]) & (position[:, None] < bounds[None, 1:])
    return inside.astype(BF16)


def on_device(
    tokens,
    lengths,
    qk_weight,
    value_weight,
    out_weight,
    in_weight,
    down_weight,
    norm_gains,
    norm_shifts,
    conv_weight,
    cotangent,
):
    tp_count = lax.axis_size("tp")
    tp_index = lax.axis_index("tp")
    ctx_index = lax.axis_index("ctx")
    _, slot_len, model_width = tokens.shape
    rows = slot_len // tp_count
    local_heads, tap_count = conv_weight.shape
    local_width = value_weight.shape[1]
    ff_width = in_weight.shape[1]
    head_size = local_width // local_heads
    heads = local_heads * tp_count
    owners = lax.axis_size("ctx")
    own_heads = heads // owners
    width = local_width * tp_count
    radius = tap_count // 2
    length = lengths[0]

    own = lax.dynamic_slice_in_dim(tokens[0], tp_index * rows, rows, axis=0)
    own_cotangent = lax.dynamic_slice_in_dim(cotangent[0], tp_index * rows, rows, axis=0)
    first_row = (ctx_index * tp_count + tp_index) * rows
    place = jnp.stack([first_row, length, side_of("ctx", 1), ctx_index]).astype(jnp.int32)

    qkv_full = gathered_early(jnp.concatenate([qk_weight[0], qk_weight[1], value_weight], axis=1))
    land_tokens = sequence_sum(token_sums(place, own))
    norm_columns = jnp.concatenate([norm_gains, norm_shifts], axis=0).T
    norm_columns = jnp.pad(norm_columns, ((0, 0), (0, LANES - norm_columns.shape[1])))
    ffn_local = jnp.concatenate([in_weight, down_weight.T, out_weight.T, norm_columns], axis=1)
    ffn_local, qkv_full, land_tokens = gate(ffn_local, qkv_full, land_tokens)
    ffn_full = gathered(ffn_local)
    tap_weights = paired(conv_weight, "tp", 1, 0).reshape(heads, tap_count).astype(F32)
    base, base_back = taps_round(tap_weights), taps_round(tap_weights[:, ::-1])

    queries, keys, values, v_plain, land_q, land_k = projections(
        place, own, land_tokens, qkv_full, head_size
    )
    v_ends = neighbour_rows(v_plain, radius)
    merged, merged_tp = to_owner(
        *third_parts(place, keys, values, land_q, owners), merge_keys
    )
    kept_v, kept_p = inverse_forward(place, land_q, land_k, owners)
    first, conv = first_and_conv(queries, values, *v_ends, land_k, base)
    merged, own_out = landmark_out(merged, merged_tp, kept_v)
    land_out = from_owners(own_out)
    context = contexts(first, conv, land_out)

    own_output, *fed, down_kept, down_sent, last_norm = feed_forward(
        place, context, own, own_cotangent, ffn_full, ff_width, local_width
    )
    output = paired(own_output, "tp", 1, 0).reshape(1, slot_len, model_width)
    down = added(down_kept, flipped(down_sent, "ctx", 1))
    grad_first_res, grad_context, in_kept, in_sent, grad_out_t, first_norm = feed_backward(
        place, fed, context, ffn_full, ff_width, local_width
    )
    g_ends = neighbour_rows(grad_context, radius)
    upper = model_width // 2
    in_other = flipped(in_sent, "ctx", 1)
    in_one = added(in_kept[:, :upper], in_other[:, :upper])
    in_two = added(in_kept[:, upper:], in_other[:, upper:])
    grad_context, down, in_one, in_two = gate(grad_context, down, in_one, in_two)
    down, in_one, in_two = over_ctx(down), over_ctx(in_one), over_tp(in_two)

    land_kept, land_sent, g_lk, g_q = attention_back(
        place, queries, grad_context, land_k, land_out, owners
    )
    own_grads, tp_grads = to_owner(land_kept, land_sent, jnp.add)
    g_conv, g_taps = conv_back(v_plain, v_ends, grad_context, g_ends, base_back)

    def parts(cells):
        return cells.reshape(rows, tp_count, local_width)

    def qkv_part(index):
        return qkv_full[:, :, index * local_width : (index + 1) * local_width]

    scale = head_size**-0.25
    means = land_tokens / landmark_counts_of(length)
    back_q = dotf("tpk,pck->tc", parts(g_q), qkv_part(0))
    own_grads, g_conv, g_taps, down, in_one, in_two, back_q = gate(
        own_grads + tp_grads, g_conv, g_taps, down, in_one, in_two, back_q
    )
    down, in_one, in_two = over_tp(down), over_tp(in_one), over_ctx(in_two)
    spread, lq_mid, lk_mid = inverse_backward(
        place, land_q, land_k, merged, own_grads, kept_v, kept_p
    )
    spread = from_owners(spread)
    fsdp_bits = bits_of("fsdp")
    spread, down, in_one, in_two = gate(spread, down, in_one, in_two)
    in_low = side_of("fsdp", fsdp_bits[0]) == 0
    in_both = added(
        jnp.where(in_low, in_one, in_two),
        flipped(jnp.where(in_low, in_two, in_one), "fsdp", fsdp_bits[0]),
    )
    down = over_fsdp(down, fsdp_bits[:1])
    g_k, g_v, g_lq = third_back(place, keys, values, land_q, spread, g_conv)

    own_columns = own_heads * head_size

    def with_mid(partial, mid):
        mid = mid.transpose(1, 0, 2).reshape(LANDMARKS, own_columns)
        mid = jnp.where(tp_index == 0, mid, 0.0)
        start = (0, ctx_index * own_columns)
        return partial + lax.dynamic_update_slice(jnp.zeros_like(partial), mid, start)

    land_grads = scale * jnp.concatenate([with_mid(g_lq, lq_mid), with_mid(g_lk, lk_mid)], axis=1)
    late = jnp.einsum("mc,mk->ck", means, land_grads, precision=HIGH)
    late = late.reshape(model_width, 2, tp_count, local_width).transpose(1, 2, 0, 3)
    land_total = sequence_sum(land_grads) / landmark_counts_of(length)
    land_total = land_total.reshape(LANDMARKS, 2, tp_count, local_width)
    land_total, down, in_both = gate(land_total, down, in_both)
    grad_down = joined_columns(over_fsdp(down, fsdp_bits[1:])).T
    grad_in = joined_columns(over_fsdp(in_both, fsdp_bits[1:]))

    g_kv = jnp.concatenate([parts(g_k), parts(g_v)], axis=2)
    back = back_q + dotf("tpk,pck->tc", g_kv, qkv_full[:, :, local_width:])
    own_grad = (grad_first_res + back).astype(BF16)
    both_grads = paired(own_grad, "tp", 1, 0).reshape(slot_len, model_width)
    through = sum(
        jnp.einsum(
            "mpk,pck->mc", land_total[:, i], qkv_part(i).astype(F32), precision=HIGH
        )
        for i in range(2)
    )
    position = ctx_index * slot_len + jnp.arange(slot_len, dtype=jnp.int32)
    onehot = landmark_rows(position, length)
    high = through.astype(BF16)
    lower = (through - high.astype(F32)).astype(BF16)
    grad_tokens = both_grads.astype(F32) + dotf(
        "tm,mc->tc", jnp.concatenate([onehot, onehot], axis=1), jnp.concatenate([high, lower])
    )
    grad_tokens = grad_tokens.reshape(1, slot_len, model_width)

    grad_q = dotf("tc,tpk->pck", own, parts(g_q)) + late[0]
    owner_count = lax.axis_size("fsdp")
    owner_rows = model_width // owner_count
    taps_grad = jnp.take(
        g_taps, jnp.array([(LANES + radius - 1 - i) % LANES for i in range(tap_count)]), axis=1
    ).reshape(tp_count, -1)
    tap_columns = -(-taps_grad.shape[1] // owner_rows)
    taps_grad = jnp.pad(taps_grad, ((0, 0), (0, tap_columns * owner_rows - taps_grad.shape[1])))
    taps_grad = jnp.tile(taps_grad.reshape(tp_count, owner_rows, tap_columns), (1, owner_count, 1))
    norm_grads = jnp.stack([first_norm[0], last_norm[0], first_norm[1], last_norm[1]], axis=1)
    small = jnp.concatenate(
        [jnp.broadcast_to(norm_grads[None], (tp_count,) + norm_grads.shape), taps_grad], axis=2
    )
    small = jnp.pad(small, ((0, 0), (0, 0), (0, LANES - small.shape[2])))
    mixed_grads = scattered(jnp.concatenate([grad_out_t, small.astype(BF16)], axis=2), "ctx")
    own_small = mixed_grads[:, local_width:]
    grad_taps = own_small[:, 4 : 4 + tap_columns].reshape(-1)[: local_heads * tap_count]

    grad_kv = dotf("tc,tpk->pck", own, g_kv)
    grad_k = grad_kv[:, :, :local_width] + late[1]
    grad_qkv = scattered(
        jnp.concatenate(
            [grad_q.astype(BF16), grad_k.astype(BF16), grad_kv[:, :, local_width:].astype(BF16)],
            axis=2,
        ),
        "ctx",
    )
    return (
        output,
        grad_tokens,
        jnp.stack([grad_qkv[:, :local_width], grad_qkv[:, local_width : 2 * local_width]]),
        grad_qkv[:, 2 * local_width :],
        mixed_grads[:, :local_width].T,
        grad_in,
        grad_down,
        own_small[:, :2].T,
        own_small[:, 2:4].T,
        grad_taps.reshape(local_heads, tap_count),
    )


def solution(mesh):
    in_specs = (
        P("fsdp", "ctx", None),
        P("fsdp"),
        P(None, "fsdp", "tp"),
        P("fsdp", "tp"),
        P("tp", "fsdp"),
        P("fsdp", "tp"),
        P("tp", "fsdp"),
        P(None, "fsdp"),
        P(None, "fsdp"),
        P("tp", None),
        P("fsdp", "ctx", None),
    )
    out_specs = (
        P("fsdp", "ctx", None),
        P("fsdp", "ctx", None),
        P(None, "fsdp", "tp"),
        P("fsdp", "tp"),
        P("tp", "fsdp"),
        P("fsdp", "tp"),
        P("tp", "fsdp"),
        P(None, "fsdp"),
        P(None, "fsdp"),
        P("tp", None),
    )
    return jax.shard_map(
        on_device, mesh=mesh, in_specs=in_specs, out_specs=out_specs, check_vma=False
    )
```

```python
import jax
import jax.numpy as jnp
from jax import lax
from jax.experimental import pallas as pl
from jax.experimental.pallas import tpu as pltpu
from jax.sharding import PartitionSpec as P

LANDMARKS = 64
NEWTON = 6
LANES = 128
VMEM_BYTES = 56 * 2**20

HIGH = lax.Precision.HIGHEST
F32 = jnp.float32
BF16 = jnp.bfloat16


def lasting(microseconds):
    return pl.CostEstimate(
        flops=int(microseconds * 1.1535e9), bytes_accessed=int(microseconds * 1e5), transcendentals=0
    )


def nn(left, right):
    return jnp.dot(left, right, preferred_element_type=F32)


def nt(left, right):
    return lax.dot_general(left, right, (((1,), (1,)), ((), ())), preferred_element_type=F32)


def split(wide):
    high = wide.astype(BF16)
    return high, (wide - high.astype(F32)).astype(BF16)


def whole(count):
    return [pl.BlockSpec(memory_space=pltpu.VMEM)] * count


SCALARS = pl.BlockSpec(memory_space=pltpu.SMEM)
PARAMS = pltpu.CompilerParams(vmem_limit_bytes=VMEM_BYTES)


def landmark_onehot(place, rows, landmark_axis):
    shape = (LANDMARKS, rows) if landmark_axis == 0 else (rows, LANDMARKS)
    landmark = lax.broadcasted_iota(jnp.int32, shape, landmark_axis)
    position = place[0] + lax.broadcasted_iota(jnp.int32, shape, 1 - landmark_axis)
    start = lax.shift_right_logical(landmark * place[1] + (LANDMARKS - 1), 6)
    end = lax.shift_right_logical((landmark + 1) * place[1] + (LANDMARKS - 1), 6)
    return jnp.where((position >= start) & (position < end), 1.0, 0.0).astype(BF16)


def live_lanes(place, rows):
    position = place[0] + lax.broadcasted_iota(jnp.int32, (1, rows), 1)
    return position < place[1]


def band(base_row):
    ring = pltpu.roll(jnp.broadcast_to(base_row, (LANES, LANES)), 0, 1, stride=1, stride_axis=0)
    gap = lax.broadcasted_iota(jnp.int32, (LANES, LANES), 0) - lax.broadcasted_iota(
        jnp.int32, (LANES, LANES), 1
    )
    zero = jnp.zeros_like(ring)
    before = jnp.where(gap >= LANES - 16, ring, zero).astype(BF16)
    here = jnp.where(jnp.abs(gap) <= 16, ring, zero).astype(BF16)
    after = jnp.where(gap <= 16 - LANES, ring, zero).astype(BF16)
    return before, here, after


def convolved(blocks, bands):
    before, here, after = bands
    return jnp.concatenate(
        [
            nn(blocks[i], before) + nn(blocks[i + 1], here) + nn(blocks[i + 2], after)
            for i in range(len(blocks) - 2)
        ],
        axis=1,
    )


def token_sums_kernel(place, tokens, sums):
    sums[...] = nn(landmark_onehot(place, tokens.shape[0], 0), tokens[...])


def token_sums(place, tokens):
    return pl.pallas_call(
        token_sums_kernel,
        out_shape=jax.ShapeDtypeStruct((LANDMARKS, tokens.shape[1]), F32),
        in_specs=[SCALARS] + whole(1),
        out_specs=whole(1)[0],
        compiler_params=PARAMS,
        cost_estimate=lasting(2.5),
        name="token_sums",
    )(place, tokens)


def landmark_counts(place):
    landmark = lax.broadcasted_iota(jnp.int32, (LANDMARKS, 1), 0)
    start = lax.shift_right_logical(landmark * place[1] + (LANDMARKS - 1), 6)
    end = lax.shift_right_logical((landmark + 1) * place[1] + (LANDMARKS - 1), 6)
    return (end - start).astype(F32)


def projection_kernel(place, tokens, sums, weights, q_out, k_out, v_out, v_plain, land_q, land_k):
    rows = tokens.shape[0]
    halves, _, packed = weights.shape
    width = packed // 3
    size = land_q.shape[2]
    position = place[0] + lax.broadcasted_iota(jnp.int32, (rows, 1), 0)
    live = jnp.where(position < place[1], 1.0, 0.0)
    scaled = live * 64**-0.25
    means = jnp.concatenate(split(sums[...] / landmark_counts(place)), axis=0)
    cells = tokens[...]
    for half in range(halves):
        for part, out in enumerate((q_out, k_out, v_out)):
            weight = weights[half, :, part * width : (part + 1) * width]
            low = ((live if part == 2 else scaled) * nn(cells, weight)).astype(BF16)
            out[half * width : (half + 1) * width, :] = low.T
            if part == 2:
                v_plain[:, half * width : (half + 1) * width] = low
                continue
            both = nn(means, weight)
            land = (64**-0.25 * (both[:LANDMARKS] + both[LANDMARKS:])).astype(BF16)
            to = land_k if part else land_q
            for head in range(width // size):
                to[half * (width // size) + head] = land[:, head * size : (head + 1) * size]


def projections(place, tokens, sums, weights, size):
    rows = tokens.shape[0]
    width = weights.shape[0] * weights.shape[2] // 3
    turned = jax.ShapeDtypeStruct((width, rows), BF16)
    land = jax.ShapeDtypeStruct((width // size, LANDMARKS, size), BF16)
    return pl.pallas_call(
        projection_kernel,
        out_shape=(turned, turned, turned, jax.ShapeDtypeStruct((rows, width), BF16), land, land),
        in_specs=[SCALARS] + whole(3),
        out_specs=tuple(whole(6)),
        compiler_params=PARAMS,
        cost_estimate=lasting(10),
        name="projections",
    )(place, tokens, sums, weights)


def by_owner(place, h, owners, kept, sent, values):
    per = kept.shape[1]
    for owner in range(owners):
        @pl.when((h >= owner * per) & (h < (owner + 1) * per))
        def _(owner=owner):
            mine = place[2] == owner % 2

            @pl.when(mine)
            def _():
                kept[owner // 2, h - owner * per] = values

            @pl.when(jnp.logical_not(mine))
            def _():
                sent[owner // 2, h - owner * per] = values


def third_kernel(place, keys, values, land_q, kept, sent):
    heads = land_q.shape[0]
    size = land_q.shape[2]
    rows = keys.shape[1]
    owners = 2 * kept.shape[0]
    live = live_lanes(place, rows)

    def head(h):
        at = pl.ds(pl.multiple_of(h * size, size), size)
        scores = jnp.where(live, nn(land_q[h], keys[at, :]), -1e30)
        top = jnp.max(scores, axis=1, keepdims=True)
        raised = jnp.where(live, jnp.exp(scores - top), 0.0)
        total = jnp.sum(raised, axis=1, keepdims=True)
        high, low = split(raised)
        value = values[at, :]
        mixed = nt(high, value) + nt(low, value)
        lane = lax.broadcasted_iota(jnp.int32, (LANDMARKS, LANES - size), 1)
        stats = jnp.where(lane == 0, top, jnp.where(lane == 1, total, 0.0))
        by_owner(place, h, owners, kept, sent, jnp.concatenate([mixed, stats], axis=1))

    def pair(i, _):
        head(2 * i)
        head(2 * i + 1)
        return 0

    lax.fori_loop(0, heads // 2, pair, 0)


def owner_parts(heads, owners):
    part = jax.ShapeDtypeStruct((owners // 2, heads // owners, LANDMARKS, LANES), F32)
    return part, part


def third_parts(place, keys, values, land_q, owners):
    return pl.pallas_call(
        third_kernel,
        out_shape=owner_parts(land_q.shape[0], owners),
        in_specs=[SCALARS] + whole(3),
        out_specs=tuple(whole(2)),
        compiler_params=PARAMS,
        cost_estimate=lasting(9),
        name="third_parts",
    )(place, keys, values, land_q)


def dot_high(left, right):
    return jnp.dot(left, right, preferred_element_type=F32, precision=HIGH)


def dot_high_nt(left, right):
    return lax.dot_general(
        left, right, (((1,), (1,)), ((), ())), preferred_element_type=F32, precision=HIGH
    )


def eye():
    row = lax.broadcasted_iota(jnp.int32, (LANDMARKS, LANDMARKS), 0)
    column = lax.broadcasted_iota(jnp.int32, (LANDMARKS, LANDMARKS), 1)
    return jnp.where(row == column, 1.0, 0.0)


def middle_map(land_q, land_k):
    scores = nt(land_q, land_k)
    raised = jnp.exp(scores - jnp.max(scores, axis=1, keepdims=True))
    return raised / jnp.sum(raised, axis=1, keepdims=True)


def inverse_kernel(place, land_q, land_k, kept_v, kept_p):
    heads = range(kept_v.shape[1])
    one = eye()
    own = [place[3] * len(heads) + h for h in heads]
    middle = [middle_map(land_q[h], land_k[h]) for h in own]
    approx = [m.T / jnp.sum(m * m, keepdims=True) for m in middle]
    for turn in range(NEWTON):
        product = [dot_high(middle[h], approx[h]) for h in heads]
        for h in heads:
            kept_v[turn, h] = approx[h]
            kept_p[turn, h] = product[h]
        bracket = [7.0 * one - p for p in product]
        bracket = [15.0 * one - dot_high(product[h], bracket[h]) for h in heads]
        bracket = [13.0 * one - dot_high(product[h], bracket[h]) for h in heads]
        approx = [0.25 * dot_high(approx[h], bracket[h]) for h in heads]
    for h in heads:
        kept_v[NEWTON, h] = approx[h]


def inverse_forward(place, land_q, land_k, owners):
    heads = land_q.shape[0] // owners
    square = (heads, LANDMARKS, LANDMARKS)
    return pl.pallas_call(
        inverse_kernel,
        out_shape=(
            jax.ShapeDtypeStruct((NEWTON + 1,) + square, F32),
            jax.ShapeDtypeStruct((NEWTON,) + square, F32),
        ),
        in_specs=[SCALARS] + whole(2),
        out_specs=tuple(whole(2)),
        compiler_params=PARAMS,
        cost_estimate=lasting(7),
        name="inverse_forward",
    )(place, land_q, land_k)


def merged_keys(one, two, size):
    one_top, two_top = one[:, size : size + 1], two[:, size : size + 1]
    top = jnp.maximum(one_top, two_top)
    summed = one * jnp.exp(one_top - top) + two * jnp.exp(two_top - top)
    lane = lax.broadcasted_iota(jnp.int32, one.shape, 1)
    return jnp.where(lane == size, top, summed)


def land_out_kernel(one, two, kept_v, merged, land_out):
    size = land_out.shape[2]
    for h in range(one.shape[0]):
        both = merged_keys(one[h], two[h], size)
        merged[h] = both
        mixed = both[:, :size] / both[:, size + 1 : size + 2]
        land_out[h] = dot_high(kept_v[NEWTON, h], mixed).astype(BF16)


def landmark_out(one, two, kept_v):
    heads = one.shape[0]
    return pl.pallas_call(
        land_out_kernel,
        out_shape=(
            jax.ShapeDtypeStruct(one.shape, F32),
            jax.ShapeDtypeStruct((heads, LANDMARKS, LANES // 2), BF16),
        ),
        in_specs=whole(3),
        out_specs=tuple(whole(2)),
        compiler_params=PARAMS,
        cost_estimate=lasting(2.2),
        name="landmark_out",
    )(one, two, kept_v)


def inverse_back_kernel(
    place, land_q, land_k, merged, grads, kept_v, kept_p, spread, g_lq, g_lk
):
    heads = range(grads.shape[0])
    size = land_q.shape[2]
    one = eye()
    own = [place[3] * len(heads) + h for h in heads]
    middle = [middle_map(land_q[h], land_k[h]) for h in own]
    turned = [m.T for m in middle]
    g_approx = []
    for h in heads:
        mixed = merged[h][:, :size] / merged[h][:, size + 1 : size + 2]
        g_land = grads[h][:, :size]
        g_approx.append(dot_high_nt(g_land, mixed))
        g_mixed = dot_high(kept_v[NEWTON, h].T, g_land)
        row_dot = jnp.sum(g_mixed * mixed, axis=1, keepdims=True)
        lane = lax.broadcasted_iota(jnp.int32, (LANDMARKS, LANES - size), 1)
        top = merged[h][:, size : size + 1]
        total = merged[h][:, size + 1 : size + 2]
        stats = jnp.where(
            lane == 0, row_dot, jnp.where(lane == 1, top, jnp.where(lane == 2, total, 0.0))
        )
        spread[h] = jnp.concatenate([g_mixed, stats], axis=1)
    g_middle = [jnp.zeros((LANDMARKS, LANDMARKS), F32) for _ in heads]
    for turn in reversed(range(NEWTON)):
        approx = [kept_v[turn, h] for h in heads]
        product = [kept_p[turn, h] for h in heads]
        first = [7.0 * one - p for p in product]
        second = [15.0 * one - dot_high(product[h], first[h]) for h in heads]
        third = [13.0 * one - dot_high(product[h], second[h]) for h in heads]
        g_third = [0.25 * dot_high(approx[h].T, g_approx[h]) for h in heads]
        g_back = [0.25 * dot_high_nt(g_approx[h], third[h]) for h in heads]
        g_product = [-dot_high_nt(g_third[h], second[h]) for h in heads]
        pt = [p.T for p in product]
        g_second = [-dot_high(pt[h], g_third[h]) for h in heads]
        g_product = [g_product[h] - dot_high_nt(g_second[h], first[h]) for h in heads]
        g_product = [g_product[h] + dot_high(pt[h], g_second[h]) for h in heads]
        g_middle = [g_middle[h] + dot_high_nt(g_product[h], approx[h]) for h in heads]
        g_approx = [g_back[h] + dot_high(turned[h], g_product[h]) for h in heads]
    for h in heads:
        m = middle[h]
        size_sum = jnp.sum(m * m, keepdims=True)
        g_size = -jnp.sum(g_approx[h] * turned[h], keepdims=True) / (size_sum * size_sum)
        g_m = g_middle[h] + g_approx[h].T / size_sum + 2.0 * g_size * m
        g_scores = m * (g_m - jnp.sum(g_m * m, axis=1, keepdims=True))
        g_lq[h] = dot_high(g_scores, land_k[own[h]].astype(F32))
        g_lk[h] = dot_high(g_scores.T, land_q[own[h]].astype(F32))


def inverse_backward(place, land_q, land_k, merged, grads, kept_v, kept_p):
    heads = grads.shape[0]
    square = jax.ShapeDtypeStruct((heads,) + land_q.shape[1:], F32)
    return pl.pallas_call(
        inverse_back_kernel,
        out_shape=(jax.ShapeDtypeStruct((heads, LANDMARKS, LANES), F32), square, square),
        in_specs=[SCALARS] + whole(6),
        out_specs=tuple(whole(3)),
        compiler_params=PARAMS,
        cost_estimate=lasting(11.5),
        name="inverse_backward",
    )(place, land_q, land_k, merged, grads, kept_v, kept_p)


def first_map(land_k, queries):
    scores = nn(land_k, queries)
    raised = jnp.exp(scores - jnp.max(scores, axis=0, keepdims=True))
    return raised * (1.0 / jnp.sum(raised, axis=0, keepdims=True))


def head_blocks(cells, ends, at):
    rows = cells.shape[1]
    left, right = ends
    return (
        [left[at, :]]
        + [cells[at, i * LANES : (i + 1) * LANES] for i in range(rows // LANES)]
        + [right[at, :]]
    )


def first_conv_kernel(queries, values, left, right, land_k, base, first, conv, ends):
    heads, _, size = land_k.shape
    ends[0] = left[...].T
    ends[1] = right[...].T

    def head(h):
        at = pl.ds(pl.multiple_of(h * size, size), size)
        first[at, :] = first_map(land_k[h], queries[at, :]).astype(BF16)
        blocks = head_blocks(values, (ends.at[0], ends.at[1]), at)
        conv[at, :] = convolved(blocks, band(base[pl.ds(h, 1), :]))

    def pair(i, _):
        head(2 * i)
        head(2 * i + 1)
        return 0

    lax.fori_loop(0, heads // 2, pair, 0)


def first_and_conv(queries, values, left, right, land_k, base):
    width, rows = queries.shape
    return pl.pallas_call(
        first_conv_kernel,
        out_shape=(
            jax.ShapeDtypeStruct((width, rows), BF16),
            jax.ShapeDtypeStruct((width, rows), F32),
        ),
        in_specs=whole(6),
        out_specs=tuple(whole(2)),
        scratch_shapes=[pltpu.VMEM((2, width, LANES), BF16)],
        compiler_params=PARAMS,
        cost_estimate=lasting(8),
        name="first_and_conv",
    )(queries, values, left, right, land_k, base)


def context_kernel(first, conv, land_out, context):
    heads, _, size = land_out.shape

    def head(h):
        at = pl.ds(pl.multiple_of(h * size, size), size)
        return (nn(land_out[h].T, first[at, :]) + conv[at, :]).astype(BF16)

    def pair(i, _):
        both = jnp.concatenate([head(2 * i), head(2 * i + 1)], axis=0)
        context[:, pl.ds(pl.multiple_of(i * LANES, LANES), LANES)] = both.T
        return 0

    lax.fori_loop(0, heads // 2, pair, 0)


def contexts(first, conv, land_out):
    width, rows = first.shape
    return pl.pallas_call(
        context_kernel,
        out_shape=jax.ShapeDtypeStruct((rows, width), BF16),
        in_specs=whole(3),
        out_specs=whole(1)[0],
        compiler_params=PARAMS,
        cost_estimate=lasting(5.5),
        name="contexts",
    )(first, conv, land_out)


def attention_back_kernel(
    place, queries, grads, land_k, land_out, kept, sent, g_lk, g_query
):
    heads, _, size = land_k.shape
    rows = queries.shape[1]
    owners = 2 * kept.shape[0]
    scaled = jnp.where(live_lanes(place, rows), 64**-0.25, 0.0)

    def pair(i, _):
        lanes = pl.ds(pl.multiple_of(i * LANES, LANES), LANES)
        turned = grads[:, lanes].T
        g_queries, g_keys = [], []
        for side in range(2):
            h = 2 * i + side
            query = queries[pl.ds(pl.multiple_of(h * size, size), size), :]
            g_context = turned[side * size : (side + 1) * size]
            first = first_map(land_k[h], query)
            g_first = nn(land_out[h], g_context)
            inner = jnp.sum(g_first * first, axis=0, keepdims=True)
            g_scores = (first * (g_first - inner)).astype(BF16)
            g_land = nt(first.astype(BF16), g_context)
            g_key = nt(g_scores, query)
            by_owner(place, h, owners, kept, sent, jnp.concatenate([g_land, g_key], axis=1))
            g_keys.append(g_key)
            g_queries.append((scaled * nn(land_k[h].T, g_scores)).astype(BF16))
        g_query[:, lanes] = jnp.concatenate(g_queries, axis=0).T
        g_lk[:, lanes] = jnp.concatenate(g_keys, axis=1)
        return 0

    lax.fori_loop(0, heads // 2, pair, 0)


def attention_back(place, queries, grads, land_k, land_out, owners):
    width, rows = queries.shape
    heads = land_k.shape[0]
    return pl.pallas_call(
        attention_back_kernel,
        out_shape=owner_parts(heads, owners)
        + (
            jax.ShapeDtypeStruct((LANDMARKS, width), F32),
            jax.ShapeDtypeStruct((rows, width), BF16),
        ),
        in_specs=[SCALARS] + whole(4),
        out_specs=tuple(whole(4)),
        compiler_params=PARAMS,
        cost_estimate=lasting(11.4),
        name="attention_back",
    )(place, queries, grads, land_k, land_out)


def conv_back_kernel(
    v_plain, v_left, v_right, grads, g_left, g_right, base_back, g_value, g_taps, ends
):
    heads = g_taps.shape[0]
    rows, width = grads.shape
    size = width // heads
    blocks_in = rows // LANES
    row = lax.broadcasted_iota(jnp.int32, (LANES, LANES), 0)
    column = lax.broadcasted_iota(jnp.int32, (LANES, LANES), 1)
    reverse = jnp.where(row + column == LANES - 1, 1.0, 0.0)
    gap = row - column
    ends[0] = g_left[...].T
    ends[1] = g_right[...].T

    def pair(i, _):
        lanes = pl.ds(pl.multiple_of(i * LANES, LANES), LANES)
        turned = grads[:, lanes].T
        plain = [v_left[LANES - 16 :, lanes]]
        plain += [v_plain[b * LANES : (b + 1) * LANES, lanes] for b in range(blocks_in)]
        plain += [v_right[:16, lanes]]
        for side in range(2):
            h = 2 * i + side
            at = pl.ds(pl.multiple_of(h * size, size), size)
            g_context = turned[side * size : (side + 1) * size]
            blocks = [ends[0, at, :]]
            blocks += [g_context[:, b * LANES : (b + 1) * LANES] for b in range(blocks_in)]
            blocks += [ends[1, at, :]]
            g_value[at, :] = convolved(blocks, band(base_back[pl.ds(h, 1), :]))
            own = (row >= size) == (side == 1)
            here = jnp.zeros((LANES, LANES), F32)
            before = jnp.zeros((16, LANES), F32)
            after = jnp.zeros((16, LANES), F32)
            for b in range(blocks_in):
                piece = turned[:, b * LANES : (b + 1) * LANES]
                masked = jnp.where(own, piece, jnp.zeros_like(piece))
                prior = plain[0] if b == 0 else plain[b][LANES - 16 :]
                later = plain[b + 2][:16]
                here = here + nn(plain[b + 1], masked)
                before = before + nn(prior, masked)
                after = after + nn(later, masked)
            empty = jnp.zeros((LANES - 16, LANES), F32)
            ring = jnp.where(jnp.abs(gap) <= 16, here, 0.0)
            ring = ring + jnp.where(
                gap >= LANES - 16, jnp.concatenate([empty, before], axis=0), 0.0
            )
            ring = ring + jnp.where(
                gap <= 16 - LANES, jnp.concatenate([after, empty], axis=0), 0.0
            )
            straight = pltpu.roll(dot_high(reverse, ring), 0, 1, stride=1, stride_axis=0)
            g_taps[pl.ds(h, 1), :] = jnp.sum(straight, axis=0, keepdims=True)
        return 0

    lax.fori_loop(0, heads // 2, pair, 0)


def conv_back(v_plain, v_ends, grads, g_ends, base_back):
    rows, width = grads.shape
    heads = base_back.shape[0]
    return pl.pallas_call(
        conv_back_kernel,
        out_shape=(
            jax.ShapeDtypeStruct((width, rows), F32),
            jax.ShapeDtypeStruct((heads, LANES), F32),
        ),
        in_specs=whole(7),
        out_specs=tuple(whole(2)),
        scratch_shapes=[pltpu.VMEM((2, width, LANES), BF16)],
        compiler_params=PARAMS,
        cost_estimate=lasting(13.6),
        name="conv_back",
    )(v_plain, *v_ends, grads, *g_ends, base_back)


def third_back_kernel(place, keys, values, land_q, spread, g_conv, g_k, g_v, g_lq):
    heads, _, size = land_q.shape
    rows = keys.shape[1]
    live = live_lanes(place, rows)
    live_row = jnp.where(live, 1.0, 0.0)
    scaled_row = live_row * 64**-0.25

    def pair(i, _):
        lanes = pl.ds(pl.multiple_of(i * LANES, LANES), LANES)
        g_keys, g_values, g_lqs = [], [], []
        for side in range(2):
            h = 2 * i + side
            at = pl.ds(pl.multiple_of(h * size, size), size)
            key, value = keys[at, :], values[at, :]
            pack = spread[h]
            g_mixed = pack[:, :size]
            row_dot = pack[:, size : size + 1]
            top = pack[:, size + 1 : size + 2]
            total = pack[:, size + 2 : size + 3]
            scores = nn(land_q[h], key)
            third = jnp.where(live, jnp.exp(scores - top), 0.0) * (1.0 / total)
            gm_high, gm_low = split(g_mixed)
            g_third = nn(gm_high, value) + nn(gm_low, value)
            g_high, g_low = split(third * (g_third - row_dot))
            g_lqs.append(nt(g_high, key) + nt(g_low, key))
            turned = land_q[h].T
            g_key = nn(turned, g_high) + nn(turned, g_low)
            g_keys.append((scaled_row * g_key).astype(BF16))
            t_high, t_low = split(third)
            gmt_high, gmt_low = split(g_mixed.T)
            g_value = nn(gmt_high, t_high) + nn(gmt_high, t_low) + nn(gmt_low, t_high)
            g_values.append((live_row * (g_value + g_conv[at, :])).astype(BF16))
        g_k[:, lanes] = jnp.concatenate(g_keys, axis=0).T
        g_v[:, lanes] = jnp.concatenate(g_values, axis=0).T
        g_lq[:, lanes] = jnp.concatenate(g_lqs, axis=1)
        return 0

    lax.fori_loop(0, heads // 2, pair, 0)


def third_back(place, keys, values, land_q, spread, g_conv):
    width, rows = keys.shape
    plain = jax.ShapeDtypeStruct((rows, width), BF16)
    return pl.pallas_call(
        third_back_kernel,
        out_shape=(plain, plain, jax.ShapeDtypeStruct((LANDMARKS, width), F32)),
        in_specs=[SCALARS] + whole(5),
        out_specs=tuple(whole(3)),
        compiler_params=PARAMS,
        cost_estimate=lasting(12),
        name="third_back",
    )(place, keys, values, land_q, spread, g_conv)


def centred_rows(rows):
    centred = rows - jnp.mean(rows, axis=1, keepdims=True)
    scale = lax.rsqrt(jnp.mean(centred * centred, axis=1, keepdims=True) + 1e-05)
    return centred * scale, scale


def norm_back(grads, gain, unit, scale):
    scaled = grads * gain
    inner = jnp.mean(scaled * unit, axis=1, keepdims=True)
    return scale * (scaled - jnp.mean(scaled, axis=1, keepdims=True) - unit * inner)


def gelu_pair(hidden):
    share = 0.5 * (1.0 + lax.erf(hidden * 0.7071067811865476))
    density = jnp.exp(-0.5 * hidden * hidden) * 0.3989422804014327
    return hidden * share, share + hidden * density


class Copies:
    def __init__(self, sems):
        self.sems, self.used, self.open = sems, 0, []

    def start(self, source, target):
        copy = pltpu.make_async_copy(source, target, self.sems.at[self.used])
        self.used += 1
        copy.start()
        return copy

    def out(self, source, target):
        self.open.append(self.start(source, target))

    def finish(self):
        for copy in self.open:
            copy.wait()


def each_tile(count, tile, body):
    def step(i, _):
        body(i, pl.ds(pl.multiple_of(i * tile, tile), tile))
        return 0

    lax.fori_loop(0, count // tile, step, 0)


def weight_grad(turned, cells, halves, which, out):
    ff = cells.shape[1] // halves
    columns = ff // 2
    for half in range(halves):
        from_column = pl.ds(pl.multiple_of(half * ff + which * columns, columns), columns)

        def rows_of(i, at, half=half, from_column=from_column):
            out[half, at, :] = nn(turned[at, :], cells[:, from_column]).astype(BF16)

        each_tile(turned.shape[0], 384, rows_of)


def feed_kernel(
    place, context_in, tokens_in, cotangent_in, weights,
    output_to, slope_to, g_fed_to, g_second_to, unit_to, scale_to, turned_to, active_to, fed_turned_to, sent_to,
    norm_grads, in_w, down_w, out_w, norms, context, tokens, cotangent,
    low, unit, scales, fed, active, slopes, g_fed, g_fed_turned, normed_turned, output, sent,
    sems,
):
    rows, width = tokens.shape
    halves, _, ff = in_w.shape
    part = out_w.shape[2]
    tile = 256
    copies = Copies(sems)
    early = [
        copies.start(weights.at[:, :, pl.ds(2 * ff, part)], out_w),
        copies.start(context_in, context),
        copies.start(tokens_in, tokens),
        copies.start(weights.at[:, :, pl.ds(2 * ff + part, LANES)], norms),
    ]
    in_copy = copies.start(weights.at[:, :, pl.ds(0, ff)], in_w)
    down_copy = copies.start(weights.at[:, :, pl.ds(ff, ff)], down_w)
    cotangent_copy = copies.start(cotangent_in, cotangent)
    for copy in early:
        copy.wait()
    columns = norms[0].astype(F32).T
    gain0, gain1 = columns[0:1], columns[1:2]
    shift0, shift1 = columns[2:3], columns[3:4]
    norm_grads[...] = jnp.zeros_like(norm_grads)

    def project(i, at):
        attended = nt(context[at, :part], out_w[0])
        for half in range(1, halves):
            attended = attended + nt(context[at, half * part : (half + 1) * part], out_w[half])
        rows_unit, scale = centred_rows(tokens[at, :].astype(F32) + attended)
        unit[at, :] = rows_unit
        scales[at, :] = jnp.broadcast_to(scale, (tile, LANES))
        normed = (rows_unit * gain0 + shift0).astype(BF16)
        low[at, :] = normed
        normed_turned[:, at] = normed.T

    each_tile(rows, tile, project)
    copies.out(unit, unit_to)
    copies.out(scales, scale_to)
    copies.out(normed_turned, turned_to)
    in_copy.wait()
    big = 512

    def hidden_rows(i, at):
        for half in range(halves):
            value, slope = gelu_pair(nn(low[at, :], in_w[half]))
            active[at, half * ff : (half + 1) * ff] = value.astype(BF16)
            slopes[at, half * ff : (half + 1) * ff] = slope.astype(BF16)

    each_tile(rows, tile, hidden_rows)
    copies.out(slopes, slope_to)
    copies.out(active, active_to)
    down_copy.wait()

    def fed_rows(i, at):
        total = nt(active[at, :ff], down_w[0])
        for half in range(1, halves):
            total = total + nt(active[at, half * ff : (half + 1) * ff], down_w[half])
        fed[at, :] = total

    each_tile(rows, big, fed_rows)
    cotangent_copy.wait()

    def second_norm(i, at):
        normed = unit[at, :] * gain0 + shift0
        unit1, scale1 = centred_rows(normed + fed[at, :])
        position = place[0] + i * tile + lax.broadcasted_iota(jnp.int32, (tile, 1), 0)
        live = jnp.where(position < place[1], 1.0, 0.0)
        output[at, :] = (live * (unit1 * gain1 + shift1)).astype(BF16)
        grads = live * cotangent[at, :].astype(F32)
        norm_grads[0:1, :] += jnp.sum(grads * unit1, axis=0, keepdims=True)
        norm_grads[1:2, :] += jnp.sum(grads, axis=0, keepdims=True)
        second = norm_back(grads, gain1, unit1, scale1)
        fed[at, :] = second
        g_low = second.astype(BF16)
        g_fed[at, :] = g_low
        g_fed_turned[:, at] = g_low.T

    each_tile(rows, tile, second_norm)
    copies.out(output, output_to)
    copies.out(fed, g_second_to)
    copies.out(g_fed, g_fed_to)
    copies.out(g_fed_turned, fed_turned_to)
    weight_grad(g_fed_turned, active, halves, 1 - place[2], sent)
    copies.out(sent, sent_to)
    copies.finish()


ANYWHERE = pl.BlockSpec(memory_space=pl.ANY)


def feed_forward(place, context, tokens, cotangent, weights, ff, part):
    rows, width = tokens.shape
    halves = weights.shape[0]
    grad = (halves, width, ff // 2)
    shapes = [
        ((rows, width), BF16), ((rows, halves * ff), BF16), ((rows, width), BF16),
        ((rows, width), F32), ((rows, width), F32), ((rows, LANES), F32), ((width, rows), BF16),
        ((rows, halves * ff), BF16), ((width, rows), BF16), (grad, BF16), ((8, width), F32),
    ]
    scratch = [
        ((halves, width, ff), BF16), ((halves, width, ff), BF16), ((halves, width, part), BF16),
        ((halves, width, LANES), BF16), ((rows, width), BF16), ((rows, width), BF16),
        ((rows, width), BF16),
        ((rows, width), BF16), ((rows, width), F32), ((rows, LANES), F32), ((rows, width), F32),
        ((rows, halves * ff), BF16), ((rows, halves * ff), BF16), ((rows, width), BF16),
        ((width, rows), BF16), ((width, rows), BF16), ((rows, width), BF16), (grad, BF16),
    ]
    return pl.pallas_call(
        feed_kernel,
        out_shape=tuple(jax.ShapeDtypeStruct(*shape) for shape in shapes),
        in_specs=[SCALARS] + [ANYWHERE] * 4,
        out_specs=tuple([ANYWHERE] * 10 + whole(1)),
        scratch_shapes=[pltpu.VMEM(*shape) for shape in scratch]
        + [pltpu.SemaphoreType.DMA((17,))],
        compiler_params=PARAMS,
        cost_estimate=lasting(29),
        name="feed_forward",
    )(place, context, tokens, cotangent, weights)


def feed_back_kernel(
    place, slope_in, g_fed_in, g_second_in, unit_in, scale_in, turned_in, context_in, weights,
    g_first_to, g_context_to, g_hidden_to, sent_to, g_out_to, norm_grads,
    in_w, down_w, out_w, norms, g_hidden, g_fed, second, unit, scales, normed_turned, context,
    g_att, g_att_turned, g_context, sent, g_out,
    sems,
):
    rows, width = second.shape
    halves, _, ff = in_w.shape
    part = out_w.shape[2]
    tile = 256
    copies = Copies(sems)
    early = [
        copies.start(g_fed_in, g_fed),
        copies.start(weights.at[:, :, pl.ds(ff, ff)], down_w),
        copies.start(slope_in, g_hidden),
    ]
    later = [
        copies.start(turned_in, normed_turned),
        copies.start(weights.at[:, :, pl.ds(0, ff)], in_w),
        copies.start(g_second_in, second),
        copies.start(unit_in, unit),
        copies.start(scale_in, scales),
        copies.start(weights.at[:, :, pl.ds(2 * ff + part, LANES)], norms),
        copies.start(weights.at[:, :, pl.ds(2 * ff, part)], out_w),
        copies.start(context_in, context),
    ]
    for copy in early:
        copy.wait()
    norm_grads[...] = jnp.zeros_like(norm_grads)
    big = 512

    def back_rows(i, at):
        for half in range(halves):
            g_act = nn(g_fed[at, :], down_w[half])
            to = slice(half * ff, (half + 1) * ff)
            g_hidden[at, to] = (g_act * g_hidden[at, to].astype(F32)).astype(BF16)

    each_tile(rows, big, back_rows)
    copies.out(g_hidden, g_hidden_to)
    later.pop(0).wait()
    weight_grad(normed_turned, g_hidden, halves, 1 - place[2], sent)
    copies.out(sent, sent_to)
    for copy in later:
        copy.wait()
    gain0 = norms[0].astype(F32).T[0:1]

    def normed_rows(i, at):
        total = second[at, :]
        for half in range(halves):
            total = total + nt(g_hidden[at, half * ff : (half + 1) * ff], in_w[half])
        second[at, :] = total

    each_tile(rows, big, normed_rows)

    def first_norm(i, at):
        grads = second[at, :]
        rows_unit, scale = unit[at, :], scales[at, 0:1]
        norm_grads[0:1, :] += jnp.sum(grads * rows_unit, axis=0, keepdims=True)
        norm_grads[1:2, :] += jnp.sum(grads, axis=0, keepdims=True)
        first = norm_back(grads, gain0, rows_unit, scale)
        second[at, :] = first
        low = first.astype(BF16)
        g_att[at, :] = low
        g_att_turned[:, at] = low.T

    each_tile(rows, tile, first_norm)
    copies.out(second, g_first_to)
    for half in range(halves):
        g_context[:, half * part : (half + 1) * part] = nn(g_att[...], out_w[half]).astype(BF16)
    copies.out(g_context, g_context_to)
    for half in range(halves):
        g_out[half] = nn(
            g_att_turned[...], context[:, half * part : (half + 1) * part]
        ).astype(BF16)
    copies.out(g_out, g_out_to)
    copies.finish()


def feed_backward(place, fed, context, weights, ff, part):
    rows, width = context.shape
    halves = weights.shape[0]
    grad = (halves, width, ff // 2)
    shapes = [
        ((rows, width), F32), ((rows, width), BF16), ((rows, halves * ff), BF16), (grad, BF16),
        ((halves, width, part), BF16), ((8, width), F32),
    ]
    scratch = [
        ((halves, width, ff), BF16), ((halves, width, ff), BF16), ((halves, width, part), BF16),
        ((halves, width, LANES), BF16), ((rows, halves * ff), BF16), ((rows, width), BF16),
        ((rows, width), F32), ((rows, width), F32),
        ((rows, LANES), F32), ((width, rows), BF16), ((rows, width), BF16),
        ((rows, width), BF16), ((width, rows), BF16), ((rows, width), BF16), (grad, BF16),
        ((halves, width, part), BF16),
    ]
    return pl.pallas_call(
        feed_back_kernel,
        out_shape=tuple(jax.ShapeDtypeStruct(*shape) for shape in shapes),
        in_specs=[SCALARS] + [ANYWHERE] * 8,
        out_specs=tuple([ANYWHERE] * 5 + whole(1)),
        scratch_shapes=[pltpu.VMEM(*shape) for shape in scratch]
        + [pltpu.SemaphoreType.DMA((16,))],
        compiler_params=PARAMS,
        cost_estimate=lasting(27),
        name="feed_backward",
    )(place, *fed, context, weights)


def kept_kernel(place, turned_in, cells_in, kept, turned, cells, sems):
    halves, width, columns = kept.shape
    ff = 2 * columns
    copies = Copies(sems)
    turned_copy = copies.start(turned_in, turned)
    pieces = []
    for half in range(halves):
        start = pl.multiple_of(half * ff + place[2] * columns, columns)
        pieces.append(copies.start(cells_in.at[:, pl.ds(start, columns)], cells.at[half]))
    turned_copy.wait()
    for half in range(halves):
        pieces[half].wait()

        def rows_of(i, at, half=half):
            kept[half, at, :] = nn(turned[at, :], cells[half]).astype(BF16)

        each_tile(width, 384, rows_of)


def kept_grad(place, turned, cells, halves):
    width, rows = turned.shape
    columns = cells.shape[1] // halves // 2
    return pl.pallas_call(
        kept_kernel,
        out_shape=jax.ShapeDtypeStruct((halves, width, columns), BF16),
        in_specs=[SCALARS] + [ANYWHERE] * 2,
        out_specs=whole(1)[0],
        scratch_shapes=[
            pltpu.VMEM((width, rows), BF16),
            pltpu.VMEM((halves, rows, columns), BF16),
            pltpu.SemaphoreType.DMA((3,)),
        ],
        compiler_params=PARAMS,
        cost_estimate=lasting(5),
        name="kept_grad",
    )(place, turned, cells)


def spread_kernel(
    place, turned_in, cells_in, other, one_kept, one_sent, two_kept, two_sent, turned, cells, sems
):
    halves, width, columns = other.shape
    ff = 2 * columns
    upper = width // 2
    quarter = columns // 2
    copies = Copies(sems)
    turned_copy = copies.start(turned_in, turned)
    pieces = []
    for half in range(halves):
        start = pl.multiple_of(half * ff + place[2] * columns, columns)
        pieces.append(copies.start(cells_in.at[:, pl.ds(start, columns)], cells.at[half]))
    turned_copy.wait()
    for piece in pieces:
        piece.wait()
    for out, which in ((one_sent, 1 - place[4]), (one_kept, place[4])):
        at = pl.ds(pl.multiple_of(which * quarter, quarter), quarter)
        for half in range(halves):
            total = nn(turned[:upper], cells[half, :, at]) + other[half, :upper, at].astype(F32)
            out[half] = total.astype(BF16)
    for out, which in ((two_sent, 1 - place[5]), (two_kept, place[5])):
        total = nn(turned[upper:], cells[which]) + other[which, upper:].astype(F32)
        out[0] = total.astype(BF16)


def spread_grad(place, turned, cells, other):
    halves, width, columns = other.shape
    rows = turned.shape[1]
    one = jax.ShapeDtypeStruct((halves, width // 2, columns // 2), BF16)
    two = jax.ShapeDtypeStruct((1, width // 2, columns), BF16)
    return pl.pallas_call(
        spread_kernel,
        out_shape=(one, one, two, two),
        in_specs=[SCALARS] + [ANYWHERE] * 2 + whole(1),
        out_specs=tuple(whole(4)),
        scratch_shapes=[
            pltpu.VMEM((width, rows), BF16),
            pltpu.VMEM((halves, rows, columns), BF16),
            pltpu.SemaphoreType.DMA((3,)),
        ],
        compiler_params=PARAMS,
        cost_estimate=lasting(6),
        name="spread_grad",
    )(place, turned, cells, other)


def flipped(values, axis, bit):
    count = lax.axis_size(axis)
    return lax.ppermute(values, axis, [(i, i ^ bit) for i in range(count)])


def side_of(axis, bit):
    return (lax.axis_index(axis) // bit) % 2


def paired(mine, axis, bit, dim):
    other = flipped(mine, axis, bit)
    both = jnp.zeros(mine.shape[:dim] + (2,) + mine.shape[dim:], mine.dtype)
    side = side_of(axis, bit)
    both = lax.dynamic_update_slice_in_dim(both, jnp.expand_dims(mine, dim), side, dim)
    return lax.dynamic_update_slice_in_dim(both, jnp.expand_dims(other, dim), 1 - side, dim)


def ctx_bits():
    bits, bit = [], 1
    while bit < lax.axis_size("ctx"):
        bits.append(bit)
        bit *= 2
    return bits


def sequence_sum(values):
    width = values.shape[1] // 2
    side = side_of("ctx", 1)
    kept = lax.dynamic_slice_in_dim(values, side * width, width, axis=1)
    sent = lax.dynamic_slice_in_dim(values, (1 - side) * width, width, axis=1)
    kept = kept + flipped(sent, "ctx", 1)
    kept = kept + flipped(kept, "tp", 1)
    for bit in ctx_bits()[1:]:
        kept = kept + flipped(kept, "ctx", bit)
    other = flipped(kept, "ctx", 1)
    return jnp.where(
        side == 0,
        jnp.concatenate([kept, other], axis=1),
        jnp.concatenate([other, kept], axis=1),
    )


def to_owner(kept, sent, combine):
    kept = combine(kept, flipped(sent, "ctx", 1))
    for bit in ctx_bits()[1:]:
        view = kept.reshape((-1, 2) + kept.shape[1:])
        side = side_of("ctx", bit)
        sent = lax.dynamic_index_in_dim(view, 1 - side, 1, False)
        kept = lax.dynamic_index_in_dim(view, side, 1, False)
        kept = combine(kept, flipped(sent, "ctx", bit))
    return kept[0], flipped(kept[0], "tp", 1)


def from_owners(part):
    whole_part = part[None]
    for bit in reversed(ctx_bits()):
        both = paired(whole_part, "ctx", bit, 1)
        whole_part = both.reshape((-1,) + part.shape)
    return whole_part.reshape((-1,) + part.shape[1:])


def merge_keys(one, two):
    size = LANES // 2
    one_top, two_top = one[..., size : size + 1], two[..., size : size + 1]
    top = jnp.maximum(one_top, two_top)
    one_factor, two_factor = jnp.exp(one_top - top), jnp.exp(two_top - top)
    summed = one * one_factor + two * two_factor
    lane = lax.broadcasted_iota(jnp.int32, summed.shape, summed.ndim - 1)
    return jnp.where(lane == size, top, summed)


def neighbour_rows(cells, count):
    pieces = lax.axis_size("ctx") * lax.axis_size("tp")
    up = [(i, i + 1) for i in range(pieces - 1)]
    before = lax.ppermute(cells[-count:], ("ctx", "tp"), up)
    after = lax.ppermute(cells[:count], ("ctx", "tp"), [(j, i) for i, j in up])
    return (
        jnp.pad(before, ((LANES - count, 0), (0, 0))),
        jnp.pad(after, ((0, LANES - count), (0, 0))),
    )


def own_quarter(shard):
    rows = shard.shape[0] // lax.axis_size("ctx")
    return lax.dynamic_slice_in_dim(shard, lax.axis_index("ctx") * rows, rows, axis=0)


def gathered(shard):
    full = lax.all_gather(own_quarter(shard), ("tp", "fsdp", "ctx"), tiled=True)
    return full.reshape(lax.axis_size("tp"), -1, shard.shape[1])


def gathered_early(shard):
    count = lax.axis_size("fsdp")
    piece = own_quarter(shard)
    if count > 4:
        held = lax.all_gather(piece, "fsdp")
    else:
        here = lax.axis_index("fsdp")
        held = jnp.zeros((count,) + piece.shape, piece.dtype)
        held = lax.dynamic_update_slice_in_dim(held, piece[None], here, 0)
        for step in range(1, count):
            moved = lax.ppermute(piece, "fsdp", [(i, (i + step) % count) for i in range(count)])
            held = lax.dynamic_update_slice_in_dim(held, moved[None], (here - step) % count, 0)
    bits = ctx_bits()
    halves = []
    for number, half in enumerate((held[: count // 2], held[count // 2 :])):
        half = half[None]
        if number == 0:
            half = paired(half[0], "tp", 1, 0)
        for place, bit in enumerate(reversed(bits[1:])):
            half = paired(half, "ctx", bit, 2 + place)
        if number == 1:
            half = paired(half[0], "tp", 1, 0)
        halves.append(paired(half, "ctx", bits[0], 1 + len(bits)))
    full = jnp.concatenate(halves, axis=1)
    return full.reshape(lax.axis_size("tp"), -1, shard.shape[1])


def bits_of(axis):
    bits, bit = [], lax.axis_size(axis) // 2
    while bit:
        bits.append(bit)
        bit //= 2
    return bits


def scattered(grads, first):
    labels = [(axis, bit) for axis in ("tp", "fsdp", "ctx") for bit in bits_of(axis)]
    order = [("ctx", 1)] + [label for label in labels if label[0] == first]
    order += [label for label in labels if label[0] != "fsdp"] + labels[::-1]
    rows = grads.shape[1] // (lax.axis_size("fsdp") * lax.axis_size("ctx"))
    kept = grads.reshape((2,) * len(labels) + (rows, grads.shape[2]))
    for label in order:
        if label not in labels:
            continue
        dim = labels.index(label)
        labels.pop(dim)
        side = side_of(*label)
        sent = lax.dynamic_index_in_dim(kept, 1 - side, dim, False)
        kept = lax.dynamic_index_in_dim(kept, side, dim, False).astype(F32)
        kept = (kept + flipped(sent, *label).astype(F32)).astype(BF16)
    return from_owners(kept).astype(F32)


def added(*parts):
    return sum(part.astype(F32) for part in parts).astype(BF16)


def cut(cells, axis, bit, dim):
    size = cells.shape[dim] // 2
    side = side_of(axis, bit)
    return (
        lax.dynamic_slice_in_dim(cells, side * size, size, axis=dim),
        lax.dynamic_slice_in_dim(cells, (1 - side) * size, size, axis=dim),
    )


def gate(*values):
    return lax.optimization_barrier(values)


def dotf(spec, *operands):
    return jnp.einsum(spec, *operands, preferred_element_type=F32)


def taps_round(taps):
    middle = taps.shape[1] // 2
    gap = jnp.zeros((taps.shape[0], LANES - taps.shape[1]), F32)
    return jnp.concatenate([taps[:, middle::-1], gap, taps[:, :middle:-1]], axis=1)


def landmark_bounds(length):
    landmark = jnp.arange(LANDMARKS + 1, dtype=jnp.int32)
    return (landmark * length + LANDMARKS - 1) // LANDMARKS


def landmark_counts_of(length):
    bounds = landmark_bounds(length)
    return (bounds[1:] - bounds[:-1]).astype(F32)[:, None]


def landmark_rows(position, length):
    bounds = landmark_bounds(length)
    inside = (position[:, None] >= bounds[None, :-1]) & (position[:, None] < bounds[None, 1:])
    return inside.astype(BF16)


def on_device(
    tokens,
    lengths,
    qk_weight,
    value_weight,
    out_weight,
    in_weight,
    down_weight,
    norm_gains,
    norm_shifts,
    conv_weight,
    cotangent,
):
    tp_count = lax.axis_size("tp")
    tp_index = lax.axis_index("tp")
    ctx_index = lax.axis_index("ctx")
    _, slot_len, model_width = tokens.shape
    rows = slot_len // tp_count
    local_heads, tap_count = conv_weight.shape
    local_width = value_weight.shape[1]
    ff_width = in_weight.shape[1]
    head_size = local_width // local_heads
    heads = local_heads * tp_count
    owners = lax.axis_size("ctx")
    own_heads = heads // owners
    width = local_width * tp_count
    radius = tap_count // 2
    length = lengths[0]

    own = lax.dynamic_slice_in_dim(tokens[0], tp_index * rows, rows, axis=0)
    own_cotangent = lax.dynamic_slice_in_dim(cotangent[0], tp_index * rows, rows, axis=0)
    first_row = (ctx_index * tp_count + tp_index) * rows
    sides = (side_of("ctx", 1), ctx_index, side_of("ctx", ctx_bits()[-1]), tp_index)
    place = jnp.stack([first_row, length, *sides]).astype(jnp.int32)

    qkv_full = gathered_early(jnp.concatenate([qk_weight[0], qk_weight[1], value_weight], axis=1))
    land_tokens = sequence_sum(token_sums(place, own))
    norm_columns = jnp.concatenate([norm_gains, norm_shifts], axis=0).T
    norm_columns = jnp.pad(norm_columns, ((0, 0), (0, LANES - norm_columns.shape[1])))
    ffn_local = jnp.concatenate([in_weight, down_weight.T, out_weight.T, norm_columns], axis=1)
    ffn_full = gathered(ffn_local)
    tap_weights = paired(conv_weight, "tp", 1, 0).reshape(heads, tap_count).astype(F32)
    base, base_back = taps_round(tap_weights), taps_round(tap_weights[:, ::-1])

    queries, keys, values, v_plain, land_q, land_k = projections(
        place, own, land_tokens, qkv_full, head_size
    )
    v_ends = neighbour_rows(v_plain, radius)
    merged, merged_tp = to_owner(
        *third_parts(place, keys, values, land_q, owners), merge_keys
    )
    kept_v, kept_p = inverse_forward(place, land_q, land_k, owners)
    first, conv = first_and_conv(queries, values, *v_ends, land_k, base)
    merged, own_out = landmark_out(merged, merged_tp, kept_v)
    land_out = from_owners(own_out)
    context = contexts(first, conv, land_out)

    own_output, *fed, active, fed_turned, down_sent, last_norm = feed_forward(
        place, context, own, own_cotangent, ffn_full, ff_width, local_width
    )
    high = ctx_bits()[-1]
    far, near = bits_of("fsdp")[:1], bits_of("fsdp")[1:]
    other_output = flipped(own_output, "tp", 1)
    down_other = flipped(down_sent, "ctx", 1)
    down_kept = kept_grad(place, fed_turned, active, tp_count)
    down_kept, down_other = gate(down_kept, down_other)
    down_mine, down_theirs = cut(down_kept, "ctx", high, 2)
    other_mine, other_theirs = cut(down_other, "ctx", high, 2)
    down_sent = added(down_theirs, other_theirs)
    down_got = flipped(down_sent, "ctx", high)
    fed[0], down_sent = gate(fed[0], down_sent)
    grad_first_res, grad_context, g_hidden, in_sent, grad_out_t, first_norm = feed_backward(
        place, fed, context, ffn_full, ff_width, local_width
    )
    in_sent, grad_context, g_hidden, other_output, down_got = gate(
        in_sent, grad_context, g_hidden, other_output, down_got
    )
    in_other = flipped(in_sent, "ctx", 1)
    g_ends = neighbour_rows(grad_context, radius)
    down = added(down_mine, other_mine, down_got)
    down_mine, down_sent = cut(down, "tp", 1, 0)
    down_got = flipped(down_sent, "tp", 1)
    grad_context, down_sent = gate(grad_context, down_sent)
    land_kept, land_sent, g_lk, g_q = attention_back(
        place, queries, grad_context, land_k, land_out, owners
    )
    land_kept, land_sent, in_other, g_ends = gate(land_kept, land_sent, in_other, g_ends)

    land_other = flipped(land_sent, "ctx", 1)
    one_kept, one_sent, two_kept, two_sent = spread_grad(place, fed[5], g_hidden, in_other)
    one_kept, one_sent, two_kept, two_sent, land_other, down_got = gate(
        one_kept, one_sent, two_kept, two_sent, land_other, down_got
    )
    land_grads = land_kept + land_other
    land_mine, land_theirs = cut(land_grads, "ctx", high, 0)
    land_got = flipped(land_theirs, "ctx", high)
    land_theirs, one_sent, two_sent = gate(land_theirs, one_sent, two_sent)
    one_got = flipped(one_sent, "ctx", high)
    two_got = flipped(two_sent, "tp", 1)
    down = added(down_mine, down_got)
    grad_context, one_sent, two_sent = gate(grad_context, one_sent, two_sent)
    g_conv, g_taps = conv_back(v_plain, v_ends, grad_context, g_ends, base_back)
    g_conv, g_taps, land_got = gate(g_conv, g_taps, land_got)
    own_grads = (land_mine + land_got)[0]
    tp_grads = flipped(own_grads, "tp", 1)

    def parts(cells):
        return cells.reshape(rows, tp_count, local_width)

    def qkv_part(index):
        return qkv_full[:, :, index * local_width : (index + 1) * local_width]

    g_q, own_grads = gate(g_q, own_grads)
    back_q = dotf("tpk,pck->tc", parts(g_q), qkv_part(0)) + grad_first_res
    back_q, tp_grads, one_got, two_got = gate(back_q, tp_grads, one_got, two_got)
    one = added(one_kept, one_got)
    two = added(two_kept, two_got)
    one_mine, one_sent = cut(one, "tp", 1, 0)
    two_mine, two_sent = cut(two, "ctx", high, 2)
    one_got = flipped(one_sent, "tp", 1)
    two_got = flipped(two_sent, "ctx", high)
    own_grads, one_sent, two_sent = gate(own_grads + tp_grads, one_sent, two_sent)
    spread, lq_mid, lk_mid = inverse_backward(
        place, land_q, land_k, merged, own_grads, kept_v, kept_p
    )
    spread, one_got, two_got = gate(spread, one_got, two_got)
    spread = from_owners(spread)

    one, two = added(one_mine, one_got)[0], added(two_mine, two_got)[0]
    pair = jnp.concatenate([jnp.concatenate([one, two], axis=0), down[0]], axis=1)
    for bit in far:
        pair_mine, pair_sent = cut(pair, "fsdp", bit, 0)
        pair_got = flipped(pair_sent, "fsdp", bit)
    grad_q = dotf("tc,tpk->pck", own, parts(g_q))
    spread, pair_sent, grad_q = gate(spread, pair_sent, grad_q)
    g_k, g_v, g_lq = third_back(place, keys, values, land_q, spread, g_conv)
    g_k, g_v, g_lq, pair_got = gate(g_k, g_v, g_lq, pair_got)

    own_columns = own_heads * head_size
    scale = head_size**-0.25

    def with_mid(partial, mid):
        mid = mid.transpose(1, 0, 2).reshape(LANDMARKS, own_columns)
        mid = jnp.where(tp_index == 0, mid, 0.0)
        start = (0, ctx_index * own_columns)
        return partial + lax.dynamic_update_slice(jnp.zeros_like(partial), mid, start)

    land_grads = scale * jnp.concatenate([with_mid(g_lq, lq_mid), with_mid(g_lk, lk_mid)], axis=1)
    counts = landmark_counts_of(length)
    g_kv = jnp.concatenate([parts(g_k), parts(g_v)], axis=2)
    own_grad = (back_q + dotf("tpk,pck->tc", g_kv, qkv_full[:, :, local_width:])).astype(BF16)
    land_total = sequence_sum(land_grads) / counts
    other_grad = flipped(own_grad, "tp", 1)

    pair = added(pair_mine, pair_got)
    for bit in near:
        pair_mine, pair_sent = cut(pair, "fsdp", bit, 0)
        pair = added(pair_mine, flipped(pair_sent, "fsdp", bit))

    means_high, means_low = split(land_tokens / counts)
    grads_high, grads_low = split(land_grads)
    late = dotf(
        "mc,mk->ck",
        jnp.concatenate([means_high, means_high, means_low]),
        jnp.concatenate([grads_high, grads_low, grads_high]),
    )
    late = late.reshape(model_width, 2, tp_count, local_width).transpose(1, 2, 0, 3)
    grad_q = (grad_q + late[0]).astype(BF16)
    grad_kv = dotf("tc,tpk->pck", own, g_kv)
    grad_k = (grad_kv[:, :, :local_width] + late[1]).astype(BF16)
    grad_v = grad_kv[:, :, local_width:].astype(BF16)

    owner_count = lax.axis_size("fsdp")
    owner_rows = model_width // owner_count
    taps_grad = jnp.concatenate([g_taps[:, radius - 1 :: -1], g_taps[:, : -radius - 2 : -1]], axis=1)
    taps_grad = taps_grad.reshape(tp_count, -1)
    tap_columns = -(-taps_grad.shape[1] // owner_rows)
    taps_grad = jnp.pad(taps_grad, ((0, 0), (0, tap_columns * owner_rows - taps_grad.shape[1])))
    taps_grad = jnp.tile(taps_grad.reshape(tp_count, owner_rows, tap_columns), (1, owner_count, 1))
    norm_grads = jnp.stack([first_norm[0], last_norm[0], first_norm[1], last_norm[1]], axis=1)
    small = jnp.concatenate(
        [jnp.broadcast_to(norm_grads[None], (tp_count,) + norm_grads.shape), taps_grad], axis=2
    )
    small = jnp.pad(small, ((0, 0), (0, 0), (0, LANES - small.shape[2]))).astype(BF16)
    rest = scattered(
        jnp.concatenate([grad_q, grad_k, grad_v, grad_out_t, small], axis=2), "ctx"
    )
    grad_qkv, grad_out = rest[:, : 3 * local_width], rest[:, 3 * local_width : 4 * local_width]
    own_small = rest[:, 4 * local_width :]
    grad_taps = own_small[:, 4 : 4 + tap_columns].reshape(-1)[: local_heads * tap_count]

    columns = pair.shape[1] // 2
    pair = from_owners(pair).reshape(owners // 2, 2, owner_rows, 2, columns)
    pair = pair.transpose(3, 2, 1, 0, 4).reshape(2, owner_rows, ff_width).astype(F32)
    grad_in, grad_down = pair[0], pair[1].T

    output = jnp.where(
        tp_index == 0,
        jnp.concatenate([own_output, other_output]),
        jnp.concatenate([other_output, own_output]),
    )[None]
    both_grads = jnp.where(
        tp_index == 0,
        jnp.concatenate([own_grad, other_grad]),
        jnp.concatenate([other_grad, own_grad]),
    )
    total_high, total_low = split(land_total)
    through = dotf(
        "mpk,pck->mc",
        jnp.concatenate([total_high, total_low])
        .reshape(2 * LANDMARKS, 2, tp_count, local_width)
        .transpose(0, 2, 1, 3)
        .reshape(2 * LANDMARKS, tp_count, 2 * local_width),
        qkv_full[:, :, : 2 * local_width],
    )
    through = jnp.concatenate(split(through[:LANDMARKS] + through[LANDMARKS:]))
    position = ctx_index * slot_len + jnp.arange(slot_len, dtype=jnp.int32)
    onehot = landmark_rows(position, length)
    grad_tokens = both_grads.astype(F32) + dotf(
        "tm,mc->tc", jnp.concatenate([onehot, onehot], axis=1), through
    )
    grad_tokens = grad_tokens.reshape(1, slot_len, model_width)
    return (
        output,
        grad_tokens,
        jnp.stack([grad_qkv[:, :local_width], grad_qkv[:, local_width : 2 * local_width]]),
        grad_qkv[:, 2 * local_width :],
        grad_out.T,
        grad_in,
        grad_down,
        own_small[:, :2].T,
        own_small[:, 2:4].T,
        grad_taps.reshape(local_heads, tap_count),
    )


def solution(mesh):
    in_specs = (
        P("fsdp", "ctx", None),
        P("fsdp"),
        P(None, "fsdp", "tp"),
        P("fsdp", "tp"),
        P("tp", "fsdp"),
        P("fsdp", "tp"),
        P("tp", "fsdp"),
        P(None, "fsdp"),
        P(None, "fsdp"),
        P("tp", None),
        P("fsdp", "ctx", None),
    )
    out_specs = (
        P("fsdp", "ctx", None),
        P("fsdp", "ctx", None),
        P(None, "fsdp", "tp"),
        P("fsdp", "tp"),
        P("tp", "fsdp"),
        P("fsdp", "tp"),
        P("tp", "fsdp"),
        P(None, "fsdp"),
        P(None, "fsdp"),
        P("tp", None),
    )
    return jax.shard_map(
        on_device, mesh=mesh, in_specs=in_specs, out_specs=out_specs, check_vma=False
    )
```

```python
import jax
import jax.numpy as jnp
from jax import lax
from jax.experimental import pallas as pl
from jax.experimental.pallas import tpu as pltpu
from jax.sharding import PartitionSpec as P

LANDMARKS = 64
NEWTON = 6
LANES = 128
VMEM_BYTES = 56 * 2**20

HIGH = lax.Precision.HIGHEST
F32 = jnp.float32
BF16 = jnp.bfloat16


def lasting(microseconds):
    return pl.CostEstimate(
        flops=int(microseconds * 1.1535e9), bytes_accessed=int(microseconds * 1e5), transcendentals=0
    )


def nn(left, right):
    return jnp.dot(left, right, preferred_element_type=F32)


def nt(left, right):
    return lax.dot_general(left, right, (((1,), (1,)), ((), ())), preferred_element_type=F32)


def split(wide):
    high = wide.astype(BF16)
    return high, (wide - high.astype(F32)).astype(BF16)


def whole(count):
    return [pl.BlockSpec(memory_space=pltpu.VMEM)] * count


SCALARS = pl.BlockSpec(memory_space=pltpu.SMEM)
PARAMS = pltpu.CompilerParams(vmem_limit_bytes=VMEM_BYTES)


def landmark_onehot(place, rows, landmark_axis):
    shape = (LANDMARKS, rows) if landmark_axis == 0 else (rows, LANDMARKS)
    landmark = lax.broadcasted_iota(jnp.int32, shape, landmark_axis)
    position = place[0] + lax.broadcasted_iota(jnp.int32, shape, 1 - landmark_axis)
    start = lax.shift_right_logical(landmark * place[1] + (LANDMARKS - 1), 6)
    end = lax.shift_right_logical((landmark + 1) * place[1] + (LANDMARKS - 1), 6)
    return jnp.where((position >= start) & (position < end), 1.0, 0.0).astype(BF16)


def live_lanes(place, rows):
    position = place[0] + lax.broadcasted_iota(jnp.int32, (1, rows), 1)
    return position < place[1]


def band(base_row):
    ring = pltpu.roll(jnp.broadcast_to(base_row, (LANES, LANES)), 0, 1, stride=1, stride_axis=0)
    gap = lax.broadcasted_iota(jnp.int32, (LANES, LANES), 0) - lax.broadcasted_iota(
        jnp.int32, (LANES, LANES), 1
    )
    zero = jnp.zeros_like(ring)
    before = jnp.where(gap >= LANES - 16, ring, zero).astype(BF16)
    here = jnp.where(jnp.abs(gap) <= 16, ring, zero).astype(BF16)
    after = jnp.where(gap <= 16 - LANES, ring, zero).astype(BF16)
    return before, here, after


def convolved(blocks, bands):
    before, here, after = bands
    return jnp.concatenate(
        [
            nn(blocks[i], before) + nn(blocks[i + 1], here) + nn(blocks[i + 2], after)
            for i in range(len(blocks) - 2)
        ],
        axis=1,
    )


def token_sums_kernel(place, tokens, sums):
    sums[...] = nn(landmark_onehot(place, tokens.shape[0], 0), tokens[...])


def token_sums(place, tokens):
    return pl.pallas_call(
        token_sums_kernel,
        out_shape=jax.ShapeDtypeStruct((LANDMARKS, tokens.shape[1]), F32),
        in_specs=[SCALARS] + whole(1),
        out_specs=whole(1)[0],
        compiler_params=PARAMS,
        cost_estimate=lasting(2.5),
        name="token_sums",
    )(place, tokens)


def landmark_counts(place):
    landmark = lax.broadcasted_iota(jnp.int32, (LANDMARKS, 1), 0)
    start = lax.shift_right_logical(landmark * place[1] + (LANDMARKS - 1), 6)
    end = lax.shift_right_logical((landmark + 1) * place[1] + (LANDMARKS - 1), 6)
    return (end - start).astype(F32)


def projection_kernel(
    place, tokens, sums, weights, q_out, k_out, v_out, v_plain, land_q, land_k, turned
):
    rows = tokens.shape[0]
    halves, _, packed = weights.shape
    width = packed // 3
    size = land_q.shape[2]
    position = place[0] + lax.broadcasted_iota(jnp.int32, (rows, 1), 0)
    live = jnp.where(position < place[1], 1.0, 0.0)
    scaled = live * 64**-0.25
    means = jnp.concatenate(split(sums[...] / landmark_counts(place)), axis=0)
    cells = tokens[...]
    turned[...] = cells.T
    for half in range(halves):
        for part, out in enumerate((q_out, k_out, v_out)):
            weight = weights[half, :, part * width : (part + 1) * width]
            low = ((live if part == 2 else scaled) * nn(cells, weight)).astype(BF16)
            out[half * width : (half + 1) * width, :] = low.T
            if part == 2:
                v_plain[:, half * width : (half + 1) * width] = low
                continue
            both = nn(means, weight)
            land = (64**-0.25 * (both[:LANDMARKS] + both[LANDMARKS:])).astype(BF16)
            to = land_k if part else land_q
            for head in range(width // size):
                to[half * (width // size) + head] = land[:, head * size : (head + 1) * size]


def projections(place, tokens, sums, weights, size):
    rows = tokens.shape[0]
    width = weights.shape[0] * weights.shape[2] // 3
    turned = jax.ShapeDtypeStruct((width, rows), BF16)
    land = jax.ShapeDtypeStruct((width // size, LANDMARKS, size), BF16)
    return pl.pallas_call(
        projection_kernel,
        out_shape=(turned, turned, turned, jax.ShapeDtypeStruct((rows, width), BF16), land, land)
        + (jax.ShapeDtypeStruct(tokens.shape[::-1], BF16),),
        in_specs=[SCALARS] + whole(3),
        out_specs=tuple(whole(7)),
        compiler_params=PARAMS,
        cost_estimate=lasting(10),
        name="projections",
    )(place, tokens, sums, weights)


def by_owner(place, h, owners, kept, sent, values):
    per = kept.shape[1]
    for owner in range(owners):
        @pl.when((h >= owner * per) & (h < (owner + 1) * per))
        def _(owner=owner):
            mine = place[2] == owner % 2

            @pl.when(mine)
            def _():
                kept[owner // 2, h - owner * per] = values

            @pl.when(jnp.logical_not(mine))
            def _():
                sent[owner // 2, h - owner * per] = values


def third_kernel(place, keys, values, land_q, kept, sent):
    heads = land_q.shape[0]
    size = land_q.shape[2]
    rows = keys.shape[1]
    owners = 2 * kept.shape[0]
    live = live_lanes(place, rows)

    def head(h):
        at = pl.ds(pl.multiple_of(h * size, size), size)
        scores = jnp.where(live, nn(land_q[h], keys[at, :]), -1e30)
        top = jnp.max(scores, axis=1, keepdims=True)
        raised = jnp.where(live, jnp.exp(scores - top), 0.0)
        total = jnp.sum(raised, axis=1, keepdims=True)
        high, low = split(raised)
        value = values[at, :]
        mixed = nt(high, value) + nt(low, value)
        lane = lax.broadcasted_iota(jnp.int32, (LANDMARKS, LANES - size), 1)
        stats = jnp.where(lane == 0, top, jnp.where(lane == 1, total, 0.0))
        by_owner(place, h, owners, kept, sent, jnp.concatenate([mixed, stats], axis=1))

    def pair(i, _):
        head(2 * i)
        head(2 * i + 1)
        return 0

    lax.fori_loop(0, heads // 2, pair, 0)


def owner_parts(heads, owners):
    part = jax.ShapeDtypeStruct((owners // 2, heads // owners, LANDMARKS, LANES), F32)
    return part, part


def third_parts(place, keys, values, land_q, owners):
    return pl.pallas_call(
        third_kernel,
        out_shape=owner_parts(land_q.shape[0], owners),
        in_specs=[SCALARS] + whole(3),
        out_specs=tuple(whole(2)),
        compiler_params=PARAMS,
        cost_estimate=lasting(9),
        name="third_parts",
    )(place, keys, values, land_q)


def dot_high(left, right):
    return jnp.dot(left, right, preferred_element_type=F32, precision=HIGH)


def dot_high_nt(left, right):
    return lax.dot_general(
        left, right, (((1,), (1,)), ((), ())), preferred_element_type=F32, precision=HIGH
    )


def eye():
    row = lax.broadcasted_iota(jnp.int32, (LANDMARKS, LANDMARKS), 0)
    column = lax.broadcasted_iota(jnp.int32, (LANDMARKS, LANDMARKS), 1)
    return jnp.where(row == column, 1.0, 0.0)


def middle_map(land_q, land_k):
    scores = nt(land_q, land_k)
    raised = jnp.exp(scores - jnp.max(scores, axis=1, keepdims=True))
    return raised / jnp.sum(raised, axis=1, keepdims=True)


def inverse_kernel(place, land_q, land_k, kept_v, kept_p):
    heads = range(kept_v.shape[1])
    one = eye()
    own = [place[3] * len(heads) + h for h in heads]
    middle = [middle_map(land_q[h], land_k[h]) for h in own]
    approx = [m.T / jnp.sum(m * m, keepdims=True) for m in middle]
    for turn in range(NEWTON):
        product = [dot_high(middle[h], approx[h]) for h in heads]
        for h in heads:
            kept_v[turn, h] = approx[h]
            kept_p[turn, h] = product[h]
        bracket = [7.0 * one - p for p in product]
        bracket = [15.0 * one - dot_high(product[h], bracket[h]) for h in heads]
        bracket = [13.0 * one - dot_high(product[h], bracket[h]) for h in heads]
        approx = [0.25 * dot_high(approx[h], bracket[h]) for h in heads]
    for h in heads:
        kept_v[NEWTON, h] = approx[h]


def inverse_forward(place, land_q, land_k, owners):
    heads = land_q.shape[0] // owners
    square = (heads, LANDMARKS, LANDMARKS)
    return pl.pallas_call(
        inverse_kernel,
        out_shape=(
            jax.ShapeDtypeStruct((NEWTON + 1,) + square, F32),
            jax.ShapeDtypeStruct((NEWTON,) + square, F32),
        ),
        in_specs=[SCALARS] + whole(2),
        out_specs=tuple(whole(2)),
        compiler_params=PARAMS,
        cost_estimate=lasting(7),
        name="inverse_forward",
    )(place, land_q, land_k)


def merged_keys(one, two, size):
    one_top, two_top = one[:, size : size + 1], two[:, size : size + 1]
    top = jnp.maximum(one_top, two_top)
    summed = one * jnp.exp(one_top - top) + two * jnp.exp(two_top - top)
    lane = lax.broadcasted_iota(jnp.int32, one.shape, 1)
    return jnp.where(lane == size, top, summed)


def land_out_kernel(one, two, kept_v, merged, land_out):
    size = land_out.shape[2]
    for h in range(one.shape[0]):
        both = merged_keys(one[h], two[h], size)
        merged[h] = both
        mixed = both[:, :size] / both[:, size + 1 : size + 2]
        land_out[h] = dot_high(kept_v[NEWTON, h], mixed).astype(BF16)


def landmark_out(one, two, kept_v):
    heads = one.shape[0]
    return pl.pallas_call(
        land_out_kernel,
        out_shape=(
            jax.ShapeDtypeStruct(one.shape, F32),
            jax.ShapeDtypeStruct((heads, LANDMARKS, LANES // 2), BF16),
        ),
        in_specs=whole(3),
        out_specs=tuple(whole(2)),
        compiler_params=PARAMS,
        cost_estimate=lasting(2.2),
        name="landmark_out",
    )(one, two, kept_v)


def inverse_back_kernel(
    place, land_q, land_k, merged, grads, kept_v, kept_p, spread, g_lq, g_lk
):
    heads = range(grads.shape[0])
    size = land_q.shape[2]
    one = eye()
    own = [place[3] * len(heads) + h for h in heads]
    middle = [middle_map(land_q[h], land_k[h]) for h in own]
    turned = [m.T for m in middle]
    g_approx = []
    for h in heads:
        mixed = merged[h][:, :size] / merged[h][:, size + 1 : size + 2]
        g_land = grads[h][:, :size]
        g_approx.append(dot_high_nt(g_land, mixed))
        g_mixed = dot_high(kept_v[NEWTON, h].T, g_land)
        row_dot = jnp.sum(g_mixed * mixed, axis=1, keepdims=True)
        lane = lax.broadcasted_iota(jnp.int32, (LANDMARKS, LANES - size), 1)
        top = merged[h][:, size : size + 1]
        total = merged[h][:, size + 1 : size + 2]
        stats = jnp.where(
            lane == 0, row_dot, jnp.where(lane == 1, top, jnp.where(lane == 2, total, 0.0))
        )
        spread[h] = jnp.concatenate([g_mixed, stats], axis=1)
    g_middle = [jnp.zeros((LANDMARKS, LANDMARKS), F32) for _ in heads]
    for turn in reversed(range(NEWTON)):
        approx = [kept_v[turn, h] for h in heads]
        product = [kept_p[turn, h] for h in heads]
        first = [7.0 * one - p for p in product]
        second = [15.0 * one - dot_high(product[h], first[h]) for h in heads]
        third = [13.0 * one - dot_high(product[h], second[h]) for h in heads]
        g_third = [0.25 * dot_high(approx[h].T, g_approx[h]) for h in heads]
        g_back = [0.25 * dot_high_nt(g_approx[h], third[h]) for h in heads]
        g_product = [-dot_high_nt(g_third[h], second[h]) for h in heads]
        pt = [p.T for p in product]
        g_second = [-dot_high(pt[h], g_third[h]) for h in heads]
        g_product = [g_product[h] - dot_high_nt(g_second[h], first[h]) for h in heads]
        g_product = [g_product[h] + dot_high(pt[h], g_second[h]) for h in heads]
        g_middle = [g_middle[h] + dot_high_nt(g_product[h], approx[h]) for h in heads]
        g_approx = [g_back[h] + dot_high(turned[h], g_product[h]) for h in heads]
    for h in heads:
        m = middle[h]
        size_sum = jnp.sum(m * m, keepdims=True)
        g_size = -jnp.sum(g_approx[h] * turned[h], keepdims=True) / (size_sum * size_sum)
        g_m = g_middle[h] + g_approx[h].T / size_sum + 2.0 * g_size * m
        g_scores = m * (g_m - jnp.sum(g_m * m, axis=1, keepdims=True))
        g_lq[h] = dot_high(g_scores, land_k[own[h]].astype(F32))
        g_lk[h] = dot_high(g_scores.T, land_q[own[h]].astype(F32))


def inverse_backward(place, land_q, land_k, merged, grads, kept_v, kept_p):
    heads = grads.shape[0]
    square = jax.ShapeDtypeStruct((heads,) + land_q.shape[1:], F32)
    return pl.pallas_call(
        inverse_back_kernel,
        out_shape=(jax.ShapeDtypeStruct((heads, LANDMARKS, LANES), F32), square, square),
        in_specs=[SCALARS] + whole(6),
        out_specs=tuple(whole(3)),
        compiler_params=PARAMS,
        cost_estimate=lasting(11.5),
        name="inverse_backward",
    )(place, land_q, land_k, merged, grads, kept_v, kept_p)


def first_map(land_k, queries):
    scores = nn(land_k, queries)
    raised = jnp.exp(scores - jnp.max(scores, axis=0, keepdims=True))
    return raised * (1.0 / jnp.sum(raised, axis=0, keepdims=True))


def head_blocks(cells, ends, at):
    rows = cells.shape[1]
    left, right = ends
    return (
        [left[at, :]]
        + [cells[at, i * LANES : (i + 1) * LANES] for i in range(rows // LANES)]
        + [right[at, :]]
    )


def first_conv_kernel(queries, values, left, right, land_k, base, first, conv, ends):
    heads, _, size = land_k.shape
    ends[0] = left[...].T
    ends[1] = right[...].T

    def head(h):
        at = pl.ds(pl.multiple_of(h * size, size), size)
        first[at, :] = first_map(land_k[h], queries[at, :]).astype(BF16)
        blocks = head_blocks(values, (ends.at[0], ends.at[1]), at)
        conv[at, :] = convolved(blocks, band(base[pl.ds(h, 1), :]))

    def pair(i, _):
        head(2 * i)
        head(2 * i + 1)
        return 0

    lax.fori_loop(0, heads // 2, pair, 0)


def first_and_conv(queries, values, left, right, land_k, base):
    width, rows = queries.shape
    return pl.pallas_call(
        first_conv_kernel,
        out_shape=(
            jax.ShapeDtypeStruct((width, rows), BF16),
            jax.ShapeDtypeStruct((width, rows), F32),
        ),
        in_specs=whole(6),
        out_specs=tuple(whole(2)),
        scratch_shapes=[pltpu.VMEM((2, width, LANES), BF16)],
        compiler_params=PARAMS,
        cost_estimate=lasting(8),
        name="first_and_conv",
    )(queries, values, left, right, land_k, base)


def context_kernel(first, conv, land_out, context):
    heads, _, size = land_out.shape

    def head(h):
        at = pl.ds(pl.multiple_of(h * size, size), size)
        return (nn(land_out[h].T, first[at, :]) + conv[at, :]).astype(BF16)

    def pair(i, _):
        both = jnp.concatenate([head(2 * i), head(2 * i + 1)], axis=0)
        context[:, pl.ds(pl.multiple_of(i * LANES, LANES), LANES)] = both.T
        return 0

    lax.fori_loop(0, heads // 2, pair, 0)


def contexts(first, conv, land_out):
    width, rows = first.shape
    return pl.pallas_call(
        context_kernel,
        out_shape=jax.ShapeDtypeStruct((rows, width), BF16),
        in_specs=whole(3),
        out_specs=whole(1)[0],
        compiler_params=PARAMS,
        cost_estimate=lasting(5.5),
        name="contexts",
    )(first, conv, land_out)


def attention_back_kernel(
    place, queries, grads, land_k, land_out, kept, sent, g_lk, g_query
):
    heads, _, size = land_k.shape
    rows = queries.shape[1]
    owners = 2 * kept.shape[0]
    scaled = jnp.where(live_lanes(place, rows), 64**-0.25, 0.0)

    def pair(i, _):
        lanes = pl.ds(pl.multiple_of(i * LANES, LANES), LANES)
        turned = grads[:, lanes].T
        g_queries, g_keys = [], []
        for side in range(2):
            h = 2 * i + side
            query = queries[pl.ds(pl.multiple_of(h * size, size), size), :]
            g_context = turned[side * size : (side + 1) * size]
            first = first_map(land_k[h], query)
            g_first = nn(land_out[h], g_context)
            inner = jnp.sum(g_first * first, axis=0, keepdims=True)
            g_scores = (first * (g_first - inner)).astype(BF16)
            g_land = nt(first.astype(BF16), g_context)
            g_key = nt(g_scores, query)
            by_owner(place, h, owners, kept, sent, jnp.concatenate([g_land, g_key], axis=1))
            g_keys.append(g_key)
            g_queries.append((scaled * nn(land_k[h].T, g_scores)).astype(BF16))
        g_query[:, lanes] = jnp.concatenate(g_queries, axis=0).T
        g_lk[:, lanes] = jnp.concatenate(g_keys, axis=1)
        return 0

    lax.fori_loop(0, heads // 2, pair, 0)


def attention_back(place, queries, grads, land_k, land_out, owners):
    width, rows = queries.shape
    heads = land_k.shape[0]
    return pl.pallas_call(
        attention_back_kernel,
        out_shape=owner_parts(heads, owners)
        + (
            jax.ShapeDtypeStruct((LANDMARKS, width), F32),
            jax.ShapeDtypeStruct((rows, width), BF16),
        ),
        in_specs=[SCALARS] + whole(4),
        out_specs=tuple(whole(4)),
        compiler_params=PARAMS,
        cost_estimate=lasting(11.4),
        name="attention_back",
    )(place, queries, grads, land_k, land_out)


def conv_back_kernel(
    v_plain, v_left, v_right, grads, g_left, g_right, base_back, g_value, g_taps, ends
):
    heads = g_taps.shape[0]
    rows, width = grads.shape
    size = width // heads
    blocks_in = rows // LANES
    row = lax.broadcasted_iota(jnp.int32, (LANES, LANES), 0)
    column = lax.broadcasted_iota(jnp.int32, (LANES, LANES), 1)
    reverse = jnp.where(row + column == LANES - 1, 1.0, 0.0)
    gap = row - column
    ends[0] = g_left[...].T
    ends[1] = g_right[...].T

    def pair(i, _):
        lanes = pl.ds(pl.multiple_of(i * LANES, LANES), LANES)
        turned = grads[:, lanes].T
        plain = [v_left[LANES - 16 :, lanes]]
        plain += [v_plain[b * LANES : (b + 1) * LANES, lanes] for b in range(blocks_in)]
        plain += [v_right[:16, lanes]]
        for side in range(2):
            h = 2 * i + side
            at = pl.ds(pl.multiple_of(h * size, size), size)
            g_context = turned[side * size : (side + 1) * size]
            blocks = [ends[0, at, :]]
            blocks += [g_context[:, b * LANES : (b + 1) * LANES] for b in range(blocks_in)]
            blocks += [ends[1, at, :]]
            g_value[at, :] = convolved(blocks, band(base_back[pl.ds(h, 1), :]))
            own = (row >= size) == (side == 1)
            here = jnp.zeros((LANES, LANES), F32)
            before = jnp.zeros((16, LANES), F32)
            after = jnp.zeros((16, LANES), F32)
            for b in range(blocks_in):
                piece = turned[:, b * LANES : (b + 1) * LANES]
                masked = jnp.where(own, piece, jnp.zeros_like(piece))
                prior = plain[0] if b == 0 else plain[b][LANES - 16 :]
                later = plain[b + 2][:16]
                here = here + nn(plain[b + 1], masked)
                before = before + nn(prior, masked)
                after = after + nn(later, masked)
            empty = jnp.zeros((LANES - 16, LANES), F32)
            ring = jnp.where(jnp.abs(gap) <= 16, here, 0.0)
            ring = ring + jnp.where(
                gap >= LANES - 16, jnp.concatenate([empty, before], axis=0), 0.0
            )
            ring = ring + jnp.where(
                gap <= 16 - LANES, jnp.concatenate([after, empty], axis=0), 0.0
            )
            straight = pltpu.roll(dot_high(reverse, ring), 0, 1, stride=1, stride_axis=0)
            g_taps[pl.ds(h, 1), :] = jnp.sum(straight, axis=0, keepdims=True)
        return 0

    lax.fori_loop(0, heads // 2, pair, 0)


def conv_back(v_plain, v_ends, grads, g_ends, base_back):
    rows, width = grads.shape
    heads = base_back.shape[0]
    return pl.pallas_call(
        conv_back_kernel,
        out_shape=(
            jax.ShapeDtypeStruct((width, rows), F32),
            jax.ShapeDtypeStruct((heads, LANES), F32),
        ),
        in_specs=whole(7),
        out_specs=tuple(whole(2)),
        scratch_shapes=[pltpu.VMEM((2, width, LANES), BF16)],
        compiler_params=PARAMS,
        cost_estimate=lasting(13.6),
        name="conv_back",
    )(v_plain, *v_ends, grads, *g_ends, base_back)


def third_back_kernel(
    place, keys, values, land_q, spread, g_conv, lq_mid, lk_mid, g_lk, last, first, taps,
    g_k, g_v, sums,
):
    heads, _, size = land_q.shape
    rows, width = g_k.shape
    own_heads = lq_mid.shape[0]
    scale = 64**-0.25
    sums[LANDMARKS:, :] = jnp.zeros((sums.shape[0] - LANDMARKS, 2 * width), F32)
    sums[LANDMARKS : LANDMARKS + 1, :] = last[...]
    sums[LANDMARKS + 1 : LANDMARKS + 2, :] = first[...]
    for h in range(heads):
        sums[LANDMARKS + 2 : LANDMARKS + 3, h * LANES : (h + 1) * LANES] = taps[h : h + 1, :]

    def mid(part, h):
        at = h - place[3] * own_heads
        mine = (at >= 0) & (at < own_heads) & (place[5] == 0)
        inside = jnp.clip(at, 0, own_heads - 1)
        return jnp.where(mine, part[inside], 0.0)

    live = live_lanes(place, rows)
    live_row = jnp.where(live, 1.0, 0.0)
    scaled_row = live_row * 64**-0.25

    def pair(i, _):
        lanes = pl.ds(pl.multiple_of(i * LANES, LANES), LANES)
        g_keys, g_values, g_lqs, lks = [], [], [], []
        for side in range(2):
            h = 2 * i + side
            at = pl.ds(pl.multiple_of(h * size, size), size)
            key, value = keys[at, :], values[at, :]
            pack = spread[h]
            g_mixed = pack[:, :size]
            row_dot = pack[:, size : size + 1]
            top = pack[:, size + 1 : size + 2]
            total = pack[:, size + 2 : size + 3]
            scores = nn(land_q[h], key)
            third = jnp.where(live, jnp.exp(scores - top), 0.0) * (1.0 / total)
            gm_high, gm_low = split(g_mixed)
            g_third = nn(gm_high, value) + nn(gm_low, value)
            g_high, g_low = split(third * (g_third - row_dot))
            g_lqs.append(nt(g_high, key) + nt(g_low, key) + mid(lq_mid, h))
            lks.append(mid(lk_mid, h))
            turned = land_q[h].T
            g_key = nn(turned, g_high) + nn(turned, g_low)
            g_keys.append((scaled_row * g_key).astype(BF16))
            t_high, t_low = split(third)
            gmt_high, gmt_low = split(g_mixed.T)
            g_value = nn(gmt_high, t_high) + nn(gmt_high, t_low) + nn(gmt_low, t_high)
            g_values.append((live_row * (g_value + g_conv[at, :])).astype(BF16))
        g_k[:, lanes] = jnp.concatenate(g_keys, axis=0).T
        g_v[:, lanes] = jnp.concatenate(g_values, axis=0).T
        sums[:LANDMARKS, lanes] = scale * jnp.concatenate(g_lqs, axis=1)
        key_lanes = pl.ds(pl.multiple_of(width + i * LANES, LANES), LANES)
        sums[:LANDMARKS, key_lanes] = scale * (g_lk[:, lanes] + jnp.concatenate(lks, axis=1))
        return 0

    lax.fori_loop(0, heads // 2, pair, 0)


def third_back(place, keys, values, land_q, spread, g_conv, lq_mid, lk_mid, g_lk, *rows_of_sums):
    width, rows = keys.shape
    plain = jax.ShapeDtypeStruct((rows, width), BF16)
    return pl.pallas_call(
        third_back_kernel,
        out_shape=(plain, plain, jax.ShapeDtypeStruct((LANDMARKS + 8, 2 * width), F32)),
        in_specs=[SCALARS] + whole(11),
        out_specs=tuple(whole(3)),
        compiler_params=PARAMS,
        cost_estimate=lasting(12),
        name="third_back",
    )(place, keys, values, land_q, spread, g_conv, lq_mid, lk_mid, g_lk, *rows_of_sums)


def centred_rows(rows):
    centred = rows - jnp.mean(rows, axis=1, keepdims=True)
    scale = lax.rsqrt(jnp.mean(centred * centred, axis=1, keepdims=True) + 1e-05)
    return centred * scale, scale


def norm_back(grads, gain, unit, scale):
    scaled = grads * gain
    inner = jnp.mean(scaled * unit, axis=1, keepdims=True)
    return scale * (scaled - jnp.mean(scaled, axis=1, keepdims=True) - unit * inner)


def gelu_pair(hidden):
    share = 0.5 * (1.0 + lax.erf(hidden * 0.7071067811865476))
    density = jnp.exp(-0.5 * hidden * hidden) * 0.3989422804014327
    return hidden * share, share + hidden * density


class Copies:
    def __init__(self, sems):
        self.sems, self.used, self.open = sems, 0, []

    def start(self, source, target):
        copy = pltpu.make_async_copy(source, target, self.sems.at[self.used])
        self.used += 1
        copy.start()
        return copy

    def out(self, source, target):
        self.open.append(self.start(source, target))

    def finish(self):
        for copy in self.open:
            copy.wait()


def each_tile(count, tile, body):
    def step(i, _):
        body(i, pl.ds(pl.multiple_of(i * tile, tile), tile))
        return 0

    lax.fori_loop(0, count // tile, step, 0)


def weight_grad(turned, cells, halves, which, out):
    ff = cells.shape[1] // halves
    columns = ff // 2
    for half in range(halves):
        from_column = pl.ds(pl.multiple_of(half * ff + which * columns, columns), columns)

        def rows_of(i, at, half=half, from_column=from_column):
            out[half, at, :] = nn(turned[at, :], cells[:, from_column]).astype(BF16)

        each_tile(turned.shape[0], 384, rows_of)


def feed_kernel(
    place, context_in, tokens_in, cotangent_in, weights,
    output_to, slope_to, g_fed_to, g_second_to, unit_to, scale_to, turned_to, active_to, fed_turned_to, sent_to,
    norm_grads, in_w, down_w, out_w, norms, context, tokens, cotangent,
    low, unit, scales, fed, active, slopes, g_fed, g_fed_turned, normed_turned, output, sent,
    sems,
):
    rows, width = tokens.shape
    halves, _, ff = in_w.shape
    part = out_w.shape[2]
    tile = 256
    copies = Copies(sems)
    early = [
        copies.start(weights.at[:, :, pl.ds(2 * ff, part)], out_w),
        copies.start(context_in, context),
        copies.start(tokens_in, tokens),
        copies.start(weights.at[:, :, pl.ds(2 * ff + part, LANES)], norms),
    ]
    in_copy = copies.start(weights.at[:, :, pl.ds(0, ff)], in_w)
    down_copy = copies.start(weights.at[:, :, pl.ds(ff, ff)], down_w)
    cotangent_copy = copies.start(cotangent_in, cotangent)
    for copy in early:
        copy.wait()
    columns = norms[0].astype(F32).T
    gain0, gain1 = columns[0:1], columns[1:2]
    shift0, shift1 = columns[2:3], columns[3:4]
    norm_grads[...] = jnp.zeros_like(norm_grads)

    def project(i, at):
        attended = nt(context[at, :part], out_w[0])
        for half in range(1, halves):
            attended = attended + nt(context[at, half * part : (half + 1) * part], out_w[half])
        rows_unit, scale = centred_rows(tokens[at, :].astype(F32) + attended)
        unit[at, :] = rows_unit
        scales[at, :] = jnp.broadcast_to(scale, (tile, LANES))
        normed = (rows_unit * gain0 + shift0).astype(BF16)
        low[at, :] = normed
        normed_turned[:, at] = normed.T

    each_tile(rows, tile, project)
    copies.out(unit, unit_to)
    copies.out(scales, scale_to)
    copies.out(normed_turned, turned_to)
    in_copy.wait()
    big = 512

    def hidden_rows(i, at):
        for half in range(halves):
            value, slope = gelu_pair(nn(low[at, :], in_w[half]))
            active[at, half * ff : (half + 1) * ff] = value.astype(BF16)
            slopes[at, half * ff : (half + 1) * ff] = slope.astype(BF16)

    each_tile(rows, tile, hidden_rows)
    copies.out(slopes, slope_to)
    copies.out(active, active_to)
    down_copy.wait()

    def fed_rows(i, at):
        total = nt(active[at, :ff], down_w[0])
        for half in range(1, halves):
            total = total + nt(active[at, half * ff : (half + 1) * ff], down_w[half])
        fed[at, :] = total

    each_tile(rows, big, fed_rows)
    cotangent_copy.wait()

    def second_norm(i, at):
        normed = unit[at, :] * gain0 + shift0
        unit1, scale1 = centred_rows(normed + fed[at, :])
        position = place[0] + i * tile + lax.broadcasted_iota(jnp.int32, (tile, 1), 0)
        live = jnp.where(position < place[1], 1.0, 0.0)
        output[at, :] = (live * (unit1 * gain1 + shift1)).astype(BF16)
        grads = live * cotangent[at, :].astype(F32)
        norm_grads[:, :width] += jnp.sum(grads * unit1, axis=0, keepdims=True)
        norm_grads[:, width:] += jnp.sum(grads, axis=0, keepdims=True)
        second = norm_back(grads, gain1, unit1, scale1)
        fed[at, :] = second
        g_low = second.astype(BF16)
        g_fed[at, :] = g_low
        g_fed_turned[:, at] = g_low.T

    each_tile(rows, tile, second_norm)
    copies.out(output, output_to)
    copies.out(fed, g_second_to)
    copies.out(g_fed, g_fed_to)
    copies.out(g_fed_turned, fed_turned_to)
    weight_grad(g_fed_turned, active, halves, 1 - place[2], sent)
    copies.out(sent, sent_to)
    copies.finish()


ANYWHERE = pl.BlockSpec(memory_space=pl.ANY)


def feed_forward(place, context, tokens, cotangent, weights, ff, part):
    rows, width = tokens.shape
    halves = weights.shape[0]
    grad = (halves, width, ff // 2)
    shapes = [
        ((rows, width), BF16), ((rows, halves * ff), BF16), ((rows, width), BF16),
        ((rows, width), F32), ((rows, width), F32), ((rows, LANES), F32), ((width, rows), BF16),
        ((rows, halves * ff), BF16), ((width, rows), BF16), (grad, BF16), ((1, 2 * width), F32),
    ]
    scratch = [
        ((halves, width, ff), BF16), ((halves, width, ff), BF16), ((halves, width, part), BF16),
        ((halves, width, LANES), BF16), ((rows, width), BF16), ((rows, width), BF16),
        ((rows, width), BF16),
        ((rows, width), BF16), ((rows, width), F32), ((rows, LANES), F32), ((rows, width), F32),
        ((rows, halves * ff), BF16), ((rows, halves * ff), BF16), ((rows, width), BF16),
        ((width, rows), BF16), ((width, rows), BF16), ((rows, width), BF16), (grad, BF16),
    ]
    return pl.pallas_call(
        feed_kernel,
        out_shape=tuple(jax.ShapeDtypeStruct(*shape) for shape in shapes),
        in_specs=[SCALARS] + [ANYWHERE] * 4,
        out_specs=tuple([ANYWHERE] * 10 + whole(1)),
        scratch_shapes=[pltpu.VMEM(*shape) for shape in scratch]
        + [pltpu.SemaphoreType.DMA((17,))],
        compiler_params=PARAMS,
        cost_estimate=lasting(29),
        name="feed_forward",
    )(place, context, tokens, cotangent, weights)


def feed_back_kernel(
    place, slope_in, g_fed_in, g_second_in, unit_in, scale_in, turned_in, weights,
    g_first_to, g_context_to, g_hidden_to, sent_to, att_turned_to, norm_grads,
    in_w, down_w, out_w, norms, g_hidden, g_fed, second, unit, scales, normed_turned,
    g_att, g_att_turned, g_context, sent,
    sems,
):
    rows, width = second.shape
    halves, _, ff = in_w.shape
    part = out_w.shape[2]
    tile = 256
    copies = Copies(sems)
    early = [
        copies.start(g_fed_in, g_fed),
        copies.start(weights.at[:, :, pl.ds(ff, ff)], down_w),
        copies.start(slope_in, g_hidden),
    ]
    later = [
        copies.start(turned_in, normed_turned),
        copies.start(weights.at[:, :, pl.ds(0, ff)], in_w),
        copies.start(g_second_in, second),
        copies.start(unit_in, unit),
        copies.start(scale_in, scales),
        copies.start(weights.at[:, :, pl.ds(2 * ff + part, LANES)], norms),
        copies.start(weights.at[:, :, pl.ds(2 * ff, part)], out_w),
    ]
    for copy in early:
        copy.wait()
    norm_grads[...] = jnp.zeros_like(norm_grads)
    big = 512

    def back_rows(i, at):
        for half in range(halves):
            g_act = nn(g_fed[at, :], down_w[half])
            to = slice(half * ff, (half + 1) * ff)
            g_hidden[at, to] = (g_act * g_hidden[at, to].astype(F32)).astype(BF16)

    each_tile(rows, big, back_rows)
    copies.out(g_hidden, g_hidden_to)
    later.pop(0).wait()
    weight_grad(normed_turned, g_hidden, halves, 1 - place[2], sent)
    copies.out(sent, sent_to)
    for copy in later:
        copy.wait()
    gain0 = norms[0].astype(F32).T[0:1]

    def normed_rows(i, at):
        total = second[at, :]
        for half in range(halves):
            total = total + nt(g_hidden[at, half * ff : (half + 1) * ff], in_w[half])
        second[at, :] = total

    each_tile(rows, big, normed_rows)

    def first_norm(i, at):
        grads = second[at, :]
        rows_unit, scale = unit[at, :], scales[at, 0:1]
        norm_grads[:, :width] += jnp.sum(grads * rows_unit, axis=0, keepdims=True)
        norm_grads[:, width:] += jnp.sum(grads, axis=0, keepdims=True)
        first = norm_back(grads, gain0, rows_unit, scale)
        second[at, :] = first
        low = first.astype(BF16)
        g_att[at, :] = low
        g_att_turned[:, at] = low.T

    each_tile(rows, tile, first_norm)
    copies.out(second, g_first_to)
    copies.out(g_att_turned, att_turned_to)
    for half in range(halves):
        g_context[:, half * part : (half + 1) * part] = nn(g_att[...], out_w[half]).astype(BF16)
    copies.out(g_context, g_context_to)
    copies.finish()


def feed_backward(place, fed, weights, ff, part):
    rows, width = fed[1].shape
    halves = weights.shape[0]
    grad = (halves, width, ff // 2)
    shapes = [
        ((rows, width), F32), ((rows, width), BF16), ((rows, halves * ff), BF16), (grad, BF16),
        ((width, rows), BF16), ((1, 2 * width), F32),
    ]
    scratch = [
        ((halves, width, ff), BF16), ((halves, width, ff), BF16), ((halves, width, part), BF16),
        ((halves, width, LANES), BF16), ((rows, halves * ff), BF16), ((rows, width), BF16),
        ((rows, width), F32), ((rows, width), F32),
        ((rows, LANES), F32), ((width, rows), BF16),
        ((rows, width), BF16), ((width, rows), BF16), ((rows, width), BF16), (grad, BF16),
    ]
    return pl.pallas_call(
        feed_back_kernel,
        out_shape=tuple(jax.ShapeDtypeStruct(*shape) for shape in shapes),
        in_specs=[SCALARS] + [ANYWHERE] * 7,
        out_specs=tuple([ANYWHERE] * 5 + whole(1)),
        scratch_shapes=[pltpu.VMEM(*shape) for shape in scratch]
        + [pltpu.SemaphoreType.DMA((16,))],
        compiler_params=PARAMS,
        cost_estimate=lasting(27),
        name="feed_backward",
    )(place, *fed, weights)


def kept_kernel(place, turned_in, cells_in, kept, turned, cells, sems):
    halves, width, columns = kept.shape
    ff = 2 * columns
    copies = Copies(sems)
    turned_copy = copies.start(turned_in, turned)
    pieces = []
    for half in range(halves):
        start = pl.multiple_of(half * ff + place[2] * columns, columns)
        pieces.append(copies.start(cells_in.at[:, pl.ds(start, columns)], cells.at[half]))
    turned_copy.wait()
    for half in range(halves):
        pieces[half].wait()

        def rows_of(i, at, half=half):
            kept[half, at, :] = nn(turned[at, :], cells[half]).astype(BF16)

        each_tile(width, 384, rows_of)


def kept_grad(place, turned, cells, halves):
    width, rows = turned.shape
    columns = cells.shape[1] // halves // 2
    return pl.pallas_call(
        kept_kernel,
        out_shape=jax.ShapeDtypeStruct((halves, width, columns), BF16),
        in_specs=[SCALARS] + [ANYWHERE] * 2,
        out_specs=whole(1)[0],
        scratch_shapes=[
            pltpu.VMEM((width, rows), BF16),
            pltpu.VMEM((halves, rows, columns), BF16),
            pltpu.SemaphoreType.DMA((3,)),
        ],
        compiler_params=PARAMS,
        cost_estimate=lasting(5),
        name="kept_grad",
    )(place, turned, cells)


def spread_kernel(
    place, turned_in, cells_in, other, one_kept, one_sent, two_kept, two_sent, turned, cells, sems
):
    halves, width, columns = other.shape
    ff = 2 * columns
    upper = width // 2
    quarter = columns // 2
    copies = Copies(sems)
    turned_copy = copies.start(turned_in, turned)
    pieces = []
    for half in range(halves):
        start = pl.multiple_of(half * ff + place[2] * columns, columns)
        pieces.append(copies.start(cells_in.at[:, pl.ds(start, columns)], cells.at[half]))
    turned_copy.wait()
    for piece in pieces:
        piece.wait()
    for out, which in ((one_sent, 1 - place[4]), (one_kept, place[4])):
        at = pl.ds(pl.multiple_of(which * quarter, quarter), quarter)
        for half in range(halves):
            total = nn(turned[:upper], cells[half, :, at]) + other[half, :upper, at].astype(F32)
            out[half] = total.astype(BF16)
    for out, which in ((two_sent, 1 - place[5]), (two_kept, place[5])):
        total = nn(turned[upper:], cells[which]) + other[which, upper:].astype(F32)
        out[0] = total.astype(BF16)


def spread_grad(place, turned, cells, other):
    halves, width, columns = other.shape
    rows = turned.shape[1]
    one = jax.ShapeDtypeStruct((halves, width // 2, columns // 2), BF16)
    two = jax.ShapeDtypeStruct((1, width // 2, columns), BF16)
    return pl.pallas_call(
        spread_kernel,
        out_shape=(one, one, two, two),
        in_specs=[SCALARS] + [ANYWHERE] * 2 + whole(1),
        out_specs=tuple(whole(4)),
        scratch_shapes=[
            pltpu.VMEM((width, rows), BF16),
            pltpu.VMEM((halves, rows, columns), BF16),
            pltpu.SemaphoreType.DMA((3,)),
        ],
        compiler_params=PARAMS,
        cost_estimate=lasting(6),
        name="spread_grad",
    )(place, turned, cells, other)


def pair_kernel(place, one_turned, one_cells, two_turned, two_cells, kept, sent):
    halves, _, columns = kept.shape
    families = ((one_turned, one_cells), (two_turned, two_cells))
    for number, (turned, cells) in enumerate(families):
        mine = place[2] == number
        for half in range(halves):
            total = nn(turned[...], cells[:, half * columns : (half + 1) * columns]).astype(BF16)

            @pl.when(mine)
            def _(half=half, total=total):
                kept[half] = total

            @pl.when(jnp.logical_not(mine))
            def _(half=half, total=total):
                sent[half] = total


def pair_grads(place, one_turned, one_cells, two_turned, two_cells, halves):
    width = one_turned.shape[0]
    shape = jax.ShapeDtypeStruct((halves, width, one_cells.shape[1] // halves), BF16)
    return pl.pallas_call(
        pair_kernel,
        out_shape=(shape, shape),
        in_specs=[SCALARS] + whole(4),
        out_specs=tuple(whole(2)),
        compiler_params=PARAMS,
        cost_estimate=lasting(6),
        name="pair_grads",
    )(place, one_turned, one_cells, two_turned, two_cells)


def flipped(values, axis, bit):
    count = lax.axis_size(axis)
    return lax.ppermute(values, axis, [(i, i ^ bit) for i in range(count)])


def side_of(axis, bit):
    return (lax.axis_index(axis) // bit) % 2


def paired(mine, axis, bit, dim):
    other = flipped(mine, axis, bit)
    both = jnp.zeros(mine.shape[:dim] + (2,) + mine.shape[dim:], mine.dtype)
    side = side_of(axis, bit)
    both = lax.dynamic_update_slice_in_dim(both, jnp.expand_dims(mine, dim), side, dim)
    return lax.dynamic_update_slice_in_dim(both, jnp.expand_dims(other, dim), 1 - side, dim)


def ctx_bits():
    bits, bit = [], 1
    while bit < lax.axis_size("ctx"):
        bits.append(bit)
        bit *= 2
    return bits


def sequence_sum(values):
    width = values.shape[1] // 2
    side = side_of("ctx", 1)
    kept = lax.dynamic_slice_in_dim(values, side * width, width, axis=1)
    sent = lax.dynamic_slice_in_dim(values, (1 - side) * width, width, axis=1)
    kept = kept + flipped(sent, "ctx", 1)
    kept = kept + flipped(kept, "tp", 1)
    for bit in ctx_bits()[1:]:
        kept = kept + flipped(kept, "ctx", bit)
    other = flipped(kept, "ctx", 1)
    return jnp.where(
        side == 0,
        jnp.concatenate([kept, other], axis=1),
        jnp.concatenate([other, kept], axis=1),
    )


def to_owner(kept, sent, combine):
    kept = combine(kept, flipped(sent, "ctx", 1))
    for bit in ctx_bits()[1:]:
        view = kept.reshape((-1, 2) + kept.shape[1:])
        side = side_of("ctx", bit)
        sent = lax.dynamic_index_in_dim(view, 1 - side, 1, False)
        kept = lax.dynamic_index_in_dim(view, side, 1, False)
        kept = combine(kept, flipped(sent, "ctx", bit))
    return kept[0], flipped(kept[0], "tp", 1)


def from_owners(part):
    whole_part = part[None]
    for bit in reversed(ctx_bits()):
        both = paired(whole_part, "ctx", bit, 1)
        whole_part = both.reshape((-1,) + part.shape)
    return whole_part.reshape((-1,) + part.shape[1:])


def merge_keys(one, two):
    size = LANES // 2
    one_top, two_top = one[..., size : size + 1], two[..., size : size + 1]
    top = jnp.maximum(one_top, two_top)
    one_factor, two_factor = jnp.exp(one_top - top), jnp.exp(two_top - top)
    summed = one * one_factor + two * two_factor
    lane = lax.broadcasted_iota(jnp.int32, summed.shape, summed.ndim - 1)
    return jnp.where(lane == size, top, summed)


def neighbour_rows(cells, count):
    pieces = lax.axis_size("ctx") * lax.axis_size("tp")
    up = [(i, i + 1) for i in range(pieces - 1)]
    before = lax.ppermute(cells[-count:], ("ctx", "tp"), up)
    after = lax.ppermute(cells[:count], ("ctx", "tp"), [(j, i) for i, j in up])
    return (
        jnp.pad(before, ((LANES - count, 0), (0, 0))),
        jnp.pad(after, ((0, LANES - count), (0, 0))),
    )


def own_quarter(shard):
    rows = shard.shape[0] // lax.axis_size("ctx")
    return lax.dynamic_slice_in_dim(shard, lax.axis_index("ctx") * rows, rows, axis=0)


def gathered(shard):
    full = lax.all_gather(own_quarter(shard), ("tp", "fsdp", "ctx"), tiled=True)
    return full.reshape(lax.axis_size("tp"), -1, shard.shape[1])


def gathered_early(shard):
    count = lax.axis_size("fsdp")
    piece = own_quarter(shard)
    if count > 4:
        held = lax.all_gather(piece, "fsdp")
    else:
        here = lax.axis_index("fsdp")
        held = jnp.zeros((count,) + piece.shape, piece.dtype)
        held = lax.dynamic_update_slice_in_dim(held, piece[None], here, 0)
        for step in range(1, count):
            moved = lax.ppermute(piece, "fsdp", [(i, (i + step) % count) for i in range(count)])
            held = lax.dynamic_update_slice_in_dim(held, moved[None], (here - step) % count, 0)
    bits = ctx_bits()
    halves = []
    for number, half in enumerate((held[: count // 2], held[count // 2 :])):
        half = half[None]
        if number == 0:
            half = paired(half[0], "tp", 1, 0)
        for place, bit in enumerate(reversed(bits[1:])):
            half = paired(half, "ctx", bit, 2 + place)
        if number == 1:
            half = paired(half[0], "tp", 1, 0)
        halves.append(paired(half, "ctx", bits[0], 1 + len(bits)))
    full = jnp.concatenate(halves, axis=1)
    return full.reshape(lax.axis_size("tp"), -1, shard.shape[1])


def bits_of(axis):
    bits, bit = [], lax.axis_size(axis) // 2
    while bit:
        bits.append(bit)
        bit //= 2
    return bits


def added(*parts):
    return sum(part.astype(F32) for part in parts).astype(BF16)


def cut(cells, axis, bit, dim):
    size = cells.shape[dim] // 2
    side = side_of(axis, bit)
    return (
        lax.dynamic_slice_in_dim(cells, side * size, size, axis=dim),
        lax.dynamic_slice_in_dim(cells, (1 - side) * size, size, axis=dim),
    )


def gate(*values):
    return lax.optimization_barrier(values)


def dotf(spec, *operands):
    return jnp.einsum(spec, *operands, preferred_element_type=F32)


def taps_round(taps):
    middle = taps.shape[1] // 2
    gap = jnp.zeros((taps.shape[0], LANES - taps.shape[1]), F32)
    return jnp.concatenate([taps[:, middle::-1], gap, taps[:, :middle:-1]], axis=1)


def landmark_bounds(length):
    landmark = jnp.arange(LANDMARKS + 1, dtype=jnp.int32)
    return (landmark * length + LANDMARKS - 1) // LANDMARKS


def landmark_counts_of(length):
    bounds = landmark_bounds(length)
    return (bounds[1:] - bounds[:-1]).astype(F32)[:, None]


def landmark_rows(position, length):
    bounds = landmark_bounds(length)
    inside = (position[:, None] >= bounds[None, :-1]) & (position[:, None] < bounds[None, 1:])
    return inside.astype(BF16)


def on_device(
    tokens,
    lengths,
    qk_weight,
    value_weight,
    out_weight,
    in_weight,
    down_weight,
    norm_gains,
    norm_shifts,
    conv_weight,
    cotangent,
):
    tp_count = lax.axis_size("tp")
    tp_index = lax.axis_index("tp")
    ctx_index = lax.axis_index("ctx")
    _, slot_len, model_width = tokens.shape
    rows = slot_len // tp_count
    local_heads, tap_count = conv_weight.shape
    local_width = value_weight.shape[1]
    ff_width = in_weight.shape[1]
    head_size = local_width // local_heads
    heads = local_heads * tp_count
    owners = lax.axis_size("ctx")
    own_heads = heads // owners
    width = local_width * tp_count
    radius = tap_count // 2
    length = lengths[0]

    own = lax.dynamic_slice_in_dim(tokens[0], tp_index * rows, rows, axis=0)
    own_cotangent = lax.dynamic_slice_in_dim(cotangent[0], tp_index * rows, rows, axis=0)
    first_row = (ctx_index * tp_count + tp_index) * rows
    sides = (side_of("ctx", 1), ctx_index, side_of("ctx", ctx_bits()[-1]), tp_index)
    place = jnp.stack([first_row, length, *sides]).astype(jnp.int32)

    qkv_full = gathered_early(jnp.concatenate([qk_weight[0], qk_weight[1], value_weight], axis=1))
    land_tokens = sequence_sum(token_sums(place, own))
    norm_columns = jnp.concatenate([norm_gains, norm_shifts], axis=0).T
    norm_columns = jnp.pad(norm_columns, ((0, 0), (0, LANES - norm_columns.shape[1])))
    ffn_local = jnp.concatenate([in_weight, down_weight.T, out_weight.T, norm_columns], axis=1)
    ffn_full = gathered(ffn_local)
    tap_weights = paired(conv_weight, "tp", 1, 0).reshape(heads, tap_count).astype(F32)
    base, base_back = taps_round(tap_weights), taps_round(tap_weights[:, ::-1])

    queries, keys, values, v_plain, land_q, land_k, own_turned = projections(
        place, own, land_tokens, qkv_full, head_size
    )
    v_ends = neighbour_rows(v_plain, radius)
    merged, merged_tp = to_owner(
        *third_parts(place, keys, values, land_q, owners), merge_keys
    )
    kept_v, kept_p = inverse_forward(place, land_q, land_k, owners)
    first, conv = first_and_conv(queries, values, *v_ends, land_k, base)
    merged, own_out = landmark_out(merged, merged_tp, kept_v)
    land_out = from_owners(own_out)
    context = contexts(first, conv, land_out)

    own_output, *fed, active, fed_turned, down_sent, last_norm = feed_forward(
        place, context, own, own_cotangent, ffn_full, ff_width, local_width
    )
    high = ctx_bits()[-1]
    far, *near = bits_of("fsdp")
    other_output = flipped(own_output, "tp", 1)
    down_other = flipped(down_sent, "ctx", 1)
    down_kept = kept_grad(place, fed_turned, active, tp_count)
    down_kept, down_other = gate(down_kept, down_other)
    down_mine, down_theirs = cut(down_kept, "ctx", high, 2)
    other_mine, other_theirs = cut(down_other, "ctx", high, 2)
    down_sent = added(down_theirs, other_theirs)
    down_got = flipped(down_sent, "ctx", high)
    fed[0], down_sent = gate(fed[0], down_sent)
    grad_first_res, grad_context, g_hidden, in_sent, att_turned, first_norm = feed_backward(
        place, fed, ffn_full, ff_width, local_width
    )
    in_sent, grad_context, g_hidden, other_output, down_got = gate(
        in_sent, grad_context, g_hidden, other_output, down_got
    )
    in_other = flipped(in_sent, "ctx", 1)
    g_ends = neighbour_rows(grad_context, radius)
    down = added(down_mine, other_mine, down_got)
    down_mine, down_sent = cut(down, "tp", 1, 0)
    down_got = flipped(down_sent, "tp", 1)
    grad_context, down_sent = gate(grad_context, down_sent)
    land_kept, land_sent, g_lk, g_q = attention_back(
        place, queries, grad_context, land_k, land_out, owners
    )
    land_kept, land_sent, in_other, g_ends = gate(land_kept, land_sent, in_other, g_ends)

    land_other = flipped(land_sent, "ctx", 1)
    one_kept, one_sent, two_kept, two_sent = spread_grad(place, fed[5], g_hidden, in_other)
    one_kept, one_sent, two_kept, two_sent, land_other, down_got = gate(
        one_kept, one_sent, two_kept, two_sent, land_other, down_got
    )
    land_grads = land_kept + land_other
    land_mine, land_theirs = cut(land_grads, "ctx", high, 0)
    land_got = flipped(land_theirs, "ctx", high)
    land_theirs, one_sent, two_sent = gate(land_theirs, one_sent, two_sent)
    one_got = flipped(one_sent, "ctx", high)
    two_got = flipped(two_sent, "tp", 1)
    down = added(down_mine, down_got)
    grad_context, one_sent, two_sent = gate(grad_context, one_sent, two_sent)
    g_conv, g_taps = conv_back(v_plain, v_ends, grad_context, g_ends, base_back)
    g_conv, g_taps, land_got = gate(g_conv, g_taps, land_got)
    own_grads = (land_mine + land_got)[0]
    tp_grads = flipped(own_grads, "tp", 1)

    def parts(cells):
        return cells.reshape(rows, tp_count, local_width)

    def qkv_part(index):
        return qkv_full[:, :, index * local_width : (index + 1) * local_width]

    g_q, own_grads = gate(g_q, own_grads)
    mixed_kept, mixed_sent = pair_grads(place, att_turned, context, own_turned, g_q, tp_count)
    mixed_kept, mixed_sent, tp_grads, one_got, two_got = gate(
        mixed_kept, mixed_sent, tp_grads, one_got, two_got
    )
    one = added(one_kept, one_got)
    two = added(two_kept, two_got)
    one_mine, one_sent = cut(one, "tp", 1, 0)
    two_mine, two_sent = cut(two, "ctx", high, 2)
    one_got = flipped(one_sent, "tp", 1)
    two_got = flipped(two_sent, "ctx", high)
    mixed_got = flipped(mixed_sent, "ctx", 1)
    own_grads, one_sent, two_sent, mixed_sent = gate(
        own_grads + tp_grads, one_sent, two_sent, mixed_sent
    )
    spread, lq_mid, lk_mid = inverse_backward(
        place, land_q, land_k, merged, own_grads, kept_v, kept_p
    )
    spread, one_got, two_got, mixed_got = gate(spread, one_got, two_got, mixed_got)
    spread = from_owners(spread)

    one, two = added(one_mine, one_got)[0], added(two_mine, two_got)[0]
    pair = jnp.concatenate([jnp.concatenate([one, two], axis=0), down[0]], axis=1)
    pair_mine, pair_sent = cut(pair, "fsdp", far, 0)
    pair_got = flipped(pair_sent, "fsdp", far)
    owner_count = lax.axis_size("fsdp")
    owner_rows = model_width // owner_count

    def by_ctx(cells):
        return cells.reshape(tp_count, owner_count, 2, -1, local_width)

    mixed = added(mixed_kept, mixed_got)
    mixed_mine, mixed_sent = cut(by_ctx(mixed), "ctx", high, 2)
    mixed_got = flipped(mixed_sent, "ctx", high)
    spread, pair_sent, mixed_sent = gate(spread, pair_sent, mixed_sent)
    g_k, g_v, sums = third_back(
        place, keys, values, land_q, spread, g_conv, lq_mid, lk_mid, g_lk, last_norm, first_norm,
        g_taps,
    )
    g_k, g_v, sums, pair_got, mixed_got = gate(g_k, g_v, sums, pair_got, mixed_got)

    sums_mine, sums_sent = cut(sums, "ctx", 1, 1)
    sums_got = flipped(sums_sent, "ctx", 1)
    kv_kept, kv_sent = pair_grads(place, own_turned, g_k, own_turned, g_v, tp_count)
    kv_kept, kv_sent, sums_got = gate(kv_kept, kv_sent, sums_got)
    kv_got = flipped(kv_sent, "ctx", 1)
    sums = sums_mine + sums_got
    sums_got = flipped(sums, "tp", 1)
    mixed = added(mixed_mine, mixed_got)
    mixed_mine, mixed_sent = cut(mixed, "tp", 1, 0)
    g_k, kv_sent, sums, mixed_sent = gate(g_k, kv_sent, sums, mixed_sent)
    mixed_got = flipped(mixed_sent, "tp", 1)
    back = (
        grad_first_res
        + dotf("tpk,pck->tc", parts(g_q), qkv_part(0))
        + dotf("tpk,pck->tc", parts(g_k), qkv_part(1))
        + dotf("tpk,pck->tc", parts(g_v), qkv_part(2))
    )
    own_grad = back.astype(BF16)
    own_grad, sums_got, kv_got, mixed_got = gate(own_grad, sums_got, kv_got, mixed_got)
    first_rows = rows // 2
    other_first = flipped(own_grad[:first_rows], "tp", 1)
    sums = sums + sums_got
    sums_got = flipped(sums, "ctx", high)
    kv = added(kv_kept, kv_got)
    kv_mine, kv_sent = cut(by_ctx(kv), "ctx", high, 2)
    sums, kv_sent = gate(sums, kv_sent)
    kv_got = flipped(kv_sent, "ctx", high)

    pair = added(pair_mine, pair_got)
    for bit in near:
        pair_mine, pair_sent = cut(pair, "fsdp", bit, 0)
        pair = added(pair_mine, flipped(pair_sent, "fsdp", bit))

    sums = sums + sums_got
    sums_got = flipped(sums, "ctx", 1)
    sums = jnp.where(
        place[2] == 0,
        jnp.concatenate([sums, sums_got], axis=1),
        jnp.concatenate([sums_got, sums], axis=1),
    )
    kv_got, pair, sums = gate(kv_got, pair, sums)
    kv = added(kv_mine, kv_got)
    kv_mine, kv_sent = cut(kv, "tp", 1, 0)
    kv_got = flipped(kv_sent, "tp", 1)
    own_grad, kv_sent = gate(own_grad, kv_sent)
    other_second = flipped(own_grad[first_rows:], "tp", 1)

    counts = landmark_counts_of(length)
    means = jnp.concatenate(split(land_tokens / counts))
    means = means.reshape(2 * LANDMARKS, owner_count, 2, -1)
    means = lax.dynamic_index_in_dim(means, place[4], 2, False).reshape(2 * LANDMARKS, -1)
    of_half = sums[:LANDMARKS].reshape(LANDMARKS, 2, tp_count, local_width)
    of_half = lax.dynamic_index_in_dim(of_half, tp_index, 2, False)
    core = place[2]
    of_half = jnp.concatenate(
        [jnp.where(core == 1, of_half[:, 0], 0.0), jnp.where(core == 0, of_half[:, 1], 0.0)],
        axis=1,
    )
    half_high, half_low = split(of_half)
    late = dotf(
        "mc,mk->ck",
        jnp.concatenate([means, means[:LANDMARKS]]),
        jnp.concatenate([half_high, half_high, half_low]),
    )
    mixed = jnp.concatenate([added(mixed_mine, mixed_got), added(kv_mine, kv_got)], axis=-1)
    mixed = (mixed.reshape(late.shape).astype(F32) + late).astype(BF16)
    small = sums[LANDMARKS:]
    for bit in (far, *near):
        mixed_mine, mixed_sent = cut(mixed, "fsdp", bit, 0)
        mixed = added(mixed_mine, flipped(mixed_sent, "fsdp", bit))
        small = small + flipped(small, "fsdp", bit)
    mixed = from_owners(mixed).reshape(owners // 2, 2, -1, 2, local_width)
    mixed = mixed.transpose(3, 1, 0, 2, 4).reshape(2, 2, owner_rows, local_width).astype(F32)
    grad_out, grad_q, grad_k, grad_v = mixed[0, 0].T, mixed[0, 1], mixed[1, 0], mixed[1, 1]

    own_columns = lax.axis_index("fsdp") * owner_rows
    norm_sums = small[:2].reshape(2, 2, model_width)[::-1]
    norm_sums = lax.dynamic_slice_in_dim(norm_sums, own_columns, owner_rows, axis=2)
    taps_sum = small[2].reshape(heads, LANES)
    taps_sum = lax.dynamic_slice_in_dim(taps_sum, tp_index * local_heads, local_heads, axis=0)
    grad_taps = jnp.concatenate(
        [taps_sum[:, radius - 1 :: -1], taps_sum[:, : -radius - 2 : -1]], axis=1
    )

    columns = pair.shape[1] // 2
    pair = from_owners(pair).reshape(owners // 2, 2, owner_rows, 2, columns)
    pair = pair.transpose(3, 2, 1, 0, 4).reshape(2, owner_rows, ff_width).astype(F32)
    grad_in, grad_down = pair[0], pair[1].T

    output = jnp.where(
        tp_index == 0,
        jnp.concatenate([own_output, other_output]),
        jnp.concatenate([other_output, own_output]),
    )[None]
    both_grads = jnp.where(
        tp_index == 0,
        jnp.concatenate([own_grad, other_first, other_second]),
        jnp.concatenate([other_first, other_second, own_grad]),
    )
    through = dotf(
        "mpk,pck->mc",
        jnp.concatenate(split(sums[:LANDMARKS] / counts))
        .reshape(2 * LANDMARKS, 2, tp_count, local_width)
        .transpose(0, 2, 1, 3)
        .reshape(2 * LANDMARKS, tp_count, 2 * local_width),
        qkv_full[:, :, : 2 * local_width],
    )
    through = jnp.concatenate(split(through[:LANDMARKS] + through[LANDMARKS:]))
    position = ctx_index * slot_len + jnp.arange(slot_len, dtype=jnp.int32)
    onehot = landmark_rows(position, length)
    grad_tokens = both_grads.astype(F32) + dotf(
        "tm,mc->tc", jnp.concatenate([onehot, onehot], axis=1), through
    )
    grad_tokens = grad_tokens.reshape(1, slot_len, model_width)
    return (
        output,
        grad_tokens,
        jnp.stack([grad_q, grad_k]),
        grad_v,
        grad_out,
        grad_in,
        grad_down,
        norm_sums[:, 0],
        norm_sums[:, 1],
        grad_taps,
    )


def solution(mesh):
    in_specs = (
        P("fsdp", "ctx", None),
        P("fsdp"),
        P(None, "fsdp", "tp"),
        P("fsdp", "tp"),
        P("tp", "fsdp"),
        P("fsdp", "tp"),
        P("tp", "fsdp"),
        P(None, "fsdp"),
        P(None, "fsdp"),
        P("tp", None),
        P("fsdp", "ctx", None),
    )
    out_specs = (
        P("fsdp", "ctx", None),
        P("fsdp", "ctx", None),
        P(None, "fsdp", "tp"),
        P("fsdp", "tp"),
        P("tp", "fsdp"),
        P("fsdp", "tp"),
        P("tp", "fsdp"),
        P(None, "fsdp"),
        P(None, "fsdp"),
        P("tp", None),
    )
    return jax.shard_map(
        on_device, mesh=mesh, in_specs=in_specs, out_specs=out_specs, check_vma=False
    )
```

```python
import jax
import jax.numpy as jnp
from jax import lax
from jax.experimental import pallas as pl
from jax.experimental.pallas import tpu as pltpu
from jax.sharding import PartitionSpec as P

LANDMARKS = 64
NEWTON = 6
LANES = 128
VMEM_BYTES = 56 * 2**20

HIGH = lax.Precision.HIGHEST
F32 = jnp.float32
BF16 = jnp.bfloat16


def lasting(microseconds):
    return pl.CostEstimate(
        flops=int(microseconds * 1.1535e9), bytes_accessed=int(microseconds * 1e5), transcendentals=0
    )


def nn(left, right):
    return jnp.dot(left, right, preferred_element_type=F32)


def nt(left, right):
    return lax.dot_general(left, right, (((1,), (1,)), ((), ())), preferred_element_type=F32)


def split(wide):
    high = wide.astype(BF16)
    return high, (wide - high.astype(F32)).astype(BF16)


def whole(count):
    return [pl.BlockSpec(memory_space=pltpu.VMEM)] * count


SCALARS = pl.BlockSpec(memory_space=pltpu.SMEM)
PARAMS = pltpu.CompilerParams(vmem_limit_bytes=VMEM_BYTES)


def landmark_onehot(place, rows, landmark_axis):
    shape = (LANDMARKS, rows) if landmark_axis == 0 else (rows, LANDMARKS)
    landmark = lax.broadcasted_iota(jnp.int32, shape, landmark_axis)
    position = place[0] + lax.broadcasted_iota(jnp.int32, shape, 1 - landmark_axis)
    start = lax.shift_right_logical(landmark * place[1] + (LANDMARKS - 1), 6)
    end = lax.shift_right_logical((landmark + 1) * place[1] + (LANDMARKS - 1), 6)
    return jnp.where((position >= start) & (position < end), 1.0, 0.0).astype(BF16)


def live_lanes(place, rows):
    position = place[0] + lax.broadcasted_iota(jnp.int32, (1, rows), 1)
    return position < place[1]


def band(base_row):
    ring = pltpu.roll(jnp.broadcast_to(base_row, (LANES, LANES)), 0, 1, stride=1, stride_axis=0)
    gap = lax.broadcasted_iota(jnp.int32, (LANES, LANES), 0) - lax.broadcasted_iota(
        jnp.int32, (LANES, LANES), 1
    )
    zero = jnp.zeros_like(ring)
    before = jnp.where(gap >= LANES - 16, ring, zero).astype(BF16)
    here = jnp.where(jnp.abs(gap) <= 16, ring, zero).astype(BF16)
    after = jnp.where(gap <= 16 - LANES, ring, zero).astype(BF16)
    return before, here, after


def convolved(blocks, bands):
    before, here, after = bands
    return jnp.concatenate(
        [
            nn(blocks[i], before) + nn(blocks[i + 1], here) + nn(blocks[i + 2], after)
            for i in range(len(blocks) - 2)
        ],
        axis=1,
    )


def token_sums_kernel(place, tokens, sums):
    sums[...] = nn(landmark_onehot(place, tokens.shape[0], 0), tokens[...])


def token_sums(place, tokens):
    return pl.pallas_call(
        token_sums_kernel,
        out_shape=jax.ShapeDtypeStruct((LANDMARKS, tokens.shape[1]), F32),
        in_specs=[SCALARS] + whole(1),
        out_specs=whole(1)[0],
        compiler_params=PARAMS,
        cost_estimate=lasting(2.5),
        name="token_sums",
    )(place, tokens)


def landmark_counts(place):
    landmark = lax.broadcasted_iota(jnp.int32, (LANDMARKS, 1), 0)
    start = lax.shift_right_logical(landmark * place[1] + (LANDMARKS - 1), 6)
    end = lax.shift_right_logical((landmark + 1) * place[1] + (LANDMARKS - 1), 6)
    return (end - start).astype(F32)


def projection_kernel(
    place, tokens, sums, weights, q_out, k_out, v_out, v_plain, land_q, land_k, turned
):
    rows = tokens.shape[0]
    halves, _, packed = weights.shape
    width = packed // 3
    size = land_q.shape[2]
    position = place[0] + lax.broadcasted_iota(jnp.int32, (rows, 1), 0)
    live = jnp.where(position < place[1], 1.0, 0.0)
    scaled = live * 64**-0.25
    means = jnp.concatenate(split(sums[...] / landmark_counts(place)), axis=0)
    cells = tokens[...]
    turned[...] = cells.T
    for half in range(halves):
        for part, out in enumerate((q_out, k_out, v_out)):
            weight = weights[half, :, part * width : (part + 1) * width]
            low = ((live if part == 2 else scaled) * nn(cells, weight)).astype(BF16)
            out[half * width : (half + 1) * width, :] = low.T
            if part == 2:
                v_plain[:, half * width : (half + 1) * width] = low
                continue
            both = nn(means, weight)
            land = (64**-0.25 * (both[:LANDMARKS] + both[LANDMARKS:])).astype(BF16)
            to = land_k if part else land_q
            for head in range(width // size):
                to[half * (width // size) + head] = land[:, head * size : (head + 1) * size]


def projections(place, tokens, sums, weights, size):
    rows = tokens.shape[0]
    width = weights.shape[0] * weights.shape[2] // 3
    turned = jax.ShapeDtypeStruct((width, rows), BF16)
    land = jax.ShapeDtypeStruct((width // size, LANDMARKS, size), BF16)
    return pl.pallas_call(
        projection_kernel,
        out_shape=(turned, turned, turned, jax.ShapeDtypeStruct((rows, width), BF16), land, land)
        + (jax.ShapeDtypeStruct(tokens.shape[::-1], BF16),),
        in_specs=[SCALARS] + whole(3),
        out_specs=tuple(whole(7)),
        compiler_params=PARAMS,
        cost_estimate=lasting(10),
        name="projections",
    )(place, tokens, sums, weights)


def by_owner(place, h, owners, kept, sent, values):
    per = kept.shape[1]
    for owner in range(owners):
        @pl.when((h >= owner * per) & (h < (owner + 1) * per))
        def _(owner=owner):
            mine = place[2] == owner % 2

            @pl.when(mine)
            def _():
                kept[owner // 2, h - owner * per] = values

            @pl.when(jnp.logical_not(mine))
            def _():
                sent[owner // 2, h - owner * per] = values


def third_kernel(place, keys, values, land_q, kept, sent):
    heads = land_q.shape[0]
    size = land_q.shape[2]
    rows = keys.shape[1]
    owners = 2 * kept.shape[0]
    live = live_lanes(place, rows)

    def head(h):
        at = pl.ds(pl.multiple_of(h * size, size), size)
        scores = jnp.where(live, nn(land_q[h], keys[at, :]), -1e30)
        top = jnp.max(scores, axis=1, keepdims=True)
        raised = jnp.where(live, jnp.exp(scores - top), 0.0)
        total = jnp.sum(raised, axis=1, keepdims=True)
        high, low = split(raised)
        value = values[at, :]
        mixed = nt(high, value) + nt(low, value)
        lane = lax.broadcasted_iota(jnp.int32, (LANDMARKS, LANES - size), 1)
        stats = jnp.where(lane == 0, top, jnp.where(lane == 1, total, 0.0))
        by_owner(place, h, owners, kept, sent, jnp.concatenate([mixed, stats], axis=1))

    def pair(i, _):
        head(2 * i)
        head(2 * i + 1)
        return 0

    lax.fori_loop(0, heads // 2, pair, 0)


def owner_parts(heads, owners):
    part = jax.ShapeDtypeStruct((owners // 2, heads // owners, LANDMARKS, LANES), F32)
    return part, part


def third_parts(place, keys, values, land_q, owners):
    return pl.pallas_call(
        third_kernel,
        out_shape=owner_parts(land_q.shape[0], owners),
        in_specs=[SCALARS] + whole(3),
        out_specs=tuple(whole(2)),
        compiler_params=PARAMS,
        cost_estimate=lasting(9),
        name="third_parts",
    )(place, keys, values, land_q)


def dot_high(left, right):
    return jnp.dot(left, right, preferred_element_type=F32, precision=HIGH)


def dot_high_nt(left, right):
    return lax.dot_general(
        left, right, (((1,), (1,)), ((), ())), preferred_element_type=F32, precision=HIGH
    )


def eye():
    row = lax.broadcasted_iota(jnp.int32, (LANDMARKS, LANDMARKS), 0)
    column = lax.broadcasted_iota(jnp.int32, (LANDMARKS, LANDMARKS), 1)
    return jnp.where(row == column, 1.0, 0.0)


def middle_map(land_q, land_k):
    scores = nt(land_q, land_k)
    raised = jnp.exp(scores - jnp.max(scores, axis=1, keepdims=True))
    return raised / jnp.sum(raised, axis=1, keepdims=True)


def inverse_kernel(place, land_q, land_k, kept_v, kept_p):
    heads = range(kept_v.shape[1])
    one = eye()
    own = [place[3] * len(heads) + h for h in heads]
    middle = [middle_map(land_q[h], land_k[h]) for h in own]
    approx = [m.T / jnp.sum(m * m, keepdims=True) for m in middle]
    for turn in range(NEWTON):
        product = [dot_high(middle[h], approx[h]) for h in heads]
        for h in heads:
            kept_v[turn, h] = approx[h]
            kept_p[turn, h] = product[h]
        bracket = [7.0 * one - p for p in product]
        bracket = [15.0 * one - dot_high(product[h], bracket[h]) for h in heads]
        bracket = [13.0 * one - dot_high(product[h], bracket[h]) for h in heads]
        approx = [0.25 * dot_high(approx[h], bracket[h]) for h in heads]
    for h in heads:
        kept_v[NEWTON, h] = approx[h]


def inverse_forward(place, land_q, land_k, owners):
    heads = land_q.shape[0] // owners
    square = (heads, LANDMARKS, LANDMARKS)
    return pl.pallas_call(
        inverse_kernel,
        out_shape=(
            jax.ShapeDtypeStruct((NEWTON + 1,) + square, F32),
            jax.ShapeDtypeStruct((NEWTON,) + square, F32),
        ),
        in_specs=[SCALARS] + whole(2),
        out_specs=tuple(whole(2)),
        compiler_params=PARAMS,
        cost_estimate=lasting(7),
        name="inverse_forward",
    )(place, land_q, land_k)


def merged_keys(one, two, size):
    one_top, two_top = one[:, size : size + 1], two[:, size : size + 1]
    top = jnp.maximum(one_top, two_top)
    summed = one * jnp.exp(one_top - top) + two * jnp.exp(two_top - top)
    lane = lax.broadcasted_iota(jnp.int32, one.shape, 1)
    return jnp.where(lane == size, top, summed)


def land_out_kernel(one, two, kept_v, merged, land_out):
    size = land_out.shape[2]
    for h in range(one.shape[0]):
        both = merged_keys(one[h], two[h], size)
        merged[h] = both
        mixed = both[:, :size] / both[:, size + 1 : size + 2]
        land_out[h] = dot_high(kept_v[NEWTON, h], mixed).astype(BF16)


def landmark_out(one, two, kept_v):
    heads = one.shape[0]
    return pl.pallas_call(
        land_out_kernel,
        out_shape=(
            jax.ShapeDtypeStruct(one.shape, F32),
            jax.ShapeDtypeStruct((heads, LANDMARKS, LANES // 2), BF16),
        ),
        in_specs=whole(3),
        out_specs=tuple(whole(2)),
        compiler_params=PARAMS,
        cost_estimate=lasting(2.2),
        name="landmark_out",
    )(one, two, kept_v)


def inverse_back_kernel(
    place, land_q, land_k, merged, grads, kept_v, kept_p, spread, g_lq, g_lk
):
    heads = range(grads.shape[0])
    size = land_q.shape[2]
    one = eye()
    own = [place[3] * len(heads) + h for h in heads]
    middle = [middle_map(land_q[h], land_k[h]) for h in own]
    turned = [m.T for m in middle]
    g_approx = []
    for h in heads:
        mixed = merged[h][:, :size] / merged[h][:, size + 1 : size + 2]
        g_land = grads[h][:, :size]
        g_approx.append(dot_high_nt(g_land, mixed))
        g_mixed = dot_high(kept_v[NEWTON, h].T, g_land)
        row_dot = jnp.sum(g_mixed * mixed, axis=1, keepdims=True)
        lane = lax.broadcasted_iota(jnp.int32, (LANDMARKS, LANES - size), 1)
        top = merged[h][:, size : size + 1]
        total = merged[h][:, size + 1 : size + 2]
        stats = jnp.where(
            lane == 0, row_dot, jnp.where(lane == 1, top, jnp.where(lane == 2, total, 0.0))
        )
        spread[h] = jnp.concatenate([g_mixed, stats], axis=1)
    g_middle = [jnp.zeros((LANDMARKS, LANDMARKS), F32) for _ in heads]
    for turn in reversed(range(NEWTON)):
        approx = [kept_v[turn, h] for h in heads]
        product = [kept_p[turn, h] for h in heads]
        first = [7.0 * one - p for p in product]
        second = [15.0 * one - dot_high(product[h], first[h]) for h in heads]
        third = [13.0 * one - dot_high(product[h], second[h]) for h in heads]
        g_third = [0.25 * dot_high(approx[h].T, g_approx[h]) for h in heads]
        g_back = [0.25 * dot_high_nt(g_approx[h], third[h]) for h in heads]
        g_product = [-dot_high_nt(g_third[h], second[h]) for h in heads]
        pt = [p.T for p in product]
        g_second = [-dot_high(pt[h], g_third[h]) for h in heads]
        g_product = [g_product[h] - dot_high_nt(g_second[h], first[h]) for h in heads]
        g_product = [g_product[h] + dot_high(pt[h], g_second[h]) for h in heads]
        g_middle = [g_middle[h] + dot_high_nt(g_product[h], approx[h]) for h in heads]
        g_approx = [g_back[h] + dot_high(turned[h], g_product[h]) for h in heads]
    for h in heads:
        m = middle[h]
        size_sum = jnp.sum(m * m, keepdims=True)
        g_size = -jnp.sum(g_approx[h] * turned[h], keepdims=True) / (size_sum * size_sum)
        g_m = g_middle[h] + g_approx[h].T / size_sum + 2.0 * g_size * m
        g_scores = m * (g_m - jnp.sum(g_m * m, axis=1, keepdims=True))
        g_lq[h] = dot_high(g_scores, land_k[own[h]].astype(F32))
        g_lk[h] = dot_high(g_scores.T, land_q[own[h]].astype(F32))


def inverse_backward(place, land_q, land_k, merged, grads, kept_v, kept_p):
    heads = grads.shape[0]
    square = jax.ShapeDtypeStruct((heads,) + land_q.shape[1:], F32)
    return pl.pallas_call(
        inverse_back_kernel,
        out_shape=(jax.ShapeDtypeStruct((heads, LANDMARKS, LANES), F32), square, square),
        in_specs=[SCALARS] + whole(6),
        out_specs=tuple(whole(3)),
        compiler_params=PARAMS,
        cost_estimate=lasting(11.5),
        name="inverse_backward",
    )(place, land_q, land_k, merged, grads, kept_v, kept_p)


def first_map(land_k, queries):
    scores = nn(land_k, queries)
    raised = jnp.exp(scores - jnp.max(scores, axis=0, keepdims=True))
    return raised * (1.0 / jnp.sum(raised, axis=0, keepdims=True))


def head_blocks(cells, ends, at):
    rows = cells.shape[1]
    left, right = ends
    return (
        [left[at, :]]
        + [cells[at, i * LANES : (i + 1) * LANES] for i in range(rows // LANES)]
        + [right[at, :]]
    )


def first_conv_kernel(queries, values, left, right, land_k, base, first, conv, ends):
    heads, _, size = land_k.shape
    ends[0] = left[...].T
    ends[1] = right[...].T

    def head(h):
        at = pl.ds(pl.multiple_of(h * size, size), size)
        first[at, :] = first_map(land_k[h], queries[at, :]).astype(BF16)
        blocks = head_blocks(values, (ends.at[0], ends.at[1]), at)
        conv[at, :] = convolved(blocks, band(base[pl.ds(h, 1), :]))

    def pair(i, _):
        head(2 * i)
        head(2 * i + 1)
        return 0

    lax.fori_loop(0, heads // 2, pair, 0)


def first_and_conv(queries, values, left, right, land_k, base):
    width, rows = queries.shape
    return pl.pallas_call(
        first_conv_kernel,
        out_shape=(
            jax.ShapeDtypeStruct((width, rows), BF16),
            jax.ShapeDtypeStruct((width, rows), F32),
        ),
        in_specs=whole(6),
        out_specs=tuple(whole(2)),
        scratch_shapes=[pltpu.VMEM((2, width, LANES), BF16)],
        compiler_params=PARAMS,
        cost_estimate=lasting(8),
        name="first_and_conv",
    )(queries, values, left, right, land_k, base)


def context_kernel(first, conv, land_out, context):
    heads, _, size = land_out.shape

    def head(h):
        at = pl.ds(pl.multiple_of(h * size, size), size)
        return (nn(land_out[h].T, first[at, :]) + conv[at, :]).astype(BF16)

    def pair(i, _):
        both = jnp.concatenate([head(2 * i), head(2 * i + 1)], axis=0)
        context[:, pl.ds(pl.multiple_of(i * LANES, LANES), LANES)] = both.T
        return 0

    lax.fori_loop(0, heads // 2, pair, 0)


def contexts(first, conv, land_out):
    width, rows = first.shape
    return pl.pallas_call(
        context_kernel,
        out_shape=jax.ShapeDtypeStruct((rows, width), BF16),
        in_specs=whole(3),
        out_specs=whole(1)[0],
        compiler_params=PARAMS,
        cost_estimate=lasting(5.5),
        name="contexts",
    )(first, conv, land_out)


def attention_back_kernel(
    place, queries, grads, land_k, land_out, kept, sent, g_lk, g_query
):
    heads, _, size = land_k.shape
    rows = queries.shape[1]
    owners = 2 * kept.shape[0]
    scaled = jnp.where(live_lanes(place, rows), 64**-0.25, 0.0)

    def pair(i, _):
        lanes = pl.ds(pl.multiple_of(i * LANES, LANES), LANES)
        turned = grads[:, lanes].T
        g_queries, g_keys = [], []
        for side in range(2):
            h = 2 * i + side
            query = queries[pl.ds(pl.multiple_of(h * size, size), size), :]
            g_context = turned[side * size : (side + 1) * size]
            first = first_map(land_k[h], query)
            g_first = nn(land_out[h], g_context)
            inner = jnp.sum(g_first * first, axis=0, keepdims=True)
            g_scores = (first * (g_first - inner)).astype(BF16)
            g_land = nt(first.astype(BF16), g_context)
            g_key = nt(g_scores, query)
            by_owner(place, h, owners, kept, sent, jnp.concatenate([g_land, g_key], axis=1))
            g_keys.append(g_key)
            g_queries.append((scaled * nn(land_k[h].T, g_scores)).astype(BF16))
        g_query[:, lanes] = jnp.concatenate(g_queries, axis=0).T
        g_lk[:, lanes] = jnp.concatenate(g_keys, axis=1)
        return 0

    lax.fori_loop(0, heads // 2, pair, 0)


def attention_back(place, queries, grads, land_k, land_out, owners):
    width, rows = queries.shape
    heads = land_k.shape[0]
    return pl.pallas_call(
        attention_back_kernel,
        out_shape=owner_parts(heads, owners)
        + (
            jax.ShapeDtypeStruct((LANDMARKS, width), F32),
            jax.ShapeDtypeStruct((rows, width), BF16),
        ),
        in_specs=[SCALARS] + whole(4),
        out_specs=tuple(whole(4)),
        compiler_params=PARAMS,
        cost_estimate=lasting(11.4),
        name="attention_back",
    )(place, queries, grads, land_k, land_out)


def conv_back_kernel(
    v_plain, v_left, v_right, grads, g_left, g_right, base_back, g_value, g_taps, ends
):
    heads = g_taps.shape[0]
    rows, width = grads.shape
    size = width // heads
    blocks_in = rows // LANES
    row = lax.broadcasted_iota(jnp.int32, (LANES, LANES), 0)
    column = lax.broadcasted_iota(jnp.int32, (LANES, LANES), 1)
    reverse = jnp.where(row + column == LANES - 1, 1.0, 0.0)
    gap = row - column
    ends[0] = g_left[...].T
    ends[1] = g_right[...].T

    def pair(i, _):
        lanes = pl.ds(pl.multiple_of(i * LANES, LANES), LANES)
        turned = grads[:, lanes].T
        plain = [v_left[LANES - 16 :, lanes]]
        plain += [v_plain[b * LANES : (b + 1) * LANES, lanes] for b in range(blocks_in)]
        plain += [v_right[:16, lanes]]
        for side in range(2):
            h = 2 * i + side
            at = pl.ds(pl.multiple_of(h * size, size), size)
            g_context = turned[side * size : (side + 1) * size]
            blocks = [ends[0, at, :]]
            blocks += [g_context[:, b * LANES : (b + 1) * LANES] for b in range(blocks_in)]
            blocks += [ends[1, at, :]]
            g_value[at, :] = convolved(blocks, band(base_back[pl.ds(h, 1), :]))
            own = (row >= size) == (side == 1)
            here = jnp.zeros((LANES, LANES), F32)
            before = jnp.zeros((16, LANES), F32)
            after = jnp.zeros((16, LANES), F32)
            for b in range(blocks_in):
                piece = turned[:, b * LANES : (b + 1) * LANES]
                masked = jnp.where(own, piece, jnp.zeros_like(piece))
                prior = plain[0] if b == 0 else plain[b][LANES - 16 :]
                later = plain[b + 2][:16]
                here = here + nn(plain[b + 1], masked)
                before = before + nn(prior, masked)
                after = after + nn(later, masked)
            empty = jnp.zeros((LANES - 16, LANES), F32)
            ring = jnp.where(jnp.abs(gap) <= 16, here, 0.0)
            ring = ring + jnp.where(
                gap >= LANES - 16, jnp.concatenate([empty, before], axis=0), 0.0
            )
            ring = ring + jnp.where(
                gap <= 16 - LANES, jnp.concatenate([after, empty], axis=0), 0.0
            )
            straight = pltpu.roll(dot_high(reverse, ring), 0, 1, stride=1, stride_axis=0)
            g_taps[pl.ds(h, 1), :] = jnp.sum(straight, axis=0, keepdims=True)
        return 0

    lax.fori_loop(0, heads // 2, pair, 0)


def conv_back(v_plain, v_ends, grads, g_ends, base_back):
    rows, width = grads.shape
    heads = base_back.shape[0]
    return pl.pallas_call(
        conv_back_kernel,
        out_shape=(
            jax.ShapeDtypeStruct((width, rows), F32),
            jax.ShapeDtypeStruct((heads, LANES), F32),
        ),
        in_specs=whole(7),
        out_specs=tuple(whole(2)),
        scratch_shapes=[pltpu.VMEM((2, width, LANES), BF16)],
        compiler_params=PARAMS,
        cost_estimate=lasting(13.6),
        name="conv_back",
    )(v_plain, *v_ends, grads, *g_ends, base_back)


def third_back_kernel(
    place, keys, values, land_q, spread, g_conv, lq_mid, lk_mid, g_lk, last, first, taps,
    g_k, g_v, sums,
):
    heads, _, size = land_q.shape
    rows, width = g_k.shape
    own_heads = lq_mid.shape[0]
    scale = 64**-0.25
    sums[LANDMARKS:, :] = jnp.zeros((sums.shape[0] - LANDMARKS, 2 * width), F32)
    sums[LANDMARKS : LANDMARKS + 1, :] = last[...]
    sums[LANDMARKS + 1 : LANDMARKS + 2, :] = first[...]
    for h in range(heads):
        sums[LANDMARKS + 2 : LANDMARKS + 3, h * LANES : (h + 1) * LANES] = taps[h : h + 1, :]

    def mid(part, h):
        at = h - place[3] * own_heads
        mine = (at >= 0) & (at < own_heads) & (place[5] == 0)
        inside = jnp.clip(at, 0, own_heads - 1)
        return jnp.where(mine, part[inside], 0.0)

    live = live_lanes(place, rows)
    live_row = jnp.where(live, 1.0, 0.0)
    scaled_row = live_row * 64**-0.25

    def pair(i, _):
        lanes = pl.ds(pl.multiple_of(i * LANES, LANES), LANES)
        g_keys, g_values, g_lqs, lks = [], [], [], []
        for side in range(2):
            h = 2 * i + side
            at = pl.ds(pl.multiple_of(h * size, size), size)
            key, value = keys[at, :], values[at, :]
            pack = spread[h]
            g_mixed = pack[:, :size]
            row_dot = pack[:, size : size + 1]
            top = pack[:, size + 1 : size + 2]
            total = pack[:, size + 2 : size + 3]
            scores = nn(land_q[h], key)
            third = jnp.where(live, jnp.exp(scores - top), 0.0) * (1.0 / total)
            gm_high, gm_low = split(g_mixed)
            g_third = nn(gm_high, value) + nn(gm_low, value)
            g_high, g_low = split(third * (g_third - row_dot))
            g_lqs.append(nt(g_high, key) + nt(g_low, key) + mid(lq_mid, h))
            lks.append(mid(lk_mid, h))
            turned = land_q[h].T
            g_key = nn(turned, g_high) + nn(turned, g_low)
            g_keys.append((scaled_row * g_key).astype(BF16))
            t_high, t_low = split(third)
            gmt_high, gmt_low = split(g_mixed.T)
            g_value = nn(gmt_high, t_high) + nn(gmt_high, t_low) + nn(gmt_low, t_high)
            g_values.append((live_row * (g_value + g_conv[at, :])).astype(BF16))
        g_k[:, lanes] = jnp.concatenate(g_keys, axis=0).T
        g_v[:, lanes] = jnp.concatenate(g_values, axis=0).T
        sums[:LANDMARKS, lanes] = scale * jnp.concatenate(g_lqs, axis=1)
        key_lanes = pl.ds(pl.multiple_of(width + i * LANES, LANES), LANES)
        sums[:LANDMARKS, key_lanes] = scale * (g_lk[:, lanes] + jnp.concatenate(lks, axis=1))
        return 0

    lax.fori_loop(0, heads // 2, pair, 0)


def third_back(place, keys, values, land_q, spread, g_conv, lq_mid, lk_mid, g_lk, *rows_of_sums):
    width, rows = keys.shape
    plain = jax.ShapeDtypeStruct((rows, width), BF16)
    return pl.pallas_call(
        third_back_kernel,
        out_shape=(plain, plain, jax.ShapeDtypeStruct((LANDMARKS + 8, 2 * width), F32)),
        in_specs=[SCALARS] + whole(11),
        out_specs=tuple(whole(3)),
        compiler_params=PARAMS,
        cost_estimate=lasting(12),
        name="third_back",
    )(place, keys, values, land_q, spread, g_conv, lq_mid, lk_mid, g_lk, *rows_of_sums)


def centred_rows(rows):
    centred = rows - jnp.mean(rows, axis=1, keepdims=True)
    scale = lax.rsqrt(jnp.mean(centred * centred, axis=1, keepdims=True) + 1e-05)
    return centred * scale, scale


def norm_back(grads, gain, unit, scale):
    scaled = grads * gain
    inner = jnp.mean(scaled * unit, axis=1, keepdims=True)
    return scale * (scaled - jnp.mean(scaled, axis=1, keepdims=True) - unit * inner)


def gelu_pair(hidden):
    share = 0.5 * (1.0 + lax.erf(hidden * 0.7071067811865476))
    density = jnp.exp(-0.5 * hidden * hidden) * 0.3989422804014327
    return hidden * share, share + hidden * density


class Copies:
    def __init__(self, sems):
        self.sems, self.used, self.open = sems, 0, []

    def start(self, source, target):
        copy = pltpu.make_async_copy(source, target, self.sems.at[self.used])
        self.used += 1
        copy.start()
        return copy

    def out(self, source, target):
        self.open.append(self.start(source, target))

    def finish(self):
        for copy in self.open:
            copy.wait()


def each_tile(count, tile, body):
    def step(i, _):
        body(i, pl.ds(pl.multiple_of(i * tile, tile), tile))
        return 0

    lax.fori_loop(0, count // tile, step, 0)


def weight_grad(turned, cells, halves, which, out):
    ff = cells.shape[1] // halves
    columns = ff // 2
    for half in range(halves):
        from_column = pl.ds(pl.multiple_of(half * ff + which * columns, columns), columns)

        def rows_of(i, at, half=half, from_column=from_column):
            out[half, at, :] = nn(turned[at, :], cells[:, from_column]).astype(BF16)

        each_tile(turned.shape[0], 384, rows_of)


def feed_kernel(
    place, context_in, tokens_in, cotangent_in, weights,
    output_to, slope_to, g_fed_to, g_second_to, unit_to, scale_to, turned_to, active_to, fed_turned_to, sent_to,
    norm_grads, in_w, down_w, out_w, norms, context, tokens, cotangent,
    low, unit, scales, fed, active, slopes, g_fed, g_fed_turned, normed_turned, output, sent,
    sems,
):
    rows, width = tokens.shape
    halves, _, ff = in_w.shape
    part = out_w.shape[2]
    tile = 256
    copies = Copies(sems)
    early = [
        copies.start(weights.at[:, :, pl.ds(2 * ff, part)], out_w),
        copies.start(context_in, context),
        copies.start(tokens_in, tokens),
        copies.start(weights.at[:, :, pl.ds(2 * ff + part, LANES)], norms),
    ]
    in_copy = copies.start(weights.at[:, :, pl.ds(0, ff)], in_w)
    down_copy = copies.start(weights.at[:, :, pl.ds(ff, ff)], down_w)
    cotangent_copy = copies.start(cotangent_in, cotangent)
    for copy in early:
        copy.wait()
    columns = norms[0].astype(F32).T
    gain0, gain1 = columns[0:1], columns[1:2]
    shift0, shift1 = columns[2:3], columns[3:4]
    norm_grads[...] = jnp.zeros_like(norm_grads)

    def project(i, at):
        attended = nt(context[at, :part], out_w[0])
        for half in range(1, halves):
            attended = attended + nt(context[at, half * part : (half + 1) * part], out_w[half])
        rows_unit, scale = centred_rows(tokens[at, :].astype(F32) + attended)
        unit[at, :] = rows_unit
        scales[at, :] = jnp.broadcast_to(scale, (tile, LANES))
        normed = (rows_unit * gain0 + shift0).astype(BF16)
        low[at, :] = normed
        normed_turned[:, at] = normed.T

    each_tile(rows, tile, project)
    copies.out(unit, unit_to)
    copies.out(scales, scale_to)
    copies.out(normed_turned, turned_to)
    in_copy.wait()
    big = 512

    def hidden_rows(i, at):
        for half in range(halves):
            value, slope = gelu_pair(nn(low[at, :], in_w[half]))
            active[at, half * ff : (half + 1) * ff] = value.astype(BF16)
            slopes[at, half * ff : (half + 1) * ff] = slope.astype(BF16)

    each_tile(rows, tile, hidden_rows)
    copies.out(slopes, slope_to)
    copies.out(active, active_to)
    down_copy.wait()

    def fed_rows(i, at):
        total = nt(active[at, :ff], down_w[0])
        for half in range(1, halves):
            total = total + nt(active[at, half * ff : (half + 1) * ff], down_w[half])
        fed[at, :] = total

    each_tile(rows, big, fed_rows)
    cotangent_copy.wait()

    def second_norm(i, at):
        normed = unit[at, :] * gain0 + shift0
        unit1, scale1 = centred_rows(normed + fed[at, :])
        position = place[0] + i * tile + lax.broadcasted_iota(jnp.int32, (tile, 1), 0)
        live = jnp.where(position < place[1], 1.0, 0.0)
        output[at, :] = (live * (unit1 * gain1 + shift1)).astype(BF16)
        grads = live * cotangent[at, :].astype(F32)
        norm_grads[:, :width] += jnp.sum(grads * unit1, axis=0, keepdims=True)
        norm_grads[:, width:] += jnp.sum(grads, axis=0, keepdims=True)
        second = norm_back(grads, gain1, unit1, scale1)
        fed[at, :] = second
        g_low = second.astype(BF16)
        g_fed[at, :] = g_low
        g_fed_turned[:, at] = g_low.T

    each_tile(rows, tile, second_norm)
    copies.out(output, output_to)
    copies.out(fed, g_second_to)
    copies.out(g_fed, g_fed_to)
    copies.out(g_fed_turned, fed_turned_to)
    weight_grad(g_fed_turned, active, halves, 1 - place[2], sent)
    copies.out(sent, sent_to)
    copies.finish()


ANYWHERE = pl.BlockSpec(memory_space=pl.ANY)


def feed_forward(place, context, tokens, cotangent, weights, ff, part):
    rows, width = tokens.shape
    halves = weights.shape[0]
    grad = (halves, width, ff // 2)
    shapes = [
        ((rows, width), BF16), ((rows, halves * ff), BF16), ((rows, width), BF16),
        ((rows, width), F32), ((rows, width), F32), ((rows, LANES), F32), ((width, rows), BF16),
        ((rows, halves * ff), BF16), ((width, rows), BF16), (grad, BF16), ((1, 2 * width), F32),
    ]
    scratch = [
        ((halves, width, ff), BF16), ((halves, width, ff), BF16), ((halves, width, part), BF16),
        ((halves, width, LANES), BF16), ((rows, width), BF16), ((rows, width), BF16),
        ((rows, width), BF16),
        ((rows, width), BF16), ((rows, width), F32), ((rows, LANES), F32), ((rows, width), F32),
        ((rows, halves * ff), BF16), ((rows, halves * ff), BF16), ((rows, width), BF16),
        ((width, rows), BF16), ((width, rows), BF16), ((rows, width), BF16), (grad, BF16),
    ]
    return pl.pallas_call(
        feed_kernel,
        out_shape=tuple(jax.ShapeDtypeStruct(*shape) for shape in shapes),
        in_specs=[SCALARS] + [ANYWHERE] * 4,
        out_specs=tuple([ANYWHERE] * 10 + whole(1)),
        scratch_shapes=[pltpu.VMEM(*shape) for shape in scratch]
        + [pltpu.SemaphoreType.DMA((17,))],
        compiler_params=PARAMS,
        cost_estimate=lasting(29),
        name="feed_forward",
    )(place, context, tokens, cotangent, weights)


def feed_back_kernel(
    place, slope_in, g_fed_in, g_second_in, unit_in, scale_in, turned_in, weights,
    g_first_to, g_context_to, g_hidden_to, sent_to, att_turned_to, norm_grads,
    in_w, down_w, out_w, norms, g_hidden, g_fed, second, unit, scales, normed_turned,
    g_att, g_att_turned, g_context, sent,
    sems,
):
    rows, width = second.shape
    halves, _, ff = in_w.shape
    part = out_w.shape[2]
    tile = 256
    copies = Copies(sems)
    early = [
        copies.start(g_fed_in, g_fed),
        copies.start(weights.at[:, :, pl.ds(ff, ff)], down_w),
        copies.start(slope_in, g_hidden),
    ]
    later = [
        copies.start(turned_in, normed_turned),
        copies.start(weights.at[:, :, pl.ds(0, ff)], in_w),
        copies.start(g_second_in, second),
        copies.start(unit_in, unit),
        copies.start(scale_in, scales),
        copies.start(weights.at[:, :, pl.ds(2 * ff + part, LANES)], norms),
        copies.start(weights.at[:, :, pl.ds(2 * ff, part)], out_w),
    ]
    for copy in early:
        copy.wait()
    norm_grads[...] = jnp.zeros_like(norm_grads)
    big = 512

    def back_rows(i, at):
        for half in range(halves):
            g_act = nn(g_fed[at, :], down_w[half])
            to = slice(half * ff, (half + 1) * ff)
            g_hidden[at, to] = (g_act * g_hidden[at, to].astype(F32)).astype(BF16)

    each_tile(rows, big, back_rows)
    copies.out(g_hidden, g_hidden_to)
    later.pop(0).wait()
    weight_grad(normed_turned, g_hidden, halves, 1 - place[2], sent)
    copies.out(sent, sent_to)
    for copy in later:
        copy.wait()
    gain0 = norms[0].astype(F32).T[0:1]

    def normed_rows(i, at):
        total = second[at, :]
        for half in range(halves):
            total = total + nt(g_hidden[at, half * ff : (half + 1) * ff], in_w[half])
        second[at, :] = total

    each_tile(rows, big, normed_rows)

    def first_norm(i, at):
        grads = second[at, :]
        rows_unit, scale = unit[at, :], scales[at, 0:1]
        norm_grads[:, :width] += jnp.sum(grads * rows_unit, axis=0, keepdims=True)
        norm_grads[:, width:] += jnp.sum(grads, axis=0, keepdims=True)
        first = norm_back(grads, gain0, rows_unit, scale)
        second[at, :] = first
        low = first.astype(BF16)
        g_att[at, :] = low
        g_att_turned[:, at] = low.T

    each_tile(rows, tile, first_norm)
    copies.out(second, g_first_to)
    copies.out(g_att_turned, att_turned_to)
    for half in range(halves):
        g_context[:, half * part : (half + 1) * part] = nn(g_att[...], out_w[half]).astype(BF16)
    copies.out(g_context, g_context_to)
    copies.finish()


def feed_backward(place, fed, weights, ff, part):
    rows, width = fed[1].shape
    halves = weights.shape[0]
    grad = (halves, width, ff // 2)
    shapes = [
        ((rows, width), F32), ((rows, width), BF16), ((rows, halves * ff), BF16), (grad, BF16),
        ((width, rows), BF16), ((1, 2 * width), F32),
    ]
    scratch = [
        ((halves, width, ff), BF16), ((halves, width, ff), BF16), ((halves, width, part), BF16),
        ((halves, width, LANES), BF16), ((rows, halves * ff), BF16), ((rows, width), BF16),
        ((rows, width), F32), ((rows, width), F32),
        ((rows, LANES), F32), ((width, rows), BF16),
        ((rows, width), BF16), ((width, rows), BF16), ((rows, width), BF16), (grad, BF16),
    ]
    return pl.pallas_call(
        feed_back_kernel,
        out_shape=tuple(jax.ShapeDtypeStruct(*shape) for shape in shapes),
        in_specs=[SCALARS] + [ANYWHERE] * 7,
        out_specs=tuple([ANYWHERE] * 5 + whole(1)),
        scratch_shapes=[pltpu.VMEM(*shape) for shape in scratch]
        + [pltpu.SemaphoreType.DMA((16,))],
        compiler_params=PARAMS,
        cost_estimate=lasting(27),
        name="feed_backward",
    )(place, *fed, weights)


def kept_kernel(place, turned_in, cells_in, kept, turned, cells, sems):
    halves, width, columns = kept.shape
    ff = 2 * columns
    copies = Copies(sems)
    turned_copy = copies.start(turned_in, turned)
    pieces = []
    for half in range(halves):
        start = pl.multiple_of(half * ff + place[2] * columns, columns)
        pieces.append(copies.start(cells_in.at[:, pl.ds(start, columns)], cells.at[half]))
    turned_copy.wait()
    for half in range(halves):
        pieces[half].wait()

        def rows_of(i, at, half=half):
            kept[half, at, :] = nn(turned[at, :], cells[half]).astype(BF16)

        each_tile(width, 384, rows_of)


def kept_grad(place, turned, cells, halves):
    width, rows = turned.shape
    columns = cells.shape[1] // halves // 2
    return pl.pallas_call(
        kept_kernel,
        out_shape=jax.ShapeDtypeStruct((halves, width, columns), BF16),
        in_specs=[SCALARS] + [ANYWHERE] * 2,
        out_specs=whole(1)[0],
        scratch_shapes=[
            pltpu.VMEM((width, rows), BF16),
            pltpu.VMEM((halves, rows, columns), BF16),
            pltpu.SemaphoreType.DMA((3,)),
        ],
        compiler_params=PARAMS,
        cost_estimate=lasting(5),
        name="kept_grad",
    )(place, turned, cells)


def spread_kernel(
    place, turned_in, cells_in, other, one_kept, one_sent, two_kept, two_sent, turned, cells, sems
):
    halves, width, columns = other.shape
    ff = 2 * columns
    upper = width // 2
    quarter = columns // 2
    copies = Copies(sems)
    turned_copy = copies.start(turned_in, turned)
    pieces = []
    for half in range(halves):
        start = pl.multiple_of(half * ff + place[2] * columns, columns)
        pieces.append(copies.start(cells_in.at[:, pl.ds(start, columns)], cells.at[half]))
    turned_copy.wait()
    for piece in pieces:
        piece.wait()
    for out, which in ((one_sent, 1 - place[4]), (one_kept, place[4])):
        at = pl.ds(pl.multiple_of(which * quarter, quarter), quarter)
        for half in range(halves):
            total = nn(turned[:upper], cells[half, :, at]) + other[half, :upper, at].astype(F32)
            out[half] = total.astype(BF16)
    for out, which in ((two_sent, 1 - place[5]), (two_kept, place[5])):
        total = nn(turned[upper:], cells[which]) + other[which, upper:].astype(F32)
        out[0] = total.astype(BF16)


def spread_grad(place, turned, cells, other):
    halves, width, columns = other.shape
    rows = turned.shape[1]
    one = jax.ShapeDtypeStruct((halves, width // 2, columns // 2), BF16)
    two = jax.ShapeDtypeStruct((1, width // 2, columns), BF16)
    return pl.pallas_call(
        spread_kernel,
        out_shape=(one, one, two, two),
        in_specs=[SCALARS] + [ANYWHERE] * 2 + whole(1),
        out_specs=tuple(whole(4)),
        scratch_shapes=[
            pltpu.VMEM((width, rows), BF16),
            pltpu.VMEM((halves, rows, columns), BF16),
            pltpu.SemaphoreType.DMA((3,)),
        ],
        compiler_params=PARAMS,
        cost_estimate=lasting(6),
        name="spread_grad",
    )(place, turned, cells, other)


def pair_kernel(
    place, one_turned_in, one_cells_in, two_turned_in, two_cells_in, kept, sent,
    one_turned, one_cells, two_turned, two_cells, sems,
):
    halves, width, columns = kept.shape
    copies = Copies(sems)
    loads = [
        copies.start(*pair)
        for pair in (
            (one_turned_in, one_turned), (one_cells_in, one_cells),
            (two_turned_in, two_turned), (two_cells_in, two_cells),
        )
    ]
    for number, (turned, cells) in enumerate(((one_turned, one_cells), (two_turned, two_cells))):
        loads[2 * number].wait()
        loads[2 * number + 1].wait()
        mine = place[2] == number

        def rows_of(i, at, turned=turned, cells=cells, mine=mine):
            total = nn(turned[at, :], cells[...]).astype(BF16)

            @pl.when(mine)
            def _():
                for half in range(halves):
                    kept[half, at, :] = total[:, half * columns : (half + 1) * columns]

            @pl.when(jnp.logical_not(mine))
            def _():
                for half in range(halves):
                    sent[half, at, :] = total[:, half * columns : (half + 1) * columns]

        each_tile(width, 384, rows_of)


def pair_grads(place, one_turned, one_cells, two_turned, two_cells, halves):
    width, rows = one_turned.shape
    shape = jax.ShapeDtypeStruct((halves, width, one_cells.shape[1] // halves), BF16)
    return pl.pallas_call(
        pair_kernel,
        out_shape=(shape, shape),
        in_specs=[SCALARS] + [ANYWHERE] * 4,
        out_specs=tuple(whole(2)),
        scratch_shapes=[
            pltpu.VMEM((width, rows), BF16), pltpu.VMEM(one_cells.shape, BF16),
            pltpu.VMEM((width, rows), BF16), pltpu.VMEM(one_cells.shape, BF16),
            pltpu.SemaphoreType.DMA((4,)),
        ],
        compiler_params=PARAMS,
        cost_estimate=lasting(6),
        name="pair_grads",
    )(place, one_turned, one_cells, two_turned, two_cells)


def rank_kernel(place, mine, got, land_tokens, weights, late, through):
    halves, width, _ = weights.shape
    part = late.shape[1] // 2
    first = place[2] == 0
    grads = (
        jnp.where(first, mine[:LANDMARKS], got[:LANDMARKS]),
        jnp.where(first, got[:LANDMARKS], mine[:LANDMARKS]),
    )
    counts = landmark_counts(place)
    total = jnp.zeros((2 * LANDMARKS, width), F32)
    for index, grad in enumerate(grads):
        both = jnp.concatenate(split(grad / counts), axis=0)
        for half in range(halves):
            weight = weights[half, :, index * part : (index + 1) * part]
            total = total + nt(both[:, half * part : (half + 1) * part], weight)
    through[...] = jnp.concatenate(split(total[:LANDMARKS] + total[LANDMARKS:]), axis=0)
    zero = jnp.zeros((LANDMARKS, part), F32)
    own = []
    for index, grad in enumerate(grads):
        columns = grad[:, :part]
        for half in range(1, halves):
            columns = jnp.where(place[5] == half, grad[:, half * part : (half + 1) * part], columns)
        own.append(jnp.where(place[2] == 1 - index, columns, zero))
    high, low = split(jnp.concatenate(own, axis=1))
    mean_high, mean_low = split(land_tokens[...] / counts)
    means = jnp.concatenate([mean_high, mean_low, mean_high, jnp.zeros_like(mean_low)], axis=0).T
    factors = jnp.concatenate([high, high, low, jnp.zeros_like(low)], axis=0)
    late[...] = nn(means, factors).astype(BF16)


def rank_parts(place, mine, got, land_tokens, weights):
    halves, width, packed = weights.shape
    return pl.pallas_call(
        rank_kernel,
        out_shape=(
            jax.ShapeDtypeStruct((width, 2 * packed // 3), BF16),
            jax.ShapeDtypeStruct((2 * LANDMARKS, width), BF16),
        ),
        in_specs=[SCALARS] + whole(4),
        out_specs=tuple(whole(2)),
        compiler_params=PARAMS,
        cost_estimate=lasting(4),
        name="rank_parts",
    )(place, mine, got, land_tokens, weights)


def flipped(values, axis, bit):
    count = lax.axis_size(axis)
    return lax.ppermute(values, axis, [(i, i ^ bit) for i in range(count)])


def side_of(axis, bit):
    return (lax.axis_index(axis) // bit) % 2


def paired(mine, axis, bit, dim):
    other = flipped(mine, axis, bit)
    both = jnp.zeros(mine.shape[:dim] + (2,) + mine.shape[dim:], mine.dtype)
    side = side_of(axis, bit)
    both = lax.dynamic_update_slice_in_dim(both, jnp.expand_dims(mine, dim), side, dim)
    return lax.dynamic_update_slice_in_dim(both, jnp.expand_dims(other, dim), 1 - side, dim)


def ctx_bits():
    bits, bit = [], 1
    while bit < lax.axis_size("ctx"):
        bits.append(bit)
        bit *= 2
    return bits


def sequence_sum(values):
    width = values.shape[1] // 2
    side = side_of("ctx", 1)
    kept = lax.dynamic_slice_in_dim(values, side * width, width, axis=1)
    sent = lax.dynamic_slice_in_dim(values, (1 - side) * width, width, axis=1)
    kept = kept + flipped(sent, "ctx", 1)
    kept = kept + flipped(kept, "tp", 1)
    for bit in ctx_bits()[1:]:
        kept = kept + flipped(kept, "ctx", bit)
    other = flipped(kept, "ctx", 1)
    return jnp.where(
        side == 0,
        jnp.concatenate([kept, other], axis=1),
        jnp.concatenate([other, kept], axis=1),
    )


def to_owner(kept, sent, combine):
    kept = combine(kept, flipped(sent, "ctx", 1))
    for bit in ctx_bits()[1:]:
        view = kept.reshape((-1, 2) + kept.shape[1:])
        side = side_of("ctx", bit)
        sent = lax.dynamic_index_in_dim(view, 1 - side, 1, False)
        kept = lax.dynamic_index_in_dim(view, side, 1, False)
        kept = combine(kept, flipped(sent, "ctx", bit))
    return kept[0], flipped(kept[0], "tp", 1)


def from_owners(part):
    whole_part = part[None]
    for bit in reversed(ctx_bits()):
        both = paired(whole_part, "ctx", bit, 1)
        whole_part = both.reshape((-1,) + part.shape)
    return whole_part.reshape((-1,) + part.shape[1:])


def merge_keys(one, two):
    size = LANES // 2
    one_top, two_top = one[..., size : size + 1], two[..., size : size + 1]
    top = jnp.maximum(one_top, two_top)
    one_factor, two_factor = jnp.exp(one_top - top), jnp.exp(two_top - top)
    summed = one * one_factor + two * two_factor
    lane = lax.broadcasted_iota(jnp.int32, summed.shape, summed.ndim - 1)
    return jnp.where(lane == size, top, summed)


def neighbour_rows(cells, count):
    pieces = lax.axis_size("ctx") * lax.axis_size("tp")
    up = [(i, i + 1) for i in range(pieces - 1)]
    before = lax.ppermute(cells[-count:], ("ctx", "tp"), up)
    after = lax.ppermute(cells[:count], ("ctx", "tp"), [(j, i) for i, j in up])
    return (
        jnp.pad(before, ((LANES - count, 0), (0, 0))),
        jnp.pad(after, ((0, LANES - count), (0, 0))),
    )


def own_quarter(shard):
    rows = shard.shape[0] // lax.axis_size("ctx")
    return lax.dynamic_slice_in_dim(shard, lax.axis_index("ctx") * rows, rows, axis=0)


def gathered(shard):
    full = lax.all_gather(own_quarter(shard), ("tp", "fsdp", "ctx"), tiled=True)
    return full.reshape(lax.axis_size("tp"), -1, shard.shape[1])


def gathered_early(shard, after):
    count = lax.axis_size("fsdp")
    piece = own_quarter(shard)
    if count > 4:
        held = lax.all_gather(piece, "fsdp")
    else:
        here = lax.axis_index("fsdp")
        held = jnp.zeros((count,) + piece.shape, piece.dtype)
        held = lax.dynamic_update_slice_in_dim(held, piece[None], here, 0)
        for step in range(1, count):
            moved = lax.ppermute(piece, "fsdp", [(i, (i + step) % count) for i in range(count)])
            held = lax.dynamic_update_slice_in_dim(held, moved[None], (here - step) % count, 0)
    held, after = gate(held, after)
    bits = ctx_bits()
    halves = []
    for number, half in enumerate((held[: count // 2], held[count // 2 :])):
        half = half[None]
        if number == 0:
            half = paired(half[0], "tp", 1, 0)
        for place, bit in enumerate(reversed(bits[1:])):
            half = paired(half, "ctx", bit, 2 + place)
        if number == 1:
            half = paired(half[0], "tp", 1, 0)
        halves.append(paired(half, "ctx", bits[0], 1 + len(bits)))
    full = jnp.concatenate(halves, axis=1)
    return full.reshape(lax.axis_size("tp"), -1, shard.shape[1]), after


def bits_of(axis):
    bits, bit = [], lax.axis_size(axis) // 2
    while bit:
        bits.append(bit)
        bit //= 2
    return bits


def added(*parts):
    return sum(part.astype(F32) for part in parts).astype(BF16)


def cut(cells, axis, bit, dim):
    size = cells.shape[dim] // 2
    side = side_of(axis, bit)
    return (
        lax.dynamic_slice_in_dim(cells, side * size, size, axis=dim),
        lax.dynamic_slice_in_dim(cells, (1 - side) * size, size, axis=dim),
    )


def gate(*values):
    return lax.optimization_barrier(values)


def dotf(spec, *operands):
    return jnp.einsum(spec, *operands, preferred_element_type=F32)


def taps_round(taps):
    middle = taps.shape[1] // 2
    gap = jnp.zeros((taps.shape[0], LANES - taps.shape[1]), F32)
    return jnp.concatenate([taps[:, middle::-1], gap, taps[:, :middle:-1]], axis=1)


def landmark_bounds(length):
    landmark = jnp.arange(LANDMARKS + 1, dtype=jnp.int32)
    return (landmark * length + LANDMARKS - 1) // LANDMARKS


def landmark_counts_of(length):
    bounds = landmark_bounds(length)
    return (bounds[1:] - bounds[:-1]).astype(F32)[:, None]


def landmark_rows(position, length):
    bounds = landmark_bounds(length)
    inside = (position[:, None] >= bounds[None, :-1]) & (position[:, None] < bounds[None, 1:])
    return inside.astype(BF16)


def on_device(
    tokens,
    lengths,
    qk_weight,
    value_weight,
    out_weight,
    in_weight,
    down_weight,
    norm_gains,
    norm_shifts,
    conv_weight,
    cotangent,
):
    tp_count = lax.axis_size("tp")
    tp_index = lax.axis_index("tp")
    ctx_index = lax.axis_index("ctx")
    _, slot_len, model_width = tokens.shape
    rows = slot_len // tp_count
    local_heads, tap_count = conv_weight.shape
    local_width = value_weight.shape[1]
    ff_width = in_weight.shape[1]
    head_size = local_width // local_heads
    heads = local_heads * tp_count
    owners = lax.axis_size("ctx")
    own_heads = heads // owners
    width = local_width * tp_count
    radius = tap_count // 2
    length = lengths[0]

    own = lax.dynamic_slice_in_dim(tokens[0], tp_index * rows, rows, axis=0)
    own_cotangent = lax.dynamic_slice_in_dim(cotangent[0], tp_index * rows, rows, axis=0)
    first_row = (ctx_index * tp_count + tp_index) * rows
    sides = (side_of("ctx", 1), ctx_index, side_of("ctx", ctx_bits()[-1]), tp_index)
    place = jnp.stack([first_row, length, *sides]).astype(jnp.int32)

    land_tokens = sequence_sum(token_sums(place, own))
    norm_columns = jnp.concatenate([norm_gains, norm_shifts], axis=0).T
    norm_columns = jnp.pad(norm_columns, ((0, 0), (0, LANES - norm_columns.shape[1])))
    ffn_local = jnp.concatenate([in_weight, down_weight.T, out_weight.T, norm_columns], axis=1)
    qkv_local = jnp.concatenate([qk_weight[0], qk_weight[1], value_weight], axis=1)
    qkv_full, ffn_local = gathered_early(qkv_local, ffn_local)
    ffn_full = gathered(ffn_local)
    tap_weights = paired(conv_weight, "tp", 1, 0).reshape(heads, tap_count).astype(F32)
    base, base_back = taps_round(tap_weights), taps_round(tap_weights[:, ::-1])

    queries, keys, values, v_plain, land_q, land_k, own_turned = projections(
        place, own, land_tokens, qkv_full, head_size
    )
    v_ends = neighbour_rows(v_plain, radius)
    merged, merged_tp = to_owner(
        *third_parts(place, keys, values, land_q, owners), merge_keys
    )
    kept_v, kept_p = inverse_forward(place, land_q, land_k, owners)
    first, conv = first_and_conv(queries, values, *v_ends, land_k, base)
    merged, own_out = landmark_out(merged, merged_tp, kept_v)
    land_out = from_owners(own_out)
    context = contexts(first, conv, land_out)

    own_output, *fed, active, fed_turned, down_sent, last_norm = feed_forward(
        place, context, own, own_cotangent, ffn_full, ff_width, local_width
    )
    high = ctx_bits()[-1]
    other_output = flipped(own_output, "tp", 1)
    down_other = flipped(down_sent, "ctx", 1)
    down_kept = kept_grad(place, fed_turned, active, tp_count)
    down_kept, down_other = gate(down_kept, down_other)
    down_mine, down_theirs = cut(down_kept, "ctx", high, 2)
    other_mine, other_theirs = cut(down_other, "ctx", high, 2)
    down_sent = added(down_theirs, other_theirs)
    down_got = flipped(down_sent, "ctx", high)
    fed[0], down_sent = gate(fed[0], down_sent)
    grad_first_res, grad_context, g_hidden, in_sent, att_turned, first_norm = feed_backward(
        place, fed, ffn_full, ff_width, local_width
    )
    in_sent, grad_context, g_hidden, other_output, down_got = gate(
        in_sent, grad_context, g_hidden, other_output, down_got
    )
    in_other = flipped(in_sent, "ctx", 1)
    g_ends = neighbour_rows(grad_context, radius)
    down = added(down_mine, other_mine, down_got)
    down_mine, down_sent = cut(down, "tp", 1, 0)
    down_got = flipped(down_sent, "tp", 1)
    grad_context, down_sent = gate(grad_context, down_sent)
    land_kept, land_sent, g_lk, g_q = attention_back(
        place, queries, grad_context, land_k, land_out, owners
    )
    land_kept, land_sent, in_other, g_ends = gate(land_kept, land_sent, in_other, g_ends)

    land_other = flipped(land_sent, "ctx", 1)
    one_kept, one_sent, two_kept, two_sent = spread_grad(place, fed[5], g_hidden, in_other)
    one_kept, one_sent, two_kept, two_sent, land_other, down_got = gate(
        one_kept, one_sent, two_kept, two_sent, land_other, down_got
    )
    land_grads = land_kept + land_other
    land_mine, land_theirs = cut(land_grads, "ctx", high, 0)
    land_got = flipped(land_theirs, "ctx", high)
    land_theirs, one_sent, two_sent = gate(land_theirs, one_sent, two_sent)
    one_got = flipped(one_sent, "ctx", high)
    two_got = flipped(two_sent, "tp", 1)
    down = added(down_mine, down_got)
    grad_context, one_sent, two_sent = gate(grad_context, one_sent, two_sent)
    g_conv, g_taps = conv_back(v_plain, v_ends, grad_context, g_ends, base_back)
    g_conv, g_taps, land_got = gate(g_conv, g_taps, land_got)
    own_grads = (land_mine + land_got)[0]
    tp_grads = flipped(own_grads, "tp", 1)

    def parts(cells):
        return cells.reshape(rows, tp_count, local_width)

    def qkv_part(index):
        return qkv_full[:, :, index * local_width : (index + 1) * local_width]

    g_q, own_grads = gate(g_q, own_grads)
    mixed_kept, mixed_sent = pair_grads(place, att_turned, context, own_turned, g_q, tp_count)
    back_q = grad_first_res + dotf("tpk,pck->tc", parts(g_q), qkv_part(0))
    mixed_kept, mixed_sent, tp_grads, one_got, two_got, back_q = gate(
        mixed_kept, mixed_sent, tp_grads, one_got, two_got, back_q
    )
    one = added(one_kept, one_got)
    two = added(two_kept, two_got)
    one_mine, one_sent = cut(one, "tp", 1, 0)
    two_mine, two_sent = cut(two, "ctx", high, 2)
    one_got = flipped(one_sent, "tp", 1)
    two_got = flipped(two_sent, "ctx", high)
    mixed_got = flipped(mixed_sent, "ctx", 1)
    own_grads, one_sent, two_sent, mixed_sent = gate(
        own_grads + tp_grads, one_sent, two_sent, mixed_sent
    )
    spread, lq_mid, lk_mid = inverse_backward(
        place, land_q, land_k, merged, own_grads, kept_v, kept_p
    )
    spread, one_got, two_got, mixed_got = gate(spread, one_got, two_got, mixed_got)
    spread = from_owners(spread)

    one, two = added(one_mine, one_got)[0], added(two_mine, two_got)[0]
    pair = jnp.concatenate([jnp.concatenate([one, two], axis=0), down[0]], axis=1)
    owner_count = lax.axis_size("fsdp")
    owner_rows = model_width // owner_count
    near, *farther = bits_of("fsdp")[::-1]

    def by_owner_bits(cells):
        return cells.reshape((2,) * (1 + len(farther)) + (-1, cells.shape[-1]))

    def cut_last(cells, bit):
        dim = cells.ndim - 3
        return tuple(piece.squeeze(dim) for piece in cut(cells, "fsdp", bit, dim))

    def by_ctx(cells):
        return cells.reshape(tp_count, owner_count, 2, -1, local_width)

    pair_mine, pair_sent = cut_last(by_owner_bits(pair), near)
    pair_got = flipped(pair_sent, "fsdp", near)
    mixed = added(mixed_kept, mixed_got)
    mixed_mine, mixed_sent = cut(by_ctx(mixed), "ctx", high, 2)
    mixed_got = flipped(mixed_sent, "ctx", high)
    spread, pair_sent, mixed_sent = gate(spread, pair_sent, mixed_sent)
    g_k, g_v, sums = third_back(
        place, keys, values, land_q, spread, g_conv, lq_mid, lk_mid, g_lk, last_norm, first_norm,
        g_taps,
    )

    sums_mine, sums_sent = cut(sums, "ctx", 1, 1)
    sums_got = flipped(sums_sent, "ctx", 1)
    g_k, sums_sent = gate(g_k, sums_sent)
    kv_kept, kv_sent = pair_grads(place, own_turned, g_k, own_turned, g_v, tp_count)
    kv_kept, kv_sent, sums_got, mixed_got, pair_got = gate(
        kv_kept, kv_sent, sums_got, mixed_got, pair_got
    )
    kv_got = flipped(kv_sent, "ctx", 1)
    sums = sums_mine + sums_got
    sums_got = flipped(sums, "tp", 1)
    mixed = added(mixed_mine, mixed_got)
    mixed_mine, mixed_sent = cut(mixed, "tp", 1, 0)
    pair = added(pair_mine, pair_got)
    g_k, kv_sent, sums, mixed_sent = gate(g_k, kv_sent, sums, mixed_sent)
    mixed_got = flipped(mixed_sent, "tp", 1)
    back_k = back_q + dotf("tpk,pck->tc", parts(g_k), qkv_part(1))
    back_k, kv_got, sums_got = gate(back_k, kv_got, sums_got)
    sums = sums + sums_got
    sums_got = flipped(sums, "ctx", high)
    kv = added(kv_kept, kv_got)
    kv_mine, kv_sent = cut(by_ctx(kv), "ctx", high, 2)
    sums, kv_sent = gate(sums, kv_sent)
    kv_got = flipped(kv_sent, "ctx", high)
    back_k, kv_sent = gate(back_k, kv_sent)
    own_grad = (back_k + dotf("tpk,pck->tc", parts(g_v), qkv_part(2))).astype(BF16)
    first_rows = 3 * rows // 8
    other_first = flipped(own_grad[:first_rows], "tp", 1)
    pair_mine, pair_sent = cut_last(pair, farther[0])
    pair_got = flipped(pair_sent, "fsdp", farther[0])
    own_grad, sums_got = gate(own_grad, sums_got)
    sums = sums + sums_got
    sums_got = flipped(sums, "ctx", 1)
    late, through = rank_parts(place, sums, sums_got, land_tokens, qkv_full)
    late, through, kv_got, mixed_got, pair_got = gate(late, through, kv_got, mixed_got, pair_got)
    pair = added(pair_mine, pair_got)
    for bit in farther[1:]:
        pair_mine, pair_sent = cut_last(pair, bit)
        pair = added(pair_mine, flipped(pair_sent, "fsdp", bit))
    kv = added(kv_mine, kv_got)
    kv_mine, kv_sent = cut(kv, "tp", 1, 0)
    kv_got = flipped(kv_sent, "tp", 1)
    own_grad, kv_sent = gate(own_grad, kv_sent)
    other_second = flipped(own_grad[first_rows:], "tp", 1)

    late = late.reshape(owner_count, 2, -1, 2 * local_width)
    late = lax.dynamic_index_in_dim(late, place[4], 1, False)
    mixed = added(
        jnp.concatenate([mixed_mine, kv_mine], axis=-1).reshape(late.shape),
        jnp.concatenate([mixed_got, kv_got], axis=-1).reshape(late.shape),
        late,
    )
    mixed = by_owner_bits(mixed)
    small = jnp.where(
        place[2] == 0,
        jnp.concatenate([sums[LANDMARKS:], sums_got[LANDMARKS:]], axis=1),
        jnp.concatenate([sums_got[LANDMARKS:], sums[LANDMARKS:]], axis=1),
    )
    small, mixed = gate(small, mixed)
    for bit in (near, *farther):
        mixed_mine, mixed_sent = cut_last(mixed, bit)
        mixed = added(mixed_mine, flipped(mixed_sent, "fsdp", bit))
        small = small + flipped(small, "fsdp", bit)

    def of_core(cells, core):
        cells = cells.reshape((owners // 2, 2) + cells.shape[1:])
        return [cells[i, core] for i in range(owners // 2)]

    mixed, other_second = gate(mixed, other_second)
    mixed = from_owners(mixed[None])
    sides = [jnp.concatenate(of_core(mixed, core), axis=0).astype(F32) for core in range(2)]
    grad_out, grad_k = sides[0][:, :local_width].T, sides[0][:, local_width:]
    grad_q, grad_v = sides[1][:, :local_width], sides[1][:, local_width:]

    own_columns = lax.axis_index("fsdp") * owner_rows
    norm_sums = small[:2].reshape(2, 2, model_width)[::-1]
    norm_sums = lax.dynamic_slice_in_dim(norm_sums, own_columns, owner_rows, axis=2)
    taps_sum = small[2].reshape(heads, LANES)
    taps_sum = lax.dynamic_slice_in_dim(taps_sum, tp_index * local_heads, local_heads, axis=0)
    grad_taps = jnp.concatenate(
        [taps_sum[:, radius - 1 :: -1], taps_sum[:, : -radius - 2 : -1]], axis=1
    )

    columns = pair.shape[1] // 2
    pair = from_owners(pair[None])
    pieces = [piece for core in range(2) for piece in of_core(pair, core)]
    grad_in = jnp.concatenate([piece[:, :columns] for piece in pieces], axis=1).astype(F32)
    grad_down = jnp.concatenate([piece[:, columns:] for piece in pieces], axis=1).astype(F32).T

    output = jnp.where(
        tp_index == 0,
        jnp.concatenate([own_output, other_output]),
        jnp.concatenate([other_output, own_output]),
    )[None]
    both_grads = jnp.where(
        tp_index == 0,
        jnp.concatenate([own_grad, other_first, other_second]),
        jnp.concatenate([other_first, other_second, own_grad]),
    )
    position = ctx_index * slot_len + jnp.arange(slot_len, dtype=jnp.int32)
    onehot = landmark_rows(position, length)
    grad_tokens = both_grads.astype(F32) + dotf(
        "tm,mc->tc", jnp.concatenate([onehot, onehot], axis=1), through
    )
    grad_tokens = grad_tokens.reshape(1, slot_len, model_width)
    return (
        output,
        grad_tokens,
        jnp.stack([grad_q, grad_k]),
        grad_v,
        grad_out,
        grad_in,
        grad_down,
        norm_sums[:, 0],
        norm_sums[:, 1],
        grad_taps,
    )


def solution(mesh):
    in_specs = (
        P("fsdp", "ctx", None),
        P("fsdp"),
        P(None, "fsdp", "tp"),
        P("fsdp", "tp"),
        P("tp", "fsdp"),
        P("fsdp", "tp"),
        P("tp", "fsdp"),
        P(None, "fsdp"),
        P(None, "fsdp"),
        P("tp", None),
        P("fsdp", "ctx", None),
    )
    out_specs = (
        P("fsdp", "ctx", None),
        P("fsdp", "ctx", None),
        P(None, "fsdp", "tp"),
        P("fsdp", "tp"),
        P("tp", "fsdp"),
        P("fsdp", "tp"),
        P("tp", "fsdp"),
        P(None, "fsdp"),
        P(None, "fsdp"),
        P("tp", None),
    )
    return jax.shard_map(
        on_device, mesh=mesh, in_specs=in_specs, out_specs=out_specs, check_vma=False
    )
```

```python
import jax
import jax.numpy as jnp
from jax import lax
from jax.experimental import pallas as pl
from jax.experimental.pallas import tpu as pltpu
from jax.sharding import PartitionSpec as P

LANDMARKS = 64
NEWTON = 6
LANES = 128
VMEM_BYTES = 56 * 2**20

HIGH = lax.Precision.HIGHEST
F32 = jnp.float32
BF16 = jnp.bfloat16


def lasting(microseconds):
    return pl.CostEstimate(
        flops=int(microseconds * 1.1535e9), bytes_accessed=int(microseconds * 1e5), transcendentals=0
    )


def nn(left, right):
    return jnp.dot(left, right, preferred_element_type=F32)


def nt(left, right):
    return lax.dot_general(left, right, (((1,), (1,)), ((), ())), preferred_element_type=F32)


def split(wide):
    high = wide.astype(BF16)
    return high, (wide - high.astype(F32)).astype(BF16)


def each_tile(count, tile, body):
    def step(i, _):
        body(i, pl.ds(pl.multiple_of(i * tile, tile), tile))
        return 0

    lax.fori_loop(0, count // tile, step, 0)


def family_grads(turned, cells, mine, kept, sent):
    halves, width, columns = kept.shape

    def rows_of(i, at):
        total = nn(turned[at, :], cells[...]).astype(BF16)

        @pl.when(mine)
        def _():
            for half in range(halves):
                kept[half, at, :] = total[:, half * columns : (half + 1) * columns]

        @pl.when(jnp.logical_not(mine))
        def _():
            for half in range(halves):
                sent[half, at, :] = total[:, half * columns : (half + 1) * columns]

    each_tile(width, 384, rows_of)


def whole(count):
    return [pl.BlockSpec(memory_space=pltpu.VMEM)] * count


SCALARS = pl.BlockSpec(memory_space=pltpu.SMEM)
PARAMS = pltpu.CompilerParams(vmem_limit_bytes=VMEM_BYTES)


def landmark_onehot(place, rows, landmark_axis):
    shape = (LANDMARKS, rows) if landmark_axis == 0 else (rows, LANDMARKS)
    landmark = lax.broadcasted_iota(jnp.int32, shape, landmark_axis)
    position = place[0] + lax.broadcasted_iota(jnp.int32, shape, 1 - landmark_axis)
    start = lax.shift_right_logical(landmark * place[1] + (LANDMARKS - 1), 6)
    end = lax.shift_right_logical((landmark + 1) * place[1] + (LANDMARKS - 1), 6)
    return jnp.where((position >= start) & (position < end), 1.0, 0.0).astype(BF16)


def live_lanes(place, rows):
    position = place[0] + lax.broadcasted_iota(jnp.int32, (1, rows), 1)
    return position < place[1]


def band(base_row):
    ring = pltpu.roll(jnp.broadcast_to(base_row, (LANES, LANES)), 0, 1, stride=1, stride_axis=0)
    gap = lax.broadcasted_iota(jnp.int32, (LANES, LANES), 0) - lax.broadcasted_iota(
        jnp.int32, (LANES, LANES), 1
    )
    zero = jnp.zeros_like(ring)
    before = jnp.where(gap >= LANES - 16, ring, zero).astype(BF16)
    here = jnp.where(jnp.abs(gap) <= 16, ring, zero).astype(BF16)
    after = jnp.where(gap <= 16 - LANES, ring, zero).astype(BF16)
    return before, here, after


def convolved(blocks, bands):
    before, here, after = bands
    return jnp.concatenate(
        [
            nn(blocks[i], before) + nn(blocks[i + 1], here) + nn(blocks[i + 2], after)
            for i in range(len(blocks) - 2)
        ],
        axis=1,
    )


def token_sums_kernel(place, tokens, sums):
    sums[...] = nn(landmark_onehot(place, tokens.shape[0], 0), tokens[...])


def token_sums(place, tokens):
    return pl.pallas_call(
        token_sums_kernel,
        out_shape=jax.ShapeDtypeStruct((LANDMARKS, tokens.shape[1]), F32),
        in_specs=[SCALARS] + whole(1),
        out_specs=whole(1)[0],
        compiler_params=PARAMS,
        cost_estimate=lasting(2.5),
        name="token_sums",
    )(place, tokens)


def landmark_counts(place):
    landmark = lax.broadcasted_iota(jnp.int32, (LANDMARKS, 1), 0)
    start = lax.shift_right_logical(landmark * place[1] + (LANDMARKS - 1), 6)
    end = lax.shift_right_logical((landmark + 1) * place[1] + (LANDMARKS - 1), 6)
    return (end - start).astype(F32)


def projection_kernel(
    place, tokens, sums, weights, q_out, k_out, v_out, v_plain, land_q, land_k, turned, kept, sent
):
    rows = tokens.shape[0]
    halves, _, packed = weights.shape
    width = packed // 3
    size = land_q.shape[2]
    position = place[0] + lax.broadcasted_iota(jnp.int32, (rows, 1), 0)
    live = jnp.where(position < place[1], 1.0, 0.0)
    scaled = live * 64**-0.25
    means = jnp.concatenate(split(sums[...] / landmark_counts(place)), axis=0)
    cells = tokens[...]
    turned[...] = cells.T
    for half in range(halves):
        for part, out in enumerate((q_out, k_out, v_out)):
            weight = weights[half, :, part * width : (part + 1) * width]
            low = ((live if part == 2 else scaled) * nn(cells, weight)).astype(BF16)
            out[half * width : (half + 1) * width, :] = low.T
            if part == 2:
                v_plain[:, half * width : (half + 1) * width] = low
                continue
            both = nn(means, weight)
            land = (64**-0.25 * (both[:LANDMARKS] + both[LANDMARKS:])).astype(BF16)
            to = land_k if part else land_q
            for head in range(width // size):
                to[half * (width // size) + head] = land[:, head * size : (head + 1) * size]
    third_heads(place, k_out, v_out, land_q, kept, sent)


def projections(place, tokens, sums, weights, size, owners):
    rows = tokens.shape[0]
    width = weights.shape[0] * weights.shape[2] // 3
    turned = jax.ShapeDtypeStruct((width, rows), BF16)
    land = jax.ShapeDtypeStruct((width // size, LANDMARKS, size), BF16)
    return pl.pallas_call(
        projection_kernel,
        out_shape=(turned, turned, turned, jax.ShapeDtypeStruct((rows, width), BF16), land, land)
        + (jax.ShapeDtypeStruct(tokens.shape[::-1], BF16),)
        + owner_parts(width // size, owners),
        in_specs=[SCALARS] + whole(3),
        out_specs=tuple(whole(9)),
        compiler_params=PARAMS,
        cost_estimate=lasting(18),
        name="projections",
    )(place, tokens, sums, weights)


def by_owner(place, h, owners, kept, sent, values):
    per = kept.shape[1]
    for owner in range(owners):
        @pl.when((h >= owner * per) & (h < (owner + 1) * per))
        def _(owner=owner):
            mine = place[2] == owner % 2

            @pl.when(mine)
            def _():
                kept[owner // 2, h - owner * per] = values

            @pl.when(jnp.logical_not(mine))
            def _():
                sent[owner // 2, h - owner * per] = values


def third_heads(place, keys, values, land_q, kept, sent):
    heads = land_q.shape[0]
    size = land_q.shape[2]
    rows = keys.shape[1]
    owners = 2 * kept.shape[0]
    live = live_lanes(place, rows)

    def head(h):
        at = pl.ds(pl.multiple_of(h * size, size), size)
        scores = jnp.where(live, nn(land_q[h], keys[at, :]), -1e30)
        top = jnp.max(scores, axis=1, keepdims=True)
        raised = jnp.where(live, jnp.exp(scores - top), 0.0)
        total = jnp.sum(raised, axis=1, keepdims=True)
        high, low = split(raised)
        value = values[at, :]
        mixed = nt(high, value) + nt(low, value)
        lane = lax.broadcasted_iota(jnp.int32, (LANDMARKS, LANES - size), 1)
        stats = jnp.where(lane == 0, top, jnp.where(lane == 1, total, 0.0))
        by_owner(place, h, owners, kept, sent, jnp.concatenate([mixed, stats], axis=1))

    def pair(i, _):
        head(2 * i)
        head(2 * i + 1)
        return 0

    lax.fori_loop(0, heads // 2, pair, 0)


def owner_parts(heads, owners):
    part = jax.ShapeDtypeStruct((owners // 2, heads // owners, LANDMARKS, LANES), F32)
    return part, part


def dot_high(left, right):
    return jnp.dot(left, right, preferred_element_type=F32, precision=HIGH)


def dot_high_nt(left, right):
    return lax.dot_general(
        left, right, (((1,), (1,)), ((), ())), preferred_element_type=F32, precision=HIGH
    )


def eye():
    row = lax.broadcasted_iota(jnp.int32, (LANDMARKS, LANDMARKS), 0)
    column = lax.broadcasted_iota(jnp.int32, (LANDMARKS, LANDMARKS), 1)
    return jnp.where(row == column, 1.0, 0.0)


def middle_map(land_q, land_k):
    scores = nt(land_q, land_k)
    raised = jnp.exp(scores - jnp.max(scores, axis=1, keepdims=True))
    return raised / jnp.sum(raised, axis=1, keepdims=True)


def inverse_kernel(place, land_q, land_k, kept_v, kept_p, kept_b, kept_c):
    heads = range(kept_v.shape[1])
    one = eye()
    own = [place[3] * len(heads) + h for h in heads]
    middle = [middle_map(land_q[h], land_k[h]) for h in own]
    approx = [m.T / jnp.sum(m * m, keepdims=True) for m in middle]
    for turn in range(NEWTON):
        product = [dot_high(middle[h], approx[h]) for h in heads]
        for h in heads:
            kept_v[turn, h] = approx[h]
            kept_p[turn, h] = product[h]
        bracket = [7.0 * one - p for p in product]
        bracket = [15.0 * one - dot_high(product[h], bracket[h]) for h in heads]
        for h in heads:
            kept_b[turn, h] = bracket[h]
        bracket = [13.0 * one - dot_high(product[h], bracket[h]) for h in heads]
        for h in heads:
            kept_c[turn, h] = bracket[h]
        approx = [0.25 * dot_high(approx[h], bracket[h]) for h in heads]
    for h in heads:
        kept_v[NEWTON, h] = approx[h]


def inverse_forward(place, land_q, land_k, owners):
    heads = land_q.shape[0] // owners
    square = (heads, LANDMARKS, LANDMARKS)
    return pl.pallas_call(
        inverse_kernel,
        out_shape=(
            jax.ShapeDtypeStruct((NEWTON + 1,) + square, F32),
            jax.ShapeDtypeStruct((NEWTON,) + square, F32),
            jax.ShapeDtypeStruct((NEWTON,) + square, F32),
            jax.ShapeDtypeStruct((NEWTON,) + square, F32),
        ),
        in_specs=[SCALARS] + whole(2),
        out_specs=tuple(whole(4)),
        compiler_params=PARAMS,
        cost_estimate=lasting(7),
        name="inverse_forward",
    )(place, land_q, land_k)


def merged_keys(one, two, size):
    one_top, two_top = one[:, size : size + 1], two[:, size : size + 1]
    top = jnp.maximum(one_top, two_top)
    summed = one * jnp.exp(one_top - top) + two * jnp.exp(two_top - top)
    lane = lax.broadcasted_iota(jnp.int32, one.shape, 1)
    return jnp.where(lane == size, top, summed)


def land_out_kernel(one, two, kept_v, merged, land_out):
    size = land_out.shape[2]
    for h in range(one.shape[0]):
        both = merged_keys(one[h], two[h], size)
        merged[h] = both
        mixed = both[:, :size] / both[:, size + 1 : size + 2]
        land_out[h] = dot_high(kept_v[NEWTON, h], mixed).astype(BF16)


def landmark_out(one, two, kept_v):
    heads = one.shape[0]
    return pl.pallas_call(
        land_out_kernel,
        out_shape=(
            jax.ShapeDtypeStruct(one.shape, F32),
            jax.ShapeDtypeStruct((heads, LANDMARKS, LANES // 2), BF16),
        ),
        in_specs=whole(3),
        out_specs=tuple(whole(2)),
        compiler_params=PARAMS,
        cost_estimate=lasting(2.2),
        name="landmark_out",
    )(one, two, kept_v)


def inverse_back_kernel(
    place, land_q, land_k, merged, grads, kept_v, kept_p, kept_b, kept_c, spread, g_lq, g_lk
):
    heads = range(grads.shape[0])
    size = land_q.shape[2]
    one = eye()
    own = [place[3] * len(heads) + h for h in heads]
    middle = [middle_map(land_q[h], land_k[h]) for h in own]
    turned = [m.T for m in middle]
    g_approx = []
    for h in heads:
        mixed = merged[h][:, :size] / merged[h][:, size + 1 : size + 2]
        g_land = grads[h][:, :size]
        g_approx.append(dot_high_nt(g_land, mixed))
        g_mixed = dot_high(kept_v[NEWTON, h].T, g_land)
        row_dot = jnp.sum(g_mixed * mixed, axis=1, keepdims=True)
        lane = lax.broadcasted_iota(jnp.int32, (LANDMARKS, LANES - size), 1)
        top = merged[h][:, size : size + 1]
        total = merged[h][:, size + 1 : size + 2]
        stats = jnp.where(
            lane == 0, row_dot, jnp.where(lane == 1, top, jnp.where(lane == 2, total, 0.0))
        )
        spread[h] = jnp.concatenate([g_mixed, stats], axis=1)
    g_middle = [jnp.zeros((LANDMARKS, LANDMARKS), F32) for _ in heads]
    for turn in reversed(range(NEWTON)):
        approx = [kept_v[turn, h] for h in heads]
        product = [kept_p[turn, h] for h in heads]
        first = [7.0 * one - p for p in product]
        second = [kept_b[turn, h] for h in heads]
        third = [kept_c[turn, h] for h in heads]
        g_third = [0.25 * dot_high(approx[h].T, g_approx[h]) for h in heads]
        g_back = [0.25 * dot_high_nt(g_approx[h], third[h]) for h in heads]
        g_product = [-dot_high_nt(g_third[h], second[h]) for h in heads]
        pt = [p.T for p in product]
        g_second = [-dot_high(pt[h], g_third[h]) for h in heads]
        g_product = [g_product[h] - dot_high_nt(g_second[h], first[h]) for h in heads]
        g_product = [g_product[h] + dot_high(pt[h], g_second[h]) for h in heads]
        g_middle = [g_middle[h] + dot_high_nt(g_product[h], approx[h]) for h in heads]
        g_approx = [g_back[h] + dot_high(turned[h], g_product[h]) for h in heads]
    for h in heads:
        m = middle[h]
        size_sum = jnp.sum(m * m, keepdims=True)
        g_size = -jnp.sum(g_approx[h] * turned[h], keepdims=True) / (size_sum * size_sum)
        g_m = g_middle[h] + g_approx[h].T / size_sum + 2.0 * g_size * m
        g_scores = m * (g_m - jnp.sum(g_m * m, axis=1, keepdims=True))
        g_lq[h] = dot_high(g_scores, land_k[own[h]].astype(F32))
        g_lk[h] = dot_high(g_scores.T, land_q[own[h]].astype(F32))


def inverse_backward(place, land_q, land_k, merged, grads, *kept):
    heads = grads.shape[0]
    square = jax.ShapeDtypeStruct((heads,) + land_q.shape[1:], F32)
    return pl.pallas_call(
        inverse_back_kernel,
        out_shape=(jax.ShapeDtypeStruct((heads, LANDMARKS, LANES), F32), square, square),
        in_specs=[SCALARS] + whole(8),
        out_specs=tuple(whole(3)),
        compiler_params=PARAMS,
        cost_estimate=lasting(11.5),
        name="inverse_backward",
    )(place, land_q, land_k, merged, grads, *kept)


def first_map(land_k, queries):
    scores = nn(land_k, queries)
    raised = jnp.exp(scores - jnp.max(scores, axis=0, keepdims=True))
    return raised * (1.0 / jnp.sum(raised, axis=0, keepdims=True))


def head_blocks(cells, ends, at):
    rows = cells.shape[1]
    left, right = ends
    return (
        [left[at, :]]
        + [cells[at, i * LANES : (i + 1) * LANES] for i in range(rows // LANES)]
        + [right[at, :]]
    )


def first_conv_kernel(queries, values, left, right, land_k, base, first, conv, ends):
    heads, _, size = land_k.shape
    ends[0] = left[...].T
    ends[1] = right[...].T

    def head(h):
        at = pl.ds(pl.multiple_of(h * size, size), size)
        first[at, :] = first_map(land_k[h], queries[at, :]).astype(BF16)
        blocks = head_blocks(values, (ends.at[0], ends.at[1]), at)
        conv[at, :] = convolved(blocks, band(base[pl.ds(h, 1), :]))

    def pair(i, _):
        head(2 * i)
        head(2 * i + 1)
        return 0

    lax.fori_loop(0, heads // 2, pair, 0)


def first_and_conv(queries, values, left, right, land_k, base):
    width, rows = queries.shape
    return pl.pallas_call(
        first_conv_kernel,
        out_shape=(
            jax.ShapeDtypeStruct((width, rows), BF16),
            jax.ShapeDtypeStruct((width, rows), F32),
        ),
        in_specs=whole(6),
        out_specs=tuple(whole(2)),
        scratch_shapes=[pltpu.VMEM((2, width, LANES), BF16)],
        compiler_params=PARAMS,
        cost_estimate=lasting(8),
        name="first_and_conv",
    )(queries, values, left, right, land_k, base)


def context_rows(first, conv, land_out, context):
    heads, _, size = land_out.shape

    def head(h):
        at = pl.ds(pl.multiple_of(h * size, size), size)
        return (nn(land_out[h].T, first[at, :]) + conv[at, :]).astype(BF16)

    def pair(i, _):
        both = jnp.concatenate([head(2 * i), head(2 * i + 1)], axis=0)
        context[:, pl.ds(pl.multiple_of(i * LANES, LANES), LANES)] = both.T
        return 0

    lax.fori_loop(0, heads // 2, pair, 0)


def attention_back_kernel(
    place, queries, grads, land_k, land_out, kept, sent, g_lk, g_query
):
    heads, _, size = land_k.shape
    rows = queries.shape[1]
    owners = 2 * kept.shape[0]
    scaled = jnp.where(live_lanes(place, rows), 64**-0.25, 0.0)

    def pair(i, _):
        lanes = pl.ds(pl.multiple_of(i * LANES, LANES), LANES)
        turned = grads[:, lanes].T
        g_queries, g_keys = [], []
        for side in range(2):
            h = 2 * i + side
            query = queries[pl.ds(pl.multiple_of(h * size, size), size), :]
            g_context = turned[side * size : (side + 1) * size]
            first = first_map(land_k[h], query)
            g_first = nn(land_out[h], g_context)
            inner = jnp.sum(g_first * first, axis=0, keepdims=True)
            g_scores = (first * (g_first - inner)).astype(BF16)
            g_land = nt(first.astype(BF16), g_context)
            g_key = nt(g_scores, query)
            by_owner(place, h, owners, kept, sent, jnp.concatenate([g_land, g_key], axis=1))
            g_keys.append(g_key)
            g_queries.append((scaled * nn(land_k[h].T, g_scores)).astype(BF16))
        g_query[:, lanes] = jnp.concatenate(g_queries, axis=0).T
        g_lk[:, lanes] = jnp.concatenate(g_keys, axis=1)
        return 0

    lax.fori_loop(0, heads // 2, pair, 0)


def attention_back(place, queries, grads, land_k, land_out, owners):
    width, rows = queries.shape
    heads = land_k.shape[0]
    return pl.pallas_call(
        attention_back_kernel,
        out_shape=owner_parts(heads, owners)
        + (
            jax.ShapeDtypeStruct((LANDMARKS, width), F32),
            jax.ShapeDtypeStruct((rows, width), BF16),
        ),
        in_specs=[SCALARS] + whole(4),
        out_specs=tuple(whole(4)),
        compiler_params=PARAMS,
        cost_estimate=lasting(11.4),
        name="attention_back",
    )(place, queries, grads, land_k, land_out)


def conv_back_kernel(
    v_plain, v_left, v_right, grads, g_left, g_right, base_back, g_value, g_taps, ends
):
    heads = g_taps.shape[0]
    rows, width = grads.shape
    size = width // heads
    blocks_in = rows // LANES
    row = lax.broadcasted_iota(jnp.int32, (LANES, LANES), 0)
    column = lax.broadcasted_iota(jnp.int32, (LANES, LANES), 1)
    reverse = jnp.where(row + column == LANES - 1, 1.0, 0.0)
    gap = row - column
    ends[0] = g_left[...].T
    ends[1] = g_right[...].T

    def pair(i, _):
        lanes = pl.ds(pl.multiple_of(i * LANES, LANES), LANES)
        turned = grads[:, lanes].T
        plain = [v_left[LANES - 16 :, lanes]]
        plain += [v_plain[b * LANES : (b + 1) * LANES, lanes] for b in range(blocks_in)]
        plain += [v_right[:16, lanes]]
        for side in range(2):
            h = 2 * i + side
            at = pl.ds(pl.multiple_of(h * size, size), size)
            g_context = turned[side * size : (side + 1) * size]
            blocks = [ends[0, at, :]]
            blocks += [g_context[:, b * LANES : (b + 1) * LANES] for b in range(blocks_in)]
            blocks += [ends[1, at, :]]
            g_value[at, :] = convolved(blocks, band(base_back[pl.ds(h, 1), :]))
            own = (row >= size) == (side == 1)
            here = jnp.zeros((LANES, LANES), F32)
            before = jnp.zeros((16, LANES), F32)
            after = jnp.zeros((16, LANES), F32)
            for b in range(blocks_in):
                piece = turned[:, b * LANES : (b + 1) * LANES]
                masked = jnp.where(own, piece, jnp.zeros_like(piece))
                prior = plain[0] if b == 0 else plain[b][LANES - 16 :]
                later = plain[b + 2][:16]
                here = here + nn(plain[b + 1], masked)
                before = before + nn(prior, masked)
                after = after + nn(later, masked)
            empty = jnp.zeros((LANES - 16, LANES), F32)
            ring = jnp.where(jnp.abs(gap) <= 16, here, 0.0)
            ring = ring + jnp.where(
                gap >= LANES - 16, jnp.concatenate([empty, before], axis=0), 0.0
            )
            ring = ring + jnp.where(
                gap <= 16 - LANES, jnp.concatenate([after, empty], axis=0), 0.0
            )
            straight = pltpu.roll(dot_high(reverse, ring), 0, 1, stride=1, stride_axis=0)
            g_taps[pl.ds(h, 1), :] = jnp.sum(straight, axis=0, keepdims=True)
        return 0

    lax.fori_loop(0, heads // 2, pair, 0)


def conv_back(v_plain, v_ends, grads, g_ends, base_back):
    rows, width = grads.shape
    heads = base_back.shape[0]
    return pl.pallas_call(
        conv_back_kernel,
        out_shape=(
            jax.ShapeDtypeStruct((width, rows), F32),
            jax.ShapeDtypeStruct((heads, LANES), F32),
        ),
        in_specs=whole(7),
        out_specs=tuple(whole(2)),
        scratch_shapes=[pltpu.VMEM((2, width, LANES), BF16)],
        compiler_params=PARAMS,
        cost_estimate=lasting(13.6),
        name="conv_back",
    )(v_plain, *v_ends, grads, *g_ends, base_back)


def third_back_kernel(
    place, keys, values, land_q, spread, g_conv, lq_mid, lk_mid, g_lk, last, first, taps, turned,
    g_k, g_v, sums, kept, sent,
):
    heads, _, size = land_q.shape
    rows, width = g_k.shape
    own_heads = lq_mid.shape[0]
    scale = 64**-0.25
    sums[LANDMARKS:, :] = jnp.zeros((sums.shape[0] - LANDMARKS, 2 * width), F32)
    sums[LANDMARKS : LANDMARKS + 1, :] = last[...]
    sums[LANDMARKS + 1 : LANDMARKS + 2, :] = first[...]
    for h in range(heads):
        sums[LANDMARKS + 2 : LANDMARKS + 3, h * LANES : (h + 1) * LANES] = taps[h : h + 1, :]

    def mid(part, h):
        at = h - place[3] * own_heads
        mine = (at >= 0) & (at < own_heads) & (place[5] == 0)
        inside = jnp.clip(at, 0, own_heads - 1)
        return jnp.where(mine, part[inside], 0.0)

    live = live_lanes(place, rows)
    live_row = jnp.where(live, 1.0, 0.0)
    scaled_row = live_row * 64**-0.25

    def pair(i, _):
        lanes = pl.ds(pl.multiple_of(i * LANES, LANES), LANES)
        g_keys, g_values, g_lqs, lks = [], [], [], []
        for side in range(2):
            h = 2 * i + side
            at = pl.ds(pl.multiple_of(h * size, size), size)
            key, value = keys[at, :], values[at, :]
            pack = spread[h]
            g_mixed = pack[:, :size]
            row_dot = pack[:, size : size + 1]
            top = pack[:, size + 1 : size + 2]
            total = pack[:, size + 2 : size + 3]
            scores = nn(land_q[h], key)
            third = jnp.where(live, jnp.exp(scores - top), 0.0) * (1.0 / total)
            gm_high, gm_low = split(g_mixed)
            g_third = nn(gm_high, value) + nn(gm_low, value)
            g_high, g_low = split(third * (g_third - row_dot))
            g_lqs.append(nt(g_high, key) + nt(g_low, key) + mid(lq_mid, h))
            lks.append(mid(lk_mid, h))
            turned = land_q[h].T
            g_key = nn(turned, g_high) + nn(turned, g_low)
            g_keys.append((scaled_row * g_key).astype(BF16))
            t_high, t_low = split(third)
            gmt_high, gmt_low = split(g_mixed.T)
            g_value = nn(gmt_high, t_high) + nn(gmt_high, t_low) + nn(gmt_low, t_high)
            g_values.append((live_row * (g_value + g_conv[at, :])).astype(BF16))
        g_k[:, lanes] = jnp.concatenate(g_keys, axis=0).T
        g_v[:, lanes] = jnp.concatenate(g_values, axis=0).T
        sums[:LANDMARKS, lanes] = scale * jnp.concatenate(g_lqs, axis=1)
        key_lanes = pl.ds(pl.multiple_of(width + i * LANES, LANES), LANES)
        sums[:LANDMARKS, key_lanes] = scale * (g_lk[:, lanes] + jnp.concatenate(lks, axis=1))
        return 0

    lax.fori_loop(0, heads // 2, pair, 0)
    for number, cells in enumerate((g_k, g_v)):
        family_grads(turned, cells, place[2] == number, kept, sent)


def third_back(
    place, keys, values, land_q, spread, g_conv, lq_mid, lk_mid, g_lk, last, first, taps, turned, halves
):
    width, rows = keys.shape
    plain = jax.ShapeDtypeStruct((rows, width), BF16)
    return pl.pallas_call(
        third_back_kernel,
        out_shape=(plain, plain, jax.ShapeDtypeStruct((LANDMARKS + 8, 2 * width), F32))
        + (jax.ShapeDtypeStruct((halves, width, width // halves), BF16),) * 2,
        in_specs=[SCALARS] + whole(12),
        out_specs=tuple(whole(5)),
        compiler_params=PARAMS,
        cost_estimate=lasting(17),
        name="third_back",
    )(
        place, keys, values, land_q, spread, g_conv, lq_mid, lk_mid, g_lk, last, first, taps, turned
    )


def centred_rows(rows):
    centred = rows - jnp.mean(rows, axis=1, keepdims=True)
    scale = lax.rsqrt(jnp.mean(centred * centred, axis=1, keepdims=True) + 1e-05)
    return centred * scale, scale


def norm_back(grads, gain, unit, scale):
    scaled = grads * gain
    inner = jnp.mean(scaled * unit, axis=1, keepdims=True)
    return scale * (scaled - jnp.mean(scaled, axis=1, keepdims=True) - unit * inner)


def gelu_pair(hidden):
    share = 0.5 * (1.0 + lax.erf(hidden * 0.7071067811865476))
    density = jnp.exp(-0.5 * hidden * hidden) * 0.3989422804014327
    return hidden * share, share + hidden * density


class Copies:
    def __init__(self, sems):
        self.sems, self.used, self.open = sems, 0, []

    def start(self, source, target):
        copy = pltpu.make_async_copy(source, target, self.sems.at[self.used])
        self.used += 1
        copy.start()
        return copy

    def out(self, source, target):
        self.open.append(self.start(source, target))

    def finish(self):
        for copy in self.open:
            copy.wait()


def weight_grad(turned, cells, halves, which, out):
    ff = cells.shape[1] // halves
    columns = ff // 2
    for half in range(halves):
        from_column = pl.ds(pl.multiple_of(half * ff + which * columns, columns), columns)

        def rows_of(i, at, half=half, from_column=from_column):
            out[half, at, :] = nn(turned[at, :], cells[:, from_column]).astype(BF16)

        each_tile(turned.shape[0], 384, rows_of)


def feed_kernel(
    place, first_in, conv_in, land_out, tokens_in, cotangent_in, weights,
    output_to, context_to, slope_to, g_fed_to, g_second_to, unit_to, scale_to, turned_to, active_to, fed_turned_to, sent_to,
    norm_grads, in_w, down_w, out_w, norms, conv, context, tokens, cotangent,
    low, unit, scales, fed, active, slopes, g_fed, g_fed_turned, normed_turned, output, sent,
    sems,
):
    rows, width = tokens.shape
    halves, _, ff = in_w.shape
    part = out_w.shape[2]
    tile = 256
    copies = Copies(sems)
    context_copies = [copies.start(first_in, g_fed_turned), copies.start(conv_in, conv)]
    early = [
        copies.start(weights.at[:, :, pl.ds(2 * ff, part)], out_w),
        copies.start(tokens_in, tokens),
        copies.start(weights.at[:, :, pl.ds(2 * ff + part, LANES)], norms),
    ]
    in_copy = copies.start(weights.at[:, :, pl.ds(0, ff)], in_w)
    down_copy = copies.start(weights.at[:, :, pl.ds(ff, ff)], down_w)
    cotangent_copy = copies.start(cotangent_in, cotangent)
    for copy in context_copies:
        copy.wait()
    context_rows(g_fed_turned, conv, land_out, context)
    copies.out(context, context_to)
    for copy in early:
        copy.wait()
    columns = norms[0].astype(F32).T
    gain0, gain1 = columns[0:1], columns[1:2]
    shift0, shift1 = columns[2:3], columns[3:4]
    norm_grads[...] = jnp.zeros_like(norm_grads)

    def project(i, at):
        attended = nt(context[at, :part], out_w[0])
        for half in range(1, halves):
            attended = attended + nt(context[at, half * part : (half + 1) * part], out_w[half])
        rows_unit, scale = centred_rows(tokens[at, :].astype(F32) + attended)
        unit[at, :] = rows_unit
        scales[at, :] = jnp.broadcast_to(scale, (tile, LANES))
        normed = (rows_unit * gain0 + shift0).astype(BF16)
        low[at, :] = normed
        normed_turned[:, at] = normed.T

    each_tile(rows, tile, project)
    copies.out(unit, unit_to)
    copies.out(scales, scale_to)
    copies.out(normed_turned, turned_to)
    in_copy.wait()
    big = 512

    def hidden_rows(i, at):
        for half in range(halves):
            value, slope = gelu_pair(nn(low[at, :], in_w[half]))
            active[at, half * ff : (half + 1) * ff] = value.astype(BF16)
            slopes[at, half * ff : (half + 1) * ff] = slope.astype(BF16)

    each_tile(rows, tile, hidden_rows)
    copies.out(slopes, slope_to)
    copies.out(active, active_to)
    down_copy.wait()

    def fed_rows(i, at):
        total = nt(active[at, :ff], down_w[0])
        for half in range(1, halves):
            total = total + nt(active[at, half * ff : (half + 1) * ff], down_w[half])
        fed[at, :] = total

    each_tile(rows, big, fed_rows)
    cotangent_copy.wait()

    def second_norm(i, at):
        normed = unit[at, :] * gain0 + shift0
        unit1, scale1 = centred_rows(normed + fed[at, :])
        position = place[0] + i * tile + lax.broadcasted_iota(jnp.int32, (tile, 1), 0)
        live = jnp.where(position < place[1], 1.0, 0.0)
        output[at, :] = (live * (unit1 * gain1 + shift1)).astype(BF16)
        grads = live * cotangent[at, :].astype(F32)
        norm_grads[:, :width] += jnp.sum(grads * unit1, axis=0, keepdims=True)
        norm_grads[:, width:] += jnp.sum(grads, axis=0, keepdims=True)
        second = norm_back(grads, gain1, unit1, scale1)
        fed[at, :] = second
        g_low = second.astype(BF16)
        g_fed[at, :] = g_low
        g_fed_turned[:, at] = g_low.T

    each_tile(rows, tile, second_norm)
    copies.out(output, output_to)
    copies.out(fed, g_second_to)
    copies.out(g_fed, g_fed_to)
    copies.out(g_fed_turned, fed_turned_to)
    weight_grad(g_fed_turned, active, halves, 1 - place[2], sent)
    copies.out(sent, sent_to)
    copies.finish()


ANYWHERE = pl.BlockSpec(memory_space=pl.ANY)


def feed_forward(place, first, conv, land_out, tokens, cotangent, weights, ff, part):
    rows, width = tokens.shape
    halves = weights.shape[0]
    grad = (halves, width, ff // 2)
    shapes = [
        ((rows, width), BF16), ((rows, width), BF16), ((rows, halves * ff), BF16),
        ((rows, width), BF16), ((rows, width), F32), ((rows, width), F32), ((rows, LANES), F32), ((width, rows), BF16),
        ((rows, halves * ff), BF16), ((width, rows), BF16), (grad, BF16), ((1, 2 * width), F32),
    ]
    scratch = [
        ((halves, width, ff), BF16), ((halves, width, ff), BF16), ((halves, width, part), BF16),
        ((halves, width, LANES), BF16), ((width, rows), F32), ((rows, width), BF16),
        ((rows, width), BF16), ((rows, width), BF16),
        ((rows, width), BF16), ((rows, width), F32), ((rows, LANES), F32), ((rows, width), F32),
        ((rows, halves * ff), BF16), ((rows, halves * ff), BF16), ((rows, width), BF16),
        ((width, rows), BF16), ((width, rows), BF16), ((rows, width), BF16), (grad, BF16),
    ]
    return pl.pallas_call(
        feed_kernel,
        out_shape=tuple(jax.ShapeDtypeStruct(*shape) for shape in shapes),
        in_specs=[SCALARS] + [ANYWHERE] * 2 + whole(1) + [ANYWHERE] * 3,
        out_specs=tuple([ANYWHERE] * 11 + whole(1)),
        scratch_shapes=[pltpu.VMEM(*shape) for shape in scratch]
        + [pltpu.SemaphoreType.DMA((19,))],
        compiler_params=PARAMS,
        cost_estimate=lasting(32),
        name="feed_forward",
    )(place, first, conv, land_out, tokens, cotangent, weights)


def feed_back_kernel(
    place, slope_in, g_fed_in, g_second_in, unit_in, scale_in, turned_in, weights,
    g_first_to, g_context_to, g_hidden_to, sent_to, att_turned_to, norm_grads,
    in_w, down_w, out_w, norms, g_hidden, g_fed, second, unit, scales, normed_turned,
    g_att, g_att_turned, g_context, sent,
    sems,
):
    rows, width = second.shape
    halves, _, ff = in_w.shape
    part = out_w.shape[2]
    tile = 256
    copies = Copies(sems)
    early = [
        copies.start(g_fed_in, g_fed),
        copies.start(weights.at[:, :, pl.ds(ff, ff)], down_w),
        copies.start(slope_in, g_hidden),
    ]
    later = [
        copies.start(turned_in, normed_turned),
        copies.start(weights.at[:, :, pl.ds(0, ff)], in_w),
        copies.start(g_second_in, second),
        copies.start(unit_in, unit),
        copies.start(scale_in, scales),
        copies.start(weights.at[:, :, pl.ds(2 * ff + part, LANES)], norms),
        copies.start(weights.at[:, :, pl.ds(2 * ff, part)], out_w),
    ]
    for copy in early:
        copy.wait()
    norm_grads[...] = jnp.zeros_like(norm_grads)
    big = 512

    def back_rows(i, at):
        for half in range(halves):
            g_act = nn(g_fed[at, :], down_w[half])
            to = slice(half * ff, (half + 1) * ff)
            g_hidden[at, to] = (g_act * g_hidden[at, to].astype(F32)).astype(BF16)

    each_tile(rows, big, back_rows)
    copies.out(g_hidden, g_hidden_to)
    later.pop(0).wait()
    weight_grad(normed_turned, g_hidden, halves, 1 - place[2], sent)
    copies.out(sent, sent_to)
    for copy in later:
        copy.wait()
    gain0 = norms[0].astype(F32).T[0:1]

    def normed_rows(i, at):
        total = second[at, :]
        for half in range(halves):
            total = total + nt(g_hidden[at, half * ff : (half + 1) * ff], in_w[half])
        second[at, :] = total

    each_tile(rows, big, normed_rows)

    def first_norm(i, at):
        grads = second[at, :]
        rows_unit, scale = unit[at, :], scales[at, 0:1]
        norm_grads[:, :width] += jnp.sum(grads * rows_unit, axis=0, keepdims=True)
        norm_grads[:, width:] += jnp.sum(grads, axis=0, keepdims=True)
        first = norm_back(grads, gain0, rows_unit, scale)
        second[at, :] = first
        low = first.astype(BF16)
        g_att[at, :] = low
        g_att_turned[:, at] = low.T

    each_tile(rows, tile, first_norm)
    copies.out(second, g_first_to)
    copies.out(g_att_turned, att_turned_to)
    for half in range(halves):
        g_context[:, half * part : (half + 1) * part] = nn(g_att[...], out_w[half]).astype(BF16)
    copies.out(g_context, g_context_to)
    copies.finish()


def feed_backward(place, fed, weights, ff, part):
    rows, width = fed[1].shape
    halves = weights.shape[0]
    grad = (halves, width, ff // 2)
    shapes = [
        ((rows, width), F32), ((rows, width), BF16), ((rows, halves * ff), BF16), (grad, BF16),
        ((width, rows), BF16), ((1, 2 * width), F32),
    ]
    scratch = [
        ((halves, width, ff), BF16), ((halves, width, ff), BF16), ((halves, width, part), BF16),
        ((halves, width, LANES), BF16), ((rows, halves * ff), BF16), ((rows, width), BF16),
        ((rows, width), F32), ((rows, width), F32),
        ((rows, LANES), F32), ((width, rows), BF16),
        ((rows, width), BF16), ((width, rows), BF16), ((rows, width), BF16), (grad, BF16),
    ]
    return pl.pallas_call(
        feed_back_kernel,
        out_shape=tuple(jax.ShapeDtypeStruct(*shape) for shape in shapes),
        in_specs=[SCALARS] + [ANYWHERE] * 7,
        out_specs=tuple([ANYWHERE] * 5 + whole(1)),
        scratch_shapes=[pltpu.VMEM(*shape) for shape in scratch]
        + [pltpu.SemaphoreType.DMA((16,))],
        compiler_params=PARAMS,
        cost_estimate=lasting(27),
        name="feed_backward",
    )(place, *fed, weights)


def kept_kernel(place, turned_in, cells_in, kept, turned, cells, sems):
    halves, width, columns = kept.shape
    ff = 2 * columns
    copies = Copies(sems)
    turned_copy = copies.start(turned_in, turned)
    pieces = []
    for half in range(halves):
        start = pl.multiple_of(half * ff + place[2] * columns, columns)
        pieces.append(copies.start(cells_in.at[:, pl.ds(start, columns)], cells.at[half]))
    turned_copy.wait()
    for half in range(halves):
        pieces[half].wait()

        def rows_of(i, at, half=half):
            kept[half, at, :] = nn(turned[at, :], cells[half]).astype(BF16)

        each_tile(width, 384, rows_of)


def kept_grad(place, turned, cells, halves):
    width, rows = turned.shape
    columns = cells.shape[1] // halves // 2
    return pl.pallas_call(
        kept_kernel,
        out_shape=jax.ShapeDtypeStruct((halves, width, columns), BF16),
        in_specs=[SCALARS] + [ANYWHERE] * 2,
        out_specs=whole(1)[0],
        scratch_shapes=[
            pltpu.VMEM((width, rows), BF16),
            pltpu.VMEM((halves, rows, columns), BF16),
            pltpu.SemaphoreType.DMA((3,)),
        ],
        compiler_params=PARAMS,
        cost_estimate=lasting(5),
        name="kept_grad",
    )(place, turned, cells)


def spread_kernel(place, turned_in, cells_in, other, kept, sent, turned, cells, sems):
    halves, width, columns = other.shape
    ff = 2 * columns
    quarter = columns // 2
    copies = Copies(sems)
    turned_copy = copies.start(turned_in, turned)
    pieces = []
    for half in range(halves):
        start = pl.multiple_of(half * ff + place[2] * columns, columns)
        pieces.append(copies.start(cells_in.at[:, pl.ds(start, columns)], cells.at[half]))
    turned_copy.wait()
    for half in range(halves):
        pieces[half].wait()

        def rows_of(i, at, half=half):
            total = nn(turned[at, :], cells[half]) + other[half, at, :].astype(F32)
            low = total.astype(BF16)
            first = place[4] == 0
            kept[half, at, :] = jnp.where(first, low[:, :quarter], low[:, quarter:])
            sent[half, at, :] = jnp.where(first, low[:, quarter:], low[:, :quarter])

        each_tile(width, 384, rows_of)


def spread_grad(place, turned, cells, other):
    halves, width, columns = other.shape
    rows = turned.shape[1]
    part = jax.ShapeDtypeStruct((halves, width, columns // 2), BF16)
    return pl.pallas_call(
        spread_kernel,
        out_shape=(part, part),
        in_specs=[SCALARS] + [ANYWHERE] * 2 + whole(1),
        out_specs=tuple(whole(2)),
        scratch_shapes=[
            pltpu.VMEM((width, rows), BF16),
            pltpu.VMEM((halves, rows, columns), BF16),
            pltpu.SemaphoreType.DMA((3,)),
        ],
        compiler_params=PARAMS,
        cost_estimate=lasting(6),
        name="spread_grad",
    )(place, turned, cells, other)


def pair_kernel(
    place, one_turned_in, one_cells_in, two_turned_in, two_cells_in, kept, sent,
    one_turned, one_cells, two_turned, two_cells, sems,
):
    copies = Copies(sems)
    loads = [
        copies.start(*pair)
        for pair in (
            (one_turned_in, one_turned), (one_cells_in, one_cells),
            (two_turned_in, two_turned), (two_cells_in, two_cells),
        )
    ]
    for number, (turned, cells) in enumerate(((one_turned, one_cells), (two_turned, two_cells))):
        loads[2 * number].wait()
        loads[2 * number + 1].wait()
        family_grads(turned, cells, place[2] == number, kept, sent)


def pair_grads(place, one_turned, one_cells, two_turned, two_cells, halves):
    width, rows = one_turned.shape
    shape = jax.ShapeDtypeStruct((halves, width, one_cells.shape[1] // halves), BF16)
    return pl.pallas_call(
        pair_kernel,
        out_shape=(shape, shape),
        in_specs=[SCALARS] + [ANYWHERE] * 4,
        out_specs=tuple(whole(2)),
        scratch_shapes=[
            pltpu.VMEM((width, rows), BF16), pltpu.VMEM(one_cells.shape, BF16),
            pltpu.VMEM((width, rows), BF16), pltpu.VMEM(one_cells.shape, BF16),
            pltpu.SemaphoreType.DMA((4,)),
        ],
        compiler_params=PARAMS,
        cost_estimate=lasting(6),
        name="pair_grads",
    )(place, one_turned, one_cells, two_turned, two_cells)


def rank_kernel(place, mine, got, land_tokens, weights, late, through, small):
    halves, width, _ = weights.shape
    part = late.shape[1] // 2
    first = place[2] == 0
    grads = (
        jnp.where(first, mine[:LANDMARKS], got[:LANDMARKS]),
        jnp.where(first, got[:LANDMARKS], mine[:LANDMARKS]),
    )
    counts = landmark_counts(place)
    total = jnp.zeros((2 * LANDMARKS, width), F32)
    for index, grad in enumerate(grads):
        both = jnp.concatenate(split(grad / counts), axis=0)
        for half in range(halves):
            weight = weights[half, :, index * part : (index + 1) * part]
            total = total + nt(both[:, half * part : (half + 1) * part], weight)
    through[...] = jnp.concatenate(split(total[:LANDMARKS] + total[LANDMARKS:]), axis=0)
    zero = jnp.zeros((LANDMARKS, part), F32)
    own = []
    for index, grad in enumerate(grads):
        columns = grad[:, :part]
        for half in range(1, halves):
            columns = jnp.where(place[5] == half, grad[:, half * part : (half + 1) * part], columns)
        own.append(jnp.where(place[2] == 1 - index, columns, zero))
    high, low = split(jnp.concatenate(own, axis=1))
    mean_high, mean_low = split(land_tokens[...] / counts)
    means = jnp.concatenate([mean_high, mean_low, mean_high, jnp.zeros_like(mean_low)], axis=0).T
    factors = jnp.concatenate([high, high, low, jnp.zeros_like(low)], axis=0)
    late[...] = nn(means, factors).astype(BF16)
    gains = jnp.where(first, mine[LANDMARKS:], got[LANDMARKS:])
    shifts = jnp.where(first, got[LANDMARKS:], mine[LANDMARKS:])
    taps = jnp.where(place[5] == 0, gains[2:3], shifts[2:3])
    rows = [gains[1:2], gains[0:1], shifts[1:2], shifts[0:1], taps]
    rows.append(jnp.zeros((small.shape[0] - len(rows), width), F32))
    small[...] = jnp.concatenate(rows, axis=0).astype(BF16)


def rank_parts(place, mine, got, land_tokens, weights):
    halves, width, packed = weights.shape
    return pl.pallas_call(
        rank_kernel,
        out_shape=(
            jax.ShapeDtypeStruct((width, 2 * packed // 3), BF16),
            jax.ShapeDtypeStruct((2 * LANDMARKS, width), BF16),
            jax.ShapeDtypeStruct((16, width), BF16),
        ),
        in_specs=[SCALARS] + whole(4),
        out_specs=tuple(whole(3)),
        compiler_params=PARAMS,
        cost_estimate=lasting(4),
        name="rank_parts",
    )(place, mine, got, land_tokens, weights)


def flipped(values, axis, bit):
    count = lax.axis_size(axis)
    return lax.ppermute(values, axis, [(i, i ^ bit) for i in range(count)])


def side_of(axis, bit):
    return (lax.axis_index(axis) // bit) % 2


def paired(mine, axis, bit, dim):
    other = flipped(mine, axis, bit)
    both = jnp.zeros(mine.shape[:dim] + (2,) + mine.shape[dim:], mine.dtype)
    side = side_of(axis, bit)
    both = lax.dynamic_update_slice_in_dim(both, jnp.expand_dims(mine, dim), side, dim)
    return lax.dynamic_update_slice_in_dim(both, jnp.expand_dims(other, dim), 1 - side, dim)


def ctx_bits():
    bits, bit = [], 1
    while bit < lax.axis_size("ctx"):
        bits.append(bit)
        bit *= 2
    return bits


def sequence_sum(values):
    width = values.shape[1] // 2
    side = side_of("ctx", 1)
    kept = lax.dynamic_slice_in_dim(values, side * width, width, axis=1)
    sent = lax.dynamic_slice_in_dim(values, (1 - side) * width, width, axis=1)
    kept = kept + flipped(sent, "ctx", 1)
    kept = kept + flipped(kept, "tp", 1)
    for bit in ctx_bits()[1:]:
        kept = kept + flipped(kept, "ctx", bit)
    other = flipped(kept, "ctx", 1)
    return jnp.where(
        side == 0,
        jnp.concatenate([kept, other], axis=1),
        jnp.concatenate([other, kept], axis=1),
    )


def to_owner(kept, sent, combine):
    kept = combine(kept, flipped(sent, "ctx", 1))
    for bit in ctx_bits()[1:]:
        view = kept.reshape((-1, 2) + kept.shape[1:])
        side = side_of("ctx", bit)
        sent = lax.dynamic_index_in_dim(view, 1 - side, 1, False)
        kept = lax.dynamic_index_in_dim(view, side, 1, False)
        kept = combine(kept, flipped(sent, "ctx", bit))
    return kept[0], flipped(kept[0], "tp", 1)


def from_owners(part):
    whole_part = part[None]
    for bit in reversed(ctx_bits()):
        both = paired(whole_part, "ctx", bit, 1)
        whole_part = both.reshape((-1,) + part.shape)
    return whole_part.reshape((-1,) + part.shape[1:])


def merge_keys(one, two):
    size = LANES // 2
    one_top, two_top = one[..., size : size + 1], two[..., size : size + 1]
    top = jnp.maximum(one_top, two_top)
    one_factor, two_factor = jnp.exp(one_top - top), jnp.exp(two_top - top)
    summed = one * one_factor + two * two_factor
    lane = lax.broadcasted_iota(jnp.int32, summed.shape, summed.ndim - 1)
    return jnp.where(lane == size, top, summed)


def neighbour_rows(cells, count):
    pieces = lax.axis_size("ctx") * lax.axis_size("tp")
    up = [(i, i + 1) for i in range(pieces - 1)]
    before = lax.ppermute(cells[-count:], ("ctx", "tp"), up)
    after = lax.ppermute(cells[:count], ("ctx", "tp"), [(j, i) for i, j in up])
    return (
        jnp.pad(before, ((LANES - count, 0), (0, 0))),
        jnp.pad(after, ((0, LANES - count), (0, 0))),
    )


def own_quarter(shard):
    rows = shard.shape[0] // lax.axis_size("ctx")
    return lax.dynamic_slice_in_dim(shard, lax.axis_index("ctx") * rows, rows, axis=0)


def gathered(shard):
    full = lax.all_gather(own_quarter(shard), ("tp", "fsdp", "ctx"), tiled=True)
    return full.reshape(lax.axis_size("tp"), -1, shard.shape[1])


def gathered_early(shard, after):
    count = lax.axis_size("fsdp")
    piece = own_quarter(shard)
    if count > 4:
        held = lax.all_gather(piece, "fsdp")
    else:
        here = lax.axis_index("fsdp")
        held = jnp.zeros((count,) + piece.shape, piece.dtype)
        held = lax.dynamic_update_slice_in_dim(held, piece[None], here, 0)
        for step in range(1, count):
            moved = lax.ppermute(piece, "fsdp", [(i, (i + step) % count) for i in range(count)])
            held = lax.dynamic_update_slice_in_dim(held, moved[None], (here - step) % count, 0)
    held, *after = gate(held, *after)
    bits = ctx_bits()
    halves = []
    for number, half in enumerate((held[: count // 2], held[count // 2 :])):
        half = half[None]
        if number == 0:
            half = paired(half[0], "tp", 1, 0)
        for place, bit in enumerate(reversed(bits[1:])):
            half = paired(half, "ctx", bit, 2 + place)
        if number == 1:
            half = paired(half[0], "tp", 1, 0)
        halves.append(paired(half, "ctx", bits[0], 1 + len(bits)))
    full = jnp.concatenate(halves, axis=1)
    return full.reshape(lax.axis_size("tp"), -1, shard.shape[1]), after


def bits_of(axis):
    bits, bit = [], lax.axis_size(axis) // 2
    while bit:
        bits.append(bit)
        bit //= 2
    return bits


def added(*parts):
    return sum(part.astype(F32) for part in parts).astype(BF16)


def cut(cells, axis, bit, dim):
    size = cells.shape[dim] // 2
    side = side_of(axis, bit)
    return (
        lax.dynamic_slice_in_dim(cells, side * size, size, axis=dim),
        lax.dynamic_slice_in_dim(cells, (1 - side) * size, size, axis=dim),
    )


def gate(*values):
    return lax.optimization_barrier(values)


def dotf(spec, *operands):
    return jnp.einsum(spec, *operands, preferred_element_type=F32)


def taps_round(taps):
    middle = taps.shape[1] // 2
    gap = jnp.zeros((taps.shape[0], LANES - taps.shape[1]), F32)
    return jnp.concatenate([taps[:, middle::-1], gap, taps[:, :middle:-1]], axis=1)


def landmark_bounds(length):
    landmark = jnp.arange(LANDMARKS + 1, dtype=jnp.int32)
    return (landmark * length + LANDMARKS - 1) // LANDMARKS


def landmark_counts_of(length):
    bounds = landmark_bounds(length)
    return (bounds[1:] - bounds[:-1]).astype(F32)[:, None]


def landmark_rows(position, length):
    bounds = landmark_bounds(length)
    inside = (position[:, None] >= bounds[None, :-1]) & (position[:, None] < bounds[None, 1:])
    return inside.astype(BF16)


def on_device(
    tokens,
    lengths,
    qk_weight,
    value_weight,
    out_weight,
    in_weight,
    down_weight,
    norm_gains,
    norm_shifts,
    conv_weight,
    cotangent,
):
    tp_count = lax.axis_size("tp")
    tp_index = lax.axis_index("tp")
    ctx_index = lax.axis_index("ctx")
    _, slot_len, model_width = tokens.shape
    rows = slot_len // tp_count
    local_heads, tap_count = conv_weight.shape
    local_width = value_weight.shape[1]
    ff_width = in_weight.shape[1]
    head_size = local_width // local_heads
    heads = local_heads * tp_count
    owners = lax.axis_size("ctx")
    own_heads = heads // owners
    width = local_width * tp_count
    radius = tap_count // 2
    length = lengths[0]

    first_row = (ctx_index * tp_count + tp_index) * rows
    sides = (side_of("ctx", 1), ctx_index, side_of("ctx", ctx_bits()[-1]), tp_index)
    place = jnp.stack([first_row, length, *sides]).astype(jnp.int32)

    norm_columns = jnp.concatenate([norm_gains, norm_shifts], axis=0).T
    norm_columns = jnp.pad(norm_columns, ((0, 0), (0, LANES - norm_columns.shape[1])))
    ffn_full = gathered(
        jnp.concatenate([in_weight, down_weight.T, out_weight.T, norm_columns], axis=1)
    )
    qkv_local = jnp.concatenate([qk_weight[0], qk_weight[1], value_weight], axis=1)
    qkv_full, (tokens, cotangent) = gathered_early(qkv_local, (tokens, cotangent))
    own = lax.dynamic_slice_in_dim(tokens[0], tp_index * rows, rows, axis=0)
    own_cotangent = lax.dynamic_slice_in_dim(cotangent[0], tp_index * rows, rows, axis=0)
    own_taps = jnp.where(ctx_index == 0, conv_weight.astype(F32), 0.0)
    tap_rows = jnp.pad(own_taps, ((0, 8 - local_heads), (0, LANES - tap_count)))
    tap_rows = jnp.where(
        jnp.arange(model_width) // LANES == tp_index,
        jnp.tile(tap_rows, (1, model_width // LANES)),
        0.0,
    )
    land_tokens = sequence_sum(jnp.concatenate([token_sums(place, own), tap_rows], axis=0))
    tap_weights = land_tokens[LANDMARKS : LANDMARKS + local_heads, : tp_count * LANES]
    tap_weights = tap_weights.reshape(local_heads, tp_count, LANES).transpose(1, 0, 2)
    tap_weights = tap_weights.reshape(heads, LANES)[:, :tap_count]
    land_tokens = land_tokens[:LANDMARKS]
    base, base_back = taps_round(tap_weights), taps_round(tap_weights[:, ::-1])

    queries, keys, values, v_plain, land_q, land_k, own_turned, *parts_of_third = projections(
        place, own, land_tokens, qkv_full, head_size, owners
    )
    v_ends = neighbour_rows(v_plain, radius)
    merged, merged_tp = to_owner(*parts_of_third, merge_keys)
    kept_turns = inverse_forward(place, land_q, land_k, owners)
    first, conv = first_and_conv(queries, values, *v_ends, land_k, base)
    merged, own_out = landmark_out(merged, merged_tp, kept_turns[0])
    land_out = from_owners(own_out)

    own_output, context, *fed, active, fed_turned, down_sent, last_norm = feed_forward(
        place, first, conv, land_out, own, own_cotangent, ffn_full, ff_width, local_width
    )
    high = ctx_bits()[-1]
    other_output = flipped(own_output, "tp", 1)
    down_other = flipped(down_sent, "ctx", 1)
    down_kept = kept_grad(place, fed_turned, active, tp_count)
    down_kept, down_other = gate(down_kept, down_other)
    down_mine, down_theirs = cut(down_kept, "ctx", high, 2)
    other_mine, other_theirs = cut(down_other, "ctx", high, 2)
    down_sent = added(down_theirs, other_theirs)
    down_got = flipped(down_sent, "ctx", high)
    fed[0], down_sent = gate(fed[0], down_sent)
    grad_first_res, grad_context, g_hidden, in_sent, att_turned, first_norm = feed_backward(
        place, fed, ffn_full, ff_width, local_width
    )
    in_sent, grad_context, g_hidden, other_output, down_got = gate(
        in_sent, grad_context, g_hidden, other_output, down_got
    )
    in_other = flipped(in_sent, "ctx", 1)
    g_ends = neighbour_rows(grad_context, radius)
    down = added(down_mine, other_mine, down_got)
    down_mine, down_sent = cut(down, "tp", 1, 0)
    down_got = flipped(down_sent, "tp", 1)
    grad_context, down_sent = gate(grad_context, down_sent)
    land_kept, land_sent, g_lk, g_q = attention_back(
        place, queries, grad_context, land_k, land_out, owners
    )
    land_kept, land_sent, in_other, g_ends = gate(land_kept, land_sent, in_other, g_ends)

    land_other = flipped(land_sent, "ctx", 1)
    in_kept, in_sent = spread_grad(place, fed[5], g_hidden, in_other)
    in_kept, in_sent, land_other, down_got = gate(in_kept, in_sent, land_other, down_got)
    land_grads = land_kept + land_other
    land_mine, land_theirs = cut(land_grads, "ctx", high, 0)
    land_got = flipped(land_theirs, "ctx", high)
    land_theirs, in_sent = gate(land_theirs, in_sent)
    in_got = flipped(in_sent, "ctx", high)
    down = added(down_mine, down_got)
    grad_context, in_sent = gate(grad_context, in_sent)
    g_conv, g_taps = conv_back(v_plain, v_ends, grad_context, g_ends, base_back)
    g_conv, g_taps, land_got = gate(g_conv, g_taps, land_got)
    own_grads = (land_mine + land_got)[0]
    tp_grads = flipped(own_grads, "tp", 1)

    def parts(cells):
        return cells.reshape(rows, tp_count, local_width)

    def qkv_part(index):
        return qkv_full[:, :, index * local_width : (index + 1) * local_width]

    g_q, own_grads = gate(g_q, own_grads)
    mixed_kept, mixed_sent = pair_grads(place, att_turned, context, own_turned, g_q, tp_count)
    back_q = grad_first_res + dotf("tpk,pck->tc", parts(g_q), qkv_part(0))
    mixed_kept, mixed_sent, tp_grads, in_got, back_q = gate(
        mixed_kept, mixed_sent, tp_grads, in_got, back_q
    )
    in_sum = added(in_kept, in_got)
    in_mine, in_sent = cut(in_sum, "tp", 1, 0)
    in_got = flipped(in_sent, "tp", 1)
    mixed_got = flipped(mixed_sent, "ctx", 1)
    own_grads, in_sent, mixed_sent = gate(own_grads + tp_grads, in_sent, mixed_sent)
    spread, lq_mid, lk_mid = inverse_backward(
        place, land_q, land_k, merged, own_grads, *kept_turns
    )
    spread, in_got, mixed_got = gate(spread, in_got, mixed_got)
    spread = from_owners(spread)

    pair = jnp.concatenate([added(in_mine, in_got)[0], down[0]], axis=1)
    owner_count = lax.axis_size("fsdp")
    owner_rows = model_width // owner_count
    near, *farther = bits_of("fsdp")[::-1]

    def by_owner_bits(cells):
        return cells.reshape((2,) * (1 + len(farther)) + (-1, cells.shape[-1]))

    def cut_last(cells, bit):
        dim = cells.ndim - 3
        return tuple(piece.squeeze(dim) for piece in cut(cells, "fsdp", bit, dim))

    def by_ctx(cells):
        return cells.reshape(tp_count, owner_count, 2, -1, local_width)

    pair_mine, pair_sent = cut_last(by_owner_bits(pair), near)
    pair_got = flipped(pair_sent, "fsdp", near)
    mixed = added(mixed_kept, mixed_got)
    mixed_mine, mixed_sent = cut(by_ctx(mixed), "ctx", high, 2)
    mixed_got = flipped(mixed_sent, "ctx", high)
    spread, pair_sent, mixed_sent = gate(spread, pair_sent, mixed_sent)
    g_k, g_v, sums, kv_kept, kv_sent = third_back(
        place, keys, values, land_q, spread, g_conv, lq_mid, lk_mid, g_lk, last_norm, first_norm,
        g_taps, own_turned, tp_count,
    )

    kv_got = flipped(kv_sent, "ctx", 1)
    sums_mine, sums_sent = cut(sums, "ctx", 1, 1)
    sums_got = flipped(sums_sent, "ctx", 1)
    kv_kept, kv_sent, sums_got, mixed_got, pair_got = gate(
        kv_kept, kv_sent, sums_got, mixed_got, pair_got
    )
    sums = sums_mine + sums_got
    sums_got = flipped(sums, "tp", 1)
    mixed = added(mixed_mine, mixed_got)
    mixed_mine, mixed_sent = cut(mixed, "tp", 1, 0)
    pair = added(pair_mine, pair_got)
    g_k, kv_sent, sums, mixed_sent = gate(g_k, kv_sent, sums, mixed_sent)
    mixed_got = flipped(mixed_sent, "tp", 1)
    back_k = back_q + dotf("tpk,pck->tc", parts(g_k), qkv_part(1))
    back_k, kv_got, sums_got = gate(back_k, kv_got, sums_got)
    sums = sums + sums_got
    sums_got = flipped(sums, "ctx", high)
    kv = added(kv_kept, kv_got)
    kv_mine, kv_sent = cut(by_ctx(kv), "ctx", high, 2)
    sums, kv_sent = gate(sums, kv_sent)
    kv_got = flipped(kv_sent, "ctx", high)
    back_k, kv_sent = gate(back_k, kv_sent)
    own_grad = (back_k + dotf("tpk,pck->tc", parts(g_v), qkv_part(2))).astype(BF16)
    first_rows = 3 * rows // 8
    other_first = flipped(own_grad[:first_rows], "tp", 1)
    pair_mine, pair_sent = cut_last(pair, farther[0])
    pair_got = flipped(pair_sent, "fsdp", farther[0])
    own_grad, sums_got = gate(own_grad, sums_got)
    sums = sums + sums_got
    sums_got = flipped(sums, "ctx", 1)
    late, through, small = rank_parts(place, sums, sums_got, land_tokens, qkv_full)
    late, through, small, kv_got, mixed_got, other_first = gate(
        late, through, small, kv_got, mixed_got, other_first
    )
    kv = added(kv_mine, kv_got)
    kv_mine, kv_sent = cut(kv, "tp", 1, 0)
    kv_got = flipped(kv_sent, "tp", 1)
    own_grad, kv_sent = gate(own_grad, kv_sent)
    other_second = flipped(own_grad[first_rows:], "tp", 1)

    kv_got, pair_got = gate(kv_got, pair_got)
    late = late.reshape(owner_count, 2, -1, 2 * local_width)
    late = lax.dynamic_index_in_dim(late, place[4], 1, False)
    mixed = added(
        jnp.concatenate([mixed_mine, kv_mine], axis=-1).reshape(late.shape),
        jnp.concatenate([mixed_got, kv_got], axis=-1).reshape(late.shape),
        late,
    )
    small = jnp.broadcast_to(small[None], (owner_count,) + small.shape)
    mixed = by_owner_bits(jnp.concatenate([mixed, small], axis=1))
    mixed_mine, mixed_sent = cut_last(mixed, near)
    mixed_got = flipped(mixed_sent, "fsdp", near)
    pair = added(pair_mine, pair_got)
    for bit in farther[1:]:
        pair_mine, pair_sent = cut_last(pair, bit)
        pair = added(pair_mine, flipped(pair_sent, "fsdp", bit))
    mixed = added(mixed_mine, mixed_got)
    for bit in farther:
        mixed_mine, mixed_sent = cut_last(mixed, bit)
        mixed = added(mixed_mine, flipped(mixed_sent, "fsdp", bit))
    small = mixed[-16:].astype(F32)
    mixed = mixed[:-16]

    def of_core(cells, core):
        cells = cells.reshape((owners // 2, 2) + cells.shape[1:])
        return [cells[i, core] for i in range(owners // 2)]

    mixed, other_second = gate(mixed, other_second)
    mixed = from_owners(mixed[None])
    sides = [jnp.concatenate(of_core(mixed, core), axis=0).astype(F32) for core in range(2)]
    grad_out, grad_k = sides[0][:, :local_width].T, sides[0][:, local_width:]
    grad_q, grad_v = sides[1][:, :local_width], sides[1][:, local_width:]

    own_columns = lax.axis_index("fsdp") * owner_rows
    norm_sums = lax.dynamic_slice_in_dim(small[:4], own_columns, owner_rows, axis=1)
    taps_sum = small[4].reshape(local_heads, LANES)
    grad_taps = jnp.concatenate(
        [taps_sum[:, radius - 1 :: -1], taps_sum[:, : -radius - 2 : -1]], axis=1
    )

    columns = pair.shape[1] // 2
    pair = from_owners(pair[None])
    pieces = [piece for core in range(2) for piece in of_core(pair, core)]
    grad_in = jnp.concatenate([piece[:, :columns] for piece in pieces], axis=1).astype(F32)
    grad_down = jnp.concatenate([piece[:, columns:] for piece in pieces], axis=1).astype(F32).T

    output = jnp.where(
        tp_index == 0,
        jnp.concatenate([own_output, other_output]),
        jnp.concatenate([other_output, own_output]),
    )[None]
    both_grads = jnp.where(
        tp_index == 0,
        jnp.concatenate([own_grad, other_first, other_second]),
        jnp.concatenate([other_first, other_second, own_grad]),
    )
    position = ctx_index * slot_len + jnp.arange(slot_len, dtype=jnp.int32)
    onehot = landmark_rows(position, length)
    grad_tokens = both_grads.astype(F32) + dotf(
        "tm,mc->tc", jnp.concatenate([onehot, onehot], axis=1), through
    )
    grad_tokens = grad_tokens.reshape(1, slot_len, model_width)
    return (
        output,
        grad_tokens,
        jnp.stack([grad_q, grad_k]),
        grad_v,
        grad_out,
        grad_in,
        grad_down,
        norm_sums[:2],
        norm_sums[2:],
        grad_taps,
    )


def solution(mesh):
    in_specs = (
        P("fsdp", "ctx", None),
        P("fsdp"),
        P(None, "fsdp", "tp"),
        P("fsdp", "tp"),
        P("tp", "fsdp"),
        P("fsdp", "tp"),
        P("tp", "fsdp"),
        P(None, "fsdp"),
        P(None, "fsdp"),
        P("tp", None),
        P("fsdp", "ctx", None),
    )
    out_specs = (
        P("fsdp", "ctx", None),
        P("fsdp", "ctx", None),
        P(None, "fsdp", "tp"),
        P("fsdp", "tp"),
        P("tp", "fsdp"),
        P("fsdp", "tp"),
        P("tp", "fsdp"),
        P(None, "fsdp"),
        P(None, "fsdp"),
        P("tp", None),
    )
    return jax.shard_map(
        on_device, mesh=mesh, in_specs=in_specs, out_specs=out_specs, check_vma=False
    )
```

```python
import jax
import jax.numpy as jnp
from jax import lax
from jax.experimental import pallas as pl
from jax.experimental.pallas import tpu as pltpu
from jax.sharding import PartitionSpec as P

LANDMARKS = 64
NEWTON = 6
LANES = 128
VMEM_BYTES = 56 * 2**20

HIGH = lax.Precision.HIGHEST
F32 = jnp.float32
BF16 = jnp.bfloat16


def lasting(microseconds):
    return pl.CostEstimate(
        flops=int(microseconds * 1.1535e9), bytes_accessed=int(microseconds * 1e5), transcendentals=0
    )


def nn(left, right):
    return jnp.dot(left, right, preferred_element_type=F32)


def nt(left, right):
    return lax.dot_general(left, right, (((1,), (1,)), ((), ())), preferred_element_type=F32)


def split(wide):
    high = wide.astype(BF16)
    return high, (wide - high.astype(F32)).astype(BF16)


def each_tile(count, tile, body):
    def step(i, _):
        body(i, pl.ds(pl.multiple_of(i * tile, tile), tile))
        return 0

    lax.fori_loop(0, count // tile, step, 0)


def family_grads(turned, cells, mine, kept, sent):
    halves, width, columns = kept.shape

    def rows_of(i, at):
        total = nn(turned[at, :], cells[...]).astype(BF16)

        @pl.when(mine)
        def _():
            for half in range(halves):
                kept[half, at, :] = total[:, half * columns : (half + 1) * columns]

        @pl.when(jnp.logical_not(mine))
        def _():
            for half in range(halves):
                sent[half, at, :] = total[:, half * columns : (half + 1) * columns]

    each_tile(width, 384, rows_of)


def whole(count):
    return [pl.BlockSpec(memory_space=pltpu.VMEM)] * count


SCALARS = pl.BlockSpec(memory_space=pltpu.SMEM)
PARAMS = pltpu.CompilerParams(vmem_limit_bytes=VMEM_BYTES)


def landmark_onehot(place, rows, landmark_axis):
    shape = (LANDMARKS, rows) if landmark_axis == 0 else (rows, LANDMARKS)
    landmark = lax.broadcasted_iota(jnp.int32, shape, landmark_axis)
    position = place[0] + lax.broadcasted_iota(jnp.int32, shape, 1 - landmark_axis)
    start = lax.shift_right_logical(landmark * place[1] + (LANDMARKS - 1), 6)
    end = lax.shift_right_logical((landmark + 1) * place[1] + (LANDMARKS - 1), 6)
    return jnp.where((position >= start) & (position < end), 1.0, 0.0).astype(BF16)


def live_lanes(place, rows):
    position = place[0] + lax.broadcasted_iota(jnp.int32, (1, rows), 1)
    return position < place[1]


def band(base_row):
    ring = pltpu.roll(jnp.broadcast_to(base_row, (LANES, LANES)), 0, 1, stride=1, stride_axis=0)
    gap = lax.broadcasted_iota(jnp.int32, (LANES, LANES), 0) - lax.broadcasted_iota(
        jnp.int32, (LANES, LANES), 1
    )
    zero = jnp.zeros_like(ring)
    before = jnp.where(gap >= LANES - 16, ring, zero).astype(BF16)
    here = jnp.where(jnp.abs(gap) <= 16, ring, zero).astype(BF16)
    after = jnp.where(gap <= 16 - LANES, ring, zero).astype(BF16)
    return before, here, after


def convolved(blocks, bands):
    count = len(blocks) - 2
    size = blocks[0].shape[0]
    stacked = jnp.concatenate(
        [jnp.concatenate(blocks[i : i + 3], axis=1) for i in range(count)], axis=0
    )
    out = nn(stacked, jnp.concatenate(bands, axis=0))
    return jnp.concatenate([out[i * size : (i + 1) * size] for i in range(count)], axis=1)


def token_sums_kernel(place, tokens, sums):
    sums[...] = nn(landmark_onehot(place, tokens.shape[0], 0), tokens[...])


def token_sums(place, tokens):
    return pl.pallas_call(
        token_sums_kernel,
        out_shape=jax.ShapeDtypeStruct((LANDMARKS, tokens.shape[1]), F32),
        in_specs=[SCALARS] + whole(1),
        out_specs=whole(1)[0],
        compiler_params=PARAMS,
        cost_estimate=lasting(2.5),
        name="token_sums",
    )(place, tokens)


def landmark_counts(place):
    landmark = lax.broadcasted_iota(jnp.int32, (LANDMARKS, 1), 0)
    start = lax.shift_right_logical(landmark * place[1] + (LANDMARKS - 1), 6)
    end = lax.shift_right_logical((landmark + 1) * place[1] + (LANDMARKS - 1), 6)
    return (end - start).astype(F32)


def projection_kernel(
    place, tokens, sums, weights, q_out, k_out, v_out, v_plain, land_q, land_k, turned, kept, sent
):
    rows = tokens.shape[0]
    halves, _, packed = weights.shape
    width = packed // 3
    size = land_q.shape[2]
    position = place[0] + lax.broadcasted_iota(jnp.int32, (rows, 1), 0)
    live = jnp.where(position < place[1], 1.0, 0.0)
    scaled = live * 64**-0.25
    means = jnp.concatenate(split(sums[...] / landmark_counts(place)), axis=0)
    cells = tokens[...]
    turned[...] = cells.T
    for half in range(halves):
        for part, out in enumerate((q_out, k_out, v_out)):
            weight = weights[half, :, part * width : (part + 1) * width]
            low = ((live if part == 2 else scaled) * nn(cells, weight)).astype(BF16)
            out[half * width : (half + 1) * width, :] = low.T
            if part == 2:
                v_plain[:, half * width : (half + 1) * width] = low
                continue
            both = nn(means, weight)
            land = (64**-0.25 * (both[:LANDMARKS] + both[LANDMARKS:])).astype(BF16)
            to = land_k if part else land_q
            for head in range(width // size):
                to[half * (width // size) + head] = land[:, head * size : (head + 1) * size]
    third_heads(place, k_out, v_out, land_q, kept, sent)


def projections(place, tokens, sums, weights, size, owners):
    rows = tokens.shape[0]
    width = weights.shape[0] * weights.shape[2] // 3
    turned = jax.ShapeDtypeStruct((width, rows), BF16)
    land = jax.ShapeDtypeStruct((width // size, LANDMARKS, size), BF16)
    return pl.pallas_call(
        projection_kernel,
        out_shape=(turned, turned, turned, jax.ShapeDtypeStruct((rows, width), BF16), land, land)
        + (jax.ShapeDtypeStruct(tokens.shape[::-1], BF16),)
        + owner_parts(width // size, owners),
        in_specs=[SCALARS] + whole(3),
        out_specs=tuple(whole(9)),
        compiler_params=PARAMS,
        cost_estimate=lasting(18),
        name="projections",
    )(place, tokens, sums, weights)


def by_owner(place, h, owners, kept, sent, values):
    per = kept.shape[1]
    for owner in range(owners):
        @pl.when((h >= owner * per) & (h < (owner + 1) * per))
        def _(owner=owner):
            mine = place[2] == owner % 2

            @pl.when(mine)
            def _():
                kept[owner // 2, h - owner * per] = values

            @pl.when(jnp.logical_not(mine))
            def _():
                sent[owner // 2, h - owner * per] = values


def third_heads(place, keys, values, land_q, kept, sent):
    heads = land_q.shape[0]
    size = land_q.shape[2]
    rows = keys.shape[1]
    owners = 2 * kept.shape[0]
    live = live_lanes(place, rows)

    def head(h):
        at = pl.ds(pl.multiple_of(h * size, size), size)
        scores = jnp.where(live, nn(land_q[h], keys[at, :]), -1e30)
        top = jnp.max(scores, axis=1, keepdims=True)
        raised = jnp.where(live, jnp.exp(scores - top), 0.0)
        total = jnp.sum(raised, axis=1, keepdims=True)
        high, low = split(raised)
        value = values[at, :]
        mixed = nt(high, value) + nt(low, value)
        lane = lax.broadcasted_iota(jnp.int32, (LANDMARKS, LANES - size), 1)
        stats = jnp.where(lane == 0, top, jnp.where(lane == 1, total, 0.0))
        by_owner(place, h, owners, kept, sent, jnp.concatenate([mixed, stats], axis=1))

    def pair(i, _):
        head(2 * i)
        head(2 * i + 1)
        return 0

    lax.fori_loop(0, heads // 2, pair, 0)


def owner_parts(heads, owners):
    part = jax.ShapeDtypeStruct((owners // 2, heads // owners, LANDMARKS, LANES), F32)
    return part, part


def dot_high(left, right):
    return jnp.dot(left, right, preferred_element_type=F32, precision=HIGH)


def dot_high_nt(left, right):
    return lax.dot_general(
        left, right, (((1,), (1,)), ((), ())), preferred_element_type=F32, precision=HIGH
    )


def eye():
    row = lax.broadcasted_iota(jnp.int32, (LANDMARKS, LANDMARKS), 0)
    column = lax.broadcasted_iota(jnp.int32, (LANDMARKS, LANDMARKS), 1)
    return jnp.where(row == column, 1.0, 0.0)


def middle_map(land_q, land_k):
    scores = nt(land_q, land_k)
    raised = jnp.exp(scores - jnp.max(scores, axis=1, keepdims=True))
    return raised / jnp.sum(raised, axis=1, keepdims=True)


def inverse_kernel(place, land_q, land_k, kept_v, kept_p, kept_b, kept_c):
    heads = range(kept_v.shape[1])
    one = eye()
    own = [place[3] * len(heads) + h for h in heads]
    middle = [middle_map(land_q[h], land_k[h]) for h in own]
    approx = [m.T / jnp.sum(m * m, keepdims=True) for m in middle]
    for turn in range(NEWTON):
        product = [dot_high(middle[h], approx[h]) for h in heads]
        for h in heads:
            kept_v[turn, h] = approx[h]
            kept_p[turn, h] = product[h]
        bracket = [7.0 * one - p for p in product]
        bracket = [15.0 * one - dot_high(product[h], bracket[h]) for h in heads]
        for h in heads:
            kept_b[turn, h] = bracket[h]
        bracket = [13.0 * one - dot_high(product[h], bracket[h]) for h in heads]
        for h in heads:
            kept_c[turn, h] = bracket[h]
        approx = [0.25 * dot_high(approx[h], bracket[h]) for h in heads]
    for h in heads:
        kept_v[NEWTON, h] = approx[h]


def inverse_forward(place, land_q, land_k, owners):
    heads = land_q.shape[0] // owners
    square = (heads, LANDMARKS, LANDMARKS)
    return pl.pallas_call(
        inverse_kernel,
        out_shape=(
            jax.ShapeDtypeStruct((NEWTON + 1,) + square, F32),
            jax.ShapeDtypeStruct((NEWTON,) + square, F32),
            jax.ShapeDtypeStruct((NEWTON,) + square, F32),
            jax.ShapeDtypeStruct((NEWTON,) + square, F32),
        ),
        in_specs=[SCALARS] + whole(2),
        out_specs=tuple(whole(4)),
        compiler_params=PARAMS,
        cost_estimate=lasting(7),
        name="inverse_forward",
    )(place, land_q, land_k)


def merged_keys(one, two, size):
    one_top, two_top = one[:, size : size + 1], two[:, size : size + 1]
    top = jnp.maximum(one_top, two_top)
    summed = one * jnp.exp(one_top - top) + two * jnp.exp(two_top - top)
    lane = lax.broadcasted_iota(jnp.int32, one.shape, 1)
    return jnp.where(lane == size, top, summed)


def land_out_kernel(one, two, kept_v, merged, land_out):
    size = land_out.shape[2]
    for h in range(one.shape[0]):
        both = merged_keys(one[h], two[h], size)
        merged[h] = both
        mixed = both[:, :size] / both[:, size + 1 : size + 2]
        land_out[h] = dot_high(kept_v[NEWTON, h], mixed).astype(BF16)


def landmark_out(one, two, kept_v):
    heads = one.shape[0]
    return pl.pallas_call(
        land_out_kernel,
        out_shape=(
            jax.ShapeDtypeStruct(one.shape, F32),
            jax.ShapeDtypeStruct((heads, LANDMARKS, LANES // 2), BF16),
        ),
        in_specs=whole(3),
        out_specs=tuple(whole(2)),
        compiler_params=PARAMS,
        cost_estimate=lasting(2.2),
        name="landmark_out",
    )(one, two, kept_v)


def inverse_back_kernel(
    place, land_q, land_k, merged, grads, kept_v, kept_p, kept_b, kept_c, spread, g_lq, g_lk
):
    heads = range(grads.shape[0])
    size = land_q.shape[2]
    one = eye()
    own = [place[3] * len(heads) + h for h in heads]
    middle = [middle_map(land_q[h], land_k[h]) for h in own]
    turned = [m.T for m in middle]
    g_approx = []
    for h in heads:
        mixed = merged[h][:, :size] / merged[h][:, size + 1 : size + 2]
        g_land = grads[h][:, :size]
        g_approx.append(dot_high_nt(g_land, mixed))
        g_mixed = dot_high(kept_v[NEWTON, h].T, g_land)
        row_dot = jnp.sum(g_mixed * mixed, axis=1, keepdims=True)
        lane = lax.broadcasted_iota(jnp.int32, (LANDMARKS, LANES - size), 1)
        top = merged[h][:, size : size + 1]
        total = merged[h][:, size + 1 : size + 2]
        stats = jnp.where(
            lane == 0, row_dot, jnp.where(lane == 1, top, jnp.where(lane == 2, total, 0.0))
        )
        spread[h] = jnp.concatenate([g_mixed, stats], axis=1)
    g_middle = [jnp.zeros((LANDMARKS, LANDMARKS), F32) for _ in heads]
    for turn in reversed(range(NEWTON)):
        approx = [kept_v[turn, h] for h in heads]
        product = [kept_p[turn, h] for h in heads]
        first = [7.0 * one - p for p in product]
        second = [kept_b[turn, h] for h in heads]
        third = [kept_c[turn, h] for h in heads]
        g_third = [0.25 * dot_high(approx[h].T, g_approx[h]) for h in heads]
        g_back = [0.25 * dot_high_nt(g_approx[h], third[h]) for h in heads]
        g_product = [-dot_high_nt(g_third[h], second[h]) for h in heads]
        pt = [p.T for p in product]
        g_second = [-dot_high(pt[h], g_third[h]) for h in heads]
        g_product = [g_product[h] - dot_high_nt(g_second[h], first[h]) for h in heads]
        g_product = [g_product[h] + dot_high(pt[h], g_second[h]) for h in heads]
        g_middle = [g_middle[h] + dot_high_nt(g_product[h], approx[h]) for h in heads]
        g_approx = [g_back[h] + dot_high(turned[h], g_product[h]) for h in heads]
    for h in heads:
        m = middle[h]
        size_sum = jnp.sum(m * m, keepdims=True)
        g_size = -jnp.sum(g_approx[h] * turned[h], keepdims=True) / (size_sum * size_sum)
        g_m = g_middle[h] + g_approx[h].T / size_sum + 2.0 * g_size * m
        g_scores = m * (g_m - jnp.sum(g_m * m, axis=1, keepdims=True))
        g_lq[h] = dot_high(g_scores, land_k[own[h]].astype(F32))
        g_lk[h] = dot_high(g_scores.T, land_q[own[h]].astype(F32))


def inverse_backward(place, land_q, land_k, merged, grads, *kept):
    heads = grads.shape[0]
    square = jax.ShapeDtypeStruct((heads,) + land_q.shape[1:], F32)
    return pl.pallas_call(
        inverse_back_kernel,
        out_shape=(jax.ShapeDtypeStruct((heads, LANDMARKS, LANES), F32), square, square),
        in_specs=[SCALARS] + whole(8),
        out_specs=tuple(whole(3)),
        compiler_params=PARAMS,
        cost_estimate=lasting(11.5),
        name="inverse_backward",
    )(place, land_q, land_k, merged, grads, *kept)


def first_map(land_k, queries):
    scores = nn(land_k, queries)
    raised = jnp.exp(scores - jnp.max(scores, axis=0, keepdims=True))
    return raised * (1.0 / jnp.sum(raised, axis=0, keepdims=True))


def head_blocks(cells, ends, at):
    rows = cells.shape[1]
    left, right = ends
    return (
        [left[at, :]]
        + [cells[at, i * LANES : (i + 1) * LANES] for i in range(rows // LANES)]
        + [right[at, :]]
    )


def first_conv_kernel(queries, values, left, right, land_k, base, first, conv, ends):
    heads, _, size = land_k.shape
    ends[0] = left[...].T
    ends[1] = right[...].T

    def head(h):
        at = pl.ds(pl.multiple_of(h * size, size), size)
        first[at, :] = first_map(land_k[h], queries[at, :]).astype(BF16)
        blocks = head_blocks(values, (ends.at[0], ends.at[1]), at)
        conv[at, :] = convolved(blocks, band(base[pl.ds(h, 1), :]))

    def pair(i, _):
        head(2 * i)
        head(2 * i + 1)
        return 0

    lax.fori_loop(0, heads // 2, pair, 0)


def first_and_conv(queries, values, left, right, land_k, base):
    width, rows = queries.shape
    return pl.pallas_call(
        first_conv_kernel,
        out_shape=(
            jax.ShapeDtypeStruct((width, rows), BF16),
            jax.ShapeDtypeStruct((width, rows), F32),
        ),
        in_specs=whole(6),
        out_specs=tuple(whole(2)),
        scratch_shapes=[pltpu.VMEM((2, width, LANES), BF16)],
        compiler_params=PARAMS,
        cost_estimate=lasting(8),
        name="first_and_conv",
    )(queries, values, left, right, land_k, base)


def context_rows(first, conv, land_out, context):
    heads, _, size = land_out.shape

    def head(h):
        at = pl.ds(pl.multiple_of(h * size, size), size)
        return (nn(land_out[h].T, first[at, :]) + conv[at, :]).astype(BF16)

    def pair(i, _):
        both = jnp.concatenate([head(2 * i), head(2 * i + 1)], axis=0)
        context[:, pl.ds(pl.multiple_of(i * LANES, LANES), LANES)] = both.T
        return 0

    lax.fori_loop(0, heads // 2, pair, 0)


def attention_back_kernel(
    place, queries, grads, land_k, land_out, kept, sent, g_lk, g_query
):
    heads, _, size = land_k.shape
    rows = queries.shape[1]
    owners = 2 * kept.shape[0]
    scaled = jnp.where(live_lanes(place, rows), 64**-0.25, 0.0)

    def pair(i, _):
        lanes = pl.ds(pl.multiple_of(i * LANES, LANES), LANES)
        turned = grads[:, lanes].T
        g_queries, g_keys = [], []
        for side in range(2):
            h = 2 * i + side
            query = queries[pl.ds(pl.multiple_of(h * size, size), size), :]
            g_context = turned[side * size : (side + 1) * size]
            first = first_map(land_k[h], query)
            g_first = nn(land_out[h], g_context)
            inner = jnp.sum(g_first * first, axis=0, keepdims=True)
            g_scores = (first * (g_first - inner)).astype(BF16)
            g_land = nt(first.astype(BF16), g_context)
            g_key = nt(g_scores, query)
            by_owner(place, h, owners, kept, sent, jnp.concatenate([g_land, g_key], axis=1))
            g_keys.append(g_key)
            g_queries.append((scaled * nn(land_k[h].T, g_scores)).astype(BF16))
        g_query[:, lanes] = jnp.concatenate(g_queries, axis=0).T
        g_lk[:, lanes] = jnp.concatenate(g_keys, axis=1)
        return 0

    lax.fori_loop(0, heads // 2, pair, 0)


def attention_back(place, queries, grads, land_k, land_out, owners):
    width, rows = queries.shape
    heads = land_k.shape[0]
    return pl.pallas_call(
        attention_back_kernel,
        out_shape=owner_parts(heads, owners)
        + (
            jax.ShapeDtypeStruct((LANDMARKS, width), F32),
            jax.ShapeDtypeStruct((rows, width), BF16),
        ),
        in_specs=[SCALARS] + whole(4),
        out_specs=tuple(whole(4)),
        compiler_params=PARAMS,
        cost_estimate=lasting(11.4),
        name="attention_back",
    )(place, queries, grads, land_k, land_out)


def conv_back_kernel(
    v_plain, v_left, v_right, grads, g_left, g_right, base_back, g_value, g_taps, ends
):
    heads = g_taps.shape[0]
    rows, width = grads.shape
    size = width // heads
    blocks_in = rows // LANES
    row = lax.broadcasted_iota(jnp.int32, (LANES, LANES), 0)
    column = lax.broadcasted_iota(jnp.int32, (LANES, LANES), 1)
    reverse = jnp.where(row + column == LANES - 1, 1.0, 0.0).astype(BF16)
    gap = jnp.concatenate([row - column, row - column], axis=1)
    ends[0] = g_left[...].T
    ends[1] = g_right[...].T

    def pair(i, _):
        lanes = pl.ds(pl.multiple_of(i * LANES, LANES), LANES)
        turned = grads[:, lanes].T
        plain = [v_left[LANES - 16 :, lanes]]
        plain += [v_plain[b * LANES : (b + 1) * LANES, lanes] for b in range(blocks_in)]
        plain += [v_right[:16, lanes]]
        for side in range(2):
            h = 2 * i + side
            at = pl.ds(pl.multiple_of(h * size, size), size)
            g_context = turned[side * size : (side + 1) * size]
            blocks = [ends[0, at, :]]
            blocks += [g_context[:, b * LANES : (b + 1) * LANES] for b in range(blocks_in)]
            blocks += [ends[1, at, :]]
            g_value[at, :] = convolved(blocks, band(base_back[pl.ds(h, 1), :]))

        def around(b):
            prior = plain[0] if b == 0 else plain[b][LANES - 16 :]
            return jnp.concatenate([prior, plain[b + 1], plain[b + 2][:16]], axis=0)

        def by_head(b):
            piece = turned[:, b * LANES : (b + 1) * LANES]
            zero = jnp.zeros_like(piece)
            return jnp.concatenate(
                [jnp.where(row < size, piece, zero), jnp.where(row >= size, piece, zero)], axis=1
            )

        total = jnp.zeros((LANES + 32, 2 * LANES), F32)
        for b in range(0, blocks_in, 2):
            total = total + nn(
                jnp.concatenate([around(b), around(b + 1)], axis=1),
                jnp.concatenate([by_head(b), by_head(b + 1)], axis=0),
            )
        empty = jnp.zeros((LANES - 16, 2 * LANES), F32)
        before, here, after = total[:16], total[16 : 16 + LANES], total[16 + LANES :]
        ring = jnp.where(jnp.abs(gap) <= 16, here, 0.0)
        ring = ring + jnp.where(gap >= LANES - 16, jnp.concatenate([empty, before], axis=0), 0.0)
        ring = ring + jnp.where(gap <= 16 - LANES, jnp.concatenate([after, empty], axis=0), 0.0)
        high, low = split(ring)
        lowest = (ring - high.astype(F32) - low.astype(F32)).astype(BF16)
        flat = nn(reverse, high) + nn(reverse, low) + nn(reverse, lowest)
        for side in range(2):
            straight = pltpu.roll(
                flat[:, side * LANES : (side + 1) * LANES], 0, 1, stride=1, stride_axis=0
            )
            g_taps[pl.ds(2 * i + side, 1), :] = jnp.sum(straight, axis=0, keepdims=True)
        return 0

    lax.fori_loop(0, heads // 2, pair, 0)


def conv_back(v_plain, v_ends, grads, g_ends, base_back):
    rows, width = grads.shape
    heads = base_back.shape[0]
    return pl.pallas_call(
        conv_back_kernel,
        out_shape=(
            jax.ShapeDtypeStruct((width, rows), F32),
            jax.ShapeDtypeStruct((heads, LANES), F32),
        ),
        in_specs=whole(7),
        out_specs=tuple(whole(2)),
        scratch_shapes=[pltpu.VMEM((2, width, LANES), BF16)],
        compiler_params=PARAMS,
        cost_estimate=lasting(13.6),
        name="conv_back",
    )(v_plain, *v_ends, grads, *g_ends, base_back)


def third_back_kernel(
    place, keys, values, land_q, spread, g_conv, lq_mid, lk_mid, g_lk, last, first, taps, turned,
    g_k, g_v, sums, kept, sent,
):
    heads, _, size = land_q.shape
    rows, width = g_k.shape
    own_heads = lq_mid.shape[0]
    scale = 64**-0.25
    sums[LANDMARKS:, :] = jnp.zeros((sums.shape[0] - LANDMARKS, 2 * width), F32)
    sums[LANDMARKS : LANDMARKS + 1, :] = last[...]
    sums[LANDMARKS + 1 : LANDMARKS + 2, :] = first[...]
    for h in range(heads):
        sums[LANDMARKS + 2 : LANDMARKS + 3, h * LANES : (h + 1) * LANES] = taps[h : h + 1, :]

    def mid(part, h):
        at = h - place[3] * own_heads
        mine = (at >= 0) & (at < own_heads) & (place[5] == 0)
        inside = jnp.clip(at, 0, own_heads - 1)
        return jnp.where(mine, part[inside], 0.0)

    live = live_lanes(place, rows)
    live_row = jnp.where(live, 1.0, 0.0)
    scaled_row = live_row * 64**-0.25

    def pair(i, _):
        lanes = pl.ds(pl.multiple_of(i * LANES, LANES), LANES)
        g_keys, g_values, g_lqs, lks = [], [], [], []
        for side in range(2):
            h = 2 * i + side
            at = pl.ds(pl.multiple_of(h * size, size), size)
            key, value = keys[at, :], values[at, :]
            pack = spread[h]
            g_mixed = pack[:, :size]
            row_dot = pack[:, size : size + 1]
            top = pack[:, size + 1 : size + 2]
            total = pack[:, size + 2 : size + 3]
            scores = nn(land_q[h], key)
            third = jnp.where(live, jnp.exp(scores - top), 0.0) * (1.0 / total)
            gm_high, gm_low = split(g_mixed)
            g_third = nn(gm_high, value) + nn(gm_low, value)
            g_high, g_low = split(third * (g_third - row_dot))
            g_lqs.append(nt(g_high, key) + nt(g_low, key) + mid(lq_mid, h))
            lks.append(mid(lk_mid, h))
            turned = land_q[h].T
            g_key = nn(turned, g_high) + nn(turned, g_low)
            g_keys.append((scaled_row * g_key).astype(BF16))
            t_high, t_low = split(third)
            gmt_high, gmt_low = split(g_mixed.T)
            g_value = nn(gmt_high, t_high) + nn(gmt_high, t_low) + nn(gmt_low, t_high)
            g_values.append((live_row * (g_value + g_conv[at, :])).astype(BF16))
        g_k[:, lanes] = jnp.concatenate(g_keys, axis=0).T
        g_v[:, lanes] = jnp.concatenate(g_values, axis=0).T
        sums[:LANDMARKS, lanes] = scale * jnp.concatenate(g_lqs, axis=1)
        key_lanes = pl.ds(pl.multiple_of(width + i * LANES, LANES), LANES)
        sums[:LANDMARKS, key_lanes] = scale * (g_lk[:, lanes] + jnp.concatenate(lks, axis=1))
        return 0

    lax.fori_loop(0, heads // 2, pair, 0)
    for number, cells in enumerate((g_k, g_v)):
        family_grads(turned, cells, place[2] == number, kept, sent)


def third_back(
    place, keys, values, land_q, spread, g_conv, lq_mid, lk_mid, g_lk, last, first, taps, turned, halves
):
    width, rows = keys.shape
    plain = jax.ShapeDtypeStruct((rows, width), BF16)
    return pl.pallas_call(
        third_back_kernel,
        out_shape=(plain, plain, jax.ShapeDtypeStruct((LANDMARKS + 8, 2 * width), F32))
        + (jax.ShapeDtypeStruct((halves, width, width // halves), BF16),) * 2,
        in_specs=[SCALARS] + whole(12),
        out_specs=tuple(whole(5)),
        compiler_params=PARAMS,
        cost_estimate=lasting(17),
        name="third_back",
    )(
        place, keys, values, land_q, spread, g_conv, lq_mid, lk_mid, g_lk, last, first, taps, turned
    )


def centred_rows(rows):
    centred = rows - jnp.mean(rows, axis=1, keepdims=True)
    scale = lax.rsqrt(jnp.mean(centred * centred, axis=1, keepdims=True) + 1e-05)
    return centred * scale, scale


def norm_back(grads, gain, unit, scale):
    scaled = grads * gain
    inner = jnp.mean(scaled * unit, axis=1, keepdims=True)
    return scale * (scaled - jnp.mean(scaled, axis=1, keepdims=True) - unit * inner)


def gelu_pair(hidden):
    share = 0.5 * (1.0 + lax.erf(hidden * 0.7071067811865476))
    density = jnp.exp(-0.5 * hidden * hidden) * 0.3989422804014327
    return hidden * share, share + hidden * density


class Copies:
    def __init__(self, sems):
        self.sems, self.used, self.open = sems, 0, []

    def start(self, source, target):
        copy = pltpu.make_async_copy(source, target, self.sems.at[self.used])
        self.used += 1
        copy.start()
        return copy

    def out(self, source, target):
        self.open.append(self.start(source, target))

    def finish(self):
        for copy in self.open:
            copy.wait()


def weight_grad(turned, cells, halves, which, out):
    ff = cells.shape[1] // halves
    columns = ff // 2
    for half in range(halves):
        from_column = pl.ds(pl.multiple_of(half * ff + which * columns, columns), columns)

        def rows_of(i, at, half=half, from_column=from_column):
            out[half, at, :] = nn(turned[at, :], cells[:, from_column]).astype(BF16)

        each_tile(turned.shape[0], 384, rows_of)


def feed_kernel(
    place, first_in, conv_in, land_out, tokens_in, cotangent_in, weights,
    output_to, context_to, slope_to, g_fed_to, g_second_to, unit_to, scale_to, turned_to, active_to, fed_turned_to, sent_to,
    norm_grads, in_w, down_w, out_w, norms, conv, context, tokens, cotangent,
    low, unit, scales, fed, active, slopes, g_fed, g_fed_turned, normed_turned, output, sent,
    sems,
):
    rows, width = tokens.shape
    halves, _, ff = in_w.shape
    part = out_w.shape[2]
    tile = 256
    copies = Copies(sems)
    context_copies = [copies.start(first_in, g_fed_turned), copies.start(conv_in, conv)]
    early = [
        copies.start(weights.at[:, :, pl.ds(2 * ff, part)], out_w),
        copies.start(tokens_in, tokens),
        copies.start(weights.at[:, :, pl.ds(2 * ff + part, LANES)], norms),
    ]
    in_copy = copies.start(weights.at[:, :, pl.ds(0, ff)], in_w)
    down_copy = copies.start(weights.at[:, :, pl.ds(ff, ff)], down_w)
    cotangent_copy = copies.start(cotangent_in, cotangent)
    for copy in context_copies:
        copy.wait()
    context_rows(g_fed_turned, conv, land_out, context)
    copies.out(context, context_to)
    for copy in early:
        copy.wait()
    columns = norms[0].astype(F32).T
    gain0, gain1 = columns[0:1], columns[1:2]
    shift0, shift1 = columns[2:3], columns[3:4]
    norm_grads[...] = jnp.zeros_like(norm_grads)

    def project(i, at):
        attended = nt(context[at, :part], out_w[0])
        for half in range(1, halves):
            attended = attended + nt(context[at, half * part : (half + 1) * part], out_w[half])
        rows_unit, scale = centred_rows(tokens[at, :].astype(F32) + attended)
        unit[at, :] = rows_unit
        scales[at, :] = jnp.broadcast_to(scale, (tile, LANES))
        normed = (rows_unit * gain0 + shift0).astype(BF16)
        low[at, :] = normed
        normed_turned[:, at] = normed.T

    each_tile(rows, tile, project)
    copies.out(unit, unit_to)
    copies.out(scales, scale_to)
    copies.out(normed_turned, turned_to)
    in_copy.wait()
    big = 512

    def hidden_rows(i, at):
        for half in range(halves):
            value, slope = gelu_pair(nn(low[at, :], in_w[half]))
            active[at, half * ff : (half + 1) * ff] = value.astype(BF16)
            slopes[at, half * ff : (half + 1) * ff] = slope.astype(BF16)

    each_tile(rows, tile, hidden_rows)
    copies.out(slopes, slope_to)
    copies.out(active, active_to)
    down_copy.wait()

    def fed_rows(i, at):
        total = nt(active[at, :ff], down_w[0])
        for half in range(1, halves):
            total = total + nt(active[at, half * ff : (half + 1) * ff], down_w[half])
        fed[at, :] = total

    each_tile(rows, big, fed_rows)
    cotangent_copy.wait()

    def second_norm(i, at):
        normed = unit[at, :] * gain0 + shift0
        unit1, scale1 = centred_rows(normed + fed[at, :])
        position = place[0] + i * tile + lax.broadcasted_iota(jnp.int32, (tile, 1), 0)
        live = jnp.where(position < place[1], 1.0, 0.0)
        output[at, :] = (live * (unit1 * gain1 + shift1)).astype(BF16)
        grads = live * cotangent[at, :].astype(F32)
        norm_grads[:, :width] += jnp.sum(grads * unit1, axis=0, keepdims=True)
        norm_grads[:, width:] += jnp.sum(grads, axis=0, keepdims=True)
        second = norm_back(grads, gain1, unit1, scale1)
        fed[at, :] = second
        g_low = second.astype(BF16)
        g_fed[at, :] = g_low
        g_fed_turned[:, at] = g_low.T

    each_tile(rows, tile, second_norm)
    copies.out(output, output_to)
    copies.out(fed, g_second_to)
    copies.out(g_fed, g_fed_to)
    copies.out(g_fed_turned, fed_turned_to)
    weight_grad(g_fed_turned, active, halves, 1 - place[2], sent)
    copies.out(sent, sent_to)
    copies.finish()


ANYWHERE = pl.BlockSpec(memory_space=pl.ANY)


def feed_forward(place, first, conv, land_out, tokens, cotangent, weights, ff, part):
    rows, width = tokens.shape
    halves = weights.shape[0]
    grad = (halves, width, ff // 2)
    shapes = [
        ((rows, width), BF16), ((rows, width), BF16), ((rows, halves * ff), BF16),
        ((rows, width), BF16), ((rows, width), F32), ((rows, width), F32), ((rows, LANES), F32), ((width, rows), BF16),
        ((rows, halves * ff), BF16), ((width, rows), BF16), (grad, BF16), ((1, 2 * width), F32),
    ]
    scratch = [
        ((halves, width, ff), BF16), ((halves, width, ff), BF16), ((halves, width, part), BF16),
        ((halves, width, LANES), BF16), ((width, rows), F32), ((rows, width), BF16),
        ((rows, width), BF16), ((rows, width), BF16),
        ((rows, width), BF16), ((rows, width), F32), ((rows, LANES), F32), ((rows, width), F32),
        ((rows, halves * ff), BF16), ((rows, halves * ff), BF16), ((rows, width), BF16),
        ((width, rows), BF16), ((width, rows), BF16), ((rows, width), BF16), (grad, BF16),
    ]
    return pl.pallas_call(
        feed_kernel,
        out_shape=tuple(jax.ShapeDtypeStruct(*shape) for shape in shapes),
        in_specs=[SCALARS] + [ANYWHERE] * 2 + whole(1) + [ANYWHERE] * 3,
        out_specs=tuple([ANYWHERE] * 11 + whole(1)),
        scratch_shapes=[pltpu.VMEM(*shape) for shape in scratch]
        + [pltpu.SemaphoreType.DMA((19,))],
        compiler_params=PARAMS,
        cost_estimate=lasting(32),
        name="feed_forward",
    )(place, first, conv, land_out, tokens, cotangent, weights)


def feed_back_kernel(
    place, slope_in, g_fed_in, g_second_in, unit_in, scale_in, turned_in, weights,
    g_first_to, g_context_to, g_hidden_to, sent_to, att_turned_to, norm_grads,
    in_w, down_w, out_w, norms, g_hidden, g_fed, second, unit, scales, normed_turned,
    g_att, g_att_turned, g_context, sent,
    sems,
):
    rows, width = second.shape
    halves, _, ff = in_w.shape
    part = out_w.shape[2]
    tile = 256
    copies = Copies(sems)
    early = [
        copies.start(g_fed_in, g_fed),
        copies.start(weights.at[:, :, pl.ds(ff, ff)], down_w),
        copies.start(slope_in, g_hidden),
    ]
    later = [
        copies.start(turned_in, normed_turned),
        copies.start(weights.at[:, :, pl.ds(0, ff)], in_w),
        copies.start(g_second_in, second),
        copies.start(unit_in, unit),
        copies.start(scale_in, scales),
        copies.start(weights.at[:, :, pl.ds(2 * ff + part, LANES)], norms),
        copies.start(weights.at[:, :, pl.ds(2 * ff, part)], out_w),
    ]
    for copy in early:
        copy.wait()
    norm_grads[...] = jnp.zeros_like(norm_grads)
    big = 512

    def back_rows(i, at):
        for half in range(halves):
            g_act = nn(g_fed[at, :], down_w[half])
            to = slice(half * ff, (half + 1) * ff)
            g_hidden[at, to] = (g_act * g_hidden[at, to].astype(F32)).astype(BF16)

    each_tile(rows, big, back_rows)
    copies.out(g_hidden, g_hidden_to)
    later.pop(0).wait()
    weight_grad(normed_turned, g_hidden, halves, 1 - place[2], sent)
    copies.out(sent, sent_to)
    for copy in later:
        copy.wait()
    gain0 = norms[0].astype(F32).T[0:1]

    def normed_rows(i, at):
        total = second[at, :]
        for half in range(halves):
            total = total + nt(g_hidden[at, half * ff : (half + 1) * ff], in_w[half])
        second[at, :] = total

    each_tile(rows, big, normed_rows)

    def first_norm(i, at):
        grads = second[at, :]
        rows_unit, scale = unit[at, :], scales[at, 0:1]
        norm_grads[:, :width] += jnp.sum(grads * rows_unit, axis=0, keepdims=True)
        norm_grads[:, width:] += jnp.sum(grads, axis=0, keepdims=True)
        first = norm_back(grads, gain0, rows_unit, scale)
        second[at, :] = first
        low = first.astype(BF16)
        g_att[at, :] = low
        g_att_turned[:, at] = low.T

    each_tile(rows, tile, first_norm)
    copies.out(second, g_first_to)
    copies.out(g_att_turned, att_turned_to)
    for half in range(halves):
        g_context[:, half * part : (half + 1) * part] = nn(g_att[...], out_w[half]).astype(BF16)
    copies.out(g_context, g_context_to)
    copies.finish()


def feed_backward(place, fed, weights, ff, part):
    rows, width = fed[1].shape
    halves = weights.shape[0]
    grad = (halves, width, ff // 2)
    shapes = [
        ((rows, width), F32), ((rows, width), BF16), ((rows, halves * ff), BF16), (grad, BF16),
        ((width, rows), BF16), ((1, 2 * width), F32),
    ]
    scratch = [
        ((halves, width, ff), BF16), ((halves, width, ff), BF16), ((halves, width, part), BF16),
        ((halves, width, LANES), BF16), ((rows, halves * ff), BF16), ((rows, width), BF16),
        ((rows, width), F32), ((rows, width), F32),
        ((rows, LANES), F32), ((width, rows), BF16),
        ((rows, width), BF16), ((width, rows), BF16), ((rows, width), BF16), (grad, BF16),
    ]
    return pl.pallas_call(
        feed_back_kernel,
        out_shape=tuple(jax.ShapeDtypeStruct(*shape) for shape in shapes),
        in_specs=[SCALARS] + [ANYWHERE] * 7,
        out_specs=tuple([ANYWHERE] * 5 + whole(1)),
        scratch_shapes=[pltpu.VMEM(*shape) for shape in scratch]
        + [pltpu.SemaphoreType.DMA((16,))],
        compiler_params=PARAMS,
        cost_estimate=lasting(27),
        name="feed_backward",
    )(place, *fed, weights)


def kept_kernel(place, turned_in, cells_in, kept, turned, cells, sems):
    halves, width, columns = kept.shape
    ff = 2 * columns
    copies = Copies(sems)
    turned_copy = copies.start(turned_in, turned)
    pieces = []
    for half in range(halves):
        start = pl.multiple_of(half * ff + place[2] * columns, columns)
        pieces.append(copies.start(cells_in.at[:, pl.ds(start, columns)], cells.at[half]))
    turned_copy.wait()
    for half in range(halves):
        pieces[half].wait()

        def rows_of(i, at, half=half):
            kept[half, at, :] = nn(turned[at, :], cells[half]).astype(BF16)

        each_tile(width, 384, rows_of)


def kept_grad(place, turned, cells, halves):
    width, rows = turned.shape
    columns = cells.shape[1] // halves // 2
    return pl.pallas_call(
        kept_kernel,
        out_shape=jax.ShapeDtypeStruct((halves, width, columns), BF16),
        in_specs=[SCALARS] + [ANYWHERE] * 2,
        out_specs=whole(1)[0],
        scratch_shapes=[
            pltpu.VMEM((width, rows), BF16),
            pltpu.VMEM((halves, rows, columns), BF16),
            pltpu.SemaphoreType.DMA((3,)),
        ],
        compiler_params=PARAMS,
        cost_estimate=lasting(5),
        name="kept_grad",
    )(place, turned, cells)


def spread_kernel(place, turned_in, cells_in, other, kept, sent, turned, cells, sems):
    halves, width, columns = other.shape
    ff = 2 * columns
    quarter = columns // 2
    copies = Copies(sems)
    turned_copy = copies.start(turned_in, turned)
    pieces = []
    for half in range(halves):
        start = pl.multiple_of(half * ff + place[2] * columns, columns)
        pieces.append(copies.start(cells_in.at[:, pl.ds(start, columns)], cells.at[half]))
    turned_copy.wait()
    for half in range(halves):
        pieces[half].wait()

        def rows_of(i, at, half=half):
            total = nn(turned[at, :], cells[half]) + other[half, at, :].astype(F32)
            low = total.astype(BF16)
            first = place[4] == 0
            kept[half, at, :] = jnp.where(first, low[:, :quarter], low[:, quarter:])
            sent[half, at, :] = jnp.where(first, low[:, quarter:], low[:, :quarter])

        each_tile(width, 384, rows_of)


def spread_grad(place, turned, cells, other):
    halves, width, columns = other.shape
    rows = turned.shape[1]
    part = jax.ShapeDtypeStruct((halves, width, columns // 2), BF16)
    return pl.pallas_call(
        spread_kernel,
        out_shape=(part, part),
        in_specs=[SCALARS] + [ANYWHERE] * 2 + whole(1),
        out_specs=tuple(whole(2)),
        scratch_shapes=[
            pltpu.VMEM((width, rows), BF16),
            pltpu.VMEM((halves, rows, columns), BF16),
            pltpu.SemaphoreType.DMA((3,)),
        ],
        compiler_params=PARAMS,
        cost_estimate=lasting(6),
        name="spread_grad",
    )(place, turned, cells, other)


def pair_kernel(
    place, one_turned_in, one_cells_in, two_turned_in, two_cells_in, kept, sent,
    one_turned, one_cells, two_turned, two_cells, sems,
):
    copies = Copies(sems)
    loads = [
        copies.start(*pair)
        for pair in (
            (one_turned_in, one_turned), (one_cells_in, one_cells),
            (two_turned_in, two_turned), (two_cells_in, two_cells),
        )
    ]
    for number, (turned, cells) in enumerate(((one_turned, one_cells), (two_turned, two_cells))):
        loads[2 * number].wait()
        loads[2 * number + 1].wait()
        family_grads(turned, cells, place[2] == number, kept, sent)


def pair_grads(place, one_turned, one_cells, two_turned, two_cells, halves):
    width, rows = one_turned.shape
    shape = jax.ShapeDtypeStruct((halves, width, one_cells.shape[1] // halves), BF16)
    return pl.pallas_call(
        pair_kernel,
        out_shape=(shape, shape),
        in_specs=[SCALARS] + [ANYWHERE] * 4,
        out_specs=tuple(whole(2)),
        scratch_shapes=[
            pltpu.VMEM((width, rows), BF16), pltpu.VMEM(one_cells.shape, BF16),
            pltpu.VMEM((width, rows), BF16), pltpu.VMEM(one_cells.shape, BF16),
            pltpu.SemaphoreType.DMA((4,)),
        ],
        compiler_params=PARAMS,
        cost_estimate=lasting(6),
        name="pair_grads",
    )(place, one_turned, one_cells, two_turned, two_cells)


def rank_kernel(place, mine, got, land_tokens, weights, late, through, small):
    halves, width, _ = weights.shape
    part = late.shape[1] // 2
    first = place[2] == 0
    grads = (
        jnp.where(first, mine[:LANDMARKS], got[:LANDMARKS]),
        jnp.where(first, got[:LANDMARKS], mine[:LANDMARKS]),
    )
    counts = landmark_counts(place)
    total = jnp.zeros((2 * LANDMARKS, width), F32)
    for index, grad in enumerate(grads):
        both = jnp.concatenate(split(grad / counts), axis=0)
        for half in range(halves):
            weight = weights[half, :, index * part : (index + 1) * part]
            total = total + nt(both[:, half * part : (half + 1) * part], weight)
    through[...] = jnp.concatenate(split(total[:LANDMARKS] + total[LANDMARKS:]), axis=0)
    zero = jnp.zeros((LANDMARKS, part), F32)
    own = []
    for index, grad in enumerate(grads):
        columns = grad[:, :part]
        for half in range(1, halves):
            columns = jnp.where(place[5] == half, grad[:, half * part : (half + 1) * part], columns)
        own.append(jnp.where(place[2] == 1 - index, columns, zero))
    high, low = split(jnp.concatenate(own, axis=1))
    mean_high, mean_low = split(land_tokens[...] / counts)
    means = jnp.concatenate([mean_high, mean_low, mean_high, jnp.zeros_like(mean_low)], axis=0).T
    factors = jnp.concatenate([high, high, low, jnp.zeros_like(low)], axis=0)
    late[...] = nn(means, factors).astype(BF16)
    gains = jnp.where(first, mine[LANDMARKS:], got[LANDMARKS:])
    shifts = jnp.where(first, got[LANDMARKS:], mine[LANDMARKS:])
    taps = jnp.where(place[5] == 0, gains[2:3], shifts[2:3])
    rows = [gains[1:2], gains[0:1], shifts[1:2], shifts[0:1], taps]
    rows.append(jnp.zeros((small.shape[0] - len(rows), width), F32))
    small[...] = jnp.concatenate(rows, axis=0).astype(BF16)


def rank_parts(place, mine, got, land_tokens, weights):
    halves, width, packed = weights.shape
    return pl.pallas_call(
        rank_kernel,
        out_shape=(
            jax.ShapeDtypeStruct((width, 2 * packed // 3), BF16),
            jax.ShapeDtypeStruct((2 * LANDMARKS, width), BF16),
            jax.ShapeDtypeStruct((16, width), BF16),
        ),
        in_specs=[SCALARS] + whole(4),
        out_specs=tuple(whole(3)),
        compiler_params=PARAMS,
        cost_estimate=lasting(4),
        name="rank_parts",
    )(place, mine, got, land_tokens, weights)


def flipped(values, axis, bit):
    count = lax.axis_size(axis)
    return lax.ppermute(values, axis, [(i, i ^ bit) for i in range(count)])


def side_of(axis, bit):
    return (lax.axis_index(axis) // bit) % 2


def paired(mine, axis, bit, dim):
    other = flipped(mine, axis, bit)
    both = jnp.zeros(mine.shape[:dim] + (2,) + mine.shape[dim:], mine.dtype)
    side = side_of(axis, bit)
    both = lax.dynamic_update_slice_in_dim(both, jnp.expand_dims(mine, dim), side, dim)
    return lax.dynamic_update_slice_in_dim(both, jnp.expand_dims(other, dim), 1 - side, dim)


def ctx_bits():
    bits, bit = [], 1
    while bit < lax.axis_size("ctx"):
        bits.append(bit)
        bit *= 2
    return bits


def sequence_halves(values):
    width = values.shape[1] // 2
    side = side_of("ctx", 1)
    kept = lax.dynamic_slice_in_dim(values, side * width, width, axis=1)
    sent = lax.dynamic_slice_in_dim(values, (1 - side) * width, width, axis=1)
    kept = kept + flipped(sent, "ctx", 1)
    kept = kept + flipped(kept, "tp", 1)
    for bit in ctx_bits()[1:]:
        kept = kept + flipped(kept, "ctx", bit)
    return kept, flipped(kept, "ctx", 1)


def joined_halves(kept, other):
    return jnp.where(
        side_of("ctx", 1) == 0,
        jnp.concatenate([kept, other], axis=1),
        jnp.concatenate([other, kept], axis=1),
    )


def to_owner(kept, sent, combine):
    kept = combine(kept, flipped(sent, "ctx", 1))
    for bit in ctx_bits()[1:]:
        view = kept.reshape((-1, 2) + kept.shape[1:])
        side = side_of("ctx", bit)
        sent = lax.dynamic_index_in_dim(view, 1 - side, 1, False)
        kept = lax.dynamic_index_in_dim(view, side, 1, False)
        kept = combine(kept, flipped(sent, "ctx", bit))
    return kept[0], flipped(kept[0], "tp", 1)


def from_owners(part):
    whole_part = part[None]
    for bit in reversed(ctx_bits()):
        both = paired(whole_part, "ctx", bit, 1)
        whole_part = both.reshape((-1,) + part.shape)
    return whole_part.reshape((-1,) + part.shape[1:])


def merge_keys(one, two):
    size = LANES // 2
    one_top, two_top = one[..., size : size + 1], two[..., size : size + 1]
    top = jnp.maximum(one_top, two_top)
    one_factor, two_factor = jnp.exp(one_top - top), jnp.exp(two_top - top)
    summed = one * one_factor + two * two_factor
    lane = lax.broadcasted_iota(jnp.int32, summed.shape, summed.ndim - 1)
    return jnp.where(lane == size, top, summed)


def neighbour_rows(cells, count):
    pieces = lax.axis_size("ctx") * lax.axis_size("tp")
    up = [(i, i + 1) for i in range(pieces - 1)]
    before = lax.ppermute(cells[-count:], ("ctx", "tp"), up)
    after = lax.ppermute(cells[:count], ("ctx", "tp"), [(j, i) for i, j in up])
    return (
        jnp.pad(before, ((LANES - count, 0), (0, 0))),
        jnp.pad(after, ((0, LANES - count), (0, 0))),
    )


def own_quarter(shard):
    rows = shard.shape[0] // lax.axis_size("ctx")
    return lax.dynamic_slice_in_dim(shard, lax.axis_index("ctx") * rows, rows, axis=0)


def gathered(shard):
    full = lax.all_gather(own_quarter(shard), ("tp", "fsdp", "ctx"), tiled=True)
    return full.reshape(lax.axis_size("tp"), -1, shard.shape[1])


def gathered_early(shard, after):
    count = lax.axis_size("fsdp")
    piece = own_quarter(shard)
    if count > 4:
        held = lax.all_gather(piece, "fsdp")
    else:
        here = lax.axis_index("fsdp")
        held = jnp.zeros((count,) + piece.shape, piece.dtype)
        held = lax.dynamic_update_slice_in_dim(held, piece[None], here, 0)
        for step in range(1, count):
            moved = lax.ppermute(piece, "fsdp", [(i, (i + step) % count) for i in range(count)])
            held = lax.dynamic_update_slice_in_dim(held, moved[None], (here - step) % count, 0)
    held, *after = gate(held, *after)
    bits = ctx_bits()
    halves = []
    for number, half in enumerate((held[: count // 2], held[count // 2 :])):
        half = half[None]
        if number == 0:
            half = paired(half[0], "tp", 1, 0)
        for place, bit in enumerate(reversed(bits[1:])):
            half = paired(half, "ctx", bit, 2 + place)
        if number == 1:
            half = paired(half[0], "tp", 1, 0)
        halves.append(paired(half, "ctx", bits[0], 1 + len(bits)))
    full = jnp.concatenate(halves, axis=1)
    return full.reshape(lax.axis_size("tp"), -1, shard.shape[1]), after


def bits_of(axis):
    bits, bit = [], lax.axis_size(axis) // 2
    while bit:
        bits.append(bit)
        bit //= 2
    return bits


def added(*parts):
    return sum(part.astype(F32) for part in parts).astype(BF16)


def cut(cells, axis, bit, dim):
    size = cells.shape[dim] // 2
    side = side_of(axis, bit)
    return (
        lax.dynamic_slice_in_dim(cells, side * size, size, axis=dim),
        lax.dynamic_slice_in_dim(cells, (1 - side) * size, size, axis=dim),
    )


def gate(*values):
    return lax.optimization_barrier(values)


def dotf(spec, *operands):
    return jnp.einsum(spec, *operands, preferred_element_type=F32)


def taps_round(taps):
    middle = taps.shape[1] // 2
    gap = jnp.zeros((taps.shape[0], LANES - taps.shape[1]), F32)
    return jnp.concatenate([taps[:, middle::-1], gap, taps[:, :middle:-1]], axis=1)


def landmark_bounds(length):
    landmark = jnp.arange(LANDMARKS + 1, dtype=jnp.int32)
    return (landmark * length + LANDMARKS - 1) // LANDMARKS


def landmark_counts_of(length):
    bounds = landmark_bounds(length)
    return (bounds[1:] - bounds[:-1]).astype(F32)[:, None]


def landmark_rows(position, length):
    bounds = landmark_bounds(length)
    inside = (position[:, None] >= bounds[None, :-1]) & (position[:, None] < bounds[None, 1:])
    return inside.astype(BF16)


def on_device(
    tokens,
    lengths,
    qk_weight,
    value_weight,
    out_weight,
    in_weight,
    down_weight,
    norm_gains,
    norm_shifts,
    conv_weight,
    cotangent,
):
    tp_count = lax.axis_size("tp")
    tp_index = lax.axis_index("tp")
    ctx_index = lax.axis_index("ctx")
    _, slot_len, model_width = tokens.shape
    rows = slot_len // tp_count
    local_heads, tap_count = conv_weight.shape
    local_width = value_weight.shape[1]
    ff_width = in_weight.shape[1]
    head_size = local_width // local_heads
    heads = local_heads * tp_count
    owners = lax.axis_size("ctx")
    own_heads = heads // owners
    width = local_width * tp_count
    radius = tap_count // 2
    length = lengths[0]

    first_row = (ctx_index * tp_count + tp_index) * rows
    sides = (side_of("ctx", 1), ctx_index, side_of("ctx", ctx_bits()[-1]), tp_index)
    place = jnp.stack([first_row, length, *sides]).astype(jnp.int32)

    norm_columns = jnp.concatenate([norm_gains, norm_shifts], axis=0).T
    norm_columns = jnp.pad(norm_columns, ((0, 0), (0, LANES - norm_columns.shape[1])))
    ffn_full = gathered(
        jnp.concatenate([in_weight, down_weight.T, out_weight.T, norm_columns], axis=1)
    )
    own = lax.dynamic_slice_in_dim(tokens[0], tp_index * rows, rows, axis=0)
    own_taps = jnp.where(ctx_index == 0, conv_weight.astype(F32), 0.0)
    tap_rows = jnp.pad(own_taps, ((0, 8 - local_heads), (0, LANES - tap_count)))
    tap_rows = jnp.where(
        jnp.arange(model_width) // LANES == tp_index,
        jnp.tile(tap_rows, (1, model_width // LANES)),
        0.0,
    )
    land_tokens = jnp.concatenate([token_sums(place, own), tap_rows], axis=0)
    qkv_local = jnp.concatenate([qk_weight[0], qk_weight[1], value_weight], axis=1)
    qkv_local, land_tokens = gate(qkv_local, land_tokens)
    land_tokens, land_other = sequence_halves(land_tokens)
    qkv_full, (cotangent, land_tokens, land_other) = gathered_early(
        qkv_local, (cotangent, land_tokens, land_other)
    )
    land_tokens = joined_halves(land_tokens, land_other)
    own_cotangent = lax.dynamic_slice_in_dim(cotangent[0], tp_index * rows, rows, axis=0)
    tap_weights = land_tokens[LANDMARKS : LANDMARKS + local_heads, : tp_count * LANES]
    tap_weights = tap_weights.reshape(local_heads, tp_count, LANES).transpose(1, 0, 2)
    tap_weights = tap_weights.reshape(heads, LANES)[:, :tap_count]
    land_tokens = land_tokens[:LANDMARKS]
    base, base_back = taps_round(tap_weights), taps_round(tap_weights[:, ::-1])

    queries, keys, values, v_plain, land_q, land_k, own_turned, *parts_of_third = projections(
        place, own, land_tokens, qkv_full, head_size, owners
    )
    v_ends = neighbour_rows(v_plain, radius)
    merged, merged_tp = to_owner(*parts_of_third, merge_keys)
    kept_turns = inverse_forward(place, land_q, land_k, owners)
    first, conv = first_and_conv(queries, values, *v_ends, land_k, base)
    merged, own_out = landmark_out(merged, merged_tp, kept_turns[0])
    land_out = from_owners(own_out)

    own_output, context, *fed, active, fed_turned, down_sent, last_norm = feed_forward(
        place, first, conv, land_out, own, own_cotangent, ffn_full, ff_width, local_width
    )
    high = ctx_bits()[-1]
    other_output = flipped(own_output, "tp", 1)
    down_other = flipped(down_sent, "ctx", 1)
    down_kept = kept_grad(place, fed_turned, active, tp_count)
    down_kept, down_other = gate(down_kept, down_other)
    down_mine, down_theirs = cut(down_kept, "ctx", high, 2)
    other_mine, other_theirs = cut(down_other, "ctx", high, 2)
    down_sent = added(down_theirs, other_theirs)
    down_got = flipped(down_sent, "ctx", high)
    fed[0], down_sent = gate(fed[0], down_sent)
    grad_first_res, grad_context, g_hidden, in_sent, att_turned, first_norm = feed_backward(
        place, fed, ffn_full, ff_width, local_width
    )
    in_sent, grad_context, g_hidden, other_output, down_got = gate(
        in_sent, grad_context, g_hidden, other_output, down_got
    )
    in_other = flipped(in_sent, "ctx", 1)
    g_ends = neighbour_rows(grad_context, radius)
    down = added(down_mine, other_mine, down_got)
    down_mine, down_sent = cut(down, "tp", 1, 0)
    down_got = flipped(down_sent, "tp", 1)
    grad_context, down_sent = gate(grad_context, down_sent)
    land_kept, land_sent, g_lk, g_q = attention_back(
        place, queries, grad_context, land_k, land_out, owners
    )
    land_kept, land_sent, in_other, g_ends = gate(land_kept, land_sent, in_other, g_ends)

    land_other = flipped(land_sent, "ctx", 1)
    in_kept, in_sent = spread_grad(place, fed[5], g_hidden, in_other)
    in_kept, in_sent, land_other, down_got = gate(in_kept, in_sent, land_other, down_got)
    land_grads = land_kept + land_other
    land_mine, land_theirs = cut(land_grads, "ctx", high, 0)
    land_got = flipped(land_theirs, "ctx", high)
    land_theirs, in_sent = gate(land_theirs, in_sent)
    in_got = flipped(in_sent, "ctx", high)
    down = added(down_mine, down_got)
    grad_context, in_sent = gate(grad_context, in_sent)
    g_conv, g_taps = conv_back(v_plain, v_ends, grad_context, g_ends, base_back)
    g_conv, g_taps, land_got = gate(g_conv, g_taps, land_got)
    own_grads = (land_mine + land_got)[0]
    tp_grads = flipped(own_grads, "tp", 1)

    def parts(cells):
        return cells.reshape(rows, tp_count, local_width)

    def qkv_part(index):
        return qkv_full[:, :, index * local_width : (index + 1) * local_width]

    g_q, own_grads = gate(g_q, own_grads)
    mixed_kept, mixed_sent = pair_grads(place, att_turned, context, own_turned, g_q, tp_count)
    back_q = grad_first_res + dotf("tpk,pck->tc", parts(g_q), qkv_part(0))
    mixed_kept, mixed_sent, tp_grads, in_got, back_q = gate(
        mixed_kept, mixed_sent, tp_grads, in_got, back_q
    )
    in_sum = added(in_kept, in_got)
    in_mine, in_sent = cut(in_sum, "tp", 1, 0)
    in_got = flipped(in_sent, "tp", 1)
    mixed_got = flipped(mixed_sent, "ctx", 1)
    own_grads, in_sent, mixed_sent = gate(own_grads + tp_grads, in_sent, mixed_sent)
    spread, lq_mid, lk_mid = inverse_backward(
        place, land_q, land_k, merged, own_grads, *kept_turns
    )
    spread, in_got, mixed_got = gate(spread, in_got, mixed_got)
    spread = from_owners(spread)

    pair = jnp.concatenate([added(in_mine, in_got)[0], down[0]], axis=1)
    owner_count = lax.axis_size("fsdp")
    owner_rows = model_width // owner_count
    near, *farther = bits_of("fsdp")[::-1]

    def by_owner_bits(cells):
        return cells.reshape((2,) * (1 + len(farther)) + (-1, cells.shape[-1]))

    def cut_last(cells, bit):
        dim = cells.ndim - 3
        return tuple(piece.squeeze(dim) for piece in cut(cells, "fsdp", bit, dim))

    def by_ctx(cells):
        return cells.reshape(tp_count, owner_count, 2, -1, local_width)

    pair_mine, pair_sent = cut_last(by_owner_bits(pair), near)
    pair_got = flipped(pair_sent, "fsdp", near)
    mixed = added(mixed_kept, mixed_got)
    mixed_mine, mixed_sent = cut(by_ctx(mixed), "ctx", high, 2)
    mixed_got = flipped(mixed_sent, "ctx", high)
    spread, pair_sent, mixed_sent = gate(spread, pair_sent, mixed_sent)
    g_k, g_v, sums, kv_kept, kv_sent = third_back(
        place, keys, values, land_q, spread, g_conv, lq_mid, lk_mid, g_lk, last_norm, first_norm,
        g_taps, own_turned, tp_count,
    )

    kv_got = flipped(kv_sent, "ctx", 1)
    sums_mine, sums_sent = cut(sums, "ctx", 1, 1)
    sums_got = flipped(sums_sent, "ctx", 1)
    kv_kept, kv_sent, sums_got, mixed_got, pair_got = gate(
        kv_kept, kv_sent, sums_got, mixed_got, pair_got
    )
    sums = sums_mine + sums_got
    sums_got = flipped(sums, "tp", 1)
    mixed = added(mixed_mine, mixed_got)
    mixed_mine, mixed_sent = cut(mixed, "tp", 1, 0)
    pair = added(pair_mine, pair_got)
    g_k, kv_sent, sums, mixed_sent = gate(g_k, kv_sent, sums, mixed_sent)
    mixed_got = flipped(mixed_sent, "tp", 1)
    back_k = back_q + dotf("tpk,pck->tc", parts(g_k), qkv_part(1))
    back_k, kv_got, sums_got = gate(back_k, kv_got, sums_got)
    sums = sums + sums_got
    sums_got = flipped(sums, "ctx", high)
    kv = added(kv_kept, kv_got)
    kv_mine, kv_sent = cut(by_ctx(kv), "ctx", high, 2)
    sums, kv_sent = gate(sums, kv_sent)
    kv_got = flipped(kv_sent, "ctx", high)
    back_k, kv_sent = gate(back_k, kv_sent)
    own_grad = (back_k + dotf("tpk,pck->tc", parts(g_v), qkv_part(2))).astype(BF16)
    first_rows = 9 * rows // 16
    other_first = flipped(own_grad[:first_rows], "tp", 1)
    pair_mine, pair_sent = cut_last(pair, farther[0])
    pair_got = flipped(pair_sent, "fsdp", farther[0])
    own_grad, sums_got = gate(own_grad, sums_got)
    sums = sums + sums_got
    sums_got = flipped(sums, "ctx", 1)
    late, through, small = rank_parts(place, sums, sums_got, land_tokens, qkv_full)
    late, through, small, kv_got, mixed_got, other_first = gate(
        late, through, small, kv_got, mixed_got, other_first
    )
    kv = added(kv_mine, kv_got)
    kv_mine, kv_sent = cut(kv, "tp", 1, 0)
    kv_got = flipped(kv_sent, "tp", 1)
    own_grad, kv_sent = gate(own_grad, kv_sent)
    other_second = flipped(own_grad[first_rows:], "tp", 1)

    kv_got, pair_got = gate(kv_got, pair_got)
    late = late.reshape(owner_count, 2, -1, 2 * local_width)
    late = lax.dynamic_index_in_dim(late, place[4], 1, False)
    mixed = added(
        jnp.concatenate([mixed_mine, kv_mine], axis=-1).reshape(late.shape),
        jnp.concatenate([mixed_got, kv_got], axis=-1).reshape(late.shape),
        late,
    )
    small = jnp.broadcast_to(small[None], (owner_count,) + small.shape)
    mixed = by_owner_bits(jnp.concatenate([mixed, small], axis=1))
    mixed_mine, mixed_sent = cut_last(mixed, near)
    mixed_got = flipped(mixed_sent, "fsdp", near)
    pair = added(pair_mine, pair_got)
    for bit in farther[1:]:
        pair_mine, pair_sent = cut_last(pair, bit)
        pair = added(pair_mine, flipped(pair_sent, "fsdp", bit))
    mixed = added(mixed_mine, mixed_got)
    for bit in farther:
        mixed_mine, mixed_sent = cut_last(mixed, bit)
        mixed = added(mixed_mine, flipped(mixed_sent, "fsdp", bit))
    small = mixed[-16:].astype(F32)
    mixed = mixed[:-16]

    def of_core(cells, core):
        cells = cells.reshape((owners // 2, 2) + cells.shape[1:])
        return [cells[i, core] for i in range(owners // 2)]

    mixed, other_second = gate(mixed, other_second)
    mixed = from_owners(mixed[None])
    sides = [jnp.concatenate(of_core(mixed, core), axis=0).astype(F32) for core in range(2)]
    grad_out, grad_k = sides[0][:, :local_width].T, sides[0][:, local_width:]
    grad_q, grad_v = sides[1][:, :local_width], sides[1][:, local_width:]

    own_columns = lax.axis_index("fsdp") * owner_rows
    norm_sums = lax.dynamic_slice_in_dim(small[:4], own_columns, owner_rows, axis=1)
    taps_sum = small[4].reshape(local_heads, LANES)
    grad_taps = jnp.concatenate(
        [taps_sum[:, radius - 1 :: -1], taps_sum[:, : -radius - 2 : -1]], axis=1
    )

    columns = pair.shape[1] // 2
    pair = from_owners(pair[None])
    pieces = [piece for core in range(2) for piece in of_core(pair, core)]
    grad_in = jnp.concatenate([piece[:, :columns] for piece in pieces], axis=1).astype(F32)
    grad_down = jnp.concatenate([piece[:, columns:] for piece in pieces], axis=1).astype(F32).T

    output = jnp.where(
        tp_index == 0,
        jnp.concatenate([own_output, other_output]),
        jnp.concatenate([other_output, own_output]),
    )[None]
    both_grads = jnp.where(
        tp_index == 0,
        jnp.concatenate([own_grad, other_first, other_second]),
        jnp.concatenate([other_first, other_second, own_grad]),
    )
    position = ctx_index * slot_len + jnp.arange(slot_len, dtype=jnp.int32)
    onehot = landmark_rows(position, length)
    grad_tokens = both_grads.astype(F32) + dotf(
        "tm,mc->tc", jnp.concatenate([onehot, onehot], axis=1), through
    )
    grad_tokens = grad_tokens.reshape(1, slot_len, model_width)
    return (
        output,
        grad_tokens,
        jnp.stack([grad_q, grad_k]),
        grad_v,
        grad_out,
        grad_in,
        grad_down,
        norm_sums[:2],
        norm_sums[2:],
        grad_taps,
    )


def solution(mesh):
    in_specs = (
        P("fsdp", "ctx", None),
        P("fsdp"),
        P(None, "fsdp", "tp"),
        P("fsdp", "tp"),
        P("tp", "fsdp"),
        P("fsdp", "tp"),
        P("tp", "fsdp"),
        P(None, "fsdp"),
        P(None, "fsdp"),
        P("tp", None),
        P("fsdp", "ctx", None),
    )
    out_specs = (
        P("fsdp", "ctx", None),
        P("fsdp", "ctx", None),
        P(None, "fsdp", "tp"),
        P("fsdp", "tp"),
        P("tp", "fsdp"),
        P("fsdp", "tp"),
        P("tp", "fsdp"),
        P(None, "fsdp"),
        P(None, "fsdp"),
        P("tp", None),
    )
    return jax.shard_map(
        on_device, mesh=mesh, in_specs=in_specs, out_specs=out_specs, check_vma=False
    )
```

```python
import jax
import jax.numpy as jnp
from jax import lax
from jax.experimental import pallas as pl
from jax.experimental.pallas import tpu as pltpu
from jax.sharding import PartitionSpec as P

LANDMARKS = 64
NEWTON = 6
LANES = 128
VMEM_BYTES = 56 * 2**20

HIGH = lax.Precision.HIGHEST
F32 = jnp.float32
BF16 = jnp.bfloat16


def lasting(microseconds):
    return pl.CostEstimate(
        flops=int(microseconds * 1.1535e9), bytes_accessed=int(microseconds * 1e5), transcendentals=0
    )


def nn(left, right):
    return jnp.dot(left, right, preferred_element_type=F32)


def nt(left, right):
    return lax.dot_general(left, right, (((1,), (1,)), ((), ())), preferred_element_type=F32)


def split(wide):
    high = wide.astype(BF16)
    return high, (wide - high.astype(F32)).astype(BF16)


def each_tile(count, tile, body):
    def step(i, _):
        body(i, pl.ds(pl.multiple_of(i * tile, tile), tile))
        return 0

    lax.fori_loop(0, count // tile, step, 0)


def family_grads(turned, cells, mine, kept, sent):
    halves, width, columns = kept.shape

    def rows_of(i, at):
        total = nn(turned[at, :], cells[...]).astype(BF16)

        @pl.when(mine)
        def _():
            for half in range(halves):
                kept[half, at, :] = total[:, half * columns : (half + 1) * columns]

        @pl.when(jnp.logical_not(mine))
        def _():
            for half in range(halves):
                sent[half, at, :] = total[:, half * columns : (half + 1) * columns]

    each_tile(width, 384, rows_of)


def whole(count):
    return [pl.BlockSpec(memory_space=pltpu.VMEM)] * count


SCALARS = pl.BlockSpec(memory_space=pltpu.SMEM)
PARAMS = pltpu.CompilerParams(vmem_limit_bytes=VMEM_BYTES)


def landmark_onehot(place, rows, landmark_axis):
    shape = (LANDMARKS, rows) if landmark_axis == 0 else (rows, LANDMARKS)
    landmark = lax.broadcasted_iota(jnp.int32, shape, landmark_axis)
    position = place[0] + lax.broadcasted_iota(jnp.int32, shape, 1 - landmark_axis)
    start = lax.shift_right_logical(landmark * place[1] + (LANDMARKS - 1), 6)
    end = lax.shift_right_logical((landmark + 1) * place[1] + (LANDMARKS - 1), 6)
    return jnp.where((position >= start) & (position < end), 1.0, 0.0).astype(BF16)


def live_lanes(place, rows):
    position = place[0] + lax.broadcasted_iota(jnp.int32, (1, rows), 1)
    return position < place[1]


def band(base_row):
    ring = pltpu.roll(jnp.broadcast_to(base_row, (LANES, LANES)), 0, 1, stride=1, stride_axis=0)
    gap = lax.broadcasted_iota(jnp.int32, (LANES, LANES), 0) - lax.broadcasted_iota(
        jnp.int32, (LANES, LANES), 1
    )
    zero = jnp.zeros_like(ring)
    before = jnp.where(gap >= LANES - 16, ring, zero).astype(BF16)
    here = jnp.where(jnp.abs(gap) <= 16, ring, zero).astype(BF16)
    after = jnp.where(gap <= 16 - LANES, ring, zero).astype(BF16)
    return before, here, after


def convolved(blocks, bands):
    count = len(blocks) - 2
    size = blocks[0].shape[0]
    stacked = jnp.concatenate(
        [jnp.concatenate(blocks[i : i + 3], axis=1) for i in range(count)], axis=0
    )
    out = nn(stacked, jnp.concatenate(bands, axis=0))
    return jnp.concatenate([out[i * size : (i + 1) * size] for i in range(count)], axis=1)


def token_sums_kernel(place, tokens, sums):
    sums[...] = nn(landmark_onehot(place, tokens.shape[0], 0), tokens[...])


def token_sums(place, tokens):
    return pl.pallas_call(
        token_sums_kernel,
        out_shape=jax.ShapeDtypeStruct((LANDMARKS, tokens.shape[1]), F32),
        in_specs=[SCALARS] + whole(1),
        out_specs=whole(1)[0],
        compiler_params=PARAMS,
        cost_estimate=lasting(2.5),
        name="token_sums",
    )(place, tokens)


def landmark_counts(place):
    landmark = lax.broadcasted_iota(jnp.int32, (LANDMARKS, 1), 0)
    start = lax.shift_right_logical(landmark * place[1] + (LANDMARKS - 1), 6)
    end = lax.shift_right_logical((landmark + 1) * place[1] + (LANDMARKS - 1), 6)
    return (end - start).astype(F32)


def projection_kernel(
    place, tokens, sums, weights, q_out, k_out, v_out, v_plain, land_q, land_k, turned, kept, sent
):
    rows = tokens.shape[0]
    halves, _, packed = weights.shape
    width = packed // 3
    size = land_q.shape[2]
    position = place[0] + lax.broadcasted_iota(jnp.int32, (rows, 1), 0)
    live = jnp.where(position < place[1], 1.0, 0.0)
    scaled = live * 64**-0.25
    means = jnp.concatenate(split(sums[...] / landmark_counts(place)), axis=0)
    cells = tokens[...]
    turned[...] = cells.T
    for half in range(halves):
        for part, out in enumerate((q_out, k_out, v_out)):
            weight = weights[half, :, part * width : (part + 1) * width]
            low = ((live if part == 2 else scaled) * nn(cells, weight)).astype(BF16)
            out[half * width : (half + 1) * width, :] = low.T
            if part == 2:
                v_plain[:, half * width : (half + 1) * width] = low
                continue
            both = nn(means, weight)
            land = (64**-0.25 * (both[:LANDMARKS] + both[LANDMARKS:])).astype(BF16)
            to = land_k if part else land_q
            for head in range(width // size):
                to[half * (width // size) + head] = land[:, head * size : (head + 1) * size]
    third_heads(place, k_out, v_out, land_q, kept, sent)


def projections(place, tokens, sums, weights, size, owners):
    rows = tokens.shape[0]
    width = weights.shape[0] * weights.shape[2] // 3
    turned = jax.ShapeDtypeStruct((width, rows), BF16)
    land = jax.ShapeDtypeStruct((width // size, LANDMARKS, size), BF16)
    return pl.pallas_call(
        projection_kernel,
        out_shape=(turned, turned, turned, jax.ShapeDtypeStruct((rows, width), BF16), land, land)
        + (jax.ShapeDtypeStruct(tokens.shape[::-1], BF16),)
        + owner_parts(width // size, owners),
        in_specs=[SCALARS] + whole(3),
        out_specs=tuple(whole(9)),
        compiler_params=PARAMS,
        cost_estimate=lasting(18),
        name="projections",
    )(place, tokens, sums, weights)


def by_owner(place, h, owners, kept, sent, values):
    per = kept.shape[1]
    for owner in range(owners):
        @pl.when((h >= owner * per) & (h < (owner + 1) * per))
        def _(owner=owner):
            mine = place[2] == owner % 2

            @pl.when(mine)
            def _():
                kept[owner // 2, h - owner * per] = values

            @pl.when(jnp.logical_not(mine))
            def _():
                sent[owner // 2, h - owner * per] = values


def third_heads(place, keys, values, land_q, kept, sent):
    heads = land_q.shape[0]
    size = land_q.shape[2]
    rows = keys.shape[1]
    owners = 2 * kept.shape[0]
    live = live_lanes(place, rows)

    def head(h):
        at = pl.ds(pl.multiple_of(h * size, size), size)
        scores = jnp.where(live, nn(land_q[h], keys[at, :]), -1e30)
        top = jnp.max(scores, axis=1, keepdims=True)
        raised = jnp.where(live, jnp.exp(scores - top), 0.0)
        total = jnp.sum(raised, axis=1, keepdims=True)
        high, low = split(raised)
        value = values[at, :]
        mixed = nt(high, value) + nt(low, value)
        lane = lax.broadcasted_iota(jnp.int32, (LANDMARKS, LANES - size), 1)
        stats = jnp.where(lane == 0, top, jnp.where(lane == 1, total, 0.0))
        by_owner(place, h, owners, kept, sent, jnp.concatenate([mixed, stats], axis=1))

    def pair(i, _):
        head(2 * i)
        head(2 * i + 1)
        return 0

    lax.fori_loop(0, heads // 2, pair, 0)


def owner_parts(heads, owners):
    part = jax.ShapeDtypeStruct((owners // 2, heads // owners, LANDMARKS, LANES), F32)
    return part, part


def dot_high(left, right):
    return jnp.dot(left, right, preferred_element_type=F32, precision=HIGH)


def dot_high_nt(left, right):
    return lax.dot_general(
        left, right, (((1,), (1,)), ((), ())), preferred_element_type=F32, precision=HIGH
    )


def eye():
    row = lax.broadcasted_iota(jnp.int32, (LANDMARKS, LANDMARKS), 0)
    column = lax.broadcasted_iota(jnp.int32, (LANDMARKS, LANDMARKS), 1)
    return jnp.where(row == column, 1.0, 0.0)


def middle_map(land_q, land_k):
    scores = nt(land_q, land_k)
    raised = jnp.exp(scores - jnp.max(scores, axis=1, keepdims=True))
    return raised / jnp.sum(raised, axis=1, keepdims=True)


def inverse_kernel(place, land_q, land_k, kept_v, kept_p, kept_b, kept_c):
    heads = range(kept_v.shape[1])
    one = eye()
    own = [place[3] * len(heads) + h for h in heads]
    middle = [middle_map(land_q[h], land_k[h]) for h in own]
    approx = [m.T / jnp.sum(m * m, keepdims=True) for m in middle]
    for turn in range(NEWTON):
        product = [dot_high(middle[h], approx[h]) for h in heads]
        for h in heads:
            kept_v[turn, h] = approx[h]
            kept_p[turn, h] = product[h]
        bracket = [7.0 * one - p for p in product]
        bracket = [15.0 * one - dot_high(product[h], bracket[h]) for h in heads]
        for h in heads:
            kept_b[turn, h] = bracket[h]
        bracket = [13.0 * one - dot_high(product[h], bracket[h]) for h in heads]
        for h in heads:
            kept_c[turn, h] = bracket[h]
        approx = [0.25 * dot_high(approx[h], bracket[h]) for h in heads]
    for h in heads:
        kept_v[NEWTON, h] = approx[h]


def inverse_forward(place, land_q, land_k, owners):
    heads = land_q.shape[0] // owners
    square = (heads, LANDMARKS, LANDMARKS)
    return pl.pallas_call(
        inverse_kernel,
        out_shape=(
            jax.ShapeDtypeStruct((NEWTON + 1,) + square, F32),
            jax.ShapeDtypeStruct((NEWTON,) + square, F32),
            jax.ShapeDtypeStruct((NEWTON,) + square, F32),
            jax.ShapeDtypeStruct((NEWTON,) + square, F32),
        ),
        in_specs=[SCALARS] + whole(2),
        out_specs=tuple(whole(4)),
        compiler_params=PARAMS,
        cost_estimate=lasting(7),
        name="inverse_forward",
    )(place, land_q, land_k)


def merged_keys(one, two, size):
    one_top, two_top = one[:, size : size + 1], two[:, size : size + 1]
    top = jnp.maximum(one_top, two_top)
    summed = one * jnp.exp(one_top - top) + two * jnp.exp(two_top - top)
    lane = lax.broadcasted_iota(jnp.int32, one.shape, 1)
    return jnp.where(lane == size, top, summed)


def land_out_kernel(one, two, kept_v, merged, land_out):
    size = land_out.shape[2]
    for h in range(one.shape[0]):
        both = merged_keys(one[h], two[h], size)
        merged[h] = both
        mixed = both[:, :size] / both[:, size + 1 : size + 2]
        land_out[h] = dot_high(kept_v[NEWTON, h], mixed).astype(BF16)


def landmark_out(one, two, kept_v):
    heads = one.shape[0]
    return pl.pallas_call(
        land_out_kernel,
        out_shape=(
            jax.ShapeDtypeStruct(one.shape, F32),
            jax.ShapeDtypeStruct((heads, LANDMARKS, LANES // 2), BF16),
        ),
        in_specs=whole(3),
        out_specs=tuple(whole(2)),
        compiler_params=PARAMS,
        cost_estimate=lasting(2.2),
        name="landmark_out",
    )(one, two, kept_v)


def inverse_back_kernel(
    place, land_q, land_k, merged, grads, kept_v, kept_p, kept_b, kept_c, spread, g_lq, g_lk
):
    heads = range(grads.shape[0])
    size = land_q.shape[2]
    one = eye()
    own = [place[3] * len(heads) + h for h in heads]
    middle = [middle_map(land_q[h], land_k[h]) for h in own]
    turned = [m.T for m in middle]
    g_approx = []
    for h in heads:
        mixed = merged[h][:, :size] / merged[h][:, size + 1 : size + 2]
        g_land = grads[h][:, :size]
        g_approx.append(dot_high_nt(g_land, mixed))
        g_mixed = dot_high(kept_v[NEWTON, h].T, g_land)
        row_dot = jnp.sum(g_mixed * mixed, axis=1, keepdims=True)
        lane = lax.broadcasted_iota(jnp.int32, (LANDMARKS, LANES - size), 1)
        top = merged[h][:, size : size + 1]
        total = merged[h][:, size + 1 : size + 2]
        stats = jnp.where(
            lane == 0, row_dot, jnp.where(lane == 1, top, jnp.where(lane == 2, total, 0.0))
        )
        spread[h] = jnp.concatenate([g_mixed, stats], axis=1)
    g_middle = [jnp.zeros((LANDMARKS, LANDMARKS), F32) for _ in heads]
    for turn in reversed(range(NEWTON)):
        approx = [kept_v[turn, h] for h in heads]
        product = [kept_p[turn, h] for h in heads]
        first = [7.0 * one - p for p in product]
        second = [kept_b[turn, h] for h in heads]
        third = [kept_c[turn, h] for h in heads]
        g_third = [0.25 * dot_high(approx[h].T, g_approx[h]) for h in heads]
        g_back = [0.25 * dot_high_nt(g_approx[h], third[h]) for h in heads]
        g_product = [-dot_high_nt(g_third[h], second[h]) for h in heads]
        pt = [p.T for p in product]
        g_second = [-dot_high(pt[h], g_third[h]) for h in heads]
        g_product = [g_product[h] - dot_high_nt(g_second[h], first[h]) for h in heads]
        g_product = [g_product[h] + dot_high(pt[h], g_second[h]) for h in heads]
        g_middle = [g_middle[h] + dot_high_nt(g_product[h], approx[h]) for h in heads]
        g_approx = [g_back[h] + dot_high(turned[h], g_product[h]) for h in heads]
    for h in heads:
        m = middle[h]
        size_sum = jnp.sum(m * m, keepdims=True)
        g_size = -jnp.sum(g_approx[h] * turned[h], keepdims=True) / (size_sum * size_sum)
        g_m = g_middle[h] + g_approx[h].T / size_sum + 2.0 * g_size * m
        g_scores = m * (g_m - jnp.sum(g_m * m, axis=1, keepdims=True))
        g_lq[h] = dot_high(g_scores, land_k[own[h]].astype(F32))
        g_lk[h] = dot_high(g_scores.T, land_q[own[h]].astype(F32))


def inverse_backward(place, land_q, land_k, merged, grads, *kept):
    heads = grads.shape[0]
    square = jax.ShapeDtypeStruct((heads,) + land_q.shape[1:], F32)
    return pl.pallas_call(
        inverse_back_kernel,
        out_shape=(jax.ShapeDtypeStruct((heads, LANDMARKS, LANES), F32), square, square),
        in_specs=[SCALARS] + whole(8),
        out_specs=tuple(whole(3)),
        compiler_params=PARAMS,
        cost_estimate=lasting(11.5),
        name="inverse_backward",
    )(place, land_q, land_k, merged, grads, *kept)


def first_map(land_k, queries):
    scores = nn(land_k, queries)
    raised = jnp.exp(scores - jnp.max(scores, axis=0, keepdims=True))
    return raised * (1.0 / jnp.sum(raised, axis=0, keepdims=True))


def head_blocks(cells, ends, at):
    rows = cells.shape[1]
    left, right = ends
    return (
        [left[at, :]]
        + [cells[at, i * LANES : (i + 1) * LANES] for i in range(rows // LANES)]
        + [right[at, :]]
    )


def first_conv_kernel(queries, values, left, right, land_k, base, first, conv, ends):
    heads, _, size = land_k.shape
    ends[0] = left[...].T
    ends[1] = right[...].T

    def head(h):
        at = pl.ds(pl.multiple_of(h * size, size), size)
        first[at, :] = first_map(land_k[h], queries[at, :]).astype(BF16)
        blocks = head_blocks(values, (ends.at[0], ends.at[1]), at)
        conv[at, :] = convolved(blocks, band(base[pl.ds(h, 1), :]))

    def pair(i, _):
        head(2 * i)
        head(2 * i + 1)
        return 0

    lax.fori_loop(0, heads // 2, pair, 0)


def first_and_conv(queries, values, left, right, land_k, base):
    width, rows = queries.shape
    return pl.pallas_call(
        first_conv_kernel,
        out_shape=(
            jax.ShapeDtypeStruct((width, rows), BF16),
            jax.ShapeDtypeStruct((width, rows), F32),
        ),
        in_specs=whole(6),
        out_specs=tuple(whole(2)),
        scratch_shapes=[pltpu.VMEM((2, width, LANES), BF16)],
        compiler_params=PARAMS,
        cost_estimate=lasting(8),
        name="first_and_conv",
    )(queries, values, left, right, land_k, base)


def context_rows(first, conv, land_out, context):
    heads, _, size = land_out.shape

    def head(h):
        at = pl.ds(pl.multiple_of(h * size, size), size)
        return (nn(land_out[h].T, first[at, :]) + conv[at, :]).astype(BF16)

    def pair(i, _):
        both = jnp.concatenate([head(2 * i), head(2 * i + 1)], axis=0)
        context[:, pl.ds(pl.multiple_of(i * LANES, LANES), LANES)] = both.T
        return 0

    lax.fori_loop(0, heads // 2, pair, 0)


def attention_back_kernel(
    place, queries, grads, land_k, land_out, kept, sent, g_lk, g_query
):
    heads, _, size = land_k.shape
    rows = queries.shape[1]
    owners = 2 * kept.shape[0]
    scaled = jnp.where(live_lanes(place, rows), 64**-0.25, 0.0)

    def pair(i, _):
        lanes = pl.ds(pl.multiple_of(i * LANES, LANES), LANES)
        turned = grads[:, lanes].T
        g_queries, g_keys = [], []
        for side in range(2):
            h = 2 * i + side
            query = queries[pl.ds(pl.multiple_of(h * size, size), size), :]
            g_context = turned[side * size : (side + 1) * size]
            first = first_map(land_k[h], query)
            g_first = nn(land_out[h], g_context)
            inner = jnp.sum(g_first * first, axis=0, keepdims=True)
            g_scores = (first * (g_first - inner)).astype(BF16)
            g_land = nt(first.astype(BF16), g_context)
            g_key = nt(g_scores, query)
            by_owner(place, h, owners, kept, sent, jnp.concatenate([g_land, g_key], axis=1))
            g_keys.append(g_key)
            g_queries.append((scaled * nn(land_k[h].T, g_scores)).astype(BF16))
        g_query[:, lanes] = jnp.concatenate(g_queries, axis=0).T
        g_lk[:, lanes] = jnp.concatenate(g_keys, axis=1)
        return 0

    lax.fori_loop(0, heads // 2, pair, 0)


def attention_back(place, queries, grads, land_k, land_out, owners):
    width, rows = queries.shape
    heads = land_k.shape[0]
    return pl.pallas_call(
        attention_back_kernel,
        out_shape=owner_parts(heads, owners)
        + (
            jax.ShapeDtypeStruct((LANDMARKS, width), F32),
            jax.ShapeDtypeStruct((rows, width), BF16),
        ),
        in_specs=[SCALARS] + whole(4),
        out_specs=tuple(whole(4)),
        compiler_params=PARAMS,
        cost_estimate=lasting(11.4),
        name="attention_back",
    )(place, queries, grads, land_k, land_out)


def conv_back_kernel(
    v_plain, v_left, v_right, grads, g_left, g_right, base_back, g_value, g_taps, ends
):
    heads = g_taps.shape[0]
    rows, width = grads.shape
    size = width // heads
    blocks_in = rows // LANES
    row = lax.broadcasted_iota(jnp.int32, (LANES, LANES), 0)
    column = lax.broadcasted_iota(jnp.int32, (LANES, LANES), 1)
    reverse = jnp.where(row + column == LANES - 1, 1.0, 0.0).astype(BF16)
    gap = jnp.concatenate([row - column, row - column], axis=1)
    ends[0] = g_left[...].T
    ends[1] = g_right[...].T

    def pair(i, _):
        lanes = pl.ds(pl.multiple_of(i * LANES, LANES), LANES)
        turned = grads[:, lanes].T
        plain = [v_left[LANES - 16 :, lanes]]
        plain += [v_plain[b * LANES : (b + 1) * LANES, lanes] for b in range(blocks_in)]
        plain += [v_right[:16, lanes]]
        for side in range(2):
            h = 2 * i + side
            at = pl.ds(pl.multiple_of(h * size, size), size)
            g_context = turned[side * size : (side + 1) * size]
            blocks = [ends[0, at, :]]
            blocks += [g_context[:, b * LANES : (b + 1) * LANES] for b in range(blocks_in)]
            blocks += [ends[1, at, :]]
            g_value[at, :] = convolved(blocks, band(base_back[pl.ds(h, 1), :]))

        def around(b):
            prior = plain[0] if b == 0 else plain[b][LANES - 16 :]
            return jnp.concatenate([prior, plain[b + 1], plain[b + 2][:16]], axis=0)

        def by_head(b):
            piece = turned[:, b * LANES : (b + 1) * LANES]
            zero = jnp.zeros_like(piece)
            return jnp.concatenate(
                [jnp.where(row < size, piece, zero), jnp.where(row >= size, piece, zero)], axis=1
            )

        total = jnp.zeros((LANES + 32, 2 * LANES), F32)
        for b in range(0, blocks_in, 2):
            total = total + nn(
                jnp.concatenate([around(b), around(b + 1)], axis=1),
                jnp.concatenate([by_head(b), by_head(b + 1)], axis=0),
            )
        empty = jnp.zeros((LANES - 16, 2 * LANES), F32)
        before, here, after = total[:16], total[16 : 16 + LANES], total[16 + LANES :]
        ring = jnp.where(jnp.abs(gap) <= 16, here, 0.0)
        ring = ring + jnp.where(gap >= LANES - 16, jnp.concatenate([empty, before], axis=0), 0.0)
        ring = ring + jnp.where(gap <= 16 - LANES, jnp.concatenate([after, empty], axis=0), 0.0)
        high, low = split(ring)
        lowest = (ring - high.astype(F32) - low.astype(F32)).astype(BF16)
        flat = nn(reverse, high) + nn(reverse, low) + nn(reverse, lowest)
        for side in range(2):
            straight = pltpu.roll(
                flat[:, side * LANES : (side + 1) * LANES], 0, 1, stride=1, stride_axis=0
            )
            g_taps[pl.ds(2 * i + side, 1), :] = jnp.sum(straight, axis=0, keepdims=True)
        return 0

    lax.fori_loop(0, heads // 2, pair, 0)


def conv_back(v_plain, v_ends, grads, g_ends, base_back):
    rows, width = grads.shape
    heads = base_back.shape[0]
    return pl.pallas_call(
        conv_back_kernel,
        out_shape=(
            jax.ShapeDtypeStruct((width, rows), F32),
            jax.ShapeDtypeStruct((heads, LANES), F32),
        ),
        in_specs=whole(7),
        out_specs=tuple(whole(2)),
        scratch_shapes=[pltpu.VMEM((2, width, LANES), BF16)],
        compiler_params=PARAMS,
        cost_estimate=lasting(13.6),
        name="conv_back",
    )(v_plain, *v_ends, grads, *g_ends, base_back)


def third_back_kernel(
    place, keys, values, land_q, spread, g_conv, lq_mid, lk_mid, g_lk, last, first, taps, turned,
    g_k, g_v, sums, kept, sent,
):
    heads, _, size = land_q.shape
    rows, width = g_k.shape
    own_heads = lq_mid.shape[0]
    scale = 64**-0.25
    sums[LANDMARKS:, :] = jnp.zeros((sums.shape[0] - LANDMARKS, 2 * width), F32)
    sums[LANDMARKS : LANDMARKS + 1, :] = last[...]
    sums[LANDMARKS + 1 : LANDMARKS + 2, :] = first[...]
    for h in range(heads):
        sums[LANDMARKS + 2 : LANDMARKS + 3, h * LANES : (h + 1) * LANES] = taps[h : h + 1, :]

    def mid(part, h):
        at = h - place[3] * own_heads
        mine = (at >= 0) & (at < own_heads) & (place[5] == 0)
        inside = jnp.clip(at, 0, own_heads - 1)
        return jnp.where(mine, part[inside], 0.0)

    live = live_lanes(place, rows)
    live_row = jnp.where(live, 1.0, 0.0)
    scaled_row = live_row * 64**-0.25

    def pair(i, _):
        lanes = pl.ds(pl.multiple_of(i * LANES, LANES), LANES)
        g_keys, g_values, g_lqs, lks = [], [], [], []
        for side in range(2):
            h = 2 * i + side
            at = pl.ds(pl.multiple_of(h * size, size), size)
            key, value = keys[at, :], values[at, :]
            pack = spread[h]
            g_mixed = pack[:, :size]
            row_dot = pack[:, size : size + 1]
            top = pack[:, size + 1 : size + 2]
            total = pack[:, size + 2 : size + 3]
            scores = nn(land_q[h], key)
            third = jnp.where(live, jnp.exp(scores - top), 0.0) * (1.0 / total)
            gm_high, gm_low = split(g_mixed)
            g_third = nn(gm_high, value) + nn(gm_low, value)
            g_high, g_low = split(third * (g_third - row_dot))
            g_lqs.append(nt(g_high, key) + nt(g_low, key) + mid(lq_mid, h))
            lks.append(mid(lk_mid, h))
            turned = land_q[h].T
            g_key = nn(turned, g_high) + nn(turned, g_low)
            g_keys.append((scaled_row * g_key).astype(BF16))
            t_high, t_low = split(third)
            gmt_high, gmt_low = split(g_mixed.T)
            g_value = nn(gmt_high, t_high) + nn(gmt_high, t_low) + nn(gmt_low, t_high)
            g_values.append((live_row * (g_value + g_conv[at, :])).astype(BF16))
        g_k[:, lanes] = jnp.concatenate(g_keys, axis=0).T
        g_v[:, lanes] = jnp.concatenate(g_values, axis=0).T
        sums[:LANDMARKS, lanes] = scale * jnp.concatenate(g_lqs, axis=1)
        key_lanes = pl.ds(pl.multiple_of(width + i * LANES, LANES), LANES)
        sums[:LANDMARKS, key_lanes] = scale * (g_lk[:, lanes] + jnp.concatenate(lks, axis=1))
        return 0

    lax.fori_loop(0, heads // 2, pair, 0)
    for number, cells in enumerate((g_k, g_v)):
        family_grads(turned, cells, place[2] == number, kept, sent)


def third_back(
    place, keys, values, land_q, spread, g_conv, lq_mid, lk_mid, g_lk, last, first, taps, turned, halves
):
    width, rows = keys.shape
    plain = jax.ShapeDtypeStruct((rows, width), BF16)
    return pl.pallas_call(
        third_back_kernel,
        out_shape=(plain, plain, jax.ShapeDtypeStruct((LANDMARKS + 8, 2 * width), F32))
        + (jax.ShapeDtypeStruct((halves, width, width // halves), BF16),) * 2,
        in_specs=[SCALARS] + whole(12),
        out_specs=tuple(whole(5)),
        compiler_params=PARAMS,
        cost_estimate=lasting(17),
        name="third_back",
    )(
        place, keys, values, land_q, spread, g_conv, lq_mid, lk_mid, g_lk, last, first, taps, turned
    )


def centred_rows(rows):
    centred = rows - jnp.mean(rows, axis=1, keepdims=True)
    scale = lax.rsqrt(jnp.mean(centred * centred, axis=1, keepdims=True) + 1e-05)
    return centred * scale, scale


def norm_back(grads, gain, unit, scale):
    scaled = grads * gain
    inner = jnp.mean(scaled * unit, axis=1, keepdims=True)
    return scale * (scaled - jnp.mean(scaled, axis=1, keepdims=True) - unit * inner)


def gelu_pair(hidden):
    share = 0.5 * (1.0 + lax.erf(hidden * 0.7071067811865476))
    density = jnp.exp(-0.5 * hidden * hidden) * 0.3989422804014327
    return hidden * share, share + hidden * density


class Copies:
    def __init__(self, sems):
        self.sems, self.used, self.open = sems, 0, []

    def start(self, source, target):
        copy = pltpu.make_async_copy(source, target, self.sems.at[self.used])
        self.used += 1
        copy.start()
        return copy

    def out(self, source, target):
        self.open.append(self.start(source, target))

    def finish(self):
        for copy in self.open:
            copy.wait()


def weight_grad(turned, cells, halves, which, out):
    ff = cells.shape[1] // halves
    columns = ff // 2
    for half in range(halves):
        from_column = pl.ds(pl.multiple_of(half * ff + which * columns, columns), columns)

        def rows_of(i, at, half=half, from_column=from_column):
            out[half, at, :] = nn(turned[at, :], cells[:, from_column]).astype(BF16)

        each_tile(turned.shape[0], 384, rows_of)


def feed_kernel(
    place, first_in, conv_in, land_out, tokens_in, cotangent_in, weights,
    output_to, context_to, slope_to, g_fed_to, g_second_to, unit_to, scale_to, turned_to, active_to, fed_turned_to, sent_to,
    norm_grads, in_w, down_w, out_w, norms, conv, context, tokens, cotangent,
    low, unit, scales, fed, active, slopes, g_fed, g_fed_turned, normed_turned, output, sent,
    sems,
):
    rows, width = tokens.shape
    halves, _, ff = in_w.shape
    part = out_w.shape[2]
    tile = 256
    copies = Copies(sems)
    context_copies = [copies.start(first_in, g_fed_turned), copies.start(conv_in, conv)]
    early = [
        copies.start(weights.at[:, :, pl.ds(2 * ff, part)], out_w),
        copies.start(tokens_in, tokens),
        copies.start(weights.at[:, :, pl.ds(2 * ff + part, LANES)], norms),
    ]
    in_copy = copies.start(weights.at[:, :, pl.ds(0, ff)], in_w)
    down_copy = copies.start(weights.at[:, :, pl.ds(ff, ff)], down_w)
    cotangent_copy = copies.start(cotangent_in, cotangent)
    for copy in context_copies:
        copy.wait()
    context_rows(g_fed_turned, conv, land_out, context)
    copies.out(context, context_to)
    for copy in early:
        copy.wait()
    columns = norms[0].astype(F32).T
    gain0, gain1 = columns[0:1], columns[1:2]
    shift0, shift1 = columns[2:3], columns[3:4]
    norm_grads[...] = jnp.zeros_like(norm_grads)

    def project(i, at):
        attended = nt(context[at, :part], out_w[0])
        for half in range(1, halves):
            attended = attended + nt(context[at, half * part : (half + 1) * part], out_w[half])
        rows_unit, scale = centred_rows(tokens[at, :].astype(F32) + attended)
        unit[at, :] = rows_unit
        scales[at, :] = jnp.broadcast_to(scale, (tile, LANES))
        normed = (rows_unit * gain0 + shift0).astype(BF16)
        low[at, :] = normed
        normed_turned[:, at] = normed.T

    each_tile(rows, tile, project)
    copies.out(unit, unit_to)
    copies.out(scales, scale_to)
    copies.out(normed_turned, turned_to)
    in_copy.wait()
    big = 512

    def hidden_rows(i, at):
        for half in range(halves):
            value, slope = gelu_pair(nn(low[at, :], in_w[half]))
            active[at, half * ff : (half + 1) * ff] = value.astype(BF16)
            slopes[at, half * ff : (half + 1) * ff] = slope.astype(BF16)

    each_tile(rows, tile, hidden_rows)
    copies.out(slopes, slope_to)
    copies.out(active, active_to)
    down_copy.wait()

    def fed_rows(i, at):
        total = nt(active[at, :ff], down_w[0])
        for half in range(1, halves):
            total = total + nt(active[at, half * ff : (half + 1) * ff], down_w[half])
        fed[at, :] = total

    each_tile(rows, big, fed_rows)
    cotangent_copy.wait()

    def second_norm(i, at):
        normed = unit[at, :] * gain0 + shift0
        unit1, scale1 = centred_rows(normed + fed[at, :])
        position = place[0] + i * tile + lax.broadcasted_iota(jnp.int32, (tile, 1), 0)
        live = jnp.where(position < place[1], 1.0, 0.0)
        output[at, :] = (live * (unit1 * gain1 + shift1)).astype(BF16)
        grads = live * cotangent[at, :].astype(F32)
        norm_grads[:, :width] += jnp.sum(grads * unit1, axis=0, keepdims=True)
        norm_grads[:, width:] += jnp.sum(grads, axis=0, keepdims=True)
        second = norm_back(grads, gain1, unit1, scale1)
        fed[at, :] = second
        g_low = second.astype(BF16)
        g_fed[at, :] = g_low
        g_fed_turned[:, at] = g_low.T

    each_tile(rows, tile, second_norm)
    copies.out(output, output_to)
    copies.out(fed, g_second_to)
    copies.out(g_fed, g_fed_to)
    copies.out(g_fed_turned, fed_turned_to)
    weight_grad(g_fed_turned, active, halves, 1 - place[2], sent)
    copies.out(sent, sent_to)
    copies.finish()


ANYWHERE = pl.BlockSpec(memory_space=pl.ANY)


def feed_forward(place, first, conv, land_out, tokens, cotangent, weights, ff, part):
    rows, width = tokens.shape
    halves = weights.shape[0]
    grad = (halves, width, ff // 2)
    shapes = [
        ((rows, width), BF16), ((rows, width), BF16), ((rows, halves * ff), BF16),
        ((rows, width), BF16), ((rows, width), F32), ((rows, width), F32), ((rows, LANES), F32), ((width, rows), BF16),
        ((rows, halves * ff), BF16), ((width, rows), BF16), (grad, BF16), ((1, 2 * width), F32),
    ]
    scratch = [
        ((halves, width, ff), BF16), ((halves, width, ff), BF16), ((halves, width, part), BF16),
        ((halves, width, LANES), BF16), ((width, rows), F32), ((rows, width), BF16),
        ((rows, width), BF16), ((rows, width), BF16),
        ((rows, width), BF16), ((rows, width), F32), ((rows, LANES), F32), ((rows, width), F32),
        ((rows, halves * ff), BF16), ((rows, halves * ff), BF16), ((rows, width), BF16),
        ((width, rows), BF16), ((width, rows), BF16), ((rows, width), BF16), (grad, BF16),
    ]
    return pl.pallas_call(
        feed_kernel,
        out_shape=tuple(jax.ShapeDtypeStruct(*shape) for shape in shapes),
        in_specs=[SCALARS] + [ANYWHERE] * 2 + whole(1) + [ANYWHERE] * 3,
        out_specs=tuple([ANYWHERE] * 11 + whole(1)),
        scratch_shapes=[pltpu.VMEM(*shape) for shape in scratch]
        + [pltpu.SemaphoreType.DMA((19,))],
        compiler_params=PARAMS,
        cost_estimate=lasting(32),
        name="feed_forward",
    )(place, first, conv, land_out, tokens, cotangent, weights)


def feed_back_kernel(
    place, slope_in, g_fed_in, g_second_in, unit_in, scale_in, turned_in, weights,
    g_first_to, g_context_to, g_hidden_to, sent_to, att_turned_to, norm_grads,
    in_w, down_w, out_w, norms, g_hidden, g_fed, second, unit, scales, normed_turned,
    g_att, g_att_turned, g_context, sent,
    sems,
):
    rows, width = second.shape
    halves, _, ff = in_w.shape
    part = out_w.shape[2]
    tile = 256
    copies = Copies(sems)
    early = [
        copies.start(g_fed_in, g_fed),
        copies.start(weights.at[:, :, pl.ds(ff, ff)], down_w),
        copies.start(slope_in, g_hidden),
    ]
    later = [
        copies.start(turned_in, normed_turned),
        copies.start(weights.at[:, :, pl.ds(0, ff)], in_w),
        copies.start(g_second_in, second),
        copies.start(unit_in, unit),
        copies.start(scale_in, scales),
        copies.start(weights.at[:, :, pl.ds(2 * ff + part, LANES)], norms),
        copies.start(weights.at[:, :, pl.ds(2 * ff, part)], out_w),
    ]
    for copy in early:
        copy.wait()
    norm_grads[...] = jnp.zeros_like(norm_grads)
    big = 512

    def back_rows(i, at):
        for half in range(halves):
            g_act = nn(g_fed[at, :], down_w[half])
            to = slice(half * ff, (half + 1) * ff)
            g_hidden[at, to] = (g_act * g_hidden[at, to].astype(F32)).astype(BF16)

    each_tile(rows, big, back_rows)
    copies.out(g_hidden, g_hidden_to)
    later.pop(0).wait()
    weight_grad(normed_turned, g_hidden, halves, 1 - place[2], sent)
    copies.out(sent, sent_to)
    for copy in later:
        copy.wait()
    gain0 = norms[0].astype(F32).T[0:1]

    def normed_rows(i, at):
        total = second[at, :]
        for half in range(halves):
            total = total + nt(g_hidden[at, half * ff : (half + 1) * ff], in_w[half])
        second[at, :] = total

    each_tile(rows, big, normed_rows)

    def first_norm(i, at):
        grads = second[at, :]
        rows_unit, scale = unit[at, :], scales[at, 0:1]
        norm_grads[:, :width] += jnp.sum(grads * rows_unit, axis=0, keepdims=True)
        norm_grads[:, width:] += jnp.sum(grads, axis=0, keepdims=True)
        first = norm_back(grads, gain0, rows_unit, scale)
        second[at, :] = first
        low = first.astype(BF16)
        g_att[at, :] = low
        g_att_turned[:, at] = low.T

    each_tile(rows, tile, first_norm)
    copies.out(second, g_first_to)
    copies.out(g_att_turned, att_turned_to)
    for half in range(halves):
        g_context[:, half * part : (half + 1) * part] = nn(g_att[...], out_w[half]).astype(BF16)
    copies.out(g_context, g_context_to)
    copies.finish()


def feed_backward(place, fed, weights, ff, part):
    rows, width = fed[1].shape
    halves = weights.shape[0]
    grad = (halves, width, ff // 2)
    shapes = [
        ((rows, width), F32), ((rows, width), BF16), ((rows, halves * ff), BF16), (grad, BF16),
        ((width, rows), BF16), ((1, 2 * width), F32),
    ]
    scratch = [
        ((halves, width, ff), BF16), ((halves, width, ff), BF16), ((halves, width, part), BF16),
        ((halves, width, LANES), BF16), ((rows, halves * ff), BF16), ((rows, width), BF16),
        ((rows, width), F32), ((rows, width), F32),
        ((rows, LANES), F32), ((width, rows), BF16),
        ((rows, width), BF16), ((width, rows), BF16), ((rows, width), BF16), (grad, BF16),
    ]
    return pl.pallas_call(
        feed_back_kernel,
        out_shape=tuple(jax.ShapeDtypeStruct(*shape) for shape in shapes),
        in_specs=[SCALARS] + [ANYWHERE] * 7,
        out_specs=tuple([ANYWHERE] * 5 + whole(1)),
        scratch_shapes=[pltpu.VMEM(*shape) for shape in scratch]
        + [pltpu.SemaphoreType.DMA((16,))],
        compiler_params=PARAMS,
        cost_estimate=lasting(27),
        name="feed_backward",
    )(place, *fed, weights)


def kept_kernel(place, turned_in, cells_in, kept, turned, cells, sems):
    halves, width, columns = kept.shape
    ff = 2 * columns
    copies = Copies(sems)
    turned_copy = copies.start(turned_in, turned)
    pieces = []
    for half in range(halves):
        start = pl.multiple_of(half * ff + place[2] * columns, columns)
        pieces.append(copies.start(cells_in.at[:, pl.ds(start, columns)], cells.at[half]))
    turned_copy.wait()
    for half in range(halves):
        pieces[half].wait()

        def rows_of(i, at, half=half):
            kept[half, at, :] = nn(turned[at, :], cells[half]).astype(BF16)

        each_tile(width, 384, rows_of)


def kept_grad(place, turned, cells, halves):
    width, rows = turned.shape
    columns = cells.shape[1] // halves // 2
    return pl.pallas_call(
        kept_kernel,
        out_shape=jax.ShapeDtypeStruct((halves, width, columns), BF16),
        in_specs=[SCALARS] + [ANYWHERE] * 2,
        out_specs=whole(1)[0],
        scratch_shapes=[
            pltpu.VMEM((width, rows), BF16),
            pltpu.VMEM((halves, rows, columns), BF16),
            pltpu.SemaphoreType.DMA((3,)),
        ],
        compiler_params=PARAMS,
        cost_estimate=lasting(5),
        name="kept_grad",
    )(place, turned, cells)


def spread_kernel(place, turned_in, cells_in, other, kept, sent, turned, cells, sems):
    halves, width, columns = other.shape
    ff = 2 * columns
    quarter = columns // 2
    copies = Copies(sems)
    turned_copy = copies.start(turned_in, turned)
    pieces = []
    for half in range(halves):
        start = pl.multiple_of(half * ff + place[2] * columns, columns)
        pieces.append(copies.start(cells_in.at[:, pl.ds(start, columns)], cells.at[half]))
    turned_copy.wait()
    for half in range(halves):
        pieces[half].wait()

        def rows_of(i, at, half=half):
            total = nn(turned[at, :], cells[half]) + other[half, at, :].astype(F32)
            low = total.astype(BF16)
            first = place[4] == 0
            kept[half, at, :] = jnp.where(first, low[:, :quarter], low[:, quarter:])
            sent[half, at, :] = jnp.where(first, low[:, quarter:], low[:, :quarter])

        each_tile(width, 384, rows_of)


def spread_grad(place, turned, cells, other):
    halves, width, columns = other.shape
    rows = turned.shape[1]
    part = jax.ShapeDtypeStruct((halves, width, columns // 2), BF16)
    return pl.pallas_call(
        spread_kernel,
        out_shape=(part, part),
        in_specs=[SCALARS] + [ANYWHERE] * 2 + whole(1),
        out_specs=tuple(whole(2)),
        scratch_shapes=[
            pltpu.VMEM((width, rows), BF16),
            pltpu.VMEM((halves, rows, columns), BF16),
            pltpu.SemaphoreType.DMA((3,)),
        ],
        compiler_params=PARAMS,
        cost_estimate=lasting(6),
        name="spread_grad",
    )(place, turned, cells, other)


def pair_kernel(
    place, one_turned_in, one_cells_in, two_turned_in, two_cells_in, kept, sent,
    one_turned, one_cells, two_turned, two_cells, sems,
):
    copies = Copies(sems)
    loads = [
        copies.start(*pair)
        for pair in (
            (one_turned_in, one_turned), (one_cells_in, one_cells),
            (two_turned_in, two_turned), (two_cells_in, two_cells),
        )
    ]
    for number, (turned, cells) in enumerate(((one_turned, one_cells), (two_turned, two_cells))):
        loads[2 * number].wait()
        loads[2 * number + 1].wait()
        family_grads(turned, cells, place[2] == number, kept, sent)


def pair_grads(place, one_turned, one_cells, two_turned, two_cells, halves):
    width, rows = one_turned.shape
    shape = jax.ShapeDtypeStruct((halves, width, one_cells.shape[1] // halves), BF16)
    return pl.pallas_call(
        pair_kernel,
        out_shape=(shape, shape),
        in_specs=[SCALARS] + [ANYWHERE] * 4,
        out_specs=tuple(whole(2)),
        scratch_shapes=[
            pltpu.VMEM((width, rows), BF16), pltpu.VMEM(one_cells.shape, BF16),
            pltpu.VMEM((width, rows), BF16), pltpu.VMEM(one_cells.shape, BF16),
            pltpu.SemaphoreType.DMA((4,)),
        ],
        compiler_params=PARAMS,
        cost_estimate=lasting(6),
        name="pair_grads",
    )(place, one_turned, one_cells, two_turned, two_cells)


def rank_kernel(place, mine, got, land_tokens, weights, late, through, small):
    halves, width, _ = weights.shape
    part = late.shape[1] // 2
    first = place[2] == 0
    grads = (
        jnp.where(first, mine[:LANDMARKS], got[:LANDMARKS]),
        jnp.where(first, got[:LANDMARKS], mine[:LANDMARKS]),
    )
    counts = landmark_counts(place)
    total = jnp.zeros((2 * LANDMARKS, width), F32)
    for index, grad in enumerate(grads):
        both = jnp.concatenate(split(grad / counts), axis=0)
        for half in range(halves):
            weight = weights[half, :, index * part : (index + 1) * part]
            total = total + nt(both[:, half * part : (half + 1) * part], weight)
    through[...] = jnp.concatenate(split(total[:LANDMARKS] + total[LANDMARKS:]), axis=0)
    zero = jnp.zeros((LANDMARKS, part), F32)
    own = []
    for index, grad in enumerate(grads):
        columns = grad[:, :part]
        for half in range(1, halves):
            columns = jnp.where(place[5] == half, grad[:, half * part : (half + 1) * part], columns)
        own.append(jnp.where(place[2] == 1 - index, columns, zero))
    high, low = split(jnp.concatenate(own, axis=1))
    mean_high, mean_low = split(land_tokens[...] / counts)
    means = jnp.concatenate([mean_high, mean_low, mean_high, jnp.zeros_like(mean_low)], axis=0).T
    factors = jnp.concatenate([high, high, low, jnp.zeros_like(low)], axis=0)
    late[...] = nn(means, factors).astype(BF16)
    gains = jnp.where(first, mine[LANDMARKS:], got[LANDMARKS:])
    shifts = jnp.where(first, got[LANDMARKS:], mine[LANDMARKS:])
    taps = jnp.where(place[5] == 0, gains[2:3], shifts[2:3])
    rows = [gains[1:2], gains[0:1], shifts[1:2], shifts[0:1], taps]
    rows.append(jnp.zeros((small.shape[0] - len(rows), width), F32))
    small[...] = jnp.concatenate(rows, axis=0).astype(BF16)


def rank_parts(place, mine, got, land_tokens, weights):
    halves, width, packed = weights.shape
    return pl.pallas_call(
        rank_kernel,
        out_shape=(
            jax.ShapeDtypeStruct((width, 2 * packed // 3), BF16),
            jax.ShapeDtypeStruct((2 * LANDMARKS, width), BF16),
            jax.ShapeDtypeStruct((16, width), BF16),
        ),
        in_specs=[SCALARS] + whole(4),
        out_specs=tuple(whole(3)),
        compiler_params=PARAMS,
        cost_estimate=lasting(4),
        name="rank_parts",
    )(place, mine, got, land_tokens, weights)


def flipped(values, axis, bit):
    count = lax.axis_size(axis)
    return lax.ppermute(values, axis, [(i, i ^ bit) for i in range(count)])


def side_of(axis, bit):
    return (lax.axis_index(axis) // bit) % 2


def paired(mine, axis, bit, dim):
    other = flipped(mine, axis, bit)
    both = jnp.zeros(mine.shape[:dim] + (2,) + mine.shape[dim:], mine.dtype)
    side = side_of(axis, bit)
    both = lax.dynamic_update_slice_in_dim(both, jnp.expand_dims(mine, dim), side, dim)
    return lax.dynamic_update_slice_in_dim(both, jnp.expand_dims(other, dim), 1 - side, dim)


def ctx_bits():
    bits, bit = [], 1
    while bit < lax.axis_size("ctx"):
        bits.append(bit)
        bit *= 2
    return bits


def sequence_start(values):
    width = values.shape[1] // 2
    side = side_of("ctx", 1)
    kept = lax.dynamic_slice_in_dim(values, side * width, width, axis=1)
    sent = lax.dynamic_slice_in_dim(values, (1 - side) * width, width, axis=1)
    kept = kept + flipped(sent, "ctx", 1)
    return kept + flipped(kept, "tp", 1)


def sequence_end(kept):
    for bit in ctx_bits()[1:]:
        kept = kept + flipped(kept, "ctx", bit)
    return kept, flipped(kept, "ctx", 1)


def joined_halves(kept, other):
    return jnp.where(
        side_of("ctx", 1) == 0,
        jnp.concatenate([kept, other], axis=1),
        jnp.concatenate([other, kept], axis=1),
    )


def to_owner(kept, sent, combine):
    kept = combine(kept, flipped(sent, "ctx", 1))
    for bit in ctx_bits()[1:]:
        view = kept.reshape((-1, 2) + kept.shape[1:])
        side = side_of("ctx", bit)
        sent = lax.dynamic_index_in_dim(view, 1 - side, 1, False)
        kept = lax.dynamic_index_in_dim(view, side, 1, False)
        kept = combine(kept, flipped(sent, "ctx", bit))
    return kept[0], flipped(kept[0], "tp", 1)


def from_owners(part):
    whole_part = part[None]
    for bit in reversed(ctx_bits()):
        both = paired(whole_part, "ctx", bit, 1)
        whole_part = both.reshape((-1,) + part.shape)
    return whole_part.reshape((-1,) + part.shape[1:])


def merge_keys(one, two):
    size = LANES // 2
    one_top, two_top = one[..., size : size + 1], two[..., size : size + 1]
    top = jnp.maximum(one_top, two_top)
    one_factor, two_factor = jnp.exp(one_top - top), jnp.exp(two_top - top)
    summed = one * one_factor + two * two_factor
    lane = lax.broadcasted_iota(jnp.int32, summed.shape, summed.ndim - 1)
    return jnp.where(lane == size, top, summed)


def neighbour_rows(cells, count):
    pieces = lax.axis_size("ctx") * lax.axis_size("tp")
    up = [(i, i + 1) for i in range(pieces - 1)]
    before = lax.ppermute(cells[-count:], ("ctx", "tp"), up)
    after = lax.ppermute(cells[:count], ("ctx", "tp"), [(j, i) for i, j in up])
    return (
        jnp.pad(before, ((LANES - count, 0), (0, 0))),
        jnp.pad(after, ((0, LANES - count), (0, 0))),
    )


def own_quarter(shard):
    rows = shard.shape[0] // lax.axis_size("ctx")
    return lax.dynamic_slice_in_dim(shard, lax.axis_index("ctx") * rows, rows, axis=0)


def gathered(shard):
    full = lax.all_gather(own_quarter(shard), ("tp", "fsdp", "ctx"), tiled=True)
    return full.reshape(lax.axis_size("tp"), -1, shard.shape[1])


def gathered_early(shard, tokens, beside):
    count = lax.axis_size("fsdp")
    piece = own_quarter(shard)
    if count > 4:
        held = lax.all_gather(piece, "fsdp")
    else:
        here = lax.axis_index("fsdp")
        held = jnp.zeros((count,) + piece.shape, piece.dtype)
        held = lax.dynamic_update_slice_in_dim(held, piece[None], here, 0)
        for step in range(1, count):
            moved = lax.ppermute(piece, "fsdp", [(i, (i + step) % count) for i in range(count)])
            held = lax.dynamic_update_slice_in_dim(held, moved[None], (here - step) % count, 0)
    bits = ctx_bits()
    full, tokens = gate(held, tokens)
    for place, bit in enumerate(reversed(bits[1:])):
        full = paired(full, "ctx", bit, 1 + place)
    after = beside(tokens)
    full, *after = gate(full, *after)
    full = paired(full, "tp", 1, 0)
    full = paired(full, "ctx", bits[0], 1 + len(bits))
    return full.reshape(lax.axis_size("tp"), -1, shard.shape[1]), after


def bits_of(axis):
    bits, bit = [], lax.axis_size(axis) // 2
    while bit:
        bits.append(bit)
        bit //= 2
    return bits


def added(*parts):
    return sum(part.astype(F32) for part in parts).astype(BF16)


def cut(cells, axis, bit, dim):
    size = cells.shape[dim] // 2
    side = side_of(axis, bit)
    return (
        lax.dynamic_slice_in_dim(cells, side * size, size, axis=dim),
        lax.dynamic_slice_in_dim(cells, (1 - side) * size, size, axis=dim),
    )


def gate(*values):
    return lax.optimization_barrier(values)


def dotf(spec, *operands):
    return jnp.einsum(spec, *operands, preferred_element_type=F32)


def taps_round(taps):
    middle = taps.shape[1] // 2
    gap = jnp.zeros((taps.shape[0], LANES - taps.shape[1]), F32)
    return jnp.concatenate([taps[:, middle::-1], gap, taps[:, :middle:-1]], axis=1)


def landmark_bounds(length):
    landmark = jnp.arange(LANDMARKS + 1, dtype=jnp.int32)
    return (landmark * length + LANDMARKS - 1) // LANDMARKS


def landmark_counts_of(length):
    bounds = landmark_bounds(length)
    return (bounds[1:] - bounds[:-1]).astype(F32)[:, None]


def landmark_rows(position, length):
    bounds = landmark_bounds(length)
    inside = (position[:, None] >= bounds[None, :-1]) & (position[:, None] < bounds[None, 1:])
    return inside.astype(BF16)


def on_device(
    tokens,
    lengths,
    qk_weight,
    value_weight,
    out_weight,
    in_weight,
    down_weight,
    norm_gains,
    norm_shifts,
    conv_weight,
    cotangent,
):
    tp_count = lax.axis_size("tp")
    tp_index = lax.axis_index("tp")
    ctx_index = lax.axis_index("ctx")
    _, slot_len, model_width = tokens.shape
    rows = slot_len // tp_count
    local_heads, tap_count = conv_weight.shape
    local_width = value_weight.shape[1]
    ff_width = in_weight.shape[1]
    head_size = local_width // local_heads
    heads = local_heads * tp_count
    owners = lax.axis_size("ctx")
    own_heads = heads // owners
    width = local_width * tp_count
    radius = tap_count // 2
    length = lengths[0]

    first_row = (ctx_index * tp_count + tp_index) * rows
    sides = (side_of("ctx", 1), ctx_index, side_of("ctx", ctx_bits()[-1]), tp_index)
    place = jnp.stack([first_row, length, *sides]).astype(jnp.int32)

    norm_columns = jnp.concatenate([norm_gains, norm_shifts], axis=0).T
    norm_columns = jnp.pad(norm_columns, ((0, 0), (0, LANES - norm_columns.shape[1])))
    ffn_full = gathered(
        jnp.concatenate([in_weight, down_weight.T, out_weight.T, norm_columns], axis=1)
    )
    own_taps = jnp.where(ctx_index == 0, conv_weight.astype(F32), 0.0)
    tap_rows = jnp.pad(own_taps, ((0, 8 - local_heads), (0, LANES - tap_count)))
    tap_rows = jnp.where(
        jnp.arange(model_width) // LANES == tp_index,
        jnp.tile(tap_rows, (1, model_width // LANES)),
        0.0,
    )

    def beside(tokens):
        own = lax.dynamic_slice_in_dim(tokens[0], tp_index * rows, rows, axis=0)
        return own, sequence_start(jnp.concatenate([token_sums(place, own), tap_rows], axis=0))

    qkv_local = jnp.concatenate([qk_weight[0], qk_weight[1], value_weight], axis=1)
    qkv_full, (own, land_tokens) = gathered_early(qkv_local, tokens, beside)
    land_tokens = joined_halves(*sequence_end(land_tokens))
    own_cotangent = lax.dynamic_slice_in_dim(cotangent[0], tp_index * rows, rows, axis=0)
    tap_weights = land_tokens[LANDMARKS : LANDMARKS + local_heads, : tp_count * LANES]
    tap_weights = tap_weights.reshape(local_heads, tp_count, LANES).transpose(1, 0, 2)
    tap_weights = tap_weights.reshape(heads, LANES)[:, :tap_count]
    land_tokens = land_tokens[:LANDMARKS]
    base, base_back = taps_round(tap_weights), taps_round(tap_weights[:, ::-1])

    queries, keys, values, v_plain, land_q, land_k, own_turned, *parts_of_third = projections(
        place, own, land_tokens, qkv_full, head_size, owners
    )
    v_ends = neighbour_rows(v_plain, radius)
    merged, merged_tp = to_owner(*parts_of_third, merge_keys)
    kept_turns = inverse_forward(place, land_q, land_k, owners)
    first, conv = first_and_conv(queries, values, *v_ends, land_k, base)
    merged, own_out = landmark_out(merged, merged_tp, kept_turns[0])
    land_out = from_owners(own_out)

    own_output, context, *fed, active, fed_turned, down_sent, last_norm = feed_forward(
        place, first, conv, land_out, own, own_cotangent, ffn_full, ff_width, local_width
    )
    high = ctx_bits()[-1]
    owner_count = lax.axis_size("fsdp")
    owner_rows = model_width // owner_count
    near, *farther = bits_of("fsdp")[::-1]

    def by_owner_bits(cells):
        return cells.reshape((2,) * (1 + len(farther)) + (-1, cells.shape[-1]))

    def cut_last(cells, bit):
        dim = cells.ndim - 3
        return tuple(piece.squeeze(dim) for piece in cut(cells, "fsdp", bit, dim))

    other_output = flipped(own_output, "tp", 1)
    down_other = flipped(down_sent, "ctx", 1)
    down_kept = kept_grad(place, fed_turned, active, tp_count)
    down_kept, down_other = gate(down_kept, down_other)
    down_mine, down_theirs = cut(down_kept, "ctx", high, 2)
    other_mine, other_theirs = cut(down_other, "ctx", high, 2)
    down_sent = added(down_theirs, other_theirs)
    down_got = flipped(down_sent, "ctx", high)
    fed[0], down_sent = gate(fed[0], down_sent)
    grad_first_res, grad_context, g_hidden, in_sent, att_turned, first_norm = feed_backward(
        place, fed, ffn_full, ff_width, local_width
    )
    in_sent, grad_context, g_hidden, other_output, down_got = gate(
        in_sent, grad_context, g_hidden, other_output, down_got
    )
    in_other = flipped(in_sent, "ctx", 1)
    g_ends = neighbour_rows(grad_context, radius)
    down = added(down_mine, other_mine, down_got)
    down_mine, down_sent = cut(down, "tp", 1, 0)
    down_got = flipped(down_sent, "tp", 1)
    grad_context, down_sent = gate(grad_context, down_sent)
    land_kept, land_sent, g_lk, g_q = attention_back(
        place, queries, grad_context, land_k, land_out, owners
    )
    land_kept, land_sent, in_other, g_ends = gate(land_kept, land_sent, in_other, g_ends)

    land_other = flipped(land_sent, "ctx", 1)
    in_kept, in_sent = spread_grad(place, fed[5], g_hidden, in_other)
    in_kept, in_sent, land_other, down_got = gate(in_kept, in_sent, land_other, down_got)
    land_grads = land_kept + land_other
    land_mine, land_theirs = cut(land_grads, "ctx", high, 0)
    land_got = flipped(land_theirs, "ctx", high)
    land_theirs, in_sent = gate(land_theirs, in_sent)
    in_got = flipped(in_sent, "ctx", high)
    down = by_owner_bits(added(down_mine, down_got)[0])
    down_mine, down_sent = cut_last(down, near)
    grad_context, in_sent, down_sent = gate(grad_context, in_sent, down_sent)
    down_got = flipped(down_sent, "fsdp", near)
    g_conv, g_taps = conv_back(v_plain, v_ends, grad_context, g_ends, base_back)
    g_conv, g_taps, land_got, down_got = gate(g_conv, g_taps, land_got, down_got)
    down = added(down_mine, down_got)
    down_mine, down_sent = cut_last(down, farther[0])
    own_grads = (land_mine + land_got)[0]
    tp_grads = flipped(own_grads, "tp", 1)

    def parts(cells):
        return cells.reshape(rows, tp_count, local_width)

    def qkv_part(index):
        return qkv_full[:, :, index * local_width : (index + 1) * local_width]

    g_q, own_grads, down_sent = gate(g_q, own_grads, down_sent)
    down_got = flipped(down_sent, "fsdp", farther[0])
    mixed_kept, mixed_sent = pair_grads(place, att_turned, context, own_turned, g_q, tp_count)
    back_q = grad_first_res + dotf("tpk,pck->tc", parts(g_q), qkv_part(0))
    mixed_kept, mixed_sent, tp_grads, back_q, down_got = gate(
        mixed_kept, mixed_sent, tp_grads, back_q, down_got
    )
    down = added(down_mine, down_got)
    for bit in farther[1:]:
        down_mine, down_sent = cut_last(down, bit)
        down = added(down_mine, flipped(down_sent, "fsdp", bit))
    mixed_got = flipped(mixed_sent, "ctx", 1)
    own_grads, mixed_sent = gate(own_grads + tp_grads, mixed_sent)
    spread, lq_mid, lk_mid = inverse_backward(
        place, land_q, land_k, merged, own_grads, *kept_turns
    )
    spread, in_got, mixed_got = gate(spread, in_got, mixed_got)
    spread = from_owners(spread)

    in_mine, in_sent = cut(added(in_kept, in_got), "tp", 1, 0)
    in_got = flipped(in_sent, "tp", 1)
    def by_ctx(cells):
        return cells.reshape(tp_count, owner_count, 2, -1, local_width)

    mixed = added(mixed_kept, mixed_got)
    mixed_mine, mixed_sent = cut(by_ctx(mixed), "ctx", high, 2)
    mixed_got = flipped(mixed_sent, "ctx", high)
    spread, in_sent, mixed_sent = gate(spread, in_sent, mixed_sent)
    g_k, g_v, sums, kv_kept, kv_sent = third_back(
        place, keys, values, land_q, spread, g_conv, lq_mid, lk_mid, g_lk, last_norm, first_norm,
        g_taps, own_turned, tp_count,
    )

    kv_got = flipped(kv_sent, "ctx", 1)
    sums_mine, sums_sent = cut(sums, "ctx", 1, 1)
    sums_got = flipped(sums_sent, "ctx", 1)
    kv_kept, kv_sent, sums_got, mixed_got, in_got = gate(
        kv_kept, kv_sent, sums_got, mixed_got, in_got
    )
    sums = sums_mine + sums_got
    sums_got = flipped(sums, "tp", 1)
    mixed = added(mixed_mine, mixed_got)
    mixed_mine, mixed_sent = cut(mixed, "tp", 1, 0)
    g_k, kv_sent, sums, mixed_sent = gate(g_k, kv_sent, sums, mixed_sent)
    mixed_got = flipped(mixed_sent, "tp", 1)
    in_mine, in_sent = cut_last(by_owner_bits(added(in_mine, in_got)[0]), near)
    in_got = flipped(in_sent, "fsdp", near)
    back_k = back_q + dotf("tpk,pck->tc", parts(g_k), qkv_part(1))
    back_k, kv_got, sums_got, mixed_got, in_got = gate(
        back_k, kv_got, sums_got, mixed_got, in_got
    )
    sums = sums + sums_got
    sums_got = flipped(sums, "ctx", high)
    kv = added(kv_kept, kv_got)
    kv_mine, kv_sent = cut(by_ctx(kv), "ctx", high, 2)
    sums, kv_sent = gate(sums, kv_sent)
    kv_got = flipped(kv_sent, "ctx", high)
    back_k, kv_sent = gate(back_k, kv_sent)
    own_grad = (back_k + dotf("tpk,pck->tc", parts(g_v), qkv_part(2))).astype(BF16)
    first_rows = 9 * rows // 16
    other_first = flipped(own_grad[:first_rows], "tp", 1)
    in_mine, in_sent = cut_last(added(in_mine, in_got), farther[0])
    in_got = flipped(in_sent, "fsdp", farther[0])
    own_grad, sums_got = gate(own_grad, sums_got)
    sums = sums + sums_got
    sums_got = flipped(sums, "ctx", 1)
    late, through, small = rank_parts(place, sums, sums_got, land_tokens, qkv_full)
    late, through, small, kv_got, in_got, other_first = gate(
        late, through, small, kv_got, in_got, other_first
    )
    kv = added(kv_mine, kv_got)
    kv_mine, kv_sent = cut(kv, "tp", 1, 0)
    kv_got = flipped(kv_sent, "tp", 1)
    own_grad, kv_sent = gate(own_grad, kv_sent)
    other_second = flipped(own_grad[first_rows:], "tp", 1)

    late = late.reshape(owner_count, 2, -1, 2 * local_width)
    late = lax.dynamic_index_in_dim(late, place[4], 1, False)
    mixed = added(
        jnp.concatenate([mixed_mine, kv_mine], axis=-1).reshape(late.shape),
        jnp.concatenate([mixed_got, kv_got], axis=-1).reshape(late.shape),
        late,
    )
    small = jnp.broadcast_to(small[None], (owner_count,) + small.shape)
    mixed = by_owner_bits(jnp.concatenate([mixed, small], axis=1))
    mixed_mine, mixed_sent = cut_last(mixed, near)
    mixed_got = flipped(mixed_sent, "fsdp", near)
    mixed = added(mixed_mine, mixed_got)
    mixed, other_second = gate(mixed, other_second)
    in_sum = added(in_mine, in_got)
    for bit in farther[1:]:
        in_mine, in_sent = cut_last(in_sum, bit)
        in_sum = added(in_mine, flipped(in_sent, "fsdp", bit))
    pair = jnp.concatenate([in_sum, down], axis=1)
    for bit in farther:
        mixed_mine, mixed_sent = cut_last(mixed, bit)
        mixed = added(mixed_mine, flipped(mixed_sent, "fsdp", bit))
    small = mixed[-16:].astype(F32)
    mixed = mixed[:-16]

    def of_core(cells, core):
        cells = cells.reshape((owners // 2, 2) + cells.shape[1:])
        return [cells[i, core] for i in range(owners // 2)]

    mixed = from_owners(mixed[None])
    sides = [jnp.concatenate(of_core(mixed, core), axis=0).astype(F32) for core in range(2)]
    grad_out, grad_k = sides[0][:, :local_width].T, sides[0][:, local_width:]
    grad_q, grad_v = sides[1][:, :local_width], sides[1][:, local_width:]

    own_columns = lax.axis_index("fsdp") * owner_rows
    norm_sums = lax.dynamic_slice_in_dim(small[:4], own_columns, owner_rows, axis=1)
    taps_sum = small[4].reshape(local_heads, LANES)
    grad_taps = jnp.concatenate(
        [taps_sum[:, radius - 1 :: -1], taps_sum[:, : -radius - 2 : -1]], axis=1
    )

    columns = pair.shape[1] // 2
    pair = from_owners(pair[None])
    pieces = [piece for core in range(2) for piece in of_core(pair, core)]
    grad_in = jnp.concatenate([piece[:, :columns] for piece in pieces], axis=1).astype(F32)
    grad_down = jnp.concatenate([piece[:, columns:] for piece in pieces], axis=1).astype(F32).T

    output = jnp.where(
        tp_index == 0,
        jnp.concatenate([own_output, other_output]),
        jnp.concatenate([other_output, own_output]),
    )[None]
    both_grads = jnp.where(
        tp_index == 0,
        jnp.concatenate([own_grad, other_first, other_second]),
        jnp.concatenate([other_first, other_second, own_grad]),
    )
    position = ctx_index * slot_len + jnp.arange(slot_len, dtype=jnp.int32)
    onehot = landmark_rows(position, length)
    grad_tokens = both_grads.astype(F32) + dotf(
        "tm,mc->tc", jnp.concatenate([onehot, onehot], axis=1), through
    )
    grad_tokens = grad_tokens.reshape(1, slot_len, model_width)
    return (
        output,
        grad_tokens,
        jnp.stack([grad_q, grad_k]),
        grad_v,
        grad_out,
        grad_in,
        grad_down,
        norm_sums[:2],
        norm_sums[2:],
        grad_taps,
    )


def solution(mesh):
    in_specs = (
        P("fsdp", "ctx", None),
        P("fsdp"),
        P(None, "fsdp", "tp"),
        P("fsdp", "tp"),
        P("tp", "fsdp"),
        P("fsdp", "tp"),
        P("tp", "fsdp"),
        P(None, "fsdp"),
        P(None, "fsdp"),
        P("tp", None),
        P("fsdp", "ctx", None),
    )
    out_specs = (
        P("fsdp", "ctx", None),
        P("fsdp", "ctx", None),
        P(None, "fsdp", "tp"),
        P("fsdp", "tp"),
        P("tp", "fsdp"),
        P("fsdp", "tp"),
        P("tp", "fsdp"),
        P(None, "fsdp"),
        P(None, "fsdp"),
        P("tp", None),
    )
    return jax.shard_map(
        on_device, mesh=mesh, in_specs=in_specs, out_specs=out_specs, check_vma=False
    )
```

```python
import jax
import jax.numpy as jnp
from jax import lax
from jax.experimental import pallas as pl
from jax.experimental.pallas import tpu as pltpu
from jax.sharding import PartitionSpec as P

LANDMARKS = 64
NEWTON = 6
LANES = 128
VMEM_BYTES = 56 * 2**20

HIGH = lax.Precision.HIGHEST
F32 = jnp.float32
BF16 = jnp.bfloat16


def lasting(microseconds):
    return pl.CostEstimate(
        flops=int(microseconds * 1.1535e9), bytes_accessed=int(microseconds * 1e5), transcendentals=0
    )


def nn(left, right):
    return jnp.dot(left, right, preferred_element_type=F32)


def nt(left, right):
    return lax.dot_general(left, right, (((1,), (1,)), ((), ())), preferred_element_type=F32)


def split(wide):
    high = wide.astype(BF16)
    return high, (wide - high.astype(F32)).astype(BF16)


def each_tile(count, tile, body):
    def step(i, _):
        body(i, pl.ds(pl.multiple_of(i * tile, tile), tile))
        return 0

    lax.fori_loop(0, count // tile, step, 0)


def family_grads(turned, cells, mine, kept, sent):
    halves, width, columns = kept.shape

    def rows_of(i, at):
        total = nn(turned[at, :], cells[...]).astype(BF16)

        @pl.when(mine)
        def _():
            for half in range(halves):
                kept[half, at, :] = total[:, half * columns : (half + 1) * columns]

        @pl.when(jnp.logical_not(mine))
        def _():
            for half in range(halves):
                sent[half, at, :] = total[:, half * columns : (half + 1) * columns]

    each_tile(width, 384, rows_of)


def whole(count):
    return [pl.BlockSpec(memory_space=pltpu.VMEM)] * count


SCALARS = pl.BlockSpec(memory_space=pltpu.SMEM)
PARAMS = pltpu.CompilerParams(vmem_limit_bytes=VMEM_BYTES)


def landmark_onehot(place, rows, landmark_axis):
    shape = (LANDMARKS, rows) if landmark_axis == 0 else (rows, LANDMARKS)
    landmark = lax.broadcasted_iota(jnp.int32, shape, landmark_axis)
    position = place[0] + lax.broadcasted_iota(jnp.int32, shape, 1 - landmark_axis)
    start = lax.shift_right_logical(landmark * place[1] + (LANDMARKS - 1), 6)
    end = lax.shift_right_logical((landmark + 1) * place[1] + (LANDMARKS - 1), 6)
    return jnp.where((position >= start) & (position < end), 1.0, 0.0).astype(BF16)


def live_lanes(place, rows):
    position = place[0] + lax.broadcasted_iota(jnp.int32, (1, rows), 1)
    return position < place[1]


def band(base_row):
    ring = pltpu.roll(jnp.broadcast_to(base_row, (LANES, LANES)), 0, 1, stride=1, stride_axis=0)
    gap = lax.broadcasted_iota(jnp.int32, (LANES, LANES), 0) - lax.broadcasted_iota(
        jnp.int32, (LANES, LANES), 1
    )
    zero = jnp.zeros_like(ring)
    before = jnp.where(gap >= LANES - 16, ring, zero).astype(BF16)
    here = jnp.where(jnp.abs(gap) <= 16, ring, zero).astype(BF16)
    after = jnp.where(gap <= 16 - LANES, ring, zero).astype(BF16)
    return before, here, after


def convolved(blocks, bands):
    count = len(blocks) - 2
    size = blocks[0].shape[0]
    stacked = jnp.concatenate(
        [jnp.concatenate(blocks[i : i + 3], axis=1) for i in range(count)], axis=0
    )
    out = nn(stacked, jnp.concatenate(bands, axis=0))
    return jnp.concatenate([out[i * size : (i + 1) * size] for i in range(count)], axis=1)


def token_sums_kernel(place, tokens, sums):
    sums[...] = nn(landmark_onehot(place, tokens.shape[0], 0), tokens[...])


def token_sums(place, tokens):
    return pl.pallas_call(
        token_sums_kernel,
        out_shape=jax.ShapeDtypeStruct((LANDMARKS, tokens.shape[1]), F32),
        in_specs=[SCALARS] + whole(1),
        out_specs=whole(1)[0],
        compiler_params=PARAMS,
        cost_estimate=lasting(2.5),
        name="token_sums",
    )(place, tokens)


def landmark_counts(place):
    landmark = lax.broadcasted_iota(jnp.int32, (LANDMARKS, 1), 0)
    start = lax.shift_right_logical(landmark * place[1] + (LANDMARKS - 1), 6)
    end = lax.shift_right_logical((landmark + 1) * place[1] + (LANDMARKS - 1), 6)
    return (end - start).astype(F32)


def projection_kernel(
    place, tokens, sums, weights, q_out, k_out, v_out, v_plain, land_q, land_k, turned, kept, sent
):
    rows = tokens.shape[0]
    halves, _, packed = weights.shape
    width = packed // 3
    size = land_q.shape[2]
    position = place[0] + lax.broadcasted_iota(jnp.int32, (rows, 1), 0)
    live = jnp.where(position < place[1], 1.0, 0.0)
    scaled = live * 64**-0.25
    means = jnp.concatenate(split(sums[...] / landmark_counts(place)), axis=0)
    cells = tokens[...]
    turned[...] = cells.T
    for half in range(halves):
        for part, out in enumerate((q_out, k_out, v_out)):
            weight = weights[half, :, part * width : (part + 1) * width]
            low = ((live if part == 2 else scaled) * nn(cells, weight)).astype(BF16)
            out[half * width : (half + 1) * width, :] = low.T
            if part == 2:
                v_plain[:, half * width : (half + 1) * width] = low
                continue
            both = nn(means, weight)
            land = (64**-0.25 * (both[:LANDMARKS] + both[LANDMARKS:])).astype(BF16)
            to = land_k if part else land_q
            for head in range(width // size):
                to[half * (width // size) + head] = land[:, head * size : (head + 1) * size]
    third_heads(place, k_out, v_out, land_q, kept, sent)


def projections(place, tokens, sums, weights, size, owners):
    rows = tokens.shape[0]
    width = weights.shape[0] * weights.shape[2] // 3
    turned = jax.ShapeDtypeStruct((width, rows), BF16)
    land = jax.ShapeDtypeStruct((width // size, LANDMARKS, size), BF16)
    return pl.pallas_call(
        projection_kernel,
        out_shape=(turned, turned, turned, jax.ShapeDtypeStruct((rows, width), BF16), land, land)
        + (jax.ShapeDtypeStruct(tokens.shape[::-1], BF16),)
        + owner_parts(width // size, owners),
        in_specs=[SCALARS] + whole(3),
        out_specs=tuple(whole(9)),
        compiler_params=PARAMS,
        cost_estimate=lasting(18),
        name="projections",
    )(place, tokens, sums, weights)


def by_owner(place, h, owners, kept, sent, values):
    per = kept.shape[1]
    for owner in range(owners):
        @pl.when((h >= owner * per) & (h < (owner + 1) * per))
        def _(owner=owner):
            mine = place[2] == owner % 2

            @pl.when(mine)
            def _():
                kept[owner // 2, h - owner * per] = values

            @pl.when(jnp.logical_not(mine))
            def _():
                sent[owner // 2, h - owner * per] = values


def third_heads(place, keys, values, land_q, kept, sent):
    heads = land_q.shape[0]
    size = land_q.shape[2]
    rows = keys.shape[1]
    owners = 2 * kept.shape[0]
    live = live_lanes(place, rows)

    def head(h):
        at = pl.ds(pl.multiple_of(h * size, size), size)
        scores = jnp.where(live, nn(land_q[h], keys[at, :]), -1e30)
        top = jnp.max(scores, axis=1, keepdims=True)
        raised = jnp.where(live, jnp.exp(scores - top), 0.0)
        total = jnp.sum(raised, axis=1, keepdims=True)
        high, low = split(raised)
        value = values[at, :]
        mixed = nt(high, value) + nt(low, value)
        lane = lax.broadcasted_iota(jnp.int32, (LANDMARKS, LANES - size), 1)
        stats = jnp.where(lane == 0, top, jnp.where(lane == 1, total, 0.0))
        by_owner(place, h, owners, kept, sent, jnp.concatenate([mixed, stats], axis=1))

    def pair(i, _):
        head(2 * i)
        head(2 * i + 1)
        return 0

    lax.fori_loop(0, heads // 2, pair, 0)


def owner_parts(heads, owners):
    part = jax.ShapeDtypeStruct((owners // 2, heads // owners, LANDMARKS, LANES), F32)
    return part, part


def dot_high(left, right):
    return jnp.dot(left, right, preferred_element_type=F32, precision=HIGH)


def dot_high_nt(left, right):
    return lax.dot_general(
        left, right, (((1,), (1,)), ((), ())), preferred_element_type=F32, precision=HIGH
    )


def eye():
    row = lax.broadcasted_iota(jnp.int32, (LANDMARKS, LANDMARKS), 0)
    column = lax.broadcasted_iota(jnp.int32, (LANDMARKS, LANDMARKS), 1)
    return jnp.where(row == column, 1.0, 0.0)


def middle_map(land_q, land_k):
    scores = nt(land_q, land_k)
    raised = jnp.exp(scores - jnp.max(scores, axis=1, keepdims=True))
    return raised / jnp.sum(raised, axis=1, keepdims=True)


def inverse_kernel(place, land_q, land_k, kept_v, kept_p, kept_b, kept_c):
    heads = range(kept_v.shape[1])
    one = eye()
    own = [place[3] * len(heads) + h for h in heads]
    middle = [middle_map(land_q[h], land_k[h]) for h in own]
    approx = [m.T / jnp.sum(m * m, keepdims=True) for m in middle]
    for turn in range(NEWTON):
        product = [dot_high(middle[h], approx[h]) for h in heads]
        for h in heads:
            kept_v[turn, h] = approx[h]
            kept_p[turn, h] = product[h]
        bracket = [7.0 * one - p for p in product]
        bracket = [15.0 * one - dot_high(product[h], bracket[h]) for h in heads]
        for h in heads:
            kept_b[turn, h] = bracket[h]
        bracket = [13.0 * one - dot_high(product[h], bracket[h]) for h in heads]
        for h in heads:
            kept_c[turn, h] = bracket[h]
        approx = [0.25 * dot_high(approx[h], bracket[h]) for h in heads]
    for h in heads:
        kept_v[NEWTON, h] = approx[h]


def inverse_forward(place, land_q, land_k, owners):
    heads = land_q.shape[0] // owners
    square = (heads, LANDMARKS, LANDMARKS)
    return pl.pallas_call(
        inverse_kernel,
        out_shape=(
            jax.ShapeDtypeStruct((NEWTON + 1,) + square, F32),
            jax.ShapeDtypeStruct((NEWTON,) + square, F32),
            jax.ShapeDtypeStruct((NEWTON,) + square, F32),
            jax.ShapeDtypeStruct((NEWTON,) + square, F32),
        ),
        in_specs=[SCALARS] + whole(2),
        out_specs=tuple(whole(4)),
        compiler_params=PARAMS,
        cost_estimate=lasting(7),
        name="inverse_forward",
    )(place, land_q, land_k)


def merged_keys(one, two, size):
    one_top, two_top = one[:, size : size + 1], two[:, size : size + 1]
    top = jnp.maximum(one_top, two_top)
    summed = one * jnp.exp(one_top - top) + two * jnp.exp(two_top - top)
    lane = lax.broadcasted_iota(jnp.int32, one.shape, 1)
    return jnp.where(lane == size, top, summed)


def land_out_kernel(one, two, kept_v, merged, land_out):
    size = land_out.shape[2]
    for h in range(one.shape[0]):
        both = merged_keys(one[h], two[h], size)
        merged[h] = both
        mixed = both[:, :size] / both[:, size + 1 : size + 2]
        land_out[h] = dot_high(kept_v[NEWTON, h], mixed).astype(BF16)


def landmark_out(one, two, kept_v):
    heads = one.shape[0]
    return pl.pallas_call(
        land_out_kernel,
        out_shape=(
            jax.ShapeDtypeStruct(one.shape, F32),
            jax.ShapeDtypeStruct((heads, LANDMARKS, LANES // 2), BF16),
        ),
        in_specs=whole(3),
        out_specs=tuple(whole(2)),
        compiler_params=PARAMS,
        cost_estimate=lasting(2.2),
        name="landmark_out",
    )(one, two, kept_v)


def inverse_back_kernel(
    place, land_q, land_k, merged, grads, kept_v, kept_p, kept_b, kept_c, spread, g_lq, g_lk
):
    heads = range(grads.shape[0])
    size = land_q.shape[2]
    one = eye()
    own = [place[3] * len(heads) + h for h in heads]
    middle = [middle_map(land_q[h], land_k[h]) for h in own]
    turned = [m.T for m in middle]
    g_approx = []
    for h in heads:
        mixed = merged[h][:, :size] / merged[h][:, size + 1 : size + 2]
        g_land = grads[h][:, :size]
        g_approx.append(dot_high_nt(g_land, mixed))
        g_mixed = dot_high(kept_v[NEWTON, h].T, g_land)
        row_dot = jnp.sum(g_mixed * mixed, axis=1, keepdims=True)
        lane = lax.broadcasted_iota(jnp.int32, (LANDMARKS, LANES - size), 1)
        top = merged[h][:, size : size + 1]
        total = merged[h][:, size + 1 : size + 2]
        stats = jnp.where(
            lane == 0, row_dot, jnp.where(lane == 1, top, jnp.where(lane == 2, total, 0.0))
        )
        spread[h] = jnp.concatenate([g_mixed, stats], axis=1)
    g_middle = [jnp.zeros((LANDMARKS, LANDMARKS), F32) for _ in heads]
    for turn in reversed(range(NEWTON)):
        approx = [kept_v[turn, h] for h in heads]
        product = [kept_p[turn, h] for h in heads]
        first = [7.0 * one - p for p in product]
        second = [kept_b[turn, h] for h in heads]
        third = [kept_c[turn, h] for h in heads]
        g_third = [0.25 * dot_high(approx[h].T, g_approx[h]) for h in heads]
        g_back = [0.25 * dot_high_nt(g_approx[h], third[h]) for h in heads]
        g_product = [-dot_high_nt(g_third[h], second[h]) for h in heads]
        pt = [p.T for p in product]
        g_second = [-dot_high(pt[h], g_third[h]) for h in heads]
        g_product = [g_product[h] - dot_high_nt(g_second[h], first[h]) for h in heads]
        g_product = [g_product[h] + dot_high(pt[h], g_second[h]) for h in heads]
        g_middle = [g_middle[h] + dot_high_nt(g_product[h], approx[h]) for h in heads]
        g_approx = [g_back[h] + dot_high(turned[h], g_product[h]) for h in heads]
    for h in heads:
        m = middle[h]
        size_sum = jnp.sum(m * m, keepdims=True)
        g_size = -jnp.sum(g_approx[h] * turned[h], keepdims=True) / (size_sum * size_sum)
        g_m = g_middle[h] + g_approx[h].T / size_sum + 2.0 * g_size * m
        g_scores = m * (g_m - jnp.sum(g_m * m, axis=1, keepdims=True))
        g_lq[h] = dot_high(g_scores, land_k[own[h]].astype(F32))
        g_lk[h] = dot_high(g_scores.T, land_q[own[h]].astype(F32))


def inverse_backward(place, land_q, land_k, merged, grads, *kept):
    heads = grads.shape[0]
    square = jax.ShapeDtypeStruct((heads,) + land_q.shape[1:], F32)
    return pl.pallas_call(
        inverse_back_kernel,
        out_shape=(jax.ShapeDtypeStruct((heads, LANDMARKS, LANES), F32), square, square),
        in_specs=[SCALARS] + whole(8),
        out_specs=tuple(whole(3)),
        compiler_params=PARAMS,
        cost_estimate=lasting(11.5),
        name="inverse_backward",
    )(place, land_q, land_k, merged, grads, *kept)


def first_map(land_k, queries):
    scores = nn(land_k, queries)
    raised = jnp.exp(scores - jnp.max(scores, axis=0, keepdims=True))
    return raised * (1.0 / jnp.sum(raised, axis=0, keepdims=True))


def head_blocks(cells, ends, at):
    rows = cells.shape[1]
    left, right = ends
    return (
        [left[at, :]]
        + [cells[at, i * LANES : (i + 1) * LANES] for i in range(rows // LANES)]
        + [right[at, :]]
    )


def first_conv_kernel(queries, values, left, right, land_k, base, first, conv, ends):
    heads, _, size = land_k.shape
    ends[0] = left[...].T
    ends[1] = right[...].T

    def head(h):
        at = pl.ds(pl.multiple_of(h * size, size), size)
        first[at, :] = first_map(land_k[h], queries[at, :]).astype(BF16)
        blocks = head_blocks(values, (ends.at[0], ends.at[1]), at)
        conv[at, :] = convolved(blocks, band(base[pl.ds(h, 1), :]))

    def pair(i, _):
        head(2 * i)
        head(2 * i + 1)
        return 0

    lax.fori_loop(0, heads // 2, pair, 0)


def first_and_conv(queries, values, left, right, land_k, base):
    width, rows = queries.shape
    return pl.pallas_call(
        first_conv_kernel,
        out_shape=(
            jax.ShapeDtypeStruct((width, rows), BF16),
            jax.ShapeDtypeStruct((width, rows), F32),
        ),
        in_specs=whole(6),
        out_specs=tuple(whole(2)),
        scratch_shapes=[pltpu.VMEM((2, width, LANES), BF16)],
        compiler_params=PARAMS,
        cost_estimate=lasting(8),
        name="first_and_conv",
    )(queries, values, left, right, land_k, base)


def context_rows(first, conv, land_out, context):
    heads, _, size = land_out.shape

    def head(h):
        at = pl.ds(pl.multiple_of(h * size, size), size)
        return (nn(land_out[h].T, first[at, :]) + conv[at, :]).astype(BF16)

    def pair(i, _):
        both = jnp.concatenate([head(2 * i), head(2 * i + 1)], axis=0)
        context[:, pl.ds(pl.multiple_of(i * LANES, LANES), LANES)] = both.T
        return 0

    lax.fori_loop(0, heads // 2, pair, 0)


def attention_back_kernel(
    place, queries, grads, land_k, land_out, kept, sent, g_lk, g_query
):
    heads, _, size = land_k.shape
    rows = queries.shape[1]
    owners = 2 * kept.shape[0]
    scaled = jnp.where(live_lanes(place, rows), 64**-0.25, 0.0)

    def pair(i, _):
        lanes = pl.ds(pl.multiple_of(i * LANES, LANES), LANES)
        turned = grads[:, lanes].T
        g_queries, g_keys = [], []
        for side in range(2):
            h = 2 * i + side
            query = queries[pl.ds(pl.multiple_of(h * size, size), size), :]
            g_context = turned[side * size : (side + 1) * size]
            first = first_map(land_k[h], query)
            g_first = nn(land_out[h], g_context)
            inner = jnp.sum(g_first * first, axis=0, keepdims=True)
            g_scores = (first * (g_first - inner)).astype(BF16)
            g_land = nt(first.astype(BF16), g_context)
            g_key = nt(g_scores, query)
            by_owner(place, h, owners, kept, sent, jnp.concatenate([g_land, g_key], axis=1))
            g_keys.append(g_key)
            g_queries.append((scaled * nn(land_k[h].T, g_scores)).astype(BF16))
        g_query[:, lanes] = jnp.concatenate(g_queries, axis=0).T
        g_lk[:, lanes] = jnp.concatenate(g_keys, axis=1)
        return 0

    lax.fori_loop(0, heads // 2, pair, 0)


def attention_back(place, queries, grads, land_k, land_out, owners):
    width, rows = queries.shape
    heads = land_k.shape[0]
    return pl.pallas_call(
        attention_back_kernel,
        out_shape=owner_parts(heads, owners)
        + (
            jax.ShapeDtypeStruct((LANDMARKS, width), F32),
            jax.ShapeDtypeStruct((rows, width), BF16),
        ),
        in_specs=[SCALARS] + whole(4),
        out_specs=tuple(whole(4)),
        compiler_params=PARAMS,
        cost_estimate=lasting(11.4),
        name="attention_back",
    )(place, queries, grads, land_k, land_out)


def conv_back_kernel(
    v_plain, v_left, v_right, grads, g_left, g_right, base_back, g_value, g_taps, ends
):
    heads = g_taps.shape[0]
    rows, width = grads.shape
    size = width // heads
    blocks_in = rows // LANES
    row = lax.broadcasted_iota(jnp.int32, (LANES, LANES), 0)
    column = lax.broadcasted_iota(jnp.int32, (LANES, LANES), 1)
    reverse = jnp.where(row + column == LANES - 1, 1.0, 0.0).astype(BF16)
    gap = jnp.concatenate([row - column, row - column], axis=1)
    ends[0] = g_left[...].T
    ends[1] = g_right[...].T

    def pair(i, _):
        lanes = pl.ds(pl.multiple_of(i * LANES, LANES), LANES)
        turned = grads[:, lanes].T
        plain = [v_left[LANES - 16 :, lanes]]
        plain += [v_plain[b * LANES : (b + 1) * LANES, lanes] for b in range(blocks_in)]
        plain += [v_right[:16, lanes]]
        for side in range(2):
            h = 2 * i + side
            at = pl.ds(pl.multiple_of(h * size, size), size)
            g_context = turned[side * size : (side + 1) * size]
            blocks = [ends[0, at, :]]
            blocks += [g_context[:, b * LANES : (b + 1) * LANES] for b in range(blocks_in)]
            blocks += [ends[1, at, :]]
            g_value[at, :] = convolved(blocks, band(base_back[pl.ds(h, 1), :]))

        def around(b):
            prior = plain[0] if b == 0 else plain[b][LANES - 16 :]
            return jnp.concatenate([prior, plain[b + 1], plain[b + 2][:16]], axis=0)

        def by_head(b):
            piece = turned[:, b * LANES : (b + 1) * LANES]
            zero = jnp.zeros_like(piece)
            return jnp.concatenate(
                [jnp.where(row < size, piece, zero), jnp.where(row >= size, piece, zero)], axis=1
            )

        total = jnp.zeros((LANES + 32, 2 * LANES), F32)
        for b in range(0, blocks_in, 2):
            total = total + nn(
                jnp.concatenate([around(b), around(b + 1)], axis=1),
                jnp.concatenate([by_head(b), by_head(b + 1)], axis=0),
            )
        empty = jnp.zeros((LANES - 16, 2 * LANES), F32)
        before, here, after = total[:16], total[16 : 16 + LANES], total[16 + LANES :]
        ring = jnp.where(jnp.abs(gap) <= 16, here, 0.0)
        ring = ring + jnp.where(gap >= LANES - 16, jnp.concatenate([empty, before], axis=0), 0.0)
        ring = ring + jnp.where(gap <= 16 - LANES, jnp.concatenate([after, empty], axis=0), 0.0)
        high, low = split(ring)
        lowest = (ring - high.astype(F32) - low.astype(F32)).astype(BF16)
        flat = nn(reverse, high) + nn(reverse, low) + nn(reverse, lowest)
        for side in range(2):
            straight = pltpu.roll(
                flat[:, side * LANES : (side + 1) * LANES], 0, 1, stride=1, stride_axis=0
            )
            g_taps[pl.ds(2 * i + side, 1), :] = jnp.sum(straight, axis=0, keepdims=True)
        return 0

    lax.fori_loop(0, heads // 2, pair, 0)


def conv_back(v_plain, v_ends, grads, g_ends, base_back):
    rows, width = grads.shape
    heads = base_back.shape[0]
    return pl.pallas_call(
        conv_back_kernel,
        out_shape=(
            jax.ShapeDtypeStruct((width, rows), F32),
            jax.ShapeDtypeStruct((heads, LANES), F32),
        ),
        in_specs=whole(7),
        out_specs=tuple(whole(2)),
        scratch_shapes=[pltpu.VMEM((2, width, LANES), BF16)],
        compiler_params=PARAMS,
        cost_estimate=lasting(13.6),
        name="conv_back",
    )(v_plain, *v_ends, grads, *g_ends, base_back)


def third_back_kernel(
    place, keys, values, land_q, spread, g_conv, lq_mid, lk_mid, g_lk, last, first, taps, turned,
    g_k, g_v, sums, kept, sent,
):
    heads, _, size = land_q.shape
    rows, width = g_k.shape
    own_heads = lq_mid.shape[0]
    scale = 64**-0.25
    sums[LANDMARKS:, :] = jnp.zeros((sums.shape[0] - LANDMARKS, 2 * width), F32)
    sums[LANDMARKS : LANDMARKS + 1, :] = last[...]
    sums[LANDMARKS + 1 : LANDMARKS + 2, :] = first[...]
    for h in range(heads):
        sums[LANDMARKS + 2 : LANDMARKS + 3, h * LANES : (h + 1) * LANES] = taps[h : h + 1, :]

    def mid(part, h):
        at = h - place[3] * own_heads
        mine = (at >= 0) & (at < own_heads) & (place[5] == 0)
        inside = jnp.clip(at, 0, own_heads - 1)
        return jnp.where(mine, part[inside], 0.0)

    live = live_lanes(place, rows)
    live_row = jnp.where(live, 1.0, 0.0)
    scaled_row = live_row * 64**-0.25

    def pair(i, _):
        lanes = pl.ds(pl.multiple_of(i * LANES, LANES), LANES)
        g_keys, g_values, g_lqs, lks = [], [], [], []
        for side in range(2):
            h = 2 * i + side
            at = pl.ds(pl.multiple_of(h * size, size), size)
            key, value = keys[at, :], values[at, :]
            pack = spread[h]
            g_mixed = pack[:, :size]
            row_dot = pack[:, size : size + 1]
            top = pack[:, size + 1 : size + 2]
            total = pack[:, size + 2 : size + 3]
            scores = nn(land_q[h], key)
            third = jnp.where(live, jnp.exp(scores - top), 0.0) * (1.0 / total)
            gm_high, gm_low = split(g_mixed)
            g_third = nn(gm_high, value) + nn(gm_low, value)
            g_high, g_low = split(third * (g_third - row_dot))
            g_lqs.append(nt(g_high, key) + nt(g_low, key) + mid(lq_mid, h))
            lks.append(mid(lk_mid, h))
            turned = land_q[h].T
            g_key = nn(turned, g_high) + nn(turned, g_low)
            g_keys.append((scaled_row * g_key).astype(BF16))
            t_high, t_low = split(third)
            gmt_high, gmt_low = split(g_mixed.T)
            g_value = nn(gmt_high, t_high) + nn(gmt_high, t_low) + nn(gmt_low, t_high)
            g_values.append((live_row * (g_value + g_conv[at, :])).astype(BF16))
        g_k[:, lanes] = jnp.concatenate(g_keys, axis=0).T
        g_v[:, lanes] = jnp.concatenate(g_values, axis=0).T
        sums[:LANDMARKS, lanes] = scale * jnp.concatenate(g_lqs, axis=1)
        key_lanes = pl.ds(pl.multiple_of(width + i * LANES, LANES), LANES)
        sums[:LANDMARKS, key_lanes] = scale * (g_lk[:, lanes] + jnp.concatenate(lks, axis=1))
        return 0

    lax.fori_loop(0, heads // 2, pair, 0)
    for number, cells in enumerate((g_k, g_v)):
        family_grads(turned, cells, place[2] == number, kept, sent)


def third_back(
    place, keys, values, land_q, spread, g_conv, lq_mid, lk_mid, g_lk, last, first, taps, turned, halves
):
    width, rows = keys.shape
    plain = jax.ShapeDtypeStruct((rows, width), BF16)
    return pl.pallas_call(
        third_back_kernel,
        out_shape=(plain, plain, jax.ShapeDtypeStruct((LANDMARKS + 8, 2 * width), F32))
        + (jax.ShapeDtypeStruct((halves, width, width // halves), BF16),) * 2,
        in_specs=[SCALARS] + whole(12),
        out_specs=tuple(whole(5)),
        compiler_params=PARAMS,
        cost_estimate=lasting(17),
        name="third_back",
    )(
        place, keys, values, land_q, spread, g_conv, lq_mid, lk_mid, g_lk, last, first, taps, turned
    )


def centred_rows(rows):
    centred = rows - jnp.mean(rows, axis=1, keepdims=True)
    scale = lax.rsqrt(jnp.mean(centred * centred, axis=1, keepdims=True) + 1e-05)
    return centred * scale, scale


def norm_back(grads, gain, unit, scale):
    scaled = grads * gain
    inner = jnp.mean(scaled * unit, axis=1, keepdims=True)
    return scale * (scaled - jnp.mean(scaled, axis=1, keepdims=True) - unit * inner)


def gelu_pair(hidden):
    share = 0.5 * (1.0 + lax.erf(hidden * 0.7071067811865476))
    density = jnp.exp(-0.5 * hidden * hidden) * 0.3989422804014327
    return hidden * share, share + hidden * density


class Copies:
    def __init__(self, sems):
        self.sems, self.used, self.open = sems, 0, []

    def start(self, source, target):
        copy = pltpu.make_async_copy(source, target, self.sems.at[self.used])
        self.used += 1
        copy.start()
        return copy

    def out(self, source, target):
        self.open.append(self.start(source, target))

    def finish(self):
        for copy in self.open:
            copy.wait()


def weight_grad(turned, cells, halves, which, out):
    ff = cells.shape[1] // halves
    columns = ff // 2
    for half in range(halves):
        from_column = pl.ds(pl.multiple_of(half * ff + which * columns, columns), columns)

        def rows_of(i, at, half=half, from_column=from_column):
            out[half, at, :] = nn(turned[at, :], cells[:, from_column]).astype(BF16)

        each_tile(turned.shape[0], 384, rows_of)


def feed_kernel(
    place, first_in, conv_in, land_out, tokens_in, cotangent_in, weights,
    output_to, context_to, slope_to, g_fed_to, g_second_to, unit_to, scale_to, turned_to, active_to, fed_turned_to, sent_to,
    norm_grads, in_w, down_w, out_w, norms, conv, context, tokens, cotangent,
    low, unit, scales, fed, active, slopes, g_fed, g_fed_turned, normed_turned, output, sent,
    sems,
):
    rows, width = tokens.shape
    halves, _, ff = in_w.shape
    part = out_w.shape[2]
    tile = 256
    copies = Copies(sems)
    context_copies = [copies.start(first_in, g_fed_turned), copies.start(conv_in, conv)]
    early = [
        copies.start(weights.at[:, :, pl.ds(2 * ff, part)], out_w),
        copies.start(tokens_in, tokens),
        copies.start(weights.at[:, :, pl.ds(2 * ff + part, LANES)], norms),
    ]
    in_copy = copies.start(weights.at[:, :, pl.ds(0, ff)], in_w)
    down_copy = copies.start(weights.at[:, :, pl.ds(ff, ff)], down_w)
    cotangent_copy = copies.start(cotangent_in, cotangent)
    for copy in context_copies:
        copy.wait()
    context_rows(g_fed_turned, conv, land_out, context)
    copies.out(context, context_to)
    for copy in early:
        copy.wait()
    columns = norms[0].astype(F32).T
    gain0, gain1 = columns[0:1], columns[1:2]
    shift0, shift1 = columns[2:3], columns[3:4]
    norm_grads[...] = jnp.zeros_like(norm_grads)

    def project(i, at):
        attended = nt(context[at, :part], out_w[0])
        for half in range(1, halves):
            attended = attended + nt(context[at, half * part : (half + 1) * part], out_w[half])
        rows_unit, scale = centred_rows(tokens[at, :].astype(F32) + attended)
        unit[at, :] = rows_unit
        scales[at, :] = jnp.broadcast_to(scale, (tile, LANES))
        normed = (rows_unit * gain0 + shift0).astype(BF16)
        low[at, :] = normed
        normed_turned[:, at] = normed.T

    each_tile(rows, tile, project)
    copies.out(unit, unit_to)
    copies.out(scales, scale_to)
    copies.out(normed_turned, turned_to)
    in_copy.wait()
    big = 512

    def hidden_rows(i, at):
        for half in range(halves):
            value, slope = gelu_pair(nn(low[at, :], in_w[half]))
            active[at, half * ff : (half + 1) * ff] = value.astype(BF16)
            slopes[at, half * ff : (half + 1) * ff] = slope.astype(BF16)

    each_tile(rows, tile, hidden_rows)
    copies.out(slopes, slope_to)
    copies.out(active, active_to)
    down_copy.wait()

    def fed_rows(i, at):
        total = nt(active[at, :ff], down_w[0])
        for half in range(1, halves):
            total = total + nt(active[at, half * ff : (half + 1) * ff], down_w[half])
        fed[at, :] = total

    each_tile(rows, big, fed_rows)
    cotangent_copy.wait()

    def second_norm(i, at):
        normed = unit[at, :] * gain0 + shift0
        unit1, scale1 = centred_rows(normed + fed[at, :])
        position = place[0] + i * tile + lax.broadcasted_iota(jnp.int32, (tile, 1), 0)
        live = jnp.where(position < place[1], 1.0, 0.0)
        output[at, :] = (live * (unit1 * gain1 + shift1)).astype(BF16)
        grads = live * cotangent[at, :].astype(F32)
        norm_grads[:, :width] += jnp.sum(grads * unit1, axis=0, keepdims=True)
        norm_grads[:, width:] += jnp.sum(grads, axis=0, keepdims=True)
        second = norm_back(grads, gain1, unit1, scale1)
        fed[at, :] = second
        g_low = second.astype(BF16)
        g_fed[at, :] = g_low
        g_fed_turned[:, at] = g_low.T

    each_tile(rows, tile, second_norm)
    copies.out(output, output_to)
    copies.out(fed, g_second_to)
    copies.out(g_fed, g_fed_to)
    copies.out(g_fed_turned, fed_turned_to)
    weight_grad(g_fed_turned, active, halves, 1 - place[2], sent)
    copies.out(sent, sent_to)
    copies.finish()


ANYWHERE = pl.BlockSpec(memory_space=pl.ANY)


def feed_forward(place, first, conv, land_out, tokens, cotangent, weights, ff, part):
    rows, width = tokens.shape
    halves = weights.shape[0]
    grad = (halves, width, ff // 2)
    shapes = [
        ((rows, width), BF16), ((rows, width), BF16), ((rows, halves * ff), BF16),
        ((rows, width), BF16), ((rows, width), F32), ((rows, width), F32), ((rows, LANES), F32), ((width, rows), BF16),
        ((rows, halves * ff), BF16), ((width, rows), BF16), (grad, BF16), ((1, 2 * width), F32),
    ]
    scratch = [
        ((halves, width, ff), BF16), ((halves, width, ff), BF16), ((halves, width, part), BF16),
        ((halves, width, LANES), BF16), ((width, rows), F32), ((rows, width), BF16),
        ((rows, width), BF16), ((rows, width), BF16),
        ((rows, width), BF16), ((rows, width), F32), ((rows, LANES), F32), ((rows, width), F32),
        ((rows, halves * ff), BF16), ((rows, halves * ff), BF16), ((rows, width), BF16),
        ((width, rows), BF16), ((width, rows), BF16), ((rows, width), BF16), (grad, BF16),
    ]
    return pl.pallas_call(
        feed_kernel,
        out_shape=tuple(jax.ShapeDtypeStruct(*shape) for shape in shapes),
        in_specs=[SCALARS] + [ANYWHERE] * 2 + whole(1) + [ANYWHERE] * 3,
        out_specs=tuple([ANYWHERE] * 11 + whole(1)),
        scratch_shapes=[pltpu.VMEM(*shape) for shape in scratch]
        + [pltpu.SemaphoreType.DMA((19,))],
        compiler_params=PARAMS,
        cost_estimate=lasting(32),
        name="feed_forward",
    )(place, first, conv, land_out, tokens, cotangent, weights)


def feed_back_kernel(
    place, slope_in, g_fed_in, g_second_in, unit_in, scale_in, turned_in, weights,
    g_first_to, g_context_to, g_hidden_to, sent_to, att_turned_to, norm_grads,
    in_w, down_w, out_w, norms, g_hidden, g_fed, second, unit, scales, normed_turned,
    g_att, g_att_turned, g_context, sent,
    sems,
):
    rows, width = second.shape
    halves, _, ff = in_w.shape
    part = out_w.shape[2]
    tile = 256
    copies = Copies(sems)
    early = [
        copies.start(g_fed_in, g_fed),
        copies.start(weights.at[:, :, pl.ds(ff, ff)], down_w),
        copies.start(slope_in, g_hidden),
    ]
    later = [
        copies.start(turned_in, normed_turned),
        copies.start(weights.at[:, :, pl.ds(0, ff)], in_w),
        copies.start(g_second_in, second),
        copies.start(unit_in, unit),
        copies.start(scale_in, scales),
        copies.start(weights.at[:, :, pl.ds(2 * ff + part, LANES)], norms),
        copies.start(weights.at[:, :, pl.ds(2 * ff, part)], out_w),
    ]
    for copy in early:
        copy.wait()
    norm_grads[...] = jnp.zeros_like(norm_grads)
    big = 512

    def back_rows(i, at):
        for half in range(halves):
            g_act = nn(g_fed[at, :], down_w[half])
            to = slice(half * ff, (half + 1) * ff)
            g_hidden[at, to] = (g_act * g_hidden[at, to].astype(F32)).astype(BF16)

    each_tile(rows, big, back_rows)
    copies.out(g_hidden, g_hidden_to)
    later.pop(0).wait()
    weight_grad(normed_turned, g_hidden, halves, 1 - place[2], sent)
    copies.out(sent, sent_to)
    for copy in later:
        copy.wait()
    gain0 = norms[0].astype(F32).T[0:1]

    def normed_rows(i, at):
        total = second[at, :]
        for half in range(halves):
            total = total + nt(g_hidden[at, half * ff : (half + 1) * ff], in_w[half])
        second[at, :] = total

    each_tile(rows, big, normed_rows)

    def first_norm(i, at):
        grads = second[at, :]
        rows_unit, scale = unit[at, :], scales[at, 0:1]
        norm_grads[:, :width] += jnp.sum(grads * rows_unit, axis=0, keepdims=True)
        norm_grads[:, width:] += jnp.sum(grads, axis=0, keepdims=True)
        first = norm_back(grads, gain0, rows_unit, scale)
        second[at, :] = first
        low = first.astype(BF16)
        g_att[at, :] = low
        g_att_turned[:, at] = low.T

    each_tile(rows, tile, first_norm)
    copies.out(second, g_first_to)
    copies.out(g_att_turned, att_turned_to)
    for half in range(halves):
        g_context[:, half * part : (half + 1) * part] = nn(g_att[...], out_w[half]).astype(BF16)
    copies.out(g_context, g_context_to)
    copies.finish()


def feed_backward(place, fed, weights, ff, part):
    rows, width = fed[1].shape
    halves = weights.shape[0]
    grad = (halves, width, ff // 2)
    shapes = [
        ((rows, width), F32), ((rows, width), BF16), ((rows, halves * ff), BF16), (grad, BF16),
        ((width, rows), BF16), ((1, 2 * width), F32),
    ]
    scratch = [
        ((halves, width, ff), BF16), ((halves, width, ff), BF16), ((halves, width, part), BF16),
        ((halves, width, LANES), BF16), ((rows, halves * ff), BF16), ((rows, width), BF16),
        ((rows, width), F32), ((rows, width), F32),
        ((rows, LANES), F32), ((width, rows), BF16),
        ((rows, width), BF16), ((width, rows), BF16), ((rows, width), BF16), (grad, BF16),
    ]
    return pl.pallas_call(
        feed_back_kernel,
        out_shape=tuple(jax.ShapeDtypeStruct(*shape) for shape in shapes),
        in_specs=[SCALARS] + [ANYWHERE] * 7,
        out_specs=tuple([ANYWHERE] * 5 + whole(1)),
        scratch_shapes=[pltpu.VMEM(*shape) for shape in scratch]
        + [pltpu.SemaphoreType.DMA((16,))],
        compiler_params=PARAMS,
        cost_estimate=lasting(27),
        name="feed_backward",
    )(place, *fed, weights)


def kept_kernel(place, turned_in, cells_in, kept, turned, cells, sems):
    halves, width, columns = kept.shape
    ff = 2 * columns
    copies = Copies(sems)
    turned_copy = copies.start(turned_in, turned)
    pieces = []
    for half in range(halves):
        start = pl.multiple_of(half * ff + place[2] * columns, columns)
        pieces.append(copies.start(cells_in.at[:, pl.ds(start, columns)], cells.at[half]))
    turned_copy.wait()
    for half in range(halves):
        pieces[half].wait()

        def rows_of(i, at, half=half):
            kept[half, at, :] = nn(turned[at, :], cells[half]).astype(BF16)

        each_tile(width, 384, rows_of)


def kept_grad(place, turned, cells, halves):
    width, rows = turned.shape
    columns = cells.shape[1] // halves // 2
    return pl.pallas_call(
        kept_kernel,
        out_shape=jax.ShapeDtypeStruct((halves, width, columns), BF16),
        in_specs=[SCALARS] + [ANYWHERE] * 2,
        out_specs=whole(1)[0],
        scratch_shapes=[
            pltpu.VMEM((width, rows), BF16),
            pltpu.VMEM((halves, rows, columns), BF16),
            pltpu.SemaphoreType.DMA((3,)),
        ],
        compiler_params=PARAMS,
        cost_estimate=lasting(5),
        name="kept_grad",
    )(place, turned, cells)


def spread_kernel(place, turned_in, cells_in, other, kept, sent, turned, cells, sems):
    halves, width, columns = other.shape
    ff = 2 * columns
    quarter = columns // 2
    copies = Copies(sems)
    turned_copy = copies.start(turned_in, turned)
    pieces = []
    for half in range(halves):
        start = pl.multiple_of(half * ff + place[2] * columns, columns)
        pieces.append(copies.start(cells_in.at[:, pl.ds(start, columns)], cells.at[half]))
    turned_copy.wait()
    for half in range(halves):
        pieces[half].wait()

        def rows_of(i, at, half=half):
            total = nn(turned[at, :], cells[half]) + other[half, at, :].astype(F32)
            low = total.astype(BF16)
            first = place[4] == 0
            kept[half, at, :] = jnp.where(first, low[:, :quarter], low[:, quarter:])
            sent[half, at, :] = jnp.where(first, low[:, quarter:], low[:, :quarter])

        each_tile(width, 384, rows_of)


def spread_grad(place, turned, cells, other):
    halves, width, columns = other.shape
    rows = turned.shape[1]
    part = jax.ShapeDtypeStruct((halves, width, columns // 2), BF16)
    return pl.pallas_call(
        spread_kernel,
        out_shape=(part, part),
        in_specs=[SCALARS] + [ANYWHERE] * 2 + whole(1),
        out_specs=tuple(whole(2)),
        scratch_shapes=[
            pltpu.VMEM((width, rows), BF16),
            pltpu.VMEM((halves, rows, columns), BF16),
            pltpu.SemaphoreType.DMA((3,)),
        ],
        compiler_params=PARAMS,
        cost_estimate=lasting(6),
        name="spread_grad",
    )(place, turned, cells, other)


def pair_kernel(
    place, one_turned_in, one_cells_in, two_turned_in, two_cells_in, kept, sent,
    one_turned, one_cells, two_turned, two_cells, sems,
):
    copies = Copies(sems)
    loads = [
        copies.start(*pair)
        for pair in (
            (one_turned_in, one_turned), (one_cells_in, one_cells),
            (two_turned_in, two_turned), (two_cells_in, two_cells),
        )
    ]
    for number, (turned, cells) in enumerate(((one_turned, one_cells), (two_turned, two_cells))):
        loads[2 * number].wait()
        loads[2 * number + 1].wait()
        family_grads(turned, cells, place[2] == number, kept, sent)


def pair_grads(place, one_turned, one_cells, two_turned, two_cells, halves):
    width, rows = one_turned.shape
    shape = jax.ShapeDtypeStruct((halves, width, one_cells.shape[1] // halves), BF16)
    return pl.pallas_call(
        pair_kernel,
        out_shape=(shape, shape),
        in_specs=[SCALARS] + [ANYWHERE] * 4,
        out_specs=tuple(whole(2)),
        scratch_shapes=[
            pltpu.VMEM((width, rows), BF16), pltpu.VMEM(one_cells.shape, BF16),
            pltpu.VMEM((width, rows), BF16), pltpu.VMEM(one_cells.shape, BF16),
            pltpu.SemaphoreType.DMA((4,)),
        ],
        compiler_params=PARAMS,
        cost_estimate=lasting(6),
        name="pair_grads",
    )(place, one_turned, one_cells, two_turned, two_cells)


def rank_kernel(place, mine, got, land_tokens, weights, late, through, small):
    halves, width, _ = weights.shape
    part = late.shape[1] // 2
    first = place[2] == 0
    grads = (
        jnp.where(first, mine[:LANDMARKS], got[:LANDMARKS]),
        jnp.where(first, got[:LANDMARKS], mine[:LANDMARKS]),
    )
    counts = landmark_counts(place)
    total = jnp.zeros((2 * LANDMARKS, width), F32)
    for index, grad in enumerate(grads):
        both = jnp.concatenate(split(grad / counts), axis=0)
        for half in range(halves):
            weight = weights[half, :, index * part : (index + 1) * part]
            total = total + nt(both[:, half * part : (half + 1) * part], weight)
    through[...] = jnp.concatenate(split(total[:LANDMARKS] + total[LANDMARKS:]), axis=0)
    zero = jnp.zeros((LANDMARKS, part), F32)
    own = []
    for index, grad in enumerate(grads):
        columns = grad[:, :part]
        for half in range(1, halves):
            columns = jnp.where(place[5] == half, grad[:, half * part : (half + 1) * part], columns)
        own.append(jnp.where(place[2] == 1 - index, columns, zero))
    high, low = split(jnp.concatenate(own, axis=1))
    mean_high, mean_low = split(land_tokens[...] / counts)
    means = jnp.concatenate([mean_high, mean_low, mean_high, jnp.zeros_like(mean_low)], axis=0).T
    factors = jnp.concatenate([high, high, low, jnp.zeros_like(low)], axis=0)
    late[...] = nn(means, factors).astype(BF16)
    gains = jnp.where(first, mine[LANDMARKS:], got[LANDMARKS:])
    shifts = jnp.where(first, got[LANDMARKS:], mine[LANDMARKS:])
    taps = jnp.where(place[5] == 0, gains[2:3], shifts[2:3])
    rows = [gains[1:2], gains[0:1], shifts[1:2], shifts[0:1], taps]
    rows.append(jnp.zeros((small.shape[0] - len(rows), width), F32))
    small[...] = jnp.concatenate(rows, axis=0).astype(BF16)


def rank_parts(place, mine, got, land_tokens, weights):
    halves, width, packed = weights.shape
    return pl.pallas_call(
        rank_kernel,
        out_shape=(
            jax.ShapeDtypeStruct((width, 2 * packed // 3), BF16),
            jax.ShapeDtypeStruct((2 * LANDMARKS, width), BF16),
            jax.ShapeDtypeStruct((16, width), BF16),
        ),
        in_specs=[SCALARS] + whole(4),
        out_specs=tuple(whole(3)),
        compiler_params=PARAMS,
        cost_estimate=lasting(4),
        name="rank_parts",
    )(place, mine, got, land_tokens, weights)


def flipped(values, axis, bit):
    count = lax.axis_size(axis)
    return lax.ppermute(values, axis, [(i, i ^ bit) for i in range(count)])


def side_of(axis, bit):
    return (lax.axis_index(axis) // bit) % 2


def paired(mine, axis, bit, dim):
    other = flipped(mine, axis, bit)
    both = jnp.zeros(mine.shape[:dim] + (2,) + mine.shape[dim:], mine.dtype)
    side = side_of(axis, bit)
    both = lax.dynamic_update_slice_in_dim(both, jnp.expand_dims(mine, dim), side, dim)
    return lax.dynamic_update_slice_in_dim(both, jnp.expand_dims(other, dim), 1 - side, dim)


def ctx_bits():
    bits, bit = [], 1
    while bit < lax.axis_size("ctx"):
        bits.append(bit)
        bit *= 2
    return bits


def sequence_start(values):
    width = values.shape[1] // 2
    side = side_of("ctx", 1)
    kept = lax.dynamic_slice_in_dim(values, side * width, width, axis=1)
    sent = lax.dynamic_slice_in_dim(values, (1 - side) * width, width, axis=1)
    kept = kept + flipped(sent, "ctx", 1)
    return kept + flipped(kept, "tp", 1)


def sequence_end(kept):
    for bit in ctx_bits()[1:]:
        kept = kept + flipped(kept, "ctx", bit)
    return kept, flipped(kept, "ctx", 1)


def joined_halves(kept, other):
    return jnp.where(
        side_of("ctx", 1) == 0,
        jnp.concatenate([kept, other], axis=1),
        jnp.concatenate([other, kept], axis=1),
    )


def to_owner(kept, sent, combine):
    kept = combine(kept, flipped(sent, "ctx", 1))
    for bit in ctx_bits()[1:]:
        view = kept.reshape((-1, 2) + kept.shape[1:])
        side = side_of("ctx", bit)
        sent = lax.dynamic_index_in_dim(view, 1 - side, 1, False)
        kept = lax.dynamic_index_in_dim(view, side, 1, False)
        kept = combine(kept, flipped(sent, "ctx", bit))
    return kept[0], flipped(kept[0], "tp", 1)


def from_owners(part):
    whole_part = part[None]
    for bit in reversed(ctx_bits()):
        both = paired(whole_part, "ctx", bit, 1)
        whole_part = both.reshape((-1,) + part.shape)
    return whole_part.reshape((-1,) + part.shape[1:])


def merge_keys(one, two):
    size = LANES // 2
    one_top, two_top = one[..., size : size + 1], two[..., size : size + 1]
    top = jnp.maximum(one_top, two_top)
    one_factor, two_factor = jnp.exp(one_top - top), jnp.exp(two_top - top)
    summed = one * one_factor + two * two_factor
    lane = lax.broadcasted_iota(jnp.int32, summed.shape, summed.ndim - 1)
    return jnp.where(lane == size, top, summed)


def neighbour_rows(cells, count):
    pieces = lax.axis_size("ctx") * lax.axis_size("tp")
    up = [(i, i + 1) for i in range(pieces - 1)]
    before = lax.ppermute(cells[-count:], ("ctx", "tp"), up)
    after = lax.ppermute(cells[:count], ("ctx", "tp"), [(j, i) for i, j in up])
    return (
        jnp.pad(before, ((LANES - count, 0), (0, 0))),
        jnp.pad(after, ((0, LANES - count), (0, 0))),
    )


def own_quarter(shard):
    rows = shard.shape[0] // lax.axis_size("ctx")
    return lax.dynamic_slice_in_dim(shard, lax.axis_index("ctx") * rows, rows, axis=0)


def gathered(shard):
    full = lax.all_gather(own_quarter(shard), ("tp", "fsdp", "ctx"), tiled=True)
    return full.reshape(lax.axis_size("tp"), -1, shard.shape[1])


def gathered_early(shard):
    count = lax.axis_size("fsdp")
    piece = own_quarter(shard)
    if count > 4:
        held = lax.all_gather(piece, "fsdp")
    else:
        here = lax.axis_index("fsdp")
        held = jnp.zeros((count,) + piece.shape, piece.dtype)
        held = lax.dynamic_update_slice_in_dim(held, piece[None], here, 0)
        for step in range(1, count):
            moved = lax.ppermute(piece, "fsdp", [(i, (i + step) % count) for i in range(count)])
            held = lax.dynamic_update_slice_in_dim(held, moved[None], (here - step) % count, 0)
    bits = ctx_bits()
    halves = []
    for number, half in enumerate((held[: count // 2], held[count // 2 :])):
        half = half[None]
        if number == 0:
            half = paired(half[0], "tp", 1, 0)
        for place, bit in enumerate(reversed(bits[1:])):
            half = paired(half, "ctx", bit, 2 + place)
        if number == 1:
            half = paired(half[0], "tp", 1, 0)
        halves.append(paired(half, "ctx", bits[0], 1 + len(bits)))
    full = jnp.concatenate(halves, axis=1)
    return full.reshape(lax.axis_size("tp"), -1, shard.shape[1])


def bits_of(axis):
    bits, bit = [], lax.axis_size(axis) // 2
    while bit:
        bits.append(bit)
        bit //= 2
    return bits


def added(*parts):
    return sum(part.astype(F32) for part in parts).astype(BF16)


def cut(cells, axis, bit, dim):
    size = cells.shape[dim] // 2
    side = side_of(axis, bit)
    return (
        lax.dynamic_slice_in_dim(cells, side * size, size, axis=dim),
        lax.dynamic_slice_in_dim(cells, (1 - side) * size, size, axis=dim),
    )


def gate(*values):
    return lax.optimization_barrier(values)


def dotf(spec, *operands):
    return jnp.einsum(spec, *operands, preferred_element_type=F32)


def taps_round(taps):
    middle = taps.shape[1] // 2
    gap = jnp.zeros((taps.shape[0], LANES - taps.shape[1]), F32)
    return jnp.concatenate([taps[:, middle::-1], gap, taps[:, :middle:-1]], axis=1)


def landmark_bounds(length):
    landmark = jnp.arange(LANDMARKS + 1, dtype=jnp.int32)
    return (landmark * length + LANDMARKS - 1) // LANDMARKS


def landmark_counts_of(length):
    bounds = landmark_bounds(length)
    return (bounds[1:] - bounds[:-1]).astype(F32)[:, None]


def landmark_rows(position, length):
    bounds = landmark_bounds(length)
    inside = (position[:, None] >= bounds[None, :-1]) & (position[:, None] < bounds[None, 1:])
    return inside.astype(BF16)


def on_device(
    tokens,
    lengths,
    qk_weight,
    value_weight,
    out_weight,
    in_weight,
    down_weight,
    norm_gains,
    norm_shifts,
    conv_weight,
    cotangent,
):
    tp_count = lax.axis_size("tp")
    tp_index = lax.axis_index("tp")
    ctx_index = lax.axis_index("ctx")
    _, slot_len, model_width = tokens.shape
    rows = slot_len // tp_count
    local_heads, tap_count = conv_weight.shape
    local_width = value_weight.shape[1]
    ff_width = in_weight.shape[1]
    head_size = local_width // local_heads
    heads = local_heads * tp_count
    owners = lax.axis_size("ctx")
    own_heads = heads // owners
    width = local_width * tp_count
    radius = tap_count // 2
    length = lengths[0]

    first_row = (ctx_index * tp_count + tp_index) * rows
    sides = (side_of("ctx", 1), ctx_index, side_of("ctx", ctx_bits()[-1]), tp_index)
    place = jnp.stack([first_row, length, *sides]).astype(jnp.int32)

    norm_columns = jnp.concatenate([norm_gains, norm_shifts], axis=0).T
    norm_columns = jnp.pad(norm_columns, ((0, 0), (0, LANES - norm_columns.shape[1])))
    ffn_full = gathered(
        jnp.concatenate([in_weight, down_weight.T, out_weight.T, norm_columns], axis=1)
    )
    own_taps = jnp.where(ctx_index == 0, conv_weight.astype(F32), 0.0)
    tap_rows = jnp.pad(own_taps, ((0, 8 - local_heads), (0, LANES - tap_count)))
    tap_rows = jnp.where(
        jnp.arange(model_width) // LANES == tp_index,
        jnp.tile(tap_rows, (1, model_width // LANES)),
        0.0,
    )
    qkv_full = gathered_early(jnp.concatenate([qk_weight[0], qk_weight[1], value_weight], axis=1))
    own = lax.dynamic_slice_in_dim(tokens[0], tp_index * rows, rows, axis=0)
    land_tokens = sequence_start(jnp.concatenate([token_sums(place, own), tap_rows], axis=0))
    land_tokens = joined_halves(*sequence_end(land_tokens))
    own_cotangent = lax.dynamic_slice_in_dim(cotangent[0], tp_index * rows, rows, axis=0)
    tap_weights = land_tokens[LANDMARKS : LANDMARKS + local_heads, : tp_count * LANES]
    tap_weights = tap_weights.reshape(local_heads, tp_count, LANES).transpose(1, 0, 2)
    tap_weights = tap_weights.reshape(heads, LANES)[:, :tap_count]
    land_tokens = land_tokens[:LANDMARKS]
    base, base_back = taps_round(tap_weights), taps_round(tap_weights[:, ::-1])

    queries, keys, values, v_plain, land_q, land_k, own_turned, *parts_of_third = projections(
        place, own, land_tokens, qkv_full, head_size, owners
    )
    v_ends = neighbour_rows(v_plain, radius)
    merged, merged_tp = to_owner(*parts_of_third, merge_keys)
    kept_turns = inverse_forward(place, land_q, land_k, owners)
    first, conv = first_and_conv(queries, values, *v_ends, land_k, base)
    merged, own_out = landmark_out(merged, merged_tp, kept_turns[0])
    land_out = from_owners(own_out)

    own_output, context, *fed, active, fed_turned, down_sent, last_norm = feed_forward(
        place, first, conv, land_out, own, own_cotangent, ffn_full, ff_width, local_width
    )
    high = ctx_bits()[-1]
    owner_count = lax.axis_size("fsdp")
    owner_rows = model_width // owner_count
    near, *farther = bits_of("fsdp")[::-1]

    def by_owner_bits(cells):
        return cells.reshape((2,) * (1 + len(farther)) + (-1, cells.shape[-1]))

    def cut_last(cells, bit):
        dim = cells.ndim - 3
        return tuple(piece.squeeze(dim) for piece in cut(cells, "fsdp", bit, dim))

    other_output = flipped(own_output, "tp", 1)
    down_other = flipped(down_sent, "ctx", 1)
    down_kept = kept_grad(place, fed_turned, active, tp_count)
    down_kept, down_other = gate(down_kept, down_other)
    down_mine, down_theirs = cut(down_kept, "ctx", high, 2)
    other_mine, other_theirs = cut(down_other, "ctx", high, 2)
    down_sent = added(down_theirs, other_theirs)
    down_got = flipped(down_sent, "ctx", high)
    fed[0], down_sent = gate(fed[0], down_sent)
    grad_first_res, grad_context, g_hidden, in_sent, att_turned, first_norm = feed_backward(
        place, fed, ffn_full, ff_width, local_width
    )
    in_sent, grad_context, g_hidden, other_output, down_got = gate(
        in_sent, grad_context, g_hidden, other_output, down_got
    )
    in_other = flipped(in_sent, "ctx", 1)
    g_ends = neighbour_rows(grad_context, radius)
    down = added(down_mine, other_mine, down_got)
    down_mine, down_sent = cut(down, "tp", 1, 0)
    down_got = flipped(down_sent, "tp", 1)
    grad_context, down_sent = gate(grad_context, down_sent)
    land_kept, land_sent, g_lk, g_q = attention_back(
        place, queries, grad_context, land_k, land_out, owners
    )
    land_kept, land_sent, in_other, g_ends = gate(land_kept, land_sent, in_other, g_ends)

    land_other = flipped(land_sent, "ctx", 1)
    in_kept, in_sent = spread_grad(place, fed[5], g_hidden, in_other)
    in_kept, in_sent, land_other, down_got = gate(in_kept, in_sent, land_other, down_got)
    land_grads = land_kept + land_other
    land_mine, land_theirs = cut(land_grads, "ctx", high, 0)
    land_got = flipped(land_theirs, "ctx", high)
    land_theirs, in_sent = gate(land_theirs, in_sent)
    in_got = flipped(in_sent, "ctx", high)
    down = added(down_mine, down_got)
    grad_context, in_sent = gate(grad_context, in_sent)
    g_conv, g_taps = conv_back(v_plain, v_ends, grad_context, g_ends, base_back)
    g_conv, g_taps, land_got = gate(g_conv, g_taps, land_got)
    own_grads = (land_mine + land_got)[0]
    tp_grads = flipped(own_grads, "tp", 1)

    def parts(cells):
        return cells.reshape(rows, tp_count, local_width)

    def qkv_part(index):
        return qkv_full[:, :, index * local_width : (index + 1) * local_width]

    g_q, own_grads = gate(g_q, own_grads)
    mixed_kept, mixed_sent = pair_grads(place, att_turned, context, own_turned, g_q, tp_count)
    back_q = grad_first_res + dotf("tpk,pck->tc", parts(g_q), qkv_part(0))
    mixed_kept, mixed_sent, tp_grads, back_q = gate(mixed_kept, mixed_sent, tp_grads, back_q)
    mixed_got = flipped(mixed_sent, "ctx", 1)
    own_grads, mixed_sent = gate(own_grads + tp_grads, mixed_sent)
    spread, lq_mid, lk_mid = inverse_backward(
        place, land_q, land_k, merged, own_grads, *kept_turns
    )
    spread, in_got, mixed_got = gate(spread, in_got, mixed_got)
    spread = from_owners(spread)

    in_mine, in_sent = cut(added(in_kept, in_got), "tp", 1, 0)
    in_got = flipped(in_sent, "tp", 1)
    def by_ctx(cells):
        return cells.reshape(tp_count, owner_count, 2, -1, local_width)

    mixed = added(mixed_kept, mixed_got)
    mixed_mine, mixed_sent = cut(by_ctx(mixed), "ctx", high, 2)
    mixed_got = flipped(mixed_sent, "ctx", high)
    spread, in_sent, mixed_sent = gate(spread, in_sent, mixed_sent)
    g_k, g_v, sums, kv_kept, kv_sent = third_back(
        place, keys, values, land_q, spread, g_conv, lq_mid, lk_mid, g_lk, last_norm, first_norm,
        g_taps, own_turned, tp_count,
    )

    kv_kept, kv_sent, sums, in_got, mixed_got = gate(kv_kept, kv_sent, sums, in_got, mixed_got)
    kv_got = flipped(kv_sent, "ctx", 1)
    sums_mine, sums_sent = cut(sums, "ctx", 1, 1)
    sums_got = flipped(sums_sent, "ctx", 1)
    kv_kept, kv_got = gate(kv_kept, kv_got)
    kv_mine, kv_sent = cut(by_ctx(added(kv_kept, kv_got)), "ctx", high, 2)
    kv_sent, sums_mine, mixed_mine, in_mine, g_k, g_v = gate(
        kv_sent, sums_mine, mixed_mine, in_mine, g_k, g_v
    )
    kv_got = flipped(kv_sent, "ctx", high)
    sums = sums_mine + sums_got
    sums_got = flipped(sums, "tp", 1)
    mixed_mine, mixed_sent = cut(added(mixed_mine, mixed_got), "tp", 1, 0)
    sums, mixed_sent, in_mine = gate(sums, mixed_sent, in_mine)
    mixed_got = flipped(mixed_sent, "tp", 1)
    pair = jnp.concatenate([added(in_mine, in_got)[0], down[0]], axis=1)
    g_k, g_v, mixed_sent, pair = gate(g_k, g_v, mixed_sent, pair)
    pair = lax.psum_scatter(pair, "fsdp", scatter_dimension=0, tiled=True)
    own_grad = (
        back_q
        + dotf("tpk,pck->tc", parts(g_k), qkv_part(1))
        + dotf("tpk,pck->tc", parts(g_v), qkv_part(2))
    ).astype(BF16)
    own_grad, sums_got, mixed_got, kv_got = gate(own_grad, sums_got, mixed_got, kv_got)
    sums = sums + sums_got
    sums_got = flipped(sums, "ctx", high)
    kv_mine, kv_sent = cut(added(kv_mine, kv_got), "tp", 1, 0)
    own_grad, sums, kv_sent = gate(own_grad, sums, kv_sent)
    kv_got = flipped(kv_sent, "tp", 1)
    first_rows = 5 * rows // 16
    other_first = flipped(own_grad[:first_rows], "tp", 1)
    other_second = flipped(own_grad[first_rows:], "tp", 1)
    sums = sums + sums_got
    sums_got = flipped(sums, "ctx", 1)
    sums, sums_got, kv_got = gate(sums, sums_got, kv_got)
    late, through, small = rank_parts(place, sums, sums_got, land_tokens, qkv_full)
    late, through, small, other_first, own_output, other_output = gate(
        late, through, small, other_first, own_output, other_output
    )
    late = late.reshape(owner_count, 2, -1, 2 * local_width)
    late = lax.dynamic_index_in_dim(late, place[4], 1, False)
    mixed = added(
        jnp.concatenate([mixed_mine, kv_mine], axis=-1).reshape(late.shape),
        jnp.concatenate([mixed_got, kv_got], axis=-1).reshape(late.shape),
        late,
    )
    small = jnp.broadcast_to(small[None], (owner_count,) + small.shape)
    mixed = by_owner_bits(jnp.concatenate([mixed, small], axis=1))
    mixed_mine, mixed_sent = cut_last(mixed, near)
    mixed_got = flipped(mixed_sent, "fsdp", near)
    mixed = added(mixed_mine, mixed_got)
    for bit in farther:
        mixed_mine, mixed_sent = cut_last(mixed, bit)
        mixed = added(mixed_mine, flipped(mixed_sent, "fsdp", bit))
    small = mixed[-16:].astype(F32)
    mixed = mixed[:-16]

    def of_core(cells, core):
        cells = cells.reshape((owners // 2, 2) + cells.shape[1:])
        return [cells[i, core] for i in range(owners // 2)]

    mixed, pair, other_second = gate(mixed, pair, other_second)
    mixed = from_owners(mixed[None])
    sides = [jnp.concatenate(of_core(mixed, core), axis=0).astype(F32) for core in range(2)]
    grad_out, grad_k = sides[0][:, :local_width].T, sides[0][:, local_width:]
    grad_q, grad_v = sides[1][:, :local_width], sides[1][:, local_width:]

    own_columns = lax.axis_index("fsdp") * owner_rows
    norm_sums = lax.dynamic_slice_in_dim(small[:4], own_columns, owner_rows, axis=1)
    taps_sum = small[4].reshape(local_heads, LANES)
    grad_taps = jnp.concatenate(
        [taps_sum[:, radius - 1 :: -1], taps_sum[:, : -radius - 2 : -1]], axis=1
    )

    columns = pair.shape[1] // 2
    pair = from_owners(pair[None])
    pieces = [piece for core in range(2) for piece in of_core(pair, core)]
    grad_in = jnp.concatenate([piece[:, :columns] for piece in pieces], axis=1).astype(F32)
    grad_down = jnp.concatenate([piece[:, columns:] for piece in pieces], axis=1).astype(F32).T

    output = jnp.where(
        tp_index == 0,
        jnp.concatenate([own_output, other_output]),
        jnp.concatenate([other_output, own_output]),
    )[None]
    both_grads = jnp.where(
        tp_index == 0,
        jnp.concatenate([own_grad, other_first, other_second]),
        jnp.concatenate([other_first, other_second, own_grad]),
    )
    position = ctx_index * slot_len + jnp.arange(slot_len, dtype=jnp.int32)
    onehot = landmark_rows(position, length)
    grad_tokens = both_grads.astype(F32) + dotf(
        "tm,mc->tc", jnp.concatenate([onehot, onehot], axis=1), through
    )
    grad_tokens = grad_tokens.reshape(1, slot_len, model_width)
    return (
        output,
        grad_tokens,
        jnp.stack([grad_q, grad_k]),
        grad_v,
        grad_out,
        grad_in,
        grad_down,
        norm_sums[:2],
        norm_sums[2:],
        grad_taps,
    )


def solution(mesh):
    in_specs = (
        P("fsdp", "ctx", None),
        P("fsdp"),
        P(None, "fsdp", "tp"),
        P("fsdp", "tp"),
        P("tp", "fsdp"),
        P("fsdp", "tp"),
        P("tp", "fsdp"),
        P(None, "fsdp"),
        P(None, "fsdp"),
        P("tp", None),
        P("fsdp", "ctx", None),
    )
    out_specs = (
        P("fsdp", "ctx", None),
        P("fsdp", "ctx", None),
        P(None, "fsdp", "tp"),
        P("fsdp", "tp"),
        P("tp", "fsdp"),
        P("fsdp", "tp"),
        P("tp", "fsdp"),
        P(None, "fsdp"),
        P(None, "fsdp"),
        P("tp", None),
    )
    return jax.shard_map(
        on_device, mesh=mesh, in_specs=in_specs, out_specs=out_specs, check_vma=False
    )
```

```python
import jax
import jax.numpy as jnp
from jax import lax
from jax.experimental import pallas as pl
from jax.experimental.pallas import tpu as pltpu
from jax.sharding import PartitionSpec as P

LANDMARKS = 64
NEWTON = 6
LANES = 128
VMEM_BYTES = 56 * 2**20

HIGH = lax.Precision.HIGHEST
F32 = jnp.float32
BF16 = jnp.bfloat16


def lasting(microseconds):
    return pl.CostEstimate(
        flops=int(microseconds * 1.1535e9), bytes_accessed=int(microseconds * 1e5), transcendentals=0
    )


def nn(left, right):
    return jnp.dot(left, right, preferred_element_type=F32)


def nt(left, right):
    return lax.dot_general(left, right, (((1,), (1,)), ((), ())), preferred_element_type=F32)


def split(wide):
    high = wide.astype(BF16)
    return high, (wide - high.astype(F32)).astype(BF16)


def each_tile(count, tile, body):
    def step(i, _):
        body(i, pl.ds(pl.multiple_of(i * tile, tile), tile))
        return 0

    lax.fori_loop(0, count // tile, step, 0)


def family_grads(turned, cells, mine, kept, sent):
    halves, width, columns = kept.shape

    def rows_of(i, at):
        total = nn(turned[at, :], cells[...]).astype(BF16)

        @pl.when(mine)
        def _():
            for half in range(halves):
                kept[half, at, :] = total[:, half * columns : (half + 1) * columns]

        @pl.when(jnp.logical_not(mine))
        def _():
            for half in range(halves):
                sent[half, at, :] = total[:, half * columns : (half + 1) * columns]

    each_tile(width, 384, rows_of)


def whole(count):
    return [pl.BlockSpec(memory_space=pltpu.VMEM)] * count


SCALARS = pl.BlockSpec(memory_space=pltpu.SMEM)
PARAMS = pltpu.CompilerParams(vmem_limit_bytes=VMEM_BYTES)


def landmark_onehot(place, rows, landmark_axis):
    shape = (LANDMARKS, rows) if landmark_axis == 0 else (rows, LANDMARKS)
    landmark = lax.broadcasted_iota(jnp.int32, shape, landmark_axis)
    position = place[0] + lax.broadcasted_iota(jnp.int32, shape, 1 - landmark_axis)
    start = lax.shift_right_logical(landmark * place[1] + (LANDMARKS - 1), 6)
    end = lax.shift_right_logical((landmark + 1) * place[1] + (LANDMARKS - 1), 6)
    return jnp.where((position >= start) & (position < end), 1.0, 0.0).astype(BF16)


def live_lanes(place, rows):
    position = place[0] + lax.broadcasted_iota(jnp.int32, (1, rows), 1)
    return position < place[1]


def band(base_row):
    ring = pltpu.roll(jnp.broadcast_to(base_row, (LANES, LANES)), 0, 1, stride=1, stride_axis=0)
    gap = lax.broadcasted_iota(jnp.int32, (LANES, LANES), 0) - lax.broadcasted_iota(
        jnp.int32, (LANES, LANES), 1
    )
    zero = jnp.zeros_like(ring)
    before = jnp.where(gap >= LANES - 16, ring, zero).astype(BF16)
    here = jnp.where(jnp.abs(gap) <= 16, ring, zero).astype(BF16)
    after = jnp.where(gap <= 16 - LANES, ring, zero).astype(BF16)
    return before, here, after


def convolved(blocks, bands):
    count = len(blocks) - 2
    size = blocks[0].shape[0]
    stacked = jnp.concatenate(
        [jnp.concatenate(blocks[i : i + 3], axis=1) for i in range(count)], axis=0
    )
    out = nn(stacked, jnp.concatenate(bands, axis=0))
    return jnp.concatenate([out[i * size : (i + 1) * size] for i in range(count)], axis=1)


def token_sums_kernel(place, tokens, sums):
    sums[...] = nn(landmark_onehot(place, tokens.shape[0], 0), tokens[...])


def token_sums(place, tokens):
    return pl.pallas_call(
        token_sums_kernel,
        out_shape=jax.ShapeDtypeStruct((LANDMARKS, tokens.shape[1]), F32),
        in_specs=[SCALARS] + whole(1),
        out_specs=whole(1)[0],
        compiler_params=PARAMS,
        cost_estimate=lasting(2.5),
        name="token_sums",
    )(place, tokens)


def landmark_counts(place):
    landmark = lax.broadcasted_iota(jnp.int32, (LANDMARKS, 1), 0)
    start = lax.shift_right_logical(landmark * place[1] + (LANDMARKS - 1), 6)
    end = lax.shift_right_logical((landmark + 1) * place[1] + (LANDMARKS - 1), 6)
    return (end - start).astype(F32)


def projection_kernel(
    place, tokens, sums, weights, q_out, k_out, v_out, v_plain, land_q, land_k, turned, kept, sent
):
    rows = tokens.shape[0]
    halves, _, packed = weights.shape
    width = packed // 3
    size = land_q.shape[2]
    position = place[0] + lax.broadcasted_iota(jnp.int32, (rows, 1), 0)
    live = jnp.where(position < place[1], 1.0, 0.0)
    scaled = live * 64**-0.25
    means = jnp.concatenate(split(sums[...] / landmark_counts(place)), axis=0)
    cells = tokens[...]
    turned[...] = cells.T
    for half in range(halves):
        for part, out in enumerate((q_out, k_out, v_out)):
            weight = weights[half, :, part * width : (part + 1) * width]
            low = ((live if part == 2 else scaled) * nn(cells, weight)).astype(BF16)
            out[half * width : (half + 1) * width, :] = low.T
            if part == 2:
                v_plain[:, half * width : (half + 1) * width] = low
                continue
            both = nn(means, weight)
            land = (64**-0.25 * (both[:LANDMARKS] + both[LANDMARKS:])).astype(BF16)
            to = land_k if part else land_q
            for head in range(width // size):
                to[half * (width // size) + head] = land[:, head * size : (head + 1) * size]
    third_heads(place, k_out, v_out, land_q, kept, sent)


def projections(place, tokens, sums, weights, size, owners):
    rows = tokens.shape[0]
    width = weights.shape[0] * weights.shape[2] // 3
    turned = jax.ShapeDtypeStruct((width, rows), BF16)
    land = jax.ShapeDtypeStruct((width // size, LANDMARKS, size), BF16)
    return pl.pallas_call(
        projection_kernel,
        out_shape=(turned, turned, turned, jax.ShapeDtypeStruct((rows, width), BF16), land, land)
        + (jax.ShapeDtypeStruct(tokens.shape[::-1], BF16),)
        + owner_parts(width // size, owners),
        in_specs=[SCALARS] + whole(3),
        out_specs=tuple(whole(9)),
        compiler_params=PARAMS,
        cost_estimate=lasting(18),
        name="projections",
    )(place, tokens, sums, weights)


def by_owner(place, h, owners, kept, sent, values):
    per = kept.shape[1]
    for owner in range(owners):
        @pl.when((h >= owner * per) & (h < (owner + 1) * per))
        def _(owner=owner):
            mine = place[2] == owner % 2

            @pl.when(mine)
            def _():
                kept[owner // 2, h - owner * per] = values

            @pl.when(jnp.logical_not(mine))
            def _():
                sent[owner // 2, h - owner * per] = values


def third_heads(place, keys, values, land_q, kept, sent):
    heads = land_q.shape[0]
    size = land_q.shape[2]
    rows = keys.shape[1]
    owners = 2 * kept.shape[0]
    live = live_lanes(place, rows)

    def head(h):
        at = pl.ds(pl.multiple_of(h * size, size), size)
        scores = jnp.where(live, nn(land_q[h], keys[at, :]), -1e30)
        top = jnp.max(scores, axis=1, keepdims=True)
        raised = jnp.where(live, jnp.exp(scores - top), 0.0)
        total = jnp.sum(raised, axis=1, keepdims=True)
        high, low = split(raised)
        value = values[at, :]
        mixed = nt(high, value) + nt(low, value)
        lane = lax.broadcasted_iota(jnp.int32, (LANDMARKS, LANES - size), 1)
        stats = jnp.where(lane == 0, top, jnp.where(lane == 1, total, 0.0))
        by_owner(place, h, owners, kept, sent, jnp.concatenate([mixed, stats], axis=1))

    def pair(i, _):
        head(2 * i)
        head(2 * i + 1)
        return 0

    lax.fori_loop(0, heads // 2, pair, 0)


def owner_parts(heads, owners):
    part = jax.ShapeDtypeStruct((owners // 2, heads // owners, LANDMARKS, LANES), F32)
    return part, part


def dot_high(left, right):
    return jnp.dot(left, right, preferred_element_type=F32, precision=HIGH)


def dot_high_nt(left, right):
    return lax.dot_general(
        left, right, (((1,), (1,)), ((), ())), preferred_element_type=F32, precision=HIGH
    )


def eye():
    row = lax.broadcasted_iota(jnp.int32, (LANDMARKS, LANDMARKS), 0)
    column = lax.broadcasted_iota(jnp.int32, (LANDMARKS, LANDMARKS), 1)
    return jnp.where(row == column, 1.0, 0.0)


def middle_map(land_q, land_k):
    scores = nt(land_q, land_k)
    raised = jnp.exp(scores - jnp.max(scores, axis=1, keepdims=True))
    return raised / jnp.sum(raised, axis=1, keepdims=True)


def inverse_kernel(place, land_q, land_k, kept_v, kept_p, kept_b, kept_c):
    heads = range(kept_v.shape[1])
    one = eye()
    own = [place[3] * len(heads) + h for h in heads]
    middle = [middle_map(land_q[h], land_k[h]) for h in own]
    approx = [m.T / jnp.sum(m * m, keepdims=True) for m in middle]
    for turn in range(NEWTON):
        product = [dot_high(middle[h], approx[h]) for h in heads]
        for h in heads:
            kept_v[turn, h] = approx[h]
            kept_p[turn, h] = product[h]
        bracket = [7.0 * one - p for p in product]
        bracket = [15.0 * one - dot_high(product[h], bracket[h]) for h in heads]
        for h in heads:
            kept_b[turn, h] = bracket[h]
        bracket = [13.0 * one - dot_high(product[h], bracket[h]) for h in heads]
        for h in heads:
            kept_c[turn, h] = bracket[h]
        approx = [0.25 * dot_high(approx[h], bracket[h]) for h in heads]
    for h in heads:
        kept_v[NEWTON, h] = approx[h]


def inverse_forward(place, land_q, land_k, owners):
    heads = land_q.shape[0] // owners
    square = (heads, LANDMARKS, LANDMARKS)
    return pl.pallas_call(
        inverse_kernel,
        out_shape=(
            jax.ShapeDtypeStruct((NEWTON + 1,) + square, F32),
            jax.ShapeDtypeStruct((NEWTON,) + square, F32),
            jax.ShapeDtypeStruct((NEWTON,) + square, F32),
            jax.ShapeDtypeStruct((NEWTON,) + square, F32),
        ),
        in_specs=[SCALARS] + whole(2),
        out_specs=tuple(whole(4)),
        compiler_params=PARAMS,
        cost_estimate=lasting(7),
        name="inverse_forward",
    )(place, land_q, land_k)


def merged_keys(one, two, size):
    one_top, two_top = one[:, size : size + 1], two[:, size : size + 1]
    top = jnp.maximum(one_top, two_top)
    summed = one * jnp.exp(one_top - top) + two * jnp.exp(two_top - top)
    lane = lax.broadcasted_iota(jnp.int32, one.shape, 1)
    return jnp.where(lane == size, top, summed)


def land_out_kernel(one, two, kept_v, merged, land_out):
    size = land_out.shape[2]
    for h in range(one.shape[0]):
        both = merged_keys(one[h], two[h], size)
        merged[h] = both
        mixed = both[:, :size] / both[:, size + 1 : size + 2]
        land_out[h] = dot_high(kept_v[NEWTON, h], mixed).astype(BF16)


def landmark_out(one, two, kept_v):
    heads = one.shape[0]
    return pl.pallas_call(
        land_out_kernel,
        out_shape=(
            jax.ShapeDtypeStruct(one.shape, F32),
            jax.ShapeDtypeStruct((heads, LANDMARKS, LANES // 2), BF16),
        ),
        in_specs=whole(3),
        out_specs=tuple(whole(2)),
        compiler_params=PARAMS,
        cost_estimate=lasting(2.2),
        name="landmark_out",
    )(one, two, kept_v)


def inverse_back_kernel(
    place, land_q, land_k, merged, grads, kept_v, kept_p, kept_b, kept_c, spread, g_lq, g_lk
):
    heads = range(grads.shape[0])
    size = land_q.shape[2]
    one = eye()
    own = [place[3] * len(heads) + h for h in heads]
    middle = [middle_map(land_q[h], land_k[h]) for h in own]
    turned = [m.T for m in middle]
    g_approx = []
    for h in heads:
        mixed = merged[h][:, :size] / merged[h][:, size + 1 : size + 2]
        g_land = grads[h][:, :size]
        g_approx.append(dot_high_nt(g_land, mixed))
        g_mixed = dot_high(kept_v[NEWTON, h].T, g_land)
        row_dot = jnp.sum(g_mixed * mixed, axis=1, keepdims=True)
        lane = lax.broadcasted_iota(jnp.int32, (LANDMARKS, LANES - size), 1)
        top = merged[h][:, size : size + 1]
        total = merged[h][:, size + 1 : size + 2]
        stats = jnp.where(
            lane == 0, row_dot, jnp.where(lane == 1, top, jnp.where(lane == 2, total, 0.0))
        )
        spread[h] = jnp.concatenate([g_mixed, stats], axis=1)
    g_middle = [jnp.zeros((LANDMARKS, LANDMARKS), F32) for _ in heads]
    for turn in reversed(range(NEWTON)):
        approx = [kept_v[turn, h] for h in heads]
        product = [kept_p[turn, h] for h in heads]
        first = [7.0 * one - p for p in product]
        second = [kept_b[turn, h] for h in heads]
        third = [kept_c[turn, h] for h in heads]
        g_third = [0.25 * dot_high(approx[h].T, g_approx[h]) for h in heads]
        g_back = [0.25 * dot_high_nt(g_approx[h], third[h]) for h in heads]
        g_product = [-dot_high_nt(g_third[h], second[h]) for h in heads]
        pt = [p.T for p in product]
        g_second = [-dot_high(pt[h], g_third[h]) for h in heads]
        g_product = [g_product[h] - dot_high_nt(g_second[h], first[h]) for h in heads]
        g_product = [g_product[h] + dot_high(pt[h], g_second[h]) for h in heads]
        g_middle = [g_middle[h] + dot_high_nt(g_product[h], approx[h]) for h in heads]
        g_approx = [g_back[h] + dot_high(turned[h], g_product[h]) for h in heads]
    for h in heads:
        m = middle[h]
        size_sum = jnp.sum(m * m, keepdims=True)
        g_size = -jnp.sum(g_approx[h] * turned[h], keepdims=True) / (size_sum * size_sum)
        g_m = g_middle[h] + g_approx[h].T / size_sum + 2.0 * g_size * m
        g_scores = m * (g_m - jnp.sum(g_m * m, axis=1, keepdims=True))
        g_lq[h] = dot_high(g_scores, land_k[own[h]].astype(F32))
        g_lk[h] = dot_high(g_scores.T, land_q[own[h]].astype(F32))


def inverse_backward(place, land_q, land_k, merged, grads, *kept):
    heads = grads.shape[0]
    square = jax.ShapeDtypeStruct((heads,) + land_q.shape[1:], F32)
    return pl.pallas_call(
        inverse_back_kernel,
        out_shape=(jax.ShapeDtypeStruct((heads, LANDMARKS, LANES), F32), square, square),
        in_specs=[SCALARS] + whole(8),
        out_specs=tuple(whole(3)),
        compiler_params=PARAMS,
        cost_estimate=lasting(11.5),
        name="inverse_backward",
    )(place, land_q, land_k, merged, grads, *kept)


def first_map(land_k, queries):
    scores = nn(land_k, queries)
    raised = jnp.exp(scores - jnp.max(scores, axis=0, keepdims=True))
    return raised * (1.0 / jnp.sum(raised, axis=0, keepdims=True))


def head_blocks(cells, ends, at):
    rows = cells.shape[1]
    left, right = ends
    return (
        [left[at, :]]
        + [cells[at, i * LANES : (i + 1) * LANES] for i in range(rows // LANES)]
        + [right[at, :]]
    )


def first_conv_kernel(queries, values, left, right, land_k, base, first, conv, ends):
    heads, _, size = land_k.shape
    ends[0] = left[...].T
    ends[1] = right[...].T

    def head(h):
        at = pl.ds(pl.multiple_of(h * size, size), size)
        first[at, :] = first_map(land_k[h], queries[at, :]).astype(BF16)
        blocks = head_blocks(values, (ends.at[0], ends.at[1]), at)
        conv[at, :] = convolved(blocks, band(base[pl.ds(h, 1), :]))

    def pair(i, _):
        head(2 * i)
        head(2 * i + 1)
        return 0

    lax.fori_loop(0, heads // 2, pair, 0)


def first_and_conv(queries, values, left, right, land_k, base):
    width, rows = queries.shape
    return pl.pallas_call(
        first_conv_kernel,
        out_shape=(
            jax.ShapeDtypeStruct((width, rows), BF16),
            jax.ShapeDtypeStruct((width, rows), F32),
        ),
        in_specs=whole(6),
        out_specs=tuple(whole(2)),
        scratch_shapes=[pltpu.VMEM((2, width, LANES), BF16)],
        compiler_params=PARAMS,
        cost_estimate=lasting(8),
        name="first_and_conv",
    )(queries, values, left, right, land_k, base)


def context_rows(first, conv, land_out, context):
    heads, _, size = land_out.shape

    def head(h):
        at = pl.ds(pl.multiple_of(h * size, size), size)
        return (nn(land_out[h].T, first[at, :]) + conv[at, :]).astype(BF16)

    def pair(i, _):
        both = jnp.concatenate([head(2 * i), head(2 * i + 1)], axis=0)
        context[:, pl.ds(pl.multiple_of(i * LANES, LANES), LANES)] = both.T
        return 0

    lax.fori_loop(0, heads // 2, pair, 0)


def attention_back_kernel(
    place, queries, grads, land_k, land_out, kept, sent, g_lk, g_query
):
    heads, _, size = land_k.shape
    rows = queries.shape[1]
    owners = 2 * kept.shape[0]
    scaled = jnp.where(live_lanes(place, rows), 64**-0.25, 0.0)

    def pair(i, _):
        lanes = pl.ds(pl.multiple_of(i * LANES, LANES), LANES)
        turned = grads[:, lanes].T
        g_queries, g_keys = [], []
        for side in range(2):
            h = 2 * i + side
            query = queries[pl.ds(pl.multiple_of(h * size, size), size), :]
            g_context = turned[side * size : (side + 1) * size]
            first = first_map(land_k[h], query)
            g_first = nn(land_out[h], g_context)
            inner = jnp.sum(g_first * first, axis=0, keepdims=True)
            g_scores = (first * (g_first - inner)).astype(BF16)
            g_land = nt(first.astype(BF16), g_context)
            g_key = nt(g_scores, query)
            by_owner(place, h, owners, kept, sent, jnp.concatenate([g_land, g_key], axis=1))
            g_keys.append(g_key)
            g_queries.append((scaled * nn(land_k[h].T, g_scores)).astype(BF16))
        g_query[:, lanes] = jnp.concatenate(g_queries, axis=0).T
        g_lk[:, lanes] = jnp.concatenate(g_keys, axis=1)
        return 0

    lax.fori_loop(0, heads // 2, pair, 0)


def attention_back(place, queries, grads, land_k, land_out, owners):
    width, rows = queries.shape
    heads = land_k.shape[0]
    return pl.pallas_call(
        attention_back_kernel,
        out_shape=owner_parts(heads, owners)
        + (
            jax.ShapeDtypeStruct((LANDMARKS, width), F32),
            jax.ShapeDtypeStruct((rows, width), BF16),
        ),
        in_specs=[SCALARS] + whole(4),
        out_specs=tuple(whole(4)),
        compiler_params=PARAMS,
        cost_estimate=lasting(11.4),
        name="attention_back",
    )(place, queries, grads, land_k, land_out)


def conv_back_kernel(
    v_plain, v_left, v_right, grads, g_left, g_right, base_back, g_value, g_taps, ends
):
    heads = g_taps.shape[0]
    rows, width = grads.shape
    size = width // heads
    blocks_in = rows // LANES
    row = lax.broadcasted_iota(jnp.int32, (LANES, LANES), 0)
    column = lax.broadcasted_iota(jnp.int32, (LANES, LANES), 1)
    reverse = jnp.where(row + column == LANES - 1, 1.0, 0.0).astype(BF16)
    gap = jnp.concatenate([row - column, row - column], axis=1)
    ends[0] = g_left[...].T
    ends[1] = g_right[...].T

    def pair(i, _):
        lanes = pl.ds(pl.multiple_of(i * LANES, LANES), LANES)
        turned = grads[:, lanes].T
        plain = [v_left[LANES - 16 :, lanes]]
        plain += [v_plain[b * LANES : (b + 1) * LANES, lanes] for b in range(blocks_in)]
        plain += [v_right[:16, lanes]]
        for side in range(2):
            h = 2 * i + side
            at = pl.ds(pl.multiple_of(h * size, size), size)
            g_context = turned[side * size : (side + 1) * size]
            blocks = [ends[0, at, :]]
            blocks += [g_context[:, b * LANES : (b + 1) * LANES] for b in range(blocks_in)]
            blocks += [ends[1, at, :]]
            g_value[at, :] = convolved(blocks, band(base_back[pl.ds(h, 1), :]))

        def around(b):
            prior = plain[0] if b == 0 else plain[b][LANES - 16 :]
            return jnp.concatenate([prior, plain[b + 1], plain[b + 2][:16]], axis=0)

        def by_head(b):
            piece = turned[:, b * LANES : (b + 1) * LANES]
            zero = jnp.zeros_like(piece)
            return jnp.concatenate(
                [jnp.where(row < size, piece, zero), jnp.where(row >= size, piece, zero)], axis=1
            )

        total = jnp.zeros((LANES + 32, 2 * LANES), F32)
        for b in range(0, blocks_in, 2):
            total = total + nn(
                jnp.concatenate([around(b), around(b + 1)], axis=1),
                jnp.concatenate([by_head(b), by_head(b + 1)], axis=0),
            )
        empty = jnp.zeros((LANES - 16, 2 * LANES), F32)
        before, here, after = total[:16], total[16 : 16 + LANES], total[16 + LANES :]
        ring = jnp.where(jnp.abs(gap) <= 16, here, 0.0)
        ring = ring + jnp.where(gap >= LANES - 16, jnp.concatenate([empty, before], axis=0), 0.0)
        ring = ring + jnp.where(gap <= 16 - LANES, jnp.concatenate([after, empty], axis=0), 0.0)
        high, low = split(ring)
        lowest = (ring - high.astype(F32) - low.astype(F32)).astype(BF16)
        flat = nn(reverse, high) + nn(reverse, low) + nn(reverse, lowest)
        for side in range(2):
            straight = pltpu.roll(
                flat[:, side * LANES : (side + 1) * LANES], 0, 1, stride=1, stride_axis=0
            )
            g_taps[pl.ds(2 * i + side, 1), :] = jnp.sum(straight, axis=0, keepdims=True)
        return 0

    lax.fori_loop(0, heads // 2, pair, 0)


def conv_back(v_plain, v_ends, grads, g_ends, base_back):
    rows, width = grads.shape
    heads = base_back.shape[0]
    return pl.pallas_call(
        conv_back_kernel,
        out_shape=(
            jax.ShapeDtypeStruct((width, rows), F32),
            jax.ShapeDtypeStruct((heads, LANES), F32),
        ),
        in_specs=whole(7),
        out_specs=tuple(whole(2)),
        scratch_shapes=[pltpu.VMEM((2, width, LANES), BF16)],
        compiler_params=PARAMS,
        cost_estimate=lasting(13.6),
        name="conv_back",
    )(v_plain, *v_ends, grads, *g_ends, base_back)


def third_back_kernel(
    place, keys, values, land_q, spread, g_conv, lq_mid, lk_mid, g_lk, last, first, taps, turned,
    g_k, g_v, sums, kept, sent,
):
    heads, _, size = land_q.shape
    rows, width = g_k.shape
    own_heads = lq_mid.shape[0]
    scale = 64**-0.25
    sums[LANDMARKS:, :] = jnp.zeros((sums.shape[0] - LANDMARKS, 2 * width), F32)
    sums[LANDMARKS : LANDMARKS + 1, :] = last[...]
    sums[LANDMARKS + 1 : LANDMARKS + 2, :] = first[...]
    for h in range(heads):
        sums[LANDMARKS + 2 : LANDMARKS + 3, h * LANES : (h + 1) * LANES] = taps[h : h + 1, :]

    def mid(part, h):
        at = h - place[3] * own_heads
        mine = (at >= 0) & (at < own_heads) & (place[5] == 0)
        inside = jnp.clip(at, 0, own_heads - 1)
        return jnp.where(mine, part[inside], 0.0)

    live = live_lanes(place, rows)
    live_row = jnp.where(live, 1.0, 0.0)
    scaled_row = live_row * 64**-0.25

    def pair(i, _):
        lanes = pl.ds(pl.multiple_of(i * LANES, LANES), LANES)
        g_keys, g_values, g_lqs, lks = [], [], [], []
        for side in range(2):
            h = 2 * i + side
            at = pl.ds(pl.multiple_of(h * size, size), size)
            key, value = keys[at, :], values[at, :]
            pack = spread[h]
            g_mixed = pack[:, :size]
            row_dot = pack[:, size : size + 1]
            top = pack[:, size + 1 : size + 2]
            total = pack[:, size + 2 : size + 3]
            scores = nn(land_q[h], key)
            third = jnp.where(live, jnp.exp(scores - top), 0.0) * (1.0 / total)
            gm_high, gm_low = split(g_mixed)
            g_third = nn(gm_high, value) + nn(gm_low, value)
            g_high, g_low = split(third * (g_third - row_dot))
            g_lqs.append(nt(g_high, key) + nt(g_low, key) + mid(lq_mid, h))
            lks.append(mid(lk_mid, h))
            turned = land_q[h].T
            g_key = nn(turned, g_high) + nn(turned, g_low)
            g_keys.append((scaled_row * g_key).astype(BF16))
            t_high, t_low = split(third)
            gmt_high, gmt_low = split(g_mixed.T)
            g_value = nn(gmt_high, t_high) + nn(gmt_high, t_low) + nn(gmt_low, t_high)
            g_values.append((live_row * (g_value + g_conv[at, :])).astype(BF16))
        g_k[:, lanes] = jnp.concatenate(g_keys, axis=0).T
        g_v[:, lanes] = jnp.concatenate(g_values, axis=0).T
        sums[:LANDMARKS, lanes] = scale * jnp.concatenate(g_lqs, axis=1)
        key_lanes = pl.ds(pl.multiple_of(width + i * LANES, LANES), LANES)
        sums[:LANDMARKS, key_lanes] = scale * (g_lk[:, lanes] + jnp.concatenate(lks, axis=1))
        return 0

    lax.fori_loop(0, heads // 2, pair, 0)
    for number, cells in enumerate((g_k, g_v)):
        family_grads(turned, cells, place[2] == number, kept, sent)


def third_back(
    place, keys, values, land_q, spread, g_conv, lq_mid, lk_mid, g_lk, last, first, taps, turned, halves
):
    width, rows = keys.shape
    plain = jax.ShapeDtypeStruct((rows, width), BF16)
    return pl.pallas_call(
        third_back_kernel,
        out_shape=(plain, plain, jax.ShapeDtypeStruct((LANDMARKS + 8, 2 * width), F32))
        + (jax.ShapeDtypeStruct((halves, width, width // halves), BF16),) * 2,
        in_specs=[SCALARS] + whole(12),
        out_specs=tuple(whole(5)),
        compiler_params=PARAMS,
        cost_estimate=lasting(17),
        name="third_back",
    )(
        place, keys, values, land_q, spread, g_conv, lq_mid, lk_mid, g_lk, last, first, taps, turned
    )


def centred_rows(rows):
    centred = rows - jnp.mean(rows, axis=1, keepdims=True)
    scale = lax.rsqrt(jnp.mean(centred * centred, axis=1, keepdims=True) + 1e-05)
    return centred * scale, scale


def norm_back(grads, gain, unit, scale):
    scaled = grads * gain
    inner = jnp.mean(scaled * unit, axis=1, keepdims=True)
    return scale * (scaled - jnp.mean(scaled, axis=1, keepdims=True) - unit * inner)


def gelu_pair(hidden):
    share = 0.5 * (1.0 + lax.erf(hidden * 0.7071067811865476))
    density = jnp.exp(-0.5 * hidden * hidden) * 0.3989422804014327
    return hidden * share, share + hidden * density


class Copies:
    def __init__(self, sems):
        self.sems, self.used, self.open = sems, 0, []

    def start(self, source, target):
        copy = pltpu.make_async_copy(source, target, self.sems.at[self.used])
        self.used += 1
        copy.start()
        return copy

    def out(self, source, target):
        self.open.append(self.start(source, target))

    def finish(self):
        for copy in self.open:
            copy.wait()


def weight_grad(turned, cells, halves, which, out):
    ff = cells.shape[1] // halves
    columns = ff // 2
    for half in range(halves):
        from_column = pl.ds(pl.multiple_of(half * ff + which * columns, columns), columns)

        def rows_of(i, at, half=half, from_column=from_column):
            out[half, at, :] = nn(turned[at, :], cells[:, from_column]).astype(BF16)

        each_tile(turned.shape[0], 384, rows_of)


def feed_kernel(
    place, first_in, conv_in, land_out, tokens_in, cotangent_in, weights,
    output_to, context_to, slope_to, g_fed_to, g_second_to, unit_to, scale_to, turned_to, active_to, fed_turned_to, sent_to,
    norm_grads, in_w, down_w, out_w, norms, conv, context, tokens, cotangent,
    low, unit, scales, fed, active, slopes, g_fed, g_fed_turned, normed_turned, output, sent,
    sems,
):
    rows, width = tokens.shape
    halves, _, ff = in_w.shape
    part = out_w.shape[2]
    tile = 256
    copies = Copies(sems)
    context_copies = [copies.start(first_in, g_fed_turned), copies.start(conv_in, conv)]
    early = [
        copies.start(weights.at[:, :, pl.ds(2 * ff, part)], out_w),
        copies.start(tokens_in, tokens),
        copies.start(weights.at[:, :, pl.ds(2 * ff + part, LANES)], norms),
    ]
    in_copy = copies.start(weights.at[:, :, pl.ds(0, ff)], in_w)
    down_copy = copies.start(weights.at[:, :, pl.ds(ff, ff)], down_w)
    cotangent_copy = copies.start(cotangent_in, cotangent)
    for copy in context_copies:
        copy.wait()
    context_rows(g_fed_turned, conv, land_out, context)
    copies.out(context, context_to)
    for copy in early:
        copy.wait()
    columns = norms[0].astype(F32).T
    gain0, gain1 = columns[0:1], columns[1:2]
    shift0, shift1 = columns[2:3], columns[3:4]
    norm_grads[...] = jnp.zeros_like(norm_grads)

    def project(i, at):
        attended = nt(context[at, :part], out_w[0])
        for half in range(1, halves):
            attended = attended + nt(context[at, half * part : (half + 1) * part], out_w[half])
        rows_unit, scale = centred_rows(tokens[at, :].astype(F32) + attended)
        unit[at, :] = rows_unit
        scales[at, :] = jnp.broadcast_to(scale, (tile, LANES))
        normed = (rows_unit * gain0 + shift0).astype(BF16)
        low[at, :] = normed
        normed_turned[:, at] = normed.T

    each_tile(rows, tile, project)
    copies.out(unit, unit_to)
    copies.out(scales, scale_to)
    copies.out(normed_turned, turned_to)
    in_copy.wait()
    big = 512

    def hidden_rows(i, at):
        for half in range(halves):
            value, slope = gelu_pair(nn(low[at, :], in_w[half]))
            active[at, half * ff : (half + 1) * ff] = value.astype(BF16)
            slopes[at, half * ff : (half + 1) * ff] = slope.astype(BF16)

    each_tile(rows, tile, hidden_rows)
    copies.out(slopes, slope_to)
    copies.out(active, active_to)
    down_copy.wait()

    def fed_rows(i, at):
        total = nt(active[at, :ff], down_w[0])
        for half in range(1, halves):
            total = total + nt(active[at, half * ff : (half + 1) * ff], down_w[half])
        fed[at, :] = total

    each_tile(rows, big, fed_rows)
    cotangent_copy.wait()

    def second_norm(i, at):
        normed = unit[at, :] * gain0 + shift0
        unit1, scale1 = centred_rows(normed + fed[at, :])
        position = place[0] + i * tile + lax.broadcasted_iota(jnp.int32, (tile, 1), 0)
        live = jnp.where(position < place[1], 1.0, 0.0)
        output[at, :] = (live * (unit1 * gain1 + shift1)).astype(BF16)
        grads = live * cotangent[at, :].astype(F32)
        norm_grads[:, :width] += jnp.sum(grads * unit1, axis=0, keepdims=True)
        norm_grads[:, width:] += jnp.sum(grads, axis=0, keepdims=True)
        second = norm_back(grads, gain1, unit1, scale1)
        fed[at, :] = second
        g_low = second.astype(BF16)
        g_fed[at, :] = g_low
        g_fed_turned[:, at] = g_low.T

    each_tile(rows, tile, second_norm)
    copies.out(output, output_to)
    copies.out(fed, g_second_to)
    copies.out(g_fed, g_fed_to)
    copies.out(g_fed_turned, fed_turned_to)
    weight_grad(g_fed_turned, active, halves, 1 - place[2], sent)
    copies.out(sent, sent_to)
    copies.finish()


ANYWHERE = pl.BlockSpec(memory_space=pl.ANY)


def feed_forward(place, first, conv, land_out, tokens, cotangent, weights, ff, part):
    rows, width = tokens.shape
    halves = weights.shape[0]
    grad = (halves, width, ff // 2)
    shapes = [
        ((rows, width), BF16), ((rows, width), BF16), ((rows, halves * ff), BF16),
        ((rows, width), BF16), ((rows, width), F32), ((rows, width), F32), ((rows, LANES), F32), ((width, rows), BF16),
        ((rows, halves * ff), BF16), ((width, rows), BF16), (grad, BF16), ((1, 2 * width), F32),
    ]
    scratch = [
        ((halves, width, ff), BF16), ((halves, width, ff), BF16), ((halves, width, part), BF16),
        ((halves, width, LANES), BF16), ((width, rows), F32), ((rows, width), BF16),
        ((rows, width), BF16), ((rows, width), BF16),
        ((rows, width), BF16), ((rows, width), F32), ((rows, LANES), F32), ((rows, width), F32),
        ((rows, halves * ff), BF16), ((rows, halves * ff), BF16), ((rows, width), BF16),
        ((width, rows), BF16), ((width, rows), BF16), ((rows, width), BF16), (grad, BF16),
    ]
    return pl.pallas_call(
        feed_kernel,
        out_shape=tuple(jax.ShapeDtypeStruct(*shape) for shape in shapes),
        in_specs=[SCALARS] + [ANYWHERE] * 2 + whole(1) + [ANYWHERE] * 3,
        out_specs=tuple([ANYWHERE] * 11 + whole(1)),
        scratch_shapes=[pltpu.VMEM(*shape) for shape in scratch]
        + [pltpu.SemaphoreType.DMA((19,))],
        compiler_params=PARAMS,
        cost_estimate=lasting(32),
        name="feed_forward",
    )(place, first, conv, land_out, tokens, cotangent, weights)


def feed_back_kernel(
    place, slope_in, g_fed_in, g_second_in, unit_in, scale_in, turned_in, weights,
    g_first_to, g_context_to, g_hidden_to, sent_to, att_turned_to, norm_grads,
    in_w, down_w, out_w, norms, g_hidden, g_fed, second, unit, scales, normed_turned,
    g_att, g_att_turned, g_context, sent,
    sems,
):
    rows, width = second.shape
    halves, _, ff = in_w.shape
    part = out_w.shape[2]
    tile = 256
    copies = Copies(sems)
    early = [
        copies.start(g_fed_in, g_fed),
        copies.start(weights.at[:, :, pl.ds(ff, ff)], down_w),
        copies.start(slope_in, g_hidden),
    ]
    later = [
        copies.start(turned_in, normed_turned),
        copies.start(weights.at[:, :, pl.ds(0, ff)], in_w),
        copies.start(g_second_in, second),
        copies.start(unit_in, unit),
        copies.start(scale_in, scales),
        copies.start(weights.at[:, :, pl.ds(2 * ff + part, LANES)], norms),
        copies.start(weights.at[:, :, pl.ds(2 * ff, part)], out_w),
    ]
    for copy in early:
        copy.wait()
    norm_grads[...] = jnp.zeros_like(norm_grads)
    big = 512

    def back_rows(i, at):
        for half in range(halves):
            g_act = nn(g_fed[at, :], down_w[half])
            to = slice(half * ff, (half + 1) * ff)
            g_hidden[at, to] = (g_act * g_hidden[at, to].astype(F32)).astype(BF16)

    each_tile(rows, big, back_rows)
    copies.out(g_hidden, g_hidden_to)
    later.pop(0).wait()
    weight_grad(normed_turned, g_hidden, halves, 1 - place[2], sent)
    copies.out(sent, sent_to)
    for copy in later:
        copy.wait()
    gain0 = norms[0].astype(F32).T[0:1]

    def normed_rows(i, at):
        total = second[at, :]
        for half in range(halves):
            total = total + nt(g_hidden[at, half * ff : (half + 1) * ff], in_w[half])
        second[at, :] = total

    each_tile(rows, big, normed_rows)

    def first_norm(i, at):
        grads = second[at, :]
        rows_unit, scale = unit[at, :], scales[at, 0:1]
        norm_grads[:, :width] += jnp.sum(grads * rows_unit, axis=0, keepdims=True)
        norm_grads[:, width:] += jnp.sum(grads, axis=0, keepdims=True)
        first = norm_back(grads, gain0, rows_unit, scale)
        second[at, :] = first
        low = first.astype(BF16)
        g_att[at, :] = low
        g_att_turned[:, at] = low.T

    each_tile(rows, tile, first_norm)
    copies.out(second, g_first_to)
    copies.out(g_att_turned, att_turned_to)
    for half in range(halves):
        g_context[:, half * part : (half + 1) * part] = nn(g_att[...], out_w[half]).astype(BF16)
    copies.out(g_context, g_context_to)
    copies.finish()


def feed_backward(place, fed, weights, ff, part):
    rows, width = fed[1].shape
    halves = weights.shape[0]
    grad = (halves, width, ff // 2)
    shapes = [
        ((rows, width), F32), ((rows, width), BF16), ((rows, halves * ff), BF16), (grad, BF16),
        ((width, rows), BF16), ((1, 2 * width), F32),
    ]
    scratch = [
        ((halves, width, ff), BF16), ((halves, width, ff), BF16), ((halves, width, part), BF16),
        ((halves, width, LANES), BF16), ((rows, halves * ff), BF16), ((rows, width), BF16),
        ((rows, width), F32), ((rows, width), F32),
        ((rows, LANES), F32), ((width, rows), BF16),
        ((rows, width), BF16), ((width, rows), BF16), ((rows, width), BF16), (grad, BF16),
    ]
    return pl.pallas_call(
        feed_back_kernel,
        out_shape=tuple(jax.ShapeDtypeStruct(*shape) for shape in shapes),
        in_specs=[SCALARS] + [ANYWHERE] * 7,
        out_specs=tuple([ANYWHERE] * 5 + whole(1)),
        scratch_shapes=[pltpu.VMEM(*shape) for shape in scratch]
        + [pltpu.SemaphoreType.DMA((16,))],
        compiler_params=PARAMS,
        cost_estimate=lasting(27),
        name="feed_backward",
    )(place, *fed, weights)


def kept_kernel(place, turned_in, cells_in, kept, turned, cells, sems):
    halves, width, columns = kept.shape
    ff = 2 * columns
    copies = Copies(sems)
    turned_copy = copies.start(turned_in, turned)
    pieces = []
    for half in range(halves):
        start = pl.multiple_of(half * ff + place[2] * columns, columns)
        pieces.append(copies.start(cells_in.at[:, pl.ds(start, columns)], cells.at[half]))
    turned_copy.wait()
    for half in range(halves):
        pieces[half].wait()

        def rows_of(i, at, half=half):
            kept[half, at, :] = nn(turned[at, :], cells[half]).astype(BF16)

        each_tile(width, 384, rows_of)


def kept_grad(place, turned, cells, halves):
    width, rows = turned.shape
    columns = cells.shape[1] // halves // 2
    return pl.pallas_call(
        kept_kernel,
        out_shape=jax.ShapeDtypeStruct((halves, width, columns), BF16),
        in_specs=[SCALARS] + [ANYWHERE] * 2,
        out_specs=whole(1)[0],
        scratch_shapes=[
            pltpu.VMEM((width, rows), BF16),
            pltpu.VMEM((halves, rows, columns), BF16),
            pltpu.SemaphoreType.DMA((3,)),
        ],
        compiler_params=PARAMS,
        cost_estimate=lasting(5),
        name="kept_grad",
    )(place, turned, cells)


def spread_kernel(place, turned_in, cells_in, other, kept, sent, turned, cells, sems):
    halves, width, columns = other.shape
    ff = 2 * columns
    quarter = columns // 2
    copies = Copies(sems)
    turned_copy = copies.start(turned_in, turned)
    pieces = []
    for half in range(halves):
        start = pl.multiple_of(half * ff + place[2] * columns, columns)
        pieces.append(copies.start(cells_in.at[:, pl.ds(start, columns)], cells.at[half]))
    turned_copy.wait()
    for half in range(halves):
        pieces[half].wait()

        def rows_of(i, at, half=half):
            total = nn(turned[at, :], cells[half]) + other[half, at, :].astype(F32)
            low = total.astype(BF16)
            first = place[4] == 0
            kept[half, at, :] = jnp.where(first, low[:, :quarter], low[:, quarter:])
            sent[half, at, :] = jnp.where(first, low[:, quarter:], low[:, :quarter])

        each_tile(width, 384, rows_of)


def spread_grad(place, turned, cells, other):
    halves, width, columns = other.shape
    rows = turned.shape[1]
    part = jax.ShapeDtypeStruct((halves, width, columns // 2), BF16)
    return pl.pallas_call(
        spread_kernel,
        out_shape=(part, part),
        in_specs=[SCALARS] + [ANYWHERE] * 2 + whole(1),
        out_specs=tuple(whole(2)),
        scratch_shapes=[
            pltpu.VMEM((width, rows), BF16),
            pltpu.VMEM((halves, rows, columns), BF16),
            pltpu.SemaphoreType.DMA((3,)),
        ],
        compiler_params=PARAMS,
        cost_estimate=lasting(6),
        name="spread_grad",
    )(place, turned, cells, other)


def pair_kernel(
    place, one_turned_in, one_cells_in, two_turned_in, two_cells_in, kept, sent,
    one_turned, one_cells, two_turned, two_cells, sems,
):
    copies = Copies(sems)
    loads = [
        copies.start(*pair)
        for pair in (
            (one_turned_in, one_turned), (one_cells_in, one_cells),
            (two_turned_in, two_turned), (two_cells_in, two_cells),
        )
    ]
    for number, (turned, cells) in enumerate(((one_turned, one_cells), (two_turned, two_cells))):
        loads[2 * number].wait()
        loads[2 * number + 1].wait()
        family_grads(turned, cells, place[2] == number, kept, sent)


def pair_grads(place, one_turned, one_cells, two_turned, two_cells, halves):
    width, rows = one_turned.shape
    shape = jax.ShapeDtypeStruct((halves, width, one_cells.shape[1] // halves), BF16)
    return pl.pallas_call(
        pair_kernel,
        out_shape=(shape, shape),
        in_specs=[SCALARS] + [ANYWHERE] * 4,
        out_specs=tuple(whole(2)),
        scratch_shapes=[
            pltpu.VMEM((width, rows), BF16), pltpu.VMEM(one_cells.shape, BF16),
            pltpu.VMEM((width, rows), BF16), pltpu.VMEM(one_cells.shape, BF16),
            pltpu.SemaphoreType.DMA((4,)),
        ],
        compiler_params=PARAMS,
        cost_estimate=lasting(6),
        name="pair_grads",
    )(place, one_turned, one_cells, two_turned, two_cells)


def rank_kernel(place, mine, got, land_tokens, weights, late, through, small):
    halves, width, _ = weights.shape
    part = late.shape[1] // 2
    first = place[2] == 0
    grads = (
        jnp.where(first, mine[:LANDMARKS], got[:LANDMARKS]),
        jnp.where(first, got[:LANDMARKS], mine[:LANDMARKS]),
    )
    counts = landmark_counts(place)
    total = jnp.zeros((2 * LANDMARKS, width), F32)
    for index, grad in enumerate(grads):
        both = jnp.concatenate(split(grad / counts), axis=0)
        for half in range(halves):
            weight = weights[half, :, index * part : (index + 1) * part]
            total = total + nt(both[:, half * part : (half + 1) * part], weight)
    through[...] = jnp.concatenate(split(total[:LANDMARKS] + total[LANDMARKS:]), axis=0)
    zero = jnp.zeros((LANDMARKS, part), F32)
    own = []
    for index, grad in enumerate(grads):
        columns = grad[:, :part]
        for half in range(1, halves):
            columns = jnp.where(place[5] == half, grad[:, half * part : (half + 1) * part], columns)
        own.append(jnp.where(place[2] == 1 - index, columns, zero))
    high, low = split(jnp.concatenate(own, axis=1))
    mean_high, mean_low = split(land_tokens[...] / counts)
    means = jnp.concatenate([mean_high, mean_low, mean_high, jnp.zeros_like(mean_low)], axis=0).T
    factors = jnp.concatenate([high, high, low, jnp.zeros_like(low)], axis=0)
    late[...] = nn(means, factors).astype(BF16)
    gains = jnp.where(first, mine[LANDMARKS:], got[LANDMARKS:])
    shifts = jnp.where(first, got[LANDMARKS:], mine[LANDMARKS:])
    taps = jnp.where(place[5] == 0, gains[2:3], shifts[2:3])
    rows = [gains[1:2], gains[0:1], shifts[1:2], shifts[0:1], taps]
    rows.append(jnp.zeros((small.shape[0] - len(rows), width), F32))
    small[...] = jnp.concatenate(rows, axis=0).astype(BF16)


def rank_parts(place, mine, got, land_tokens, weights):
    halves, width, packed = weights.shape
    return pl.pallas_call(
        rank_kernel,
        out_shape=(
            jax.ShapeDtypeStruct((width, 2 * packed // 3), BF16),
            jax.ShapeDtypeStruct((2 * LANDMARKS, width), BF16),
            jax.ShapeDtypeStruct((16, width), BF16),
        ),
        in_specs=[SCALARS] + whole(4),
        out_specs=tuple(whole(3)),
        compiler_params=PARAMS,
        cost_estimate=lasting(4),
        name="rank_parts",
    )(place, mine, got, land_tokens, weights)


def flipped(values, axis, bit):
    count = lax.axis_size(axis)
    return lax.ppermute(values, axis, [(i, i ^ bit) for i in range(count)])


def side_of(axis, bit):
    return (lax.axis_index(axis) // bit) % 2


def paired(mine, axis, bit, dim):
    other = flipped(mine, axis, bit)
    both = jnp.zeros(mine.shape[:dim] + (2,) + mine.shape[dim:], mine.dtype)
    side = side_of(axis, bit)
    both = lax.dynamic_update_slice_in_dim(both, jnp.expand_dims(mine, dim), side, dim)
    return lax.dynamic_update_slice_in_dim(both, jnp.expand_dims(other, dim), 1 - side, dim)


def ctx_bits():
    bits, bit = [], 1
    while bit < lax.axis_size("ctx"):
        bits.append(bit)
        bit *= 2
    return bits


def sequence_start(values):
    width = values.shape[1] // 2
    side = side_of("ctx", 1)
    kept = lax.dynamic_slice_in_dim(values, side * width, width, axis=1)
    sent = lax.dynamic_slice_in_dim(values, (1 - side) * width, width, axis=1)
    kept = kept + flipped(sent, "ctx", 1)
    return kept + flipped(kept, "tp", 1)


def sequence_end(kept):
    for bit in ctx_bits()[1:]:
        kept = kept + flipped(kept, "ctx", bit)
    return kept, flipped(kept, "ctx", 1)


def joined_halves(kept, other):
    return jnp.where(
        side_of("ctx", 1) == 0,
        jnp.concatenate([kept, other], axis=1),
        jnp.concatenate([other, kept], axis=1),
    )


def to_owner(kept, sent, combine):
    kept = combine(kept, flipped(sent, "ctx", 1))
    for bit in ctx_bits()[1:]:
        view = kept.reshape((-1, 2) + kept.shape[1:])
        side = side_of("ctx", bit)
        sent = lax.dynamic_index_in_dim(view, 1 - side, 1, False)
        kept = lax.dynamic_index_in_dim(view, side, 1, False)
        kept = combine(kept, flipped(sent, "ctx", bit))
    return kept[0], flipped(kept[0], "tp", 1)


def from_owners(part):
    whole_part = part[None]
    for bit in reversed(ctx_bits()):
        both = paired(whole_part, "ctx", bit, 1)
        whole_part = both.reshape((-1,) + part.shape)
    return whole_part.reshape((-1,) + part.shape[1:])


def merge_keys(one, two):
    size = LANES // 2
    one_top, two_top = one[..., size : size + 1], two[..., size : size + 1]
    top = jnp.maximum(one_top, two_top)
    one_factor, two_factor = jnp.exp(one_top - top), jnp.exp(two_top - top)
    summed = one * one_factor + two * two_factor
    lane = lax.broadcasted_iota(jnp.int32, summed.shape, summed.ndim - 1)
    return jnp.where(lane == size, top, summed)


def neighbour_rows(cells, count):
    pieces = lax.axis_size("ctx") * lax.axis_size("tp")
    up = [(i, i + 1) for i in range(pieces - 1)]
    before = lax.ppermute(cells[-count:], ("ctx", "tp"), up)
    after = lax.ppermute(cells[:count], ("ctx", "tp"), [(j, i) for i, j in up])
    return (
        jnp.pad(before, ((LANES - count, 0), (0, 0))),
        jnp.pad(after, ((0, LANES - count), (0, 0))),
    )


def own_quarter(shard):
    rows = shard.shape[0] // lax.axis_size("ctx")
    return lax.dynamic_slice_in_dim(shard, lax.axis_index("ctx") * rows, rows, axis=0)


def gathered(shard):
    full = lax.all_gather(own_quarter(shard), ("tp", "fsdp", "ctx"), tiled=True)
    return full.reshape(lax.axis_size("tp"), -1, shard.shape[1])


def gathered_early(shard):
    count = lax.axis_size("fsdp")
    piece = own_quarter(shard)
    if count > 4:
        held = lax.all_gather(piece, "fsdp")
    else:
        here = lax.axis_index("fsdp")
        held = jnp.zeros((count,) + piece.shape, piece.dtype)
        held = lax.dynamic_update_slice_in_dim(held, piece[None], here, 0)
        for step in range(1, count):
            moved = lax.ppermute(piece, "fsdp", [(i, (i + step) % count) for i in range(count)])
            held = lax.dynamic_update_slice_in_dim(held, moved[None], (here - step) % count, 0)
    bits = ctx_bits()
    halves = []
    for number, half in enumerate((held[: count // 2], held[count // 2 :])):
        half = half[None]
        if number == 0:
            half = paired(half[0], "tp", 1, 0)
        for place, bit in enumerate(reversed(bits[1:])):
            half = paired(half, "ctx", bit, 2 + place)
        if number == 1:
            half = paired(half[0], "tp", 1, 0)
        halves.append(paired(half, "ctx", bits[0], 1 + len(bits)))
    full = jnp.concatenate(halves, axis=1)
    return full.reshape(lax.axis_size("tp"), -1, shard.shape[1])


def bits_of(axis):
    bits, bit = [], lax.axis_size(axis) // 2
    while bit:
        bits.append(bit)
        bit //= 2
    return bits


def added(*parts):
    return sum(part.astype(F32) for part in parts).astype(BF16)


def cut(cells, axis, bit, dim):
    size = cells.shape[dim] // 2
    side = side_of(axis, bit)
    return (
        lax.dynamic_slice_in_dim(cells, side * size, size, axis=dim),
        lax.dynamic_slice_in_dim(cells, (1 - side) * size, size, axis=dim),
    )


def gate(*values):
    return lax.optimization_barrier(values)


def dotf(spec, *operands):
    return jnp.einsum(spec, *operands, preferred_element_type=F32)


def taps_round(taps):
    middle = taps.shape[1] // 2
    gap = jnp.zeros((taps.shape[0], LANES - taps.shape[1]), F32)
    return jnp.concatenate([taps[:, middle::-1], gap, taps[:, :middle:-1]], axis=1)


def landmark_bounds(length):
    landmark = jnp.arange(LANDMARKS + 1, dtype=jnp.int32)
    return (landmark * length + LANDMARKS - 1) // LANDMARKS


def landmark_counts_of(length):
    bounds = landmark_bounds(length)
    return (bounds[1:] - bounds[:-1]).astype(F32)[:, None]


def landmark_rows(position, length):
    bounds = landmark_bounds(length)
    inside = (position[:, None] >= bounds[None, :-1]) & (position[:, None] < bounds[None, 1:])
    return inside.astype(BF16)


def on_device(
    tokens,
    lengths,
    qk_weight,
    value_weight,
    out_weight,
    in_weight,
    down_weight,
    norm_gains,
    norm_shifts,
    conv_weight,
    cotangent,
):
    tp_count = lax.axis_size("tp")
    tp_index = lax.axis_index("tp")
    ctx_index = lax.axis_index("ctx")
    _, slot_len, model_width = tokens.shape
    rows = slot_len // tp_count
    local_heads, tap_count = conv_weight.shape
    local_width = value_weight.shape[1]
    ff_width = in_weight.shape[1]
    head_size = local_width // local_heads
    heads = local_heads * tp_count
    owners = lax.axis_size("ctx")
    own_heads = heads // owners
    width = local_width * tp_count
    radius = tap_count // 2
    length = lengths[0]

    first_row = (ctx_index * tp_count + tp_index) * rows
    sides = (side_of("ctx", 1), ctx_index, side_of("ctx", ctx_bits()[-1]), tp_index)
    place = jnp.stack([first_row, length, *sides]).astype(jnp.int32)

    norm_columns = jnp.concatenate([norm_gains, norm_shifts], axis=0).T
    norm_columns = jnp.pad(norm_columns, ((0, 0), (0, LANES - norm_columns.shape[1])))
    ffn_full = gathered(
        jnp.concatenate([in_weight, down_weight.T, out_weight.T, norm_columns], axis=1)
    )
    own_taps = jnp.where(ctx_index == 0, conv_weight.astype(F32), 0.0)
    tap_rows = jnp.pad(own_taps, ((0, 8 - local_heads), (0, LANES - tap_count)))
    tap_rows = jnp.where(
        jnp.arange(model_width) // LANES == tp_index,
        jnp.tile(tap_rows, (1, model_width // LANES)),
        0.0,
    )
    qkv_full = gathered_early(jnp.concatenate([qk_weight[0], qk_weight[1], value_weight], axis=1))
    own = lax.dynamic_slice_in_dim(tokens[0], tp_index * rows, rows, axis=0)
    land_tokens = sequence_start(jnp.concatenate([token_sums(place, own), tap_rows], axis=0))
    land_tokens = joined_halves(*sequence_end(land_tokens))
    own_cotangent = lax.dynamic_slice_in_dim(cotangent[0], tp_index * rows, rows, axis=0)
    tap_weights = land_tokens[LANDMARKS : LANDMARKS + local_heads, : tp_count * LANES]
    tap_weights = tap_weights.reshape(local_heads, tp_count, LANES).transpose(1, 0, 2)
    tap_weights = tap_weights.reshape(heads, LANES)[:, :tap_count]
    land_tokens = land_tokens[:LANDMARKS]
    base, base_back = taps_round(tap_weights), taps_round(tap_weights[:, ::-1])

    queries, keys, values, v_plain, land_q, land_k, own_turned, *parts_of_third = projections(
        place, own, land_tokens, qkv_full, head_size, owners
    )
    v_ends = neighbour_rows(v_plain, radius)
    merged, merged_tp = to_owner(*parts_of_third, merge_keys)
    kept_turns = inverse_forward(place, land_q, land_k, owners)
    first, conv = first_and_conv(queries, values, *v_ends, land_k, base)
    merged, own_out = landmark_out(merged, merged_tp, kept_turns[0])
    land_out = from_owners(own_out)

    own_output, context, *fed, active, fed_turned, down_sent, last_norm = feed_forward(
        place, first, conv, land_out, own, own_cotangent, ffn_full, ff_width, local_width
    )
    high = ctx_bits()[-1]
    owner_count = lax.axis_size("fsdp")
    owner_rows = model_width // owner_count
    near, *farther = bits_of("fsdp")[::-1]

    def by_owner_bits(cells):
        return cells.reshape((2,) * (1 + len(farther)) + (-1, cells.shape[-1]))

    def cut_last(cells, bit):
        dim = cells.ndim - 3
        return tuple(piece.squeeze(dim) for piece in cut(cells, "fsdp", bit, dim))

    other_output = flipped(own_output, "tp", 1)
    down_other = flipped(down_sent, "ctx", 1)
    down_kept = kept_grad(place, fed_turned, active, tp_count)
    down_kept, down_other = gate(down_kept, down_other)
    down_mine, down_theirs = cut(down_kept, "ctx", high, 2)
    other_mine, other_theirs = cut(down_other, "ctx", high, 2)
    down_sent = added(down_theirs, other_theirs)
    down_got = flipped(down_sent, "ctx", high)
    fed[0], down_sent = gate(fed[0], down_sent)
    grad_first_res, grad_context, g_hidden, in_sent, att_turned, first_norm = feed_backward(
        place, fed, ffn_full, ff_width, local_width
    )
    in_sent, grad_context, g_hidden, other_output, down_got = gate(
        in_sent, grad_context, g_hidden, other_output, down_got
    )
    in_other = flipped(in_sent, "ctx", 1)
    g_ends = neighbour_rows(grad_context, radius)
    down = added(down_mine, other_mine, down_got)
    down_mine, down_sent = cut(down, "tp", 1, 0)
    down_got = flipped(down_sent, "tp", 1)
    grad_context, down_sent = gate(grad_context, down_sent)
    land_kept, land_sent, g_lk, g_q = attention_back(
        place, queries, grad_context, land_k, land_out, owners
    )
    land_kept, land_sent, in_other, g_ends = gate(land_kept, land_sent, in_other, g_ends)

    land_other = flipped(land_sent, "ctx", 1)
    in_kept, in_sent = spread_grad(place, fed[5], g_hidden, in_other)
    in_kept, in_sent, land_other, down_got = gate(in_kept, in_sent, land_other, down_got)
    land_grads = land_kept + land_other
    land_mine, land_theirs = cut(land_grads, "ctx", high, 0)
    land_got = flipped(land_theirs, "ctx", high)
    land_theirs, in_sent = gate(land_theirs, in_sent)
    in_got = flipped(in_sent, "ctx", high)
    down = added(down_mine, down_got)
    grad_context, in_sent = gate(grad_context, in_sent)
    g_conv, g_taps = conv_back(v_plain, v_ends, grad_context, g_ends, base_back)
    g_conv, g_taps, land_got = gate(g_conv, g_taps, land_got)
    own_grads = (land_mine + land_got)[0]
    tp_grads = flipped(own_grads, "tp", 1)

    def parts(cells):
        return cells.reshape(rows, tp_count, local_width)

    def qkv_part(index):
        return qkv_full[:, :, index * local_width : (index + 1) * local_width]

    g_q, own_grads = gate(g_q, own_grads)
    mixed_kept, mixed_sent = pair_grads(place, att_turned, context, own_turned, g_q, tp_count)
    back_q = grad_first_res + dotf("tpk,pck->tc", parts(g_q), qkv_part(0))
    mixed_kept, mixed_sent, tp_grads, back_q = gate(mixed_kept, mixed_sent, tp_grads, back_q)
    mixed_got = flipped(mixed_sent, "ctx", 1)
    own_grads, mixed_sent = gate(own_grads + tp_grads, mixed_sent)
    spread, lq_mid, lk_mid = inverse_backward(
        place, land_q, land_k, merged, own_grads, *kept_turns
    )
    spread, in_got, mixed_got = gate(spread, in_got, mixed_got)
    spread = from_owners(spread)

    in_mine, in_sent = cut(added(in_kept, in_got), "tp", 1, 0)
    in_got = flipped(in_sent, "tp", 1)
    def by_ctx(cells):
        return cells.reshape(tp_count, owner_count, 2, -1, local_width)

    mixed = added(mixed_kept, mixed_got)
    mixed_mine, mixed_sent = cut(by_ctx(mixed), "ctx", high, 2)
    mixed_got = flipped(mixed_sent, "ctx", high)
    spread, in_sent, mixed_sent = gate(spread, in_sent, mixed_sent)
    g_k, g_v, sums, kv_kept, kv_sent = third_back(
        place, keys, values, land_q, spread, g_conv, lq_mid, lk_mid, g_lk, last_norm, first_norm,
        g_taps, own_turned, tp_count,
    )

    kv_kept, kv_sent, sums, in_got, mixed_got = gate(kv_kept, kv_sent, sums, in_got, mixed_got)
    kv_got = flipped(kv_sent, "ctx", 1)
    sums_mine, sums_sent = cut(sums, "ctx", 1, 1)
    sums_got = flipped(sums_sent, "ctx", 1)
    kv_kept, kv_got = gate(kv_kept, kv_got)
    kv_mine, kv_sent = cut(by_ctx(added(kv_kept, kv_got)), "ctx", high, 2)
    kv_sent, sums_mine, mixed_mine, in_mine, g_k = gate(
        kv_sent, sums_mine, mixed_mine, in_mine, g_k
    )
    kv_got = flipped(kv_sent, "ctx", high)
    sums = sums_mine + sums_got
    sums_got = flipped(sums, "tp", 1)
    mixed_mine, mixed_sent = cut(added(mixed_mine, mixed_got), "tp", 1, 0)
    sums, mixed_sent, in_mine = gate(sums, mixed_sent, in_mine)
    mixed_got = flipped(mixed_sent, "tp", 1)
    pair = jnp.concatenate([added(in_mine, in_got)[0], down[0]], axis=1)
    g_k, mixed_sent, pair = gate(g_k, mixed_sent, pair)
    pair = lax.psum_scatter(pair, "fsdp", scatter_dimension=0, tiled=True)
    back_k = back_q + dotf("tpk,pck->tc", parts(g_k), qkv_part(1))
    back_k, g_v, sums_got, mixed_got, kv_got = gate(back_k, g_v, sums_got, mixed_got, kv_got)
    sums = sums + sums_got
    sums_got = flipped(sums, "ctx", high)
    kv_mine, kv_sent = cut(added(kv_mine, kv_got), "tp", 1, 0)
    g_v, sums, kv_sent = gate(g_v, sums, kv_sent)
    kv_got = flipped(kv_sent, "tp", 1)
    own_grad = (back_k + dotf("tpk,pck->tc", parts(g_v), qkv_part(2))).astype(BF16)
    first_rows = 5 * rows // 16
    other_first = flipped(own_grad[:first_rows], "tp", 1)
    other_second = flipped(own_grad[first_rows:], "tp", 1)
    sums = sums + sums_got
    sums_got = flipped(sums, "ctx", 1)
    sums, sums_got, kv_got = gate(sums, sums_got, kv_got)
    late, through, small = rank_parts(place, sums, sums_got, land_tokens, qkv_full)
    late, through, small, other_first, own_output, other_output = gate(
        late, through, small, other_first, own_output, other_output
    )
    late = late.reshape(owner_count, 2, -1, 2 * local_width)
    late = lax.dynamic_index_in_dim(late, place[4], 1, False)
    mixed = added(
        jnp.concatenate([mixed_mine, kv_mine], axis=-1).reshape(late.shape),
        jnp.concatenate([mixed_got, kv_got], axis=-1).reshape(late.shape),
        late,
    )
    small = jnp.broadcast_to(small[None], (owner_count,) + small.shape)
    mixed = by_owner_bits(jnp.concatenate([mixed, small], axis=1))
    mixed_mine, mixed_sent = cut_last(mixed, near)
    mixed_sent, pair = gate(mixed_sent, pair)
    mixed_got = flipped(mixed_sent, "fsdp", near)
    mixed = added(mixed_mine, mixed_got)
    for bit in farther:
        mixed_mine, mixed_sent = cut_last(mixed, bit)
        mixed = added(mixed_mine, flipped(mixed_sent, "fsdp", bit))
    small = mixed[-16:].astype(F32)
    mixed = mixed[:-16]

    def of_core(cells, core):
        cells = cells.reshape((owners // 2, 2) + cells.shape[1:])
        return [cells[i, core] for i in range(owners // 2)]

    mixed, other_second = gate(mixed, other_second)
    mixed = from_owners(mixed[None])
    sides = [jnp.concatenate(of_core(mixed, core), axis=0).astype(F32) for core in range(2)]
    grad_out, grad_k = sides[0][:, :local_width].T, sides[0][:, local_width:]
    grad_q, grad_v = sides[1][:, :local_width], sides[1][:, local_width:]

    own_columns = lax.axis_index("fsdp") * owner_rows
    norm_sums = lax.dynamic_slice_in_dim(small[:4], own_columns, owner_rows, axis=1)
    taps_sum = small[4].reshape(local_heads, LANES)
    grad_taps = jnp.concatenate(
        [taps_sum[:, radius - 1 :: -1], taps_sum[:, : -radius - 2 : -1]], axis=1
    )

    columns = pair.shape[1] // 2
    pair = from_owners(pair[None])
    pieces = [piece for core in range(2) for piece in of_core(pair, core)]
    grad_in = jnp.concatenate([piece[:, :columns] for piece in pieces], axis=1).astype(F32)
    grad_down = jnp.concatenate([piece[:, columns:] for piece in pieces], axis=1).astype(F32).T

    output = jnp.where(
        tp_index == 0,
        jnp.concatenate([own_output, other_output]),
        jnp.concatenate([other_output, own_output]),
    )[None]
    both_grads = jnp.where(
        tp_index == 0,
        jnp.concatenate([own_grad, other_first, other_second]),
        jnp.concatenate([other_first, other_second, own_grad]),
    )
    position = ctx_index * slot_len + jnp.arange(slot_len, dtype=jnp.int32)
    onehot = landmark_rows(position, length)
    grad_tokens = both_grads.astype(F32) + dotf(
        "tm,mc->tc", jnp.concatenate([onehot, onehot], axis=1), through
    )
    grad_tokens = grad_tokens.reshape(1, slot_len, model_width)
    return (
        output,
        grad_tokens,
        jnp.stack([grad_q, grad_k]),
        grad_v,
        grad_out,
        grad_in,
        grad_down,
        norm_sums[:2],
        norm_sums[2:],
        grad_taps,
    )


def solution(mesh):
    in_specs = (
        P("fsdp", "ctx", None),
        P("fsdp"),
        P(None, "fsdp", "tp"),
        P("fsdp", "tp"),
        P("tp", "fsdp"),
        P("fsdp", "tp"),
        P("tp", "fsdp"),
        P(None, "fsdp"),
        P(None, "fsdp"),
        P("tp", None),
        P("fsdp", "ctx", None),
    )
    out_specs = (
        P("fsdp", "ctx", None),
        P("fsdp", "ctx", None),
        P(None, "fsdp", "tp"),
        P("fsdp", "tp"),
        P("tp", "fsdp"),
        P("fsdp", "tp"),
        P("tp", "fsdp"),
        P(None, "fsdp"),
        P(None, "fsdp"),
        P("tp", None),
    )
    return jax.shard_map(
        on_device, mesh=mesh, in_specs=in_specs, out_specs=out_specs, check_vma=False
    )
```

```python
import jax
import jax.numpy as jnp
from jax import lax
from jax.experimental import pallas as pl
from jax.experimental.pallas import tpu as pltpu
from jax.sharding import PartitionSpec as P

LANDMARKS = 64
NEWTON = 6
LANES = 128
VMEM_BYTES = 56 * 2**20

HIGH = lax.Precision.HIGHEST
F32 = jnp.float32
BF16 = jnp.bfloat16


def lasting(microseconds):
    return pl.CostEstimate(
        flops=int(microseconds * 1.1535e9), bytes_accessed=int(microseconds * 1e5), transcendentals=0
    )


def nn(left, right):
    return jnp.dot(left, right, preferred_element_type=F32)


def nt(left, right):
    return lax.dot_general(left, right, (((1,), (1,)), ((), ())), preferred_element_type=F32)


def split(wide):
    high = wide.astype(BF16)
    return high, (wide - high.astype(F32)).astype(BF16)


def each_tile(count, tile, body):
    def step(i, _):
        body(i, pl.ds(pl.multiple_of(i * tile, tile), tile))
        return 0

    lax.fori_loop(0, count // tile, step, 0)


def family_grads(turned, cells, mine, kept, sent):
    halves, width, columns = kept.shape

    def rows_of(i, at):
        total = nn(turned[at, :], cells[...]).astype(BF16)

        @pl.when(mine)
        def _():
            for half in range(halves):
                kept[half, at, :] = total[:, half * columns : (half + 1) * columns]

        @pl.when(jnp.logical_not(mine))
        def _():
            for half in range(halves):
                sent[half, at, :] = total[:, half * columns : (half + 1) * columns]

    each_tile(width, 384, rows_of)


def whole(count):
    return [pl.BlockSpec(memory_space=pltpu.VMEM)] * count


SCALARS = pl.BlockSpec(memory_space=pltpu.SMEM)
PARAMS = pltpu.CompilerParams(vmem_limit_bytes=VMEM_BYTES)


def landmark_onehot(place, rows, landmark_axis):
    shape = (LANDMARKS, rows) if landmark_axis == 0 else (rows, LANDMARKS)
    landmark = lax.broadcasted_iota(jnp.int32, shape, landmark_axis)
    position = place[0] + lax.broadcasted_iota(jnp.int32, shape, 1 - landmark_axis)
    start = lax.shift_right_logical(landmark * place[1] + (LANDMARKS - 1), 6)
    end = lax.shift_right_logical((landmark + 1) * place[1] + (LANDMARKS - 1), 6)
    return jnp.where((position >= start) & (position < end), 1.0, 0.0).astype(BF16)


def live_lanes(place, rows):
    position = place[0] + lax.broadcasted_iota(jnp.int32, (1, rows), 1)
    return position < place[1]


def band(base_row):
    ring = pltpu.roll(jnp.broadcast_to(base_row, (LANES, LANES)), 0, 1, stride=1, stride_axis=0)
    gap = lax.broadcasted_iota(jnp.int32, (LANES, LANES), 0) - lax.broadcasted_iota(
        jnp.int32, (LANES, LANES), 1
    )
    zero = jnp.zeros_like(ring)
    before = jnp.where(gap >= LANES - 16, ring, zero).astype(BF16)
    here = jnp.where(jnp.abs(gap) <= 16, ring, zero).astype(BF16)
    after = jnp.where(gap <= 16 - LANES, ring, zero).astype(BF16)
    return before, here, after


def convolved(blocks, bands):
    count = len(blocks) - 2
    size = blocks[0].shape[0]
    stacked = jnp.concatenate(
        [jnp.concatenate(blocks[i : i + 3], axis=1) for i in range(count)], axis=0
    )
    out = nn(stacked, jnp.concatenate(bands, axis=0))
    return jnp.concatenate([out[i * size : (i + 1) * size] for i in range(count)], axis=1)


def token_sums_kernel(place, tokens, sums):
    sums[...] = nn(landmark_onehot(place, tokens.shape[0], 0), tokens[...])


def token_sums(place, tokens):
    return pl.pallas_call(
        token_sums_kernel,
        out_shape=jax.ShapeDtypeStruct((LANDMARKS, tokens.shape[1]), F32),
        in_specs=[SCALARS] + whole(1),
        out_specs=whole(1)[0],
        compiler_params=PARAMS,
        cost_estimate=lasting(2.5),
        name="token_sums",
    )(place, tokens)


def landmark_counts(place):
    landmark = lax.broadcasted_iota(jnp.int32, (LANDMARKS, 1), 0)
    start = lax.shift_right_logical(landmark * place[1] + (LANDMARKS - 1), 6)
    end = lax.shift_right_logical((landmark + 1) * place[1] + (LANDMARKS - 1), 6)
    return (end - start).astype(F32)


def projection_kernel(
    place, tokens, sums, weights, q_out, k_out, v_out, v_plain, land_q, land_k, turned, kept, sent
):
    rows = tokens.shape[0]
    halves, _, packed = weights.shape
    width = packed // 3
    size = land_q.shape[2]
    position = place[0] + lax.broadcasted_iota(jnp.int32, (rows, 1), 0)
    live = jnp.where(position < place[1], 1.0, 0.0)
    scaled = live * 64**-0.25
    means = jnp.concatenate(split(sums[...] / landmark_counts(place)), axis=0)
    cells = tokens[...]
    turned[...] = cells.T
    for half in range(halves):
        for part, out in enumerate((q_out, k_out, v_out)):
            weight = weights[half, :, part * width : (part + 1) * width]
            low = ((live if part == 2 else scaled) * nn(cells, weight)).astype(BF16)
            out[half * width : (half + 1) * width, :] = low.T
            if part == 2:
                v_plain[:, half * width : (half + 1) * width] = low
                continue
            both = nn(means, weight)
            land = (64**-0.25 * (both[:LANDMARKS] + both[LANDMARKS:])).astype(BF16)
            to = land_k if part else land_q
            for head in range(width // size):
                to[half * (width // size) + head] = land[:, head * size : (head + 1) * size]
    third_heads(place, k_out, v_out, land_q, kept, sent)


def projections(place, tokens, sums, weights, size, owners):
    rows = tokens.shape[0]
    width = weights.shape[0] * weights.shape[2] // 3
    turned = jax.ShapeDtypeStruct((width, rows), BF16)
    land = jax.ShapeDtypeStruct((width // size, LANDMARKS, size), BF16)
    return pl.pallas_call(
        projection_kernel,
        out_shape=(turned, turned, turned, jax.ShapeDtypeStruct((rows, width), BF16), land, land)
        + (jax.ShapeDtypeStruct(tokens.shape[::-1], BF16),)
        + owner_parts(width // size, owners),
        in_specs=[SCALARS] + whole(3),
        out_specs=tuple(whole(9)),
        compiler_params=PARAMS,
        cost_estimate=lasting(18),
        name="projections",
    )(place, tokens, sums, weights)


def by_owner(place, h, owners, kept, sent, values):
    per = kept.shape[1]
    for owner in range(owners):
        @pl.when((h >= owner * per) & (h < (owner + 1) * per))
        def _(owner=owner):
            mine = place[2] == owner % 2

            @pl.when(mine)
            def _():
                kept[owner // 2, h - owner * per] = values

            @pl.when(jnp.logical_not(mine))
            def _():
                sent[owner // 2, h - owner * per] = values


def third_heads(place, keys, values, land_q, kept, sent):
    heads = land_q.shape[0]
    size = land_q.shape[2]
    rows = keys.shape[1]
    owners = 2 * kept.shape[0]
    live = live_lanes(place, rows)

    def head(h):
        at = pl.ds(pl.multiple_of(h * size, size), size)
        scores = jnp.where(live, nn(land_q[h], keys[at, :]), -1e30)
        top = jnp.max(scores, axis=1, keepdims=True)
        raised = jnp.where(live, jnp.exp(scores - top), 0.0)
        total = jnp.sum(raised, axis=1, keepdims=True)
        high, low = split(raised)
        value = values[at, :]
        mixed = nt(high, value) + nt(low, value)
        lane = lax.broadcasted_iota(jnp.int32, (LANDMARKS, LANES - size), 1)
        stats = jnp.where(lane == 0, top, jnp.where(lane == 1, total, 0.0))
        by_owner(place, h, owners, kept, sent, jnp.concatenate([mixed, stats], axis=1))

    def pair(i, _):
        head(2 * i)
        head(2 * i + 1)
        return 0

    lax.fori_loop(0, heads // 2, pair, 0)


def owner_parts(heads, owners):
    part = jax.ShapeDtypeStruct((owners // 2, heads // owners, LANDMARKS, LANES), F32)
    return part, part


def dot_high(left, right):
    return jnp.dot(left, right, preferred_element_type=F32, precision=HIGH)


def dot_high_nt(left, right):
    return lax.dot_general(
        left, right, (((1,), (1,)), ((), ())), preferred_element_type=F32, precision=HIGH
    )


def eye():
    row = lax.broadcasted_iota(jnp.int32, (LANDMARKS, LANDMARKS), 0)
    column = lax.broadcasted_iota(jnp.int32, (LANDMARKS, LANDMARKS), 1)
    return jnp.where(row == column, 1.0, 0.0)


def middle_map(land_q, land_k):
    scores = nt(land_q, land_k)
    raised = jnp.exp(scores - jnp.max(scores, axis=1, keepdims=True))
    return raised / jnp.sum(raised, axis=1, keepdims=True)


def inverse_kernel(place, land_q, land_k, kept_v, kept_p, kept_b, kept_c):
    heads = range(kept_v.shape[1])
    one = eye()
    own = [place[3] * len(heads) + h for h in heads]
    middle = [middle_map(land_q[h], land_k[h]) for h in own]
    approx = [m.T / jnp.sum(m * m, keepdims=True) for m in middle]
    for turn in range(NEWTON):
        product = [dot_high(middle[h], approx[h]) for h in heads]
        for h in heads:
            kept_v[turn, h] = approx[h]
            kept_p[turn, h] = product[h]
        bracket = [7.0 * one - p for p in product]
        bracket = [15.0 * one - dot_high(product[h], bracket[h]) for h in heads]
        for h in heads:
            kept_b[turn, h] = bracket[h]
        bracket = [13.0 * one - dot_high(product[h], bracket[h]) for h in heads]
        for h in heads:
            kept_c[turn, h] = bracket[h]
        approx = [0.25 * dot_high(approx[h], bracket[h]) for h in heads]
    for h in heads:
        kept_v[NEWTON, h] = approx[h]


def inverse_forward(place, land_q, land_k, owners):
    heads = land_q.shape[0] // owners
    square = (heads, LANDMARKS, LANDMARKS)
    return pl.pallas_call(
        inverse_kernel,
        out_shape=(
            jax.ShapeDtypeStruct((NEWTON + 1,) + square, F32),
            jax.ShapeDtypeStruct((NEWTON,) + square, F32),
            jax.ShapeDtypeStruct((NEWTON,) + square, F32),
            jax.ShapeDtypeStruct((NEWTON,) + square, F32),
        ),
        in_specs=[SCALARS] + whole(2),
        out_specs=tuple(whole(4)),
        compiler_params=PARAMS,
        cost_estimate=lasting(7),
        name="inverse_forward",
    )(place, land_q, land_k)


def merged_keys(one, two, size):
    one_top, two_top = one[:, size : size + 1], two[:, size : size + 1]
    top = jnp.maximum(one_top, two_top)
    summed = one * jnp.exp(one_top - top) + two * jnp.exp(two_top - top)
    lane = lax.broadcasted_iota(jnp.int32, one.shape, 1)
    return jnp.where(lane == size, top, summed)


def land_out_kernel(one, two, kept_v, merged, land_out):
    size = land_out.shape[2]
    for h in range(one.shape[0]):
        both = merged_keys(one[h], two[h], size)
        merged[h] = both
        mixed = both[:, :size] / both[:, size + 1 : size + 2]
        land_out[h] = dot_high(kept_v[NEWTON, h], mixed).astype(BF16)


def landmark_out(one, two, kept_v):
    heads = one.shape[0]
    return pl.pallas_call(
        land_out_kernel,
        out_shape=(
            jax.ShapeDtypeStruct(one.shape, F32),
            jax.ShapeDtypeStruct((heads, LANDMARKS, LANES // 2), BF16),
        ),
        in_specs=whole(3),
        out_specs=tuple(whole(2)),
        compiler_params=PARAMS,
        cost_estimate=lasting(2.2),
        name="landmark_out",
    )(one, two, kept_v)


def inverse_back_kernel(
    place, land_q, land_k, merged, grads, kept_v, kept_p, kept_b, kept_c, spread, g_lq, g_lk
):
    heads = range(grads.shape[0])
    size = land_q.shape[2]
    one = eye()
    own = [place[3] * len(heads) + h for h in heads]
    middle = [middle_map(land_q[h], land_k[h]) for h in own]
    turned = [m.T for m in middle]
    g_approx = []
    for h in heads:
        mixed = merged[h][:, :size] / merged[h][:, size + 1 : size + 2]
        g_land = grads[h][:, :size]
        g_approx.append(dot_high_nt(g_land, mixed))
        g_mixed = dot_high(kept_v[NEWTON, h].T, g_land)
        row_dot = jnp.sum(g_mixed * mixed, axis=1, keepdims=True)
        lane = lax.broadcasted_iota(jnp.int32, (LANDMARKS, LANES - size), 1)
        top = merged[h][:, size : size + 1]
        total = merged[h][:, size + 1 : size + 2]
        stats = jnp.where(
            lane == 0, row_dot, jnp.where(lane == 1, top, jnp.where(lane == 2, total, 0.0))
        )
        spread[h] = jnp.concatenate([g_mixed, stats], axis=1)
    g_middle = [jnp.zeros((LANDMARKS, LANDMARKS), F32) for _ in heads]
    for turn in reversed(range(NEWTON)):
        approx = [kept_v[turn, h] for h in heads]
        product = [kept_p[turn, h] for h in heads]
        first = [7.0 * one - p for p in product]
        second = [kept_b[turn, h] for h in heads]
        third = [kept_c[turn, h] for h in heads]
        g_third = [0.25 * dot_high(approx[h].T, g_approx[h]) for h in heads]
        g_back = [0.25 * dot_high_nt(g_approx[h], third[h]) for h in heads]
        g_product = [-dot_high_nt(g_third[h], second[h]) for h in heads]
        pt = [p.T for p in product]
        g_second = [-dot_high(pt[h], g_third[h]) for h in heads]
        g_product = [g_product[h] - dot_high_nt(g_second[h], first[h]) for h in heads]
        g_product = [g_product[h] + dot_high(pt[h], g_second[h]) for h in heads]
        g_middle = [g_middle[h] + dot_high_nt(g_product[h], approx[h]) for h in heads]
        g_approx = [g_back[h] + dot_high(turned[h], g_product[h]) for h in heads]
    for h in heads:
        m = middle[h]
        size_sum = jnp.sum(m * m, keepdims=True)
        g_size = -jnp.sum(g_approx[h] * turned[h], keepdims=True) / (size_sum * size_sum)
        g_m = g_middle[h] + g_approx[h].T / size_sum + 2.0 * g_size * m
        g_scores = m * (g_m - jnp.sum(g_m * m, axis=1, keepdims=True))
        g_lq[h] = dot_high(g_scores, land_k[own[h]].astype(F32))
        g_lk[h] = dot_high(g_scores.T, land_q[own[h]].astype(F32))


def inverse_backward(place, land_q, land_k, merged, grads, *kept):
    heads = grads.shape[0]
    square = jax.ShapeDtypeStruct((heads,) + land_q.shape[1:], F32)
    return pl.pallas_call(
        inverse_back_kernel,
        out_shape=(jax.ShapeDtypeStruct((heads, LANDMARKS, LANES), F32), square, square),
        in_specs=[SCALARS] + whole(8),
        out_specs=tuple(whole(3)),
        compiler_params=PARAMS,
        cost_estimate=lasting(11.5),
        name="inverse_backward",
    )(place, land_q, land_k, merged, grads, *kept)


def first_map(land_k, queries):
    scores = nn(land_k, queries)
    raised = jnp.exp(scores - jnp.max(scores, axis=0, keepdims=True))
    return raised * (1.0 / jnp.sum(raised, axis=0, keepdims=True))


def head_blocks(cells, ends, at):
    rows = cells.shape[1]
    left, right = ends
    return (
        [left[at, :]]
        + [cells[at, i * LANES : (i + 1) * LANES] for i in range(rows // LANES)]
        + [right[at, :]]
    )


def first_conv_kernel(queries, values, left, right, land_k, base, first, conv, ends):
    heads, _, size = land_k.shape
    ends[0] = left[...].T
    ends[1] = right[...].T

    def head(h):
        at = pl.ds(pl.multiple_of(h * size, size), size)
        first[at, :] = first_map(land_k[h], queries[at, :]).astype(BF16)
        blocks = head_blocks(values, (ends.at[0], ends.at[1]), at)
        conv[at, :] = convolved(blocks, band(base[pl.ds(h, 1), :]))

    def pair(i, _):
        head(2 * i)
        head(2 * i + 1)
        return 0

    lax.fori_loop(0, heads // 2, pair, 0)


def first_and_conv(queries, values, left, right, land_k, base):
    width, rows = queries.shape
    return pl.pallas_call(
        first_conv_kernel,
        out_shape=(
            jax.ShapeDtypeStruct((width, rows), BF16),
            jax.ShapeDtypeStruct((width, rows), F32),
        ),
        in_specs=whole(6),
        out_specs=tuple(whole(2)),
        scratch_shapes=[pltpu.VMEM((2, width, LANES), BF16)],
        compiler_params=PARAMS,
        cost_estimate=lasting(8),
        name="first_and_conv",
    )(queries, values, left, right, land_k, base)


def context_rows(first, conv, land_out, context):
    heads, _, size = land_out.shape

    def head(h):
        at = pl.ds(pl.multiple_of(h * size, size), size)
        return (nn(land_out[h].T, first[at, :]) + conv[at, :]).astype(BF16)

    def pair(i, _):
        both = jnp.concatenate([head(2 * i), head(2 * i + 1)], axis=0)
        context[:, pl.ds(pl.multiple_of(i * LANES, LANES), LANES)] = both.T
        return 0

    lax.fori_loop(0, heads // 2, pair, 0)


def attention_back_kernel(
    place, queries, grads, land_k, land_out, kept, sent, g_lk, g_query
):
    heads, _, size = land_k.shape
    rows = queries.shape[1]
    owners = 2 * kept.shape[0]
    scaled = jnp.where(live_lanes(place, rows), 64**-0.25, 0.0)

    def pair(i, _):
        lanes = pl.ds(pl.multiple_of(i * LANES, LANES), LANES)
        turned = grads[:, lanes].T
        g_queries, g_keys = [], []
        for side in range(2):
            h = 2 * i + side
            query = queries[pl.ds(pl.multiple_of(h * size, size), size), :]
            g_context = turned[side * size : (side + 1) * size]
            first = first_map(land_k[h], query)
            g_first = nn(land_out[h], g_context)
            inner = jnp.sum(g_first * first, axis=0, keepdims=True)
            g_scores = (first * (g_first - inner)).astype(BF16)
            g_land = nt(first.astype(BF16), g_context)
            g_key = nt(g_scores, query)
            by_owner(place, h, owners, kept, sent, jnp.concatenate([g_land, g_key], axis=1))
            g_keys.append(g_key)
            g_queries.append((scaled * nn(land_k[h].T, g_scores)).astype(BF16))
        g_query[:, lanes] = jnp.concatenate(g_queries, axis=0).T
        g_lk[:, lanes] = jnp.concatenate(g_keys, axis=1)
        return 0

    lax.fori_loop(0, heads // 2, pair, 0)


def attention_back(place, queries, grads, land_k, land_out, owners):
    width, rows = queries.shape
    heads = land_k.shape[0]
    return pl.pallas_call(
        attention_back_kernel,
        out_shape=owner_parts(heads, owners)
        + (
            jax.ShapeDtypeStruct((LANDMARKS, width), F32),
            jax.ShapeDtypeStruct((rows, width), BF16),
        ),
        in_specs=[SCALARS] + whole(4),
        out_specs=tuple(whole(4)),
        compiler_params=PARAMS,
        cost_estimate=lasting(11.4),
        name="attention_back",
    )(place, queries, grads, land_k, land_out)


def conv_back_kernel(
    v_plain, v_left, v_right, grads, g_left, g_right, base_back, g_value, g_taps, ends
):
    heads = g_taps.shape[0]
    rows, width = grads.shape
    size = width // heads
    blocks_in = rows // LANES
    row = lax.broadcasted_iota(jnp.int32, (LANES, LANES), 0)
    column = lax.broadcasted_iota(jnp.int32, (LANES, LANES), 1)
    reverse = jnp.where(row + column == LANES - 1, 1.0, 0.0).astype(BF16)
    gap = jnp.concatenate([row - column, row - column], axis=1)
    ends[0] = g_left[...].T
    ends[1] = g_right[...].T

    def pair(i, _):
        lanes = pl.ds(pl.multiple_of(i * LANES, LANES), LANES)
        turned = grads[:, lanes].T
        plain = [v_left[LANES - 16 :, lanes]]
        plain += [v_plain[b * LANES : (b + 1) * LANES, lanes] for b in range(blocks_in)]
        plain += [v_right[:16, lanes]]
        for side in range(2):
            h = 2 * i + side
            at = pl.ds(pl.multiple_of(h * size, size), size)
            g_context = turned[side * size : (side + 1) * size]
            blocks = [ends[0, at, :]]
            blocks += [g_context[:, b * LANES : (b + 1) * LANES] for b in range(blocks_in)]
            blocks += [ends[1, at, :]]
            g_value[at, :] = convolved(blocks, band(base_back[pl.ds(h, 1), :]))

        def around(b):
            prior = plain[0] if b == 0 else plain[b][LANES - 16 :]
            return jnp.concatenate([prior, plain[b + 1], plain[b + 2][:16]], axis=0)

        def by_head(b):
            piece = turned[:, b * LANES : (b + 1) * LANES]
            zero = jnp.zeros_like(piece)
            return jnp.concatenate(
                [jnp.where(row < size, piece, zero), jnp.where(row >= size, piece, zero)], axis=1
            )

        total = jnp.zeros((LANES + 32, 2 * LANES), F32)
        for b in range(0, blocks_in, 2):
            total = total + nn(
                jnp.concatenate([around(b), around(b + 1)], axis=1),
                jnp.concatenate([by_head(b), by_head(b + 1)], axis=0),
            )
        empty = jnp.zeros((LANES - 16, 2 * LANES), F32)
        before, here, after = total[:16], total[16 : 16 + LANES], total[16 + LANES :]
        ring = jnp.where(jnp.abs(gap) <= 16, here, 0.0)
        ring = ring + jnp.where(gap >= LANES - 16, jnp.concatenate([empty, before], axis=0), 0.0)
        ring = ring + jnp.where(gap <= 16 - LANES, jnp.concatenate([after, empty], axis=0), 0.0)
        high, low = split(ring)
        lowest = (ring - high.astype(F32) - low.astype(F32)).astype(BF16)
        flat = nn(reverse, high) + nn(reverse, low) + nn(reverse, lowest)
        for side in range(2):
            straight = pltpu.roll(
                flat[:, side * LANES : (side + 1) * LANES], 0, 1, stride=1, stride_axis=0
            )
            g_taps[pl.ds(2 * i + side, 1), :] = jnp.sum(straight, axis=0, keepdims=True)
        return 0

    lax.fori_loop(0, heads // 2, pair, 0)


def conv_back(v_plain, v_ends, grads, g_ends, base_back):
    rows, width = grads.shape
    heads = base_back.shape[0]
    return pl.pallas_call(
        conv_back_kernel,
        out_shape=(
            jax.ShapeDtypeStruct((width, rows), F32),
            jax.ShapeDtypeStruct((heads, LANES), F32),
        ),
        in_specs=whole(7),
        out_specs=tuple(whole(2)),
        scratch_shapes=[pltpu.VMEM((2, width, LANES), BF16)],
        compiler_params=PARAMS,
        cost_estimate=lasting(13.6),
        name="conv_back",
    )(v_plain, *v_ends, grads, *g_ends, base_back)


def third_back_kernel(
    place, keys, values, land_q, spread, g_conv, lq_mid, lk_mid, g_lk, last, first, taps, turned,
    g_k, g_v, sums, kept, sent,
):
    heads, _, size = land_q.shape
    rows, width = g_k.shape
    own_heads = lq_mid.shape[0]
    scale = 64**-0.25
    sums[LANDMARKS:, :] = jnp.zeros((sums.shape[0] - LANDMARKS, 2 * width), F32)
    sums[LANDMARKS : LANDMARKS + 1, :] = last[...]
    sums[LANDMARKS + 1 : LANDMARKS + 2, :] = first[...]
    for h in range(heads):
        sums[LANDMARKS + 2 : LANDMARKS + 3, h * LANES : (h + 1) * LANES] = taps[h : h + 1, :]

    def mid(part, h):
        at = h - place[3] * own_heads
        mine = (at >= 0) & (at < own_heads) & (place[5] == 0)
        inside = jnp.clip(at, 0, own_heads - 1)
        return jnp.where(mine, part[inside], 0.0)

    live = live_lanes(place, rows)
    live_row = jnp.where(live, 1.0, 0.0)
    scaled_row = live_row * 64**-0.25

    def pair(i, _):
        lanes = pl.ds(pl.multiple_of(i * LANES, LANES), LANES)
        g_keys, g_values, g_lqs, lks = [], [], [], []
        for side in range(2):
            h = 2 * i + side
            at = pl.ds(pl.multiple_of(h * size, size), size)
            key, value = keys[at, :], values[at, :]
            pack = spread[h]
            g_mixed = pack[:, :size]
            row_dot = pack[:, size : size + 1]
            top = pack[:, size + 1 : size + 2]
            total = pack[:, size + 2 : size + 3]
            scores = nn(land_q[h], key)
            third = jnp.where(live, jnp.exp(scores - top), 0.0) * (1.0 / total)
            gm_high, gm_low = split(g_mixed)
            g_third = nn(gm_high, value) + nn(gm_low, value)
            g_high, g_low = split(third * (g_third - row_dot))
            g_lqs.append(nt(g_high, key) + nt(g_low, key) + mid(lq_mid, h))
            lks.append(mid(lk_mid, h))
            turned = land_q[h].T
            g_key = nn(turned, g_high) + nn(turned, g_low)
            g_keys.append((scaled_row * g_key).astype(BF16))
            t_high, t_low = split(third)
            gmt_high, gmt_low = split(g_mixed.T)
            g_value = nn(gmt_high, t_high) + nn(gmt_high, t_low) + nn(gmt_low, t_high)
            g_values.append((live_row * (g_value + g_conv[at, :])).astype(BF16))
        g_k[:, lanes] = jnp.concatenate(g_keys, axis=0).T
        g_v[:, lanes] = jnp.concatenate(g_values, axis=0).T
        sums[:LANDMARKS, lanes] = scale * jnp.concatenate(g_lqs, axis=1)
        key_lanes = pl.ds(pl.multiple_of(width + i * LANES, LANES), LANES)
        sums[:LANDMARKS, key_lanes] = scale * (g_lk[:, lanes] + jnp.concatenate(lks, axis=1))
        return 0

    lax.fori_loop(0, heads // 2, pair, 0)
    for number, cells in enumerate((g_k, g_v)):
        family_grads(turned, cells, place[2] == number, kept, sent)


def third_back(
    place, keys, values, land_q, spread, g_conv, lq_mid, lk_mid, g_lk, last, first, taps, turned, halves
):
    width, rows = keys.shape
    plain = jax.ShapeDtypeStruct((rows, width), BF16)
    return pl.pallas_call(
        third_back_kernel,
        out_shape=(plain, plain, jax.ShapeDtypeStruct((LANDMARKS + 8, 2 * width), F32))
        + (jax.ShapeDtypeStruct((halves, width, width // halves), BF16),) * 2,
        in_specs=[SCALARS] + whole(12),
        out_specs=tuple(whole(5)),
        compiler_params=PARAMS,
        cost_estimate=lasting(17),
        name="third_back",
    )(
        place, keys, values, land_q, spread, g_conv, lq_mid, lk_mid, g_lk, last, first, taps, turned
    )


def centred_rows(rows):
    centred = rows - jnp.mean(rows, axis=1, keepdims=True)
    scale = lax.rsqrt(jnp.mean(centred * centred, axis=1, keepdims=True) + 1e-05)
    return centred * scale, scale


def norm_back(grads, gain, unit, scale):
    scaled = grads * gain
    inner = jnp.mean(scaled * unit, axis=1, keepdims=True)
    return scale * (scaled - jnp.mean(scaled, axis=1, keepdims=True) - unit * inner)


def gelu_pair(hidden):
    share = 0.5 * (1.0 + lax.erf(hidden * 0.7071067811865476))
    density = jnp.exp(-0.5 * hidden * hidden) * 0.3989422804014327
    return hidden * share, share + hidden * density


class Copies:
    def __init__(self, sems):
        self.sems, self.used, self.open = sems, 0, []

    def start(self, source, target):
        copy = pltpu.make_async_copy(source, target, self.sems.at[self.used])
        self.used += 1
        copy.start()
        return copy

    def out(self, source, target):
        self.open.append(self.start(source, target))

    def finish(self):
        for copy in self.open:
            copy.wait()


def weight_grad(turned, cells, halves, which, out):
    ff = cells.shape[1] // halves
    columns = ff // 2
    for half in range(halves):
        from_column = pl.ds(pl.multiple_of(half * ff + which * columns, columns), columns)

        def rows_of(i, at, half=half, from_column=from_column):
            out[half, at, :] = nn(turned[at, :], cells[:, from_column]).astype(BF16)

        each_tile(turned.shape[0], 384, rows_of)


def feed_kernel(
    place, first_in, conv_in, land_out, tokens_in, cotangent_in, weights,
    output_to, context_to, slope_to, g_fed_to, g_second_to, unit_to, scale_to, turned_to, active_to, fed_turned_to, sent_to,
    norm_grads, in_w, down_w, out_w, norms, conv, context, tokens, cotangent,
    low, unit, scales, fed, active, slopes, g_fed, g_fed_turned, normed_turned, output, sent,
    sems,
):
    rows, width = tokens.shape
    halves, _, ff = in_w.shape
    part = out_w.shape[2]
    tile = 256
    copies = Copies(sems)
    context_copies = [copies.start(first_in, g_fed_turned), copies.start(conv_in, conv)]
    early = [
        copies.start(weights.at[:, :, pl.ds(2 * ff, part)], out_w),
        copies.start(tokens_in, tokens),
        copies.start(weights.at[:, :, pl.ds(2 * ff + part, LANES)], norms),
    ]
    in_copy = copies.start(weights.at[:, :, pl.ds(0, ff)], in_w)
    down_copy = copies.start(weights.at[:, :, pl.ds(ff, ff)], down_w)
    cotangent_copy = copies.start(cotangent_in, cotangent)
    for copy in context_copies:
        copy.wait()
    context_rows(g_fed_turned, conv, land_out, context)
    copies.out(context, context_to)
    for copy in early:
        copy.wait()
    columns = norms[0].astype(F32).T
    gain0, gain1 = columns[0:1], columns[1:2]
    shift0, shift1 = columns[2:3], columns[3:4]
    norm_grads[...] = jnp.zeros_like(norm_grads)

    def project(i, at):
        attended = nt(context[at, :part], out_w[0])
        for half in range(1, halves):
            attended = attended + nt(context[at, half * part : (half + 1) * part], out_w[half])
        rows_unit, scale = centred_rows(tokens[at, :].astype(F32) + attended)
        unit[at, :] = rows_unit
        scales[at, :] = jnp.broadcast_to(scale, (tile, LANES))
        normed = (rows_unit * gain0 + shift0).astype(BF16)
        low[at, :] = normed
        normed_turned[:, at] = normed.T

    each_tile(rows, tile, project)
    copies.out(unit, unit_to)
    copies.out(scales, scale_to)
    copies.out(normed_turned, turned_to)
    in_copy.wait()
    big = 512

    def hidden_rows(i, at):
        for half in range(halves):
            value, slope = gelu_pair(nn(low[at, :], in_w[half]))
            active[at, half * ff : (half + 1) * ff] = value.astype(BF16)
            slopes[at, half * ff : (half + 1) * ff] = slope.astype(BF16)

    each_tile(rows, tile, hidden_rows)
    copies.out(slopes, slope_to)
    copies.out(active, active_to)
    down_copy.wait()

    def fed_rows(i, at):
        total = nt(active[at, :ff], down_w[0])
        for half in range(1, halves):
            total = total + nt(active[at, half * ff : (half + 1) * ff], down_w[half])
        fed[at, :] = total

    each_tile(rows, big, fed_rows)
    cotangent_copy.wait()

    def second_norm(i, at):
        normed = unit[at, :] * gain0 + shift0
        unit1, scale1 = centred_rows(normed + fed[at, :])
        position = place[0] + i * tile + lax.broadcasted_iota(jnp.int32, (tile, 1), 0)
        live = jnp.where(position < place[1], 1.0, 0.0)
        output[at, :] = (live * (unit1 * gain1 + shift1)).astype(BF16)
        grads = live * cotangent[at, :].astype(F32)
        norm_grads[:, :width] += jnp.sum(grads * unit1, axis=0, keepdims=True)
        norm_grads[:, width:] += jnp.sum(grads, axis=0, keepdims=True)
        second = norm_back(grads, gain1, unit1, scale1)
        fed[at, :] = second
        g_low = second.astype(BF16)
        g_fed[at, :] = g_low
        g_fed_turned[:, at] = g_low.T

    each_tile(rows, tile, second_norm)
    copies.out(output, output_to)
    copies.out(fed, g_second_to)
    copies.out(g_fed, g_fed_to)
    copies.out(g_fed_turned, fed_turned_to)
    weight_grad(g_fed_turned, active, halves, 1 - place[2], sent)
    copies.out(sent, sent_to)
    copies.finish()


ANYWHERE = pl.BlockSpec(memory_space=pl.ANY)


def feed_forward(place, first, conv, land_out, tokens, cotangent, weights, ff, part):
    rows, width = tokens.shape
    halves = weights.shape[0]
    grad = (halves, width, ff // 2)
    shapes = [
        ((rows, width), BF16), ((rows, width), BF16), ((rows, halves * ff), BF16),
        ((rows, width), BF16), ((rows, width), F32), ((rows, width), F32), ((rows, LANES), F32), ((width, rows), BF16),
        ((rows, halves * ff), BF16), ((width, rows), BF16), (grad, BF16), ((1, 2 * width), F32),
    ]
    scratch = [
        ((halves, width, ff), BF16), ((halves, width, ff), BF16), ((halves, width, part), BF16),
        ((halves, width, LANES), BF16), ((width, rows), F32), ((rows, width), BF16),
        ((rows, width), BF16), ((rows, width), BF16),
        ((rows, width), BF16), ((rows, width), F32), ((rows, LANES), F32), ((rows, width), F32),
        ((rows, halves * ff), BF16), ((rows, halves * ff), BF16), ((rows, width), BF16),
        ((width, rows), BF16), ((width, rows), BF16), ((rows, width), BF16), (grad, BF16),
    ]
    return pl.pallas_call(
        feed_kernel,
        out_shape=tuple(jax.ShapeDtypeStruct(*shape) for shape in shapes),
        in_specs=[SCALARS] + [ANYWHERE] * 2 + whole(1) + [ANYWHERE] * 3,
        out_specs=tuple([ANYWHERE] * 11 + whole(1)),
        scratch_shapes=[pltpu.VMEM(*shape) for shape in scratch]
        + [pltpu.SemaphoreType.DMA((19,))],
        compiler_params=PARAMS,
        cost_estimate=lasting(32),
        name="feed_forward",
    )(place, first, conv, land_out, tokens, cotangent, weights)


def feed_back_kernel(
    place, slope_in, g_fed_in, g_second_in, unit_in, scale_in, turned_in, weights,
    g_first_to, g_context_to, g_hidden_to, sent_to, att_turned_to, norm_grads,
    in_w, down_w, out_w, norms, g_hidden, g_fed, second, unit, scales, normed_turned,
    g_att, g_att_turned, g_context, sent,
    sems,
):
    rows, width = second.shape
    halves, _, ff = in_w.shape
    part = out_w.shape[2]
    tile = 256
    copies = Copies(sems)
    early = [
        copies.start(g_fed_in, g_fed),
        copies.start(weights.at[:, :, pl.ds(ff, ff)], down_w),
        copies.start(slope_in, g_hidden),
    ]
    later = [
        copies.start(turned_in, normed_turned),
        copies.start(weights.at[:, :, pl.ds(0, ff)], in_w),
        copies.start(g_second_in, second),
        copies.start(unit_in, unit),
        copies.start(scale_in, scales),
        copies.start(weights.at[:, :, pl.ds(2 * ff + part, LANES)], norms),
        copies.start(weights.at[:, :, pl.ds(2 * ff, part)], out_w),
    ]
    for copy in early:
        copy.wait()
    norm_grads[...] = jnp.zeros_like(norm_grads)
    big = 512

    def back_rows(i, at):
        for half in range(halves):
            g_act = nn(g_fed[at, :], down_w[half])
            to = slice(half * ff, (half + 1) * ff)
            g_hidden[at, to] = (g_act * g_hidden[at, to].astype(F32)).astype(BF16)

    each_tile(rows, big, back_rows)
    copies.out(g_hidden, g_hidden_to)
    later.pop(0).wait()
    weight_grad(normed_turned, g_hidden, halves, 1 - place[2], sent)
    copies.out(sent, sent_to)
    for copy in later:
        copy.wait()
    gain0 = norms[0].astype(F32).T[0:1]

    def normed_rows(i, at):
        total = second[at, :]
        for half in range(halves):
            total = total + nt(g_hidden[at, half * ff : (half + 1) * ff], in_w[half])
        second[at, :] = total

    each_tile(rows, big, normed_rows)

    def first_norm(i, at):
        grads = second[at, :]
        rows_unit, scale = unit[at, :], scales[at, 0:1]
        norm_grads[:, :width] += jnp.sum(grads * rows_unit, axis=0, keepdims=True)
        norm_grads[:, width:] += jnp.sum(grads, axis=0, keepdims=True)
        first = norm_back(grads, gain0, rows_unit, scale)
        second[at, :] = first
        low = first.astype(BF16)
        g_att[at, :] = low
        g_att_turned[:, at] = low.T

    each_tile(rows, tile, first_norm)
    copies.out(second, g_first_to)
    copies.out(g_att_turned, att_turned_to)
    for half in range(halves):
        g_context[:, half * part : (half + 1) * part] = nn(g_att[...], out_w[half]).astype(BF16)
    copies.out(g_context, g_context_to)
    copies.finish()


def feed_backward(place, fed, weights, ff, part):
    rows, width = fed[1].shape
    halves = weights.shape[0]
    grad = (halves, width, ff // 2)
    shapes = [
        ((rows, width), F32), ((rows, width), BF16), ((rows, halves * ff), BF16), (grad, BF16),
        ((width, rows), BF16), ((1, 2 * width), F32),
    ]
    scratch = [
        ((halves, width, ff), BF16), ((halves, width, ff), BF16), ((halves, width, part), BF16),
        ((halves, width, LANES), BF16), ((rows, halves * ff), BF16), ((rows, width), BF16),
        ((rows, width), F32), ((rows, width), F32),
        ((rows, LANES), F32), ((width, rows), BF16),
        ((rows, width), BF16), ((width, rows), BF16), ((rows, width), BF16), (grad, BF16),
    ]
    return pl.pallas_call(
        feed_back_kernel,
        out_shape=tuple(jax.ShapeDtypeStruct(*shape) for shape in shapes),
        in_specs=[SCALARS] + [ANYWHERE] * 7,
        out_specs=tuple([ANYWHERE] * 5 + whole(1)),
        scratch_shapes=[pltpu.VMEM(*shape) for shape in scratch]
        + [pltpu.SemaphoreType.DMA((16,))],
        compiler_params=PARAMS,
        cost_estimate=lasting(27),
        name="feed_backward",
    )(place, *fed, weights)


def kept_kernel(place, turned_in, cells_in, kept, turned, cells, sems):
    halves, width, columns = kept.shape
    ff = 2 * columns
    copies = Copies(sems)
    turned_copy = copies.start(turned_in, turned)
    pieces = []
    for half in range(halves):
        start = pl.multiple_of(half * ff + place[2] * columns, columns)
        pieces.append(copies.start(cells_in.at[:, pl.ds(start, columns)], cells.at[half]))
    turned_copy.wait()
    for half in range(halves):
        pieces[half].wait()

        def rows_of(i, at, half=half):
            kept[half, at, :] = nn(turned[at, :], cells[half]).astype(BF16)

        each_tile(width, 384, rows_of)


def kept_grad(place, turned, cells, halves):
    width, rows = turned.shape
    columns = cells.shape[1] // halves // 2
    return pl.pallas_call(
        kept_kernel,
        out_shape=jax.ShapeDtypeStruct((halves, width, columns), BF16),
        in_specs=[SCALARS] + [ANYWHERE] * 2,
        out_specs=whole(1)[0],
        scratch_shapes=[
            pltpu.VMEM((width, rows), BF16),
            pltpu.VMEM((halves, rows, columns), BF16),
            pltpu.SemaphoreType.DMA((3,)),
        ],
        compiler_params=PARAMS,
        cost_estimate=lasting(5),
        name="kept_grad",
    )(place, turned, cells)


def spread_kernel(place, turned_in, cells_in, other, kept, sent, turned, cells, sems):
    halves, width, columns = other.shape
    ff = 2 * columns
    quarter = columns // 2
    copies = Copies(sems)
    turned_copy = copies.start(turned_in, turned)
    pieces = []
    for half in range(halves):
        start = pl.multiple_of(half * ff + place[2] * columns, columns)
        pieces.append(copies.start(cells_in.at[:, pl.ds(start, columns)], cells.at[half]))
    turned_copy.wait()
    for half in range(halves):
        pieces[half].wait()

        def rows_of(i, at, half=half):
            total = nn(turned[at, :], cells[half]) + other[half, at, :].astype(F32)
            low = total.astype(BF16)
            first = place[4] == 0
            kept[half, at, :] = jnp.where(first, low[:, :quarter], low[:, quarter:])
            sent[half, at, :] = jnp.where(first, low[:, quarter:], low[:, :quarter])

        each_tile(width, 384, rows_of)


def spread_grad(place, turned, cells, other):
    halves, width, columns = other.shape
    rows = turned.shape[1]
    part = jax.ShapeDtypeStruct((halves, width, columns // 2), BF16)
    return pl.pallas_call(
        spread_kernel,
        out_shape=(part, part),
        in_specs=[SCALARS] + [ANYWHERE] * 2 + whole(1),
        out_specs=tuple(whole(2)),
        scratch_shapes=[
            pltpu.VMEM((width, rows), BF16),
            pltpu.VMEM((halves, rows, columns), BF16),
            pltpu.SemaphoreType.DMA((3,)),
        ],
        compiler_params=PARAMS,
        cost_estimate=lasting(6),
        name="spread_grad",
    )(place, turned, cells, other)


def pair_kernel(
    place, one_turned_in, one_cells_in, two_turned_in, two_cells_in, kept, sent,
    one_turned, one_cells, two_turned, two_cells, sems,
):
    copies = Copies(sems)
    loads = [
        copies.start(*pair)
        for pair in (
            (one_turned_in, one_turned), (one_cells_in, one_cells),
            (two_turned_in, two_turned), (two_cells_in, two_cells),
        )
    ]
    for number, (turned, cells) in enumerate(((one_turned, one_cells), (two_turned, two_cells))):
        loads[2 * number].wait()
        loads[2 * number + 1].wait()
        family_grads(turned, cells, place[2] == number, kept, sent)


def pair_grads(place, one_turned, one_cells, two_turned, two_cells, halves):
    width, rows = one_turned.shape
    shape = jax.ShapeDtypeStruct((halves, width, one_cells.shape[1] // halves), BF16)
    return pl.pallas_call(
        pair_kernel,
        out_shape=(shape, shape),
        in_specs=[SCALARS] + [ANYWHERE] * 4,
        out_specs=tuple(whole(2)),
        scratch_shapes=[
            pltpu.VMEM((width, rows), BF16), pltpu.VMEM(one_cells.shape, BF16),
            pltpu.VMEM((width, rows), BF16), pltpu.VMEM(one_cells.shape, BF16),
            pltpu.SemaphoreType.DMA((4,)),
        ],
        compiler_params=PARAMS,
        cost_estimate=lasting(6),
        name="pair_grads",
    )(place, one_turned, one_cells, two_turned, two_cells)


def rank_kernel(place, mine, got, land_tokens, weights, late, through, small):
    halves, width, _ = weights.shape
    part = late.shape[1] // 2
    first = place[2] == 0
    grads = (
        jnp.where(first, mine[:LANDMARKS], got[:LANDMARKS]),
        jnp.where(first, got[:LANDMARKS], mine[:LANDMARKS]),
    )
    counts = landmark_counts(place)
    total = jnp.zeros((2 * LANDMARKS, width), F32)
    for index, grad in enumerate(grads):
        both = jnp.concatenate(split(grad / counts), axis=0)
        for half in range(halves):
            weight = weights[half, :, index * part : (index + 1) * part]
            total = total + nt(both[:, half * part : (half + 1) * part], weight)
    through[...] = jnp.concatenate(split(total[:LANDMARKS] + total[LANDMARKS:]), axis=0)
    zero = jnp.zeros((LANDMARKS, part), F32)
    own = []
    for index, grad in enumerate(grads):
        columns = grad[:, :part]
        for half in range(1, halves):
            columns = jnp.where(place[5] == half, grad[:, half * part : (half + 1) * part], columns)
        own.append(jnp.where(place[2] == 1 - index, columns, zero))
    high, low = split(jnp.concatenate(own, axis=1))
    mean_high, mean_low = split(land_tokens[...] / counts)
    means = jnp.concatenate([mean_high, mean_low, mean_high, jnp.zeros_like(mean_low)], axis=0).T
    factors = jnp.concatenate([high, high, low, jnp.zeros_like(low)], axis=0)
    late[...] = nn(means, factors).astype(BF16)
    gains = jnp.where(first, mine[LANDMARKS:], got[LANDMARKS:])
    shifts = jnp.where(first, got[LANDMARKS:], mine[LANDMARKS:])
    taps = jnp.where(place[5] == 0, gains[2:3], shifts[2:3])
    rows = [gains[1:2], gains[0:1], shifts[1:2], shifts[0:1], taps]
    rows.append(jnp.zeros((small.shape[0] - len(rows), width), F32))
    small[...] = jnp.concatenate(rows, axis=0).astype(BF16)


def rank_parts(place, mine, got, land_tokens, weights):
    halves, width, packed = weights.shape
    return pl.pallas_call(
        rank_kernel,
        out_shape=(
            jax.ShapeDtypeStruct((width, 2 * packed // 3), BF16),
            jax.ShapeDtypeStruct((2 * LANDMARKS, width), BF16),
            jax.ShapeDtypeStruct((16, width), BF16),
        ),
        in_specs=[SCALARS] + whole(4),
        out_specs=tuple(whole(3)),
        compiler_params=PARAMS,
        cost_estimate=lasting(4),
        name="rank_parts",
    )(place, mine, got, land_tokens, weights)


def token_grad_kernel(
    back_in, g_k_in, g_v_in, weights, own_grad, back, g_k, g_v, k_w, v_w, sems
):
    rows, width = back.shape
    halves, _, part = k_w.shape
    copies = Copies(sems)
    first = [
        copies.start(g_k_in, g_k),
        copies.start(weights.at[:, :, pl.ds(part, part)], k_w),
    ]
    later = [
        copies.start(back_in, back),
        copies.start(g_v_in, g_v),
        copies.start(weights.at[:, :, pl.ds(2 * part, part)], v_w),
    ]
    for copy in first + later:
        copy.wait()

    def rows_of(i, at):
        total = back[at, :]
        for half in range(halves):
            columns = slice(half * part, (half + 1) * part)
            total = total + nt(g_k[at, columns], k_w[half]) + nt(g_v[at, columns], v_w[half])
        own_grad[at, :] = total.astype(BF16)

    each_tile(rows, 512, rows_of)


def token_grad(back, g_k, g_v, weights):
    rows, width = back.shape
    halves, _, packed = weights.shape
    shapes = [((rows, width), F32), ((rows, width), BF16), ((rows, width), BF16)]
    shapes += [((halves, width, packed // 3), BF16)] * 2
    return pl.pallas_call(
        token_grad_kernel,
        out_shape=jax.ShapeDtypeStruct((rows, width), BF16),
        in_specs=[ANYWHERE] * 4,
        out_specs=whole(1)[0],
        scratch_shapes=[pltpu.VMEM(*shape) for shape in shapes]
        + [pltpu.SemaphoreType.DMA((5,))],
        compiler_params=PARAMS,
        cost_estimate=lasting(6),
        name="token_grad",
    )(back, g_k, g_v, weights)


def flipped(values, axis, bit):
    count = lax.axis_size(axis)
    return lax.ppermute(values, axis, [(i, i ^ bit) for i in range(count)])


def side_of(axis, bit):
    return (lax.axis_index(axis) // bit) % 2


def paired(mine, axis, bit, dim):
    other = flipped(mine, axis, bit)
    both = jnp.zeros(mine.shape[:dim] + (2,) + mine.shape[dim:], mine.dtype)
    side = side_of(axis, bit)
    both = lax.dynamic_update_slice_in_dim(both, jnp.expand_dims(mine, dim), side, dim)
    return lax.dynamic_update_slice_in_dim(both, jnp.expand_dims(other, dim), 1 - side, dim)


def ctx_bits():
    bits, bit = [], 1
    while bit < lax.axis_size("ctx"):
        bits.append(bit)
        bit *= 2
    return bits


def sequence_start(values):
    width = values.shape[1] // 2
    side = side_of("ctx", 1)
    kept = lax.dynamic_slice_in_dim(values, side * width, width, axis=1)
    sent = lax.dynamic_slice_in_dim(values, (1 - side) * width, width, axis=1)
    kept = kept + flipped(sent, "ctx", 1)
    return kept + flipped(kept, "tp", 1)


def sequence_end(kept):
    for bit in ctx_bits()[1:]:
        kept = kept + flipped(kept, "ctx", bit)
    return kept, flipped(kept, "ctx", 1)


def joined_halves(kept, other):
    return jnp.where(
        side_of("ctx", 1) == 0,
        jnp.concatenate([kept, other], axis=1),
        jnp.concatenate([other, kept], axis=1),
    )


def to_owner(kept, sent, combine):
    kept = combine(kept, flipped(sent, "ctx", 1))
    for bit in ctx_bits()[1:]:
        view = kept.reshape((-1, 2) + kept.shape[1:])
        side = side_of("ctx", bit)
        sent = lax.dynamic_index_in_dim(view, 1 - side, 1, False)
        kept = lax.dynamic_index_in_dim(view, side, 1, False)
        kept = combine(kept, flipped(sent, "ctx", bit))
    return kept[0], flipped(kept[0], "tp", 1)


def from_owners(part):
    whole_part = part[None]
    for bit in reversed(ctx_bits()):
        both = paired(whole_part, "ctx", bit, 1)
        whole_part = both.reshape((-1,) + part.shape)
    return whole_part.reshape((-1,) + part.shape[1:])


def merge_keys(one, two):
    size = LANES // 2
    one_top, two_top = one[..., size : size + 1], two[..., size : size + 1]
    top = jnp.maximum(one_top, two_top)
    one_factor, two_factor = jnp.exp(one_top - top), jnp.exp(two_top - top)
    summed = one * one_factor + two * two_factor
    lane = lax.broadcasted_iota(jnp.int32, summed.shape, summed.ndim - 1)
    return jnp.where(lane == size, top, summed)


def neighbour_rows(cells, count):
    pieces = lax.axis_size("ctx") * lax.axis_size("tp")
    up = [(i, i + 1) for i in range(pieces - 1)]
    before = lax.ppermute(cells[-count:], ("ctx", "tp"), up)
    after = lax.ppermute(cells[:count], ("ctx", "tp"), [(j, i) for i, j in up])
    return (
        jnp.pad(before, ((LANES - count, 0), (0, 0))),
        jnp.pad(after, ((0, LANES - count), (0, 0))),
    )


def own_quarter(shard):
    rows = shard.shape[0] // lax.axis_size("ctx")
    return lax.dynamic_slice_in_dim(shard, lax.axis_index("ctx") * rows, rows, axis=0)


def gathered(shard):
    full = lax.all_gather(own_quarter(shard), ("tp", "fsdp", "ctx"), tiled=True)
    return full.reshape(lax.axis_size("tp"), -1, shard.shape[1])


def gathered_early(shard, beside):
    count = lax.axis_size("fsdp")
    piece = own_quarter(shard)
    if count > 4:
        held = lax.all_gather(piece, "fsdp")
    else:
        here = lax.axis_index("fsdp")
        held = jnp.zeros((count,) + piece.shape, piece.dtype)
        held = lax.dynamic_update_slice_in_dim(held, piece[None], here, 0)
        for step in range(1, count):
            moved = lax.ppermute(piece, "fsdp", [(i, (i + step) % count) for i in range(count)])
            held = lax.dynamic_update_slice_in_dim(held, moved[None], (here - step) % count, 0)
    held, beside = gate(held, beside)
    bits = ctx_bits()
    halves = []
    for number, half in enumerate((held[: count // 2], held[count // 2 :])):
        half = half[None]
        if number == 0:
            half = paired(half[0], "tp", 1, 0)
        for place, bit in enumerate(reversed(bits[1:])):
            half = paired(half, "ctx", bit, 2 + place)
        if number == 1:
            half = paired(half[0], "tp", 1, 0)
        halves.append(paired(half, "ctx", bits[0], 1 + len(bits)))
    full = jnp.concatenate(halves, axis=1)
    return full.reshape(lax.axis_size("tp"), -1, shard.shape[1]), beside


def bits_of(axis):
    bits, bit = [], lax.axis_size(axis) // 2
    while bit:
        bits.append(bit)
        bit //= 2
    return bits


def added(*parts):
    return sum(part.astype(F32) for part in parts).astype(BF16)


def cut(cells, axis, bit, dim):
    size = cells.shape[dim] // 2
    side = side_of(axis, bit)
    return (
        lax.dynamic_slice_in_dim(cells, side * size, size, axis=dim),
        lax.dynamic_slice_in_dim(cells, (1 - side) * size, size, axis=dim),
    )


def gate(*values):
    return lax.optimization_barrier(values)


def dotf(spec, *operands):
    return jnp.einsum(spec, *operands, preferred_element_type=F32)


def taps_round(taps):
    middle = taps.shape[1] // 2
    gap = jnp.zeros((taps.shape[0], LANES - taps.shape[1]), F32)
    return jnp.concatenate([taps[:, middle::-1], gap, taps[:, :middle:-1]], axis=1)


def landmark_bounds(length):
    landmark = jnp.arange(LANDMARKS + 1, dtype=jnp.int32)
    return (landmark * length + LANDMARKS - 1) // LANDMARKS


def landmark_counts_of(length):
    bounds = landmark_bounds(length)
    return (bounds[1:] - bounds[:-1]).astype(F32)[:, None]


def landmark_rows(position, length):
    bounds = landmark_bounds(length)
    inside = (position[:, None] >= bounds[None, :-1]) & (position[:, None] < bounds[None, 1:])
    return inside.astype(BF16)


def on_device(
    tokens,
    lengths,
    qk_weight,
    value_weight,
    out_weight,
    in_weight,
    down_weight,
    norm_gains,
    norm_shifts,
    conv_weight,
    cotangent,
):
    tp_count = lax.axis_size("tp")
    tp_index = lax.axis_index("tp")
    ctx_index = lax.axis_index("ctx")
    _, slot_len, model_width = tokens.shape
    rows = slot_len // tp_count
    local_heads, tap_count = conv_weight.shape
    local_width = value_weight.shape[1]
    ff_width = in_weight.shape[1]
    head_size = local_width // local_heads
    heads = local_heads * tp_count
    owners = lax.axis_size("ctx")
    own_heads = heads // owners
    width = local_width * tp_count
    radius = tap_count // 2
    length = lengths[0]

    first_row = (ctx_index * tp_count + tp_index) * rows
    sides = (side_of("ctx", 1), ctx_index, side_of("ctx", ctx_bits()[-1]), tp_index)
    place = jnp.stack([first_row, length, *sides]).astype(jnp.int32)

    norm_columns = jnp.concatenate([norm_gains, norm_shifts], axis=0).T
    norm_columns = jnp.pad(norm_columns, ((0, 0), (0, LANES - norm_columns.shape[1])))
    ffn_full = gathered(
        jnp.concatenate([in_weight, down_weight.T, out_weight.T, norm_columns], axis=1)
    )
    own_taps = jnp.where(ctx_index == 0, conv_weight.astype(F32), 0.0)
    tap_rows = jnp.pad(own_taps, ((0, 8 - local_heads), (0, LANES - tap_count)))
    tap_rows = jnp.where(
        jnp.arange(model_width) // LANES == tp_index,
        jnp.tile(tap_rows, (1, model_width // LANES)),
        0.0,
    )
    own = lax.dynamic_slice_in_dim(tokens[0], tp_index * rows, rows, axis=0)
    land_tokens = sequence_start(jnp.concatenate([token_sums(place, own), tap_rows], axis=0))
    qkv_full, land_tokens = gathered_early(
        jnp.concatenate([qk_weight[0], qk_weight[1], value_weight], axis=1), land_tokens
    )
    land_tokens = joined_halves(*sequence_end(land_tokens))
    own_cotangent = lax.dynamic_slice_in_dim(cotangent[0], tp_index * rows, rows, axis=0)
    tap_weights = land_tokens[LANDMARKS : LANDMARKS + local_heads, : tp_count * LANES]
    tap_weights = tap_weights.reshape(local_heads, tp_count, LANES).transpose(1, 0, 2)
    tap_weights = tap_weights.reshape(heads, LANES)[:, :tap_count]
    land_tokens = land_tokens[:LANDMARKS]
    base, base_back = taps_round(tap_weights), taps_round(tap_weights[:, ::-1])

    queries, keys, values, v_plain, land_q, land_k, own_turned, *parts_of_third = projections(
        place, own, land_tokens, qkv_full, head_size, owners
    )
    v_ends = neighbour_rows(v_plain, radius)
    merged, merged_tp = to_owner(*parts_of_third, merge_keys)
    kept_turns = inverse_forward(place, land_q, land_k, owners)
    first, conv = first_and_conv(queries, values, *v_ends, land_k, base)
    merged, own_out = landmark_out(merged, merged_tp, kept_turns[0])
    land_out = from_owners(own_out)

    own_output, context, *fed, active, fed_turned, down_sent, last_norm = feed_forward(
        place, first, conv, land_out, own, own_cotangent, ffn_full, ff_width, local_width
    )
    high = ctx_bits()[-1]
    owner_count = lax.axis_size("fsdp")
    owner_rows = model_width // owner_count
    near, *farther = bits_of("fsdp")[::-1]

    def by_owner_bits(cells):
        return cells.reshape((2,) * (1 + len(farther)) + (-1, cells.shape[-1]))

    def cut_last(cells, bit):
        dim = cells.ndim - 3
        return tuple(piece.squeeze(dim) for piece in cut(cells, "fsdp", bit, dim))

    other_output = flipped(own_output, "tp", 1)
    down_other = flipped(down_sent, "ctx", 1)
    down_kept = kept_grad(place, fed_turned, active, tp_count)
    down_kept, down_other = gate(down_kept, down_other)
    down_mine, down_theirs = cut(down_kept, "ctx", high, 2)
    other_mine, other_theirs = cut(down_other, "ctx", high, 2)
    down_sent = added(down_theirs, other_theirs)
    down_got = flipped(down_sent, "ctx", high)
    fed[0], down_sent = gate(fed[0], down_sent)
    grad_first_res, grad_context, g_hidden, in_sent, att_turned, first_norm = feed_backward(
        place, fed, ffn_full, ff_width, local_width
    )
    in_sent, grad_context, g_hidden, other_output, down_got = gate(
        in_sent, grad_context, g_hidden, other_output, down_got
    )
    in_other = flipped(in_sent, "ctx", 1)
    g_ends = neighbour_rows(grad_context, radius)
    down = added(down_mine, other_mine, down_got)
    down_mine, down_sent = cut(down, "tp", 1, 0)
    down_got = flipped(down_sent, "tp", 1)
    grad_context, down_sent = gate(grad_context, down_sent)
    land_kept, land_sent, g_lk, g_q = attention_back(
        place, queries, grad_context, land_k, land_out, owners
    )
    land_kept, land_sent, in_other, g_ends = gate(land_kept, land_sent, in_other, g_ends)

    land_other = flipped(land_sent, "ctx", 1)
    in_kept, in_sent = spread_grad(place, fed[5], g_hidden, in_other)
    in_kept, in_sent, land_other, down_got = gate(in_kept, in_sent, land_other, down_got)
    land_grads = land_kept + land_other
    land_mine, land_theirs = cut(land_grads, "ctx", high, 0)
    land_got = flipped(land_theirs, "ctx", high)
    land_theirs, in_sent = gate(land_theirs, in_sent)
    in_got = flipped(in_sent, "ctx", high)
    down = added(down_mine, down_got)
    grad_context, in_sent = gate(grad_context, in_sent)
    g_conv, g_taps = conv_back(v_plain, v_ends, grad_context, g_ends, base_back)
    g_conv, g_taps, land_got = gate(g_conv, g_taps, land_got)
    own_grads = (land_mine + land_got)[0]
    tp_grads = flipped(own_grads, "tp", 1)

    def parts(cells):
        return cells.reshape(rows, tp_count, local_width)

    def qkv_part(index):
        return qkv_full[:, :, index * local_width : (index + 1) * local_width]

    g_q, own_grads = gate(g_q, own_grads)
    mixed_kept, mixed_sent = pair_grads(place, att_turned, context, own_turned, g_q, tp_count)
    back_q = grad_first_res + dotf("tpk,pck->tc", parts(g_q), qkv_part(0))
    mixed_kept, mixed_sent, tp_grads, back_q = gate(mixed_kept, mixed_sent, tp_grads, back_q)
    mixed_got = flipped(mixed_sent, "ctx", 1)
    own_grads, mixed_sent = gate(own_grads + tp_grads, mixed_sent)
    spread, lq_mid, lk_mid = inverse_backward(
        place, land_q, land_k, merged, own_grads, *kept_turns
    )
    spread, in_got, mixed_got = gate(spread, in_got, mixed_got)
    spread = from_owners(spread)

    in_mine, in_sent = cut(added(in_kept, in_got), "tp", 1, 0)
    in_got = flipped(in_sent, "tp", 1)
    def by_ctx(cells):
        return cells.reshape(tp_count, owner_count, 2, -1, local_width)

    mixed = added(mixed_kept, mixed_got)
    mixed_mine, mixed_sent = cut(by_ctx(mixed), "ctx", high, 2)
    mixed_got = flipped(mixed_sent, "ctx", high)
    spread, in_sent, mixed_sent = gate(spread, in_sent, mixed_sent)
    g_k, g_v, sums, kv_kept, kv_sent = third_back(
        place, keys, values, land_q, spread, g_conv, lq_mid, lk_mid, g_lk, last_norm, first_norm,
        g_taps, own_turned, tp_count,
    )

    kv_kept, kv_sent, sums, in_got, mixed_got = gate(kv_kept, kv_sent, sums, in_got, mixed_got)
    kv_got = flipped(kv_sent, "ctx", 1)
    sums_mine, sums_sent = cut(sums, "ctx", 1, 1)
    sums_got = flipped(sums_sent, "ctx", 1)
    kv_kept, kv_got = gate(kv_kept, kv_got)
    kv_mine, kv_sent = cut(by_ctx(added(kv_kept, kv_got)), "ctx", high, 2)
    kv_sent, sums_mine, mixed_mine, in_mine, g_k = gate(
        kv_sent, sums_mine, mixed_mine, in_mine, g_k
    )
    kv_got = flipped(kv_sent, "ctx", high)
    sums = sums_mine + sums_got
    sums_got = flipped(sums, "tp", 1)
    mixed_mine, mixed_sent = cut(added(mixed_mine, mixed_got), "tp", 1, 0)
    sums, mixed_sent, in_mine = gate(sums, mixed_sent, in_mine)
    mixed_got = flipped(mixed_sent, "tp", 1)
    pair = jnp.concatenate([added(in_mine, in_got)[0], down[0]], axis=1)
    g_k, mixed_sent, pair = gate(g_k, mixed_sent, pair)
    pair = lax.psum_scatter(pair, "fsdp", scatter_dimension=0, tiled=True)
    own_grad = token_grad(back_q, g_k, g_v, qkv_full)
    own_grad, sums_got, mixed_got, kv_got = gate(own_grad, sums_got, mixed_got, kv_got)
    sums = sums + sums_got
    sums_got = flipped(sums, "ctx", high)
    kv_mine, kv_sent = cut(added(kv_mine, kv_got), "tp", 1, 0)
    own_grad, sums, kv_sent = gate(own_grad, sums, kv_sent)
    kv_got = flipped(kv_sent, "tp", 1)
    other_grad = flipped(own_grad, "tp", 1)
    sums = sums + sums_got
    sums_got = flipped(sums, "ctx", 1)
    sums, sums_got, kv_got = gate(sums, sums_got, kv_got)
    late, through, small = rank_parts(place, sums, sums_got, land_tokens, qkv_full)
    late, through, small, own_output, other_output = gate(
        late, through, small, own_output, other_output
    )
    late = late.reshape(owner_count, 2, -1, 2 * local_width)
    late = lax.dynamic_index_in_dim(late, place[4], 1, False)
    mixed = added(
        jnp.concatenate([mixed_mine, kv_mine], axis=-1).reshape(late.shape),
        jnp.concatenate([mixed_got, kv_got], axis=-1).reshape(late.shape),
        late,
    )
    small = jnp.broadcast_to(small[None], (owner_count,) + small.shape)
    mixed = by_owner_bits(jnp.concatenate([mixed, small], axis=1))
    mixed_mine, mixed_sent = cut_last(mixed, near)
    mixed_sent, pair = gate(mixed_sent, pair)
    mixed_got = flipped(mixed_sent, "fsdp", near)
    mixed = added(mixed_mine, mixed_got)
    for bit in farther:
        mixed_mine, mixed_sent = cut_last(mixed, bit)
        mixed = added(mixed_mine, flipped(mixed_sent, "fsdp", bit))
    small = mixed[-16:].astype(F32)
    mixed = mixed[:-16]

    def of_core(cells, core):
        cells = cells.reshape((owners // 2, 2) + cells.shape[1:])
        return [cells[i, core] for i in range(owners // 2)]

    mixed, other_grad = gate(mixed, other_grad)
    mixed = from_owners(mixed[None])
    sides = [jnp.concatenate(of_core(mixed, core), axis=0).astype(F32) for core in range(2)]
    grad_out, grad_k = sides[0][:, :local_width].T, sides[0][:, local_width:]
    grad_q, grad_v = sides[1][:, :local_width], sides[1][:, local_width:]

    own_columns = lax.axis_index("fsdp") * owner_rows
    norm_sums = lax.dynamic_slice_in_dim(small[:4], own_columns, owner_rows, axis=1)
    taps_sum = small[4].reshape(local_heads, LANES)
    grad_taps = jnp.concatenate(
        [taps_sum[:, radius - 1 :: -1], taps_sum[:, : -radius - 2 : -1]], axis=1
    )

    columns = pair.shape[1] // 2
    pair = from_owners(pair[None])
    pieces = [piece for core in range(2) for piece in of_core(pair, core)]
    grad_in = jnp.concatenate([piece[:, :columns] for piece in pieces], axis=1).astype(F32)
    grad_down = jnp.concatenate([piece[:, columns:] for piece in pieces], axis=1).astype(F32).T

    output = jnp.where(
        tp_index == 0,
        jnp.concatenate([own_output, other_output]),
        jnp.concatenate([other_output, own_output]),
    )[None]
    both_grads = jnp.where(
        tp_index == 0,
        jnp.concatenate([own_grad, other_grad]),
        jnp.concatenate([other_grad, own_grad]),
    )
    position = ctx_index * slot_len + jnp.arange(slot_len, dtype=jnp.int32)
    onehot = landmark_rows(position, length)
    grad_tokens = both_grads.astype(F32) + dotf(
        "tm,mc->tc", jnp.concatenate([onehot, onehot], axis=1), through
    )
    grad_tokens = grad_tokens.reshape(1, slot_len, model_width)
    return (
        output,
        grad_tokens,
        jnp.stack([grad_q, grad_k]),
        grad_v,
        grad_out,
        grad_in,
        grad_down,
        norm_sums[:2],
        norm_sums[2:],
        grad_taps,
    )


def solution(mesh):
    in_specs = (
        P("fsdp", "ctx", None),
        P("fsdp"),
        P(None, "fsdp", "tp"),
        P("fsdp", "tp"),
        P("tp", "fsdp"),
        P("fsdp", "tp"),
        P("tp", "fsdp"),
        P(None, "fsdp"),
        P(None, "fsdp"),
        P("tp", None),
        P("fsdp", "ctx", None),
    )
    out_specs = (
        P("fsdp", "ctx", None),
        P("fsdp", "ctx", None),
        P(None, "fsdp", "tp"),
        P("fsdp", "tp"),
        P("tp", "fsdp"),
        P("fsdp", "tp"),
        P("tp", "fsdp"),
        P(None, "fsdp"),
        P(None, "fsdp"),
        P("tp", None),
    )
    return jax.shard_map(
        on_device, mesh=mesh, in_specs=in_specs, out_specs=out_specs, check_vma=False
    )
```

```python
import jax
import jax.numpy as jnp
from jax import lax
from jax.experimental import pallas as pl
from jax.experimental.pallas import tpu as pltpu
from jax.sharding import PartitionSpec as P

LANDMARKS = 64
NEWTON = 6
LANES = 128
VMEM_BYTES = 56 * 2**20

HIGH = lax.Precision.HIGHEST
F32 = jnp.float32
BF16 = jnp.bfloat16


def lasting(microseconds):
    return pl.CostEstimate(
        flops=int(microseconds * 1.1535e9), bytes_accessed=int(microseconds * 1e5), transcendentals=0
    )


def nn(left, right):
    return jnp.dot(left, right, preferred_element_type=F32)


def nt(left, right):
    return lax.dot_general(left, right, (((1,), (1,)), ((), ())), preferred_element_type=F32)


def split(wide):
    high = wide.astype(BF16)
    return high, (wide - high.astype(F32)).astype(BF16)


def each_tile(count, tile, body):
    def step(i, _):
        body(i, pl.ds(pl.multiple_of(i * tile, tile), tile))
        return 0

    lax.fori_loop(0, count // tile, step, 0)


def family_grads(turned, cells, mine, kept, sent):
    halves, width, columns = kept.shape

    def rows_of(i, at):
        total = nn(turned[at, :], cells[...]).astype(BF16)

        @pl.when(mine)
        def _():
            for half in range(halves):
                kept[half, at, :] = total[:, half * columns : (half + 1) * columns]

        @pl.when(jnp.logical_not(mine))
        def _():
            for half in range(halves):
                sent[half, at, :] = total[:, half * columns : (half + 1) * columns]

    each_tile(width, 384, rows_of)


def whole(count):
    return [pl.BlockSpec(memory_space=pltpu.VMEM)] * count


SCALARS = pl.BlockSpec(memory_space=pltpu.SMEM)
PARAMS = pltpu.CompilerParams(vmem_limit_bytes=VMEM_BYTES)


def landmark_onehot(place, rows, landmark_axis):
    shape = (LANDMARKS, rows) if landmark_axis == 0 else (rows, LANDMARKS)
    landmark = lax.broadcasted_iota(jnp.int32, shape, landmark_axis)
    position = place[0] + lax.broadcasted_iota(jnp.int32, shape, 1 - landmark_axis)
    start = lax.shift_right_logical(landmark * place[1] + (LANDMARKS - 1), 6)
    end = lax.shift_right_logical((landmark + 1) * place[1] + (LANDMARKS - 1), 6)
    return jnp.where((position >= start) & (position < end), 1.0, 0.0).astype(BF16)


def live_lanes(place, rows):
    position = place[0] + lax.broadcasted_iota(jnp.int32, (1, rows), 1)
    return position < place[1]


def band(base_row):
    ring = pltpu.roll(jnp.broadcast_to(base_row, (LANES, LANES)), 0, 1, stride=1, stride_axis=0)
    gap = lax.broadcasted_iota(jnp.int32, (LANES, LANES), 0) - lax.broadcasted_iota(
        jnp.int32, (LANES, LANES), 1
    )
    zero = jnp.zeros_like(ring)
    before = jnp.where(gap >= LANES - 16, ring, zero).astype(BF16)
    here = jnp.where(jnp.abs(gap) <= 16, ring, zero).astype(BF16)
    after = jnp.where(gap <= 16 - LANES, ring, zero).astype(BF16)
    return before, here, after


def convolved(blocks, bands):
    count = len(blocks) - 2
    size = blocks[0].shape[0]
    stacked = jnp.concatenate(
        [jnp.concatenate(blocks[i : i + 3], axis=1) for i in range(count)], axis=0
    )
    out = nn(stacked, jnp.concatenate(bands, axis=0))
    return jnp.concatenate([out[i * size : (i + 1) * size] for i in range(count)], axis=1)


def token_sums_kernel(place, tokens, sums):
    sums[...] = nn(landmark_onehot(place, tokens.shape[0], 0), tokens[...])


def token_sums(place, tokens):
    return pl.pallas_call(
        token_sums_kernel,
        out_shape=jax.ShapeDtypeStruct((LANDMARKS, tokens.shape[1]), F32),
        in_specs=[SCALARS] + whole(1),
        out_specs=whole(1)[0],
        compiler_params=PARAMS,
        cost_estimate=lasting(2.5),
        name="token_sums",
    )(place, tokens)


def landmark_counts(place):
    landmark = lax.broadcasted_iota(jnp.int32, (LANDMARKS, 1), 0)
    start = lax.shift_right_logical(landmark * place[1] + (LANDMARKS - 1), 6)
    end = lax.shift_right_logical((landmark + 1) * place[1] + (LANDMARKS - 1), 6)
    return (end - start).astype(F32)


def projection_kernel(
    place, tokens, sums, weights, q_out, k_out, v_out, v_plain, land_q, land_k, turned, kept, sent
):
    rows = tokens.shape[0]
    halves, _, packed = weights.shape
    width = packed // 3
    size = land_q.shape[2]
    position = place[0] + lax.broadcasted_iota(jnp.int32, (rows, 1), 0)
    live = jnp.where(position < place[1], 1.0, 0.0)
    scaled = live * 64**-0.25
    means = jnp.concatenate(split(sums[...] / landmark_counts(place)), axis=0)
    cells = tokens[...]
    turned[...] = cells.T
    for half in range(halves):
        for part, out in enumerate((q_out, k_out, v_out)):
            weight = weights[half, :, part * width : (part + 1) * width]
            low = ((live if part == 2 else scaled) * nn(cells, weight)).astype(BF16)
            out[half * width : (half + 1) * width, :] = low.T
            if part == 2:
                v_plain[:, half * width : (half + 1) * width] = low
                continue
            both = nn(means, weight)
            land = (64**-0.25 * (both[:LANDMARKS] + both[LANDMARKS:])).astype(BF16)
            to = land_k if part else land_q
            for head in range(width // size):
                to[half * (width // size) + head] = land[:, head * size : (head + 1) * size]
    third_heads(place, k_out, v_out, land_q, kept, sent)


def projections(place, tokens, sums, weights, size, owners):
    rows = tokens.shape[0]
    width = weights.shape[0] * weights.shape[2] // 3
    turned = jax.ShapeDtypeStruct((width, rows), BF16)
    land = jax.ShapeDtypeStruct((width // size, LANDMARKS, size), BF16)
    return pl.pallas_call(
        projection_kernel,
        out_shape=(turned, turned, turned, jax.ShapeDtypeStruct((rows, width), BF16), land, land)
        + (jax.ShapeDtypeStruct(tokens.shape[::-1], BF16),)
        + owner_parts(width // size, owners),
        in_specs=[SCALARS] + whole(3),
        out_specs=tuple(whole(9)),
        compiler_params=PARAMS,
        cost_estimate=lasting(18),
        name="projections",
    )(place, tokens, sums, weights)


def by_owner(place, h, owners, kept, sent, values):
    per = kept.shape[1]
    for owner in range(owners):
        @pl.when((h >= owner * per) & (h < (owner + 1) * per))
        def _(owner=owner):
            mine = place[2] == owner % 2

            @pl.when(mine)
            def _():
                kept[owner // 2, h - owner * per] = values

            @pl.when(jnp.logical_not(mine))
            def _():
                sent[owner // 2, h - owner * per] = values


def third_heads(place, keys, values, land_q, kept, sent):
    heads = land_q.shape[0]
    size = land_q.shape[2]
    rows = keys.shape[1]
    owners = 2 * kept.shape[0]
    live = live_lanes(place, rows)

    def head(h):
        at = pl.ds(pl.multiple_of(h * size, size), size)
        scores = jnp.where(live, nn(land_q[h], keys[at, :]), -1e30)
        top = jnp.max(scores, axis=1, keepdims=True)
        raised = jnp.where(live, jnp.exp(scores - top), 0.0)
        total = jnp.sum(raised, axis=1, keepdims=True)
        high, low = split(raised)
        value = values[at, :]
        mixed = nt(high, value) + nt(low, value)
        lane = lax.broadcasted_iota(jnp.int32, (LANDMARKS, LANES - size), 1)
        stats = jnp.where(lane == 0, top, jnp.where(lane == 1, total, 0.0))
        by_owner(place, h, owners, kept, sent, jnp.concatenate([mixed, stats], axis=1))

    def pair(i, _):
        head(2 * i)
        head(2 * i + 1)
        return 0

    lax.fori_loop(0, heads // 2, pair, 0)


def owner_parts(heads, owners):
    part = jax.ShapeDtypeStruct((owners // 2, heads // owners, LANDMARKS, LANES), F32)
    return part, part


def dot_high(left, right):
    return jnp.dot(left, right, preferred_element_type=F32, precision=HIGH)


def dot_high_nt(left, right):
    return lax.dot_general(
        left, right, (((1,), (1,)), ((), ())), preferred_element_type=F32, precision=HIGH
    )


def eye():
    row = lax.broadcasted_iota(jnp.int32, (LANDMARKS, LANDMARKS), 0)
    column = lax.broadcasted_iota(jnp.int32, (LANDMARKS, LANDMARKS), 1)
    return jnp.where(row == column, 1.0, 0.0)


def middle_map(land_q, land_k):
    scores = nt(land_q, land_k)
    raised = jnp.exp(scores - jnp.max(scores, axis=1, keepdims=True))
    return raised / jnp.sum(raised, axis=1, keepdims=True)


def inverse_kernel(place, land_q, land_k, kept_v, kept_p, kept_b, kept_c):
    heads = range(kept_v.shape[1])
    one = eye()
    own = [place[3] * len(heads) + h for h in heads]
    middle = [middle_map(land_q[h], land_k[h]) for h in own]
    approx = [m.T / jnp.sum(m * m, keepdims=True) for m in middle]
    for turn in range(NEWTON):
        product = [dot_high(middle[h], approx[h]) for h in heads]
        for h in heads:
            kept_v[turn, h] = approx[h]
            kept_p[turn, h] = product[h]
        bracket = [7.0 * one - p for p in product]
        bracket = [15.0 * one - dot_high(product[h], bracket[h]) for h in heads]
        for h in heads:
            kept_b[turn, h] = bracket[h]
        bracket = [13.0 * one - dot_high(product[h], bracket[h]) for h in heads]
        for h in heads:
            kept_c[turn, h] = bracket[h]
        approx = [0.25 * dot_high(approx[h], bracket[h]) for h in heads]
    for h in heads:
        kept_v[NEWTON, h] = approx[h]


def inverse_forward(place, land_q, land_k, owners):
    heads = land_q.shape[0] // owners
    square = (heads, LANDMARKS, LANDMARKS)
    return pl.pallas_call(
        inverse_kernel,
        out_shape=(
            jax.ShapeDtypeStruct((NEWTON + 1,) + square, F32),
            jax.ShapeDtypeStruct((NEWTON,) + square, F32),
            jax.ShapeDtypeStruct((NEWTON,) + square, F32),
            jax.ShapeDtypeStruct((NEWTON,) + square, F32),
        ),
        in_specs=[SCALARS] + whole(2),
        out_specs=tuple(whole(4)),
        compiler_params=PARAMS,
        cost_estimate=lasting(7),
        name="inverse_forward",
    )(place, land_q, land_k)


def merged_keys(one, two, size):
    one_top, two_top = one[:, size : size + 1], two[:, size : size + 1]
    top = jnp.maximum(one_top, two_top)
    summed = one * jnp.exp(one_top - top) + two * jnp.exp(two_top - top)
    lane = lax.broadcasted_iota(jnp.int32, one.shape, 1)
    return jnp.where(lane == size, top, summed)


def land_out_kernel(one, two, kept_v, merged, land_out):
    size = land_out.shape[2]
    for h in range(one.shape[0]):
        both = merged_keys(one[h], two[h], size)
        merged[h] = both
        mixed = both[:, :size] / both[:, size + 1 : size + 2]
        land_out[h] = dot_high(kept_v[NEWTON, h], mixed).astype(BF16)


def landmark_out(one, two, kept_v):
    heads = one.shape[0]
    return pl.pallas_call(
        land_out_kernel,
        out_shape=(
            jax.ShapeDtypeStruct(one.shape, F32),
            jax.ShapeDtypeStruct((heads, LANDMARKS, LANES // 2), BF16),
        ),
        in_specs=whole(3),
        out_specs=tuple(whole(2)),
        compiler_params=PARAMS,
        cost_estimate=lasting(2.2),
        name="landmark_out",
    )(one, two, kept_v)


def inverse_back_kernel(
    place, land_q, land_k, merged, grads, kept_v, kept_p, kept_b, kept_c, spread, g_lq, g_lk
):
    heads = range(grads.shape[0])
    size = land_q.shape[2]
    one = eye()
    own = [place[3] * len(heads) + h for h in heads]
    middle = [middle_map(land_q[h], land_k[h]) for h in own]
    turned = [m.T for m in middle]
    g_approx = []
    for h in heads:
        mixed = merged[h][:, :size] / merged[h][:, size + 1 : size + 2]
        g_land = grads[h][:, :size]
        g_approx.append(dot_high_nt(g_land, mixed))
        g_mixed = dot_high(kept_v[NEWTON, h].T, g_land)
        row_dot = jnp.sum(g_mixed * mixed, axis=1, keepdims=True)
        lane = lax.broadcasted_iota(jnp.int32, (LANDMARKS, LANES - size), 1)
        top = merged[h][:, size : size + 1]
        total = merged[h][:, size + 1 : size + 2]
        stats = jnp.where(
            lane == 0, row_dot, jnp.where(lane == 1, top, jnp.where(lane == 2, total, 0.0))
        )
        spread[h] = jnp.concatenate([g_mixed, stats], axis=1)
    g_middle = [jnp.zeros((LANDMARKS, LANDMARKS), F32) for _ in heads]
    for turn in reversed(range(NEWTON)):
        approx = [kept_v[turn, h] for h in heads]
        product = [kept_p[turn, h] for h in heads]
        first = [7.0 * one - p for p in product]
        second = [kept_b[turn, h] for h in heads]
        third = [kept_c[turn, h] for h in heads]
        g_third = [0.25 * dot_high(approx[h].T, g_approx[h]) for h in heads]
        g_back = [0.25 * dot_high_nt(g_approx[h], third[h]) for h in heads]
        g_product = [-dot_high_nt(g_third[h], second[h]) for h in heads]
        pt = [p.T for p in product]
        g_second = [-dot_high(pt[h], g_third[h]) for h in heads]
        g_product = [g_product[h] - dot_high_nt(g_second[h], first[h]) for h in heads]
        g_product = [g_product[h] + dot_high(pt[h], g_second[h]) for h in heads]
        g_middle = [g_middle[h] + dot_high_nt(g_product[h], approx[h]) for h in heads]
        g_approx = [g_back[h] + dot_high(turned[h], g_product[h]) for h in heads]
    for h in heads:
        m = middle[h]
        size_sum = jnp.sum(m * m, keepdims=True)
        g_size = -jnp.sum(g_approx[h] * turned[h], keepdims=True) / (size_sum * size_sum)
        g_m = g_middle[h] + g_approx[h].T / size_sum + 2.0 * g_size * m
        g_scores = m * (g_m - jnp.sum(g_m * m, axis=1, keepdims=True))
        g_lq[h] = dot_high(g_scores, land_k[own[h]].astype(F32))
        g_lk[h] = dot_high(g_scores.T, land_q[own[h]].astype(F32))


def inverse_backward(place, land_q, land_k, merged, grads, *kept):
    heads = grads.shape[0]
    square = jax.ShapeDtypeStruct((heads,) + land_q.shape[1:], F32)
    return pl.pallas_call(
        inverse_back_kernel,
        out_shape=(jax.ShapeDtypeStruct((heads, LANDMARKS, LANES), F32), square, square),
        in_specs=[SCALARS] + whole(8),
        out_specs=tuple(whole(3)),
        compiler_params=PARAMS,
        cost_estimate=lasting(11.5),
        name="inverse_backward",
    )(place, land_q, land_k, merged, grads, *kept)


def first_map(land_k, queries):
    scores = nn(land_k, queries)
    raised = jnp.exp(scores - jnp.max(scores, axis=0, keepdims=True))
    return raised * (1.0 / jnp.sum(raised, axis=0, keepdims=True))


def head_blocks(cells, ends, at):
    rows = cells.shape[1]
    left, right = ends
    return (
        [left[at, :]]
        + [cells[at, i * LANES : (i + 1) * LANES] for i in range(rows // LANES)]
        + [right[at, :]]
    )


def first_conv_kernel(queries, values, left, right, land_k, base, first, conv, ends):
    heads, _, size = land_k.shape
    ends[0] = left[...].T
    ends[1] = right[...].T

    def head(h):
        at = pl.ds(pl.multiple_of(h * size, size), size)
        first[at, :] = first_map(land_k[h], queries[at, :]).astype(BF16)
        blocks = head_blocks(values, (ends.at[0], ends.at[1]), at)
        conv[at, :] = convolved(blocks, band(base[pl.ds(h, 1), :]))

    def pair(i, _):
        head(2 * i)
        head(2 * i + 1)
        return 0

    lax.fori_loop(0, heads // 2, pair, 0)


def first_and_conv(queries, values, left, right, land_k, base):
    width, rows = queries.shape
    return pl.pallas_call(
        first_conv_kernel,
        out_shape=(
            jax.ShapeDtypeStruct((width, rows), BF16),
            jax.ShapeDtypeStruct((width, rows), F32),
        ),
        in_specs=whole(6),
        out_specs=tuple(whole(2)),
        scratch_shapes=[pltpu.VMEM((2, width, LANES), BF16)],
        compiler_params=PARAMS,
        cost_estimate=lasting(8),
        name="first_and_conv",
    )(queries, values, left, right, land_k, base)


def context_rows(first, conv, land_out, context):
    heads, _, size = land_out.shape

    def head(h):
        at = pl.ds(pl.multiple_of(h * size, size), size)
        return (nn(land_out[h].T, first[at, :]) + conv[at, :]).astype(BF16)

    def pair(i, _):
        both = jnp.concatenate([head(2 * i), head(2 * i + 1)], axis=0)
        context[:, pl.ds(pl.multiple_of(i * LANES, LANES), LANES)] = both.T
        return 0

    lax.fori_loop(0, heads // 2, pair, 0)


def attention_back_kernel(
    place, queries, grads, land_k, land_out, kept, sent, g_lk, g_query
):
    heads, _, size = land_k.shape
    rows = queries.shape[1]
    owners = 2 * kept.shape[0]
    scaled = jnp.where(live_lanes(place, rows), 64**-0.25, 0.0)

    def pair(i, _):
        lanes = pl.ds(pl.multiple_of(i * LANES, LANES), LANES)
        turned = grads[:, lanes].T
        g_queries, g_keys = [], []
        for side in range(2):
            h = 2 * i + side
            query = queries[pl.ds(pl.multiple_of(h * size, size), size), :]
            g_context = turned[side * size : (side + 1) * size]
            first = first_map(land_k[h], query)
            g_first = nn(land_out[h], g_context)
            inner = jnp.sum(g_first * first, axis=0, keepdims=True)
            g_scores = (first * (g_first - inner)).astype(BF16)
            g_land = nt(first.astype(BF16), g_context)
            g_key = nt(g_scores, query)
            by_owner(place, h, owners, kept, sent, jnp.concatenate([g_land, g_key], axis=1))
            g_keys.append(g_key)
            g_queries.append((scaled * nn(land_k[h].T, g_scores)).astype(BF16))
        g_query[:, lanes] = jnp.concatenate(g_queries, axis=0).T
        g_lk[:, lanes] = jnp.concatenate(g_keys, axis=1)
        return 0

    lax.fori_loop(0, heads // 2, pair, 0)


def attention_back(place, queries, grads, land_k, land_out, owners):
    width, rows = queries.shape
    heads = land_k.shape[0]
    return pl.pallas_call(
        attention_back_kernel,
        out_shape=owner_parts(heads, owners)
        + (
            jax.ShapeDtypeStruct((LANDMARKS, width), F32),
            jax.ShapeDtypeStruct((rows, width), BF16),
        ),
        in_specs=[SCALARS] + whole(4),
        out_specs=tuple(whole(4)),
        compiler_params=PARAMS,
        cost_estimate=lasting(11.4),
        name="attention_back",
    )(place, queries, grads, land_k, land_out)


def conv_back_kernel(
    v_plain, v_left, v_right, grads, g_left, g_right, base_back, g_value, g_taps, ends
):
    heads = g_taps.shape[0]
    rows, width = grads.shape
    size = width // heads
    blocks_in = rows // LANES
    row = lax.broadcasted_iota(jnp.int32, (LANES, LANES), 0)
    column = lax.broadcasted_iota(jnp.int32, (LANES, LANES), 1)
    reverse = jnp.where(row + column == LANES - 1, 1.0, 0.0).astype(BF16)
    gap = jnp.concatenate([row - column, row - column], axis=1)
    ends[0] = g_left[...].T
    ends[1] = g_right[...].T

    def pair(i, _):
        lanes = pl.ds(pl.multiple_of(i * LANES, LANES), LANES)
        turned = grads[:, lanes].T
        plain = [v_left[LANES - 16 :, lanes]]
        plain += [v_plain[b * LANES : (b + 1) * LANES, lanes] for b in range(blocks_in)]
        plain += [v_right[:16, lanes]]
        for side in range(2):
            h = 2 * i + side
            at = pl.ds(pl.multiple_of(h * size, size), size)
            g_context = turned[side * size : (side + 1) * size]
            blocks = [ends[0, at, :]]
            blocks += [g_context[:, b * LANES : (b + 1) * LANES] for b in range(blocks_in)]
            blocks += [ends[1, at, :]]
            g_value[at, :] = convolved(blocks, band(base_back[pl.ds(h, 1), :]))

        def around(b):
            prior = plain[0] if b == 0 else plain[b][LANES - 16 :]
            return jnp.concatenate([prior, plain[b + 1], plain[b + 2][:16]], axis=0)

        def by_head(b):
            piece = turned[:, b * LANES : (b + 1) * LANES]
            zero = jnp.zeros_like(piece)
            return jnp.concatenate(
                [jnp.where(row < size, piece, zero), jnp.where(row >= size, piece, zero)], axis=1
            )

        total = jnp.zeros((LANES + 32, 2 * LANES), F32)
        for b in range(0, blocks_in, 2):
            total = total + nn(
                jnp.concatenate([around(b), around(b + 1)], axis=1),
                jnp.concatenate([by_head(b), by_head(b + 1)], axis=0),
            )
        empty = jnp.zeros((LANES - 16, 2 * LANES), F32)
        before, here, after = total[:16], total[16 : 16 + LANES], total[16 + LANES :]
        ring = jnp.where(jnp.abs(gap) <= 16, here, 0.0)
        ring = ring + jnp.where(gap >= LANES - 16, jnp.concatenate([empty, before], axis=0), 0.0)
        ring = ring + jnp.where(gap <= 16 - LANES, jnp.concatenate([after, empty], axis=0), 0.0)
        high, low = split(ring)
        lowest = (ring - high.astype(F32) - low.astype(F32)).astype(BF16)
        flat = nn(reverse, high) + nn(reverse, low) + nn(reverse, lowest)
        for side in range(2):
            straight = pltpu.roll(
                flat[:, side * LANES : (side + 1) * LANES], 0, 1, stride=1, stride_axis=0
            )
            g_taps[pl.ds(2 * i + side, 1), :] = jnp.sum(straight, axis=0, keepdims=True)
        return 0

    lax.fori_loop(0, heads // 2, pair, 0)


def conv_back(v_plain, v_ends, grads, g_ends, base_back):
    rows, width = grads.shape
    heads = base_back.shape[0]
    return pl.pallas_call(
        conv_back_kernel,
        out_shape=(
            jax.ShapeDtypeStruct((width, rows), F32),
            jax.ShapeDtypeStruct((heads, LANES), F32),
        ),
        in_specs=whole(7),
        out_specs=tuple(whole(2)),
        scratch_shapes=[pltpu.VMEM((2, width, LANES), BF16)],
        compiler_params=PARAMS,
        cost_estimate=lasting(13.6),
        name="conv_back",
    )(v_plain, *v_ends, grads, *g_ends, base_back)


def third_back_kernel(
    place, keys, values, land_q, spread, g_conv, lq_mid, lk_mid, g_lk, last, first, taps, turned,
    g_k, g_v, sums, kept, sent,
):
    heads, _, size = land_q.shape
    rows, width = g_k.shape
    own_heads = lq_mid.shape[0]
    scale = 64**-0.25
    sums[LANDMARKS:, :] = jnp.zeros((sums.shape[0] - LANDMARKS, 2 * width), F32)
    sums[LANDMARKS : LANDMARKS + 1, :] = last[...]
    sums[LANDMARKS + 1 : LANDMARKS + 2, :] = first[...]
    for h in range(heads):
        sums[LANDMARKS + 2 : LANDMARKS + 3, h * LANES : (h + 1) * LANES] = taps[h : h + 1, :]

    def mid(part, h):
        at = h - place[3] * own_heads
        mine = (at >= 0) & (at < own_heads) & (place[5] == 0)
        inside = jnp.clip(at, 0, own_heads - 1)
        return jnp.where(mine, part[inside], 0.0)

    live = live_lanes(place, rows)
    live_row = jnp.where(live, 1.0, 0.0)
    scaled_row = live_row * 64**-0.25

    def pair(i, _):
        lanes = pl.ds(pl.multiple_of(i * LANES, LANES), LANES)
        g_keys, g_values, g_lqs, lks = [], [], [], []
        for side in range(2):
            h = 2 * i + side
            at = pl.ds(pl.multiple_of(h * size, size), size)
            key, value = keys[at, :], values[at, :]
            pack = spread[h]
            g_mixed = pack[:, :size]
            row_dot = pack[:, size : size + 1]
            top = pack[:, size + 1 : size + 2]
            total = pack[:, size + 2 : size + 3]
            scores = nn(land_q[h], key)
            third = jnp.where(live, jnp.exp(scores - top), 0.0) * (1.0 / total)
            gm_high, gm_low = split(g_mixed)
            g_third = nn(gm_high, value) + nn(gm_low, value)
            g_high, g_low = split(third * (g_third - row_dot))
            g_lqs.append(nt(g_high, key) + nt(g_low, key) + mid(lq_mid, h))
            lks.append(mid(lk_mid, h))
            turned = land_q[h].T
            g_key = nn(turned, g_high) + nn(turned, g_low)
            g_keys.append((scaled_row * g_key).astype(BF16))
            t_high, t_low = split(third)
            gmt_high, gmt_low = split(g_mixed.T)
            g_value = nn(gmt_high, t_high) + nn(gmt_high, t_low) + nn(gmt_low, t_high)
            g_values.append((live_row * (g_value + g_conv[at, :])).astype(BF16))
        g_k[:, lanes] = jnp.concatenate(g_keys, axis=0).T
        g_v[:, lanes] = jnp.concatenate(g_values, axis=0).T
        sums[:LANDMARKS, lanes] = scale * jnp.concatenate(g_lqs, axis=1)
        key_lanes = pl.ds(pl.multiple_of(width + i * LANES, LANES), LANES)
        sums[:LANDMARKS, key_lanes] = scale * (g_lk[:, lanes] + jnp.concatenate(lks, axis=1))
        return 0

    lax.fori_loop(0, heads // 2, pair, 0)
    for number, cells in enumerate((g_k, g_v)):
        family_grads(turned, cells, place[2] == number, kept, sent)


def third_back(
    place, keys, values, land_q, spread, g_conv, lq_mid, lk_mid, g_lk, last, first, taps, turned, halves
):
    width, rows = keys.shape
    plain = jax.ShapeDtypeStruct((rows, width), BF16)
    return pl.pallas_call(
        third_back_kernel,
        out_shape=(plain, plain, jax.ShapeDtypeStruct((LANDMARKS + 8, 2 * width), F32))
        + (jax.ShapeDtypeStruct((halves, width, width // halves), BF16),) * 2,
        in_specs=[SCALARS] + whole(12),
        out_specs=tuple(whole(5)),
        compiler_params=PARAMS,
        cost_estimate=lasting(17),
        name="third_back",
    )(
        place, keys, values, land_q, spread, g_conv, lq_mid, lk_mid, g_lk, last, first, taps, turned
    )


def centred_rows(rows):
    centred = rows - jnp.mean(rows, axis=1, keepdims=True)
    scale = lax.rsqrt(jnp.mean(centred * centred, axis=1, keepdims=True) + 1e-05)
    return centred * scale, scale


def norm_back(grads, gain, unit, scale):
    scaled = grads * gain
    inner = jnp.mean(scaled * unit, axis=1, keepdims=True)
    return scale * (scaled - jnp.mean(scaled, axis=1, keepdims=True) - unit * inner)


def gelu_pair(hidden):
    share = 0.5 * (1.0 + lax.erf(hidden * 0.7071067811865476))
    density = jnp.exp(-0.5 * hidden * hidden) * 0.3989422804014327
    return hidden * share, share + hidden * density


class Copies:
    def __init__(self, sems):
        self.sems, self.used, self.open = sems, 0, []

    def start(self, source, target):
        copy = pltpu.make_async_copy(source, target, self.sems.at[self.used])
        self.used += 1
        copy.start()
        return copy

    def out(self, source, target):
        self.open.append(self.start(source, target))

    def finish(self):
        for copy in self.open:
            copy.wait()


def weight_grad(turned, cells, halves, which, out):
    ff = cells.shape[1] // halves
    columns = ff // 2
    for half in range(halves):
        from_column = pl.ds(pl.multiple_of(half * ff + which * columns, columns), columns)

        def rows_of(i, at, half=half, from_column=from_column):
            out[half, at, :] = nn(turned[at, :], cells[:, from_column]).astype(BF16)

        each_tile(turned.shape[0], 384, rows_of)


def feed_kernel(
    place, first_in, conv_in, land_out, tokens_in, cotangent_in, weights,
    output_to, context_to, slope_to, g_fed_to, g_second_to, unit_to, scale_to, turned_to, active_to, fed_turned_to, sent_to,
    norm_grads, in_w, down_w, out_w, norms, conv, context, tokens, cotangent,
    low, unit, scales, fed, active, slopes, g_fed, g_fed_turned, normed_turned, output, sent,
    sems,
):
    rows, width = tokens.shape
    halves, _, ff = in_w.shape
    part = out_w.shape[2]
    tile = 256
    copies = Copies(sems)
    context_copies = [copies.start(first_in, g_fed_turned), copies.start(conv_in, conv)]
    early = [
        copies.start(weights.at[:, :, pl.ds(2 * ff, part)], out_w),
        copies.start(tokens_in, tokens),
        copies.start(weights.at[:, :, pl.ds(2 * ff + part, LANES)], norms),
    ]
    in_copy = copies.start(weights.at[:, :, pl.ds(0, ff)], in_w)
    down_copy = copies.start(weights.at[:, :, pl.ds(ff, ff)], down_w)
    cotangent_copy = copies.start(cotangent_in, cotangent)
    for copy in context_copies:
        copy.wait()
    context_rows(g_fed_turned, conv, land_out, context)
    copies.out(context, context_to)
    for copy in early:
        copy.wait()
    columns = norms[0].astype(F32).T
    gain0, gain1 = columns[0:1], columns[1:2]
    shift0, shift1 = columns[2:3], columns[3:4]
    norm_grads[...] = jnp.zeros_like(norm_grads)

    def project(i, at):
        attended = nt(context[at, :part], out_w[0])
        for half in range(1, halves):
            attended = attended + nt(context[at, half * part : (half + 1) * part], out_w[half])
        rows_unit, scale = centred_rows(tokens[at, :].astype(F32) + attended)
        unit[at, :] = rows_unit
        scales[at, :] = jnp.broadcast_to(scale, (tile, LANES))
        normed = (rows_unit * gain0 + shift0).astype(BF16)
        low[at, :] = normed
        normed_turned[:, at] = normed.T

    each_tile(rows, tile, project)
    copies.out(unit, unit_to)
    copies.out(scales, scale_to)
    copies.out(normed_turned, turned_to)
    in_copy.wait()
    big = 512

    def hidden_rows(i, at):
        for half in range(halves):
            value, slope = gelu_pair(nn(low[at, :], in_w[half]))
            active[at, half * ff : (half + 1) * ff] = value.astype(BF16)
            slopes[at, half * ff : (half + 1) * ff] = slope.astype(BF16)

    each_tile(rows, tile, hidden_rows)
    copies.out(slopes, slope_to)
    copies.out(active, active_to)
    down_copy.wait()

    def fed_rows(i, at):
        total = nt(active[at, :ff], down_w[0])
        for half in range(1, halves):
            total = total + nt(active[at, half * ff : (half + 1) * ff], down_w[half])
        fed[at, :] = total

    each_tile(rows, big, fed_rows)
    cotangent_copy.wait()

    def second_norm(i, at):
        normed = unit[at, :] * gain0 + shift0
        unit1, scale1 = centred_rows(normed + fed[at, :])
        position = place[0] + i * tile + lax.broadcasted_iota(jnp.int32, (tile, 1), 0)
        live = jnp.where(position < place[1], 1.0, 0.0)
        output[at, :] = (live * (unit1 * gain1 + shift1)).astype(BF16)
        grads = live * cotangent[at, :].astype(F32)
        norm_grads[:, :width] += jnp.sum(grads * unit1, axis=0, keepdims=True)
        norm_grads[:, width:] += jnp.sum(grads, axis=0, keepdims=True)
        second = norm_back(grads, gain1, unit1, scale1)
        fed[at, :] = second
        g_low = second.astype(BF16)
        g_fed[at, :] = g_low
        g_fed_turned[:, at] = g_low.T

    each_tile(rows, tile, second_norm)
    copies.out(output, output_to)
    copies.out(fed, g_second_to)
    copies.out(g_fed, g_fed_to)
    copies.out(g_fed_turned, fed_turned_to)
    weight_grad(g_fed_turned, active, halves, 1 - place[2], sent)
    copies.out(sent, sent_to)
    copies.finish()


ANYWHERE = pl.BlockSpec(memory_space=pl.ANY)


def feed_forward(place, first, conv, land_out, tokens, cotangent, weights, ff, part):
    rows, width = tokens.shape
    halves = weights.shape[0]
    grad = (halves, width, ff // 2)
    shapes = [
        ((rows, width), BF16), ((rows, width), BF16), ((rows, halves * ff), BF16),
        ((rows, width), BF16), ((rows, width), F32), ((rows, width), F32), ((rows, LANES), F32), ((width, rows), BF16),
        ((rows, halves * ff), BF16), ((width, rows), BF16), (grad, BF16), ((1, 2 * width), F32),
    ]
    scratch = [
        ((halves, width, ff), BF16), ((halves, width, ff), BF16), ((halves, width, part), BF16),
        ((halves, width, LANES), BF16), ((width, rows), F32), ((rows, width), BF16),
        ((rows, width), BF16), ((rows, width), BF16),
        ((rows, width), BF16), ((rows, width), F32), ((rows, LANES), F32), ((rows, width), F32),
        ((rows, halves * ff), BF16), ((rows, halves * ff), BF16), ((rows, width), BF16),
        ((width, rows), BF16), ((width, rows), BF16), ((rows, width), BF16), (grad, BF16),
    ]
    return pl.pallas_call(
        feed_kernel,
        out_shape=tuple(jax.ShapeDtypeStruct(*shape) for shape in shapes),
        in_specs=[SCALARS] + [ANYWHERE] * 2 + whole(1) + [ANYWHERE] * 3,
        out_specs=tuple([ANYWHERE] * 11 + whole(1)),
        scratch_shapes=[pltpu.VMEM(*shape) for shape in scratch]
        + [pltpu.SemaphoreType.DMA((19,))],
        compiler_params=PARAMS,
        cost_estimate=lasting(32),
        name="feed_forward",
    )(place, first, conv, land_out, tokens, cotangent, weights)


def feed_back_kernel(
    place, slope_in, g_fed_in, g_second_in, unit_in, scale_in, turned_in, weights,
    g_first_to, g_context_to, g_hidden_to, sent_to, att_turned_to, norm_grads,
    in_w, down_w, out_w, norms, g_hidden, g_fed, second, unit, scales, normed_turned,
    g_att, g_att_turned, g_context, sent,
    sems,
):
    rows, width = second.shape
    halves, _, ff = in_w.shape
    part = out_w.shape[2]
    tile = 256
    copies = Copies(sems)
    early = [
        copies.start(g_fed_in, g_fed),
        copies.start(weights.at[:, :, pl.ds(ff, ff)], down_w),
        copies.start(slope_in, g_hidden),
    ]
    later = [
        copies.start(turned_in, normed_turned),
        copies.start(weights.at[:, :, pl.ds(0, ff)], in_w),
        copies.start(g_second_in, second),
        copies.start(unit_in, unit),
        copies.start(scale_in, scales),
        copies.start(weights.at[:, :, pl.ds(2 * ff + part, LANES)], norms),
        copies.start(weights.at[:, :, pl.ds(2 * ff, part)], out_w),
    ]
    for copy in early:
        copy.wait()
    norm_grads[...] = jnp.zeros_like(norm_grads)
    big = 512

    def back_rows(i, at):
        for half in range(halves):
            g_act = nn(g_fed[at, :], down_w[half])
            to = slice(half * ff, (half + 1) * ff)
            g_hidden[at, to] = (g_act * g_hidden[at, to].astype(F32)).astype(BF16)

    each_tile(rows, big, back_rows)
    copies.out(g_hidden, g_hidden_to)
    later.pop(0).wait()
    weight_grad(normed_turned, g_hidden, halves, 1 - place[2], sent)
    copies.out(sent, sent_to)
    for copy in later:
        copy.wait()
    gain0 = norms[0].astype(F32).T[0:1]

    def normed_rows(i, at):
        total = second[at, :]
        for half in range(halves):
            total = total + nt(g_hidden[at, half * ff : (half + 1) * ff], in_w[half])
        second[at, :] = total

    each_tile(rows, big, normed_rows)

    def first_norm(i, at):
        grads = second[at, :]
        rows_unit, scale = unit[at, :], scales[at, 0:1]
        norm_grads[:, :width] += jnp.sum(grads * rows_unit, axis=0, keepdims=True)
        norm_grads[:, width:] += jnp.sum(grads, axis=0, keepdims=True)
        first = norm_back(grads, gain0, rows_unit, scale)
        second[at, :] = first
        low = first.astype(BF16)
        g_att[at, :] = low
        g_att_turned[:, at] = low.T

    each_tile(rows, tile, first_norm)
    copies.out(second, g_first_to)
    copies.out(g_att_turned, att_turned_to)
    for half in range(halves):
        g_context[:, half * part : (half + 1) * part] = nn(g_att[...], out_w[half]).astype(BF16)
    copies.out(g_context, g_context_to)
    copies.finish()


def feed_backward(place, fed, weights, ff, part):
    rows, width = fed[1].shape
    halves = weights.shape[0]
    grad = (halves, width, ff // 2)
    shapes = [
        ((rows, width), F32), ((rows, width), BF16), ((rows, halves * ff), BF16), (grad, BF16),
        ((width, rows), BF16), ((1, 2 * width), F32),
    ]
    scratch = [
        ((halves, width, ff), BF16), ((halves, width, ff), BF16), ((halves, width, part), BF16),
        ((halves, width, LANES), BF16), ((rows, halves * ff), BF16), ((rows, width), BF16),
        ((rows, width), F32), ((rows, width), F32),
        ((rows, LANES), F32), ((width, rows), BF16),
        ((rows, width), BF16), ((width, rows), BF16), ((rows, width), BF16), (grad, BF16),
    ]
    return pl.pallas_call(
        feed_back_kernel,
        out_shape=tuple(jax.ShapeDtypeStruct(*shape) for shape in shapes),
        in_specs=[SCALARS] + [ANYWHERE] * 7,
        out_specs=tuple([ANYWHERE] * 5 + whole(1)),
        scratch_shapes=[pltpu.VMEM(*shape) for shape in scratch]
        + [pltpu.SemaphoreType.DMA((16,))],
        compiler_params=PARAMS,
        cost_estimate=lasting(27),
        name="feed_backward",
    )(place, *fed, weights)


def kept_kernel(place, turned_in, cells_in, kept, turned, cells, sems):
    halves, width, columns = kept.shape
    ff = 2 * columns
    copies = Copies(sems)
    turned_copy = copies.start(turned_in, turned)
    pieces = []
    for half in range(halves):
        start = pl.multiple_of(half * ff + place[2] * columns, columns)
        pieces.append(copies.start(cells_in.at[:, pl.ds(start, columns)], cells.at[half]))
    turned_copy.wait()
    for half in range(halves):
        pieces[half].wait()

        def rows_of(i, at, half=half):
            kept[half, at, :] = nn(turned[at, :], cells[half]).astype(BF16)

        each_tile(width, 384, rows_of)


def kept_grad(place, turned, cells, halves):
    width, rows = turned.shape
    columns = cells.shape[1] // halves // 2
    return pl.pallas_call(
        kept_kernel,
        out_shape=jax.ShapeDtypeStruct((halves, width, columns), BF16),
        in_specs=[SCALARS] + [ANYWHERE] * 2,
        out_specs=whole(1)[0],
        scratch_shapes=[
            pltpu.VMEM((width, rows), BF16),
            pltpu.VMEM((halves, rows, columns), BF16),
            pltpu.SemaphoreType.DMA((3,)),
        ],
        compiler_params=PARAMS,
        cost_estimate=lasting(5),
        name="kept_grad",
    )(place, turned, cells)


def spread_kernel(place, turned_in, cells_in, other, kept, sent, turned, cells, sems):
    halves, width, columns = other.shape
    ff = 2 * columns
    quarter = columns // 2
    copies = Copies(sems)
    turned_copy = copies.start(turned_in, turned)
    pieces = []
    for half in range(halves):
        start = pl.multiple_of(half * ff + place[2] * columns, columns)
        pieces.append(copies.start(cells_in.at[:, pl.ds(start, columns)], cells.at[half]))
    turned_copy.wait()
    for half in range(halves):
        pieces[half].wait()

        def rows_of(i, at, half=half):
            total = nn(turned[at, :], cells[half]) + other[half, at, :].astype(F32)
            low = total.astype(BF16)
            first = place[4] == 0
            kept[half, at, :] = jnp.where(first, low[:, :quarter], low[:, quarter:])
            sent[half, at, :] = jnp.where(first, low[:, quarter:], low[:, :quarter])

        each_tile(width, 384, rows_of)


def spread_grad(place, turned, cells, other):
    halves, width, columns = other.shape
    rows = turned.shape[1]
    part = jax.ShapeDtypeStruct((halves, width, columns // 2), BF16)
    return pl.pallas_call(
        spread_kernel,
        out_shape=(part, part),
        in_specs=[SCALARS] + [ANYWHERE] * 2 + whole(1),
        out_specs=tuple(whole(2)),
        scratch_shapes=[
            pltpu.VMEM((width, rows), BF16),
            pltpu.VMEM((halves, rows, columns), BF16),
            pltpu.SemaphoreType.DMA((3,)),
        ],
        compiler_params=PARAMS,
        cost_estimate=lasting(6),
        name="spread_grad",
    )(place, turned, cells, other)


def pair_kernel(
    place, one_turned_in, one_cells_in, two_turned_in, two_cells_in, kept, sent,
    one_turned, one_cells, two_turned, two_cells, sems,
):
    copies = Copies(sems)
    loads = [
        copies.start(*pair)
        for pair in (
            (one_turned_in, one_turned), (one_cells_in, one_cells),
            (two_turned_in, two_turned), (two_cells_in, two_cells),
        )
    ]
    for number, (turned, cells) in enumerate(((one_turned, one_cells), (two_turned, two_cells))):
        loads[2 * number].wait()
        loads[2 * number + 1].wait()
        family_grads(turned, cells, place[2] == number, kept, sent)


def pair_grads(place, one_turned, one_cells, two_turned, two_cells, halves):
    width, rows = one_turned.shape
    shape = jax.ShapeDtypeStruct((halves, width, one_cells.shape[1] // halves), BF16)
    return pl.pallas_call(
        pair_kernel,
        out_shape=(shape, shape),
        in_specs=[SCALARS] + [ANYWHERE] * 4,
        out_specs=tuple(whole(2)),
        scratch_shapes=[
            pltpu.VMEM((width, rows), BF16), pltpu.VMEM(one_cells.shape, BF16),
            pltpu.VMEM((width, rows), BF16), pltpu.VMEM(one_cells.shape, BF16),
            pltpu.SemaphoreType.DMA((4,)),
        ],
        compiler_params=PARAMS,
        cost_estimate=lasting(6),
        name="pair_grads",
    )(place, one_turned, one_cells, two_turned, two_cells)


def rank_kernel(place, mine, got, land_tokens, weights, late, through, small):
    halves, width, _ = weights.shape
    part = late.shape[1] // 2
    first = place[2] == 0
    grads = (
        jnp.where(first, mine[:LANDMARKS], got[:LANDMARKS]),
        jnp.where(first, got[:LANDMARKS], mine[:LANDMARKS]),
    )
    counts = landmark_counts(place)
    total = jnp.zeros((2 * LANDMARKS, width), F32)
    for index, grad in enumerate(grads):
        both = jnp.concatenate(split(grad / counts), axis=0)
        for half in range(halves):
            weight = weights[half, :, index * part : (index + 1) * part]
            total = total + nt(both[:, half * part : (half + 1) * part], weight)
    through[...] = jnp.concatenate(split(total[:LANDMARKS] + total[LANDMARKS:]), axis=0)
    zero = jnp.zeros((LANDMARKS, part), F32)
    own = []
    for index, grad in enumerate(grads):
        columns = grad[:, :part]
        for half in range(1, halves):
            columns = jnp.where(place[5] == half, grad[:, half * part : (half + 1) * part], columns)
        own.append(jnp.where(place[2] == 1 - index, columns, zero))
    high, low = split(jnp.concatenate(own, axis=1))
    mean_high, mean_low = split(land_tokens[...] / counts)
    means = jnp.concatenate([mean_high, mean_low, mean_high, jnp.zeros_like(mean_low)], axis=0).T
    factors = jnp.concatenate([high, high, low, jnp.zeros_like(low)], axis=0)
    late[...] = nn(means, factors).astype(BF16)
    gains = jnp.where(first, mine[LANDMARKS:], got[LANDMARKS:])
    shifts = jnp.where(first, got[LANDMARKS:], mine[LANDMARKS:])
    taps = jnp.where(place[5] == 0, gains[2:3], shifts[2:3])
    rows = [gains[1:2], gains[0:1], shifts[1:2], shifts[0:1], taps]
    rows.append(jnp.zeros((small.shape[0] - len(rows), width), F32))
    small[...] = jnp.concatenate(rows, axis=0).astype(BF16)


def rank_parts(place, mine, got, land_tokens, weights):
    halves, width, packed = weights.shape
    return pl.pallas_call(
        rank_kernel,
        out_shape=(
            jax.ShapeDtypeStruct((width, 2 * packed // 3), BF16),
            jax.ShapeDtypeStruct((2 * LANDMARKS, width), BF16),
            jax.ShapeDtypeStruct((16, width), BF16),
        ),
        in_specs=[SCALARS] + whole(4),
        out_specs=tuple(whole(3)),
        compiler_params=PARAMS,
        cost_estimate=lasting(4),
        name="rank_parts",
    )(place, mine, got, land_tokens, weights)


def token_grad_kernel(
    back_in, g_k_in, g_v_in, weights, own_grad, back, g_k, g_v, k_w, v_w, sems
):
    rows, width = back.shape
    halves, _, part = k_w.shape
    copies = Copies(sems)
    first = [
        copies.start(g_k_in, g_k),
        copies.start(weights.at[:, :, pl.ds(part, part)], k_w),
    ]
    later = [
        copies.start(back_in, back),
        copies.start(g_v_in, g_v),
        copies.start(weights.at[:, :, pl.ds(2 * part, part)], v_w),
    ]
    for copy in first + later:
        copy.wait()

    def rows_of(i, at):
        total = back[at, :]
        for half in range(halves):
            columns = slice(half * part, (half + 1) * part)
            total = total + nt(g_k[at, columns], k_w[half]) + nt(g_v[at, columns], v_w[half])
        own_grad[at, :] = total.astype(BF16)

    each_tile(rows, 512, rows_of)


def token_grad(back, g_k, g_v, weights):
    rows, width = back.shape
    halves, _, packed = weights.shape
    shapes = [((rows, width), F32), ((rows, width), BF16), ((rows, width), BF16)]
    shapes += [((halves, width, packed // 3), BF16)] * 2
    return pl.pallas_call(
        token_grad_kernel,
        out_shape=jax.ShapeDtypeStruct((rows, width), BF16),
        in_specs=[ANYWHERE] * 4,
        out_specs=whole(1)[0],
        scratch_shapes=[pltpu.VMEM(*shape) for shape in shapes]
        + [pltpu.SemaphoreType.DMA((5,))],
        compiler_params=PARAMS,
        cost_estimate=lasting(6),
        name="token_grad",
    )(back, g_k, g_v, weights)


def flipped(values, axis, bit):
    count = lax.axis_size(axis)
    return lax.ppermute(values, axis, [(i, i ^ bit) for i in range(count)])


def side_of(axis, bit):
    return (lax.axis_index(axis) // bit) % 2


def paired(mine, axis, bit, dim):
    other = flipped(mine, axis, bit)
    both = jnp.zeros(mine.shape[:dim] + (2,) + mine.shape[dim:], mine.dtype)
    side = side_of(axis, bit)
    both = lax.dynamic_update_slice_in_dim(both, jnp.expand_dims(mine, dim), side, dim)
    return lax.dynamic_update_slice_in_dim(both, jnp.expand_dims(other, dim), 1 - side, dim)


def ctx_bits():
    bits, bit = [], 1
    while bit < lax.axis_size("ctx"):
        bits.append(bit)
        bit *= 2
    return bits


def sequence_start(values):
    width = values.shape[1] // 2
    side = side_of("ctx", 1)
    kept = lax.dynamic_slice_in_dim(values, side * width, width, axis=1)
    sent = lax.dynamic_slice_in_dim(values, (1 - side) * width, width, axis=1)
    kept = kept + flipped(sent, "ctx", 1)
    return kept + flipped(kept, "tp", 1)


def sequence_end(kept):
    for bit in ctx_bits()[1:]:
        kept = kept + flipped(kept, "ctx", bit)
    return kept, flipped(kept, "ctx", 1)


def joined_halves(kept, other):
    return jnp.where(
        side_of("ctx", 1) == 0,
        jnp.concatenate([kept, other], axis=1),
        jnp.concatenate([other, kept], axis=1),
    )


def to_owner(kept, sent, combine):
    kept = combine(kept, flipped(sent, "ctx", 1))
    for bit in ctx_bits()[1:]:
        view = kept.reshape((-1, 2) + kept.shape[1:])
        side = side_of("ctx", bit)
        sent = lax.dynamic_index_in_dim(view, 1 - side, 1, False)
        kept = lax.dynamic_index_in_dim(view, side, 1, False)
        kept = combine(kept, flipped(sent, "ctx", bit))
    return kept[0], flipped(kept[0], "tp", 1)


def from_owners(part):
    whole_part = part[None]
    for bit in reversed(ctx_bits()):
        both = paired(whole_part, "ctx", bit, 1)
        whole_part = both.reshape((-1,) + part.shape)
    return whole_part.reshape((-1,) + part.shape[1:])


def merge_keys(one, two):
    size = LANES // 2
    one_top, two_top = one[..., size : size + 1], two[..., size : size + 1]
    top = jnp.maximum(one_top, two_top)
    one_factor, two_factor = jnp.exp(one_top - top), jnp.exp(two_top - top)
    summed = one * one_factor + two * two_factor
    lane = lax.broadcasted_iota(jnp.int32, summed.shape, summed.ndim - 1)
    return jnp.where(lane == size, top, summed)


def neighbour_rows(cells, count):
    pieces = lax.axis_size("ctx") * lax.axis_size("tp")
    up = [(i, i + 1) for i in range(pieces - 1)]
    before = lax.ppermute(cells[-count:], ("ctx", "tp"), up)
    after = lax.ppermute(cells[:count], ("ctx", "tp"), [(j, i) for i, j in up])
    return (
        jnp.pad(before, ((LANES - count, 0), (0, 0))),
        jnp.pad(after, ((0, LANES - count), (0, 0))),
    )


def own_quarter(shard):
    rows = shard.shape[0] // lax.axis_size("ctx")
    return lax.dynamic_slice_in_dim(shard, lax.axis_index("ctx") * rows, rows, axis=0)


def gathered(shard):
    full = lax.all_gather(own_quarter(shard), ("tp", "fsdp", "ctx"), tiled=True)
    return full.reshape(lax.axis_size("tp"), -1, shard.shape[1])


def gathered_early(shard, beside):
    count = lax.axis_size("fsdp")
    piece = own_quarter(shard)
    if count > 4:
        held = lax.all_gather(piece, "fsdp")
    else:
        here = lax.axis_index("fsdp")
        held = jnp.zeros((count,) + piece.shape, piece.dtype)
        held = lax.dynamic_update_slice_in_dim(held, piece[None], here, 0)
        for step in range(1, count):
            moved = lax.ppermute(piece, "fsdp", [(i, (i + step) % count) for i in range(count)])
            held = lax.dynamic_update_slice_in_dim(held, moved[None], (here - step) % count, 0)
    held, beside = gate(held, beside)
    bits = ctx_bits()
    halves = []
    for number, half in enumerate((held[: count // 4], held[count // 4 :])):
        half = half[None]
        if number == 0:
            half = paired(half[0], "tp", 1, 0)
        for place, bit in enumerate(reversed(bits[1:])):
            half = paired(half, "ctx", bit, 2 + place)
        if number == 1:
            half = paired(half[0], "tp", 1, 0)
        halves.append(paired(half, "ctx", bits[0], 1 + len(bits)))
    full = jnp.concatenate(halves, axis=1)
    return full.reshape(lax.axis_size("tp"), -1, shard.shape[1]), beside


def bits_of(axis):
    bits, bit = [], lax.axis_size(axis) // 2
    while bit:
        bits.append(bit)
        bit //= 2
    return bits


def added(*parts):
    return sum(part.astype(F32) for part in parts).astype(BF16)


def cut(cells, axis, bit, dim):
    size = cells.shape[dim] // 2
    side = side_of(axis, bit)
    return (
        lax.dynamic_slice_in_dim(cells, side * size, size, axis=dim),
        lax.dynamic_slice_in_dim(cells, (1 - side) * size, size, axis=dim),
    )


def gate(*values):
    return lax.optimization_barrier(values)


def dotf(spec, *operands):
    return jnp.einsum(spec, *operands, preferred_element_type=F32)


def taps_round(taps):
    middle = taps.shape[1] // 2
    gap = jnp.zeros((taps.shape[0], LANES - taps.shape[1]), F32)
    return jnp.concatenate([taps[:, middle::-1], gap, taps[:, :middle:-1]], axis=1)


def landmark_bounds(length):
    landmark = jnp.arange(LANDMARKS + 1, dtype=jnp.int32)
    return (landmark * length + LANDMARKS - 1) // LANDMARKS


def landmark_counts_of(length):
    bounds = landmark_bounds(length)
    return (bounds[1:] - bounds[:-1]).astype(F32)[:, None]


def landmark_rows(position, length):
    bounds = landmark_bounds(length)
    inside = (position[:, None] >= bounds[None, :-1]) & (position[:, None] < bounds[None, 1:])
    return inside.astype(BF16)


def on_device(
    tokens,
    lengths,
    qk_weight,
    value_weight,
    out_weight,
    in_weight,
    down_weight,
    norm_gains,
    norm_shifts,
    conv_weight,
    cotangent,
):
    tp_count = lax.axis_size("tp")
    tp_index = lax.axis_index("tp")
    ctx_index = lax.axis_index("ctx")
    _, slot_len, model_width = tokens.shape
    rows = slot_len // tp_count
    local_heads, tap_count = conv_weight.shape
    local_width = value_weight.shape[1]
    ff_width = in_weight.shape[1]
    head_size = local_width // local_heads
    heads = local_heads * tp_count
    owners = lax.axis_size("ctx")
    own_heads = heads // owners
    width = local_width * tp_count
    radius = tap_count // 2
    length = lengths[0]

    first_row = (ctx_index * tp_count + tp_index) * rows
    sides = (side_of("ctx", 1), ctx_index, side_of("ctx", ctx_bits()[-1]), tp_index)
    place = jnp.stack([first_row, length, *sides]).astype(jnp.int32)

    norm_columns = jnp.concatenate([norm_gains, norm_shifts], axis=0).T
    norm_columns = jnp.pad(norm_columns, ((0, 0), (0, LANES - norm_columns.shape[1])))
    ffn_full = gathered(
        jnp.concatenate([in_weight, down_weight.T, out_weight.T, norm_columns], axis=1)
    )
    own_taps = jnp.where(ctx_index == 0, conv_weight.astype(F32), 0.0)
    tap_rows = jnp.pad(own_taps, ((0, 8 - local_heads), (0, LANES - tap_count)))
    tap_rows = jnp.where(
        jnp.arange(model_width) // LANES == tp_index,
        jnp.tile(tap_rows, (1, model_width // LANES)),
        0.0,
    )
    own = lax.dynamic_slice_in_dim(tokens[0], tp_index * rows, rows, axis=0)
    land_tokens = sequence_start(jnp.concatenate([token_sums(place, own), tap_rows], axis=0))
    qkv_full, land_tokens = gathered_early(
        jnp.concatenate([qk_weight[0], qk_weight[1], value_weight], axis=1), land_tokens
    )
    land_tokens = joined_halves(*sequence_end(land_tokens))
    own_cotangent = lax.dynamic_slice_in_dim(cotangent[0], tp_index * rows, rows, axis=0)
    tap_weights = land_tokens[LANDMARKS : LANDMARKS + local_heads, : tp_count * LANES]
    tap_weights = tap_weights.reshape(local_heads, tp_count, LANES).transpose(1, 0, 2)
    tap_weights = tap_weights.reshape(heads, LANES)[:, :tap_count]
    land_tokens = land_tokens[:LANDMARKS]
    base, base_back = taps_round(tap_weights), taps_round(tap_weights[:, ::-1])

    queries, keys, values, v_plain, land_q, land_k, own_turned, *parts_of_third = projections(
        place, own, land_tokens, qkv_full, head_size, owners
    )
    v_ends = neighbour_rows(v_plain, radius)
    merged, merged_tp = to_owner(*parts_of_third, merge_keys)
    kept_turns = inverse_forward(place, land_q, land_k, owners)
    first, conv = first_and_conv(queries, values, *v_ends, land_k, base)
    merged, own_out = landmark_out(merged, merged_tp, kept_turns[0])
    land_out = from_owners(own_out)

    own_output, context, *fed, active, fed_turned, down_sent, last_norm = feed_forward(
        place, first, conv, land_out, own, own_cotangent, ffn_full, ff_width, local_width
    )
    high = ctx_bits()[-1]
    owner_count = lax.axis_size("fsdp")
    owner_rows = model_width // owner_count
    near, *farther = bits_of("fsdp")[::-1]

    def by_owner_bits(cells):
        return cells.reshape((2,) * (1 + len(farther)) + (-1, cells.shape[-1]))

    def cut_last(cells, bit):
        dim = cells.ndim - 3
        return tuple(piece.squeeze(dim) for piece in cut(cells, "fsdp", bit, dim))

    other_output = flipped(own_output, "tp", 1)
    down_other = flipped(down_sent, "ctx", 1)
    down_kept = kept_grad(place, fed_turned, active, tp_count)
    down_kept, down_other = gate(down_kept, down_other)
    down_mine, down_theirs = cut(down_kept, "ctx", high, 2)
    other_mine, other_theirs = cut(down_other, "ctx", high, 2)
    down_sent = added(down_theirs, other_theirs)
    down_got = flipped(down_sent, "ctx", high)
    fed[0], down_sent = gate(fed[0], down_sent)
    grad_first_res, grad_context, g_hidden, in_sent, att_turned, first_norm = feed_backward(
        place, fed, ffn_full, ff_width, local_width
    )
    in_sent, grad_context, g_hidden, other_output, down_got = gate(
        in_sent, grad_context, g_hidden, other_output, down_got
    )
    in_other = flipped(in_sent, "ctx", 1)
    g_ends = neighbour_rows(grad_context, radius)
    down = added(down_mine, other_mine, down_got)
    down_mine, down_sent = cut(down, "tp", 1, 0)
    down_got = flipped(down_sent, "tp", 1)
    grad_context, down_sent = gate(grad_context, down_sent)
    land_kept, land_sent, g_lk, g_q = attention_back(
        place, queries, grad_context, land_k, land_out, owners
    )
    land_kept, land_sent, in_other, g_ends = gate(land_kept, land_sent, in_other, g_ends)

    land_other = flipped(land_sent, "ctx", 1)
    in_kept, in_sent = spread_grad(place, fed[5], g_hidden, in_other)
    in_kept, in_sent, land_other, down_got = gate(in_kept, in_sent, land_other, down_got)
    land_grads = land_kept + land_other
    land_mine, land_theirs = cut(land_grads, "ctx", high, 0)
    land_got = flipped(land_theirs, "ctx", high)
    land_theirs, in_sent = gate(land_theirs, in_sent)
    in_got = flipped(in_sent, "ctx", high)
    down = added(down_mine, down_got)
    grad_context, in_sent = gate(grad_context, in_sent)
    g_conv, g_taps = conv_back(v_plain, v_ends, grad_context, g_ends, base_back)
    g_conv, g_taps, land_got = gate(g_conv, g_taps, land_got)
    own_grads = (land_mine + land_got)[0]
    tp_grads = flipped(own_grads, "tp", 1)

    def parts(cells):
        return cells.reshape(rows, tp_count, local_width)

    def qkv_part(index):
        return qkv_full[:, :, index * local_width : (index + 1) * local_width]

    g_q, own_grads = gate(g_q, own_grads)
    mixed_kept, mixed_sent = pair_grads(place, att_turned, context, own_turned, g_q, tp_count)
    back_q = grad_first_res + dotf("tpk,pck->tc", parts(g_q), qkv_part(0))
    mixed_kept, mixed_sent, tp_grads, back_q = gate(mixed_kept, mixed_sent, tp_grads, back_q)
    mixed_got = flipped(mixed_sent, "ctx", 1)
    own_grads, mixed_sent = gate(own_grads + tp_grads, mixed_sent)
    spread, lq_mid, lk_mid = inverse_backward(
        place, land_q, land_k, merged, own_grads, *kept_turns
    )
    spread, in_got, mixed_got = gate(spread, in_got, mixed_got)
    spread = from_owners(spread)

    in_mine, in_sent = cut(added(in_kept, in_got), "tp", 1, 0)
    in_got = flipped(in_sent, "tp", 1)
    def by_ctx(cells):
        return cells.reshape(tp_count, owner_count, 2, -1, local_width)

    mixed = added(mixed_kept, mixed_got)
    mixed_mine, mixed_sent = cut(by_ctx(mixed), "ctx", high, 2)
    mixed_got = flipped(mixed_sent, "ctx", high)
    spread, in_sent, mixed_sent = gate(spread, in_sent, mixed_sent)
    g_k, g_v, sums, kv_kept, kv_sent = third_back(
        place, keys, values, land_q, spread, g_conv, lq_mid, lk_mid, g_lk, last_norm, first_norm,
        g_taps, own_turned, tp_count,
    )

    kv_kept, kv_sent, sums, in_got, mixed_got = gate(kv_kept, kv_sent, sums, in_got, mixed_got)
    kv_got = flipped(kv_sent, "ctx", 1)
    sums_mine, sums_sent = cut(sums, "ctx", 1, 1)
    sums_got = flipped(sums_sent, "ctx", 1)
    kv_kept, kv_got = gate(kv_kept, kv_got)
    kv_mine, kv_sent = cut(by_ctx(added(kv_kept, kv_got)), "ctx", high, 2)
    kv_sent, sums_mine, mixed_mine, in_mine, g_k = gate(
        kv_sent, sums_mine, mixed_mine, in_mine, g_k
    )
    kv_got = flipped(kv_sent, "ctx", high)
    sums = sums_mine + sums_got
    sums_got = flipped(sums, "tp", 1)
    mixed_mine, mixed_sent = cut(added(mixed_mine, mixed_got), "tp", 1, 0)
    sums, mixed_sent, in_mine = gate(sums, mixed_sent, in_mine)
    mixed_got = flipped(mixed_sent, "tp", 1)
    pair = jnp.concatenate([added(in_mine, in_got)[0], down[0]], axis=1)
    g_k, mixed_sent, pair, sums_got = gate(g_k, mixed_sent, pair, sums_got)
    sums = sums + sums_got
    g_k, sums = gate(g_k, sums)
    sums_got = flipped(sums, "ctx", high)
    pair = lax.psum_scatter(pair, "fsdp", scatter_dimension=0, tiled=True)
    own_grad = token_grad(back_q, g_k, g_v, qkv_full)
    first_rows = 3 * rows // 16
    other_first = flipped(own_grad[:first_rows], "tp", 1)
    own_grad, other_first, sums_got, mixed_got, kv_got = gate(
        own_grad, other_first, sums_got, mixed_got, kv_got
    )
    kv_mine, kv_sent = cut(added(kv_mine, kv_got), "tp", 1, 0)
    own_grad, sums, kv_sent = gate(own_grad, sums, kv_sent)
    kv_got = flipped(kv_sent, "tp", 1)
    other_second = flipped(own_grad[first_rows:], "tp", 1)
    sums = sums + sums_got
    sums_got = flipped(sums, "ctx", 1)
    sums, sums_got, kv_got = gate(sums, sums_got, kv_got)
    late, through, small = rank_parts(place, sums, sums_got, land_tokens, qkv_full)
    late, through, small, own_output, other_output = gate(
        late, through, small, own_output, other_output
    )
    late = late.reshape(owner_count, 2, -1, 2 * local_width)
    late = lax.dynamic_index_in_dim(late, place[4], 1, False)
    mixed = added(
        jnp.concatenate([mixed_mine, kv_mine], axis=-1).reshape(late.shape),
        jnp.concatenate([mixed_got, kv_got], axis=-1).reshape(late.shape),
        late,
    )
    small = jnp.broadcast_to(small[None], (owner_count,) + small.shape)
    mixed = by_owner_bits(jnp.concatenate([mixed, small], axis=1))
    mixed_mine, mixed_sent = cut_last(mixed, near)
    mixed_sent, pair = gate(mixed_sent, pair)
    mixed_got = flipped(mixed_sent, "fsdp", near)
    mixed = added(mixed_mine, mixed_got)
    for bit in farther:
        mixed_mine, mixed_sent = cut_last(mixed, bit)
        mixed = added(mixed_mine, flipped(mixed_sent, "fsdp", bit))
    small = mixed[-16:].astype(F32)
    mixed = mixed[:-16]

    def of_core(cells, core):
        cells = cells.reshape((owners // 2, 2) + cells.shape[1:])
        return [cells[i, core] for i in range(owners // 2)]

    mixed, other_second = gate(mixed, other_second)
    mixed = from_owners(mixed[None])
    sides = [jnp.concatenate(of_core(mixed, core), axis=0).astype(F32) for core in range(2)]
    grad_out, grad_k = sides[0][:, :local_width].T, sides[0][:, local_width:]
    grad_q, grad_v = sides[1][:, :local_width], sides[1][:, local_width:]

    own_columns = lax.axis_index("fsdp") * owner_rows
    norm_sums = lax.dynamic_slice_in_dim(small[:4], own_columns, owner_rows, axis=1)
    taps_sum = small[4].reshape(local_heads, LANES)
    grad_taps = jnp.concatenate(
        [taps_sum[:, radius - 1 :: -1], taps_sum[:, : -radius - 2 : -1]], axis=1
    )

    columns = pair.shape[1] // 2
    pair = from_owners(pair[None])
    pieces = [piece for core in range(2) for piece in of_core(pair, core)]
    grad_in = jnp.concatenate([piece[:, :columns] for piece in pieces], axis=1).astype(F32)
    grad_down = jnp.concatenate([piece[:, columns:] for piece in pieces], axis=1).astype(F32).T

    output = jnp.where(
        tp_index == 0,
        jnp.concatenate([own_output, other_output]),
        jnp.concatenate([other_output, own_output]),
    )[None]
    both_grads = jnp.where(
        tp_index == 0,
        jnp.concatenate([own_grad, other_first, other_second]),
        jnp.concatenate([other_first, other_second, own_grad]),
    )
    position = ctx_index * slot_len + jnp.arange(slot_len, dtype=jnp.int32)
    onehot = landmark_rows(position, length)
    grad_tokens = both_grads.astype(F32) + dotf(
        "tm,mc->tc", jnp.concatenate([onehot, onehot], axis=1), through
    )
    grad_tokens = grad_tokens.reshape(1, slot_len, model_width)
    return (
        output,
        grad_tokens,
        jnp.stack([grad_q, grad_k]),
        grad_v,
        grad_out,
        grad_in,
        grad_down,
        norm_sums[:2],
        norm_sums[2:],
        grad_taps,
    )


def solution(mesh):
    in_specs = (
        P("fsdp", "ctx", None),
        P("fsdp"),
        P(None, "fsdp", "tp"),
        P("fsdp", "tp"),
        P("tp", "fsdp"),
        P("fsdp", "tp"),
        P("tp", "fsdp"),
        P(None, "fsdp"),
        P(None, "fsdp"),
        P("tp", None),
        P("fsdp", "ctx", None),
    )
    out_specs = (
        P("fsdp", "ctx", None),
        P("fsdp", "ctx", None),
        P(None, "fsdp", "tp"),
        P("fsdp", "tp"),
        P("tp", "fsdp"),
        P("fsdp", "tp"),
        P("tp", "fsdp"),
        P(None, "fsdp"),
        P(None, "fsdp"),
        P("tp", None),
    )
    return jax.shard_map(
        on_device, mesh=mesh, in_specs=in_specs, out_specs=out_specs, check_vma=False
    )
```

```python
import jax
import jax.numpy as jnp
from jax import lax
from jax.experimental import pallas as pl
from jax.experimental.pallas import tpu as pltpu
from jax.sharding import PartitionSpec as P

LANDMARKS = 64
NEWTON = 6
LANES = 128
VMEM_BYTES = 56 * 2**20

HIGH = lax.Precision.HIGHEST
F32 = jnp.float32
BF16 = jnp.bfloat16


def lasting(microseconds):
    return pl.CostEstimate(
        flops=int(microseconds * 1.1535e9), bytes_accessed=int(microseconds * 1e5), transcendentals=0
    )


def nn(left, right):
    return jnp.dot(left, right, preferred_element_type=F32)


def nt(left, right):
    return lax.dot_general(left, right, (((1,), (1,)), ((), ())), preferred_element_type=F32)


def split(wide):
    high = wide.astype(BF16)
    return high, (wide - high.astype(F32)).astype(BF16)


def each_tile(count, tile, body):
    def step(i, _):
        body(i, pl.ds(pl.multiple_of(i * tile, tile), tile))
        return 0

    lax.fori_loop(0, count // tile, step, 0)


def family_grads(turned, cells, mine, kept, sent):
    halves, width, columns = kept.shape

    def rows_of(i, at):
        total = nn(turned[at, :], cells[...]).astype(BF16)

        @pl.when(mine)
        def _():
            for half in range(halves):
                kept[half, at, :] = total[:, half * columns : (half + 1) * columns]

        @pl.when(jnp.logical_not(mine))
        def _():
            for half in range(halves):
                sent[half, at, :] = total[:, half * columns : (half + 1) * columns]

    each_tile(width, 384, rows_of)


def whole(count):
    return [pl.BlockSpec(memory_space=pltpu.VMEM)] * count


SCALARS = pl.BlockSpec(memory_space=pltpu.SMEM)
PARAMS = pltpu.CompilerParams(vmem_limit_bytes=VMEM_BYTES)


def landmark_onehot(place, rows, landmark_axis):
    shape = (LANDMARKS, rows) if landmark_axis == 0 else (rows, LANDMARKS)
    landmark = lax.broadcasted_iota(jnp.int32, shape, landmark_axis)
    position = place[0] + lax.broadcasted_iota(jnp.int32, shape, 1 - landmark_axis)
    start = lax.shift_right_logical(landmark * place[1] + (LANDMARKS - 1), 6)
    end = lax.shift_right_logical((landmark + 1) * place[1] + (LANDMARKS - 1), 6)
    return jnp.where((position >= start) & (position < end), 1.0, 0.0).astype(BF16)


def live_lanes(place, rows):
    position = place[0] + lax.broadcasted_iota(jnp.int32, (1, rows), 1)
    return position < place[1]


def band(base_row):
    ring = pltpu.roll(jnp.broadcast_to(base_row, (LANES, LANES)), 0, 1, stride=1, stride_axis=0)
    gap = lax.broadcasted_iota(jnp.int32, (LANES, LANES), 0) - lax.broadcasted_iota(
        jnp.int32, (LANES, LANES), 1
    )
    zero = jnp.zeros_like(ring)
    before = jnp.where(gap >= LANES - 16, ring, zero).astype(BF16)
    here = jnp.where(jnp.abs(gap) <= 16, ring, zero).astype(BF16)
    after = jnp.where(gap <= 16 - LANES, ring, zero).astype(BF16)
    return before, here, after


def convolved(blocks, bands):
    count = len(blocks) - 2
    size = blocks[0].shape[0]
    stacked = jnp.concatenate(
        [jnp.concatenate(blocks[i : i + 3], axis=1) for i in range(count)], axis=0
    )
    out = nn(stacked, jnp.concatenate(bands, axis=0))
    return jnp.concatenate([out[i * size : (i + 1) * size] for i in range(count)], axis=1)


def token_sums_kernel(place, tokens, sums):
    sums[...] = nn(landmark_onehot(place, tokens.shape[0], 0), tokens[...])


def token_sums(place, tokens):
    return pl.pallas_call(
        token_sums_kernel,
        out_shape=jax.ShapeDtypeStruct((LANDMARKS, tokens.shape[1]), F32),
        in_specs=[SCALARS] + whole(1),
        out_specs=whole(1)[0],
        compiler_params=PARAMS,
        cost_estimate=lasting(2.5),
        name="token_sums",
    )(place, tokens)


def landmark_counts(place):
    landmark = lax.broadcasted_iota(jnp.int32, (LANDMARKS, 1), 0)
    start = lax.shift_right_logical(landmark * place[1] + (LANDMARKS - 1), 6)
    end = lax.shift_right_logical((landmark + 1) * place[1] + (LANDMARKS - 1), 6)
    return (end - start).astype(F32)


def projection_kernel(
    place, tokens, sums, weights, q_out, k_out, v_out, v_plain, land_q, land_k, turned, kept, sent
):
    rows = tokens.shape[0]
    halves, _, packed = weights.shape
    width = packed // 3
    size = land_q.shape[2]
    position = place[0] + lax.broadcasted_iota(jnp.int32, (rows, 1), 0)
    live = jnp.where(position < place[1], 1.0, 0.0)
    scaled = live * 64**-0.25
    means = jnp.concatenate(split(sums[...] / landmark_counts(place)), axis=0)
    cells = tokens[...]
    turned[...] = cells.T
    for half in range(halves):
        for part, out in enumerate((q_out, k_out, v_out)):
            weight = weights[half, :, part * width : (part + 1) * width]
            low = ((live if part == 2 else scaled) * nn(cells, weight)).astype(BF16)
            out[half * width : (half + 1) * width, :] = low.T
            if part == 2:
                v_plain[:, half * width : (half + 1) * width] = low
                continue
            both = nn(means, weight)
            land = (64**-0.25 * (both[:LANDMARKS] + both[LANDMARKS:])).astype(BF16)
            to = land_k if part else land_q
            for head in range(width // size):
                to[half * (width // size) + head] = land[:, head * size : (head + 1) * size]
    third_heads(place, k_out, v_out, land_q, kept, sent)


def projections(place, tokens, sums, weights, size, owners):
    rows = tokens.shape[0]
    width = weights.shape[0] * weights.shape[2] // 3
    turned = jax.ShapeDtypeStruct((width, rows), BF16)
    land = jax.ShapeDtypeStruct((width // size, LANDMARKS, size), BF16)
    return pl.pallas_call(
        projection_kernel,
        out_shape=(turned, turned, turned, jax.ShapeDtypeStruct((rows, width), BF16), land, land)
        + (jax.ShapeDtypeStruct(tokens.shape[::-1], BF16),)
        + owner_parts(width // size, owners),
        in_specs=[SCALARS] + whole(3),
        out_specs=tuple(whole(9)),
        compiler_params=PARAMS,
        cost_estimate=lasting(18),
        name="projections",
    )(place, tokens, sums, weights)


def by_owner(place, h, owners, kept, sent, values):
    per = kept.shape[1]
    for owner in range(owners):
        @pl.when((h >= owner * per) & (h < (owner + 1) * per))
        def _(owner=owner):
            mine = place[2] == owner % 2

            @pl.when(mine)
            def _():
                kept[owner // 2, h - owner * per] = values

            @pl.when(jnp.logical_not(mine))
            def _():
                sent[owner // 2, h - owner * per] = values


def third_heads(place, keys, values, land_q, kept, sent):
    heads = land_q.shape[0]
    size = land_q.shape[2]
    rows = keys.shape[1]
    owners = 2 * kept.shape[0]
    live = live_lanes(place, rows)

    def head(h):
        at = pl.ds(pl.multiple_of(h * size, size), size)
        scores = jnp.where(live, nn(land_q[h], keys[at, :]), -1e30)
        top = jnp.max(scores, axis=1, keepdims=True)
        raised = jnp.where(live, jnp.exp(scores - top), 0.0)
        total = jnp.sum(raised, axis=1, keepdims=True)
        high, low = split(raised)
        value = values[at, :]
        mixed = nt(high, value) + nt(low, value)
        lane = lax.broadcasted_iota(jnp.int32, (LANDMARKS, LANES - size), 1)
        stats = jnp.where(lane == 0, top, jnp.where(lane == 1, total, 0.0))
        by_owner(place, h, owners, kept, sent, jnp.concatenate([mixed, stats], axis=1))

    def pair(i, _):
        head(2 * i)
        head(2 * i + 1)
        return 0

    lax.fori_loop(0, heads // 2, pair, 0)


def owner_parts(heads, owners):
    part = jax.ShapeDtypeStruct((owners // 2, heads // owners, LANDMARKS, LANES), F32)
    return part, part


def dot_high(left, right):
    return jnp.dot(left, right, preferred_element_type=F32, precision=HIGH)


def dot_high_nt(left, right):
    return lax.dot_general(
        left, right, (((1,), (1,)), ((), ())), preferred_element_type=F32, precision=HIGH
    )


def eye():
    row = lax.broadcasted_iota(jnp.int32, (LANDMARKS, LANDMARKS), 0)
    column = lax.broadcasted_iota(jnp.int32, (LANDMARKS, LANDMARKS), 1)
    return jnp.where(row == column, 1.0, 0.0)


def middle_map(land_q, land_k):
    scores = nt(land_q, land_k)
    raised = jnp.exp(scores - jnp.max(scores, axis=1, keepdims=True))
    return raised / jnp.sum(raised, axis=1, keepdims=True)


def inverse_kernel(place, land_q, land_k, kept_v, kept_p, kept_b, kept_c):
    heads = range(kept_v.shape[1])
    one = eye()
    own = [place[3] * len(heads) + h for h in heads]
    middle = [middle_map(land_q[h], land_k[h]) for h in own]
    approx = [m.T / jnp.sum(m * m, keepdims=True) for m in middle]
    for turn in range(NEWTON):
        product = [dot_high(middle[h], approx[h]) for h in heads]
        for h in heads:
            kept_v[turn, h] = approx[h]
            kept_p[turn, h] = product[h]
        bracket = [7.0 * one - p for p in product]
        bracket = [15.0 * one - dot_high(product[h], bracket[h]) for h in heads]
        for h in heads:
            kept_b[turn, h] = bracket[h]
        bracket = [13.0 * one - dot_high(product[h], bracket[h]) for h in heads]
        for h in heads:
            kept_c[turn, h] = bracket[h]
        approx = [0.25 * dot_high(approx[h], bracket[h]) for h in heads]
    for h in heads:
        kept_v[NEWTON, h] = approx[h]


def inverse_forward(place, land_q, land_k, owners):
    heads = land_q.shape[0] // owners
    square = (heads, LANDMARKS, LANDMARKS)
    return pl.pallas_call(
        inverse_kernel,
        out_shape=(
            jax.ShapeDtypeStruct((NEWTON + 1,) + square, F32),
            jax.ShapeDtypeStruct((NEWTON,) + square, F32),
            jax.ShapeDtypeStruct((NEWTON,) + square, F32),
            jax.ShapeDtypeStruct((NEWTON,) + square, F32),
        ),
        in_specs=[SCALARS] + whole(2),
        out_specs=tuple(whole(4)),
        compiler_params=PARAMS,
        cost_estimate=lasting(7),
        name="inverse_forward",
    )(place, land_q, land_k)


def merged_keys(one, two, size):
    one_top, two_top = one[:, size : size + 1], two[:, size : size + 1]
    top = jnp.maximum(one_top, two_top)
    summed = one * jnp.exp(one_top - top) + two * jnp.exp(two_top - top)
    lane = lax.broadcasted_iota(jnp.int32, one.shape, 1)
    return jnp.where(lane == size, top, summed)


def land_out_kernel(one, two, kept_v, merged, land_out):
    size = land_out.shape[2]
    for h in range(one.shape[0]):
        both = merged_keys(one[h], two[h], size)
        merged[h] = both
        mixed = both[:, :size] / both[:, size + 1 : size + 2]
        land_out[h] = dot_high(kept_v[NEWTON, h], mixed).astype(BF16)


def landmark_out(one, two, kept_v):
    heads = one.shape[0]
    return pl.pallas_call(
        land_out_kernel,
        out_shape=(
            jax.ShapeDtypeStruct(one.shape, F32),
            jax.ShapeDtypeStruct((heads, LANDMARKS, LANES // 2), BF16),
        ),
        in_specs=whole(3),
        out_specs=tuple(whole(2)),
        compiler_params=PARAMS,
        cost_estimate=lasting(2.2),
        name="landmark_out",
    )(one, two, kept_v)


def inverse_back_kernel(
    place, land_q, land_k, merged, grads, kept_v, kept_p, kept_b, kept_c, spread, g_lq, g_lk
):
    heads = range(grads.shape[0])
    size = land_q.shape[2]
    one = eye()
    own = [place[3] * len(heads) + h for h in heads]
    middle = [middle_map(land_q[h], land_k[h]) for h in own]
    turned = [m.T for m in middle]
    g_approx = []
    for h in heads:
        mixed = merged[h][:, :size] / merged[h][:, size + 1 : size + 2]
        g_land = grads[h][:, :size]
        g_approx.append(dot_high_nt(g_land, mixed))
        g_mixed = dot_high(kept_v[NEWTON, h].T, g_land)
        row_dot = jnp.sum(g_mixed * mixed, axis=1, keepdims=True)
        lane = lax.broadcasted_iota(jnp.int32, (LANDMARKS, LANES - size), 1)
        top = merged[h][:, size : size + 1]
        total = merged[h][:, size + 1 : size + 2]
        stats = jnp.where(
            lane == 0, row_dot, jnp.where(lane == 1, top, jnp.where(lane == 2, total, 0.0))
        )
        spread[h] = jnp.concatenate([g_mixed, stats], axis=1)
    g_middle = [jnp.zeros((LANDMARKS, LANDMARKS), F32) for _ in heads]
    for turn in reversed(range(NEWTON)):
        approx = [kept_v[turn, h] for h in heads]
        product = [kept_p[turn, h] for h in heads]
        first = [7.0 * one - p for p in product]
        second = [kept_b[turn, h] for h in heads]
        third = [kept_c[turn, h] for h in heads]
        g_third = [0.25 * dot_high(approx[h].T, g_approx[h]) for h in heads]
        g_back = [0.25 * dot_high_nt(g_approx[h], third[h]) for h in heads]
        g_product = [-dot_high_nt(g_third[h], second[h]) for h in heads]
        pt = [p.T for p in product]
        g_second = [-dot_high(pt[h], g_third[h]) for h in heads]
        g_product = [g_product[h] - dot_high_nt(g_second[h], first[h]) for h in heads]
        g_product = [g_product[h] + dot_high(pt[h], g_second[h]) for h in heads]
        g_middle = [g_middle[h] + dot_high_nt(g_product[h], approx[h]) for h in heads]
        g_approx = [g_back[h] + dot_high(turned[h], g_product[h]) for h in heads]
    for h in heads:
        m = middle[h]
        size_sum = jnp.sum(m * m, keepdims=True)
        g_size = -jnp.sum(g_approx[h] * turned[h], keepdims=True) / (size_sum * size_sum)
        g_m = g_middle[h] + g_approx[h].T / size_sum + 2.0 * g_size * m
        g_scores = m * (g_m - jnp.sum(g_m * m, axis=1, keepdims=True))
        g_lq[h] = dot_high(g_scores, land_k[own[h]].astype(F32))
        g_lk[h] = dot_high(g_scores.T, land_q[own[h]].astype(F32))


def inverse_backward(place, land_q, land_k, merged, grads, *kept):
    heads = grads.shape[0]
    square = jax.ShapeDtypeStruct((heads,) + land_q.shape[1:], F32)
    return pl.pallas_call(
        inverse_back_kernel,
        out_shape=(jax.ShapeDtypeStruct((heads, LANDMARKS, LANES), F32), square, square),
        in_specs=[SCALARS] + whole(8),
        out_specs=tuple(whole(3)),
        compiler_params=PARAMS,
        cost_estimate=lasting(11.5),
        name="inverse_backward",
    )(place, land_q, land_k, merged, grads, *kept)


def first_map(land_k, queries):
    scores = nn(land_k, queries)
    raised = jnp.exp(scores - jnp.max(scores, axis=0, keepdims=True))
    return raised * (1.0 / jnp.sum(raised, axis=0, keepdims=True))


def head_blocks(cells, ends, at):
    rows = cells.shape[1]
    left, right = ends
    return (
        [left[at, :]]
        + [cells[at, i * LANES : (i + 1) * LANES] for i in range(rows // LANES)]
        + [right[at, :]]
    )


def first_conv_kernel(queries, values, left, right, land_k, base, first, conv, ends):
    heads, _, size = land_k.shape
    ends[0] = left[...].T
    ends[1] = right[...].T

    def head(h):
        at = pl.ds(pl.multiple_of(h * size, size), size)
        first[at, :] = first_map(land_k[h], queries[at, :]).astype(BF16)
        blocks = head_blocks(values, (ends.at[0], ends.at[1]), at)
        conv[at, :] = convolved(blocks, band(base[pl.ds(h, 1), :]))

    def pair(i, _):
        head(2 * i)
        head(2 * i + 1)
        return 0

    lax.fori_loop(0, heads // 2, pair, 0)


def first_and_conv(queries, values, left, right, land_k, base):
    width, rows = queries.shape
    return pl.pallas_call(
        first_conv_kernel,
        out_shape=(
            jax.ShapeDtypeStruct((width, rows), BF16),
            jax.ShapeDtypeStruct((width, rows), F32),
        ),
        in_specs=whole(6),
        out_specs=tuple(whole(2)),
        scratch_shapes=[pltpu.VMEM((2, width, LANES), BF16)],
        compiler_params=PARAMS,
        cost_estimate=lasting(8),
        name="first_and_conv",
    )(queries, values, left, right, land_k, base)


def context_rows(first, conv, land_out, context):
    heads, _, size = land_out.shape

    def head(h):
        at = pl.ds(pl.multiple_of(h * size, size), size)
        return (nn(land_out[h].T, first[at, :]) + conv[at, :]).astype(BF16)

    def pair(i, _):
        both = jnp.concatenate([head(2 * i), head(2 * i + 1)], axis=0)
        context[:, pl.ds(pl.multiple_of(i * LANES, LANES), LANES)] = both.T
        return 0

    lax.fori_loop(0, heads // 2, pair, 0)


def attention_back_kernel(
    place, queries, grads, land_k, land_out, kept, sent, g_lk, g_query
):
    heads, _, size = land_k.shape
    rows = queries.shape[1]
    owners = 2 * kept.shape[0]
    scaled = jnp.where(live_lanes(place, rows), 64**-0.25, 0.0)

    def pair(i, _):
        lanes = pl.ds(pl.multiple_of(i * LANES, LANES), LANES)
        turned = grads[:, lanes].T
        g_queries, g_keys = [], []
        for side in range(2):
            h = 2 * i + side
            query = queries[pl.ds(pl.multiple_of(h * size, size), size), :]
            g_context = turned[side * size : (side + 1) * size]
            first = first_map(land_k[h], query)
            g_first = nn(land_out[h], g_context)
            inner = jnp.sum(g_first * first, axis=0, keepdims=True)
            g_scores = (first * (g_first - inner)).astype(BF16)
            g_land = nt(first.astype(BF16), g_context)
            g_key = nt(g_scores, query)
            by_owner(place, h, owners, kept, sent, jnp.concatenate([g_land, g_key], axis=1))
            g_keys.append(g_key)
            g_queries.append((scaled * nn(land_k[h].T, g_scores)).astype(BF16))
        g_query[:, lanes] = jnp.concatenate(g_queries, axis=0).T
        g_lk[:, lanes] = jnp.concatenate(g_keys, axis=1)
        return 0

    lax.fori_loop(0, heads // 2, pair, 0)


def attention_back(place, queries, grads, land_k, land_out, owners):
    width, rows = queries.shape
    heads = land_k.shape[0]
    return pl.pallas_call(
        attention_back_kernel,
        out_shape=owner_parts(heads, owners)
        + (
            jax.ShapeDtypeStruct((LANDMARKS, width), F32),
            jax.ShapeDtypeStruct((rows, width), BF16),
        ),
        in_specs=[SCALARS] + whole(4),
        out_specs=tuple(whole(4)),
        compiler_params=PARAMS,
        cost_estimate=lasting(11.4),
        name="attention_back",
    )(place, queries, grads, land_k, land_out)


def conv_back_kernel(
    v_plain, v_left, v_right, grads, g_left, g_right, base_back, g_value, g_taps, ends
):
    heads = g_taps.shape[0]
    rows, width = grads.shape
    size = width // heads
    blocks_in = rows // LANES
    row = lax.broadcasted_iota(jnp.int32, (LANES, LANES), 0)
    column = lax.broadcasted_iota(jnp.int32, (LANES, LANES), 1)
    reverse = jnp.where(row + column == LANES - 1, 1.0, 0.0).astype(BF16)
    gap = jnp.concatenate([row - column, row - column], axis=1)
    ends[0] = g_left[...].T
    ends[1] = g_right[...].T

    def pair(i, _):
        lanes = pl.ds(pl.multiple_of(i * LANES, LANES), LANES)
        turned = grads[:, lanes].T
        plain = [v_left[LANES - 16 :, lanes]]
        plain += [v_plain[b * LANES : (b + 1) * LANES, lanes] for b in range(blocks_in)]
        plain += [v_right[:16, lanes]]
        for side in range(2):
            h = 2 * i + side
            at = pl.ds(pl.multiple_of(h * size, size), size)
            g_context = turned[side * size : (side + 1) * size]
            blocks = [ends[0, at, :]]
            blocks += [g_context[:, b * LANES : (b + 1) * LANES] for b in range(blocks_in)]
            blocks += [ends[1, at, :]]
            g_value[at, :] = convolved(blocks, band(base_back[pl.ds(h, 1), :]))

        def around(b):
            prior = plain[0] if b == 0 else plain[b][LANES - 16 :]
            return jnp.concatenate([prior, plain[b + 1], plain[b + 2][:16]], axis=0)

        def by_head(b):
            piece = turned[:, b * LANES : (b + 1) * LANES]
            zero = jnp.zeros_like(piece)
            return jnp.concatenate(
                [jnp.where(row < size, piece, zero), jnp.where(row >= size, piece, zero)], axis=1
            )

        total = jnp.zeros((LANES + 32, 2 * LANES), F32)
        for b in range(0, blocks_in, 2):
            total = total + nn(
                jnp.concatenate([around(b), around(b + 1)], axis=1),
                jnp.concatenate([by_head(b), by_head(b + 1)], axis=0),
            )
        empty = jnp.zeros((LANES - 16, 2 * LANES), F32)
        before, here, after = total[:16], total[16 : 16 + LANES], total[16 + LANES :]
        ring = jnp.where(jnp.abs(gap) <= 16, here, 0.0)
        ring = ring + jnp.where(gap >= LANES - 16, jnp.concatenate([empty, before], axis=0), 0.0)
        ring = ring + jnp.where(gap <= 16 - LANES, jnp.concatenate([after, empty], axis=0), 0.0)
        high, low = split(ring)
        lowest = (ring - high.astype(F32) - low.astype(F32)).astype(BF16)
        flat = nn(reverse, high) + nn(reverse, low) + nn(reverse, lowest)
        for side in range(2):
            straight = pltpu.roll(
                flat[:, side * LANES : (side + 1) * LANES], 0, 1, stride=1, stride_axis=0
            )
            g_taps[pl.ds(2 * i + side, 1), :] = jnp.sum(straight, axis=0, keepdims=True)
        return 0

    lax.fori_loop(0, heads // 2, pair, 0)


def conv_back(v_plain, v_ends, grads, g_ends, base_back):
    rows, width = grads.shape
    heads = base_back.shape[0]
    return pl.pallas_call(
        conv_back_kernel,
        out_shape=(
            jax.ShapeDtypeStruct((width, rows), F32),
            jax.ShapeDtypeStruct((heads, LANES), F32),
        ),
        in_specs=whole(7),
        out_specs=tuple(whole(2)),
        scratch_shapes=[pltpu.VMEM((2, width, LANES), BF16)],
        compiler_params=PARAMS,
        cost_estimate=lasting(13.6),
        name="conv_back",
    )(v_plain, *v_ends, grads, *g_ends, base_back)


def third_back_kernel(
    place, keys, values, land_q, spread, g_conv, lq_mid, lk_mid, g_lk, last, first, taps, turned,
    g_k, g_v, sums, kept, sent,
):
    heads, _, size = land_q.shape
    rows, width = g_k.shape
    own_heads = lq_mid.shape[0]
    scale = 64**-0.25
    sums[LANDMARKS:, :] = jnp.zeros((sums.shape[0] - LANDMARKS, 2 * width), F32)
    sums[LANDMARKS : LANDMARKS + 1, :] = last[...]
    sums[LANDMARKS + 1 : LANDMARKS + 2, :] = first[...]
    for h in range(heads):
        sums[LANDMARKS + 2 : LANDMARKS + 3, h * LANES : (h + 1) * LANES] = taps[h : h + 1, :]

    def mid(part, h):
        at = h - place[3] * own_heads
        mine = (at >= 0) & (at < own_heads) & (place[5] == 0)
        inside = jnp.clip(at, 0, own_heads - 1)
        return jnp.where(mine, part[inside], 0.0)

    live = live_lanes(place, rows)
    live_row = jnp.where(live, 1.0, 0.0)
    scaled_row = live_row * 64**-0.25

    def pair(i, _):
        lanes = pl.ds(pl.multiple_of(i * LANES, LANES), LANES)
        g_keys, g_values, g_lqs, lks = [], [], [], []
        for side in range(2):
            h = 2 * i + side
            at = pl.ds(pl.multiple_of(h * size, size), size)
            key, value = keys[at, :], values[at, :]
            pack = spread[h]
            g_mixed = pack[:, :size]
            row_dot = pack[:, size : size + 1]
            top = pack[:, size + 1 : size + 2]
            total = pack[:, size + 2 : size + 3]
            scores = nn(land_q[h], key)
            third = jnp.where(live, jnp.exp(scores - top), 0.0) * (1.0 / total)
            gm_high, gm_low = split(g_mixed)
            g_third = nn(gm_high, value) + nn(gm_low, value)
            g_high, g_low = split(third * (g_third - row_dot))
            g_lqs.append(nt(g_high, key) + nt(g_low, key) + mid(lq_mid, h))
            lks.append(mid(lk_mid, h))
            turned = land_q[h].T
            g_key = nn(turned, g_high) + nn(turned, g_low)
            g_keys.append((scaled_row * g_key).astype(BF16))
            t_high, t_low = split(third)
            gmt_high, gmt_low = split(g_mixed.T)
            g_value = nn(gmt_high, t_high) + nn(gmt_high, t_low) + nn(gmt_low, t_high)
            g_values.append((live_row * (g_value + g_conv[at, :])).astype(BF16))
        g_k[:, lanes] = jnp.concatenate(g_keys, axis=0).T
        g_v[:, lanes] = jnp.concatenate(g_values, axis=0).T
        sums[:LANDMARKS, lanes] = scale * jnp.concatenate(g_lqs, axis=1)
        key_lanes = pl.ds(pl.multiple_of(width + i * LANES, LANES), LANES)
        sums[:LANDMARKS, key_lanes] = scale * (g_lk[:, lanes] + jnp.concatenate(lks, axis=1))
        return 0

    lax.fori_loop(0, heads // 2, pair, 0)
    for number, cells in enumerate((g_k, g_v)):
        family_grads(turned, cells, place[2] == number, kept, sent)


def third_back(
    place, keys, values, land_q, spread, g_conv, lq_mid, lk_mid, g_lk, last, first, taps, turned, halves
):
    width, rows = keys.shape
    plain = jax.ShapeDtypeStruct((rows, width), BF16)
    return pl.pallas_call(
        third_back_kernel,
        out_shape=(plain, plain, jax.ShapeDtypeStruct((LANDMARKS + 8, 2 * width), F32))
        + (jax.ShapeDtypeStruct((halves, width, width // halves), BF16),) * 2,
        in_specs=[SCALARS] + whole(12),
        out_specs=tuple(whole(5)),
        compiler_params=PARAMS,
        cost_estimate=lasting(17),
        name="third_back",
    )(
        place, keys, values, land_q, spread, g_conv, lq_mid, lk_mid, g_lk, last, first, taps, turned
    )


def centred_rows(rows):
    centred = rows - jnp.mean(rows, axis=1, keepdims=True)
    scale = lax.rsqrt(jnp.mean(centred * centred, axis=1, keepdims=True) + 1e-05)
    return centred * scale, scale


def norm_back(grads, gain, unit, scale):
    scaled = grads * gain
    inner = jnp.mean(scaled * unit, axis=1, keepdims=True)
    return scale * (scaled - jnp.mean(scaled, axis=1, keepdims=True) - unit * inner)


def gelu_pair(hidden):
    share = 0.5 * (1.0 + lax.erf(hidden * 0.7071067811865476))
    density = jnp.exp(-0.5 * hidden * hidden) * 0.3989422804014327
    return hidden * share, share + hidden * density


class Copies:
    def __init__(self, sems):
        self.sems, self.used, self.open = sems, 0, []

    def start(self, source, target):
        copy = pltpu.make_async_copy(source, target, self.sems.at[self.used])
        self.used += 1
        copy.start()
        return copy

    def out(self, source, target):
        self.open.append(self.start(source, target))

    def finish(self):
        for copy in self.open:
            copy.wait()


def weight_grad(turned, cells, halves, which, out):
    ff = cells.shape[1] // halves
    columns = ff // 2
    for half in range(halves):
        from_column = pl.ds(pl.multiple_of(half * ff + which * columns, columns), columns)

        def rows_of(i, at, half=half, from_column=from_column):
            out[half, at, :] = nn(turned[at, :], cells[:, from_column]).astype(BF16)

        each_tile(turned.shape[0], 384, rows_of)


def feed_kernel(
    place, first_in, conv_in, land_out, tokens_in, cotangent_in, weights,
    output_to, context_to, slope_to, g_fed_to, g_second_to, unit_to, scale_to, turned_to, active_to, fed_turned_to, sent_to,
    norm_grads, in_w, down_w, out_w, norms, conv, context, tokens, cotangent,
    low, unit, scales, fed, active, slopes, g_fed, g_fed_turned, normed_turned, output, sent,
    sems,
):
    rows, width = tokens.shape
    halves, _, ff = in_w.shape
    part = out_w.shape[2]
    tile = 256
    copies = Copies(sems)
    context_copies = [copies.start(first_in, g_fed_turned), copies.start(conv_in, conv)]
    early = [
        copies.start(weights.at[:, :, pl.ds(2 * ff, part)], out_w),
        copies.start(tokens_in, tokens),
        copies.start(weights.at[:, :, pl.ds(2 * ff + part, LANES)], norms),
    ]
    in_copy = copies.start(weights.at[:, :, pl.ds(0, ff)], in_w)
    down_copy = copies.start(weights.at[:, :, pl.ds(ff, ff)], down_w)
    cotangent_copy = copies.start(cotangent_in, cotangent)
    for copy in context_copies:
        copy.wait()
    context_rows(g_fed_turned, conv, land_out, context)
    copies.out(context, context_to)
    for copy in early:
        copy.wait()
    columns = norms[0].astype(F32).T
    gain0, gain1 = columns[0:1], columns[1:2]
    shift0, shift1 = columns[2:3], columns[3:4]
    norm_grads[...] = jnp.zeros_like(norm_grads)

    def project(i, at):
        attended = nt(context[at, :part], out_w[0])
        for half in range(1, halves):
            attended = attended + nt(context[at, half * part : (half + 1) * part], out_w[half])
        rows_unit, scale = centred_rows(tokens[at, :].astype(F32) + attended)
        unit[at, :] = rows_unit
        scales[at, :] = jnp.broadcast_to(scale, (tile, LANES))
        normed = (rows_unit * gain0 + shift0).astype(BF16)
        low[at, :] = normed
        normed_turned[:, at] = normed.T

    each_tile(rows, tile, project)
    copies.out(unit, unit_to)
    copies.out(scales, scale_to)
    copies.out(normed_turned, turned_to)
    in_copy.wait()
    big = 512

    def hidden_rows(i, at):
        for half in range(halves):
            value, slope = gelu_pair(nn(low[at, :], in_w[half]))
            active[at, half * ff : (half + 1) * ff] = value.astype(BF16)
            slopes[at, half * ff : (half + 1) * ff] = slope.astype(BF16)

    each_tile(rows, tile, hidden_rows)
    copies.out(slopes, slope_to)
    copies.out(active, active_to)
    down_copy.wait()

    def fed_rows(i, at):
        total = nt(active[at, :ff], down_w[0])
        for half in range(1, halves):
            total = total + nt(active[at, half * ff : (half + 1) * ff], down_w[half])
        fed[at, :] = total

    each_tile(rows, big, fed_rows)
    cotangent_copy.wait()

    def second_norm(i, at):
        normed = unit[at, :] * gain0 + shift0
        unit1, scale1 = centred_rows(normed + fed[at, :])
        position = place[0] + i * tile + lax.broadcasted_iota(jnp.int32, (tile, 1), 0)
        live = jnp.where(position < place[1], 1.0, 0.0)
        output[at, :] = (live * (unit1 * gain1 + shift1)).astype(BF16)
        grads = live * cotangent[at, :].astype(F32)
        norm_grads[:, :width] += jnp.sum(grads * unit1, axis=0, keepdims=True)
        norm_grads[:, width:] += jnp.sum(grads, axis=0, keepdims=True)
        second = norm_back(grads, gain1, unit1, scale1)
        fed[at, :] = second
        g_low = second.astype(BF16)
        g_fed[at, :] = g_low
        g_fed_turned[:, at] = g_low.T

    each_tile(rows, tile, second_norm)
    copies.out(output, output_to)
    copies.out(fed, g_second_to)
    copies.out(g_fed, g_fed_to)
    copies.out(g_fed_turned, fed_turned_to)
    weight_grad(g_fed_turned, active, halves, 1 - place[2], sent)
    copies.out(sent, sent_to)
    copies.finish()


ANYWHERE = pl.BlockSpec(memory_space=pl.ANY)


def feed_forward(place, first, conv, land_out, tokens, cotangent, weights, ff, part):
    rows, width = tokens.shape
    halves = weights.shape[0]
    grad = (halves, width, ff // 2)
    shapes = [
        ((rows, width), BF16), ((rows, width), BF16), ((rows, halves * ff), BF16),
        ((rows, width), BF16), ((rows, width), F32), ((rows, width), F32), ((rows, LANES), F32), ((width, rows), BF16),
        ((rows, halves * ff), BF16), ((width, rows), BF16), (grad, BF16), ((1, 2 * width), F32),
    ]
    scratch = [
        ((halves, width, ff), BF16), ((halves, width, ff), BF16), ((halves, width, part), BF16),
        ((halves, width, LANES), BF16), ((width, rows), F32), ((rows, width), BF16),
        ((rows, width), BF16), ((rows, width), BF16),
        ((rows, width), BF16), ((rows, width), F32), ((rows, LANES), F32), ((rows, width), F32),
        ((rows, halves * ff), BF16), ((rows, halves * ff), BF16), ((rows, width), BF16),
        ((width, rows), BF16), ((width, rows), BF16), ((rows, width), BF16), (grad, BF16),
    ]
    return pl.pallas_call(
        feed_kernel,
        out_shape=tuple(jax.ShapeDtypeStruct(*shape) for shape in shapes),
        in_specs=[SCALARS] + [ANYWHERE] * 2 + whole(1) + [ANYWHERE] * 3,
        out_specs=tuple([ANYWHERE] * 11 + whole(1)),
        scratch_shapes=[pltpu.VMEM(*shape) for shape in scratch]
        + [pltpu.SemaphoreType.DMA((19,))],
        compiler_params=PARAMS,
        cost_estimate=lasting(32),
        name="feed_forward",
    )(place, first, conv, land_out, tokens, cotangent, weights)


def feed_back_kernel(
    place, slope_in, g_fed_in, g_second_in, unit_in, scale_in, turned_in, weights,
    g_first_to, g_context_to, g_hidden_to, sent_to, att_turned_to, norm_grads,
    in_w, down_w, out_w, norms, g_hidden, g_fed, second, unit, scales, normed_turned,
    g_att, g_att_turned, g_context, sent,
    sems,
):
    rows, width = second.shape
    halves, _, ff = in_w.shape
    part = out_w.shape[2]
    tile = 256
    copies = Copies(sems)
    early = [
        copies.start(g_fed_in, g_fed),
        copies.start(weights.at[:, :, pl.ds(ff, ff)], down_w),
        copies.start(slope_in, g_hidden),
    ]
    later = [
        copies.start(turned_in, normed_turned),
        copies.start(weights.at[:, :, pl.ds(0, ff)], in_w),
        copies.start(g_second_in, second),
        copies.start(unit_in, unit),
        copies.start(scale_in, scales),
        copies.start(weights.at[:, :, pl.ds(2 * ff + part, LANES)], norms),
        copies.start(weights.at[:, :, pl.ds(2 * ff, part)], out_w),
    ]
    for copy in early:
        copy.wait()
    norm_grads[...] = jnp.zeros_like(norm_grads)
    big = 512

    def back_rows(i, at):
        for half in range(halves):
            g_act = nn(g_fed[at, :], down_w[half])
            to = slice(half * ff, (half + 1) * ff)
            g_hidden[at, to] = (g_act * g_hidden[at, to].astype(F32)).astype(BF16)

    each_tile(rows, big, back_rows)
    copies.out(g_hidden, g_hidden_to)
    later.pop(0).wait()
    weight_grad(normed_turned, g_hidden, halves, 1 - place[2], sent)
    copies.out(sent, sent_to)
    for copy in later:
        copy.wait()
    gain0 = norms[0].astype(F32).T[0:1]

    def normed_rows(i, at):
        total = second[at, :]
        for half in range(halves):
            total = total + nt(g_hidden[at, half * ff : (half + 1) * ff], in_w[half])
        second[at, :] = total

    each_tile(rows, big, normed_rows)

    def first_norm(i, at):
        grads = second[at, :]
        rows_unit, scale = unit[at, :], scales[at, 0:1]
        norm_grads[:, :width] += jnp.sum(grads * rows_unit, axis=0, keepdims=True)
        norm_grads[:, width:] += jnp.sum(grads, axis=0, keepdims=True)
        first = norm_back(grads, gain0, rows_unit, scale)
        second[at, :] = first
        low = first.astype(BF16)
        g_att[at, :] = low
        g_att_turned[:, at] = low.T

    each_tile(rows, tile, first_norm)
    copies.out(second, g_first_to)
    copies.out(g_att_turned, att_turned_to)
    for half in range(halves):
        g_context[:, half * part : (half + 1) * part] = nn(g_att[...], out_w[half]).astype(BF16)
    copies.out(g_context, g_context_to)
    copies.finish()


def feed_backward(place, fed, weights, ff, part):
    rows, width = fed[1].shape
    halves = weights.shape[0]
    grad = (halves, width, ff // 2)
    shapes = [
        ((rows, width), F32), ((rows, width), BF16), ((rows, halves * ff), BF16), (grad, BF16),
        ((width, rows), BF16), ((1, 2 * width), F32),
    ]
    scratch = [
        ((halves, width, ff), BF16), ((halves, width, ff), BF16), ((halves, width, part), BF16),
        ((halves, width, LANES), BF16), ((rows, halves * ff), BF16), ((rows, width), BF16),
        ((rows, width), F32), ((rows, width), F32),
        ((rows, LANES), F32), ((width, rows), BF16),
        ((rows, width), BF16), ((width, rows), BF16), ((rows, width), BF16), (grad, BF16),
    ]
    return pl.pallas_call(
        feed_back_kernel,
        out_shape=tuple(jax.ShapeDtypeStruct(*shape) for shape in shapes),
        in_specs=[SCALARS] + [ANYWHERE] * 7,
        out_specs=tuple([ANYWHERE] * 5 + whole(1)),
        scratch_shapes=[pltpu.VMEM(*shape) for shape in scratch]
        + [pltpu.SemaphoreType.DMA((16,))],
        compiler_params=PARAMS,
        cost_estimate=lasting(27),
        name="feed_backward",
    )(place, *fed, weights)


def kept_kernel(place, turned_in, cells_in, kept, turned, cells, sems):
    halves, width, columns = kept.shape
    ff = 2 * columns
    copies = Copies(sems)
    turned_copy = copies.start(turned_in, turned)
    pieces = []
    for half in range(halves):
        start = pl.multiple_of(half * ff + place[2] * columns, columns)
        pieces.append(copies.start(cells_in.at[:, pl.ds(start, columns)], cells.at[half]))
    turned_copy.wait()
    for half in range(halves):
        pieces[half].wait()

        def rows_of(i, at, half=half):
            kept[half, at, :] = nn(turned[at, :], cells[half]).astype(BF16)

        each_tile(width, 384, rows_of)


def kept_grad(place, turned, cells, halves):
    width, rows = turned.shape
    columns = cells.shape[1] // halves // 2
    return pl.pallas_call(
        kept_kernel,
        out_shape=jax.ShapeDtypeStruct((halves, width, columns), BF16),
        in_specs=[SCALARS] + [ANYWHERE] * 2,
        out_specs=whole(1)[0],
        scratch_shapes=[
            pltpu.VMEM((width, rows), BF16),
            pltpu.VMEM((halves, rows, columns), BF16),
            pltpu.SemaphoreType.DMA((3,)),
        ],
        compiler_params=PARAMS,
        cost_estimate=lasting(5),
        name="kept_grad",
    )(place, turned, cells)


def spread_kernel(place, turned_in, cells_in, other, kept, sent, turned, cells, sems):
    halves, width, columns = other.shape
    ff = 2 * columns
    quarter = columns // 2
    copies = Copies(sems)
    turned_copy = copies.start(turned_in, turned)
    pieces = []
    for half in range(halves):
        start = pl.multiple_of(half * ff + place[2] * columns, columns)
        pieces.append(copies.start(cells_in.at[:, pl.ds(start, columns)], cells.at[half]))
    turned_copy.wait()
    for half in range(halves):
        pieces[half].wait()

        def rows_of(i, at, half=half):
            total = nn(turned[at, :], cells[half]) + other[half, at, :].astype(F32)
            low = total.astype(BF16)
            first = place[4] == 0
            kept[half, at, :] = jnp.where(first, low[:, :quarter], low[:, quarter:])
            sent[half, at, :] = jnp.where(first, low[:, quarter:], low[:, :quarter])

        each_tile(width, 384, rows_of)


def spread_grad(place, turned, cells, other):
    halves, width, columns = other.shape
    rows = turned.shape[1]
    part = jax.ShapeDtypeStruct((halves, width, columns // 2), BF16)
    return pl.pallas_call(
        spread_kernel,
        out_shape=(part, part),
        in_specs=[SCALARS] + [ANYWHERE] * 2 + whole(1),
        out_specs=tuple(whole(2)),
        scratch_shapes=[
            pltpu.VMEM((width, rows), BF16),
            pltpu.VMEM((halves, rows, columns), BF16),
            pltpu.SemaphoreType.DMA((3,)),
        ],
        compiler_params=PARAMS,
        cost_estimate=lasting(6),
        name="spread_grad",
    )(place, turned, cells, other)


def pair_kernel(
    place, one_turned_in, one_cells_in, two_turned_in, two_cells_in, kept, sent,
    one_turned, one_cells, two_turned, two_cells, sems,
):
    copies = Copies(sems)
    loads = [
        copies.start(*pair)
        for pair in (
            (one_turned_in, one_turned), (one_cells_in, one_cells),
            (two_turned_in, two_turned), (two_cells_in, two_cells),
        )
    ]
    for number, (turned, cells) in enumerate(((one_turned, one_cells), (two_turned, two_cells))):
        loads[2 * number].wait()
        loads[2 * number + 1].wait()
        family_grads(turned, cells, place[2] == number, kept, sent)


def pair_grads(place, one_turned, one_cells, two_turned, two_cells, halves):
    width, rows = one_turned.shape
    shape = jax.ShapeDtypeStruct((halves, width, one_cells.shape[1] // halves), BF16)
    return pl.pallas_call(
        pair_kernel,
        out_shape=(shape, shape),
        in_specs=[SCALARS] + [ANYWHERE] * 4,
        out_specs=tuple(whole(2)),
        scratch_shapes=[
            pltpu.VMEM((width, rows), BF16), pltpu.VMEM(one_cells.shape, BF16),
            pltpu.VMEM((width, rows), BF16), pltpu.VMEM(one_cells.shape, BF16),
            pltpu.SemaphoreType.DMA((4,)),
        ],
        compiler_params=PARAMS,
        cost_estimate=lasting(6),
        name="pair_grads",
    )(place, one_turned, one_cells, two_turned, two_cells)


def rank_kernel(place, mine, got, land_tokens, weights, late, through, small):
    halves, width, _ = weights.shape
    part = late.shape[1] // 2
    first = place[2] == 0
    grads = (
        jnp.where(first, mine[:LANDMARKS], got[:LANDMARKS]),
        jnp.where(first, got[:LANDMARKS], mine[:LANDMARKS]),
    )
    counts = landmark_counts(place)
    total = jnp.zeros((2 * LANDMARKS, width), F32)
    for index, grad in enumerate(grads):
        both = jnp.concatenate(split(grad / counts), axis=0)
        for half in range(halves):
            weight = weights[half, :, index * part : (index + 1) * part]
            total = total + nt(both[:, half * part : (half + 1) * part], weight)
    through[...] = jnp.concatenate(split(total[:LANDMARKS] + total[LANDMARKS:]), axis=0)
    zero = jnp.zeros((LANDMARKS, part), F32)
    own = []
    for index, grad in enumerate(grads):
        columns = grad[:, :part]
        for half in range(1, halves):
            columns = jnp.where(place[5] == half, grad[:, half * part : (half + 1) * part], columns)
        own.append(jnp.where(place[2] == 1 - index, columns, zero))
    high, low = split(jnp.concatenate(own, axis=1))
    mean_high, mean_low = split(land_tokens[...] / counts)
    means = jnp.concatenate([mean_high, mean_low, mean_high, jnp.zeros_like(mean_low)], axis=0).T
    factors = jnp.concatenate([high, high, low, jnp.zeros_like(low)], axis=0)
    late[...] = nn(means, factors).astype(BF16)
    gains = jnp.where(first, mine[LANDMARKS:], got[LANDMARKS:])
    shifts = jnp.where(first, got[LANDMARKS:], mine[LANDMARKS:])
    taps = jnp.where(place[5] == 0, gains[2:3], shifts[2:3])
    rows = [gains[1:2], gains[0:1], shifts[1:2], shifts[0:1], taps]
    rows.append(jnp.zeros((small.shape[0] - len(rows), width), F32))
    small[...] = jnp.concatenate(rows, axis=0).astype(BF16)


def rank_parts(place, mine, got, land_tokens, weights):
    halves, width, packed = weights.shape
    return pl.pallas_call(
        rank_kernel,
        out_shape=(
            jax.ShapeDtypeStruct((width, 2 * packed // 3), BF16),
            jax.ShapeDtypeStruct((2 * LANDMARKS, width), BF16),
            jax.ShapeDtypeStruct((16, width), BF16),
        ),
        in_specs=[SCALARS] + whole(4),
        out_specs=tuple(whole(3)),
        compiler_params=PARAMS,
        cost_estimate=lasting(4),
        name="rank_parts",
    )(place, mine, got, land_tokens, weights)


def token_grad_kernel(
    back_in, g_k_in, g_v_in, weights, own_grad, back, g_k, g_v, k_w, v_w, sems
):
    rows, width = back.shape
    halves, _, part = k_w.shape
    copies = Copies(sems)
    first = [
        copies.start(g_k_in, g_k),
        copies.start(weights.at[:, :, pl.ds(part, part)], k_w),
    ]
    later = [
        copies.start(back_in, back),
        copies.start(g_v_in, g_v),
        copies.start(weights.at[:, :, pl.ds(2 * part, part)], v_w),
    ]
    for copy in first + later:
        copy.wait()

    def rows_of(i, at):
        total = back[at, :]
        for half in range(halves):
            columns = slice(half * part, (half + 1) * part)
            total = total + nt(g_k[at, columns], k_w[half]) + nt(g_v[at, columns], v_w[half])
        own_grad[at, :] = total.astype(BF16)

    each_tile(rows, 512, rows_of)


def token_grad(back, g_k, g_v, weights):
    rows, width = back.shape
    halves, _, packed = weights.shape
    shapes = [((rows, width), F32), ((rows, width), BF16), ((rows, width), BF16)]
    shapes += [((halves, width, packed // 3), BF16)] * 2
    return pl.pallas_call(
        token_grad_kernel,
        out_shape=jax.ShapeDtypeStruct((rows, width), BF16),
        in_specs=[ANYWHERE] * 4,
        out_specs=whole(1)[0],
        scratch_shapes=[pltpu.VMEM(*shape) for shape in shapes]
        + [pltpu.SemaphoreType.DMA((5,))],
        compiler_params=PARAMS,
        cost_estimate=lasting(6),
        name="token_grad",
    )(back, g_k, g_v, weights)


def flipped(values, axis, bit):
    count = lax.axis_size(axis)
    return lax.ppermute(values, axis, [(i, i ^ bit) for i in range(count)])


def side_of(axis, bit):
    return (lax.axis_index(axis) // bit) % 2


def paired(mine, axis, bit, dim):
    other = flipped(mine, axis, bit)
    both = jnp.zeros(mine.shape[:dim] + (2,) + mine.shape[dim:], mine.dtype)
    side = side_of(axis, bit)
    both = lax.dynamic_update_slice_in_dim(both, jnp.expand_dims(mine, dim), side, dim)
    return lax.dynamic_update_slice_in_dim(both, jnp.expand_dims(other, dim), 1 - side, dim)


def ctx_bits():
    bits, bit = [], 1
    while bit < lax.axis_size("ctx"):
        bits.append(bit)
        bit *= 2
    return bits


def sequence_start(values):
    width = values.shape[1] // 2
    side = side_of("ctx", 1)
    kept = lax.dynamic_slice_in_dim(values, side * width, width, axis=1)
    sent = lax.dynamic_slice_in_dim(values, (1 - side) * width, width, axis=1)
    kept = kept + flipped(sent, "ctx", 1)
    return kept + flipped(kept, "tp", 1)


def sequence_end(kept):
    for bit in ctx_bits()[1:]:
        kept = kept + flipped(kept, "ctx", bit)
    return kept, flipped(kept, "ctx", 1)


def joined_halves(kept, other):
    return jnp.where(
        side_of("ctx", 1) == 0,
        jnp.concatenate([kept, other], axis=1),
        jnp.concatenate([other, kept], axis=1),
    )


def to_owner(kept, sent, combine):
    kept = combine(kept, flipped(sent, "ctx", 1))
    for bit in ctx_bits()[1:]:
        view = kept.reshape((-1, 2) + kept.shape[1:])
        side = side_of("ctx", bit)
        sent = lax.dynamic_index_in_dim(view, 1 - side, 1, False)
        kept = lax.dynamic_index_in_dim(view, side, 1, False)
        kept = combine(kept, flipped(sent, "ctx", bit))
    return kept[0], flipped(kept[0], "tp", 1)


def from_owners(part):
    whole_part = part[None]
    for bit in reversed(ctx_bits()):
        both = paired(whole_part, "ctx", bit, 1)
        whole_part = both.reshape((-1,) + part.shape)
    return whole_part.reshape((-1,) + part.shape[1:])


def merge_keys(one, two):
    size = LANES // 2
    one_top, two_top = one[..., size : size + 1], two[..., size : size + 1]
    top = jnp.maximum(one_top, two_top)
    one_factor, two_factor = jnp.exp(one_top - top), jnp.exp(two_top - top)
    summed = one * one_factor + two * two_factor
    lane = lax.broadcasted_iota(jnp.int32, summed.shape, summed.ndim - 1)
    return jnp.where(lane == size, top, summed)


def neighbour_rows(cells, count):
    pieces = lax.axis_size("ctx") * lax.axis_size("tp")
    up = [(i, i + 1) for i in range(pieces - 1)]
    before = lax.ppermute(cells[-count:], ("ctx", "tp"), up)
    after = lax.ppermute(cells[:count], ("ctx", "tp"), [(j, i) for i, j in up])
    return (
        jnp.pad(before, ((LANES - count, 0), (0, 0))),
        jnp.pad(after, ((0, LANES - count), (0, 0))),
    )


def own_quarter(shard):
    rows = shard.shape[0] // lax.axis_size("ctx")
    return lax.dynamic_slice_in_dim(shard, lax.axis_index("ctx") * rows, rows, axis=0)


def gathered(shard):
    full = lax.all_gather(own_quarter(shard), ("tp", "fsdp", "ctx"), tiled=True)
    return full.reshape(lax.axis_size("tp"), -1, shard.shape[1])


def gathered_early(shard, beside):
    count = lax.axis_size("fsdp")
    piece = own_quarter(shard)
    if count > 4:
        held = lax.all_gather(piece, "fsdp")
    else:
        here = lax.axis_index("fsdp")
        held = jnp.zeros((count,) + piece.shape, piece.dtype)
        held = lax.dynamic_update_slice_in_dim(held, piece[None], here, 0)
        for step in range(1, count):
            moved = lax.ppermute(piece, "fsdp", [(i, (i + step) % count) for i in range(count)])
            held = lax.dynamic_update_slice_in_dim(held, moved[None], (here - step) % count, 0)
    held, beside = gate(held, beside)
    bits = ctx_bits()
    halves = []
    for number, half in enumerate((held[: count // 2], held[count // 2 :])):
        half = half[None]
        if number == 0:
            half = paired(half[0], "tp", 1, 0)
        for place, bit in enumerate(reversed(bits[1:])):
            half = paired(half, "ctx", bit, 2 + place)
        if number == 1:
            half = paired(half[0], "tp", 1, 0)
        halves.append(paired(half, "ctx", bits[0], 1 + len(bits)))
    full = jnp.concatenate(halves, axis=1)
    return full.reshape(lax.axis_size("tp"), -1, shard.shape[1]), beside


def bits_of(axis):
    bits, bit = [], lax.axis_size(axis) // 2
    while bit:
        bits.append(bit)
        bit //= 2
    return bits


def added(*parts):
    return sum(part.astype(F32) for part in parts).astype(BF16)


def cut(cells, axis, bit, dim):
    size = cells.shape[dim] // 2
    side = side_of(axis, bit)
    return (
        lax.dynamic_slice_in_dim(cells, side * size, size, axis=dim),
        lax.dynamic_slice_in_dim(cells, (1 - side) * size, size, axis=dim),
    )


def gate(*values):
    return lax.optimization_barrier(values)


def dotf(spec, *operands):
    return jnp.einsum(spec, *operands, preferred_element_type=F32)


def taps_round(taps):
    middle = taps.shape[1] // 2
    gap = jnp.zeros((taps.shape[0], LANES - taps.shape[1]), F32)
    return jnp.concatenate([taps[:, middle::-1], gap, taps[:, :middle:-1]], axis=1)


def landmark_bounds(length):
    landmark = jnp.arange(LANDMARKS + 1, dtype=jnp.int32)
    return (landmark * length + LANDMARKS - 1) // LANDMARKS


def landmark_counts_of(length):
    bounds = landmark_bounds(length)
    return (bounds[1:] - bounds[:-1]).astype(F32)[:, None]


def landmark_rows(position, length):
    bounds = landmark_bounds(length)
    inside = (position[:, None] >= bounds[None, :-1]) & (position[:, None] < bounds[None, 1:])
    return inside.astype(BF16)


def on_device(
    tokens,
    lengths,
    qk_weight,
    value_weight,
    out_weight,
    in_weight,
    down_weight,
    norm_gains,
    norm_shifts,
    conv_weight,
    cotangent,
):
    tp_count = lax.axis_size("tp")
    tp_index = lax.axis_index("tp")
    ctx_index = lax.axis_index("ctx")
    _, slot_len, model_width = tokens.shape
    rows = slot_len // tp_count
    local_heads, tap_count = conv_weight.shape
    local_width = value_weight.shape[1]
    ff_width = in_weight.shape[1]
    head_size = local_width // local_heads
    heads = local_heads * tp_count
    owners = lax.axis_size("ctx")
    own_heads = heads // owners
    width = local_width * tp_count
    radius = tap_count // 2
    length = lengths[0]

    first_row = (ctx_index * tp_count + tp_index) * rows
    sides = (side_of("ctx", 1), ctx_index, side_of("ctx", ctx_bits()[-1]), tp_index)
    place = jnp.stack([first_row, length, *sides]).astype(jnp.int32)

    norm_columns = jnp.concatenate([norm_gains, norm_shifts], axis=0).T
    norm_columns = jnp.pad(norm_columns, ((0, 0), (0, LANES - norm_columns.shape[1])))
    ffn_full = gathered(
        jnp.concatenate([in_weight, down_weight.T, out_weight.T, norm_columns], axis=1)
    )
    own_taps = jnp.where(ctx_index == 0, conv_weight.astype(F32), 0.0)
    tap_rows = jnp.pad(own_taps, ((0, 8 - local_heads), (0, LANES - tap_count)))
    tap_rows = jnp.where(
        jnp.arange(model_width) // LANES == tp_index,
        jnp.tile(tap_rows, (1, model_width // LANES)),
        0.0,
    )
    own = lax.dynamic_slice_in_dim(tokens[0], tp_index * rows, rows, axis=0)
    land_tokens = sequence_start(jnp.concatenate([token_sums(place, own), tap_rows], axis=0))
    qkv_full, land_tokens = gathered_early(
        jnp.concatenate([qk_weight[0], qk_weight[1], value_weight], axis=1), land_tokens
    )
    land_tokens = joined_halves(*sequence_end(land_tokens))
    own_cotangent = lax.dynamic_slice_in_dim(cotangent[0], tp_index * rows, rows, axis=0)
    tap_weights = land_tokens[LANDMARKS : LANDMARKS + local_heads, : tp_count * LANES]
    tap_weights = tap_weights.reshape(local_heads, tp_count, LANES).transpose(1, 0, 2)
    tap_weights = tap_weights.reshape(heads, LANES)[:, :tap_count]
    land_tokens = land_tokens[:LANDMARKS]
    base, base_back = taps_round(tap_weights), taps_round(tap_weights[:, ::-1])

    queries, keys, values, v_plain, land_q, land_k, own_turned, *parts_of_third = projections(
        place, own, land_tokens, qkv_full, head_size, owners
    )
    v_ends = neighbour_rows(v_plain, radius)
    merged, merged_tp = to_owner(*parts_of_third, merge_keys)
    kept_turns = inverse_forward(place, land_q, land_k, owners)
    first, conv = first_and_conv(queries, values, *v_ends, land_k, base)
    merged, own_out = landmark_out(merged, merged_tp, kept_turns[0])
    land_out = from_owners(own_out)

    own_output, context, *fed, active, fed_turned, down_sent, last_norm = feed_forward(
        place, first, conv, land_out, own, own_cotangent, ffn_full, ff_width, local_width
    )
    high = ctx_bits()[-1]
    owner_count = lax.axis_size("fsdp")
    owner_rows = model_width // owner_count
    near, *farther = bits_of("fsdp")[::-1]

    def by_owner_bits(cells):
        return cells.reshape((2,) * (1 + len(farther)) + (-1, cells.shape[-1]))

    def cut_last(cells, bit):
        dim = cells.ndim - 3
        return tuple(piece.squeeze(dim) for piece in cut(cells, "fsdp", bit, dim))

    other_output = flipped(own_output, "tp", 1)
    down_other = flipped(down_sent, "ctx", 1)
    down_kept = kept_grad(place, fed_turned, active, tp_count)
    down_kept, down_other = gate(down_kept, down_other)
    down_mine, down_theirs = cut(down_kept, "ctx", high, 2)
    other_mine, other_theirs = cut(down_other, "ctx", high, 2)
    down_sent = added(down_theirs, other_theirs)
    down_got = flipped(down_sent, "ctx", high)
    fed[0], down_sent = gate(fed[0], down_sent)
    grad_first_res, grad_context, g_hidden, in_sent, att_turned, first_norm = feed_backward(
        place, fed, ffn_full, ff_width, local_width
    )
    in_sent, grad_context, g_hidden, other_output, down_got = gate(
        in_sent, grad_context, g_hidden, other_output, down_got
    )
    in_other = flipped(in_sent, "ctx", 1)
    g_ends = neighbour_rows(grad_context, radius)
    down = added(down_mine, other_mine, down_got)
    down_mine, down_sent = cut(down, "tp", 1, 0)
    down_got = flipped(down_sent, "tp", 1)
    grad_context, down_sent = gate(grad_context, down_sent)
    land_kept, land_sent, g_lk, g_q = attention_back(
        place, queries, grad_context, land_k, land_out, owners
    )
    land_kept, land_sent, in_other, g_ends = gate(land_kept, land_sent, in_other, g_ends)

    land_other = flipped(land_sent, "ctx", 1)
    in_kept, in_sent = spread_grad(place, fed[5], g_hidden, in_other)
    in_kept, in_sent, land_other, down_got = gate(in_kept, in_sent, land_other, down_got)
    land_grads = land_kept + land_other
    land_mine, land_theirs = cut(land_grads, "ctx", high, 0)
    land_got = flipped(land_theirs, "ctx", high)
    land_theirs, in_sent = gate(land_theirs, in_sent)
    in_got = flipped(in_sent, "ctx", high)
    down = added(down_mine, down_got)
    grad_context, in_sent = gate(grad_context, in_sent)
    g_conv, g_taps = conv_back(v_plain, v_ends, grad_context, g_ends, base_back)
    g_conv, g_taps, land_got = gate(g_conv, g_taps, land_got)
    own_grads = (land_mine + land_got)[0]
    tp_grads = flipped(own_grads, "tp", 1)

    def parts(cells):
        return cells.reshape(rows, tp_count, local_width)

    def qkv_part(index):
        return qkv_full[:, :, index * local_width : (index + 1) * local_width]

    g_q, own_grads = gate(g_q, own_grads)
    mixed_kept, mixed_sent = pair_grads(place, att_turned, context, own_turned, g_q, tp_count)
    back_q = grad_first_res + dotf("tpk,pck->tc", parts(g_q), qkv_part(0))
    mixed_kept, mixed_sent, tp_grads, back_q = gate(mixed_kept, mixed_sent, tp_grads, back_q)
    mixed_got = flipped(mixed_sent, "ctx", 1)
    own_grads, mixed_sent = gate(own_grads + tp_grads, mixed_sent)
    spread, lq_mid, lk_mid = inverse_backward(
        place, land_q, land_k, merged, own_grads, *kept_turns
    )
    spread, in_got, mixed_got = gate(spread, in_got, mixed_got)
    spread = from_owners(spread)

    in_mine, in_sent = cut(added(in_kept, in_got), "tp", 1, 0)
    in_got = flipped(in_sent, "tp", 1)
    def by_ctx(cells):
        return cells.reshape(tp_count, owner_count, 2, -1, local_width)

    mixed = added(mixed_kept, mixed_got)
    mixed_mine, mixed_sent = cut(by_ctx(mixed), "ctx", high, 2)
    mixed_got = flipped(mixed_sent, "ctx", high)
    spread, in_sent, mixed_sent = gate(spread, in_sent, mixed_sent)
    g_k, g_v, sums, kv_kept, kv_sent = third_back(
        place, keys, values, land_q, spread, g_conv, lq_mid, lk_mid, g_lk, last_norm, first_norm,
        g_taps, own_turned, tp_count,
    )

    kv_kept, kv_sent, sums, in_got, mixed_got = gate(kv_kept, kv_sent, sums, in_got, mixed_got)
    kv_got = flipped(kv_sent, "ctx", 1)
    sums_mine, sums_sent = cut(sums, "ctx", 1, 1)
    sums_got = flipped(sums_sent, "ctx", 1)
    kv_kept, kv_got = gate(kv_kept, kv_got)
    kv_mine, kv_sent = cut(by_ctx(added(kv_kept, kv_got)), "ctx", high, 2)
    kv_sent, sums_mine, mixed_mine, in_mine, g_k = gate(
        kv_sent, sums_mine, mixed_mine, in_mine, g_k
    )
    kv_got = flipped(kv_sent, "ctx", high)
    sums = sums_mine + sums_got
    sums_got = flipped(sums, "tp", 1)
    mixed_mine, mixed_sent = cut(added(mixed_mine, mixed_got), "tp", 1, 0)
    sums, mixed_sent, in_mine = gate(sums, mixed_sent, in_mine)
    mixed_got = flipped(mixed_sent, "tp", 1)
    pair = jnp.concatenate([added(in_mine, in_got)[0], down[0]], axis=1)
    g_k, mixed_sent, pair = gate(g_k, mixed_sent, pair)
    pair = lax.psum_scatter(pair, "fsdp", scatter_dimension=0, tiled=True)
    own_grad = token_grad(back_q, g_k, g_v, qkv_full)
    own_grad, sums_got, mixed_got = gate(own_grad, sums_got, mixed_got)
    first_rows = rows // 8
    other_first = flipped(own_grad[:first_rows], "tp", 1)
    own_grad, other_first, kv_got = gate(own_grad, other_first, kv_got)
    sums = sums + sums_got
    sums_got = flipped(sums, "ctx", high)
    kv_mine, kv_sent = cut(added(kv_mine, kv_got), "tp", 1, 0)
    own_grad, sums, kv_sent = gate(own_grad, sums, kv_sent)
    kv_got = flipped(kv_sent, "tp", 1)
    other_second = flipped(own_grad[first_rows:], "tp", 1)
    sums = sums + sums_got
    sums_got = flipped(sums, "ctx", 1)
    sums, sums_got, kv_got = gate(sums, sums_got, kv_got)
    late, through, small = rank_parts(place, sums, sums_got, land_tokens, qkv_full)
    late, through, small, own_output, other_output = gate(
        late, through, small, own_output, other_output
    )
    late = late.reshape(owner_count, 2, -1, 2 * local_width)
    late = lax.dynamic_index_in_dim(late, place[4], 1, False)
    mixed = added(
        jnp.concatenate([mixed_mine, kv_mine], axis=-1).reshape(late.shape),
        jnp.concatenate([mixed_got, kv_got], axis=-1).reshape(late.shape),
        late,
    )
    small = jnp.broadcast_to(small[None], (owner_count,) + small.shape)
    mixed = by_owner_bits(jnp.concatenate([mixed, small], axis=1))
    mixed_mine, mixed_sent = cut_last(mixed, near)
    mixed_sent, pair = gate(mixed_sent, pair)
    mixed_got = flipped(mixed_sent, "fsdp", near)
    mixed = added(mixed_mine, mixed_got)
    for bit in farther:
        mixed_mine, mixed_sent = cut_last(mixed, bit)
        mixed = added(mixed_mine, flipped(mixed_sent, "fsdp", bit))
    small = mixed[-16:].astype(F32)
    mixed = mixed[:-16]

    def of_core(cells, core):
        cells = cells.reshape((owners // 2, 2) + cells.shape[1:])
        return [cells[i, core] for i in range(owners // 2)]

    mixed, other_second = gate(mixed, other_second)
    mixed = from_owners(mixed[None])
    sides = [jnp.concatenate(of_core(mixed, core), axis=0).astype(F32) for core in range(2)]
    grad_out, grad_k = sides[0][:, :local_width].T, sides[0][:, local_width:]
    grad_q, grad_v = sides[1][:, :local_width], sides[1][:, local_width:]

    own_columns = lax.axis_index("fsdp") * owner_rows
    norm_sums = lax.dynamic_slice_in_dim(small[:4], own_columns, owner_rows, axis=1)
    taps_sum = small[4].reshape(local_heads, LANES)
    grad_taps = jnp.concatenate(
        [taps_sum[:, radius - 1 :: -1], taps_sum[:, : -radius - 2 : -1]], axis=1
    )

    columns = pair.shape[1] // 2
    pair = from_owners(pair[None])
    pieces = [piece for core in range(2) for piece in of_core(pair, core)]
    grad_in = jnp.concatenate([piece[:, :columns] for piece in pieces], axis=1).astype(F32)
    grad_down = jnp.concatenate([piece[:, columns:] for piece in pieces], axis=1).astype(F32).T

    output = jnp.where(
        tp_index == 0,
        jnp.concatenate([own_output, other_output]),
        jnp.concatenate([other_output, own_output]),
    )[None]
    both_grads = jnp.where(
        tp_index == 0,
        jnp.concatenate([own_grad, other_first, other_second]),
        jnp.concatenate([other_first, other_second, own_grad]),
    )
    position = ctx_index * slot_len + jnp.arange(slot_len, dtype=jnp.int32)
    onehot = landmark_rows(position, length)
    grad_tokens = both_grads.astype(F32) + dotf(
        "tm,mc->tc", jnp.concatenate([onehot, onehot], axis=1), through
    )
    grad_tokens = grad_tokens.reshape(1, slot_len, model_width)
    return (
        output,
        grad_tokens,
        jnp.stack([grad_q, grad_k]),
        grad_v,
        grad_out,
        grad_in,
        grad_down,
        norm_sums[:2],
        norm_sums[2:],
        grad_taps,
    )


def solution(mesh):
    in_specs = (
        P("fsdp", "ctx", None),
        P("fsdp"),
        P(None, "fsdp", "tp"),
        P("fsdp", "tp"),
        P("tp", "fsdp"),
        P("fsdp", "tp"),
        P("tp", "fsdp"),
        P(None, "fsdp"),
        P(None, "fsdp"),
        P("tp", None),
        P("fsdp", "ctx", None),
    )
    out_specs = (
        P("fsdp", "ctx", None),
        P("fsdp", "ctx", None),
        P(None, "fsdp", "tp"),
        P("fsdp", "tp"),
        P("tp", "fsdp"),
        P("fsdp", "tp"),
        P("tp", "fsdp"),
        P(None, "fsdp"),
        P(None, "fsdp"),
        P("tp", None),
    )
    return jax.shard_map(
        on_device, mesh=mesh, in_specs=in_specs, out_specs=out_specs, check_vma=False
    )
```

```python
import jax
import jax.numpy as jnp
from jax import lax
from jax.experimental import pallas as pl
from jax.experimental.pallas import tpu as pltpu
from jax.sharding import PartitionSpec as P

LANDMARKS = 64
NEWTON = 6
LANES = 128
VMEM_BYTES = 56 * 2**20

HIGH = lax.Precision.HIGHEST
F32 = jnp.float32
BF16 = jnp.bfloat16


def lasting(microseconds):
    return pl.CostEstimate(
        flops=int(microseconds * 1.1535e9), bytes_accessed=int(microseconds * 1e5), transcendentals=0
    )


def nn(left, right):
    return jnp.dot(left, right, preferred_element_type=F32)


def nt(left, right):
    return lax.dot_general(left, right, (((1,), (1,)), ((), ())), preferred_element_type=F32)


def split(wide):
    high = wide.astype(BF16)
    return high, (wide - high.astype(F32)).astype(BF16)


def each_tile(count, tile, body):
    def step(i, _):
        body(i, pl.ds(pl.multiple_of(i * tile, tile), tile))
        return 0

    lax.fori_loop(0, count // tile, step, 0)


def family_grads(turned, cells, mine, kept, sent):
    halves, width, columns = kept.shape

    def rows_of(i, at):
        total = nn(turned[at, :], cells[...]).astype(BF16)

        @pl.when(mine)
        def _():
            for half in range(halves):
                kept[half, at, :] = total[:, half * columns : (half + 1) * columns]

        @pl.when(jnp.logical_not(mine))
        def _():
            for half in range(halves):
                sent[half, at, :] = total[:, half * columns : (half + 1) * columns]

    each_tile(width, 384, rows_of)


def whole(count):
    return [pl.BlockSpec(memory_space=pltpu.VMEM)] * count


SCALARS = pl.BlockSpec(memory_space=pltpu.SMEM)
PARAMS = pltpu.CompilerParams(vmem_limit_bytes=VMEM_BYTES)


def landmark_onehot(place, rows, landmark_axis):
    shape = (LANDMARKS, rows) if landmark_axis == 0 else (rows, LANDMARKS)
    landmark = lax.broadcasted_iota(jnp.int32, shape, landmark_axis)
    position = place[0] + lax.broadcasted_iota(jnp.int32, shape, 1 - landmark_axis)
    start = lax.shift_right_logical(landmark * place[1] + (LANDMARKS - 1), 6)
    end = lax.shift_right_logical((landmark + 1) * place[1] + (LANDMARKS - 1), 6)
    return jnp.where((position >= start) & (position < end), 1.0, 0.0).astype(BF16)


def live_lanes(place, rows):
    position = place[0] + lax.broadcasted_iota(jnp.int32, (1, rows), 1)
    return position < place[1]


def band(base_row):
    ring = pltpu.roll(jnp.broadcast_to(base_row, (LANES, LANES)), 0, 1, stride=1, stride_axis=0)
    gap = lax.broadcasted_iota(jnp.int32, (LANES, LANES), 0) - lax.broadcasted_iota(
        jnp.int32, (LANES, LANES), 1
    )
    zero = jnp.zeros_like(ring)
    before = jnp.where(gap >= LANES - 16, ring, zero).astype(BF16)
    here = jnp.where(jnp.abs(gap) <= 16, ring, zero).astype(BF16)
    after = jnp.where(gap <= 16 - LANES, ring, zero).astype(BF16)
    return before, here, after


def convolved(blocks, bands):
    count = len(blocks) - 2
    size = blocks[0].shape[0]
    stacked = jnp.concatenate(
        [jnp.concatenate(blocks[i : i + 3], axis=1) for i in range(count)], axis=0
    )
    out = nn(stacked, jnp.concatenate(bands, axis=0))
    return jnp.concatenate([out[i * size : (i + 1) * size] for i in range(count)], axis=1)


def token_sums_kernel(place, tokens, sums):
    sums[...] = nn(landmark_onehot(place, tokens.shape[0], 0), tokens[...])


def token_sums(place, tokens):
    return pl.pallas_call(
        token_sums_kernel,
        out_shape=jax.ShapeDtypeStruct((LANDMARKS, tokens.shape[1]), F32),
        in_specs=[SCALARS] + whole(1),
        out_specs=whole(1)[0],
        compiler_params=PARAMS,
        cost_estimate=lasting(2.5),
        name="token_sums",
    )(place, tokens)


def landmark_counts(place):
    landmark = lax.broadcasted_iota(jnp.int32, (LANDMARKS, 1), 0)
    start = lax.shift_right_logical(landmark * place[1] + (LANDMARKS - 1), 6)
    end = lax.shift_right_logical((landmark + 1) * place[1] + (LANDMARKS - 1), 6)
    return (end - start).astype(F32)


def projection_kernel(
    place, tokens, sums, weights, q_out, k_out, v_out, v_plain, land_q, land_k, turned, kept, sent
):
    rows = tokens.shape[0]
    halves, _, packed = weights.shape
    width = packed // 3
    size = land_q.shape[2]
    position = place[0] + lax.broadcasted_iota(jnp.int32, (rows, 1), 0)
    live = jnp.where(position < place[1], 1.0, 0.0)
    scaled = live * 64**-0.25
    means = jnp.concatenate(split(sums[...] / landmark_counts(place)), axis=0)
    cells = tokens[...]
    turned[...] = cells.T
    for half in range(halves):
        for part, out in enumerate((q_out, k_out, v_out)):
            weight = weights[half, :, part * width : (part + 1) * width]
            low = ((live if part == 2 else scaled) * nn(cells, weight)).astype(BF16)
            out[half * width : (half + 1) * width, :] = low.T
            if part == 2:
                v_plain[:, half * width : (half + 1) * width] = low
                continue
            both = nn(means, weight)
            land = (64**-0.25 * (both[:LANDMARKS] + both[LANDMARKS:])).astype(BF16)
            to = land_k if part else land_q
            for head in range(width // size):
                to[half * (width // size) + head] = land[:, head * size : (head + 1) * size]
    third_heads(place, k_out, v_out, land_q, kept, sent)


def projections(place, tokens, sums, weights, size, owners):
    rows = tokens.shape[0]
    width = weights.shape[0] * weights.shape[2] // 3
    turned = jax.ShapeDtypeStruct((width, rows), BF16)
    land = jax.ShapeDtypeStruct((width // size, LANDMARKS, size), BF16)
    return pl.pallas_call(
        projection_kernel,
        out_shape=(turned, turned, turned, jax.ShapeDtypeStruct((rows, width), BF16), land, land)
        + (jax.ShapeDtypeStruct(tokens.shape[::-1], BF16),)
        + owner_parts(width // size, owners),
        in_specs=[SCALARS] + whole(3),
        out_specs=tuple(whole(9)),
        compiler_params=PARAMS,
        cost_estimate=lasting(18),
        name="projections",
    )(place, tokens, sums, weights)


def by_owner(place, h, owners, kept, sent, values):
    per = kept.shape[1]
    for owner in range(owners):
        @pl.when((h >= owner * per) & (h < (owner + 1) * per))
        def _(owner=owner):
            mine = place[2] == owner % 2

            @pl.when(mine)
            def _():
                kept[owner // 2, h - owner * per] = values

            @pl.when(jnp.logical_not(mine))
            def _():
                sent[owner // 2, h - owner * per] = values


def third_heads(place, keys, values, land_q, kept, sent):
    heads = land_q.shape[0]
    size = land_q.shape[2]
    rows = keys.shape[1]
    owners = 2 * kept.shape[0]
    live = live_lanes(place, rows)

    def head(h):
        at = pl.ds(pl.multiple_of(h * size, size), size)
        scores = jnp.where(live, nn(land_q[h], keys[at, :]), -1e30)
        top = jnp.max(scores, axis=1, keepdims=True)
        raised = jnp.where(live, jnp.exp(scores - top), 0.0)
        total = jnp.sum(raised, axis=1, keepdims=True)
        high, low = split(raised)
        value = values[at, :]
        mixed = nt(high, value) + nt(low, value)
        lane = lax.broadcasted_iota(jnp.int32, (LANDMARKS, LANES - size), 1)
        stats = jnp.where(lane == 0, top, jnp.where(lane == 1, total, 0.0))
        by_owner(place, h, owners, kept, sent, jnp.concatenate([mixed, stats], axis=1))

    def pair(i, _):
        head(2 * i)
        head(2 * i + 1)
        return 0

    lax.fori_loop(0, heads // 2, pair, 0)


def owner_parts(heads, owners):
    part = jax.ShapeDtypeStruct((owners // 2, heads // owners, LANDMARKS, LANES), F32)
    return part, part


def dot_high(left, right):
    return jnp.dot(left, right, preferred_element_type=F32, precision=HIGH)


def dot_high_nt(left, right):
    return lax.dot_general(
        left, right, (((1,), (1,)), ((), ())), preferred_element_type=F32, precision=HIGH
    )


def eye():
    row = lax.broadcasted_iota(jnp.int32, (LANDMARKS, LANDMARKS), 0)
    column = lax.broadcasted_iota(jnp.int32, (LANDMARKS, LANDMARKS), 1)
    return jnp.where(row == column, 1.0, 0.0)


def middle_map(land_q, land_k):
    scores = nt(land_q, land_k)
    raised = jnp.exp(scores - jnp.max(scores, axis=1, keepdims=True))
    return raised / jnp.sum(raised, axis=1, keepdims=True)


def inverse_kernel(place, land_q, land_k, kept_v, kept_p, kept_b, kept_c):
    heads = range(kept_v.shape[1])
    one = eye()
    own = [place[3] * len(heads) + h for h in heads]
    middle = [middle_map(land_q[h], land_k[h]) for h in own]
    approx = [m.T / jnp.sum(m * m, keepdims=True) for m in middle]
    for turn in range(NEWTON):
        product = [dot_high(middle[h], approx[h]) for h in heads]
        for h in heads:
            kept_v[turn, h] = approx[h]
            kept_p[turn, h] = product[h]
        bracket = [7.0 * one - p for p in product]
        bracket = [15.0 * one - dot_high(product[h], bracket[h]) for h in heads]
        for h in heads:
            kept_b[turn, h] = bracket[h]
        bracket = [13.0 * one - dot_high(product[h], bracket[h]) for h in heads]
        for h in heads:
            kept_c[turn, h] = bracket[h]
        approx = [0.25 * dot_high(approx[h], bracket[h]) for h in heads]
    for h in heads:
        kept_v[NEWTON, h] = approx[h]


def inverse_forward(place, land_q, land_k, owners):
    heads = land_q.shape[0] // owners
    square = (heads, LANDMARKS, LANDMARKS)
    return pl.pallas_call(
        inverse_kernel,
        out_shape=(
            jax.ShapeDtypeStruct((NEWTON + 1,) + square, F32),
            jax.ShapeDtypeStruct((NEWTON,) + square, F32),
            jax.ShapeDtypeStruct((NEWTON,) + square, F32),
            jax.ShapeDtypeStruct((NEWTON,) + square, F32),
        ),
        in_specs=[SCALARS] + whole(2),
        out_specs=tuple(whole(4)),
        compiler_params=PARAMS,
        cost_estimate=lasting(7),
        name="inverse_forward",
    )(place, land_q, land_k)


def merged_keys(one, two, size):
    one_top, two_top = one[:, size : size + 1], two[:, size : size + 1]
    top = jnp.maximum(one_top, two_top)
    summed = one * jnp.exp(one_top - top) + two * jnp.exp(two_top - top)
    lane = lax.broadcasted_iota(jnp.int32, one.shape, 1)
    return jnp.where(lane == size, top, summed)


def land_out_kernel(one, two, kept_v, merged, land_out):
    size = land_out.shape[2]
    for h in range(one.shape[0]):
        both = merged_keys(one[h], two[h], size)
        merged[h] = both
        mixed = both[:, :size] / both[:, size + 1 : size + 2]
        land_out[h] = dot_high(kept_v[NEWTON, h], mixed).astype(BF16)


def landmark_out(one, two, kept_v):
    heads = one.shape[0]
    return pl.pallas_call(
        land_out_kernel,
        out_shape=(
            jax.ShapeDtypeStruct(one.shape, F32),
            jax.ShapeDtypeStruct((heads, LANDMARKS, LANES // 2), BF16),
        ),
        in_specs=whole(3),
        out_specs=tuple(whole(2)),
        compiler_params=PARAMS,
        cost_estimate=lasting(2.2),
        name="landmark_out",
    )(one, two, kept_v)


def inverse_back_kernel(
    place, land_q, land_k, merged, grads, kept_v, kept_p, kept_b, kept_c, spread, g_lq, g_lk
):
    heads = range(grads.shape[0])
    size = land_q.shape[2]
    one = eye()
    own = [place[3] * len(heads) + h for h in heads]
    middle = [middle_map(land_q[h], land_k[h]) for h in own]
    turned = [m.T for m in middle]
    g_approx = []
    for h in heads:
        mixed = merged[h][:, :size] / merged[h][:, size + 1 : size + 2]
        g_land = grads[h][:, :size]
        g_approx.append(dot_high_nt(g_land, mixed))
        g_mixed = dot_high(kept_v[NEWTON, h].T, g_land)
        row_dot = jnp.sum(g_mixed * mixed, axis=1, keepdims=True)
        lane = lax.broadcasted_iota(jnp.int32, (LANDMARKS, LANES - size), 1)
        top = merged[h][:, size : size + 1]
        total = merged[h][:, size + 1 : size + 2]
        stats = jnp.where(
            lane == 0, row_dot, jnp.where(lane == 1, top, jnp.where(lane == 2, total, 0.0))
        )
        spread[h] = jnp.concatenate([g_mixed, stats], axis=1)
    g_middle = [jnp.zeros((LANDMARKS, LANDMARKS), F32) for _ in heads]
    for turn in reversed(range(NEWTON)):
        approx = [kept_v[turn, h] for h in heads]
        product = [kept_p[turn, h] for h in heads]
        first = [7.0 * one - p for p in product]
        second = [kept_b[turn, h] for h in heads]
        third = [kept_c[turn, h] for h in heads]
        g_third = [0.25 * dot_high(approx[h].T, g_approx[h]) for h in heads]
        g_back = [0.25 * dot_high_nt(g_approx[h], third[h]) for h in heads]
        g_product = [-dot_high_nt(g_third[h], second[h]) for h in heads]
        pt = [p.T for p in product]
        g_second = [-dot_high(pt[h], g_third[h]) for h in heads]
        g_product = [g_product[h] - dot_high_nt(g_second[h], first[h]) for h in heads]
        g_product = [g_product[h] + dot_high(pt[h], g_second[h]) for h in heads]
        g_middle = [g_middle[h] + dot_high_nt(g_product[h], approx[h]) for h in heads]
        g_approx = [g_back[h] + dot_high(turned[h], g_product[h]) for h in heads]
    for h in heads:
        m = middle[h]
        size_sum = jnp.sum(m * m, keepdims=True)
        g_size = -jnp.sum(g_approx[h] * turned[h], keepdims=True) / (size_sum * size_sum)
        g_m = g_middle[h] + g_approx[h].T / size_sum + 2.0 * g_size * m
        g_scores = m * (g_m - jnp.sum(g_m * m, axis=1, keepdims=True))
        g_lq[h] = dot_high(g_scores, land_k[own[h]].astype(F32))
        g_lk[h] = dot_high(g_scores.T, land_q[own[h]].astype(F32))


def inverse_backward(place, land_q, land_k, merged, grads, *kept):
    heads = grads.shape[0]
    square = jax.ShapeDtypeStruct((heads,) + land_q.shape[1:], F32)
    return pl.pallas_call(
        inverse_back_kernel,
        out_shape=(jax.ShapeDtypeStruct((heads, LANDMARKS, LANES), F32), square, square),
        in_specs=[SCALARS] + whole(8),
        out_specs=tuple(whole(3)),
        compiler_params=PARAMS,
        cost_estimate=lasting(11.5),
        name="inverse_backward",
    )(place, land_q, land_k, merged, grads, *kept)


def first_map(land_k, queries):
    scores = nn(land_k, queries)
    raised = jnp.exp(scores - jnp.max(scores, axis=0, keepdims=True))
    return raised * (1.0 / jnp.sum(raised, axis=0, keepdims=True))


def head_blocks(cells, ends, at):
    rows = cells.shape[1]
    left, right = ends
    return (
        [left[at, :]]
        + [cells[at, i * LANES : (i + 1) * LANES] for i in range(rows // LANES)]
        + [right[at, :]]
    )


def first_conv_kernel(queries, values, left, right, land_k, base, first, conv, ends):
    heads, _, size = land_k.shape
    ends[0] = left[...].T
    ends[1] = right[...].T

    def head(h):
        at = pl.ds(pl.multiple_of(h * size, size), size)
        first[at, :] = first_map(land_k[h], queries[at, :]).astype(BF16)
        blocks = head_blocks(values, (ends.at[0], ends.at[1]), at)
        conv[at, :] = convolved(blocks, band(base[pl.ds(h, 1), :]))

    def pair(i, _):
        head(2 * i)
        head(2 * i + 1)
        return 0

    lax.fori_loop(0, heads // 2, pair, 0)


def first_and_conv(queries, values, left, right, land_k, base):
    width, rows = queries.shape
    return pl.pallas_call(
        first_conv_kernel,
        out_shape=(
            jax.ShapeDtypeStruct((width, rows), BF16),
            jax.ShapeDtypeStruct((width, rows), F32),
        ),
        in_specs=whole(6),
        out_specs=tuple(whole(2)),
        scratch_shapes=[pltpu.VMEM((2, width, LANES), BF16)],
        compiler_params=PARAMS,
        cost_estimate=lasting(8),
        name="first_and_conv",
    )(queries, values, left, right, land_k, base)


def context_rows(first, conv, land_out, context):
    heads, _, size = land_out.shape

    def head(h):
        at = pl.ds(pl.multiple_of(h * size, size), size)
        return (nn(land_out[h].T, first[at, :]) + conv[at, :]).astype(BF16)

    def pair(i, _):
        both = jnp.concatenate([head(2 * i), head(2 * i + 1)], axis=0)
        context[:, pl.ds(pl.multiple_of(i * LANES, LANES), LANES)] = both.T
        return 0

    lax.fori_loop(0, heads // 2, pair, 0)


def attention_back_kernel(
    place, queries, grads, land_k, land_out, kept, sent, g_lk, g_query
):
    heads, _, size = land_k.shape
    rows = queries.shape[1]
    owners = 2 * kept.shape[0]
    scaled = jnp.where(live_lanes(place, rows), 64**-0.25, 0.0)

    def pair(i, _):
        lanes = pl.ds(pl.multiple_of(i * LANES, LANES), LANES)
        turned = grads[:, lanes].T
        g_queries, g_keys = [], []
        for side in range(2):
            h = 2 * i + side
            query = queries[pl.ds(pl.multiple_of(h * size, size), size), :]
            g_context = turned[side * size : (side + 1) * size]
            first = first_map(land_k[h], query)
            g_first = nn(land_out[h], g_context)
            inner = jnp.sum(g_first * first, axis=0, keepdims=True)
            g_scores = (first * (g_first - inner)).astype(BF16)
            g_land = nt(first.astype(BF16), g_context)
            g_key = nt(g_scores, query)
            by_owner(place, h, owners, kept, sent, jnp.concatenate([g_land, g_key], axis=1))
            g_keys.append(g_key)
            g_queries.append((scaled * nn(land_k[h].T, g_scores)).astype(BF16))
        g_query[:, lanes] = jnp.concatenate(g_queries, axis=0).T
        g_lk[:, lanes] = jnp.concatenate(g_keys, axis=1)
        return 0

    lax.fori_loop(0, heads // 2, pair, 0)


def attention_back(place, queries, grads, land_k, land_out, owners):
    width, rows = queries.shape
    heads = land_k.shape[0]
    return pl.pallas_call(
        attention_back_kernel,
        out_shape=owner_parts(heads, owners)
        + (
            jax.ShapeDtypeStruct((LANDMARKS, width), F32),
            jax.ShapeDtypeStruct((rows, width), BF16),
        ),
        in_specs=[SCALARS] + whole(4),
        out_specs=tuple(whole(4)),
        compiler_params=PARAMS,
        cost_estimate=lasting(11.4),
        name="attention_back",
    )(place, queries, grads, land_k, land_out)


def conv_back_kernel(
    v_plain, v_left, v_right, grads, g_left, g_right, base_back, g_value, g_taps, ends
):
    heads = g_taps.shape[0]
    rows, width = grads.shape
    size = width // heads
    blocks_in = rows // LANES
    row = lax.broadcasted_iota(jnp.int32, (LANES, LANES), 0)
    column = lax.broadcasted_iota(jnp.int32, (LANES, LANES), 1)
    reverse = jnp.where(row + column == LANES - 1, 1.0, 0.0).astype(BF16)
    gap = jnp.concatenate([row - column, row - column], axis=1)
    ends[0] = g_left[...].T
    ends[1] = g_right[...].T

    def pair(i, _):
        lanes = pl.ds(pl.multiple_of(i * LANES, LANES), LANES)
        turned = grads[:, lanes].T
        plain = [v_left[LANES - 16 :, lanes]]
        plain += [v_plain[b * LANES : (b + 1) * LANES, lanes] for b in range(blocks_in)]
        plain += [v_right[:16, lanes]]
        for side in range(2):
            h = 2 * i + side
            at = pl.ds(pl.multiple_of(h * size, size), size)
            g_context = turned[side * size : (side + 1) * size]
            blocks = [ends[0, at, :]]
            blocks += [g_context[:, b * LANES : (b + 1) * LANES] for b in range(blocks_in)]
            blocks += [ends[1, at, :]]
            g_value[at, :] = convolved(blocks, band(base_back[pl.ds(h, 1), :]))

        def around(b):
            prior = plain[0] if b == 0 else plain[b][LANES - 16 :]
            return jnp.concatenate([prior, plain[b + 1], plain[b + 2][:16]], axis=0)

        def by_head(b):
            piece = turned[:, b * LANES : (b + 1) * LANES]
            zero = jnp.zeros_like(piece)
            return jnp.concatenate(
                [jnp.where(row < size, piece, zero), jnp.where(row >= size, piece, zero)], axis=1
            )

        total = jnp.zeros((LANES + 32, 2 * LANES), F32)
        for b in range(0, blocks_in, 2):
            total = total + nn(
                jnp.concatenate([around(b), around(b + 1)], axis=1),
                jnp.concatenate([by_head(b), by_head(b + 1)], axis=0),
            )
        empty = jnp.zeros((LANES - 16, 2 * LANES), F32)
        before, here, after = total[:16], total[16 : 16 + LANES], total[16 + LANES :]
        ring = jnp.where(jnp.abs(gap) <= 16, here, 0.0)
        ring = ring + jnp.where(gap >= LANES - 16, jnp.concatenate([empty, before], axis=0), 0.0)
        ring = ring + jnp.where(gap <= 16 - LANES, jnp.concatenate([after, empty], axis=0), 0.0)
        high, low = split(ring)
        lowest = (ring - high.astype(F32) - low.astype(F32)).astype(BF16)
        flat = nn(reverse, high) + nn(reverse, low) + nn(reverse, lowest)
        for side in range(2):
            straight = pltpu.roll(
                flat[:, side * LANES : (side + 1) * LANES], 0, 1, stride=1, stride_axis=0
            )
            g_taps[pl.ds(2 * i + side, 1), :] = jnp.sum(straight, axis=0, keepdims=True)
        return 0

    lax.fori_loop(0, heads // 2, pair, 0)


def conv_back(v_plain, v_ends, grads, g_ends, base_back):
    rows, width = grads.shape
    heads = base_back.shape[0]
    return pl.pallas_call(
        conv_back_kernel,
        out_shape=(
            jax.ShapeDtypeStruct((width, rows), F32),
            jax.ShapeDtypeStruct((heads, LANES), F32),
        ),
        in_specs=whole(7),
        out_specs=tuple(whole(2)),
        scratch_shapes=[pltpu.VMEM((2, width, LANES), BF16)],
        compiler_params=PARAMS,
        cost_estimate=lasting(13.6),
        name="conv_back",
    )(v_plain, *v_ends, grads, *g_ends, base_back)


def third_back_kernel(
    place, keys, values, land_q, spread, g_conv, lq_mid, lk_mid, g_lk, last, first, taps, turned,
    g_k, g_v, sums, kept, sent,
):
    heads, _, size = land_q.shape
    rows, width = g_k.shape
    own_heads = lq_mid.shape[0]
    scale = 64**-0.25
    sums[LANDMARKS:, :] = jnp.zeros((sums.shape[0] - LANDMARKS, 2 * width), F32)
    sums[LANDMARKS : LANDMARKS + 1, :] = last[...]
    sums[LANDMARKS + 1 : LANDMARKS + 2, :] = first[...]
    for h in range(heads):
        sums[LANDMARKS + 2 : LANDMARKS + 3, h * LANES : (h + 1) * LANES] = taps[h : h + 1, :]

    def mid(part, h):
        at = h - place[3] * own_heads
        mine = (at >= 0) & (at < own_heads) & (place[5] == 0)
        inside = jnp.clip(at, 0, own_heads - 1)
        return jnp.where(mine, part[inside], 0.0)

    live = live_lanes(place, rows)
    live_row = jnp.where(live, 1.0, 0.0)
    scaled_row = live_row * 64**-0.25

    def pair(i, _):
        lanes = pl.ds(pl.multiple_of(i * LANES, LANES), LANES)
        g_keys, g_values, g_lqs, lks = [], [], [], []
        for side in range(2):
            h = 2 * i + side
            at = pl.ds(pl.multiple_of(h * size, size), size)
            key, value = keys[at, :], values[at, :]
            pack = spread[h]
            g_mixed = pack[:, :size]
            row_dot = pack[:, size : size + 1]
            top = pack[:, size + 1 : size + 2]
            total = pack[:, size + 2 : size + 3]
            scores = nn(land_q[h], key)
            third = jnp.where(live, jnp.exp(scores - top), 0.0) * (1.0 / total)
            gm_high, gm_low = split(g_mixed)
            g_third = nn(gm_high, value) + nn(gm_low, value)
            g_high, g_low = split(third * (g_third - row_dot))
            g_lqs.append(nt(g_high, key) + nt(g_low, key) + mid(lq_mid, h))
            lks.append(mid(lk_mid, h))
            turned = land_q[h].T
            g_key = nn(turned, g_high) + nn(turned, g_low)
            g_keys.append((scaled_row * g_key).astype(BF16))
            t_high, t_low = split(third)
            gmt_high, gmt_low = split(g_mixed.T)
            g_value = nn(gmt_high, t_high) + nn(gmt_high, t_low) + nn(gmt_low, t_high)
            g_values.append((live_row * (g_value + g_conv[at, :])).astype(BF16))
        g_k[:, lanes] = jnp.concatenate(g_keys, axis=0).T
        g_v[:, lanes] = jnp.concatenate(g_values, axis=0).T
        sums[:LANDMARKS, lanes] = scale * jnp.concatenate(g_lqs, axis=1)
        key_lanes = pl.ds(pl.multiple_of(width + i * LANES, LANES), LANES)
        sums[:LANDMARKS, key_lanes] = scale * (g_lk[:, lanes] + jnp.concatenate(lks, axis=1))
        return 0

    lax.fori_loop(0, heads // 2, pair, 0)
    for number, cells in enumerate((g_k, g_v)):
        family_grads(turned, cells, place[2] == number, kept, sent)


def third_back(
    place, keys, values, land_q, spread, g_conv, lq_mid, lk_mid, g_lk, last, first, taps, turned, halves
):
    width, rows = keys.shape
    plain = jax.ShapeDtypeStruct((rows, width), BF16)
    return pl.pallas_call(
        third_back_kernel,
        out_shape=(plain, plain, jax.ShapeDtypeStruct((LANDMARKS + 8, 2 * width), F32))
        + (jax.ShapeDtypeStruct((halves, width, width // halves), BF16),) * 2,
        in_specs=[SCALARS] + whole(12),
        out_specs=tuple(whole(5)),
        compiler_params=PARAMS,
        cost_estimate=lasting(17),
        name="third_back",
    )(
        place, keys, values, land_q, spread, g_conv, lq_mid, lk_mid, g_lk, last, first, taps, turned
    )


def centred_rows(rows):
    centred = rows - jnp.mean(rows, axis=1, keepdims=True)
    scale = lax.rsqrt(jnp.mean(centred * centred, axis=1, keepdims=True) + 1e-05)
    return centred * scale, scale


def norm_back(grads, gain, unit, scale):
    scaled = grads * gain
    inner = jnp.mean(scaled * unit, axis=1, keepdims=True)
    return scale * (scaled - jnp.mean(scaled, axis=1, keepdims=True) - unit * inner)


def gelu_pair(hidden):
    share = 0.5 * (1.0 + lax.erf(hidden * 0.7071067811865476))
    density = jnp.exp(-0.5 * hidden * hidden) * 0.3989422804014327
    return hidden * share, share + hidden * density


class Copies:
    def __init__(self, sems):
        self.sems, self.used, self.open = sems, 0, []

    def start(self, source, target):
        copy = pltpu.make_async_copy(source, target, self.sems.at[self.used])
        self.used += 1
        copy.start()
        return copy

    def out(self, source, target):
        self.open.append(self.start(source, target))

    def finish(self):
        for copy in self.open:
            copy.wait()


def weight_grad(turned, cells, halves, which, out):
    ff = cells.shape[1] // halves
    columns = ff // 2
    for half in range(halves):
        from_column = pl.ds(pl.multiple_of(half * ff + which * columns, columns), columns)

        def rows_of(i, at, half=half, from_column=from_column):
            out[half, at, :] = nn(turned[at, :], cells[:, from_column]).astype(BF16)

        each_tile(turned.shape[0], 384, rows_of)


def feed_kernel(
    place, first_in, conv_in, land_out, tokens_in, cotangent_in, weights,
    output_to, context_to, slope_to, g_fed_to, g_second_to, unit_to, scale_to, turned_to, active_to, fed_turned_to, sent_to,
    norm_grads, in_w, down_w, out_w, norms, conv, context, tokens, cotangent,
    low, unit, scales, fed, active, slopes, g_fed, g_fed_turned, normed_turned, output, sent,
    sems,
):
    rows, width = tokens.shape
    halves, _, ff = in_w.shape
    part = out_w.shape[2]
    tile = 256
    copies = Copies(sems)
    context_copies = [copies.start(first_in, g_fed_turned), copies.start(conv_in, conv)]
    early = [
        copies.start(weights.at[:, :, pl.ds(2 * ff, part)], out_w),
        copies.start(tokens_in, tokens),
        copies.start(weights.at[:, :, pl.ds(2 * ff + part, LANES)], norms),
    ]
    in_copy = copies.start(weights.at[:, :, pl.ds(0, ff)], in_w)
    down_copy = copies.start(weights.at[:, :, pl.ds(ff, ff)], down_w)
    cotangent_copy = copies.start(cotangent_in, cotangent)
    for copy in context_copies:
        copy.wait()
    context_rows(g_fed_turned, conv, land_out, context)
    copies.out(context, context_to)
    for copy in early:
        copy.wait()
    columns = norms[0].astype(F32).T
    gain0, gain1 = columns[0:1], columns[1:2]
    shift0, shift1 = columns[2:3], columns[3:4]
    norm_grads[...] = jnp.zeros_like(norm_grads)

    def project(i, at):
        attended = nt(context[at, :part], out_w[0])
        for half in range(1, halves):
            attended = attended + nt(context[at, half * part : (half + 1) * part], out_w[half])
        rows_unit, scale = centred_rows(tokens[at, :].astype(F32) + attended)
        unit[at, :] = rows_unit
        scales[at, :] = jnp.broadcast_to(scale, (tile, LANES))
        normed = (rows_unit * gain0 + shift0).astype(BF16)
        low[at, :] = normed
        normed_turned[:, at] = normed.T

    each_tile(rows, tile, project)
    copies.out(unit, unit_to)
    copies.out(scales, scale_to)
    copies.out(normed_turned, turned_to)
    in_copy.wait()
    big = 512

    def hidden_rows(i, at):
        for half in range(halves):
            value, slope = gelu_pair(nn(low[at, :], in_w[half]))
            active[at, half * ff : (half + 1) * ff] = value.astype(BF16)
            slopes[at, half * ff : (half + 1) * ff] = slope.astype(BF16)

    each_tile(rows, tile, hidden_rows)
    copies.out(slopes, slope_to)
    copies.out(active, active_to)
    down_copy.wait()

    def fed_rows(i, at):
        total = nt(active[at, :ff], down_w[0])
        for half in range(1, halves):
            total = total + nt(active[at, half * ff : (half + 1) * ff], down_w[half])
        fed[at, :] = total

    each_tile(rows, big, fed_rows)
    cotangent_copy.wait()

    def second_norm(i, at):
        normed = unit[at, :] * gain0 + shift0
        unit1, scale1 = centred_rows(normed + fed[at, :])
        position = place[0] + i * tile + lax.broadcasted_iota(jnp.int32, (tile, 1), 0)
        live = jnp.where(position < place[1], 1.0, 0.0)
        output[at, :] = (live * (unit1 * gain1 + shift1)).astype(BF16)
        grads = live * cotangent[at, :].astype(F32)
        norm_grads[:, :width] += jnp.sum(grads * unit1, axis=0, keepdims=True)
        norm_grads[:, width:] += jnp.sum(grads, axis=0, keepdims=True)
        second = norm_back(grads, gain1, unit1, scale1)
        fed[at, :] = second
        g_low = second.astype(BF16)
        g_fed[at, :] = g_low
        g_fed_turned[:, at] = g_low.T

    each_tile(rows, tile, second_norm)
    copies.out(output, output_to)
    copies.out(fed, g_second_to)
    copies.out(g_fed, g_fed_to)
    copies.out(g_fed_turned, fed_turned_to)
    weight_grad(g_fed_turned, active, halves, 1 - place[2], sent)
    copies.out(sent, sent_to)
    copies.finish()


ANYWHERE = pl.BlockSpec(memory_space=pl.ANY)


def feed_forward(place, first, conv, land_out, tokens, cotangent, weights, ff, part):
    rows, width = tokens.shape
    halves = weights.shape[0]
    grad = (halves, width, ff // 2)
    shapes = [
        ((rows, width), BF16), ((rows, width), BF16), ((rows, halves * ff), BF16),
        ((rows, width), BF16), ((rows, width), F32), ((rows, width), F32), ((rows, LANES), F32), ((width, rows), BF16),
        ((rows, halves * ff), BF16), ((width, rows), BF16), (grad, BF16), ((1, 2 * width), F32),
    ]
    scratch = [
        ((halves, width, ff), BF16), ((halves, width, ff), BF16), ((halves, width, part), BF16),
        ((halves, width, LANES), BF16), ((width, rows), F32), ((rows, width), BF16),
        ((rows, width), BF16), ((rows, width), BF16),
        ((rows, width), BF16), ((rows, width), F32), ((rows, LANES), F32), ((rows, width), F32),
        ((rows, halves * ff), BF16), ((rows, halves * ff), BF16), ((rows, width), BF16),
        ((width, rows), BF16), ((width, rows), BF16), ((rows, width), BF16), (grad, BF16),
    ]
    return pl.pallas_call(
        feed_kernel,
        out_shape=tuple(jax.ShapeDtypeStruct(*shape) for shape in shapes),
        in_specs=[SCALARS] + [ANYWHERE] * 2 + whole(1) + [ANYWHERE] * 3,
        out_specs=tuple([ANYWHERE] * 11 + whole(1)),
        scratch_shapes=[pltpu.VMEM(*shape) for shape in scratch]
        + [pltpu.SemaphoreType.DMA((19,))],
        compiler_params=PARAMS,
        cost_estimate=lasting(32),
        name="feed_forward",
    )(place, first, conv, land_out, tokens, cotangent, weights)


def feed_back_kernel(
    place, slope_in, g_fed_in, g_second_in, unit_in, scale_in, turned_in, weights,
    g_first_to, g_context_to, g_hidden_to, sent_to, att_turned_to, norm_grads,
    in_w, down_w, out_w, norms, g_hidden, g_fed, second, unit, scales, normed_turned,
    g_att, g_att_turned, g_context, sent,
    sems,
):
    rows, width = second.shape
    halves, _, ff = in_w.shape
    part = out_w.shape[2]
    tile = 256
    copies = Copies(sems)
    early = [
        copies.start(g_fed_in, g_fed),
        copies.start(weights.at[:, :, pl.ds(ff, ff)], down_w),
        copies.start(slope_in, g_hidden),
    ]
    later = [
        copies.start(turned_in, normed_turned),
        copies.start(weights.at[:, :, pl.ds(0, ff)], in_w),
        copies.start(g_second_in, second),
        copies.start(unit_in, unit),
        copies.start(scale_in, scales),
        copies.start(weights.at[:, :, pl.ds(2 * ff + part, LANES)], norms),
        copies.start(weights.at[:, :, pl.ds(2 * ff, part)], out_w),
    ]
    for copy in early:
        copy.wait()
    norm_grads[...] = jnp.zeros_like(norm_grads)
    big = 512

    def back_rows(i, at):
        for half in range(halves):
            g_act = nn(g_fed[at, :], down_w[half])
            to = slice(half * ff, (half + 1) * ff)
            g_hidden[at, to] = (g_act * g_hidden[at, to].astype(F32)).astype(BF16)

    each_tile(rows, big, back_rows)
    copies.out(g_hidden, g_hidden_to)
    later.pop(0).wait()
    weight_grad(normed_turned, g_hidden, halves, 1 - place[2], sent)
    copies.out(sent, sent_to)
    for copy in later:
        copy.wait()
    gain0 = norms[0].astype(F32).T[0:1]

    def normed_rows(i, at):
        total = second[at, :]
        for half in range(halves):
            total = total + nt(g_hidden[at, half * ff : (half + 1) * ff], in_w[half])
        second[at, :] = total

    each_tile(rows, big, normed_rows)

    def first_norm(i, at):
        grads = second[at, :]
        rows_unit, scale = unit[at, :], scales[at, 0:1]
        norm_grads[:, :width] += jnp.sum(grads * rows_unit, axis=0, keepdims=True)
        norm_grads[:, width:] += jnp.sum(grads, axis=0, keepdims=True)
        first = norm_back(grads, gain0, rows_unit, scale)
        second[at, :] = first
        low = first.astype(BF16)
        g_att[at, :] = low
        g_att_turned[:, at] = low.T

    each_tile(rows, tile, first_norm)
    copies.out(second, g_first_to)
    copies.out(g_att_turned, att_turned_to)
    for half in range(halves):
        g_context[:, half * part : (half + 1) * part] = nn(g_att[...], out_w[half]).astype(BF16)
    copies.out(g_context, g_context_to)
    copies.finish()


def feed_backward(place, fed, weights, ff, part):
    rows, width = fed[1].shape
    halves = weights.shape[0]
    grad = (halves, width, ff // 2)
    shapes = [
        ((rows, width), F32), ((rows, width), BF16), ((rows, halves * ff), BF16), (grad, BF16),
        ((width, rows), BF16), ((1, 2 * width), F32),
    ]
    scratch = [
        ((halves, width, ff), BF16), ((halves, width, ff), BF16), ((halves, width, part), BF16),
        ((halves, width, LANES), BF16), ((rows, halves * ff), BF16), ((rows, width), BF16),
        ((rows, width), F32), ((rows, width), F32),
        ((rows, LANES), F32), ((width, rows), BF16),
        ((rows, width), BF16), ((width, rows), BF16), ((rows, width), BF16), (grad, BF16),
    ]
    return pl.pallas_call(
        feed_back_kernel,
        out_shape=tuple(jax.ShapeDtypeStruct(*shape) for shape in shapes),
        in_specs=[SCALARS] + [ANYWHERE] * 7,
        out_specs=tuple([ANYWHERE] * 5 + whole(1)),
        scratch_shapes=[pltpu.VMEM(*shape) for shape in scratch]
        + [pltpu.SemaphoreType.DMA((16,))],
        compiler_params=PARAMS,
        cost_estimate=lasting(27),
        name="feed_backward",
    )(place, *fed, weights)


def kept_kernel(place, turned_in, cells_in, kept, turned, cells, sems):
    halves, width, columns = kept.shape
    ff = 2 * columns
    copies = Copies(sems)
    turned_copy = copies.start(turned_in, turned)
    pieces = []
    for half in range(halves):
        start = pl.multiple_of(half * ff + place[2] * columns, columns)
        pieces.append(copies.start(cells_in.at[:, pl.ds(start, columns)], cells.at[half]))
    turned_copy.wait()
    for half in range(halves):
        pieces[half].wait()

        def rows_of(i, at, half=half):
            kept[half, at, :] = nn(turned[at, :], cells[half]).astype(BF16)

        each_tile(width, 384, rows_of)


def kept_grad(place, turned, cells, halves):
    width, rows = turned.shape
    columns = cells.shape[1] // halves // 2
    return pl.pallas_call(
        kept_kernel,
        out_shape=jax.ShapeDtypeStruct((halves, width, columns), BF16),
        in_specs=[SCALARS] + [ANYWHERE] * 2,
        out_specs=whole(1)[0],
        scratch_shapes=[
            pltpu.VMEM((width, rows), BF16),
            pltpu.VMEM((halves, rows, columns), BF16),
            pltpu.SemaphoreType.DMA((3,)),
        ],
        compiler_params=PARAMS,
        cost_estimate=lasting(5),
        name="kept_grad",
    )(place, turned, cells)


def spread_kernel(place, turned_in, cells_in, other, kept, sent, turned, cells, sems):
    halves, width, columns = other.shape
    ff = 2 * columns
    quarter = columns // 2
    copies = Copies(sems)
    turned_copy = copies.start(turned_in, turned)
    pieces = []
    for half in range(halves):
        start = pl.multiple_of(half * ff + place[2] * columns, columns)
        pieces.append(copies.start(cells_in.at[:, pl.ds(start, columns)], cells.at[half]))
    turned_copy.wait()
    for half in range(halves):
        pieces[half].wait()

        def rows_of(i, at, half=half):
            total = nn(turned[at, :], cells[half]) + other[half, at, :].astype(F32)
            low = total.astype(BF16)
            first = place[4] == 0
            kept[half, at, :] = jnp.where(first, low[:, :quarter], low[:, quarter:])
            sent[half, at, :] = jnp.where(first, low[:, quarter:], low[:, :quarter])

        each_tile(width, 384, rows_of)


def spread_grad(place, turned, cells, other):
    halves, width, columns = other.shape
    rows = turned.shape[1]
    part = jax.ShapeDtypeStruct((halves, width, columns // 2), BF16)
    return pl.pallas_call(
        spread_kernel,
        out_shape=(part, part),
        in_specs=[SCALARS] + [ANYWHERE] * 2 + whole(1),
        out_specs=tuple(whole(2)),
        scratch_shapes=[
            pltpu.VMEM((width, rows), BF16),
            pltpu.VMEM((halves, rows, columns), BF16),
            pltpu.SemaphoreType.DMA((3,)),
        ],
        compiler_params=PARAMS,
        cost_estimate=lasting(6),
        name="spread_grad",
    )(place, turned, cells, other)


def pair_kernel(
    place, one_turned_in, one_cells_in, two_turned_in, two_cells_in, kept, sent,
    one_turned, one_cells, two_turned, two_cells, sems,
):
    copies = Copies(sems)
    loads = [
        copies.start(*pair)
        for pair in (
            (one_turned_in, one_turned), (one_cells_in, one_cells),
            (two_turned_in, two_turned), (two_cells_in, two_cells),
        )
    ]
    for number, (turned, cells) in enumerate(((one_turned, one_cells), (two_turned, two_cells))):
        loads[2 * number].wait()
        loads[2 * number + 1].wait()
        family_grads(turned, cells, place[2] == number, kept, sent)


def pair_grads(place, one_turned, one_cells, two_turned, two_cells, halves):
    width, rows = one_turned.shape
    shape = jax.ShapeDtypeStruct((halves, width, one_cells.shape[1] // halves), BF16)
    return pl.pallas_call(
        pair_kernel,
        out_shape=(shape, shape),
        in_specs=[SCALARS] + [ANYWHERE] * 4,
        out_specs=tuple(whole(2)),
        scratch_shapes=[
            pltpu.VMEM((width, rows), BF16), pltpu.VMEM(one_cells.shape, BF16),
            pltpu.VMEM((width, rows), BF16), pltpu.VMEM(one_cells.shape, BF16),
            pltpu.SemaphoreType.DMA((4,)),
        ],
        compiler_params=PARAMS,
        cost_estimate=lasting(6),
        name="pair_grads",
    )(place, one_turned, one_cells, two_turned, two_cells)


def rank_kernel(place, mine, got, land_tokens, weights, late, through, small):
    halves, width, _ = weights.shape
    part = late.shape[1] // 2
    first = place[2] == 0
    grads = (
        jnp.where(first, mine[:LANDMARKS], got[:LANDMARKS]),
        jnp.where(first, got[:LANDMARKS], mine[:LANDMARKS]),
    )
    counts = landmark_counts(place)
    total = jnp.zeros((2 * LANDMARKS, width), F32)
    for index, grad in enumerate(grads):
        both = jnp.concatenate(split(grad / counts), axis=0)
        for half in range(halves):
            weight = weights[half, :, index * part : (index + 1) * part]
            total = total + nt(both[:, half * part : (half + 1) * part], weight)
    through[...] = jnp.concatenate(split(total[:LANDMARKS] + total[LANDMARKS:]), axis=0)
    zero = jnp.zeros((LANDMARKS, part), F32)
    own = []
    for index, grad in enumerate(grads):
        columns = grad[:, :part]
        for half in range(1, halves):
            columns = jnp.where(place[5] == half, grad[:, half * part : (half + 1) * part], columns)
        own.append(jnp.where(place[2] == 1 - index, columns, zero))
    high, low = split(jnp.concatenate(own, axis=1))
    mean_high, mean_low = split(land_tokens[...] / counts)
    means = jnp.concatenate([mean_high, mean_low, mean_high, jnp.zeros_like(mean_low)], axis=0).T
    factors = jnp.concatenate([high, high, low, jnp.zeros_like(low)], axis=0)
    late[...] = nn(means, factors).astype(BF16)
    gains = jnp.where(first, mine[LANDMARKS:], got[LANDMARKS:])
    shifts = jnp.where(first, got[LANDMARKS:], mine[LANDMARKS:])
    taps = jnp.where(place[5] == 0, gains[2:3], shifts[2:3])
    rows = [gains[1:2], gains[0:1], shifts[1:2], shifts[0:1], taps]
    rows.append(jnp.zeros((small.shape[0] - len(rows), width), F32))
    small[...] = jnp.concatenate(rows, axis=0).astype(BF16)


def rank_parts(place, mine, got, land_tokens, weights):
    halves, width, packed = weights.shape
    return pl.pallas_call(
        rank_kernel,
        out_shape=(
            jax.ShapeDtypeStruct((width, 2 * packed // 3), BF16),
            jax.ShapeDtypeStruct((2 * LANDMARKS, width), BF16),
            jax.ShapeDtypeStruct((16, width), BF16),
        ),
        in_specs=[SCALARS] + whole(4),
        out_specs=tuple(whole(3)),
        compiler_params=PARAMS,
        cost_estimate=lasting(4),
        name="rank_parts",
    )(place, mine, got, land_tokens, weights)


def token_grad_kernel(
    back_in, g_k_in, g_v_in, weights, own_grad, back, g_k, g_v, k_w, v_w, sems
):
    rows, width = back.shape
    halves, _, part = k_w.shape
    copies = Copies(sems)
    first = [
        copies.start(g_k_in, g_k),
        copies.start(weights.at[:, :, pl.ds(part, part)], k_w),
    ]
    later = [
        copies.start(back_in, back),
        copies.start(g_v_in, g_v),
        copies.start(weights.at[:, :, pl.ds(2 * part, part)], v_w),
    ]
    for copy in first + later:
        copy.wait()

    def rows_of(i, at):
        total = back[at, :]
        for half in range(halves):
            columns = slice(half * part, (half + 1) * part)
            total = total + nt(g_k[at, columns], k_w[half]) + nt(g_v[at, columns], v_w[half])
        own_grad[at, :] = total.astype(BF16)

    each_tile(rows, 512, rows_of)


def token_grad(back, g_k, g_v, weights):
    rows, width = back.shape
    halves, _, packed = weights.shape
    shapes = [((rows, width), F32), ((rows, width), BF16), ((rows, width), BF16)]
    shapes += [((halves, width, packed // 3), BF16)] * 2
    return pl.pallas_call(
        token_grad_kernel,
        out_shape=jax.ShapeDtypeStruct((rows, width), BF16),
        in_specs=[ANYWHERE] * 4,
        out_specs=whole(1)[0],
        scratch_shapes=[pltpu.VMEM(*shape) for shape in shapes]
        + [pltpu.SemaphoreType.DMA((5,))],
        compiler_params=PARAMS,
        cost_estimate=lasting(6),
        name="token_grad",
    )(back, g_k, g_v, weights)


def flipped(values, axis, bit):
    count = lax.axis_size(axis)
    return lax.ppermute(values, axis, [(i, i ^ bit) for i in range(count)])


def side_of(axis, bit):
    return (lax.axis_index(axis) // bit) % 2


def paired(mine, axis, bit, dim):
    other = flipped(mine, axis, bit)
    both = jnp.zeros(mine.shape[:dim] + (2,) + mine.shape[dim:], mine.dtype)
    side = side_of(axis, bit)
    both = lax.dynamic_update_slice_in_dim(both, jnp.expand_dims(mine, dim), side, dim)
    return lax.dynamic_update_slice_in_dim(both, jnp.expand_dims(other, dim), 1 - side, dim)


def ctx_bits():
    bits, bit = [], 1
    while bit < lax.axis_size("ctx"):
        bits.append(bit)
        bit *= 2
    return bits


def sequence_start(values):
    width = values.shape[1] // 2
    side = side_of("ctx", 1)
    kept = lax.dynamic_slice_in_dim(values, side * width, width, axis=1)
    sent = lax.dynamic_slice_in_dim(values, (1 - side) * width, width, axis=1)
    kept = kept + flipped(sent, "ctx", 1)
    return kept + flipped(kept, "tp", 1)


def sequence_end(kept):
    for bit in ctx_bits()[1:]:
        kept = kept + flipped(kept, "ctx", bit)
    return kept, flipped(kept, "ctx", 1)


def joined_halves(kept, other):
    return jnp.where(
        side_of("ctx", 1) == 0,
        jnp.concatenate([kept, other], axis=1),
        jnp.concatenate([other, kept], axis=1),
    )


def to_owner(kept, sent, combine):
    kept = combine(kept, flipped(sent, "ctx", 1))
    for bit in ctx_bits()[1:]:
        view = kept.reshape((-1, 2) + kept.shape[1:])
        side = side_of("ctx", bit)
        sent = lax.dynamic_index_in_dim(view, 1 - side, 1, False)
        kept = lax.dynamic_index_in_dim(view, side, 1, False)
        kept = combine(kept, flipped(sent, "ctx", bit))
    return kept[0], flipped(kept[0], "tp", 1)


def from_owners(part):
    whole_part = part[None]
    for bit in reversed(ctx_bits()):
        both = paired(whole_part, "ctx", bit, 1)
        whole_part = both.reshape((-1,) + part.shape)
    return whole_part.reshape((-1,) + part.shape[1:])


def merge_keys(one, two):
    size = LANES // 2
    one_top, two_top = one[..., size : size + 1], two[..., size : size + 1]
    top = jnp.maximum(one_top, two_top)
    one_factor, two_factor = jnp.exp(one_top - top), jnp.exp(two_top - top)
    summed = one * one_factor + two * two_factor
    lane = lax.broadcasted_iota(jnp.int32, summed.shape, summed.ndim - 1)
    return jnp.where(lane == size, top, summed)


def neighbour_rows(cells, count):
    pieces = lax.axis_size("ctx") * lax.axis_size("tp")
    up = [(i, i + 1) for i in range(pieces - 1)]
    before = lax.ppermute(cells[-count:], ("ctx", "tp"), up)
    after = lax.ppermute(cells[:count], ("ctx", "tp"), [(j, i) for i, j in up])
    return (
        jnp.pad(before, ((LANES - count, 0), (0, 0))),
        jnp.pad(after, ((0, LANES - count), (0, 0))),
    )


def own_quarter(shard):
    rows = shard.shape[0] // lax.axis_size("ctx")
    return lax.dynamic_slice_in_dim(shard, lax.axis_index("ctx") * rows, rows, axis=0)


def gathered(shard):
    full = lax.all_gather(own_quarter(shard), ("tp", "fsdp", "ctx"), tiled=True)
    return full.reshape(lax.axis_size("tp"), -1, shard.shape[1])


def gathered_early(shard, beside):
    count = lax.axis_size("fsdp")
    piece = own_quarter(shard)
    if count > 4:
        held = lax.all_gather(piece, "fsdp")
    else:
        here = lax.axis_index("fsdp")
        held = jnp.zeros((count,) + piece.shape, piece.dtype)
        held = lax.dynamic_update_slice_in_dim(held, piece[None], here, 0)
        for step in range(1, count):
            moved = lax.ppermute(piece, "fsdp", [(i, (i + step) % count) for i in range(count)])
            held = lax.dynamic_update_slice_in_dim(held, moved[None], (here - step) % count, 0)
    held, beside = gate(held, beside)
    bits = ctx_bits()
    halves = []
    for number, half in enumerate((held[: count // 2], held[count // 2 :])):
        half = half[None]
        if number == 0:
            half = paired(half[0], "tp", 1, 0)
        for place, bit in enumerate(reversed(bits[1:])):
            half = paired(half, "ctx", bit, 2 + place)
        if number == 1:
            half = paired(half[0], "tp", 1, 0)
        halves.append(paired(half, "ctx", bits[0], 1 + len(bits)))
    full = jnp.concatenate(halves, axis=1)
    return full.reshape(lax.axis_size("tp"), -1, shard.shape[1]), beside


def bits_of(axis):
    bits, bit = [], lax.axis_size(axis) // 2
    while bit:
        bits.append(bit)
        bit //= 2
    return bits


def added(*parts):
    return sum(part.astype(F32) for part in parts).astype(BF16)


def cut(cells, axis, bit, dim):
    size = cells.shape[dim] // 2
    side = side_of(axis, bit)
    return (
        lax.dynamic_slice_in_dim(cells, side * size, size, axis=dim),
        lax.dynamic_slice_in_dim(cells, (1 - side) * size, size, axis=dim),
    )


def gate(*values):
    return lax.optimization_barrier(values)


def dotf(spec, *operands):
    return jnp.einsum(spec, *operands, preferred_element_type=F32)


def taps_round(taps):
    middle = taps.shape[1] // 2
    gap = jnp.zeros((taps.shape[0], LANES - taps.shape[1]), F32)
    return jnp.concatenate([taps[:, middle::-1], gap, taps[:, :middle:-1]], axis=1)


def landmark_bounds(length):
    landmark = jnp.arange(LANDMARKS + 1, dtype=jnp.int32)
    return (landmark * length + LANDMARKS - 1) // LANDMARKS


def landmark_counts_of(length):
    bounds = landmark_bounds(length)
    return (bounds[1:] - bounds[:-1]).astype(F32)[:, None]


def landmark_rows(position, length):
    bounds = landmark_bounds(length)
    inside = (position[:, None] >= bounds[None, :-1]) & (position[:, None] < bounds[None, 1:])
    return inside.astype(BF16)


def on_device(
    tokens,
    lengths,
    qk_weight,
    value_weight,
    out_weight,
    in_weight,
    down_weight,
    norm_gains,
    norm_shifts,
    conv_weight,
    cotangent,
):
    tp_count = lax.axis_size("tp")
    tp_index = lax.axis_index("tp")
    ctx_index = lax.axis_index("ctx")
    _, slot_len, model_width = tokens.shape
    rows = slot_len // tp_count
    local_heads, tap_count = conv_weight.shape
    local_width = value_weight.shape[1]
    ff_width = in_weight.shape[1]
    head_size = local_width // local_heads
    heads = local_heads * tp_count
    owners = lax.axis_size("ctx")
    own_heads = heads // owners
    width = local_width * tp_count
    radius = tap_count // 2
    length = lengths[0]

    first_row = (ctx_index * tp_count + tp_index) * rows
    sides = (side_of("ctx", 1), ctx_index, side_of("ctx", ctx_bits()[-1]), tp_index)
    place = jnp.stack([first_row, length, *sides]).astype(jnp.int32)

    norm_columns = jnp.concatenate([norm_gains, norm_shifts], axis=0).T
    norm_columns = jnp.pad(norm_columns, ((0, 0), (0, LANES - norm_columns.shape[1])))
    ffn_full = gathered(
        jnp.concatenate([in_weight, down_weight.T, out_weight.T, norm_columns], axis=1)
    )
    own_taps = jnp.where(ctx_index == 0, conv_weight.astype(F32), 0.0)
    tap_rows = jnp.pad(own_taps, ((0, 8 - local_heads), (0, LANES - tap_count)))
    tap_rows = jnp.where(
        jnp.arange(model_width) // LANES == tp_index,
        jnp.tile(tap_rows, (1, model_width // LANES)),
        0.0,
    )
    own = lax.dynamic_slice_in_dim(tokens[0], tp_index * rows, rows, axis=0)
    land_tokens = sequence_start(jnp.concatenate([token_sums(place, own), tap_rows], axis=0))
    qkv_full, land_tokens = gathered_early(
        jnp.concatenate([qk_weight[0], qk_weight[1], value_weight], axis=1), land_tokens
    )
    land_tokens = joined_halves(*sequence_end(land_tokens))
    own_cotangent = lax.dynamic_slice_in_dim(cotangent[0], tp_index * rows, rows, axis=0)
    tap_weights = land_tokens[LANDMARKS : LANDMARKS + local_heads, : tp_count * LANES]
    tap_weights = tap_weights.reshape(local_heads, tp_count, LANES).transpose(1, 0, 2)
    tap_weights = tap_weights.reshape(heads, LANES)[:, :tap_count]
    land_tokens = land_tokens[:LANDMARKS]
    base, base_back = taps_round(tap_weights), taps_round(tap_weights[:, ::-1])

    queries, keys, values, v_plain, land_q, land_k, own_turned, *parts_of_third = projections(
        place, own, land_tokens, qkv_full, head_size, owners
    )
    v_ends = neighbour_rows(v_plain, radius)
    merged, merged_tp = to_owner(*parts_of_third, merge_keys)
    kept_turns = inverse_forward(place, land_q, land_k, owners)
    first, conv = first_and_conv(queries, values, *v_ends, land_k, base)
    merged, own_out = landmark_out(merged, merged_tp, kept_turns[0])
    land_out = from_owners(own_out)

    own_output, context, *fed, active, fed_turned, down_sent, last_norm = feed_forward(
        place, first, conv, land_out, own, own_cotangent, ffn_full, ff_width, local_width
    )
    high = ctx_bits()[-1]
    owner_count = lax.axis_size("fsdp")
    owner_rows = model_width // owner_count
    near, *farther = bits_of("fsdp")[::-1]

    def by_owner_bits(cells):
        return cells.reshape((2,) * (1 + len(farther)) + (-1, cells.shape[-1]))

    def cut_last(cells, bit):
        dim = cells.ndim - 3
        return tuple(piece.squeeze(dim) for piece in cut(cells, "fsdp", bit, dim))

    other_output = flipped(own_output, "tp", 1)
    down_other = flipped(down_sent, "ctx", 1)
    down_kept = kept_grad(place, fed_turned, active, tp_count)
    down_kept, down_other = gate(down_kept, down_other)
    down_mine, down_theirs = cut(down_kept, "ctx", high, 2)
    other_mine, other_theirs = cut(down_other, "ctx", high, 2)
    down_sent = added(down_theirs, other_theirs)
    down_got = flipped(down_sent, "ctx", high)
    fed[0], down_sent = gate(fed[0], down_sent)
    grad_first_res, grad_context, g_hidden, in_sent, att_turned, first_norm = feed_backward(
        place, fed, ffn_full, ff_width, local_width
    )
    in_sent, grad_context, g_hidden, other_output, down_got = gate(
        in_sent, grad_context, g_hidden, other_output, down_got
    )
    in_other = flipped(in_sent, "ctx", 1)
    g_ends = neighbour_rows(grad_context, radius)
    down = added(down_mine, other_mine, down_got)
    down_mine, down_sent = cut(down, "tp", 1, 0)
    down_got = flipped(down_sent, "tp", 1)
    grad_context, down_sent = gate(grad_context, down_sent)
    land_kept, land_sent, g_lk, g_q = attention_back(
        place, queries, grad_context, land_k, land_out, owners
    )
    land_kept, land_sent, in_other, g_ends = gate(land_kept, land_sent, in_other, g_ends)

    land_other = flipped(land_sent, "ctx", 1)
    in_kept, in_sent = spread_grad(place, fed[5], g_hidden, in_other)
    in_kept, in_sent, land_other, down_got = gate(in_kept, in_sent, land_other, down_got)
    land_grads = land_kept + land_other
    land_mine, land_theirs = cut(land_grads, "ctx", high, 0)
    land_got = flipped(land_theirs, "ctx", high)
    land_theirs, in_sent = gate(land_theirs, in_sent)
    in_got = flipped(in_sent, "ctx", high)
    down = added(down_mine, down_got)
    grad_context, in_sent = gate(grad_context, in_sent)
    g_conv, g_taps = conv_back(v_plain, v_ends, grad_context, g_ends, base_back)
    g_conv, g_taps, land_got = gate(g_conv, g_taps, land_got)
    own_grads = (land_mine + land_got)[0]
    tp_grads = flipped(own_grads, "tp", 1)

    def parts(cells):
        return cells.reshape(rows, tp_count, local_width)

    def qkv_part(index):
        return qkv_full[:, :, index * local_width : (index + 1) * local_width]

    g_q, own_grads = gate(g_q, own_grads)
    mixed_kept, mixed_sent = pair_grads(place, att_turned, context, own_turned, g_q, tp_count)
    back_q = grad_first_res + dotf("tpk,pck->tc", parts(g_q), qkv_part(0))
    mixed_kept, mixed_sent, tp_grads, back_q = gate(mixed_kept, mixed_sent, tp_grads, back_q)
    mixed_got = flipped(mixed_sent, "ctx", 1)
    own_grads, mixed_sent = gate(own_grads + tp_grads, mixed_sent)
    spread, lq_mid, lk_mid = inverse_backward(
        place, land_q, land_k, merged, own_grads, *kept_turns
    )
    spread, in_got, mixed_got = gate(spread, in_got, mixed_got)
    spread = from_owners(spread)

    in_mine, in_sent = cut(added(in_kept, in_got), "tp", 1, 0)
    in_got = flipped(in_sent, "tp", 1)
    def by_ctx(cells):
        return cells.reshape(tp_count, owner_count, 2, -1, local_width)

    mixed = added(mixed_kept, mixed_got)
    mixed_mine, mixed_sent = cut(by_ctx(mixed), "ctx", high, 2)
    mixed_got = flipped(mixed_sent, "ctx", high)
    spread, in_sent, mixed_sent = gate(spread, in_sent, mixed_sent)
    g_k, g_v, sums, kv_kept, kv_sent = third_back(
        place, keys, values, land_q, spread, g_conv, lq_mid, lk_mid, g_lk, last_norm, first_norm,
        g_taps, own_turned, tp_count,
    )

    kv_kept, kv_sent, sums, in_got, mixed_got = gate(kv_kept, kv_sent, sums, in_got, mixed_got)
    kv_got = flipped(kv_sent, "ctx", 1)
    sums_mine, sums_sent = cut(sums, "ctx", 1, 1)
    sums_got = flipped(sums_sent, "ctx", 1)
    kv_kept, kv_got = gate(kv_kept, kv_got)
    kv_mine, kv_sent = cut(by_ctx(added(kv_kept, kv_got)), "ctx", high, 2)
    kv_sent, sums_mine, mixed_mine, in_mine, g_k = gate(
        kv_sent, sums_mine, mixed_mine, in_mine, g_k
    )
    kv_got = flipped(kv_sent, "ctx", high)
    sums = sums_mine + sums_got
    sums_got = flipped(sums, "tp", 1)
    mixed_mine, mixed_sent = cut(added(mixed_mine, mixed_got), "tp", 1, 0)
    sums, mixed_sent, in_mine = gate(sums, mixed_sent, in_mine)
    mixed_got = flipped(mixed_sent, "tp", 1)
    pair = jnp.concatenate([added(in_mine, in_got)[0], down[0]], axis=1)
    g_k, mixed_sent, pair = gate(g_k, mixed_sent, pair)
    pair = lax.psum_scatter(pair, "fsdp", scatter_dimension=0, tiled=True)
    own_grad = token_grad(back_q, g_k, g_v, qkv_full)
    own_grad, sums_got, mixed_got = gate(own_grad, sums_got, mixed_got)
    first_rows = 3 * rows // 16
    other_first = flipped(own_grad[:first_rows], "tp", 1)
    own_grad, other_first, kv_got = gate(own_grad, other_first, kv_got)
    sums = sums + sums_got
    sums_got = flipped(sums, "ctx", high)
    kv_mine, kv_sent = cut(added(kv_mine, kv_got), "tp", 1, 0)
    own_grad, sums, kv_sent = gate(own_grad, sums, kv_sent)
    kv_got = flipped(kv_sent, "tp", 1)
    other_second = flipped(own_grad[first_rows:], "tp", 1)
    sums = sums + sums_got
    sums_got = flipped(sums, "ctx", 1)
    late, through, small = rank_parts(place, sums, sums_got, land_tokens, qkv_full)
    late, through, small, kv_got, own_output, other_output = gate(
        late, through, small, kv_got, own_output, other_output
    )
    late = late.reshape(owner_count, 2, -1, 2 * local_width)
    late = lax.dynamic_index_in_dim(late, place[4], 1, False)
    mixed = added(
        jnp.concatenate([mixed_mine, kv_mine], axis=-1).reshape(late.shape),
        jnp.concatenate([mixed_got, kv_got], axis=-1).reshape(late.shape),
        late,
    )
    small = jnp.broadcast_to(small[None], (owner_count,) + small.shape)
    mixed = by_owner_bits(jnp.concatenate([mixed, small], axis=1))
    mixed_mine, mixed_sent = cut_last(mixed, near)
    mixed_sent, pair = gate(mixed_sent, pair)
    mixed_got = flipped(mixed_sent, "fsdp", near)
    mixed = added(mixed_mine, mixed_got)
    for bit in farther:
        mixed_mine, mixed_sent = cut_last(mixed, bit)
        mixed = added(mixed_mine, flipped(mixed_sent, "fsdp", bit))
    small = mixed[-16:].astype(F32)
    mixed = mixed[:-16]

    def of_core(cells, core):
        cells = cells.reshape((owners // 2, 2) + cells.shape[1:])
        return [cells[i, core] for i in range(owners // 2)]

    mixed, other_second = gate(mixed, other_second)
    mixed = from_owners(mixed[None])
    sides = [jnp.concatenate(of_core(mixed, core), axis=0).astype(F32) for core in range(2)]
    grad_out, grad_k = sides[0][:, :local_width].T, sides[0][:, local_width:]
    grad_q, grad_v = sides[1][:, :local_width], sides[1][:, local_width:]

    own_columns = lax.axis_index("fsdp") * owner_rows
    norm_sums = lax.dynamic_slice_in_dim(small[:4], own_columns, owner_rows, axis=1)
    taps_sum = small[4].reshape(local_heads, LANES)
    grad_taps = jnp.concatenate(
        [taps_sum[:, radius - 1 :: -1], taps_sum[:, : -radius - 2 : -1]], axis=1
    )

    columns = pair.shape[1] // 2
    pair = from_owners(pair[None])
    pieces = [piece for core in range(2) for piece in of_core(pair, core)]
    grad_in = jnp.concatenate([piece[:, :columns] for piece in pieces], axis=1).astype(F32)
    grad_down = jnp.concatenate([piece[:, columns:] for piece in pieces], axis=1).astype(F32).T

    output = jnp.where(
        tp_index == 0,
        jnp.concatenate([own_output, other_output]),
        jnp.concatenate([other_output, own_output]),
    )[None]
    both_grads = jnp.where(
        tp_index == 0,
        jnp.concatenate([own_grad, other_first, other_second]),
        jnp.concatenate([other_first, other_second, own_grad]),
    )
    position = ctx_index * slot_len + jnp.arange(slot_len, dtype=jnp.int32)
    onehot = landmark_rows(position, length)
    grad_tokens = both_grads.astype(F32) + dotf(
        "tm,mc->tc", jnp.concatenate([onehot, onehot], axis=1), through
    )
    grad_tokens = grad_tokens.reshape(1, slot_len, model_width)
    return (
        output,
        grad_tokens,
        jnp.stack([grad_q, grad_k]),
        grad_v,
        grad_out,
        grad_in,
        grad_down,
        norm_sums[:2],
        norm_sums[2:],
        grad_taps,
    )


def solution(mesh):
    in_specs = (
        P("fsdp", "ctx", None),
        P("fsdp"),
        P(None, "fsdp", "tp"),
        P("fsdp", "tp"),
        P("tp", "fsdp"),
        P("fsdp", "tp"),
        P("tp", "fsdp"),
        P(None, "fsdp"),
        P(None, "fsdp"),
        P("tp", None),
        P("fsdp", "ctx", None),
    )
    out_specs = (
        P("fsdp", "ctx", None),
        P("fsdp", "ctx", None),
        P(None, "fsdp", "tp"),
        P("fsdp", "tp"),
        P("tp", "fsdp"),
        P("fsdp", "tp"),
        P("tp", "fsdp"),
        P(None, "fsdp"),
        P(None, "fsdp"),
        P("tp", None),
    )
    return jax.shard_map(
        on_device, mesh=mesh, in_specs=in_specs, out_specs=out_specs, check_vma=False
    )
```

```python
import jax
import jax.numpy as jnp
from jax import lax
from jax.experimental import pallas as pl
from jax.experimental.pallas import tpu as pltpu
from jax.sharding import PartitionSpec as P

LANDMARKS = 64
NEWTON = 6
LANES = 128
VMEM_BYTES = 56 * 2**20

HIGH = lax.Precision.HIGHEST
F32 = jnp.float32
BF16 = jnp.bfloat16


def lasting(microseconds):
    return pl.CostEstimate(
        flops=int(microseconds * 1.1535e9), bytes_accessed=int(microseconds * 1e5), transcendentals=0
    )


def nn(left, right):
    return jnp.dot(left, right, preferred_element_type=F32)


def nt(left, right):
    return lax.dot_general(left, right, (((1,), (1,)), ((), ())), preferred_element_type=F32)


def split(wide):
    high = wide.astype(BF16)
    return high, (wide - high.astype(F32)).astype(BF16)


def each_tile(count, tile, body):
    def step(i, _):
        body(i, pl.ds(pl.multiple_of(i * tile, tile), tile))
        return 0

    lax.fori_loop(0, count // tile, step, 0)


def family_grads(turned, cells, mine, kept, sent):
    halves, width, columns = kept.shape

    def rows_of(i, at):
        total = nn(turned[at, :], cells[...]).astype(BF16)

        @pl.when(mine)
        def _():
            for half in range(halves):
                kept[half, at, :] = total[:, half * columns : (half + 1) * columns]

        @pl.when(jnp.logical_not(mine))
        def _():
            for half in range(halves):
                sent[half, at, :] = total[:, half * columns : (half + 1) * columns]

    each_tile(width, 384, rows_of)


def whole(count):
    return [pl.BlockSpec(memory_space=pltpu.VMEM)] * count


SCALARS = pl.BlockSpec(memory_space=pltpu.SMEM)
PARAMS = pltpu.CompilerParams(vmem_limit_bytes=VMEM_BYTES)


def landmark_onehot(place, rows, landmark_axis):
    shape = (LANDMARKS, rows) if landmark_axis == 0 else (rows, LANDMARKS)
    landmark = lax.broadcasted_iota(jnp.int32, shape, landmark_axis)
    position = place[0] + lax.broadcasted_iota(jnp.int32, shape, 1 - landmark_axis)
    start = lax.shift_right_logical(landmark * place[1] + (LANDMARKS - 1), 6)
    end = lax.shift_right_logical((landmark + 1) * place[1] + (LANDMARKS - 1), 6)
    return jnp.where((position >= start) & (position < end), 1.0, 0.0).astype(BF16)


def live_lanes(place, rows):
    position = place[0] + lax.broadcasted_iota(jnp.int32, (1, rows), 1)
    return position < place[1]


def band(base_row):
    ring = pltpu.roll(jnp.broadcast_to(base_row, (LANES, LANES)), 0, 1, stride=1, stride_axis=0)
    gap = lax.broadcasted_iota(jnp.int32, (LANES, LANES), 0) - lax.broadcasted_iota(
        jnp.int32, (LANES, LANES), 1
    )
    zero = jnp.zeros_like(ring)
    before = jnp.where(gap >= LANES - 16, ring, zero).astype(BF16)
    here = jnp.where(jnp.abs(gap) <= 16, ring, zero).astype(BF16)
    after = jnp.where(gap <= 16 - LANES, ring, zero).astype(BF16)
    return before, here, after


def convolved(blocks, bands):
    count = len(blocks) - 2
    size = blocks[0].shape[0]
    stacked = jnp.concatenate(
        [jnp.concatenate(blocks[i : i + 3], axis=1) for i in range(count)], axis=0
    )
    out = nn(stacked, jnp.concatenate(bands, axis=0))
    return jnp.concatenate([out[i * size : (i + 1) * size] for i in range(count)], axis=1)


def token_sums_kernel(place, tokens, sums):
    sums[...] = nn(landmark_onehot(place, tokens.shape[0], 0), tokens[...])


def token_sums(place, tokens):
    return pl.pallas_call(
        token_sums_kernel,
        out_shape=jax.ShapeDtypeStruct((LANDMARKS, tokens.shape[1]), F32),
        in_specs=[SCALARS] + whole(1),
        out_specs=whole(1)[0],
        compiler_params=PARAMS,
        cost_estimate=lasting(2.5),
        name="token_sums",
    )(place, tokens)


def landmark_counts(place):
    landmark = lax.broadcasted_iota(jnp.int32, (LANDMARKS, 1), 0)
    start = lax.shift_right_logical(landmark * place[1] + (LANDMARKS - 1), 6)
    end = lax.shift_right_logical((landmark + 1) * place[1] + (LANDMARKS - 1), 6)
    return (end - start).astype(F32)


def projection_kernel(
    place, tokens, sums, weights, q_out, k_out, v_out, v_plain, land_q, land_k, turned, kept, sent
):
    rows = tokens.shape[0]
    halves, _, packed = weights.shape
    width = packed // 3
    size = land_q.shape[2]
    position = place[0] + lax.broadcasted_iota(jnp.int32, (rows, 1), 0)
    live = jnp.where(position < place[1], 1.0, 0.0)
    scaled = live * 64**-0.25
    means = jnp.concatenate(split(sums[...] / landmark_counts(place)), axis=0)
    cells = tokens[...]
    turned[...] = cells.T
    for half in range(halves):
        for part, out in enumerate((q_out, k_out, v_out)):
            weight = weights[half, :, part * width : (part + 1) * width]
            low = ((live if part == 2 else scaled) * nn(cells, weight)).astype(BF16)
            out[half * width : (half + 1) * width, :] = low.T
            if part == 2:
                v_plain[:, half * width : (half + 1) * width] = low
                continue
            both = nn(means, weight)
            land = (64**-0.25 * (both[:LANDMARKS] + both[LANDMARKS:])).astype(BF16)
            to = land_k if part else land_q
            for head in range(width // size):
                to[half * (width // size) + head] = land[:, head * size : (head + 1) * size]
    third_heads(place, k_out, v_out, land_q, kept, sent)


def projections(place, tokens, sums, weights, size, owners):
    rows = tokens.shape[0]
    width = weights.shape[0] * weights.shape[2] // 3
    turned = jax.ShapeDtypeStruct((width, rows), BF16)
    land = jax.ShapeDtypeStruct((width // size, LANDMARKS, size), BF16)
    return pl.pallas_call(
        projection_kernel,
        out_shape=(turned, turned, turned, jax.ShapeDtypeStruct((rows, width), BF16), land, land)
        + (jax.ShapeDtypeStruct(tokens.shape[::-1], BF16),)
        + owner_parts(width // size, owners),
        in_specs=[SCALARS] + whole(3),
        out_specs=tuple(whole(9)),
        compiler_params=PARAMS,
        cost_estimate=lasting(18),
        name="projections",
    )(place, tokens, sums, weights)


def by_owner(place, h, owners, kept, sent, values):
    per = kept.shape[1]
    for owner in range(owners):
        @pl.when((h >= owner * per) & (h < (owner + 1) * per))
        def _(owner=owner):
            mine = place[2] == owner % 2

            @pl.when(mine)
            def _():
                kept[owner // 2, h - owner * per] = values

            @pl.when(jnp.logical_not(mine))
            def _():
                sent[owner // 2, h - owner * per] = values


def third_heads(place, keys, values, land_q, kept, sent):
    heads = land_q.shape[0]
    size = land_q.shape[2]
    rows = keys.shape[1]
    owners = 2 * kept.shape[0]
    live = live_lanes(place, rows)

    def head(h):
        at = pl.ds(pl.multiple_of(h * size, size), size)
        scores = jnp.where(live, nn(land_q[h], keys[at, :]), -1e30)
        top = jnp.max(scores, axis=1, keepdims=True)
        raised = jnp.where(live, jnp.exp(scores - top), 0.0)
        total = jnp.sum(raised, axis=1, keepdims=True)
        high, low = split(raised)
        value = values[at, :]
        mixed = nt(high, value) + nt(low, value)
        lane = lax.broadcasted_iota(jnp.int32, (LANDMARKS, LANES - size), 1)
        stats = jnp.where(lane == 0, top, jnp.where(lane == 1, total, 0.0))
        by_owner(place, h, owners, kept, sent, jnp.concatenate([mixed, stats], axis=1))

    def pair(i, _):
        head(2 * i)
        head(2 * i + 1)
        return 0

    lax.fori_loop(0, heads // 2, pair, 0)


def owner_parts(heads, owners):
    part = jax.ShapeDtypeStruct((owners // 2, heads // owners, LANDMARKS, LANES), F32)
    return part, part


def dot_high(left, right):
    return jnp.dot(left, right, preferred_element_type=F32, precision=HIGH)


def dot_high_nt(left, right):
    return lax.dot_general(
        left, right, (((1,), (1,)), ((), ())), preferred_element_type=F32, precision=HIGH
    )


def eye():
    row = lax.broadcasted_iota(jnp.int32, (LANDMARKS, LANDMARKS), 0)
    column = lax.broadcasted_iota(jnp.int32, (LANDMARKS, LANDMARKS), 1)
    return jnp.where(row == column, 1.0, 0.0)


def middle_map(land_q, land_k):
    scores = nt(land_q, land_k)
    raised = jnp.exp(scores - jnp.max(scores, axis=1, keepdims=True))
    return raised / jnp.sum(raised, axis=1, keepdims=True)


def inverse_kernel(place, land_q, land_k, kept_v, kept_p, kept_b, kept_c):
    heads = range(kept_v.shape[1])
    one = eye()
    own = [place[3] * len(heads) + h for h in heads]
    middle = [middle_map(land_q[h], land_k[h]) for h in own]
    approx = [m.T / jnp.sum(m * m, keepdims=True) for m in middle]
    for turn in range(NEWTON):
        product = [dot_high(middle[h], approx[h]) for h in heads]
        for h in heads:
            kept_v[turn, h] = approx[h]
            kept_p[turn, h] = product[h]
        bracket = [7.0 * one - p for p in product]
        bracket = [15.0 * one - dot_high(product[h], bracket[h]) for h in heads]
        for h in heads:
            kept_b[turn, h] = bracket[h]
        bracket = [13.0 * one - dot_high(product[h], bracket[h]) for h in heads]
        for h in heads:
            kept_c[turn, h] = bracket[h]
        approx = [0.25 * dot_high(approx[h], bracket[h]) for h in heads]
    for h in heads:
        kept_v[NEWTON, h] = approx[h]


def inverse_forward(place, land_q, land_k, owners):
    heads = land_q.shape[0] // owners
    square = (heads, LANDMARKS, LANDMARKS)
    return pl.pallas_call(
        inverse_kernel,
        out_shape=(
            jax.ShapeDtypeStruct((NEWTON + 1,) + square, F32),
            jax.ShapeDtypeStruct((NEWTON,) + square, F32),
            jax.ShapeDtypeStruct((NEWTON,) + square, F32),
            jax.ShapeDtypeStruct((NEWTON,) + square, F32),
        ),
        in_specs=[SCALARS] + whole(2),
        out_specs=tuple(whole(4)),
        compiler_params=PARAMS,
        cost_estimate=lasting(7),
        name="inverse_forward",
    )(place, land_q, land_k)


def merged_keys(one, two, size):
    one_top, two_top = one[:, size : size + 1], two[:, size : size + 1]
    top = jnp.maximum(one_top, two_top)
    summed = one * jnp.exp(one_top - top) + two * jnp.exp(two_top - top)
    lane = lax.broadcasted_iota(jnp.int32, one.shape, 1)
    return jnp.where(lane == size, top, summed)


def land_out_kernel(one, two, kept_v, merged, land_out):
    size = land_out.shape[2]
    for h in range(one.shape[0]):
        both = merged_keys(one[h], two[h], size)
        merged[h] = both
        mixed = both[:, :size] / both[:, size + 1 : size + 2]
        land_out[h] = dot_high(kept_v[NEWTON, h], mixed).astype(BF16)


def landmark_out(one, two, kept_v):
    heads = one.shape[0]
    return pl.pallas_call(
        land_out_kernel,
        out_shape=(
            jax.ShapeDtypeStruct(one.shape, F32),
            jax.ShapeDtypeStruct((heads, LANDMARKS, LANES // 2), BF16),
        ),
        in_specs=whole(3),
        out_specs=tuple(whole(2)),
        compiler_params=PARAMS,
        cost_estimate=lasting(2.2),
        name="landmark_out",
    )(one, two, kept_v)


def inverse_back_kernel(
    place, land_q, land_k, merged, grads, kept_v, kept_p, kept_b, kept_c, spread, g_lq, g_lk
):
    heads = range(grads.shape[0])
    size = land_q.shape[2]
    one = eye()
    own = [place[3] * len(heads) + h for h in heads]
    middle = [middle_map(land_q[h], land_k[h]) for h in own]
    turned = [m.T for m in middle]
    g_approx = []
    for h in heads:
        mixed = merged[h][:, :size] / merged[h][:, size + 1 : size + 2]
        g_land = grads[h][:, :size]
        g_approx.append(dot_high_nt(g_land, mixed))
        g_mixed = dot_high(kept_v[NEWTON, h].T, g_land)
        row_dot = jnp.sum(g_mixed * mixed, axis=1, keepdims=True)
        lane = lax.broadcasted_iota(jnp.int32, (LANDMARKS, LANES - size), 1)
        top = merged[h][:, size : size + 1]
        total = merged[h][:, size + 1 : size + 2]
        stats = jnp.where(
            lane == 0, row_dot, jnp.where(lane == 1, top, jnp.where(lane == 2, total, 0.0))
        )
        spread[h] = jnp.concatenate([g_mixed, stats], axis=1)
    g_middle = [jnp.zeros((LANDMARKS, LANDMARKS), F32) for _ in heads]
    for turn in reversed(range(NEWTON)):
        approx = [kept_v[turn, h] for h in heads]
        product = [kept_p[turn, h] for h in heads]
        first = [7.0 * one - p for p in product]
        second = [kept_b[turn, h] for h in heads]
        third = [kept_c[turn, h] for h in heads]
        g_third = [0.25 * dot_high(approx[h].T, g_approx[h]) for h in heads]
        g_back = [0.25 * dot_high_nt(g_approx[h], third[h]) for h in heads]
        g_product = [-dot_high_nt(g_third[h], second[h]) for h in heads]
        pt = [p.T for p in product]
        g_second = [-dot_high(pt[h], g_third[h]) for h in heads]
        g_product = [g_product[h] - dot_high_nt(g_second[h], first[h]) for h in heads]
        g_product = [g_product[h] + dot_high(pt[h], g_second[h]) for h in heads]
        g_middle = [g_middle[h] + dot_high_nt(g_product[h], approx[h]) for h in heads]
        g_approx = [g_back[h] + dot_high(turned[h], g_product[h]) for h in heads]
    for h in heads:
        m = middle[h]
        size_sum = jnp.sum(m * m, keepdims=True)
        g_size = -jnp.sum(g_approx[h] * turned[h], keepdims=True) / (size_sum * size_sum)
        g_m = g_middle[h] + g_approx[h].T / size_sum + 2.0 * g_size * m
        g_scores = m * (g_m - jnp.sum(g_m * m, axis=1, keepdims=True))
        g_lq[h] = dot_high(g_scores, land_k[own[h]].astype(F32))
        g_lk[h] = dot_high(g_scores.T, land_q[own[h]].astype(F32))


def inverse_backward(place, land_q, land_k, merged, grads, *kept):
    heads = grads.shape[0]
    square = jax.ShapeDtypeStruct((heads,) + land_q.shape[1:], F32)
    return pl.pallas_call(
        inverse_back_kernel,
        out_shape=(jax.ShapeDtypeStruct((heads, LANDMARKS, LANES), F32), square, square),
        in_specs=[SCALARS] + whole(8),
        out_specs=tuple(whole(3)),
        compiler_params=PARAMS,
        cost_estimate=lasting(11.5),
        name="inverse_backward",
    )(place, land_q, land_k, merged, grads, *kept)


def first_map(land_k, queries):
    scores = nn(land_k, queries)
    raised = jnp.exp(scores - jnp.max(scores, axis=0, keepdims=True))
    return raised * (1.0 / jnp.sum(raised, axis=0, keepdims=True))


def head_blocks(cells, ends, at):
    rows = cells.shape[1]
    left, right = ends
    return (
        [left[at, :]]
        + [cells[at, i * LANES : (i + 1) * LANES] for i in range(rows // LANES)]
        + [right[at, :]]
    )


def first_conv_kernel(queries, values, left, right, land_k, base, first, conv, ends):
    heads, _, size = land_k.shape
    ends[0] = left[...].T
    ends[1] = right[...].T

    def head(h):
        at = pl.ds(pl.multiple_of(h * size, size), size)
        first[at, :] = first_map(land_k[h], queries[at, :]).astype(BF16)
        blocks = head_blocks(values, (ends.at[0], ends.at[1]), at)
        conv[at, :] = convolved(blocks, band(base[pl.ds(h, 1), :]))

    def pair(i, _):
        head(2 * i)
        head(2 * i + 1)
        return 0

    lax.fori_loop(0, heads // 2, pair, 0)


def first_and_conv(queries, values, left, right, land_k, base):
    width, rows = queries.shape
    return pl.pallas_call(
        first_conv_kernel,
        out_shape=(
            jax.ShapeDtypeStruct((width, rows), BF16),
            jax.ShapeDtypeStruct((width, rows), F32),
        ),
        in_specs=whole(6),
        out_specs=tuple(whole(2)),
        scratch_shapes=[pltpu.VMEM((2, width, LANES), BF16)],
        compiler_params=PARAMS,
        cost_estimate=lasting(8),
        name="first_and_conv",
    )(queries, values, left, right, land_k, base)


def context_rows(first, conv, land_out, context):
    heads, _, size = land_out.shape

    def head(h):
        at = pl.ds(pl.multiple_of(h * size, size), size)
        return (nn(land_out[h].T, first[at, :]) + conv[at, :]).astype(BF16)

    def pair(i, _):
        both = jnp.concatenate([head(2 * i), head(2 * i + 1)], axis=0)
        context[:, pl.ds(pl.multiple_of(i * LANES, LANES), LANES)] = both.T
        return 0

    lax.fori_loop(0, heads // 2, pair, 0)


def attention_back_kernel(
    place, queries, grads, land_k, land_out, kept, sent, g_lk, g_query
):
    heads, _, size = land_k.shape
    rows = queries.shape[1]
    owners = 2 * kept.shape[0]
    scaled = jnp.where(live_lanes(place, rows), 64**-0.25, 0.0)

    def pair(i, _):
        lanes = pl.ds(pl.multiple_of(i * LANES, LANES), LANES)
        turned = grads[:, lanes].T
        g_queries, g_keys = [], []
        for side in range(2):
            h = 2 * i + side
            query = queries[pl.ds(pl.multiple_of(h * size, size), size), :]
            g_context = turned[side * size : (side + 1) * size]
            first = first_map(land_k[h], query)
            g_first = nn(land_out[h], g_context)
            inner = jnp.sum(g_first * first, axis=0, keepdims=True)
            g_scores = (first * (g_first - inner)).astype(BF16)
            g_land = nt(first.astype(BF16), g_context)
            g_key = nt(g_scores, query)
            by_owner(place, h, owners, kept, sent, jnp.concatenate([g_land, g_key], axis=1))
            g_keys.append(g_key)
            g_queries.append((scaled * nn(land_k[h].T, g_scores)).astype(BF16))
        g_query[:, lanes] = jnp.concatenate(g_queries, axis=0).T
        g_lk[:, lanes] = jnp.concatenate(g_keys, axis=1)
        return 0

    lax.fori_loop(0, heads // 2, pair, 0)


def attention_back(place, queries, grads, land_k, land_out, owners):
    width, rows = queries.shape
    heads = land_k.shape[0]
    return pl.pallas_call(
        attention_back_kernel,
        out_shape=owner_parts(heads, owners)
        + (
            jax.ShapeDtypeStruct((LANDMARKS, width), F32),
            jax.ShapeDtypeStruct((rows, width), BF16),
        ),
        in_specs=[SCALARS] + whole(4),
        out_specs=tuple(whole(4)),
        compiler_params=PARAMS,
        cost_estimate=lasting(11.4),
        name="attention_back",
    )(place, queries, grads, land_k, land_out)


def conv_back_kernel(
    v_plain, v_left, v_right, grads, g_left, g_right, base_back, g_value, g_taps, ends
):
    heads = g_taps.shape[0]
    rows, width = grads.shape
    size = width // heads
    blocks_in = rows // LANES
    row = lax.broadcasted_iota(jnp.int32, (LANES, LANES), 0)
    column = lax.broadcasted_iota(jnp.int32, (LANES, LANES), 1)
    reverse = jnp.where(row + column == LANES - 1, 1.0, 0.0).astype(BF16)
    gap = jnp.concatenate([row - column, row - column], axis=1)
    ends[0] = g_left[...].T
    ends[1] = g_right[...].T

    def pair(i, _):
        lanes = pl.ds(pl.multiple_of(i * LANES, LANES), LANES)
        turned = grads[:, lanes].T
        plain = [v_left[LANES - 16 :, lanes]]
        plain += [v_plain[b * LANES : (b + 1) * LANES, lanes] for b in range(blocks_in)]
        plain += [v_right[:16, lanes]]
        for side in range(2):
            h = 2 * i + side
            at = pl.ds(pl.multiple_of(h * size, size), size)
            g_context = turned[side * size : (side + 1) * size]
            blocks = [ends[0, at, :]]
            blocks += [g_context[:, b * LANES : (b + 1) * LANES] for b in range(blocks_in)]
            blocks += [ends[1, at, :]]
            g_value[at, :] = convolved(blocks, band(base_back[pl.ds(h, 1), :]))

        def around(b):
            prior = plain[0] if b == 0 else plain[b][LANES - 16 :]
            return jnp.concatenate([prior, plain[b + 1], plain[b + 2][:16]], axis=0)

        def by_head(b):
            piece = turned[:, b * LANES : (b + 1) * LANES]
            zero = jnp.zeros_like(piece)
            return jnp.concatenate(
                [jnp.where(row < size, piece, zero), jnp.where(row >= size, piece, zero)], axis=1
            )

        total = jnp.zeros((LANES + 32, 2 * LANES), F32)
        for b in range(0, blocks_in, 2):
            total = total + nn(
                jnp.concatenate([around(b), around(b + 1)], axis=1),
                jnp.concatenate([by_head(b), by_head(b + 1)], axis=0),
            )
        empty = jnp.zeros((LANES - 16, 2 * LANES), F32)
        before, here, after = total[:16], total[16 : 16 + LANES], total[16 + LANES :]
        ring = jnp.where(jnp.abs(gap) <= 16, here, 0.0)
        ring = ring + jnp.where(gap >= LANES - 16, jnp.concatenate([empty, before], axis=0), 0.0)
        ring = ring + jnp.where(gap <= 16 - LANES, jnp.concatenate([after, empty], axis=0), 0.0)
        high, low = split(ring)
        lowest = (ring - high.astype(F32) - low.astype(F32)).astype(BF16)
        flat = nn(reverse, high) + nn(reverse, low) + nn(reverse, lowest)
        for side in range(2):
            straight = pltpu.roll(
                flat[:, side * LANES : (side + 1) * LANES], 0, 1, stride=1, stride_axis=0
            )
            g_taps[pl.ds(2 * i + side, 1), :] = jnp.sum(straight, axis=0, keepdims=True)
        return 0

    lax.fori_loop(0, heads // 2, pair, 0)


def conv_back(v_plain, v_ends, grads, g_ends, base_back):
    rows, width = grads.shape
    heads = base_back.shape[0]
    return pl.pallas_call(
        conv_back_kernel,
        out_shape=(
            jax.ShapeDtypeStruct((width, rows), F32),
            jax.ShapeDtypeStruct((heads, LANES), F32),
        ),
        in_specs=whole(7),
        out_specs=tuple(whole(2)),
        scratch_shapes=[pltpu.VMEM((2, width, LANES), BF16)],
        compiler_params=PARAMS,
        cost_estimate=lasting(13.6),
        name="conv_back",
    )(v_plain, *v_ends, grads, *g_ends, base_back)


def third_back_kernel(
    place, keys, values, land_q, spread, g_conv, lq_mid, lk_mid, g_lk, last, first, taps, turned,
    g_k, g_v, sums, kept, sent,
):
    heads, _, size = land_q.shape
    rows, width = g_k.shape
    own_heads = lq_mid.shape[0]
    scale = 64**-0.25
    sums[LANDMARKS:, :] = jnp.zeros((sums.shape[0] - LANDMARKS, 2 * width), F32)
    sums[LANDMARKS : LANDMARKS + 1, :] = last[...]
    sums[LANDMARKS + 1 : LANDMARKS + 2, :] = first[...]
    for h in range(heads):
        sums[LANDMARKS + 2 : LANDMARKS + 3, h * LANES : (h + 1) * LANES] = taps[h : h + 1, :]

    def mid(part, h):
        at = h - place[3] * own_heads
        mine = (at >= 0) & (at < own_heads) & (place[5] == 0)
        inside = jnp.clip(at, 0, own_heads - 1)
        return jnp.where(mine, part[inside], 0.0)

    live = live_lanes(place, rows)
    live_row = jnp.where(live, 1.0, 0.0)
    scaled_row = live_row * 64**-0.25

    def pair(i, _):
        lanes = pl.ds(pl.multiple_of(i * LANES, LANES), LANES)
        g_keys, g_values, g_lqs, lks = [], [], [], []
        for side in range(2):
            h = 2 * i + side
            at = pl.ds(pl.multiple_of(h * size, size), size)
            key, value = keys[at, :], values[at, :]
            pack = spread[h]
            g_mixed = pack[:, :size]
            row_dot = pack[:, size : size + 1]
            top = pack[:, size + 1 : size + 2]
            total = pack[:, size + 2 : size + 3]
            scores = nn(land_q[h], key)
            third = jnp.where(live, jnp.exp(scores - top), 0.0) * (1.0 / total)
            gm_high, gm_low = split(g_mixed)
            g_third = nn(gm_high, value) + nn(gm_low, value)
            g_high, g_low = split(third * (g_third - row_dot))
            g_lqs.append(nt(g_high, key) + nt(g_low, key) + mid(lq_mid, h))
            lks.append(mid(lk_mid, h))
            turned = land_q[h].T
            g_key = nn(turned, g_high) + nn(turned, g_low)
            g_keys.append((scaled_row * g_key).astype(BF16))
            t_high, t_low = split(third)
            gmt_high, gmt_low = split(g_mixed.T)
            g_value = nn(gmt_high, t_high) + nn(gmt_high, t_low) + nn(gmt_low, t_high)
            g_values.append((live_row * (g_value + g_conv[at, :])).astype(BF16))
        g_k[:, lanes] = jnp.concatenate(g_keys, axis=0).T
        g_v[:, lanes] = jnp.concatenate(g_values, axis=0).T
        sums[:LANDMARKS, lanes] = scale * jnp.concatenate(g_lqs, axis=1)
        key_lanes = pl.ds(pl.multiple_of(width + i * LANES, LANES), LANES)
        sums[:LANDMARKS, key_lanes] = scale * (g_lk[:, lanes] + jnp.concatenate(lks, axis=1))
        return 0

    lax.fori_loop(0, heads // 2, pair, 0)
    for number, cells in enumerate((g_k, g_v)):
        family_grads(turned, cells, place[2] == number, kept, sent)


def third_back(
    place, keys, values, land_q, spread, g_conv, lq_mid, lk_mid, g_lk, last, first, taps, turned, halves
):
    width, rows = keys.shape
    plain = jax.ShapeDtypeStruct((rows, width), BF16)
    return pl.pallas_call(
        third_back_kernel,
        out_shape=(plain, plain, jax.ShapeDtypeStruct((LANDMARKS + 8, 2 * width), F32))
        + (jax.ShapeDtypeStruct((halves, width, width // halves), BF16),) * 2,
        in_specs=[SCALARS] + whole(12),
        out_specs=tuple(whole(5)),
        compiler_params=PARAMS,
        cost_estimate=lasting(17),
        name="third_back",
    )(
        place, keys, values, land_q, spread, g_conv, lq_mid, lk_mid, g_lk, last, first, taps, turned
    )


def centred_rows(rows):
    centred = rows - jnp.mean(rows, axis=1, keepdims=True)
    scale = lax.rsqrt(jnp.mean(centred * centred, axis=1, keepdims=True) + 1e-05)
    return centred * scale, scale


def norm_back(grads, gain, unit, scale):
    scaled = grads * gain
    inner = jnp.mean(scaled * unit, axis=1, keepdims=True)
    return scale * (scaled - jnp.mean(scaled, axis=1, keepdims=True) - unit * inner)


def gelu_pair(hidden):
    share = 0.5 * (1.0 + lax.erf(hidden * 0.7071067811865476))
    density = jnp.exp(-0.5 * hidden * hidden) * 0.3989422804014327
    return hidden * share, share + hidden * density


class Copies:
    def __init__(self, sems):
        self.sems, self.used, self.open = sems, 0, []

    def start(self, source, target):
        copy = pltpu.make_async_copy(source, target, self.sems.at[self.used])
        self.used += 1
        copy.start()
        return copy

    def out(self, source, target):
        self.open.append(self.start(source, target))

    def finish(self):
        for copy in self.open:
            copy.wait()


def weight_grad(turned, cells, halves, which, out):
    ff = cells.shape[1] // halves
    columns = ff // 2
    for half in range(halves):
        from_column = pl.ds(pl.multiple_of(half * ff + which * columns, columns), columns)

        def rows_of(i, at, half=half, from_column=from_column):
            out[half, at, :] = nn(turned[at, :], cells[:, from_column]).astype(BF16)

        each_tile(turned.shape[0], 384, rows_of)


def feed_kernel(
    place, first_in, conv_in, land_out, tokens_in, cotangent_in, weights,
    output_to, context_to, slope_to, g_fed_to, g_second_to, unit_to, scale_to, turned_to, active_to, fed_turned_to, sent_to,
    norm_grads, in_w, down_w, out_w, norms, conv, context, tokens, cotangent,
    low, unit, scales, fed, active, slopes, g_fed, g_fed_turned, normed_turned, output, sent,
    sems,
):
    rows, width = tokens.shape
    halves, _, ff = in_w.shape
    part = out_w.shape[2]
    tile = 256
    copies = Copies(sems)
    context_copies = [copies.start(first_in, g_fed_turned), copies.start(conv_in, conv)]
    early = [
        copies.start(weights.at[:, :, pl.ds(2 * ff, part)], out_w),
        copies.start(tokens_in, tokens),
        copies.start(weights.at[:, :, pl.ds(2 * ff + part, LANES)], norms),
    ]
    in_copy = copies.start(weights.at[:, :, pl.ds(0, ff)], in_w)
    down_copy = copies.start(weights.at[:, :, pl.ds(ff, ff)], down_w)
    cotangent_copy = copies.start(cotangent_in, cotangent)
    for copy in context_copies:
        copy.wait()
    context_rows(g_fed_turned, conv, land_out, context)
    copies.out(context, context_to)
    for copy in early:
        copy.wait()
    columns = norms[0].astype(F32).T
    gain0, gain1 = columns[0:1], columns[1:2]
    shift0, shift1 = columns[2:3], columns[3:4]
    norm_grads[...] = jnp.zeros_like(norm_grads)

    def project(i, at):
        attended = nt(context[at, :part], out_w[0])
        for half in range(1, halves):
            attended = attended + nt(context[at, half * part : (half + 1) * part], out_w[half])
        rows_unit, scale = centred_rows(tokens[at, :].astype(F32) + attended)
        unit[at, :] = rows_unit
        scales[at, :] = jnp.broadcast_to(scale, (tile, LANES))
        normed = (rows_unit * gain0 + shift0).astype(BF16)
        low[at, :] = normed
        normed_turned[:, at] = normed.T

    each_tile(rows, tile, project)
    copies.out(unit, unit_to)
    copies.out(scales, scale_to)
    copies.out(normed_turned, turned_to)
    in_copy.wait()
    big = 512

    def hidden_rows(i, at):
        for half in range(halves):
            value, slope = gelu_pair(nn(low[at, :], in_w[half]))
            active[at, half * ff : (half + 1) * ff] = value.astype(BF16)
            slopes[at, half * ff : (half + 1) * ff] = slope.astype(BF16)

    each_tile(rows, tile, hidden_rows)
    copies.out(slopes, slope_to)
    copies.out(active, active_to)
    down_copy.wait()

    def fed_rows(i, at):
        total = nt(active[at, :ff], down_w[0])
        for half in range(1, halves):
            total = total + nt(active[at, half * ff : (half + 1) * ff], down_w[half])
        fed[at, :] = total

    each_tile(rows, big, fed_rows)
    cotangent_copy.wait()

    def second_norm(i, at):
        normed = unit[at, :] * gain0 + shift0
        unit1, scale1 = centred_rows(normed + fed[at, :])
        position = place[0] + i * tile + lax.broadcasted_iota(jnp.int32, (tile, 1), 0)
        live = jnp.where(position < place[1], 1.0, 0.0)
        output[at, :] = (live * (unit1 * gain1 + shift1)).astype(BF16)
        grads = live * cotangent[at, :].astype(F32)
        norm_grads[:, :width] += jnp.sum(grads * unit1, axis=0, keepdims=True)
        norm_grads[:, width:] += jnp.sum(grads, axis=0, keepdims=True)
        second = norm_back(grads, gain1, unit1, scale1)
        fed[at, :] = second
        g_low = second.astype(BF16)
        g_fed[at, :] = g_low
        g_fed_turned[:, at] = g_low.T

    each_tile(rows, tile, second_norm)
    copies.out(output, output_to)
    copies.out(fed, g_second_to)
    copies.out(g_fed, g_fed_to)
    copies.out(g_fed_turned, fed_turned_to)
    weight_grad(g_fed_turned, active, halves, 1 - place[2], sent)
    copies.out(sent, sent_to)
    copies.finish()


ANYWHERE = pl.BlockSpec(memory_space=pl.ANY)


def feed_forward(place, first, conv, land_out, tokens, cotangent, weights, ff, part):
    rows, width = tokens.shape
    halves = weights.shape[0]
    grad = (halves, width, ff // 2)
    shapes = [
        ((rows, width), BF16), ((rows, width), BF16), ((rows, halves * ff), BF16),
        ((rows, width), BF16), ((rows, width), F32), ((rows, width), F32), ((rows, LANES), F32), ((width, rows), BF16),
        ((rows, halves * ff), BF16), ((width, rows), BF16), (grad, BF16), ((1, 2 * width), F32),
    ]
    scratch = [
        ((halves, width, ff), BF16), ((halves, width, ff), BF16), ((halves, width, part), BF16),
        ((halves, width, LANES), BF16), ((width, rows), F32), ((rows, width), BF16),
        ((rows, width), BF16), ((rows, width), BF16),
        ((rows, width), BF16), ((rows, width), F32), ((rows, LANES), F32), ((rows, width), F32),
        ((rows, halves * ff), BF16), ((rows, halves * ff), BF16), ((rows, width), BF16),
        ((width, rows), BF16), ((width, rows), BF16), ((rows, width), BF16), (grad, BF16),
    ]
    return pl.pallas_call(
        feed_kernel,
        out_shape=tuple(jax.ShapeDtypeStruct(*shape) for shape in shapes),
        in_specs=[SCALARS] + [ANYWHERE] * 2 + whole(1) + [ANYWHERE] * 3,
        out_specs=tuple([ANYWHERE] * 11 + whole(1)),
        scratch_shapes=[pltpu.VMEM(*shape) for shape in scratch]
        + [pltpu.SemaphoreType.DMA((19,))],
        compiler_params=PARAMS,
        cost_estimate=lasting(32),
        name="feed_forward",
    )(place, first, conv, land_out, tokens, cotangent, weights)


def feed_back_kernel(
    place, slope_in, g_fed_in, g_second_in, unit_in, scale_in, turned_in, weights,
    g_first_to, g_context_to, g_hidden_to, sent_to, att_turned_to, norm_grads,
    in_w, down_w, out_w, norms, g_hidden, g_fed, second, unit, scales, normed_turned,
    g_att, g_att_turned, g_context, sent,
    sems,
):
    rows, width = second.shape
    halves, _, ff = in_w.shape
    part = out_w.shape[2]
    tile = 256
    copies = Copies(sems)
    early = [
        copies.start(g_fed_in, g_fed),
        copies.start(weights.at[:, :, pl.ds(ff, ff)], down_w),
        copies.start(slope_in, g_hidden),
    ]
    later = [
        copies.start(turned_in, normed_turned),
        copies.start(weights.at[:, :, pl.ds(0, ff)], in_w),
        copies.start(g_second_in, second),
        copies.start(unit_in, unit),
        copies.start(scale_in, scales),
        copies.start(weights.at[:, :, pl.ds(2 * ff + part, LANES)], norms),
        copies.start(weights.at[:, :, pl.ds(2 * ff, part)], out_w),
    ]
    for copy in early:
        copy.wait()
    norm_grads[...] = jnp.zeros_like(norm_grads)
    big = 512

    def back_rows(i, at):
        for half in range(halves):
            g_act = nn(g_fed[at, :], down_w[half])
            to = slice(half * ff, (half + 1) * ff)
            g_hidden[at, to] = (g_act * g_hidden[at, to].astype(F32)).astype(BF16)

    each_tile(rows, big, back_rows)
    copies.out(g_hidden, g_hidden_to)
    later.pop(0).wait()
    weight_grad(normed_turned, g_hidden, halves, 1 - place[2], sent)
    copies.out(sent, sent_to)
    for copy in later:
        copy.wait()
    gain0 = norms[0].astype(F32).T[0:1]

    def normed_rows(i, at):
        total = second[at, :]
        for half in range(halves):
            total = total + nt(g_hidden[at, half * ff : (half + 1) * ff], in_w[half])
        second[at, :] = total

    each_tile(rows, big, normed_rows)

    def first_norm(i, at):
        grads = second[at, :]
        rows_unit, scale = unit[at, :], scales[at, 0:1]
        norm_grads[:, :width] += jnp.sum(grads * rows_unit, axis=0, keepdims=True)
        norm_grads[:, width:] += jnp.sum(grads, axis=0, keepdims=True)
        first = norm_back(grads, gain0, rows_unit, scale)
        second[at, :] = first
        low = first.astype(BF16)
        g_att[at, :] = low
        g_att_turned[:, at] = low.T

    each_tile(rows, tile, first_norm)
    copies.out(second, g_first_to)
    copies.out(g_att_turned, att_turned_to)
    for half in range(halves):
        g_context[:, half * part : (half + 1) * part] = nn(g_att[...], out_w[half]).astype(BF16)
    copies.out(g_context, g_context_to)
    copies.finish()


def feed_backward(place, fed, weights, ff, part):
    rows, width = fed[1].shape
    halves = weights.shape[0]
    grad = (halves, width, ff // 2)
    shapes = [
        ((rows, width), F32), ((rows, width), BF16), ((rows, halves * ff), BF16), (grad, BF16),
        ((width, rows), BF16), ((1, 2 * width), F32),
    ]
    scratch = [
        ((halves, width, ff), BF16), ((halves, width, ff), BF16), ((halves, width, part), BF16),
        ((halves, width, LANES), BF16), ((rows, halves * ff), BF16), ((rows, width), BF16),
        ((rows, width), F32), ((rows, width), F32),
        ((rows, LANES), F32), ((width, rows), BF16),
        ((rows, width), BF16), ((width, rows), BF16), ((rows, width), BF16), (grad, BF16),
    ]
    return pl.pallas_call(
        feed_back_kernel,
        out_shape=tuple(jax.ShapeDtypeStruct(*shape) for shape in shapes),
        in_specs=[SCALARS] + [ANYWHERE] * 7,
        out_specs=tuple([ANYWHERE] * 5 + whole(1)),
        scratch_shapes=[pltpu.VMEM(*shape) for shape in scratch]
        + [pltpu.SemaphoreType.DMA((16,))],
        compiler_params=PARAMS,
        cost_estimate=lasting(27),
        name="feed_backward",
    )(place, *fed, weights)


def kept_kernel(place, turned_in, cells_in, kept, turned, cells, sems):
    halves, width, columns = kept.shape
    ff = 2 * columns
    copies = Copies(sems)
    turned_copy = copies.start(turned_in, turned)
    pieces = []
    for half in range(halves):
        start = pl.multiple_of(half * ff + place[2] * columns, columns)
        pieces.append(copies.start(cells_in.at[:, pl.ds(start, columns)], cells.at[half]))
    turned_copy.wait()
    for half in range(halves):
        pieces[half].wait()

        def rows_of(i, at, half=half):
            kept[half, at, :] = nn(turned[at, :], cells[half]).astype(BF16)

        each_tile(width, 384, rows_of)


def kept_grad(place, turned, cells, halves):
    width, rows = turned.shape
    columns = cells.shape[1] // halves // 2
    return pl.pallas_call(
        kept_kernel,
        out_shape=jax.ShapeDtypeStruct((halves, width, columns), BF16),
        in_specs=[SCALARS] + [ANYWHERE] * 2,
        out_specs=whole(1)[0],
        scratch_shapes=[
            pltpu.VMEM((width, rows), BF16),
            pltpu.VMEM((halves, rows, columns), BF16),
            pltpu.SemaphoreType.DMA((3,)),
        ],
        compiler_params=PARAMS,
        cost_estimate=lasting(5),
        name="kept_grad",
    )(place, turned, cells)


def spread_kernel(place, turned_in, cells_in, other, kept, sent, turned, cells, sems):
    halves, width, columns = other.shape
    ff = 2 * columns
    quarter = columns // 2
    copies = Copies(sems)
    turned_copy = copies.start(turned_in, turned)
    pieces = []
    for half in range(halves):
        start = pl.multiple_of(half * ff + place[2] * columns, columns)
        pieces.append(copies.start(cells_in.at[:, pl.ds(start, columns)], cells.at[half]))
    turned_copy.wait()
    for half in range(halves):
        pieces[half].wait()

        def rows_of(i, at, half=half):
            total = nn(turned[at, :], cells[half]) + other[half, at, :].astype(F32)
            low = total.astype(BF16)
            first = place[4] == 0
            kept[half, at, :] = jnp.where(first, low[:, :quarter], low[:, quarter:])
            sent[half, at, :] = jnp.where(first, low[:, quarter:], low[:, :quarter])

        each_tile(width, 384, rows_of)


def spread_grad(place, turned, cells, other):
    halves, width, columns = other.shape
    rows = turned.shape[1]
    part = jax.ShapeDtypeStruct((halves, width, columns // 2), BF16)
    return pl.pallas_call(
        spread_kernel,
        out_shape=(part, part),
        in_specs=[SCALARS] + [ANYWHERE] * 2 + whole(1),
        out_specs=tuple(whole(2)),
        scratch_shapes=[
            pltpu.VMEM((width, rows), BF16),
            pltpu.VMEM((halves, rows, columns), BF16),
            pltpu.SemaphoreType.DMA((3,)),
        ],
        compiler_params=PARAMS,
        cost_estimate=lasting(6),
        name="spread_grad",
    )(place, turned, cells, other)


def pair_kernel(
    place, one_turned_in, one_cells_in, two_turned_in, two_cells_in, kept, sent,
    one_turned, one_cells, two_turned, two_cells, sems,
):
    copies = Copies(sems)
    loads = [
        copies.start(*pair)
        for pair in (
            (one_turned_in, one_turned), (one_cells_in, one_cells),
            (two_turned_in, two_turned), (two_cells_in, two_cells),
        )
    ]
    for number, (turned, cells) in enumerate(((one_turned, one_cells), (two_turned, two_cells))):
        loads[2 * number].wait()
        loads[2 * number + 1].wait()
        family_grads(turned, cells, place[2] == number, kept, sent)


def pair_grads(place, one_turned, one_cells, two_turned, two_cells, halves):
    width, rows = one_turned.shape
    shape = jax.ShapeDtypeStruct((halves, width, one_cells.shape[1] // halves), BF16)
    return pl.pallas_call(
        pair_kernel,
        out_shape=(shape, shape),
        in_specs=[SCALARS] + [ANYWHERE] * 4,
        out_specs=tuple(whole(2)),
        scratch_shapes=[
            pltpu.VMEM((width, rows), BF16), pltpu.VMEM(one_cells.shape, BF16),
            pltpu.VMEM((width, rows), BF16), pltpu.VMEM(one_cells.shape, BF16),
            pltpu.SemaphoreType.DMA((4,)),
        ],
        compiler_params=PARAMS,
        cost_estimate=lasting(6),
        name="pair_grads",
    )(place, one_turned, one_cells, two_turned, two_cells)


def rank_kernel(place, mine, got, land_tokens, weights, late, through, small):
    halves, width, _ = weights.shape
    part = late.shape[1] // 2
    first = place[2] == 0
    grads = (
        jnp.where(first, mine[:LANDMARKS], got[:LANDMARKS]),
        jnp.where(first, got[:LANDMARKS], mine[:LANDMARKS]),
    )
    counts = landmark_counts(place)
    total = jnp.zeros((2 * LANDMARKS, width), F32)
    for index, grad in enumerate(grads):
        both = jnp.concatenate(split(grad / counts), axis=0)
        for half in range(halves):
            weight = weights[half, :, index * part : (index + 1) * part]
            total = total + nt(both[:, half * part : (half + 1) * part], weight)
    through[...] = jnp.concatenate(split(total[:LANDMARKS] + total[LANDMARKS:]), axis=0)
    zero = jnp.zeros((LANDMARKS, part), F32)
    own = []
    for index, grad in enumerate(grads):
        columns = grad[:, :part]
        for half in range(1, halves):
            columns = jnp.where(place[5] == half, grad[:, half * part : (half + 1) * part], columns)
        own.append(jnp.where(place[2] == 1 - index, columns, zero))
    high, low = split(jnp.concatenate(own, axis=1))
    mean_high, mean_low = split(land_tokens[...] / counts)
    means = jnp.concatenate([mean_high, mean_low, mean_high, jnp.zeros_like(mean_low)], axis=0).T
    factors = jnp.concatenate([high, high, low, jnp.zeros_like(low)], axis=0)
    late[...] = nn(means, factors).astype(BF16)
    gains = jnp.where(first, mine[LANDMARKS:], got[LANDMARKS:])
    shifts = jnp.where(first, got[LANDMARKS:], mine[LANDMARKS:])
    taps = jnp.where(place[5] == 0, gains[2:3], shifts[2:3])
    rows = [gains[1:2], gains[0:1], shifts[1:2], shifts[0:1], taps]
    rows.append(jnp.zeros((small.shape[0] - len(rows), width), F32))
    small[...] = jnp.concatenate(rows, axis=0).astype(BF16)


def rank_parts(place, mine, got, land_tokens, weights):
    halves, width, packed = weights.shape
    return pl.pallas_call(
        rank_kernel,
        out_shape=(
            jax.ShapeDtypeStruct((width, 2 * packed // 3), BF16),
            jax.ShapeDtypeStruct((2 * LANDMARKS, width), BF16),
            jax.ShapeDtypeStruct((16, width), BF16),
        ),
        in_specs=[SCALARS] + whole(4),
        out_specs=tuple(whole(3)),
        compiler_params=PARAMS,
        cost_estimate=lasting(4),
        name="rank_parts",
    )(place, mine, got, land_tokens, weights)


def token_grad_kernel(
    back_in, g_k_in, g_v_in, weights, own_grad, back, g_k, g_v, k_w, v_w, sems
):
    rows, width = back.shape
    halves, _, part = k_w.shape
    copies = Copies(sems)
    first = [
        copies.start(g_k_in, g_k),
        copies.start(weights.at[:, :, pl.ds(part, part)], k_w),
    ]
    later = [
        copies.start(back_in, back),
        copies.start(g_v_in, g_v),
        copies.start(weights.at[:, :, pl.ds(2 * part, part)], v_w),
    ]
    for copy in first + later:
        copy.wait()

    def rows_of(i, at):
        total = back[at, :]
        for half in range(halves):
            columns = slice(half * part, (half + 1) * part)
            total = total + nt(g_k[at, columns], k_w[half]) + nt(g_v[at, columns], v_w[half])
        own_grad[at, :] = total.astype(BF16)

    each_tile(rows, 512, rows_of)


def token_grad(back, g_k, g_v, weights):
    rows, width = back.shape
    halves, _, packed = weights.shape
    shapes = [((rows, width), F32), ((rows, width), BF16), ((rows, width), BF16)]
    shapes += [((halves, width, packed // 3), BF16)] * 2
    return pl.pallas_call(
        token_grad_kernel,
        out_shape=jax.ShapeDtypeStruct((rows, width), BF16),
        in_specs=[ANYWHERE] * 4,
        out_specs=whole(1)[0],
        scratch_shapes=[pltpu.VMEM(*shape) for shape in shapes]
        + [pltpu.SemaphoreType.DMA((5,))],
        compiler_params=PARAMS,
        cost_estimate=lasting(6),
        name="token_grad",
    )(back, g_k, g_v, weights)


def flipped(values, axis, bit):
    count = lax.axis_size(axis)
    return lax.ppermute(values, axis, [(i, i ^ bit) for i in range(count)])


def side_of(axis, bit):
    return (lax.axis_index(axis) // bit) % 2


def paired(mine, axis, bit, dim):
    other = flipped(mine, axis, bit)
    both = jnp.zeros(mine.shape[:dim] + (2,) + mine.shape[dim:], mine.dtype)
    side = side_of(axis, bit)
    both = lax.dynamic_update_slice_in_dim(both, jnp.expand_dims(mine, dim), side, dim)
    return lax.dynamic_update_slice_in_dim(both, jnp.expand_dims(other, dim), 1 - side, dim)


def ctx_bits():
    bits, bit = [], 1
    while bit < lax.axis_size("ctx"):
        bits.append(bit)
        bit *= 2
    return bits


def sequence_start(values):
    width = values.shape[1] // 2
    side = side_of("ctx", 1)
    kept = lax.dynamic_slice_in_dim(values, side * width, width, axis=1)
    sent = lax.dynamic_slice_in_dim(values, (1 - side) * width, width, axis=1)
    kept = kept + flipped(sent, "ctx", 1)
    return kept + flipped(kept, "tp", 1)


def sequence_end(kept):
    for bit in ctx_bits()[1:]:
        kept = kept + flipped(kept, "ctx", bit)
    return kept, flipped(kept, "ctx", 1)


def joined_halves(kept, other):
    return jnp.where(
        side_of("ctx", 1) == 0,
        jnp.concatenate([kept, other], axis=1),
        jnp.concatenate([other, kept], axis=1),
    )


def to_owner(kept, sent, combine):
    kept = combine(kept, flipped(sent, "ctx", 1))
    for bit in ctx_bits()[1:]:
        view = kept.reshape((-1, 2) + kept.shape[1:])
        side = side_of("ctx", bit)
        sent = lax.dynamic_index_in_dim(view, 1 - side, 1, False)
        kept = lax.dynamic_index_in_dim(view, side, 1, False)
        kept = combine(kept, flipped(sent, "ctx", bit))
    return kept[0], flipped(kept[0], "tp", 1)


def from_owners(part):
    whole_part = part[None]
    for bit in reversed(ctx_bits()):
        both = paired(whole_part, "ctx", bit, 1)
        whole_part = both.reshape((-1,) + part.shape)
    return whole_part.reshape((-1,) + part.shape[1:])


def merge_keys(one, two):
    size = LANES // 2
    one_top, two_top = one[..., size : size + 1], two[..., size : size + 1]
    top = jnp.maximum(one_top, two_top)
    one_factor, two_factor = jnp.exp(one_top - top), jnp.exp(two_top - top)
    summed = one * one_factor + two * two_factor
    lane = lax.broadcasted_iota(jnp.int32, summed.shape, summed.ndim - 1)
    return jnp.where(lane == size, top, summed)


def neighbour_rows(cells, count):
    pieces = lax.axis_size("ctx") * lax.axis_size("tp")
    up = [(i, i + 1) for i in range(pieces - 1)]
    before = lax.ppermute(cells[-count:], ("ctx", "tp"), up)
    after = lax.ppermute(cells[:count], ("ctx", "tp"), [(j, i) for i, j in up])
    return (
        jnp.pad(before, ((LANES - count, 0), (0, 0))),
        jnp.pad(after, ((0, LANES - count), (0, 0))),
    )


def own_quarter(shard):
    rows = shard.shape[0] // lax.axis_size("ctx")
    return lax.dynamic_slice_in_dim(shard, lax.axis_index("ctx") * rows, rows, axis=0)


def gathered(shard):
    full = lax.all_gather(own_quarter(shard), ("tp", "fsdp", "ctx"), tiled=True)
    return full.reshape(lax.axis_size("tp"), -1, shard.shape[1])


def gathered_early(shard, beside):
    count = lax.axis_size("fsdp")
    piece = own_quarter(shard)
    if count > 4:
        held = lax.all_gather(piece, "fsdp")
    else:
        here = lax.axis_index("fsdp")
        held = jnp.zeros((count,) + piece.shape, piece.dtype)
        held = lax.dynamic_update_slice_in_dim(held, piece[None], here, 0)
        for step in range(1, count):
            moved = lax.ppermute(piece, "fsdp", [(i, (i + step) % count) for i in range(count)])
            held = lax.dynamic_update_slice_in_dim(held, moved[None], (here - step) % count, 0)
    held, beside = gate(held, beside)
    bits = ctx_bits()
    halves = []
    for number, half in enumerate((held[: count // 2], held[count // 2 :])):
        half = half[None]
        if number == 0:
            half = paired(half[0], "tp", 1, 0)
        for place, bit in enumerate(reversed(bits[1:])):
            half = paired(half, "ctx", bit, 2 + place)
        if number == 1:
            half = paired(half[0], "tp", 1, 0)
        halves.append(paired(half, "ctx", bits[0], 1 + len(bits)))
    full = jnp.concatenate(halves, axis=1)
    return full.reshape(lax.axis_size("tp"), -1, shard.shape[1]), beside


def bits_of(axis):
    bits, bit = [], lax.axis_size(axis) // 2
    while bit:
        bits.append(bit)
        bit //= 2
    return bits


def added(*parts):
    return sum(part.astype(F32) for part in parts).astype(BF16)


def cut(cells, axis, bit, dim):
    size = cells.shape[dim] // 2
    side = side_of(axis, bit)
    return (
        lax.dynamic_slice_in_dim(cells, side * size, size, axis=dim),
        lax.dynamic_slice_in_dim(cells, (1 - side) * size, size, axis=dim),
    )


def gate(*values):
    return lax.optimization_barrier(values)


def dotf(spec, *operands):
    return jnp.einsum(spec, *operands, preferred_element_type=F32)


def taps_round(taps):
    middle = taps.shape[1] // 2
    gap = jnp.zeros((taps.shape[0], LANES - taps.shape[1]), F32)
    return jnp.concatenate([taps[:, middle::-1], gap, taps[:, :middle:-1]], axis=1)


def landmark_bounds(length):
    landmark = jnp.arange(LANDMARKS + 1, dtype=jnp.int32)
    return (landmark * length + LANDMARKS - 1) // LANDMARKS


def landmark_counts_of(length):
    bounds = landmark_bounds(length)
    return (bounds[1:] - bounds[:-1]).astype(F32)[:, None]


def landmark_rows(position, length):
    bounds = landmark_bounds(length)
    inside = (position[:, None] >= bounds[None, :-1]) & (position[:, None] < bounds[None, 1:])
    return inside.astype(BF16)


def on_device(
    tokens,
    lengths,
    qk_weight,
    value_weight,
    out_weight,
    in_weight,
    down_weight,
    norm_gains,
    norm_shifts,
    conv_weight,
    cotangent,
):
    tp_count = lax.axis_size("tp")
    tp_index = lax.axis_index("tp")
    ctx_index = lax.axis_index("ctx")
    _, slot_len, model_width = tokens.shape
    rows = slot_len // tp_count
    local_heads, tap_count = conv_weight.shape
    local_width = value_weight.shape[1]
    ff_width = in_weight.shape[1]
    head_size = local_width // local_heads
    heads = local_heads * tp_count
    owners = lax.axis_size("ctx")
    own_heads = heads // owners
    width = local_width * tp_count
    radius = tap_count // 2
    length = lengths[0]

    first_row = (ctx_index * tp_count + tp_index) * rows
    sides = (side_of("ctx", 1), ctx_index, side_of("ctx", ctx_bits()[-1]), tp_index)
    place = jnp.stack([first_row, length, *sides]).astype(jnp.int32)

    norm_columns = jnp.concatenate([norm_gains, norm_shifts], axis=0).T
    norm_columns = jnp.pad(norm_columns, ((0, 0), (0, LANES - norm_columns.shape[1])))
    ffn_full = gathered(
        jnp.concatenate([in_weight, down_weight.T, out_weight.T, norm_columns], axis=1)
    )
    own_taps = jnp.where(ctx_index == 0, conv_weight.astype(F32), 0.0)
    tap_rows = jnp.pad(own_taps, ((0, 8 - local_heads), (0, LANES - tap_count)))
    tap_rows = jnp.where(
        jnp.arange(model_width) // LANES == tp_index,
        jnp.tile(tap_rows, (1, model_width // LANES)),
        0.0,
    )
    own = lax.dynamic_slice_in_dim(tokens[0], tp_index * rows, rows, axis=0)
    land_tokens = sequence_start(jnp.concatenate([token_sums(place, own), tap_rows], axis=0))
    qkv_full, land_tokens = gathered_early(
        jnp.concatenate([qk_weight[0], qk_weight[1], value_weight], axis=1), land_tokens
    )
    land_tokens = joined_halves(*sequence_end(land_tokens))
    own_cotangent = lax.dynamic_slice_in_dim(cotangent[0], tp_index * rows, rows, axis=0)
    tap_weights = land_tokens[LANDMARKS : LANDMARKS + local_heads, : tp_count * LANES]
    tap_weights = tap_weights.reshape(local_heads, tp_count, LANES).transpose(1, 0, 2)
    tap_weights = tap_weights.reshape(heads, LANES)[:, :tap_count]
    land_tokens = land_tokens[:LANDMARKS]
    base, base_back = taps_round(tap_weights), taps_round(tap_weights[:, ::-1])

    queries, keys, values, v_plain, land_q, land_k, own_turned, *parts_of_third = projections(
        place, own, land_tokens, qkv_full, head_size, owners
    )
    v_ends = neighbour_rows(v_plain, radius)
    merged, merged_tp = to_owner(*parts_of_third, merge_keys)
    kept_turns = inverse_forward(place, land_q, land_k, owners)
    first, conv = first_and_conv(queries, values, *v_ends, land_k, base)
    merged, own_out = landmark_out(merged, merged_tp, kept_turns[0])
    land_out = from_owners(own_out)

    own_output, context, *fed, active, fed_turned, down_sent, last_norm = feed_forward(
        place, first, conv, land_out, own, own_cotangent, ffn_full, ff_width, local_width
    )
    high = ctx_bits()[-1]
    owner_count = lax.axis_size("fsdp")
    owner_rows = model_width // owner_count
    near, *farther = bits_of("fsdp")[::-1]

    def by_owner_bits(cells):
        return cells.reshape((2,) * (1 + len(farther)) + (-1, cells.shape[-1]))

    def cut_last(cells, bit):
        dim = cells.ndim - 3
        return tuple(piece.squeeze(dim) for piece in cut(cells, "fsdp", bit, dim))

    other_output = flipped(own_output, "tp", 1)
    down_other = flipped(down_sent, "ctx", 1)
    down_kept = kept_grad(place, fed_turned, active, tp_count)
    down_kept, down_other = gate(down_kept, down_other)
    down_mine, down_theirs = cut(down_kept, "ctx", high, 2)
    other_mine, other_theirs = cut(down_other, "ctx", high, 2)
    down_sent = added(down_theirs, other_theirs)
    down_got = flipped(down_sent, "ctx", high)
    fed[0], down_sent = gate(fed[0], down_sent)
    grad_first_res, grad_context, g_hidden, in_sent, att_turned, first_norm = feed_backward(
        place, fed, ffn_full, ff_width, local_width
    )
    in_sent, grad_context, g_hidden, other_output, down_got = gate(
        in_sent, grad_context, g_hidden, other_output, down_got
    )
    in_other = flipped(in_sent, "ctx", 1)
    g_ends = neighbour_rows(grad_context, radius)
    down = added(down_mine, other_mine, down_got)
    down_mine, down_sent = cut(down, "tp", 1, 0)
    down_got = flipped(down_sent, "tp", 1)
    grad_context, down_sent = gate(grad_context, down_sent)
    land_kept, land_sent, g_lk, g_q = attention_back(
        place, queries, grad_context, land_k, land_out, owners
    )
    land_kept, land_sent, in_other, g_ends = gate(land_kept, land_sent, in_other, g_ends)

    land_other = flipped(land_sent, "ctx", 1)
    in_kept, in_sent = spread_grad(place, fed[5], g_hidden, in_other)
    in_kept, in_sent, land_other, down_got = gate(in_kept, in_sent, land_other, down_got)
    land_grads = land_kept + land_other
    land_mine, land_theirs = cut(land_grads, "ctx", high, 0)
    land_got = flipped(land_theirs, "ctx", high)
    land_theirs, in_sent = gate(land_theirs, in_sent)
    in_got = flipped(in_sent, "ctx", high)
    down = added(down_mine, down_got)
    grad_context, in_sent = gate(grad_context, in_sent)
    g_conv, g_taps = conv_back(v_plain, v_ends, grad_context, g_ends, base_back)
    g_conv, g_taps, land_got = gate(g_conv, g_taps, land_got)
    own_grads = (land_mine + land_got)[0]
    tp_grads = flipped(own_grads, "tp", 1)

    def parts(cells):
        return cells.reshape(rows, tp_count, local_width)

    def qkv_part(index):
        return qkv_full[:, :, index * local_width : (index + 1) * local_width]

    g_q, own_grads = gate(g_q, own_grads)
    mixed_kept, mixed_sent = pair_grads(place, att_turned, context, own_turned, g_q, tp_count)
    back_q = grad_first_res + dotf("tpk,pck->tc", parts(g_q), qkv_part(0))
    mixed_kept, mixed_sent, tp_grads, back_q = gate(mixed_kept, mixed_sent, tp_grads, back_q)
    mixed_got = flipped(mixed_sent, "ctx", 1)
    own_grads, mixed_sent = gate(own_grads + tp_grads, mixed_sent)
    spread, lq_mid, lk_mid = inverse_backward(
        place, land_q, land_k, merged, own_grads, *kept_turns
    )
    spread, in_got, mixed_got = gate(spread, in_got, mixed_got)
    spread = from_owners(spread)

    in_mine, in_sent = cut(added(in_kept, in_got), "tp", 1, 0)
    in_got = flipped(in_sent, "tp", 1)
    def by_ctx(cells):
        return cells.reshape(tp_count, owner_count, 2, -1, local_width)

    mixed = added(mixed_kept, mixed_got)
    mixed_mine, mixed_sent = cut(by_ctx(mixed), "ctx", high, 2)
    mixed_got = flipped(mixed_sent, "ctx", high)
    spread, in_sent, mixed_sent = gate(spread, in_sent, mixed_sent)
    g_k, g_v, sums, kv_kept, kv_sent = third_back(
        place, keys, values, land_q, spread, g_conv, lq_mid, lk_mid, g_lk, last_norm, first_norm,
        g_taps, own_turned, tp_count,
    )

    kv_kept, kv_sent, sums, in_got, mixed_got = gate(kv_kept, kv_sent, sums, in_got, mixed_got)
    kv_got = flipped(kv_sent, "ctx", 1)
    sums_mine, sums_sent = cut(sums, "ctx", 1, 1)
    sums_got = flipped(sums_sent, "ctx", 1)
    kv_kept, kv_got = gate(kv_kept, kv_got)
    kv_mine, kv_sent = cut(by_ctx(added(kv_kept, kv_got)), "ctx", high, 2)
    kv_sent, sums_mine, mixed_mine, in_mine, g_k = gate(
        kv_sent, sums_mine, mixed_mine, in_mine, g_k
    )
    kv_got = flipped(kv_sent, "ctx", high)
    sums = sums_mine + sums_got
    sums_got = flipped(sums, "tp", 1)
    mixed_mine, mixed_sent = cut(added(mixed_mine, mixed_got), "tp", 1, 0)
    sums, mixed_sent, in_mine = gate(sums, mixed_sent, in_mine)
    mixed_got = flipped(mixed_sent, "tp", 1)
    pair = jnp.concatenate([added(in_mine, in_got)[0], down[0]], axis=1)
    g_k, mixed_sent, pair = gate(g_k, mixed_sent, pair)
    pair = lax.psum_scatter(pair, "fsdp", scatter_dimension=0, tiled=True)
    own_grad = token_grad(back_q, g_k, g_v, qkv_full)
    own_grad, sums_got, mixed_got, kv_got = gate(own_grad, sums_got, mixed_got, kv_got)
    sums = sums + sums_got
    sums_got = flipped(sums, "ctx", high)
    kv_mine, kv_sent = cut(added(kv_mine, kv_got), "tp", 1, 0)
    own_grad, sums, kv_sent = gate(own_grad, sums, kv_sent)
    kv_got = flipped(kv_sent, "tp", 1)
    other_grad = flipped(own_grad, "tp", 1)
    sums = sums + sums_got
    sums_got = flipped(sums, "ctx", 1)
    sums, sums_got, kv_got = gate(sums, sums_got, kv_got)
    late, through, small = rank_parts(place, sums, sums_got, land_tokens, qkv_full)
    late, through, small, own_output, other_output = gate(
        late, through, small, own_output, other_output
    )
    late = late.reshape(owner_count, 2, -1, 2 * local_width)
    late = lax.dynamic_index_in_dim(late, place[4], 1, False)
    mixed = added(
        jnp.concatenate([mixed_mine, kv_mine], axis=-1).reshape(late.shape),
        jnp.concatenate([mixed_got, kv_got], axis=-1).reshape(late.shape),
        late,
    )
    small = jnp.broadcast_to(small[None], (owner_count,) + small.shape)
    mixed = by_owner_bits(jnp.concatenate([mixed, small], axis=1))
    mixed_mine, mixed_sent = cut_last(mixed, near)
    mixed_sent, pair = gate(mixed_sent, pair)
    mixed_got = flipped(mixed_sent, "fsdp", near)
    mixed = added(mixed_mine, mixed_got)
    for bit in farther:
        mixed_mine, mixed_sent = cut_last(mixed, bit)
        mixed = added(mixed_mine, flipped(mixed_sent, "fsdp", bit))
    small = mixed[-16:].astype(F32)
    mixed = mixed[:-16]

    def of_core(cells, core):
        cells = cells.reshape((owners // 2, 2) + cells.shape[1:])
        return [cells[i, core] for i in range(owners // 2)]

    mixed = from_owners(mixed[None])
    mixed, other_grad = gate(mixed, other_grad)
    sides = [jnp.concatenate(of_core(mixed, core), axis=0).astype(F32) for core in range(2)]
    grad_out, grad_k = sides[0][:, :local_width].T, sides[0][:, local_width:]
    grad_q, grad_v = sides[1][:, :local_width], sides[1][:, local_width:]

    own_columns = lax.axis_index("fsdp") * owner_rows
    norm_sums = lax.dynamic_slice_in_dim(small[:4], own_columns, owner_rows, axis=1)
    taps_sum = small[4].reshape(local_heads, LANES)
    grad_taps = jnp.concatenate(
        [taps_sum[:, radius - 1 :: -1], taps_sum[:, : -radius - 2 : -1]], axis=1
    )

    columns = pair.shape[1] // 2
    pair = from_owners(pair[None])
    pieces = [piece for core in range(2) for piece in of_core(pair, core)]
    grad_in = jnp.concatenate([piece[:, :columns] for piece in pieces], axis=1).astype(F32)
    grad_down = jnp.concatenate([piece[:, columns:] for piece in pieces], axis=1).astype(F32).T

    output = jnp.where(
        tp_index == 0,
        jnp.concatenate([own_output, other_output]),
        jnp.concatenate([other_output, own_output]),
    )[None]
    both_grads = jnp.where(
        tp_index == 0,
        jnp.concatenate([own_grad, other_grad]),
        jnp.concatenate([other_grad, own_grad]),
    )
    position = ctx_index * slot_len + jnp.arange(slot_len, dtype=jnp.int32)
    onehot = landmark_rows(position, length)
    grad_tokens = both_grads.astype(F32) + dotf(
        "tm,mc->tc", jnp.concatenate([onehot, onehot], axis=1), through
    )
    grad_tokens = grad_tokens.reshape(1, slot_len, model_width)
    return (
        output,
        grad_tokens,
        jnp.stack([grad_q, grad_k]),
        grad_v,
        grad_out,
        grad_in,
        grad_down,
        norm_sums[:2],
        norm_sums[2:],
        grad_taps,
    )


def solution(mesh):
    in_specs = (
        P("fsdp", "ctx", None),
        P("fsdp"),
        P(None, "fsdp", "tp"),
        P("fsdp", "tp"),
        P("tp", "fsdp"),
        P("fsdp", "tp"),
        P("tp", "fsdp"),
        P(None, "fsdp"),
        P(None, "fsdp"),
        P("tp", None),
        P("fsdp", "ctx", None),
    )
    out_specs = (
        P("fsdp", "ctx", None),
        P("fsdp", "ctx", None),
        P(None, "fsdp", "tp"),
        P("fsdp", "tp"),
        P("tp", "fsdp"),
        P("fsdp", "tp"),
        P("tp", "fsdp"),
        P(None, "fsdp"),
        P(None, "fsdp"),
        P("tp", None),
    )
    return jax.shard_map(
        on_device, mesh=mesh, in_specs=in_specs, out_specs=out_specs, check_vma=False
    )
```
